32 devices in a mesh: rep: 2 (over core), fsdp: 16 (over z, y, x).
Axes of the slice: x: 2, y: 2, z: 4, core: 2. Of those that a mesh axis runs over, the one named last changes fastest.
Arguments:
- hidden_in: bfloat16 [4096, 768], P(('rep', 'fsdp')), may hold values from -6 to 6
- targets: bfloat16 [4096, 768], P(('rep', 'fsdp')), may hold values from -6 to 6
- doc_ids: int32 [4096], P(('rep', 'fsdp')), may hold values from 0 to 15, as said below
- seg_nums: int32 [32], P(('rep', 'fsdp')), may hold values from 0 to 15, as said below
- valid_flags: int32 [4096], P(('rep', 'fsdp')), may hold values from 0 to 1, as said below
- seg_mats: bfloat16 [768, 9216], P('fsdp')
- seg_vecs: bfloat16 [9216], P('fsdp')
- cls_mats: bfloat16 [768, 9216], P('fsdp')
- cls_vecs: bfloat16 [9216], P('fsdp')
- seg_pos: bfloat16 [16, 768], replicated, may hold values from -3 to 3
Outputs:
- output: bfloat16 [4096, 768], P(('rep', 'fsdp'))
- input_grad: bfloat16 [4096, 768], P(('rep', 'fsdp'))
- seg_mats_grad: float32 [768, 9216], P('fsdp')
- seg_vecs_grad: float32 [9216], P('fsdp')
- cls_mats_grad: float32 [768, 9216], P('fsdp')
- cls_vecs_grad: float32 [9216], P('fsdp')
- seg_pos_grad: float32 [16, 768], replicated
- loss: float32 [], replicated
The draws below stay inside these ranges and needn't reach their ends.
Inputs may be any that keep to these rules, and one draw needn't show every extreme that they name: `doc_ids`: all slots of one aligned segment of 128 slots share an id; within each sequence of 2048 slots a segment's id is the index, counted from the sequence's start, of the first segment of its document, and a fully padded segment carries its own index. `seg_nums`: A segment's index within its document; 0 for a fully padded segment. `valid_flags`: in each segment the valid slots come first; a segment is fully padded or holds one document's tokens with its first slot valid; only a document's last segment is partly padded, and fully padded segments follow all documents of their sequence.
All inputs are finite; a program needn't handle non-finite values.
Results may differ from the reference program's by a relative error of at most 0.014.
Values may be sent and summed in bfloat16 or wider, within the bound.
No kernel may reach another device: no remote copies, remote signals or barrier semaphores. Data moves between devices by JAX's collectives and lax.ppermute only.
A program may use at most 192 MiB of HBM per device.

```python
from functools import partial
import jax
import jax.numpy as jnp
from jax import lax

D = 768
HEADS = 12
HEAD_DIM = 64
FF = 3072
SEG = 128
SEQ = 2048
TOKENS = 4096
SEG_SEQ = 16


def packing_layout(base_key):
    seq_total = TOKENS // SEQ
    seg_total = SEQ // SEG
    key_list = jax.random.split(jax.random.fold_in(base_key, 7), 5)
    start_rates = jax.random.randint(key_list[0], (seq_total, 1), 1, 5)
    start_coins = jax.random.randint(key_list[1], (seq_total, seg_total), 0, 16)
    starts = start_coins % jnp.power(2, start_rates) == 0
    seq_index = jnp.arange(seq_total)[:, None]
    seg_index = jnp.arange(seg_total)[None, :]
    jitter = jax.random.randint(key_list[2], (seq_total, 1), 0, 2)
    pad_count = 1 + (3 * seg_total // 4 - 1) * seq_index // max(seq_total - 1, 1) + jitter
    whole_seq = jax.random.randint(key_list[3], (), 0, seq_total)
    pad_count = jnp.where(seq_index == whole_seq, 0, pad_count)
    real_seg = seg_index < seg_total - pad_count
    starts = jnp.where(seq_index == whole_seq, seg_index == 0, starts | (seg_index == 0))
    marks = jnp.where(starts | jnp.logical_not(real_seg), seg_index, 0)
    doc_first = lax.cummax(marks, axis=1)
    seg_number = jnp.where(real_seg, seg_index - doc_first, 0)
    ending = jnp.concatenate([starts[:, 1:] | jnp.logical_not(real_seg[:, 1:]), jnp.ones((seq_total, 1), dtype=bool)], axis=1)
    fills = jax.random.randint(key_list[4], (seq_total, seg_total), 1, SEG + 1)
    counts = jnp.where(real_seg, jnp.where(ending, fills, SEG), 0)
    slot_index = jnp.arange(SEG)
    valid_rows = (slot_index[None, None, :] < counts[:, :, None]).astype(jnp.int32).reshape(TOKENS)
    doc_rows = jnp.broadcast_to(doc_first[:, :, None], (seq_total, seg_total, SEG)).reshape(TOKENS)
    return (doc_rows.astype(jnp.int32), seg_number.reshape(TOKENS // SEG).astype(jnp.int32), valid_rows)


def draw_doc_ids(key, part):
    return packing_layout(key)[0]


def draw_seg_nums(key, part):
    return packing_layout(key)[1]


def draw_valid_flags(key, part):
    return packing_layout(key)[2]


def matrix_draw(base_key):
    columns = 4 * D + 2 * FF
    column_ids = jnp.arange(columns)
    column_scale = jnp.where(column_ids < 3 * D, D ** (-0.5), jnp.where(column_ids < 4 * D, 4.0 * D ** (-0.5), jnp.where(column_ids < 4 * D + FF, D ** (-0.5), FF ** (-0.5))))
    values_raw = jax.random.normal(base_key, (D, columns), jnp.float32)
    return (values_raw * column_scale[None, :]).astype(jnp.bfloat16)


def vector_draw(base_key):
    total_len = 8 * D + FF
    entry_ids = jnp.arange(total_len)
    is_gain = (entry_ids >= 4 * D) & (entry_ids < 5 * D) | (entry_ids >= 6 * D) & (entry_ids < 7 * D)
    first_key, second_key = jax.random.split(base_key)
    bias_part = 0.3 * jax.random.normal(first_key, (total_len,), jnp.float32)
    gain_part = jax.random.uniform(second_key, (total_len,), jnp.float32, 0.6, 1.4)
    return jnp.where(is_gain, gain_part, bias_part).astype(jnp.bfloat16)


def draw_seg_mats(key, part):
    return matrix_draw(jax.random.fold_in(key, 11))


def draw_cls_mats(key, part):
    return matrix_draw(jax.random.fold_in(key, 12))


def draw_seg_vecs(key, part):
    return vector_draw(jax.random.fold_in(key, 13))


def draw_cls_vecs(key, part):
    return vector_draw(jax.random.fold_in(key, 14))


def levels(rng, dims, cuts, low, top_value):
    factor_of, own = 1.0, jax.random.fold_in(rng, 6)
    for dim, parts in cuts:
        draws = jnp.exp(jax.random.uniform(jax.random.fold_in(own, dim), (parts,), jnp.float32, low / len(cuts), top_value / len(cuts)))
        factor_of = factor_of * jnp.repeat(draws, dims[dim] // parts).reshape([-1 if axis == dim else 1 for axis in range(len(dims))])
    return factor_of


def gaussian(rng, dims, deviation, most, shards=(), held_as=jnp.bfloat16):
    result = deviation * jax.random.normal(rng, dims, jnp.float32)
    if shards:
        result = result * levels(rng, dims, shards, -0.22, 0.18)
    return jnp.clip(result, -most, most).astype(held_as)


def setup_inputs(seed: int = 0) -> dict:
    splits = jax.random.split(jax.random.key(seed), 11)
    hidden_in = gaussian(splits[0], (TOKENS, D), 1.0, 6.0, ((0, 32),))
    targets = gaussian(splits[1], (TOKENS, D), 1.0, 6.0, ((0, 32),))
    doc_ids = draw_doc_ids(jax.random.fold_in(splits[10], 71), 0)
    seg_nums = draw_seg_nums(jax.random.fold_in(splits[10], 71), 0)
    valid_flags = draw_valid_flags(jax.random.fold_in(splits[10], 71), 0)
    seg_mats = draw_seg_mats(jax.random.fold_in(splits[10], 71), 0)
    seg_vecs = draw_seg_vecs(jax.random.fold_in(splits[10], 71), 0)
    cls_mats = draw_cls_mats(jax.random.fold_in(splits[10], 71), 0)
    cls_vecs = draw_cls_vecs(jax.random.fold_in(splits[10], 71), 0)
    seg_pos = gaussian(splits[9], (SEG_SEQ, D), 0.5, 3.0)
    return {"hidden_in": hidden_in, "targets": targets, "doc_ids": doc_ids, "seg_nums": seg_nums, "valid_flags": valid_flags, "seg_mats": seg_mats, "seg_vecs": seg_vecs, "cls_mats": cls_mats, "cls_vecs": cls_vecs, "seg_pos": seg_pos}


@jax.custom_vjp
def low(v):
    return lax.optimization_barrier(v.astype(jnp.bfloat16)).astype(jnp.float32)

@jax.custom_vjp
def low_back(v):
    return v

def low_keep(v):
    return (low(v), None)

def low_pass(kept, grad):
    return (grad,)

def back_keep(v):
    return (v, None)

def back_low(kept, grad):
    return (low(grad),)
low.defvjp(low_keep, low_pass)
low_back.defvjp(back_keep, back_low)
HIGHEST = lax.Precision.HIGHEST
NORM_EPS = 1e-05
MASK_FILL = -1e+30

def layer_norm(summed, gain_vec, shift_vec):
    row_mean = lax.optimization_barrier(jnp.mean(summed, axis=-1, keepdims=True))
    centered = summed - row_mean
    row_var = lax.optimization_barrier(jnp.mean(centered * centered, axis=-1, keepdims=True))
    return centered * lax.rsqrt(row_var + NORM_EPS) * gain_vec + shift_vec

def post_block(rows_in, matrix, vector, allowed):
    model_width = rows_in.shape[-1]
    qkv_weight = matrix[:, :3 * model_width]
    out_weight = matrix[:, 3 * model_width:4 * model_width]
    up_weight = matrix[:, 4 * model_width:4 * model_width + FF]
    down_weight = matrix[:, 4 * model_width + FF:]
    pieces = [vector[offset * model_width:(offset + 1) * model_width] for offset in range(8)]
    query_bias, value_bias, out_bias, down_bias, gain_first, shift_first, gain_second, shift_second = pieces
    up_bias = vector[8 * model_width:]
    inputs = low(rows_in)
    projected = jnp.einsum('brd,de->bre', inputs, qkv_weight, precision=HIGHEST)
    head_shape = rows_in.shape[:2] + (HEADS, HEAD_DIM)
    queries = low(low_back(projected[..., :model_width] + query_bias)).reshape(head_shape)
    keys_in = low(low_back(projected[..., model_width:2 * model_width])).reshape(head_shape)
    values = low(low_back(projected[..., 2 * model_width:] + value_bias)).reshape(head_shape)
    scores = low_back(jnp.einsum('bqhe,bkhe->bhqk', queries, keys_in, precision=HIGHEST) * HEAD_DIM ** (-0.5))
    scores = jnp.where(allowed[:, None], scores, MASK_FILL)
    weights = low(jax.nn.softmax(scores, axis=-1))
    mixed_rows = jnp.einsum('bhqk,bkhe->bqhe', weights, values, precision=HIGHEST).reshape(rows_in.shape)
    mixed_rows = low(low_back(mixed_rows))
    branch = low_back(jnp.einsum('brd,de->bre', mixed_rows, out_weight, precision=HIGHEST) + out_bias)
    first_out = layer_norm(rows_in + branch, gain_first, shift_first)
    pre_act = low_back(jnp.einsum('brd,df->brf', low(first_out), up_weight, precision=HIGHEST) + up_bias)
    activated = low(jax.nn.gelu(pre_act, approximate=False))
    second = low_back(jnp.einsum('brf,df->brd', activated, down_weight, precision=HIGHEST) + down_bias)
    return layer_norm(first_out + second, gain_second, shift_second)

def one_sequence(params, pieces):
    seg_mats, seg_vecs, cls_mats, cls_vecs, seg_pos = params
    rows_seq, target_seq, live_seq, lead_doc, lead_num = pieces
    seg_total = SEQ // SEG
    live_grid = live_seq.reshape(seg_total, SEG)
    token_grid = rows_seq.reshape(seg_total, SEG, D)
    seg_allowed = (live_grid[:, None, :] > 0.5) | jnp.eye(SEG, dtype=bool)[None]
    first_out = post_block(token_grid, seg_mats, seg_vecs, seg_allowed)
    position_hot = (lead_num[:, None] == jnp.arange(seg_total)[None, :]).astype(first_out.dtype)
    heads_in = first_out[:, 0, :] + jnp.dot(position_hot, seg_pos, precision=HIGHEST)
    lead_live = live_grid[:, 0] > 0.5
    cls_allowed = (lead_doc[:, None] == lead_doc[None, :]) & lead_live[None, :] | jnp.eye(seg_total, dtype=bool)
    top_out = post_block(heads_in[None], cls_mats, cls_vecs, cls_allowed[None])[0]
    combined = jnp.concatenate([top_out[:, None, :], first_out[:, 1:, :]], axis=1).reshape(SEQ, D)
    output_seq = combined * live_seq[:, None]
    diff_seq = (output_seq - target_seq) * live_seq[:, None]
    return (output_seq, jnp.sum(diff_seq * diff_seq))

def reference(hidden_in, targets, doc_ids, seg_nums, valid_flags, seg_mats, seg_vecs, cls_mats, cls_vecs, seg_pos):
    seq_total = TOKENS // SEQ
    seg_total = SEQ // SEG
    live_rows = valid_flags.astype(jnp.float32)
    count_all = jnp.sum(live_rows)
    lead_doc = doc_ids.reshape(seq_total, seg_total, SEG)[:, :, 0]
    lead_num = seg_nums.reshape(seq_total, seg_total)
    target_rows = targets.astype(jnp.float32).reshape(seq_total, SEQ, D)
    live_seqs = live_rows.reshape(seq_total, SEQ)

    def objective(hidden_f, seg_mats_f, seg_vecs_f, cls_mats_f, cls_vecs_f, seg_pos_f):
        params = (seg_mats_f, seg_vecs_f, cls_mats_f, cls_vecs_f, seg_pos_f)
        outputs, squares = lax.map(jax.checkpoint(partial(one_sequence, params)), (hidden_f.reshape(seq_total, SEQ, D), target_rows, live_seqs, lead_doc, lead_num))
        square_sum = jnp.sum(squares)
        return (square_sum * (TOKENS * 0.5) / count_all, (outputs, square_sum))
    primals = tuple((argument.astype(jnp.float32) for argument in (hidden_in, seg_mats, seg_vecs, cls_mats, cls_vecs, seg_pos)))
    objective_value, pullback, extras = jax.vjp(objective, *primals, has_aux=True)
    outputs, square_sum = extras
    gradients = pullback(jnp.ones_like(objective_value))
    loss = square_sum / (count_all * D)
    return (outputs.reshape(TOKENS, D).astype(jnp.bfloat16), gradients[0].astype(jnp.bfloat16), gradients[1], gradients[2], gradients[3], gradients[4], gradients[5], loss)
```

```python
import jax
import jax.numpy as jnp
from jax import lax
from jax.sharding import PartitionSpec as P

HEADS = 12
HEAD_DIM = 64
FF = 3072
SEG = 128
SEQ = 2048


NORM_EPS = 1e-05
MASK_FILL = -1e30
SQRT_HALF = 0.7071067811865476
INV_SQRT_TWO_PI = 0.3989422804014327


def swapped(value, axis, apart):
    mask = 2**apart
    pairs = [(source, source ^ mask) for source in range(lax.axis_size(axis))]
    return lax.ppermute(value, axis, pairs)


def product_plain(left_side, right_side):
    return jnp.dot(left_side, right_side, preferred_element_type=jnp.float32)


def product_left(left_side, right_side):
    return lax.dot_general(
        left_side, right_side, (((0,), (0,)), ((), ())), preferred_element_type=jnp.float32
    )


def product_right(left_side, right_side):
    return lax.dot_general(
        left_side, right_side, (((1,), (1,)), ((), ())), preferred_element_type=jnp.float32
    )


def row_total(array_in):
    return jnp.sum(array_in.astype(jnp.float32), axis=0)


def unpack_weights(gathered, model_width, ff_width):
    matrix, vector = gathered
    vector = vector.astype(jnp.float32)
    pieces = tuple(
        (vector[offset * model_width : (offset + 1) * model_width] for offset in range(8))
    )
    return (
        (
            matrix[:, : 3 * model_width],
            matrix[:, 3 * model_width : 4 * model_width],
            matrix[:, 4 * model_width : 4 * model_width + ff_width],
            matrix[:, 4 * model_width + ff_width :],
        )
        + pieces
        + (vector[8 * model_width :],)
    )


def norm_forward(summed, gain_vec, shift_vec):
    row_mean = jnp.mean(summed, axis=-1, keepdims=True)
    centered = summed - row_mean
    inv_dev = lax.rsqrt(jnp.mean(centered * centered, axis=-1, keepdims=True) + NORM_EPS)
    normed = centered * inv_dev
    return (normed * gain_vec + shift_vec, normed, inv_dev)


def norm_backward(grad_out, normed, inv_dev, gain_vec):
    scaled = grad_out * gain_vec
    mean_one = jnp.mean(scaled, axis=-1, keepdims=True)
    mean_two = jnp.mean(scaled * normed, axis=-1, keepdims=True)
    grad_in = inv_dev * (scaled - mean_one - normed * mean_two)
    return (grad_in, jnp.sum(grad_out * normed, axis=0), jnp.sum(grad_out, axis=0))


def gelu_value(before):
    return 0.5 * before * (1.0 + lax.erf(before * SQRT_HALF))


def gelu_slope(before):
    return (
        0.5 * (1.0 + lax.erf(before * SQRT_HALF))
        + before * jnp.exp(-0.5 * before * before) * INV_SQRT_TWO_PI
    )


def attention_scores(queries, keys_in, allowed, score_scale):
    raw_scores = (
        jnp.einsum("bqhe,bkhe->bhqk", queries, keys_in, preferred_element_type=jnp.float32)
        * score_scale
    )
    return jnp.where(allowed, raw_scores, MASK_FILL)


def attention_forward(queries, keys_in, values, allowed, score_scale):
    scores = attention_scores(queries, keys_in, allowed, score_scale)
    row_top = jnp.max(scores, axis=-1, keepdims=True)
    log_total = row_top + jnp.log(jnp.sum(jnp.exp(scores - row_top), axis=-1, keepdims=True))
    weights = jnp.exp(scores - log_total).astype(jnp.bfloat16)
    mixed_rows = jnp.einsum("bhqk,bkhe->bqhe", weights, values, preferred_element_type=jnp.float32)
    return (mixed_rows, log_total)


def attention_backward(queries, keys_in, values, allowed, score_scale, log_total, grad_mixed):
    probabilities = jnp.exp(attention_scores(queries, keys_in, allowed, score_scale) - log_total)
    grad_probs = jnp.einsum(
        "bqhe,bkhe->bhqk", grad_mixed, values, preferred_element_type=jnp.float32
    )
    inner_sum = jnp.sum(grad_probs * probabilities, axis=-1, keepdims=True)
    grad_scores = (probabilities * (grad_probs - inner_sum)).astype(jnp.bfloat16)
    grad_query = (
        jnp.einsum("bhqk,bkhe->bqhe", grad_scores, keys_in, preferred_element_type=jnp.float32)
        * score_scale
    )
    grad_key = (
        jnp.einsum("bhqk,bqhe->bkhe", grad_scores, queries, preferred_element_type=jnp.float32)
        * score_scale
    )
    grad_value = jnp.einsum(
        "bhqk,bqhe->bkhe",
        probabilities.astype(jnp.bfloat16),
        grad_mixed,
        preferred_element_type=jnp.float32,
    )
    return (grad_query, grad_key, grad_value)


def block_forward(rows_in, unpacked, attend):
    (
        qkv_weight,
        out_weight,
        up_weight,
        down_weight,
        query_bias,
        value_bias,
        out_bias,
        down_bias,
        gain_first,
        shift_first,
        gain_second,
        shift_second,
        up_bias,
    ) = unpacked
    model_width = rows_in.shape[1]
    inputs = rows_in.astype(jnp.bfloat16)
    projected = product_plain(inputs, qkv_weight)
    queries = (projected[:, :model_width] + query_bias).astype(jnp.bfloat16)
    keys_in = projected[:, model_width : 2 * model_width].astype(jnp.bfloat16)
    values = (projected[:, 2 * model_width :] + value_bias).astype(jnp.bfloat16)
    mixed_rows, attend_kept = attend(queries, keys_in, values)
    mixed_rows = mixed_rows.astype(jnp.bfloat16)
    summed_first = rows_in + product_plain(mixed_rows, out_weight) + out_bias
    first_out, normed_first, inv_first = norm_forward(summed_first, gain_first, shift_first)
    first_low = first_out.astype(jnp.bfloat16)
    pre_act = product_plain(first_low, up_weight) + up_bias
    activated = gelu_value(pre_act).astype(jnp.bfloat16)
    summed_second = first_out + product_right(activated, down_weight) + down_bias
    block_out, normed_second, inv_second = norm_forward(summed_second, gain_second, shift_second)
    saved_state = (
        inputs,
        queries,
        keys_in,
        values,
        attend_kept,
        mixed_rows,
        normed_first,
        inv_first,
        first_low,
        pre_act,
        activated,
        normed_second,
        inv_second,
    )
    return (block_out, saved_state)


def block_backward(grad_out, unpacked, saved_state, attend_back):
    (
        qkv_weight,
        out_weight,
        up_weight,
        down_weight,
        query_bias,
        value_bias,
        out_bias,
        down_bias,
        gain_first,
        shift_first,
        gain_second,
        shift_second,
        up_bias,
    ) = unpacked
    (
        inputs,
        queries,
        keys_in,
        values,
        attend_kept,
        mixed_rows,
        normed_first,
        inv_first,
        first_low,
        pre_act,
        activated,
        normed_second,
        inv_second,
    ) = saved_state
    grad_second, grad_gain_second, grad_shift_second = norm_backward(
        grad_out, normed_second, inv_second, gain_second
    )
    second_low = grad_second.astype(jnp.bfloat16)
    grad_pre = (product_plain(second_low, down_weight) * gelu_slope(pre_act)).astype(jnp.bfloat16)
    grad_first = grad_second + product_right(grad_pre, up_weight)
    grad_summed, grad_gain_first, grad_shift_first = norm_backward(
        grad_first, normed_first, inv_first, gain_first
    )
    branch_low = grad_summed.astype(jnp.bfloat16)
    grad_mixed = product_right(branch_low, out_weight).astype(jnp.bfloat16)
    grad_query, grad_key, grad_value = attend_back(
        queries, keys_in, values, attend_kept, grad_mixed
    )
    grad_proj = jnp.concatenate([grad_query, grad_key, grad_value], axis=1)
    grad_rows = grad_summed + product_right(grad_proj, qkv_weight)
    vector_grad = jnp.concatenate(
        [
            row_total(grad_query),
            row_total(grad_value),
            row_total(branch_low),
            row_total(second_low),
            grad_gain_first,
            grad_shift_first,
            grad_gain_second,
            grad_shift_second,
            row_total(grad_pre),
        ]
    )
    weight_rows = (
        inputs,
        grad_proj,
        mixed_rows,
        branch_low,
        first_low,
        grad_pre,
        second_low,
        activated,
    )
    return (grad_rows, weight_rows, vector_grad)


def weight_products(weight_rows):
    inputs, grad_proj, mixed_rows, branch_low, first_low, grad_pre, second_low, activated = (
        weight_rows
    )
    return (
        product_left(inputs, grad_proj),
        product_left(mixed_rows, branch_low),
        product_left(first_low, grad_pre),
        product_left(second_low, activated),
    )


def local(
    hidden_in,
    targets,
    doc_ids,
    seg_nums,
    valid_flags,
    seg_mats,
    seg_vecs,
    cls_mats,
    cls_vecs,
    seg_pos,
):
    tok_rows, model_width = hidden_in.shape
    ff_width = FF
    seg_len = SEG
    group_span = SEQ // tok_rows
    seg_count = tok_rows // seg_len
    score_scale = HEAD_DIM ** (-0.5)
    head_shape = (HEADS, HEAD_DIM)
    live_rows = valid_flags.astype(jnp.float32)
    rank_full = lax.axis_index("fsdp")
    seg_gathered = (
        lax.all_gather(seg_mats, "fsdp", axis=0, tiled=True),
        lax.all_gather(seg_vecs, "fsdp", axis=0, tiled=True),
    )
    seg_unpacked = unpack_weights(seg_gathered, model_width, ff_width)
    cls_gathered = (
        lax.all_gather(cls_mats, "fsdp", axis=0, tiled=True),
        lax.all_gather(cls_vecs, "fsdp", axis=0, tiled=True),
    )
    cls_unpacked = unpack_weights(cls_gathered, model_width, ff_width)
    seg_allowed = (live_rows.reshape(seg_count, 1, 1, seg_len) > 0.5) | jnp.eye(seg_len, dtype=bool)
    seg_shape = (seg_count, seg_len) + head_shape

    def seg_attend(queries, keys_in, values):
        mixed_rows, log_total = attention_forward(
            queries.reshape(seg_shape),
            keys_in.reshape(seg_shape),
            values.reshape(seg_shape),
            seg_allowed,
            score_scale,
        )
        return (mixed_rows.reshape(tok_rows, model_width), log_total)

    def seg_attend_back(queries, keys_in, values, log_total, grad_mixed):
        grad_parts = attention_backward(
            queries.reshape(seg_shape),
            keys_in.reshape(seg_shape),
            values.reshape(seg_shape),
            seg_allowed,
            score_scale,
            log_total,
            grad_mixed.reshape(seg_shape),
        )
        return tuple(
            (
                grad_part.reshape(tok_rows, model_width).astype(jnp.bfloat16)
                for grad_part in grad_parts
            )
        )

    first_out, seg_saved = block_forward(hidden_in.astype(jnp.float32), seg_unpacked, seg_attend)
    first_grid = first_out.reshape(seg_count, seg_len, model_width)
    position_hot = (seg_nums[:, None] == jnp.arange(seg_pos.shape[0])[None, :]).astype(jnp.float32)
    position_rows = jnp.sum(
        position_hot[:, :, None] * seg_pos.astype(jnp.float32)[None, :, :], axis=1
    )
    heads_in = first_grid[:, 0, :] + position_rows
    lead_live = live_rows.reshape(seg_count, seg_len)[:, 0]
    lead_doc = doc_ids.reshape(seg_count, seg_len)[:, 0]
    lead_labels = jnp.where(lead_live > 0.5, lead_doc, -1).astype(jnp.bfloat16)
    lead_doc_low = lead_doc.astype(jnp.bfloat16)
    bit_count = group_span.bit_length() - 1
    key_total = group_span * seg_count
    own_slot = rank_full % group_span * seg_count + jnp.arange(seg_count)
    query_shape = (1, seg_count) + head_shape
    key_shape = (1, key_total) + head_shape

    def cls_attend(queries, keys_in, values):
        paired = jnp.concatenate([keys_in, values], axis=1)
        labels = lead_labels
        for bit_level in range(bit_count):
            other_pair, other_labels = swapped((paired, labels), "fsdp", bit_level)
            upper_half = rank_full // (1 << bit_level) % 2 == 1
            paired = jnp.where(
                upper_half,
                jnp.concatenate([other_pair, paired]),
                jnp.concatenate([paired, other_pair]),
            )
            labels = jnp.where(
                upper_half,
                jnp.concatenate([other_labels, labels]),
                jnp.concatenate([labels, other_labels]),
            )
        allowed = (labels[None, :] == lead_doc_low[:, None]) | (
            jnp.arange(key_total)[None, :] == own_slot[:, None]
        )
        allowed = allowed[None, None]
        mixed_rows, log_total = attention_forward(
            queries.reshape(query_shape),
            paired[:, :model_width].reshape(key_shape),
            paired[:, model_width:].reshape(key_shape),
            allowed,
            score_scale,
        )
        return (mixed_rows.reshape(seg_count, model_width), (paired, allowed, log_total))

    def cls_attend_back(queries, keys_in, values, attend_kept, grad_mixed):
        paired, allowed, log_total = attend_kept
        grad_query, grad_key, grad_value = attention_backward(
            queries.reshape(query_shape),
            paired[:, :model_width].reshape(key_shape),
            paired[:, model_width:].reshape(key_shape),
            allowed,
            score_scale,
            log_total,
            grad_mixed.reshape(query_shape),
        )
        grad_pair = jnp.concatenate(
            [grad_key.reshape(key_total, model_width), grad_value.reshape(key_total, model_width)],
            axis=1,
        )
        for bit_level in reversed(range(bit_count)):
            half_rows = grad_pair.shape[0] // 2
            upper_half = rank_full // (1 << bit_level) % 2 == 1
            kept_half = jnp.where(upper_half, grad_pair[half_rows:], grad_pair[:half_rows])
            sent_half = jnp.where(upper_half, grad_pair[:half_rows], grad_pair[half_rows:])
            grad_pair = kept_half + swapped(
                sent_half.astype(jnp.bfloat16), "fsdp", bit_level
            ).astype(sent_half.dtype)
        grad_pair = grad_pair.astype(jnp.bfloat16)
        return (
            grad_query.reshape(seg_count, model_width).astype(jnp.bfloat16),
            grad_pair[:, :model_width],
            grad_pair[:, model_width:],
        )

    top_out, cls_saved = block_forward(heads_in, cls_unpacked, cls_attend)
    combined = jnp.concatenate([top_out[:, None, :], first_grid[:, 1:, :]], axis=1).reshape(
        tok_rows, model_width
    )
    output_rows = combined * live_rows[:, None]
    diff_rows = (output_rows - targets.astype(jnp.float32)) * live_rows[:, None]
    count_all, square_all = lax.psum(
        (jnp.sum(live_rows), jnp.sum(diff_rows * diff_rows)), ("rep", "fsdp")
    )
    loss_value = square_all / (count_all * model_width)
    slots_all = tok_rows * lax.axis_size("rep") * lax.axis_size("fsdp")
    grad_grid = (diff_rows * (slots_all / count_all)).reshape(seg_count, seg_len, model_width)
    cls_back = unpack_weights(
        (
            lax.all_gather(cls_mats, "fsdp", axis=0, tiled=True),
            lax.all_gather(cls_vecs, "fsdp", axis=0, tiled=True),
        ),
        model_width,
        ff_width,
    )
    heads_grad, cls_weight_rows, cls_g_vec = block_backward(
        grad_grid[:, 0, :], cls_back, cls_saved, cls_attend_back
    )
    cls_g_qkv, cls_g_out, cls_g_up, cls_g_down = weight_products(cls_weight_rows)
    pos_local = jnp.sum(position_hot[:, :, None] * heads_grad[:, None, :], axis=0)
    seg_grad_out = jnp.concatenate([heads_grad[:, None, :], grad_grid[:, 1:, :]], axis=1).reshape(
        tok_rows, model_width
    )
    seg_back = unpack_weights(
        (
            lax.all_gather(seg_mats, "fsdp", axis=0, tiled=True),
            lax.all_gather(seg_vecs, "fsdp", axis=0, tiled=True),
        ),
        model_width,
        ff_width,
    )
    input_grad, seg_weight_rows, seg_g_vec = block_backward(
        seg_grad_out, seg_back, seg_saved, seg_attend_back
    )
    seg_g_qkv, seg_g_out, seg_g_up, seg_g_down = weight_products(seg_weight_rows)
    owner_rows = tuple(
        (
            lax.psum_scatter(seg_g_qkv, "fsdp", scatter_dimension=0, tiled=True),
            lax.psum_scatter(seg_g_out, "fsdp", scatter_dimension=0, tiled=True),
            lax.psum_scatter(seg_g_up, "fsdp", scatter_dimension=0, tiled=True),
            lax.psum_scatter(seg_g_down, "fsdp", scatter_dimension=0, tiled=True),
            lax.psum_scatter(seg_g_vec, "fsdp", scatter_dimension=0, tiled=True),
            lax.psum_scatter(cls_g_qkv, "fsdp", scatter_dimension=0, tiled=True),
            lax.psum_scatter(cls_g_out, "fsdp", scatter_dimension=0, tiled=True),
            lax.psum_scatter(cls_g_up, "fsdp", scatter_dimension=0, tiled=True),
            lax.psum_scatter(cls_g_down, "fsdp", scatter_dimension=0, tiled=True),
            lax.psum_scatter(cls_g_vec, "fsdp", scatter_dimension=0, tiled=True),
        )
    )
    replica_share = (
        lax.psum_scatter(
            owner_rows[0].astype(jnp.bfloat16), "rep", scatter_dimension=1, tiled=True
        ).astype(jnp.float32),
        lax.psum_scatter(
            owner_rows[1].astype(jnp.bfloat16), "rep", scatter_dimension=1, tiled=True
        ).astype(jnp.float32),
        lax.psum_scatter(
            owner_rows[2].astype(jnp.bfloat16), "rep", scatter_dimension=1, tiled=True
        ).astype(jnp.float32),
        lax.psum_scatter(
            owner_rows[3].astype(jnp.bfloat16), "rep", scatter_dimension=1, tiled=True
        ).astype(jnp.float32),
        lax.psum_scatter(
            owner_rows[4].astype(jnp.bfloat16), "rep", scatter_dimension=0, tiled=True
        ).astype(jnp.float32),
        lax.psum_scatter(
            owner_rows[5].astype(jnp.bfloat16), "rep", scatter_dimension=1, tiled=True
        ).astype(jnp.float32),
        lax.psum_scatter(
            owner_rows[6].astype(jnp.bfloat16), "rep", scatter_dimension=1, tiled=True
        ).astype(jnp.float32),
        lax.psum_scatter(
            owner_rows[7].astype(jnp.bfloat16), "rep", scatter_dimension=1, tiled=True
        ).astype(jnp.float32),
        lax.psum_scatter(
            owner_rows[8].astype(jnp.bfloat16), "rep", scatter_dimension=1, tiled=True
        ).astype(jnp.float32),
        lax.psum_scatter(
            owner_rows[9].astype(jnp.bfloat16), "rep", scatter_dimension=0, tiled=True
        ).astype(jnp.float32),
    )
    all_summed = (
        lax.all_gather(replica_share[0].astype(jnp.bfloat16), "rep", axis=1, tiled=True).astype(
            jnp.float32
        ),
        lax.all_gather(replica_share[1].astype(jnp.bfloat16), "rep", axis=1, tiled=True).astype(
            jnp.float32
        ),
        lax.all_gather(replica_share[2].astype(jnp.bfloat16), "rep", axis=1, tiled=True).astype(
            jnp.float32
        ),
        lax.all_gather(replica_share[3].astype(jnp.bfloat16), "rep", axis=1, tiled=True).astype(
            jnp.float32
        ),
        lax.all_gather(replica_share[4].astype(jnp.bfloat16), "rep", axis=0, tiled=True).astype(
            jnp.float32
        ),
        lax.all_gather(replica_share[5].astype(jnp.bfloat16), "rep", axis=1, tiled=True).astype(
            jnp.float32
        ),
        lax.all_gather(replica_share[6].astype(jnp.bfloat16), "rep", axis=1, tiled=True).astype(
            jnp.float32
        ),
        lax.all_gather(replica_share[7].astype(jnp.bfloat16), "rep", axis=1, tiled=True).astype(
            jnp.float32
        ),
        lax.all_gather(replica_share[8].astype(jnp.bfloat16), "rep", axis=1, tiled=True).astype(
            jnp.float32
        ),
        lax.all_gather(replica_share[9].astype(jnp.bfloat16), "rep", axis=0, tiled=True).astype(
            jnp.float32
        ),
    )
    seg_summed = all_summed[:5]
    cls_summed = all_summed[5:]
    pos_total = lax.psum(pos_local, ("rep", "fsdp"))
    seg_mat_grad = jnp.concatenate(
        [seg_summed[0], seg_summed[1], seg_summed[2], seg_summed[3]], axis=1
    )
    cls_mat_grad = jnp.concatenate(
        [cls_summed[0], cls_summed[1], cls_summed[2], cls_summed[3]], axis=1
    )
    return (
        output_rows.astype(jnp.bfloat16),
        input_grad.astype(jnp.bfloat16),
        seg_mat_grad,
        seg_summed[4],
        cls_mat_grad,
        cls_summed[4],
        pos_total,
        loss_value,
    )


LINE = 4
PLANE = 4
CORES = 2


def line_pairs(apart):
    total = LINE * PLANE
    return [(source, (source + apart * PLANE) % total) for source in range(total)]


def plane_pairs(mask):
    return [(source, source ^ mask) for source in range(LINE * PLANE)]


def along_line(value, apart):
    return lax.ppermute(value, "fsdp", line_pairs(apart))


def in_plane(value, mask):
    return lax.ppermute(value, "fsdp", plane_pairs(mask))


def other_core(value):
    return lax.ppermute(value, "rep", [(0, 1), (1, 0)])


def placed(whole, piece, *where):
    return lax.dynamic_update_slice(whole, piece, where)


def one_of(stack, index):
    return lax.dynamic_index_in_dim(stack, index, 0, keepdims=False)


def line_gather(piece, line_at):
    whole = jnp.zeros((LINE,) + piece.shape, piece.dtype)
    zeros = (0,) * piece.ndim
    whole = placed(whole, piece[None], line_at, *zeros)
    for apart in range(1, LINE):
        whole = placed(
            whole, along_line(piece, apart)[None], (line_at - apart) % LINE, *zeros
        )
    return whole


def plane_gather(piece, plane_at):
    whole = jnp.zeros((PLANE,) + piece.shape, piece.dtype)
    zeros = (0,) * piece.ndim
    whole = placed(whole, piece[None], plane_at, *zeros)
    for mask in range(1, PLANE):
        whole = placed(whole, in_plane(piece, mask)[None], plane_at ^ mask, *zeros)
    return whole


def plane_sum(piece):
    return piece + in_plane(piece, 1) + in_plane(piece, 2) + in_plane(piece, 3)


def weight_gather(piece, line_at, plane_at, core_at):
    rows, columns = piece.shape
    line = line_gather(piece, line_at)
    half = LINE // 2
    from_x, from_y = in_plane(line, 1), in_plane(line, 2)
    far_low, far_high = in_plane(from_x[:half], 2), in_plane(from_y[half:], 1)
    whole = jnp.zeros((LINE, PLANE, CORES, rows, columns), piece.dtype)
    for block, at, low in (
        (line, plane_at, 0),
        (from_x, plane_at ^ 1, 0),
        (from_y, plane_at ^ 2, 0),
        (far_low, plane_at ^ 3, 0),
        (far_high, plane_at ^ 3, half),
    ):
        whole = placed(whole, block[:, None, None], low, at, core_at, 0, 0)
        whole = placed(whole, other_core(block)[:, None, None], low, at, 1 - core_at, 0, 0)
    return whole.reshape(LINE * PLANE * CORES * rows, columns)


def plane_reduce(part_of):
    half = LINE // 2
    far = part_of(3).astype(jnp.bfloat16)
    from_y, from_x = in_plane(far[:half], 2), in_plane(far[half:], 1)
    to_x, to_y = part_of(1), part_of(2)
    to_x = jnp.concatenate([to_x[:half] + from_y.astype(jnp.float32), to_x[half:]])
    to_y = jnp.concatenate([to_y[:half], to_y[half:] + from_x.astype(jnp.float32)])
    got_x = in_plane(to_x.astype(jnp.bfloat16), 1)
    got_y = in_plane(to_y.astype(jnp.bfloat16), 2)
    kept = part_of(0) + got_x.astype(jnp.float32) + got_y.astype(jnp.float32)
    sent = kept.astype(jnp.bfloat16)
    total = kept[0]
    for apart in range(1, LINE):
        total = total + along_line(sent[apart], apart).astype(jnp.float32)
    return total


def slice_local(
    hidden_in,
    targets,
    doc_ids,
    seg_nums,
    valid_flags,
    seg_mats,
    seg_vecs,
    cls_mats,
    cls_vecs,
    seg_pos,
):
    tok_rows, model_width = hidden_in.shape
    ff_width = FF
    score_scale = HEAD_DIM ** (-0.5)
    low, wide = jnp.bfloat16, jnp.float32
    rank = lax.axis_index("fsdp")
    core_at = lax.axis_index("rep")
    line_at, plane_at = rank // PLANE, rank % PLANE
    group = LINE * PLANE
    own_rows, total_columns = seg_mats.shape
    half_rows = own_rows // CORES
    live_rows = valid_flags.astype(wide)

    seg_half = one_of(seg_mats.reshape(CORES, half_rows, total_columns), core_at)
    cls_half = one_of(cls_mats.reshape(CORES, half_rows, total_columns), core_at)
    vec_size = seg_vecs.shape[0]
    lanes = 128
    vec_block = jnp.concatenate([seg_vecs, cls_vecs]).reshape(2 * vec_size // lanes, lanes)
    count_row = jnp.full((1, lanes), jnp.sum(live_rows), wide).astype(low)
    vec_block = jnp.concatenate(
        [
            vec_block,
            count_row,
            jnp.zeros((half_rows - vec_block.shape[0] - 1, lanes), low),
        ]
    )
    edges = (0, 3 * model_width, 4 * model_width + ff_width, total_columns)
    where_at = (line_at, plane_at, core_at)
    qkv_full = weight_gather(
        jnp.concatenate([seg_half[:, : edges[1]], vec_block], axis=1), *where_at
    )
    up_full = weight_gather(seg_half[:, edges[1] : edges[2]], *where_at)
    down_full = weight_gather(
        jnp.concatenate(
            [seg_half[:, edges[2] :], cls_half[:, 3 * model_width : 4 * model_width]], axis=1
        ),
        *where_at,
    )
    qkv_weight = qkv_full[:, : edges[1]]
    vec_rows = qkv_full[:, edges[1] :].reshape(group, CORES, half_rows, lanes)
    vec_count = 2 * vec_size // lanes
    count_all = jnp.sum(vec_rows[:, :, vec_count, 0].astype(wide))
    both_vecs = vec_rows[:, 0, :vec_count].reshape(group, 2 * vec_size).astype(wide)
    seg_vector = both_vecs[:, :vec_size].reshape(group * vec_size)
    cls_vector = both_vecs[:, vec_size:].reshape(group * vec_size)
    out_weight, up_weight = up_full[:, :model_width], up_full[:, model_width:]
    down_weight, cls_out_full = down_full[:, :ff_width], down_full[:, ff_width:]

    def pieces_of(vector):
        return tuple(
            vector[offset * model_width : (offset + 1) * model_width] for offset in range(8)
        ) + (vector[8 * model_width :],)

    seg_unpacked = (qkv_weight, out_weight, up_weight, down_weight) + pieces_of(seg_vector)

    head_part = model_width // PLANE
    ff_part = ff_width // PLANE
    quarters = jnp.concatenate(
        [
            cls_half[:, : 3 * model_width]
            .reshape(half_rows, 3, PLANE, head_part)
            .transpose(2, 0, 1, 3)
            .reshape(PLANE, half_rows, 3 * head_part),
            cls_half[:, 4 * model_width : 4 * model_width + ff_width]
            .reshape(half_rows, PLANE, ff_part)
            .transpose(1, 0, 2),
            cls_half[:, 4 * model_width + ff_width :]
            .reshape(half_rows, PLANE, ff_part)
            .transpose(1, 0, 2),
        ],
        axis=2,
    )
    quarter_width = quarters.shape[2]
    plane_rows = jnp.zeros((PLANE, half_rows, quarter_width), low)
    plane_rows = placed(plane_rows, one_of(quarters, plane_at)[None], plane_at, 0, 0)
    for mask in range(1, PLANE):
        plane_rows = placed(
            plane_rows,
            in_plane(one_of(quarters, plane_at ^ mask), mask)[None],
            plane_at ^ mask,
            0,
            0,
        )
    quarter_rows = line_gather(plane_rows, line_at)[:, :, None]
    quarter_full = jnp.zeros((LINE, PLANE, CORES, half_rows, quarter_width), low)
    quarter_full = placed(quarter_full, quarter_rows, 0, 0, core_at, 0, 0)
    quarter_full = placed(quarter_full, other_core(quarter_rows), 0, 0, 1 - core_at, 0, 0)
    quarter_full = quarter_full.reshape(model_width, quarter_width)
    cls_qkv = quarter_full[:, : 3 * head_part]
    cls_up = quarter_full[:, 3 * head_part : 3 * head_part + ff_part]
    cls_down = quarter_full[:, 3 * head_part + ff_part :]
    cls_out = one_of(cls_out_full.reshape(PLANE, head_part, model_width), plane_at)

    seg_allowed = (live_rows.reshape(1, 1, 1, tok_rows) > 0.5) | jnp.eye(tok_rows, dtype=bool)
    seg_shape = (1, tok_rows, HEADS, HEAD_DIM)

    def seg_attend(queries, keys_in, values):
        mixed_rows, log_total = attention_forward(
            queries.reshape(seg_shape),
            keys_in.reshape(seg_shape),
            values.reshape(seg_shape),
            seg_allowed,
            score_scale,
        )
        return (mixed_rows.reshape(tok_rows, model_width), log_total)

    def seg_attend_back(queries, keys_in, values, log_total, grad_mixed):
        grad_parts = attention_backward(
            queries.reshape(seg_shape),
            keys_in.reshape(seg_shape),
            values.reshape(seg_shape),
            seg_allowed,
            score_scale,
            log_total,
            grad_mixed.reshape(seg_shape),
        )
        return tuple(part.reshape(tok_rows, model_width).astype(low) for part in grad_parts)

    first_out, seg_saved = block_forward(hidden_in.astype(wide), seg_unpacked, seg_attend)
    not_head = (jnp.arange(tok_rows) > 0).astype(wide)[:, None]
    target_rows = targets.astype(wide)
    plain_diff = (first_out * live_rows[:, None] - target_rows) * live_rows[:, None]
    rest_square = jnp.sum(plain_diff * plain_diff * not_head)

    own_num = seg_nums.astype(wide)
    position_hot = (seg_nums[:, None] == jnp.arange(seg_pos.shape[0])[None, :]).astype(wide)
    position_row = jnp.sum(position_hot[:, :, None] * seg_pos.astype(wide)[None, :, :], axis=1)
    facts = jnp.concatenate(
        [
            live_rows[:1],
            doc_ids[:1].astype(wide),
            own_num,
            rest_square[None],
            jnp.zeros((lanes - 4,), wide),
        ]
    )[None]
    head_row = jnp.concatenate([first_out[:1] + position_row, target_rows[:1], facts], axis=1)
    all_heads = plane_gather(line_gather(head_row, line_at), plane_at)
    all_heads = all_heads.transpose(1, 0, 2, 3).reshape(group, head_row.shape[1])
    heads_in = all_heads[:, :model_width]
    head_targets = all_heads[:, model_width : 2 * model_width]
    head_facts = all_heads[:, 2 * model_width :]
    head_live, head_doc, head_num = (head_facts[:, at] for at in range(3))
    rest_total = jnp.sum(head_facts[:, 3])

    (
        query_bias,
        value_bias,
        out_bias,
        down_bias,
        gain_first,
        shift_first,
        gain_second,
        shift_second,
        up_bias,
    ) = pieces_of(cls_vector)
    query_bias = one_of(query_bias.reshape(PLANE, head_part), plane_at)
    value_bias = one_of(value_bias.reshape(PLANE, head_part), plane_at)
    up_bias = one_of(up_bias.reshape(PLANE, ff_part), plane_at)
    allowed = ((head_live[None, :] > 0.5) & (head_doc[:, None] == head_doc[None, :])) | jnp.eye(
        group, dtype=bool
    )
    allowed = allowed[None, None]
    part_shape = (1, group, HEADS // PLANE, HEAD_DIM)
    cls_inputs = heads_in.astype(low)
    projected = product_plain(cls_inputs, cls_qkv)
    queries = (projected[:, :head_part] + query_bias).astype(low).reshape(part_shape)
    keys_in = projected[:, head_part : 2 * head_part].astype(low).reshape(part_shape)
    values = (projected[:, 2 * head_part :] + value_bias).astype(low).reshape(part_shape)
    mixed, log_total = attention_forward(queries, keys_in, values, allowed, score_scale)
    mixed = mixed.reshape(group, head_part).astype(low)
    summed_first = heads_in + plane_sum(product_plain(mixed, cls_out)) + out_bias
    cls_first, normed_first, inv_first = norm_forward(summed_first, gain_first, shift_first)
    cls_first_low = cls_first.astype(low)
    pre_act = product_plain(cls_first_low, cls_up) + up_bias
    activated = gelu_value(pre_act).astype(low)
    summed_second = cls_first + plane_sum(product_right(activated, cls_down)) + down_bias
    top_out, normed_second, inv_second = norm_forward(summed_second, gain_second, shift_second)

    out_scale = (tok_rows * group * CORES) / count_all
    head_diff = (top_out * head_live[:, None] - head_targets) * head_live[:, None]
    square_all = rest_total + jnp.sum(head_diff * head_diff)
    square_all = square_all + other_core(jnp.full((8, lanes), square_all))[0, 0]
    loss_value = square_all / (count_all * model_width)
    top_row = lax.dynamic_slice(top_out, (rank, 0), (1, model_width))
    output_rows = jnp.concatenate([top_row, first_out[1:]]) * live_rows[:, None]

    grad_top = head_diff * out_scale
    grad_second, grad_gain_second, grad_shift_second = norm_backward(
        grad_top, normed_second, inv_second, gain_second
    )
    second_low = grad_second.astype(low)
    grad_pre = (product_plain(second_low, cls_down) * gelu_slope(pre_act)).astype(low)
    grad_first = grad_second + plane_sum(product_right(grad_pre, cls_up))
    grad_summed, grad_gain_first, grad_shift_first = norm_backward(
        grad_first, normed_first, inv_first, gain_first
    )
    branch_low = grad_summed.astype(low)
    grad_mixed = product_right(branch_low, cls_out).astype(low).reshape(part_shape)
    grad_parts = attention_backward(
        queries, keys_in, values, allowed, score_scale, log_total, grad_mixed
    )
    grad_proj = jnp.concatenate(
        [part.reshape(group, head_part).astype(low) for part in grad_parts], axis=1
    )
    heads_grad = grad_summed + plane_sum(product_right(grad_proj, cls_qkv))
    head_row_grad = lax.dynamic_slice(heads_grad, (rank, 0), (1, model_width))
    number_hot = (jnp.arange(seg_pos.shape[0])[:, None] == head_num[None, :]).astype(wide)
    pos_local = jnp.dot(number_hot, heads_grad, precision=lax.Precision.HIGHEST)
    pos_total = pos_local + other_core(pos_local)

    shared = plane_gather(
        jnp.concatenate([grad_proj, mixed, grad_pre, activated], axis=1), plane_at
    )
    shared = shared.transpose(1, 0, 2)
    cuts = (0, head_part, 2 * head_part, 3 * head_part, 4 * head_part)
    pieces = [shared[:, :, cuts[at] : cuts[at + 1]].reshape(group, model_width) for at in range(4)]
    pieces += [
        shared[:, :, cuts[4] : cuts[4] + ff_part].reshape(group, ff_width),
        shared[:, :, cuts[4] + ff_part :].reshape(group, ff_width),
    ]
    grad_q, grad_k, grad_v, mixed_all, grad_pre_all, activated_all = pieces
    row_data = jnp.concatenate(
        [
            cls_inputs,
            grad_q,
            grad_k,
            grad_v,
            mixed_all,
            branch_low,
            cls_first_low,
            grad_pre_all,
            second_low,
            activated_all,
        ],
        axis=1,
    )
    row_data = jnp.concatenate([row_data, other_core(row_data)])
    sizes = (
        model_width,
        3 * model_width,
        model_width,
        model_width,
        model_width,
        ff_width,
        model_width,
        ff_width,
    )
    row_parts, start = [], 0
    for size in sizes:
        row_parts.append(row_data[:, start : start + size])
        start += size
    own_hot = (
        jnp.arange(model_width)[:, None] == rank * own_rows + jnp.arange(own_rows)[None, :]
    ).astype(low)

    def own_features(values_in):
        return product_plain(values_in, own_hot).astype(low)

    cls_mat_grad = jnp.concatenate(
        [
            product_left(own_features(row_parts[left]), row_parts[right])
            for left, right in ((0, 1), (2, 3), (4, 5), (6, 7))
        ],
        axis=1,
    )
    norm_grads = jnp.stack(
        [grad_gain_first, grad_shift_first, grad_gain_second, grad_shift_second]
    )
    norm_grads = norm_grads + other_core(norm_grads)
    cls_vec_all = jnp.concatenate(
        [
            row_total(row_parts[1][:, :model_width]),
            row_total(row_parts[1][:, 2 * model_width :]),
            row_total(row_parts[3]),
            row_total(row_parts[6]),
            norm_grads.reshape(4 * model_width),
            row_total(row_parts[5]),
        ]
    )
    cls_vec_grad = one_of(cls_vec_all.reshape(group, vec_size), rank)

    seg_grad_out = jnp.concatenate([head_row_grad, (plain_diff * out_scale)[1:]])
    input_grad, seg_rows, vector_grad = block_backward(
        seg_grad_out, seg_unpacked, seg_saved, seg_attend_back
    )
    seg_inputs, seg_proj, seg_mixed, seg_branch, seg_first, seg_pre, seg_second, seg_act = seg_rows

    def both_cores(values_in):
        return jnp.concatenate([values_in, other_core(values_in)])

    def own_half(values_in):
        halves = values_in.reshape(tok_rows, CORES, -1).transpose(1, 0, 2)
        return jnp.concatenate(
            [one_of(halves, core_at), other_core(one_of(halves, 1 - core_at))]
        )

    column = jnp.arange(model_width)
    mask_of, step_of, row_of = (
        column // (LINE * own_rows),
        column // own_rows % LINE,
        column % own_rows,
    )
    source = ((line_at + step_of) % LINE * PLANE + (plane_at ^ mask_of)) * own_rows + row_of
    order_hot = (jnp.arange(model_width)[:, None] == source[None, :]).astype(low)

    def ordered(values_in):
        return product_plain(values_in, order_hot).astype(low)

    vec_parts = vector_grad.reshape(group, vec_size).astype(low)
    rank_order = source.reshape(group, own_rows)[:, 0] // own_rows
    rank_hot = (rank_order[:, None] == jnp.arange(group)[None, :]).astype(low)
    vec_parts = product_plain(rank_hot, vec_parts)
    vec_lines = -(-vec_size // lanes)
    vec_parts = jnp.pad(vec_parts, ((0, 0), (0, vec_lines * lanes - vec_size)))
    vec_parts = jnp.pad(
        vec_parts.reshape(PLANE, LINE, vec_lines, lanes),
        ((0, 0), (0, 0), (0, own_rows - vec_lines), (0, 0)),
    )

    def reduced(pairs_in, extra):
        ready = [(ordered(both_cores(left)), own_half(right)) for left, right in pairs_in]
        span = LINE * own_rows

        def part_of(mask):
            parts = [
                product_left(left[:, mask * span : (mask + 1) * span], right).reshape(
                    LINE, own_rows, right.shape[1]
                )
                for left, right in ready
            ]
            if extra is not None:
                parts.append(extra[mask])
            return jnp.concatenate(parts, axis=2)

        return plane_reduce(part_of)

    mlp_sum = reduced(((seg_first, seg_pre), (seg_second, seg_act)), None)
    attn_sum = reduced(((seg_inputs, seg_proj), (seg_mixed, seg_branch)), vec_parts)
    mine = jnp.concatenate([attn_sum, mlp_sum], axis=1)
    theirs = other_core(mine)
    first_half = jnp.where(core_at == 0, mine, theirs)
    second_half = jnp.where(core_at == 0, theirs, mine)
    qkv_half, out_half = 3 * model_width // CORES, model_width // CORES
    up_half = ff_width // CORES
    widths = (qkv_half, out_half, lanes, up_half, up_half)
    starts = [sum(widths[:at]) for at in range(6)]
    columns = []
    for at in (0, 1, 3, 4):
        columns += [
            first_half[:, starts[at] : starts[at + 1]],
            second_half[:, starts[at] : starts[at + 1]],
        ]
    seg_mat_grad = jnp.concatenate(columns, axis=1)
    seg_vec_grad = (mine + theirs)[:vec_lines, starts[2] : starts[3]]
    seg_vec_grad = seg_vec_grad.reshape(vec_lines * lanes)[:vec_size]
    return (
        output_rows.astype(low),
        input_grad.astype(low),
        seg_mat_grad,
        seg_vec_grad,
        cls_mat_grad,
        cls_vec_grad,
        pos_total,
        loss_value,
    )


def solution(mesh):
    in_specs = (
        P(("rep", "fsdp"), None),
        P(("rep", "fsdp"), None),
        P(("rep", "fsdp")),
        P(("rep", "fsdp")),
        P(("rep", "fsdp")),
        P("fsdp", None),
        P("fsdp"),
        P("fsdp", None),
        P("fsdp"),
        P(),
    )
    out_specs = (
        P(("rep", "fsdp"), None),
        P(("rep", "fsdp"), None),
        P("fsdp", None),
        P("fsdp"),
        P("fsdp", None),
        P("fsdp"),
        P(),
        P(),
    )
    one_slice = dict(mesh.shape) == {"rep": CORES, "fsdp": LINE * PLANE}
    body = slice_local if one_slice else local
    return jax.shard_map(body, mesh=mesh, in_specs=in_specs, out_specs=out_specs, check_vma=False)
```

```python
import math

import jax
import jax.numpy as jnp
from jax import lax
from jax.experimental import pallas as pl
from jax.experimental.pallas import tpu as pltpu
from jax.sharding import PartitionSpec as P

HEADS = 12
HEAD_DIM = 64
FF = 3072
SEG = 128
SEQ = 2048


NORM_EPS = 1e-05
MASK_FILL = -1e30
SQRT_HALF = 0.7071067811865476
INV_SQRT_TWO_PI = 0.3989422804014327


def swapped(value, axis, apart):
    mask = 2**apart
    pairs = [(source, source ^ mask) for source in range(lax.axis_size(axis))]
    return lax.ppermute(value, axis, pairs)


def product_plain(left_side, right_side):
    return jnp.dot(left_side, right_side, preferred_element_type=jnp.float32)


def product_left(left_side, right_side):
    return lax.dot_general(
        left_side, right_side, (((0,), (0,)), ((), ())), preferred_element_type=jnp.float32
    )


def product_right(left_side, right_side):
    return lax.dot_general(
        left_side, right_side, (((1,), (1,)), ((), ())), preferred_element_type=jnp.float32
    )


def row_total(array_in):
    return jnp.sum(array_in.astype(jnp.float32), axis=0)


def unpack_weights(gathered, model_width, ff_width):
    matrix, vector = gathered
    vector = vector.astype(jnp.float32)
    pieces = tuple(
        (vector[offset * model_width : (offset + 1) * model_width] for offset in range(8))
    )
    return (
        (
            matrix[:, : 3 * model_width],
            matrix[:, 3 * model_width : 4 * model_width],
            matrix[:, 4 * model_width : 4 * model_width + ff_width],
            matrix[:, 4 * model_width + ff_width :],
        )
        + pieces
        + (vector[8 * model_width :],)
    )


def norm_forward(summed, gain_vec, shift_vec):
    row_mean = jnp.mean(summed, axis=-1, keepdims=True)
    centered = summed - row_mean
    inv_dev = lax.rsqrt(jnp.mean(centered * centered, axis=-1, keepdims=True) + NORM_EPS)
    normed = centered * inv_dev
    return (normed * gain_vec + shift_vec, normed, inv_dev)


def norm_backward(grad_out, normed, inv_dev, gain_vec):
    scaled = grad_out * gain_vec
    mean_one = jnp.mean(scaled, axis=-1, keepdims=True)
    mean_two = jnp.mean(scaled * normed, axis=-1, keepdims=True)
    grad_in = inv_dev * (scaled - mean_one - normed * mean_two)
    return (grad_in, jnp.sum(grad_out * normed, axis=0), jnp.sum(grad_out, axis=0))


def gelu_value(before):
    return 0.5 * before * (1.0 + lax.erf(before * SQRT_HALF))


def gelu_slope(before):
    return (
        0.5 * (1.0 + lax.erf(before * SQRT_HALF))
        + before * jnp.exp(-0.5 * before * before) * INV_SQRT_TWO_PI
    )


def attention_scores(queries, keys_in, allowed, score_scale):
    raw_scores = (
        jnp.einsum("bqhe,bkhe->bhqk", queries, keys_in, preferred_element_type=jnp.float32)
        * score_scale
    )
    return jnp.where(allowed, raw_scores, MASK_FILL)


def attention_forward(queries, keys_in, values, allowed, score_scale):
    scores = attention_scores(queries, keys_in, allowed, score_scale)
    row_top = jnp.max(scores, axis=-1, keepdims=True)
    log_total = row_top + jnp.log(jnp.sum(jnp.exp(scores - row_top), axis=-1, keepdims=True))
    weights = jnp.exp(scores - log_total).astype(jnp.bfloat16)
    mixed_rows = jnp.einsum("bhqk,bkhe->bqhe", weights, values, preferred_element_type=jnp.float32)
    return (mixed_rows, log_total)


def attention_backward(queries, keys_in, values, allowed, score_scale, log_total, grad_mixed):
    probabilities = jnp.exp(attention_scores(queries, keys_in, allowed, score_scale) - log_total)
    grad_probs = jnp.einsum(
        "bqhe,bkhe->bhqk", grad_mixed, values, preferred_element_type=jnp.float32
    )
    inner_sum = jnp.sum(grad_probs * probabilities, axis=-1, keepdims=True)
    grad_scores = (probabilities * (grad_probs - inner_sum)).astype(jnp.bfloat16)
    grad_query = (
        jnp.einsum("bhqk,bkhe->bqhe", grad_scores, keys_in, preferred_element_type=jnp.float32)
        * score_scale
    )
    grad_key = (
        jnp.einsum("bhqk,bqhe->bkhe", grad_scores, queries, preferred_element_type=jnp.float32)
        * score_scale
    )
    grad_value = jnp.einsum(
        "bhqk,bqhe->bkhe",
        probabilities.astype(jnp.bfloat16),
        grad_mixed,
        preferred_element_type=jnp.float32,
    )
    return (grad_query, grad_key, grad_value)


def block_forward(rows_in, unpacked, attend):
    (
        qkv_weight,
        out_weight,
        up_weight,
        down_weight,
        query_bias,
        value_bias,
        out_bias,
        down_bias,
        gain_first,
        shift_first,
        gain_second,
        shift_second,
        up_bias,
    ) = unpacked
    model_width = rows_in.shape[1]
    inputs = rows_in.astype(jnp.bfloat16)
    projected = product_plain(inputs, qkv_weight)
    queries = (projected[:, :model_width] + query_bias).astype(jnp.bfloat16)
    keys_in = projected[:, model_width : 2 * model_width].astype(jnp.bfloat16)
    values = (projected[:, 2 * model_width :] + value_bias).astype(jnp.bfloat16)
    mixed_rows, attend_kept = attend(queries, keys_in, values)
    mixed_rows = mixed_rows.astype(jnp.bfloat16)
    summed_first = rows_in + product_plain(mixed_rows, out_weight) + out_bias
    first_out, normed_first, inv_first = norm_forward(summed_first, gain_first, shift_first)
    first_low = first_out.astype(jnp.bfloat16)
    pre_act = product_plain(first_low, up_weight) + up_bias
    activated = gelu_value(pre_act).astype(jnp.bfloat16)
    summed_second = first_out + product_right(activated, down_weight) + down_bias
    block_out, normed_second, inv_second = norm_forward(summed_second, gain_second, shift_second)
    saved_state = (
        inputs,
        queries,
        keys_in,
        values,
        attend_kept,
        mixed_rows,
        normed_first,
        inv_first,
        first_low,
        pre_act,
        activated,
        normed_second,
        inv_second,
    )
    return (block_out, saved_state)


def block_backward(grad_out, unpacked, saved_state, attend_back):
    (
        qkv_weight,
        out_weight,
        up_weight,
        down_weight,
        query_bias,
        value_bias,
        out_bias,
        down_bias,
        gain_first,
        shift_first,
        gain_second,
        shift_second,
        up_bias,
    ) = unpacked
    (
        inputs,
        queries,
        keys_in,
        values,
        attend_kept,
        mixed_rows,
        normed_first,
        inv_first,
        first_low,
        pre_act,
        activated,
        normed_second,
        inv_second,
    ) = saved_state
    grad_second, grad_gain_second, grad_shift_second = norm_backward(
        grad_out, normed_second, inv_second, gain_second
    )
    second_low = grad_second.astype(jnp.bfloat16)
    grad_pre = (product_plain(second_low, down_weight) * gelu_slope(pre_act)).astype(jnp.bfloat16)
    grad_first = grad_second + product_right(grad_pre, up_weight)
    grad_summed, grad_gain_first, grad_shift_first = norm_backward(
        grad_first, normed_first, inv_first, gain_first
    )
    branch_low = grad_summed.astype(jnp.bfloat16)
    grad_mixed = product_right(branch_low, out_weight).astype(jnp.bfloat16)
    grad_query, grad_key, grad_value = attend_back(
        queries, keys_in, values, attend_kept, grad_mixed
    )
    grad_proj = jnp.concatenate([grad_query, grad_key, grad_value], axis=1)
    grad_rows = grad_summed + product_right(grad_proj, qkv_weight)
    vector_grad = jnp.concatenate(
        [
            row_total(grad_query),
            row_total(grad_value),
            row_total(branch_low),
            row_total(second_low),
            grad_gain_first,
            grad_shift_first,
            grad_gain_second,
            grad_shift_second,
            row_total(grad_pre),
        ]
    )
    weight_rows = (
        inputs,
        grad_proj,
        mixed_rows,
        branch_low,
        first_low,
        grad_pre,
        second_low,
        activated,
    )
    return (grad_rows, weight_rows, vector_grad)


def weight_products(weight_rows):
    inputs, grad_proj, mixed_rows, branch_low, first_low, grad_pre, second_low, activated = (
        weight_rows
    )
    return (
        product_left(inputs, grad_proj),
        product_left(mixed_rows, branch_low),
        product_left(first_low, grad_pre),
        product_left(second_low, activated),
    )


def local(
    hidden_in,
    targets,
    doc_ids,
    seg_nums,
    valid_flags,
    seg_mats,
    seg_vecs,
    cls_mats,
    cls_vecs,
    seg_pos,
):
    tok_rows, model_width = hidden_in.shape
    ff_width = FF
    seg_len = SEG
    group_span = SEQ // tok_rows
    seg_count = tok_rows // seg_len
    score_scale = HEAD_DIM ** (-0.5)
    head_shape = (HEADS, HEAD_DIM)
    live_rows = valid_flags.astype(jnp.float32)
    rank_full = lax.axis_index("fsdp")
    seg_gathered = (
        lax.all_gather(seg_mats, "fsdp", axis=0, tiled=True),
        lax.all_gather(seg_vecs, "fsdp", axis=0, tiled=True),
    )
    seg_unpacked = unpack_weights(seg_gathered, model_width, ff_width)
    cls_gathered = (
        lax.all_gather(cls_mats, "fsdp", axis=0, tiled=True),
        lax.all_gather(cls_vecs, "fsdp", axis=0, tiled=True),
    )
    cls_unpacked = unpack_weights(cls_gathered, model_width, ff_width)
    seg_allowed = (live_rows.reshape(seg_count, 1, 1, seg_len) > 0.5) | jnp.eye(seg_len, dtype=bool)
    seg_shape = (seg_count, seg_len) + head_shape

    def seg_attend(queries, keys_in, values):
        mixed_rows, log_total = attention_forward(
            queries.reshape(seg_shape),
            keys_in.reshape(seg_shape),
            values.reshape(seg_shape),
            seg_allowed,
            score_scale,
        )
        return (mixed_rows.reshape(tok_rows, model_width), log_total)

    def seg_attend_back(queries, keys_in, values, log_total, grad_mixed):
        grad_parts = attention_backward(
            queries.reshape(seg_shape),
            keys_in.reshape(seg_shape),
            values.reshape(seg_shape),
            seg_allowed,
            score_scale,
            log_total,
            grad_mixed.reshape(seg_shape),
        )
        return tuple(
            (
                grad_part.reshape(tok_rows, model_width).astype(jnp.bfloat16)
                for grad_part in grad_parts
            )
        )

    first_out, seg_saved = block_forward(hidden_in.astype(jnp.float32), seg_unpacked, seg_attend)
    first_grid = first_out.reshape(seg_count, seg_len, model_width)
    position_hot = (seg_nums[:, None] == jnp.arange(seg_pos.shape[0])[None, :]).astype(jnp.float32)
    position_rows = jnp.sum(
        position_hot[:, :, None] * seg_pos.astype(jnp.float32)[None, :, :], axis=1
    )
    heads_in = first_grid[:, 0, :] + position_rows
    lead_live = live_rows.reshape(seg_count, seg_len)[:, 0]
    lead_doc = doc_ids.reshape(seg_count, seg_len)[:, 0]
    lead_labels = jnp.where(lead_live > 0.5, lead_doc, -1).astype(jnp.bfloat16)
    lead_doc_low = lead_doc.astype(jnp.bfloat16)
    bit_count = group_span.bit_length() - 1
    key_total = group_span * seg_count
    own_slot = rank_full % group_span * seg_count + jnp.arange(seg_count)
    query_shape = (1, seg_count) + head_shape
    key_shape = (1, key_total) + head_shape

    def cls_attend(queries, keys_in, values):
        paired = jnp.concatenate([keys_in, values], axis=1)
        labels = lead_labels
        for bit_level in range(bit_count):
            other_pair, other_labels = swapped((paired, labels), "fsdp", bit_level)
            upper_half = rank_full // (1 << bit_level) % 2 == 1
            paired = jnp.where(
                upper_half,
                jnp.concatenate([other_pair, paired]),
                jnp.concatenate([paired, other_pair]),
            )
            labels = jnp.where(
                upper_half,
                jnp.concatenate([other_labels, labels]),
                jnp.concatenate([labels, other_labels]),
            )
        allowed = (labels[None, :] == lead_doc_low[:, None]) | (
            jnp.arange(key_total)[None, :] == own_slot[:, None]
        )
        allowed = allowed[None, None]
        mixed_rows, log_total = attention_forward(
            queries.reshape(query_shape),
            paired[:, :model_width].reshape(key_shape),
            paired[:, model_width:].reshape(key_shape),
            allowed,
            score_scale,
        )
        return (mixed_rows.reshape(seg_count, model_width), (paired, allowed, log_total))

    def cls_attend_back(queries, keys_in, values, attend_kept, grad_mixed):
        paired, allowed, log_total = attend_kept
        grad_query, grad_key, grad_value = attention_backward(
            queries.reshape(query_shape),
            paired[:, :model_width].reshape(key_shape),
            paired[:, model_width:].reshape(key_shape),
            allowed,
            score_scale,
            log_total,
            grad_mixed.reshape(query_shape),
        )
        grad_pair = jnp.concatenate(
            [grad_key.reshape(key_total, model_width), grad_value.reshape(key_total, model_width)],
            axis=1,
        )
        for bit_level in reversed(range(bit_count)):
            half_rows = grad_pair.shape[0] // 2
            upper_half = rank_full // (1 << bit_level) % 2 == 1
            kept_half = jnp.where(upper_half, grad_pair[half_rows:], grad_pair[:half_rows])
            sent_half = jnp.where(upper_half, grad_pair[:half_rows], grad_pair[half_rows:])
            grad_pair = kept_half + swapped(
                sent_half.astype(jnp.bfloat16), "fsdp", bit_level
            ).astype(sent_half.dtype)
        grad_pair = grad_pair.astype(jnp.bfloat16)
        return (
            grad_query.reshape(seg_count, model_width).astype(jnp.bfloat16),
            grad_pair[:, :model_width],
            grad_pair[:, model_width:],
        )

    top_out, cls_saved = block_forward(heads_in, cls_unpacked, cls_attend)
    combined = jnp.concatenate([top_out[:, None, :], first_grid[:, 1:, :]], axis=1).reshape(
        tok_rows, model_width
    )
    output_rows = combined * live_rows[:, None]
    diff_rows = (output_rows - targets.astype(jnp.float32)) * live_rows[:, None]
    count_all, square_all = lax.psum(
        (jnp.sum(live_rows), jnp.sum(diff_rows * diff_rows)), ("rep", "fsdp")
    )
    loss_value = square_all / (count_all * model_width)
    slots_all = tok_rows * lax.axis_size("rep") * lax.axis_size("fsdp")
    grad_grid = (diff_rows * (slots_all / count_all)).reshape(seg_count, seg_len, model_width)
    cls_back = unpack_weights(
        (
            lax.all_gather(cls_mats, "fsdp", axis=0, tiled=True),
            lax.all_gather(cls_vecs, "fsdp", axis=0, tiled=True),
        ),
        model_width,
        ff_width,
    )
    heads_grad, cls_weight_rows, cls_g_vec = block_backward(
        grad_grid[:, 0, :], cls_back, cls_saved, cls_attend_back
    )
    cls_g_qkv, cls_g_out, cls_g_up, cls_g_down = weight_products(cls_weight_rows)
    pos_local = jnp.sum(position_hot[:, :, None] * heads_grad[:, None, :], axis=0)
    seg_grad_out = jnp.concatenate([heads_grad[:, None, :], grad_grid[:, 1:, :]], axis=1).reshape(
        tok_rows, model_width
    )
    seg_back = unpack_weights(
        (
            lax.all_gather(seg_mats, "fsdp", axis=0, tiled=True),
            lax.all_gather(seg_vecs, "fsdp", axis=0, tiled=True),
        ),
        model_width,
        ff_width,
    )
    input_grad, seg_weight_rows, seg_g_vec = block_backward(
        seg_grad_out, seg_back, seg_saved, seg_attend_back
    )
    seg_g_qkv, seg_g_out, seg_g_up, seg_g_down = weight_products(seg_weight_rows)
    owner_rows = tuple(
        (
            lax.psum_scatter(seg_g_qkv, "fsdp", scatter_dimension=0, tiled=True),
            lax.psum_scatter(seg_g_out, "fsdp", scatter_dimension=0, tiled=True),
            lax.psum_scatter(seg_g_up, "fsdp", scatter_dimension=0, tiled=True),
            lax.psum_scatter(seg_g_down, "fsdp", scatter_dimension=0, tiled=True),
            lax.psum_scatter(seg_g_vec, "fsdp", scatter_dimension=0, tiled=True),
            lax.psum_scatter(cls_g_qkv, "fsdp", scatter_dimension=0, tiled=True),
            lax.psum_scatter(cls_g_out, "fsdp", scatter_dimension=0, tiled=True),
            lax.psum_scatter(cls_g_up, "fsdp", scatter_dimension=0, tiled=True),
            lax.psum_scatter(cls_g_down, "fsdp", scatter_dimension=0, tiled=True),
            lax.psum_scatter(cls_g_vec, "fsdp", scatter_dimension=0, tiled=True),
        )
    )
    replica_share = (
        lax.psum_scatter(
            owner_rows[0].astype(jnp.bfloat16), "rep", scatter_dimension=1, tiled=True
        ).astype(jnp.float32),
        lax.psum_scatter(
            owner_rows[1].astype(jnp.bfloat16), "rep", scatter_dimension=1, tiled=True
        ).astype(jnp.float32),
        lax.psum_scatter(
            owner_rows[2].astype(jnp.bfloat16), "rep", scatter_dimension=1, tiled=True
        ).astype(jnp.float32),
        lax.psum_scatter(
            owner_rows[3].astype(jnp.bfloat16), "rep", scatter_dimension=1, tiled=True
        ).astype(jnp.float32),
        lax.psum_scatter(
            owner_rows[4].astype(jnp.bfloat16), "rep", scatter_dimension=0, tiled=True
        ).astype(jnp.float32),
        lax.psum_scatter(
            owner_rows[5].astype(jnp.bfloat16), "rep", scatter_dimension=1, tiled=True
        ).astype(jnp.float32),
        lax.psum_scatter(
            owner_rows[6].astype(jnp.bfloat16), "rep", scatter_dimension=1, tiled=True
        ).astype(jnp.float32),
        lax.psum_scatter(
            owner_rows[7].astype(jnp.bfloat16), "rep", scatter_dimension=1, tiled=True
        ).astype(jnp.float32),
        lax.psum_scatter(
            owner_rows[8].astype(jnp.bfloat16), "rep", scatter_dimension=1, tiled=True
        ).astype(jnp.float32),
        lax.psum_scatter(
            owner_rows[9].astype(jnp.bfloat16), "rep", scatter_dimension=0, tiled=True
        ).astype(jnp.float32),
    )
    all_summed = (
        lax.all_gather(replica_share[0].astype(jnp.bfloat16), "rep", axis=1, tiled=True).astype(
            jnp.float32
        ),
        lax.all_gather(replica_share[1].astype(jnp.bfloat16), "rep", axis=1, tiled=True).astype(
            jnp.float32
        ),
        lax.all_gather(replica_share[2].astype(jnp.bfloat16), "rep", axis=1, tiled=True).astype(
            jnp.float32
        ),
        lax.all_gather(replica_share[3].astype(jnp.bfloat16), "rep", axis=1, tiled=True).astype(
            jnp.float32
        ),
        lax.all_gather(replica_share[4].astype(jnp.bfloat16), "rep", axis=0, tiled=True).astype(
            jnp.float32
        ),
        lax.all_gather(replica_share[5].astype(jnp.bfloat16), "rep", axis=1, tiled=True).astype(
            jnp.float32
        ),
        lax.all_gather(replica_share[6].astype(jnp.bfloat16), "rep", axis=1, tiled=True).astype(
            jnp.float32
        ),
        lax.all_gather(replica_share[7].astype(jnp.bfloat16), "rep", axis=1, tiled=True).astype(
            jnp.float32
        ),
        lax.all_gather(replica_share[8].astype(jnp.bfloat16), "rep", axis=1, tiled=True).astype(
            jnp.float32
        ),
        lax.all_gather(replica_share[9].astype(jnp.bfloat16), "rep", axis=0, tiled=True).astype(
            jnp.float32
        ),
    )
    seg_summed = all_summed[:5]
    cls_summed = all_summed[5:]
    pos_total = lax.psum(pos_local, ("rep", "fsdp"))
    seg_mat_grad = jnp.concatenate(
        [seg_summed[0], seg_summed[1], seg_summed[2], seg_summed[3]], axis=1
    )
    cls_mat_grad = jnp.concatenate(
        [cls_summed[0], cls_summed[1], cls_summed[2], cls_summed[3]], axis=1
    )
    return (
        output_rows.astype(jnp.bfloat16),
        input_grad.astype(jnp.bfloat16),
        seg_mat_grad,
        seg_summed[4],
        cls_mat_grad,
        cls_summed[4],
        pos_total,
        loss_value,
    )


LINE = 4
PLANE = 4
CORES = 2
LANES = 128
GROUP = LINE * PLANE
LOW, WIDE = jnp.bfloat16, jnp.float32
MODEL = HEADS * HEAD_DIM
SPAN = 2 * LANES
TILE_START = (0, 1, 3, 4)


def line_pairs(apart):
    return [(source, (source + apart * PLANE) % GROUP) for source in range(GROUP)]


def plane_pairs(mask):
    return [(source, source ^ mask) for source in range(GROUP)]


def along_line(value, apart):
    return lax.ppermute(value, "fsdp", line_pairs(apart))


def in_plane(value, mask):
    return lax.ppermute(value, "fsdp", plane_pairs(mask))


def other_core(value):
    return lax.ppermute(value, "rep", [(0, 1), (1, 0)])


def shape_of(dims, dtype=WIDE):
    return jax.ShapeDtypeStruct(dims, dtype)


def run_kernel(body, name, outs, where, blocks, arrays, scratch=(), outs_far=False, flops=0):
    in_specs = [pl.BlockSpec(memory_space=pltpu.SMEM)]
    in_specs += [pl.BlockSpec(memory_space=pl.ANY)] * len(blocks)
    in_specs += [pl.BlockSpec(memory_space=pltpu.VMEM)] * len(arrays)
    out_space = pl.ANY if outs_far else pltpu.VMEM
    moved = sum(x.size * x.dtype.itemsize for x in list(blocks) + list(arrays))
    moved += sum(math.prod(o.shape) * jnp.dtype(o.dtype).itemsize for o in outs)
    return pl.pallas_call(
        body,
        name=name,
        out_shape=tuple(outs),
        in_specs=in_specs,
        out_specs=tuple(pl.BlockSpec(memory_space=out_space) for _ in outs),
        scratch_shapes=list(scratch),
        cost_estimate=pl.CostEstimate(flops=flops, bytes_accessed=moved, transcendentals=0),
        compiler_params=pltpu.CompilerParams(vmem_limit_bytes=VMEM_BYTES),
    )(where, *blocks, *arrays)


VMEM_BYTES = 48 * 1024 * 1024
BLOCK_PLAN = (
    (0, 0, LINE),
    (1, 0, LINE),
    (2, 0, LINE),
    (3, 0, LINE // 2),
    (3, LINE // 2, LINE // 2),
)
WEIGHT_COPIES = LINE * PLANE * CORES


def start_weight(where, blocks, scratch, sems):
    line_at, plane_at, core_at = where[0], where[1], where[2]
    copies = []
    for block_at, block in enumerate(blocks):
        mask, first, count = BLOCK_PLAN[block_at % len(BLOCK_PLAN)]
        core = core_at if block_at < len(BLOCK_PLAN) else 1 - core_at
        for step in range(count):
            target = scratch.at[(line_at + LINE - first - step) % LINE, plane_at ^ mask, core]
            copies.append(pltpu.make_async_copy(block.at[step], target, sems.at[len(copies)]))
    for copy in copies:
        copy.start()
    return copies


def wait_all(copies):
    for copy in copies:
        copy.wait()


def rows_view(scratch, first, last):
    value = scratch[:, :, :, :, first:last]
    return value.reshape(LINE * PLANE * CORES * value.shape[3], last - first)


def weight_scratch(rows, columns):
    return [
        pltpu.VMEM((LINE, PLANE, CORES, rows, columns), LOW),
        pltpu.SemaphoreType.DMA((WEIGHT_COPIES,)),
    ]


def prepare_kernel(where, seg, cls, vecs, first_out, second_out, third_out, quarter_out, kept):
    core_at, plane_at = where[2], where[1]
    half = seg.shape[1]
    qkv = 3 * MODEL
    own = seg[core_at]
    own_cls = cls[core_at]
    first_out[:, :qkv] = own[:, :qkv]
    first_out[:, qkv:] = vecs[...]
    second_out[...] = own[:, qkv : 4 * MODEL + FF]
    third_out[:, :FF] = own[:, 4 * MODEL + FF :]
    third_out[:, FF:] = own_cls[:, qkv : 4 * MODEL]
    part = FF // PLANE
    for at in range(PLANE):
        first = TILE_START[at] * LANES
        for piece in range(3):
            kept[at, :, piece * SPAN : (piece + 1) * SPAN] = own_cls[
                :, piece * MODEL + first : piece * MODEL + first + SPAN
            ]
        for piece in range(2):
            start = 4 * MODEL + piece * FF + at * part
            kept[at, :, 3 * SPAN + piece * part : 3 * SPAN + (piece + 1) * part] = own_cls[
                :, start : start + part
            ]
    for mask in range(PLANE):
        quarter_out[mask] = kept[plane_at ^ mask]


def lane_mask(rows, head):
    lane = lax.broadcasted_iota(jnp.int32, (rows, LANES), 1)
    return (lane < HEAD_DIM) if head == 0 else (lane >= HEAD_DIM)


def masked(value, mask):
    return jnp.where(mask, value, jnp.zeros_like(value))


def head_probabilities(query, key, allowed):
    scores = product_right(query, key) * HEAD_DIM ** (-0.5)
    scores = jnp.where(allowed, scores, MASK_FILL)
    raised = jnp.exp(scores - jnp.max(scores, axis=-1, keepdims=True))
    return raised / jnp.sum(raised, axis=-1, keepdims=True)


def attend_tiles(qkv, width, allowed):
    rows = qkv.shape[0]
    mixed = []
    for tile in range(width // LANES):
        at = tile * LANES
        query, key, value = (
            qkv[:, piece * width + at : piece * width + at + LANES] for piece in range(3)
        )
        total = jnp.zeros((rows, LANES), WIDE)
        for head in range(2):
            mask = lane_mask(rows, head)
            weights = head_probabilities(masked(query, mask), key, allowed).astype(LOW)
            total = total + product_plain(weights, masked(value, mask))
        mixed.append(total.astype(LOW))
    return mixed


def attend_tiles_back(qkv, grad_mixed, width, allowed):
    rows = qkv.shape[0]
    scale = HEAD_DIM ** (-0.5)
    results = ([], [], [])
    for tile in range(width // LANES):
        at = tile * LANES
        query, key, value = (
            qkv[:, piece * width + at : piece * width + at + LANES] for piece in range(3)
        )
        grad = grad_mixed[:, at : at + LANES]
        totals = [jnp.zeros((rows, LANES), WIDE) for _ in range(3)]
        for head in range(2):
            mask = lane_mask(rows, head)
            query_low, key_low, grad_low = (masked(x, mask) for x in (query, key, grad))
            chance = head_probabilities(query_low, key, allowed)
            grad_chance = product_right(grad_low, value)
            inner = jnp.sum(grad_chance * chance, axis=-1, keepdims=True)
            grad_scores = (chance * (grad_chance - inner)).astype(LOW)
            totals[0] = totals[0] + product_plain(grad_scores, key_low)
            totals[1] = totals[1] + product_left(grad_scores, query_low)
            totals[2] = totals[2] + product_left(chance.astype(LOW), grad_low)
        results[0].append((totals[0] * scale).astype(LOW))
        results[1].append((totals[1] * scale).astype(LOW))
        results[2].append(totals[2].astype(LOW))
    return results[0] + results[1] + results[2]


def token_allowed(live_row):
    shape = (SEG, SEG)
    same = lax.broadcasted_iota(jnp.int32, shape, 0) == lax.broadcasted_iota(jnp.int32, shape, 1)
    return (live_row > 0.5) | same


def qkv_kernel(where, *refs):
    blocks = refs[:10]
    hidden, live_row, qkv_out, both_out, vectors_out, count_out, weight, sems, flat = refs[10:]
    copies = start_weight(where, blocks, weight, sems)
    wait_all(copies)
    qkv = 3 * MODEL
    piece = (8 * MODEL + FF) // GROUP
    lines = -(-piece // LANES)
    count = jnp.zeros((1, LANES), WIDE)
    for chip in range(GROUP):
        at = (chip // PLANE, chip % PLANE)
        rows = weight[at[0], at[1], 0, 0:16, qkv:].astype(WIDE)
        for block in range(2):
            joined = jnp.concatenate(
                [rows[block * lines + r : block * lines + r + 1] for r in range(lines)], axis=1
            )
            flat[block : block + 1, chip * piece : (chip + 1) * piece] = joined[:, :piece]
        for core in range(CORES):
            rows_core = weight[at[0], at[1], core, 0:16, qkv:].astype(WIDE)
            count = count + rows_core[2 * lines : 2 * lines + 1]
    rows_each = (8 * MODEL + FF) // MODEL
    for block in range(2):
        for row in range(rows_each):
            vectors_out[block * rows_each + row : block * rows_each + row + 1, :] = flat[
                block : block + 1, row * MODEL : (row + 1) * MODEL
            ]
    count_out[...] = jnp.broadcast_to(count, count_out.shape)
    inputs = hidden[...]
    projected = product_plain(inputs, rows_view(weight, 0, qkv))
    qkv_out[:, :MODEL] = (projected[:, :MODEL] + vectors_out[0:1, :]).astype(LOW)
    qkv_out[:, MODEL : 2 * MODEL] = projected[:, MODEL : 2 * MODEL].astype(LOW)
    qkv_out[:, 2 * MODEL :] = (projected[:, 2 * MODEL :] + vectors_out[1:2, :]).astype(LOW)
    both_out[:, :MODEL] = inputs
    for tile, value in enumerate(attend_tiles(qkv_out[...], MODEL, token_allowed(live_row[...]))):
        both_out[:, MODEL + tile * LANES : MODEL + (tile + 1) * LANES] = value


def norm_rows(summed):
    row_mean = jnp.mean(summed, axis=-1, keepdims=True)
    centered = summed - row_mean
    inv_dev = lax.rsqrt(jnp.mean(centered * centered, axis=-1, keepdims=True) + NORM_EPS)
    return centered * inv_dev, inv_dev


def norm_rows_back(grad_out, normed, inv_dev, gain):
    scaled = grad_out * gain
    mean_one = jnp.mean(scaled, axis=-1, keepdims=True)
    mean_two = jnp.mean(scaled * normed, axis=-1, keepdims=True)
    return inv_dev * (scaled - mean_one - normed * mean_two)


def column_sum(value):
    return jnp.sum(value.astype(WIDE), axis=0, keepdims=True)


def four_rows(vectors, first):
    return jnp.concatenate([vectors[first + at : first + at + 1, :] for at in range(4)], axis=1)


def gelu_both(before):
    half = 0.5 * (1.0 + lax.erf(before * SQRT_HALF))
    slope = half + before * jnp.exp(-0.5 * before * before) * INV_SQRT_TWO_PI
    return before * half, slope


def up_kernel(where, *refs):
    blocks = refs[:10]
    hidden, both, vectors, normed_out, inv_out, slope_out, act_out, send_out = refs[10:18]
    weight, sems = refs[18:]
    copies = start_weight(where, blocks, weight, sems)
    wait_all(copies)
    core_at = where[2]
    branch = product_plain(both[:, MODEL:], rows_view(weight, 0, MODEL))
    normed, inv_dev = norm_rows(hidden[...].astype(WIDE) + branch + vectors[2:3, :])
    normed_out[...] = normed
    inv_out[...] = inv_dev
    first_low = (normed * vectors[4:5, :] + vectors[5:6, :]).astype(LOW)
    send_out[:, :MODEL] = first_low
    chunk = MODEL
    for at in range(FF // chunk):
        first = MODEL + at * chunk
        before = product_plain(first_low, rows_view(weight, first, first + chunk))
        value, slope = gelu_both(before + vectors[8 + at : 9 + at, :])
        act_out[:, at * chunk : (at + 1) * chunk] = value.astype(LOW)
        slope_out[:, at * chunk : (at + 1) * chunk] = slope
    half = FF // CORES
    sent = pl.multiple_of((1 - core_at) * half, LANES)
    send_out[:, MODEL:] = act_out[:, pl.ds(sent, half)]


def down_kernel(where, *refs):
    blocks = refs[:10]
    act, normed_first, vectors, targets, live, seg_pos = refs[10:16]
    normed_out, inv_out, diff_out, rows_out, head_out, cls_out = refs[16:22]
    weight, sems = refs[22:]
    copies = start_weight(where, blocks, weight, sems)
    wait_all(copies)
    plane_at, doc, number = where[1], where[3], where[4]
    first = normed_first[...] * vectors[4:5, :] + vectors[5:6, :]
    down = product_right(act[...], rows_view(weight, 0, FF))
    normed, inv_dev = norm_rows(first + down + vectors[3:4, :])
    normed_out[...] = normed
    inv_out[...] = inv_dev
    rows = normed * vectors[6:7, :] + vectors[7:8, :]
    live_rows = live[...]
    target_rows = targets[...].astype(WIDE)
    output = rows * live_rows
    rows_out[...] = output
    diff = (output - target_rows) * live_rows
    row_at = lax.broadcasted_iota(jnp.int32, (SEG, 1), 0)
    diff = jnp.where(row_at > 0, diff, 0.0)
    diff_out[...] = diff
    table = seg_pos[...].astype(WIDE)
    chosen = lax.broadcasted_iota(jnp.int32, table.shape, 0) == number
    position = jnp.sum(jnp.where(chosen, table, 0.0), axis=0, keepdims=True)
    head_out[:, :MODEL] = rows[0:1, :] + position
    head_out[:, MODEL : 2 * MODEL] = target_rows[0:1, :]
    square = jnp.sum(column_sum(diff * diff), axis=1, keepdims=True)
    lane = lax.broadcasted_iota(jnp.int32, (1, LANES), 1)
    facts = jnp.where(lane == 0, live_rows[0:1, :], 0.0)
    facts = jnp.where(lane == 1, doc.astype(WIDE), facts)
    facts = jnp.where(lane == 2, number.astype(WIDE), facts)
    facts = jnp.where(lane == 3, square, facts)
    head_out[:, 2 * MODEL :] = facts
    part = weight[plane_at, :, :, :, FF:].reshape(3, HEAD_DIM, MODEL)
    cls_out[...] = jnp.zeros_like(cls_out)
    cls_out[pl.ds(plane_at % 2, 3)] = part


def mlp_back_kernel(where, *refs):
    up_blocks, down_blocks = refs[:10], refs[10:20]
    diff, count, normed, inv_dev, vectors, slope = refs[20:26]
    grad_out, pre_out, send_out, sums_out = refs[26:30]
    up_weight, up_sems, down_weight, down_sems = refs[30:]
    down_copies = start_weight(where, down_blocks, down_weight, down_sems)
    up_copies = start_weight(where, up_blocks, up_weight, up_sems)
    core_at = where[2]
    scale = (SEG * GROUP * CORES) / count[0:1, 0:1]
    grad_top = diff[...] * scale
    normed_rows = normed[...]
    grad = norm_rows_back(grad_top, normed_rows, inv_dev[...], vectors[6:7, :])
    second = grad.astype(LOW)
    sums_out[1:2, 0:MODEL] = column_sum(second)
    sums_out[1:2, MODEL : 2 * MODEL] = column_sum(grad_top * normed_rows)
    sums_out[1:2, 2 * MODEL : 3 * MODEL] = column_sum(grad_top)
    send_out[:, :MODEL] = second
    wait_all(down_copies)
    chunk = MODEL
    for at in range(FF // chunk):
        columns = slice(at * chunk, (at + 1) * chunk)
        before = product_plain(second, rows_view(down_weight, at * chunk, (at + 1) * chunk))
        pre = (before * slope[:, columns]).astype(LOW)
        pre_out[:, columns] = pre
        sums_out[0:1, columns] = column_sum(pre)
    wait_all(up_copies)
    grad_out[...] = grad + product_right(pre_out[...], rows_view(up_weight, MODEL, MODEL + FF))
    half = FF // CORES
    sent = pl.multiple_of((1 - core_at) * half, LANES)
    send_out[:, MODEL:] = pre_out[:, pl.ds(sent, half)]


def scatter_parts(where, parts, outs, sems):
    line_at, plane_at = where[0], where[1]
    far_low, far_high, to_x, to_y, kept = outs
    half = LINE // 2
    copies = []
    for mask in range(PLANE):
        for step in range(LINE):
            source = parts.at[(line_at + step) % LINE * PLANE + (plane_at ^ mask)]
            if mask == 3:
                target = far_low.at[step] if step < half else far_high.at[step - half]
            else:
                target = (kept, to_x, to_y)[mask].at[step]
            copies.append(pltpu.make_async_copy(source, target, sems.at[len(copies)]))
    for copy in copies:
        copy.start()
    wait_all(copies)


def mlp_weight_kernel(where, *refs):
    first, first_got, second, second_got, pre, act = refs[:6]
    outs = refs[6:11]
    left, right, parts, sems = refs[11:]
    core_at = where[2]
    half = FF // CORES
    kept = pl.multiple_of(core_at * half, LANES)
    rows = GROUP * CORES * 24
    for at, (own, got, tail, got_tail) in enumerate(
        ((first, first_got, pre, second_got), (second, second_got, act, first_got))
    ):
        left[:SEG] = own[:, :MODEL]
        left[SEG:] = got[:, :MODEL]
        right[:SEG] = tail[:, pl.ds(kept, half)]
        right[SEG:] = got_tail[:, MODEL:]
        for piece in range(half // MODEL):
            start = piece * MODEL
            product = product_left(left[...], right[:, start : start + MODEL]).astype(LOW)
            parts[:, :, at * half + start : at * half + start + MODEL] = product.reshape(
                GROUP, rows // GROUP, MODEL
            )
    scatter_parts(where, parts, outs, sems)


def attn_weight_kernel(where, *refs):
    both, both_got, proj, got, branch = refs[:5]
    outs = refs[5:10]
    left, right, parts, sems = refs[10:]
    core_at = where[2]
    rows = MODEL
    qkv_half, out_half = 3 * MODEL // CORES, MODEL // CORES
    left[:SEG] = both[...]
    left[SEG:] = both_got[...]
    right[:SEG, :qkv_half] = proj[:, pl.ds(pl.multiple_of(core_at * qkv_half, LANES), qkv_half)]
    right[:SEG, qkv_half:] = branch[:, pl.ds(pl.multiple_of(core_at * out_half, LANES), out_half)]
    right[SEG:] = got[...]
    for piece in range(4):
        start = piece * out_half
        side = left[:, :MODEL] if piece < 3 else left[:, MODEL:]
        product = product_left(side, right[:, start : start + out_half]).astype(LOW)
        parts[:, :, start : start + out_half] = product.reshape(GROUP, rows // GROUP, out_half)
    scatter_parts(where, parts, outs, sems)


def fold_kernel(where, kept, got_x, got_y, own_out, *sent):
    for step in range(LINE):
        total = (
            kept[step].astype(WIDE) + got_x[step].astype(WIDE) + got_y[step].astype(WIDE)
        )
        if step == 0:
            own_out[...] = total
        else:
            sent[step - 1][...] = total.astype(LOW)


def reduce_parts(where, parts):
    far_low, far_high, to_x, to_y, kept = parts
    half = LINE // 2
    from_y, from_x = in_plane(far_low, 2), in_plane(far_high, 1)
    to_x = to_x.at[:half].add(from_y)
    to_y = to_y.at[half:].add(from_x)
    got_x, got_y = in_plane(to_x, 1), in_plane(to_y, 2)
    _, rows, columns = kept.shape
    folded = run_kernel(
        fold_kernel,
        "fold",
        [shape_of((rows, columns))] + [shape_of((rows, columns), LOW)] * (LINE - 1),
        where,
        (),
        (kept, got_x, got_y),
    )
    total = folded[0]
    for apart in range(1, LINE):
        total = total + along_line(folded[apart], apart).astype(WIDE)
    return total


def seg_back_kernel(where, *refs):
    qkv_blocks, up_blocks, down_blocks = refs[:10], refs[10:20], refs[20:30]
    (
        dheads,
        top_row,
        grad_first,
        normed_second,
        inv_second,
        slope,
        normed_first,
        inv_first,
        first_low,
        act,
        qkv,
        vectors,
        live_row,
        sums_in,
        out_rows,
    ) = refs[30:45]
    input_out, proj_out, branch_out, send_out, head_out, output_out = refs[45:51]
    qkv_weight, qkv_sems, up_weight, up_sems, down_weight, down_sems, mixed_grad = refs[51:]
    down_copies = start_weight(where, down_blocks, down_weight, down_sems)
    up_copies = start_weight(where, up_blocks, up_weight, up_sems)
    qkv_copies = start_weight(where, qkv_blocks, qkv_weight, qkv_sems)
    core_at = where[2]
    few = 16
    row_at = lax.broadcasted_iota(jnp.int32, (few, 1), 0)
    grad_top = dheads[...]
    normed_head = normed_second[0:1, :]
    grad = norm_rows_back(grad_top, normed_head, inv_second[0:1, :], vectors[6:7, :])
    second = grad.astype(LOW)
    second_few = jnp.where(row_at == 0, grad, 0.0).astype(LOW)
    head_out[:, 0:MODEL] = first_low[0:1, :MODEL]
    head_out[:, MODEL : 2 * MODEL] = second
    wait_all(down_copies)
    chunk = MODEL
    pre_parts = []
    base = 2 * MODEL
    for at in range(FF // chunk):
        columns = slice(at * chunk, (at + 1) * chunk)
        before = product_plain(second_few, rows_view(down_weight, at * chunk, (at + 1) * chunk))
        pre = (before * slope[0:few, columns]).astype(LOW)
        pre_parts.append(pre)
        head_out[:, base + at * chunk : base + (at + 1) * chunk] = pre[0:1, :]
    head_out[:, base + FF : base + 2 * FF] = act[0:1, :]
    wait_all(up_copies)
    pre_few = jnp.concatenate(pre_parts, axis=1)
    head_first = product_right(pre_few, rows_view(up_weight, MODEL, MODEL + FF))[0:1, :] + grad
    all_rows = lax.broadcasted_iota(jnp.int32, (SEG, 1), 0)
    grad_rows = jnp.where(all_rows == 0, head_first, grad_first[...])
    normed = normed_first[...]
    grad_summed = norm_rows_back(grad_rows, normed, inv_first[...], vectors[4:5, :])
    branch = grad_summed.astype(LOW)
    branch_out[...] = branch
    mixed_grad[...] = product_right(branch, rows_view(up_weight, 0, MODEL)).astype(LOW)
    pieces = attend_tiles_back(qkv[...], mixed_grad[...], MODEL, token_allowed(live_row[...]))
    for tile, value in enumerate(pieces):
        proj_out[:, tile * LANES : (tile + 1) * LANES] = value
    wait_all(qkv_copies)
    grad_in = grad_summed + product_right(proj_out[...], rows_view(qkv_weight, 0, 3 * MODEL))
    input_out[...] = grad_in.astype(LOW)
    qkv_half, out_half = 3 * MODEL // CORES, MODEL // CORES
    other = 1 - core_at
    send_out[:, :qkv_half] = proj_out[:, pl.ds(pl.multiple_of(other * qkv_half, LANES), qkv_half)]
    send_out[:, qkv_half:] = branch_out[
        :, pl.ds(pl.multiple_of(other * out_half, LANES), out_half)
    ]
    sums = (
        column_sum(proj_out[:, :MODEL]),
        column_sum(proj_out[:, 2 * MODEL :]),
        column_sum(branch),
        sums_in[1:2, 0:MODEL] + second.astype(WIDE),
        column_sum(grad_rows * normed),
        column_sum(grad_rows),
        sums_in[1:2, MODEL : 2 * MODEL] + grad_top * normed_head,
        sums_in[1:2, 2 * MODEL : 3 * MODEL] + grad_top,
    )
    base = 2 * MODEL + 2 * FF
    for at, value in enumerate(sums):
        head_out[:, base + at * MODEL : base + (at + 1) * MODEL] = value.astype(LOW)
    base = base + 8 * MODEL
    for at, pre in enumerate(pre_parts):
        columns = slice(at * chunk, (at + 1) * chunk)
        total = sums_in[0:1, columns] + column_sum(pre)
        head_out[:, base + at * chunk : base + (at + 1) * chunk] = total.astype(LOW)
    live_head = live_row[0:1, 0:1]
    output_out[...] = jnp.where(all_rows == 0, top_row[...] * live_head, out_rows[...]).astype(LOW)


def cls_weight_kernel(where, *refs):
    blocks = refs[: LINE * CORES]
    out, sems = refs[LINE * CORES :]
    line_at, plane_at, core_at = where[0], where[1], where[2]
    copies = []
    for block_at, block in enumerate(blocks):
        step, core = block_at % LINE, (core_at if block_at < LINE else 1 - core_at)
        for mask in range(PLANE):
            target = out.at[(line_at + LINE - step) % LINE, plane_at ^ mask, core]
            copies.append(pltpu.make_async_copy(block.at[mask], target, sems.at[len(copies)]))
    for copy in copies:
        copy.start()
    wait_all(copies)


def row_from_column(column, size):
    shape = (size, size)
    same = lax.broadcasted_iota(jnp.int32, shape, 0) == lax.broadcasted_iota(jnp.int32, shape, 1)
    return jnp.sum(jnp.where(same, column, 0.0), axis=0, keepdims=True)


def head_allowed(heads):
    facts = heads[:, 2 * MODEL :]
    live, doc = facts[:, 0:1], facts[:, 1:2]
    shape = (GROUP, GROUP)
    same = lax.broadcasted_iota(jnp.int32, shape, 0) == lax.broadcasted_iota(jnp.int32, shape, 1)
    live_row, doc_row = row_from_column(live, GROUP), row_from_column(doc, GROUP)
    return ((live_row > 0.5) & (doc == doc_row)) | same


def quarter_mask(plane_at):
    lane = lax.broadcasted_iota(jnp.int32, (GROUP, SPAN), 1)
    first = (plane_at % 2) * HEAD_DIM
    return (lane >= first) & (lane < first + 3 * HEAD_DIM)


def plane_piece(vectors, row, plane_at):
    value = jnp.zeros((1, SPAN), WIDE)
    for at in range(PLANE):
        first = TILE_START[at] * LANES
        value = jnp.where(plane_at == at, vectors[row : row + 1, first : first + SPAN], value)
    return value


def cls_attend_kernel(where, *refs):
    stacks, vectors, weight, out_weight = refs[:4], refs[4], refs[5], refs[6]
    heads_out, qkv_out, mixed_out, part_out = refs[7:]
    line_at, plane_at = where[0], where[1]
    for mask, stack in enumerate(stacks):
        for step in range(LINE):
            row = (line_at + LINE - step) % LINE * PLANE + (plane_at ^ mask)
            heads_out[pl.ds(row, 1), :] = stack[step : step + 1, :]
    heads = heads_out[...]
    inputs = heads[:, :MODEL].astype(LOW)
    projected = product_plain(inputs, weight[:, : 3 * SPAN])
    query = projected[:, :SPAN] + plane_piece(vectors, 12, plane_at)
    value = projected[:, 2 * SPAN :] + plane_piece(vectors, 13, plane_at)
    qkv_out[:, :SPAN] = query.astype(LOW)
    qkv_out[:, SPAN : 2 * SPAN] = projected[:, SPAN : 2 * SPAN].astype(LOW)
    qkv_out[:, 2 * SPAN :] = value.astype(LOW)
    mixed = attend_tiles(qkv_out[...], SPAN, head_allowed(heads))
    mixed = masked(jnp.concatenate(mixed, axis=1), quarter_mask(plane_at))
    mixed_out[...] = mixed
    part_out[...] = product_plain(mixed, out_weight[...])


def cls_mlp_kernel(where, *refs):
    heads, own, got_one, got_two, got_three, vectors, weight = refs[:7]
    normed_out, inv_out, low_out, act_out, slope_out, part_out = refs[7:]
    plane_at = where[1]
    branch = own[...] + got_one[...] + got_two[...] + got_three[...]
    normed, inv_dev = norm_rows(heads[:, :MODEL] + branch + vectors[14:15, :])
    normed_out[...] = normed
    inv_out[...] = inv_dev
    low = (normed * vectors[16:17, :] + vectors[17:18, :]).astype(LOW)
    low_out[...] = low
    part = FF // PLANE
    first = 3 * SPAN
    bias = vectors[pl.ds(20 + plane_at, 1), :]
    before = product_plain(low, weight[:, first : first + part]) + bias
    value, slope = gelu_both(before)
    act = value.astype(LOW)
    act_out[...] = act
    slope_out[...] = slope
    part_out[...] = product_right(act, weight[:, first + part :])


def cls_top_kernel(where, *refs):
    heads, own, got_one, got_two, got_three, vectors, weight = refs[:7]
    normed_first, count, slope = refs[7:10]
    top_out, square_out, grad_out, second_out, pre_out, part_out, sums_out = refs[10:17]
    held = refs[17]
    rank = where[0] * PLANE + where[1]
    first = normed_first[...] * vectors[16:17, :] + vectors[17:18, :]
    down = own[...] + got_one[...] + got_two[...] + got_three[...]
    normed, inv_dev = norm_rows(first + down + vectors[15:16, :])
    rows = normed * vectors[18:19, :] + vectors[19:20, :]
    held[...] = rows
    top_out[...] = held[pl.ds(rank, 1), :]
    facts = heads[:, 2 * MODEL :]
    live = facts[:, 0:1]
    diff = (rows * live - heads[:, MODEL : 2 * MODEL]) * live
    square = jnp.sum(column_sum(diff * diff), axis=1, keepdims=True)
    square = square + jnp.sum(facts[:, 3:4], axis=0, keepdims=True)
    square_out[...] = jnp.broadcast_to(square, square_out.shape)
    grad_top = diff * ((SEG * GROUP * CORES) / count[0:1, 0:1])
    grad = norm_rows_back(grad_top, normed, inv_dev, vectors[18:19, :])
    sums_out[0:1, :] = column_sum(grad_top * normed)
    sums_out[1:2, :] = column_sum(grad_top)
    grad_out[...] = grad
    second = grad.astype(LOW)
    second_out[...] = second
    part = FF // PLANE
    at = 3 * SPAN
    pre = (product_plain(second, weight[:, at + part :]) * slope[...]).astype(LOW)
    pre_out[...] = pre
    part_out[...] = product_right(pre, weight[:, at : at + part])


def cls_attend_back_kernel(where, *refs):
    heads, own, got_one, got_two, got_three, vectors, weight, out_weight = refs[:8]
    grad_in, normed_first, inv_first, qkv = refs[8:12]
    grad_out, branch_out, proj_out, part_out, sums_out = refs[12:]
    plane_at = where[1]
    grad_first = grad_in[...] + own[...] + got_one[...] + got_two[...] + got_three[...]
    normed = normed_first[...]
    grad = norm_rows_back(grad_first, normed, inv_first[...], vectors[16:17, :])
    sums_out[0:1, :] = column_sum(grad_first * normed)
    sums_out[1:2, :] = column_sum(grad_first)
    grad_out[...] = grad
    branch = grad.astype(LOW)
    branch_out[...] = branch
    mask = quarter_mask(plane_at)
    mixed_grad = masked(product_right(branch, out_weight[...]).astype(LOW), mask)
    pieces = attend_tiles_back(qkv[...], mixed_grad, SPAN, head_allowed(heads[...]))
    tiles = SPAN // LANES
    for piece in range(3):
        joined = jnp.concatenate(pieces[piece * tiles : (piece + 1) * tiles], axis=1)
        proj_out[:, piece * SPAN : (piece + 1) * SPAN] = masked(joined, mask)
    part_out[...] = product_right(proj_out[...], weight[:, : 3 * SPAN])


def cls_end_kernel(where, *refs):
    heads, grad, own, got_one, got_two, got_three = refs[:6]
    square, sums_back, sums_top = refs[6:9]
    row_out, shared_out, held = refs[9:]
    rank = where[0] * PLANE + where[1]
    total = grad[...] + own[...] + got_one[...] + got_two[...] + got_three[...]
    held[...] = total
    row_out[...] = held[pl.ds(rank, 1), :]
    number = row_from_column(heads[:, 2 * MODEL + 2 : 2 * MODEL + 3], GROUP)
    entry = lax.broadcasted_iota(jnp.int32, (GROUP, GROUP), 0).astype(WIDE)
    hot = (entry == number).astype(WIDE)
    shared_out[0:GROUP, :] = jnp.dot(hot, total, precision=lax.Precision.HIGHEST)
    shared_out[GROUP : GROUP + 1, 0:LANES] = square[0:1, :]
    shared_out[GROUP + 1 : GROUP + 3, :] = sums_back[0:2, :]
    shared_out[GROUP + 3 : GROUP + 5, :] = sums_top[0:2, :]


def cls_rows_kernel(where, *refs):
    packs = refs[:4]
    heads, branch, low, second = refs[4:8]
    out, kept = refs[8:]
    plane_at = where[1]
    for mask, pack in enumerate(packs):
        kept[plane_at ^ mask] = pack[...]
    starts = (MODEL, 2 * MODEL, 3 * MODEL, 4 * MODEL)
    out[:, 0:MODEL] = heads[:, :MODEL].astype(LOW)
    for piece, start in enumerate(starts):
        from_at = piece * SPAN
        for tile in range(MODEL // LANES):
            total = None
            for at in range(PLANE):
                inner = tile - TILE_START[at]
                if inner in (0, 1):
                    first = from_at + inner * LANES
                    value = kept[at, :, first : first + LANES]
                    total = value if total is None else total + value
            out[:, start + tile * LANES : start + (tile + 1) * LANES] = total
    out[:, 5 * MODEL : 6 * MODEL] = branch[...]
    out[:, 6 * MODEL : 7 * MODEL] = low[...]
    out[:, 7 * MODEL + FF : 8 * MODEL + FF] = second[...]
    part = FF // PLANE
    for at in range(PLANE):
        first = 4 * SPAN
        out[:, 7 * MODEL + at * part : 7 * MODEL + (at + 1) * part] = kept[
            at, :, first : first + part
        ]
        out[:, 8 * MODEL + FF + at * part : 8 * MODEL + FF + (at + 1) * part] = kept[
            at, :, first + part : first + 2 * part
        ]


def own_features(rank, width):
    shape = (MODEL, width)
    feature = lax.broadcasted_iota(jnp.int32, shape, 0)
    column = lax.broadcasted_iota(jnp.int32, shape, 1)
    return (feature == rank * width + column).astype(LOW)


def cls_owner_kernel(where, *refs):
    own, got, mats_out, vecs_out, rows = refs
    rank = where[0] * PLANE + where[1]
    width = mats_out.shape[0]
    rows[:GROUP] = own[...]
    rows[GROUP:] = got[...]
    chosen = own_features(rank, width)
    plan = (
        (0, MODEL, 3 * MODEL, 0),
        (4 * MODEL, 5 * MODEL, MODEL, 3 * MODEL),
        (6 * MODEL, 7 * MODEL, FF, 4 * MODEL),
        (7 * MODEL + FF, 8 * MODEL + FF, FF, 4 * MODEL + FF),
    )
    for left, right, size, target in plan:
        side = product_plain(rows[:, left : left + MODEL], chosen).astype(LOW)
        mats_out[:, target : target + size] = product_left(side, rows[:, right : right + size])
    vecs_out[...] = jnp.zeros_like(vecs_out)
    for at, start in ((0, MODEL), (1, 3 * MODEL), (2, 5 * MODEL), (3, 7 * MODEL + FF)):
        vecs_out[at : at + 1, :] = column_sum(rows[:, start : start + MODEL])
    for at in range(FF // MODEL):
        start = 7 * MODEL + at * MODEL
        vecs_out[8 + at : 9 + at, :] = column_sum(rows[:, start : start + MODEL])


def seg_owner_kernel(where, *refs):
    attn, attn_got, mlp, mlp_got = refs[:4]
    own_rows, got_rows = refs[4:6]
    mats_out, vecs_out, rows = refs[6:]
    core_at = where[2]
    rank = where[0] * PLANE + where[1]
    width = mats_out.shape[0]
    rows[:GROUP] = own_rows[...]
    rows[GROUP:] = got_rows[...]
    chosen = own_features(rank, width)
    qkv_half, out_half, half = 3 * MODEL // CORES, MODEL // CORES, FF // CORES
    own_at, got_at = core_at, 1 - core_at

    def put(base, size, own, got):
        mats_out[:, pl.ds(pl.multiple_of(base + own_at * size, LANES), size)] = own
        mats_out[:, pl.ds(pl.multiple_of(base + got_at * size, LANES), size)] = got

    put(0, qkv_half, attn[:, :qkv_half], attn_got[:, :qkv_half])
    put(3 * MODEL, out_half, attn[:, qkv_half:], attn_got[:, qkv_half:])
    put(4 * MODEL, half, mlp[:, :half], mlp_got[:, :half])
    put(4 * MODEL + FF, half, mlp[:, half:], mlp_got[:, half:])
    for left, right, target in (
        (0, 2 * MODEL, 4 * MODEL),
        (MODEL, 2 * MODEL + FF, 4 * MODEL + FF),
    ):
        side = product_plain(rows[:, left : left + MODEL], chosen).astype(LOW)
        mats_out[:, target : target + FF] = mats_out[:, target : target + FF] + product_left(
            side, rows[:, right : right + FF]
        )
    base = 2 * MODEL + 2 * FF
    for at in range(8 + FF // MODEL):
        start = base + at * MODEL
        vecs_out[at : at + 1, :] = column_sum(rows[:, start : start + MODEL])


def plane_parts(part):
    return (part,) + tuple(in_plane(part, mask) for mask in range(1, PLANE))


def weight_blocks(piece):
    line = jnp.stack([piece] + [along_line(piece, apart) for apart in range(1, LINE)])
    half = LINE // 2
    from_x, from_y = in_plane(line, 1), in_plane(line, 2)
    far_low, far_high = in_plane(from_x[:half], 2), in_plane(from_y[half:], 1)
    own = (line, from_x, from_y, far_low, far_high)
    return own + tuple(other_core(block) for block in own)


def slice_local(
    hidden_in,
    targets,
    doc_ids,
    seg_nums,
    valid_flags,
    seg_mats,
    seg_vecs,
    cls_mats,
    cls_vecs,
    seg_pos,
):
    rank, core_at = lax.axis_index("fsdp"), lax.axis_index("rep")
    line_at, plane_at = rank // PLANE, rank % PLANE
    where = jnp.stack([line_at, plane_at, core_at, doc_ids[0], seg_nums[0]]).astype(jnp.int32)
    own_rows, total_columns = seg_mats.shape
    half_rows = own_rows // CORES
    vec_size = seg_vecs.shape[0]
    vec_lines = -(-vec_size // LANES)
    live = valid_flags.astype(WIDE)
    live_row, live_column = live[None, :], live[:, None]

    pad = vec_lines * LANES - vec_size
    vec_block = jnp.stack([jnp.pad(seg_vecs, (0, pad)), jnp.pad(cls_vecs, (0, pad))])
    vec_block = vec_block.reshape(2 * vec_lines, LANES)
    count_row = jnp.full((1, LANES), jnp.sum(live), WIDE).astype(LOW)
    blank = jnp.zeros((half_rows - 2 * vec_lines - 1, LANES), LOW)
    vec_block = jnp.concatenate([vec_block, count_row, blank])
    qkv_columns, up_columns, down_columns = 3 * MODEL + LANES, MODEL + FF, FF + MODEL
    quarter = 3 * SPAN + 2 * FF // PLANE
    first_piece, second_piece, third_piece, quarters = run_kernel(
        prepare_kernel,
        "prepare",
        [
            shape_of((half_rows, qkv_columns), LOW),
            shape_of((half_rows, up_columns), LOW),
            shape_of((half_rows, down_columns), LOW),
            shape_of((PLANE, half_rows, quarter), LOW),
        ],
        where,
        (),
        (
            seg_mats.reshape(CORES, half_rows, total_columns),
            cls_mats.reshape(CORES, half_rows, total_columns),
            vec_block,
        ),
        [pltpu.VMEM((PLANE, half_rows, quarter), LOW)],
    )
    qkv_blocks = weight_blocks(first_piece)
    up_blocks = weight_blocks(second_piece)
    down_blocks = weight_blocks(third_piece)
    own_plane = jnp.stack(
        [quarters[0]] + [in_plane(quarters[mask], mask) for mask in range(1, PLANE)]
    )
    cls_line = (own_plane,) + tuple(along_line(own_plane, apart) for apart in range(1, LINE))
    cls_line = cls_line + tuple(other_core(block) for block in cls_line)

    qkv, both, vectors, count = run_kernel(
        qkv_kernel,
        "seg_qkv",
        [
            shape_of((SEG, 3 * MODEL), LOW),
            shape_of((SEG, 2 * MODEL), LOW),
            shape_of((2 * (8 * MODEL + FF) // MODEL, MODEL)),
            shape_of((8, LANES)),
        ],
        where,
        qkv_blocks,
        (hidden_in, live_row),
        weight_scratch(half_rows, qkv_columns) + [pltpu.VMEM((2, 8 * MODEL + FF), WIDE)],
        flops=2 * SEG * MODEL * 3 * MODEL,
    )
    both_got = other_core(both)
    normed_first, inv_first, slope, act, first_send = run_kernel(
        up_kernel,
        "seg_up",
        [
            shape_of((SEG, MODEL)),
            shape_of((SEG, 1)),
            shape_of((SEG, FF)),
            shape_of((SEG, FF), LOW),
            shape_of((SEG, MODEL + FF // CORES), LOW),
        ],
        where,
        up_blocks,
        (hidden_in, both, vectors),
        weight_scratch(half_rows, up_columns),
        flops=2 * SEG * MODEL * up_columns,
    )
    first_got = other_core(first_send)
    normed_second, inv_second, diff, out_rows, head_row, cls_out = run_kernel(
        down_kernel,
        "seg_down",
        [
            shape_of((SEG, MODEL)),
            shape_of((SEG, 1)),
            shape_of((SEG, MODEL)),
            shape_of((SEG, MODEL)),
            shape_of((1, 2 * MODEL + LANES)),
            shape_of((4, HEAD_DIM, MODEL), LOW),
        ],
        where,
        down_blocks,
        (act, normed_first, vectors, targets, live_column, seg_pos),
        weight_scratch(half_rows, down_columns),
        flops=2 * SEG * MODEL * FF,
    )
    cls_out = cls_out.reshape(SPAN, MODEL)
    cls_weight = run_kernel(
        cls_weight_kernel,
        "head_weight",
        [shape_of((LINE, PLANE, CORES, half_rows, quarter), LOW)],
        where,
        cls_line,
        (),
        [pltpu.SemaphoreType.DMA((WEIGHT_COPIES,))],
    )[0].reshape(MODEL, quarter)

    head_stack = jnp.concatenate(
        [head_row] + [along_line(head_row, apart) for apart in range(1, LINE)]
    )
    heads, cls_qkv, cls_mixed, part = run_kernel(
        cls_attend_kernel,
        "head_attend",
        [
            shape_of((GROUP, 2 * MODEL + LANES)),
            shape_of((GROUP, 3 * SPAN), LOW),
            shape_of((GROUP, SPAN), LOW),
            shape_of((GROUP, MODEL)),
        ],
        where,
        (),
        plane_parts(head_stack) + (vectors, cls_weight, cls_out),
    )
    grad_first, pre, second_send, sums = run_kernel(
        mlp_back_kernel,
        "seg_mlp_back",
        [
            shape_of((SEG, MODEL)),
            shape_of((SEG, FF), LOW),
            shape_of((SEG, MODEL + FF // CORES), LOW),
            shape_of((2, FF)),
        ],
        where,
        up_blocks + down_blocks,
        (diff, count, normed_second, inv_second, vectors, slope),
        weight_scratch(half_rows, up_columns) + weight_scratch(half_rows, down_columns),
        flops=4 * SEG * MODEL * FF,
    )
    second_got = other_core(second_send)
    part_rows = LINE // 2

    def part_shapes(columns):
        return [
            shape_of((count_of, own_rows, columns), LOW)
            for count_of in (part_rows, part_rows, LINE, LINE, LINE)
        ]

    mlp_parts = run_kernel(
        mlp_weight_kernel,
        "seg_mlp_weight",
        part_shapes(FF),
        where,
        (),
        (first_send, first_got, second_send, second_got, pre, act),
        [
            pltpu.VMEM((2 * SEG, MODEL), LOW),
            pltpu.VMEM((2 * SEG, FF // CORES), LOW),
            pltpu.VMEM((GROUP, own_rows, FF), LOW),
            pltpu.SemaphoreType.DMA((GROUP,)),
        ],
        outs_far=True,
        flops=4 * SEG * MODEL * FF,
    )
    mlp_sum = reduce_parts(where, mlp_parts)

    cls_normed, cls_inv, cls_low, cls_act, cls_slope, part = run_kernel(
        cls_mlp_kernel,
        "head_mlp",
        [
            shape_of((GROUP, MODEL)),
            shape_of((GROUP, 1)),
            shape_of((GROUP, MODEL), LOW),
            shape_of((GROUP, FF // PLANE), LOW),
            shape_of((GROUP, FF // PLANE)),
            shape_of((GROUP, MODEL)),
        ],
        where,
        (),
        (heads,) + plane_parts(part) + (vectors, cls_weight),
    )
    top_row, square, cls_grad, cls_second, cls_pre, part, top_sums = run_kernel(
        cls_top_kernel,
        "head_top",
        [
            shape_of((1, MODEL)),
            shape_of((8, LANES)),
            shape_of((GROUP, MODEL)),
            shape_of((GROUP, MODEL), LOW),
            shape_of((GROUP, FF // PLANE), LOW),
            shape_of((GROUP, MODEL)),
            shape_of((2, MODEL)),
        ],
        where,
        (),
        (heads,) + plane_parts(part) + (vectors, cls_weight, cls_normed, count, cls_slope),
        [pltpu.VMEM((GROUP, MODEL), WIDE)],
    )
    cls_grad, cls_branch, cls_proj, part, back_sums = run_kernel(
        cls_attend_back_kernel,
        "head_attend_back",
        [
            shape_of((GROUP, MODEL)),
            shape_of((GROUP, MODEL), LOW),
            shape_of((GROUP, 3 * SPAN), LOW),
            shape_of((GROUP, MODEL)),
            shape_of((2, MODEL)),
        ],
        where,
        (),
        (heads,)
        + plane_parts(part)
        + (vectors, cls_weight, cls_out, cls_grad, cls_normed, cls_inv, cls_qkv),
    )
    dheads, shared = run_kernel(
        cls_end_kernel,
        "head_end",
        [shape_of((1, MODEL)), shape_of((GROUP + 8, MODEL))],
        where,
        (),
        (heads, cls_grad) + plane_parts(part) + (square, back_sums, top_sums),
        [pltpu.VMEM((GROUP, MODEL), WIDE)],
    )

    head_width = 2 * MODEL + 2 * FF + 8 * MODEL + FF
    input_grad, proj, branch, attn_send, head_data, output = run_kernel(
        seg_back_kernel,
        "seg_back",
        [
            shape_of((SEG, MODEL), LOW),
            shape_of((SEG, 3 * MODEL), LOW),
            shape_of((SEG, MODEL), LOW),
            shape_of((SEG, 2 * MODEL), LOW),
            shape_of((1, head_width), LOW),
            shape_of((SEG, MODEL), LOW),
        ],
        where,
        qkv_blocks + up_blocks + down_blocks,
        (
            dheads,
            top_row,
            grad_first,
            normed_second,
            inv_second,
            slope,
            normed_first,
            inv_first,
            first_send,
            act,
            qkv,
            vectors,
            live_row,
            sums,
            out_rows,
        ),
        weight_scratch(half_rows, qkv_columns)
        + weight_scratch(half_rows, up_columns)
        + weight_scratch(half_rows, down_columns)
        + [pltpu.VMEM((SEG, MODEL), LOW)],
        flops=4 * SEG * MODEL * 4 * MODEL,
    )
    attn_got = other_core(attn_send)
    attn_parts = run_kernel(
        attn_weight_kernel,
        "seg_attn_weight",
        part_shapes(2 * MODEL),
        where,
        (),
        (both, both_got, proj, attn_got, branch),
        [
            pltpu.VMEM((2 * SEG, 2 * MODEL), LOW),
            pltpu.VMEM((2 * SEG, 2 * MODEL), LOW),
            pltpu.VMEM((GROUP, own_rows, 2 * MODEL), LOW),
            pltpu.SemaphoreType.DMA((GROUP,)),
        ],
        outs_far=True,
        flops=4 * SEG * MODEL * 2 * MODEL,
    )
    attn_sum = reduce_parts(where, attn_parts)

    pack = jnp.concatenate([cls_proj, cls_mixed, cls_pre, cls_act], axis=1)
    row_width = 6 * MODEL + 2 * MODEL + 2 * FF
    cls_rows = run_kernel(
        cls_rows_kernel,
        "head_rows",
        [shape_of((GROUP, row_width), LOW)],
        where,
        (),
        plane_parts(pack) + (heads, cls_branch, cls_low, cls_second),
        [pltpu.VMEM((PLANE,) + pack.shape, LOW)],
    )[0]
    vec_rows = (8 * MODEL + FF) // MODEL
    cls_mats_grad, cls_vec_rows = run_kernel(
        cls_owner_kernel,
        "head_owner",
        [shape_of((own_rows, total_columns)), shape_of((vec_rows, MODEL))],
        where,
        (),
        (cls_rows, other_core(cls_rows)),
        [pltpu.VMEM((CORES * GROUP, row_width), LOW)],
        flops=64 * own_rows * total_columns,
    )
    shared = shared + other_core(shared)
    pos_total = shared[:GROUP]
    loss_value = shared[GROUP, 0] / (count[0, 0] * MODEL)
    norm_grads = shared[GROUP + 1 : GROUP + 5]
    cls_vec_rows = jnp.concatenate([cls_vec_rows[:4], norm_grads, cls_vec_rows[8:]])

    head_line = jnp.concatenate(
        [head_data] + [along_line(head_data, apart) for apart in range(1, LINE)]
    )
    head_all = jnp.concatenate(plane_parts(head_line))
    seg_mats_grad, seg_vec_rows = run_kernel(
        seg_owner_kernel,
        "seg_owner",
        [shape_of((own_rows, total_columns)), shape_of((vec_rows, MODEL))],
        where,
        (),
        (attn_sum, other_core(attn_sum), mlp_sum, other_core(mlp_sum))
        + (head_all, other_core(head_all)),
        [pltpu.VMEM((CORES * GROUP, head_width), LOW)],
        flops=64 * own_rows * total_columns,
    )

    def own_vector(rows):
        return lax.dynamic_index_in_dim(rows.reshape(GROUP, vec_size), rank, 0, keepdims=False)

    return (
        output,
        input_grad,
        seg_mats_grad,
        own_vector(seg_vec_rows),
        cls_mats_grad,
        own_vector(cls_vec_rows),
        pos_total,
        loss_value,
    )


def solution(mesh):
    in_specs = (
        P(("rep", "fsdp"), None),
        P(("rep", "fsdp"), None),
        P(("rep", "fsdp")),
        P(("rep", "fsdp")),
        P(("rep", "fsdp")),
        P("fsdp", None),
        P("fsdp"),
        P("fsdp", None),
        P("fsdp"),
        P(),
    )
    out_specs = (
        P(("rep", "fsdp"), None),
        P(("rep", "fsdp"), None),
        P("fsdp", None),
        P("fsdp"),
        P("fsdp", None),
        P("fsdp"),
        P(),
        P(),
    )
    one_slice = dict(mesh.shape) == {"rep": CORES, "fsdp": LINE * PLANE}
    body = slice_local if one_slice else local
    return jax.shard_map(body, mesh=mesh, in_specs=in_specs, out_specs=out_specs, check_vma=False)
```

```python
import math

import jax
import jax.numpy as jnp
from jax import lax
from jax.experimental import pallas as pl
from jax.experimental.pallas import tpu as pltpu
from jax.sharding import PartitionSpec as P

HEADS = 12
HEAD_DIM = 64
FF = 3072
SEG = 128
SEQ = 2048


NORM_EPS = 1e-05
MASK_FILL = -1e30
SQRT_HALF = 0.7071067811865476
INV_SQRT_TWO_PI = 0.3989422804014327


def swapped(value, axis, apart):
    mask = 2**apart
    pairs = [(source, source ^ mask) for source in range(lax.axis_size(axis))]
    return lax.ppermute(value, axis, pairs)


def product_plain(left_side, right_side):
    return jnp.dot(left_side, right_side, preferred_element_type=jnp.float32)


def product_left(left_side, right_side):
    return lax.dot_general(
        left_side, right_side, (((0,), (0,)), ((), ())), preferred_element_type=jnp.float32
    )


def product_right(left_side, right_side):
    return lax.dot_general(
        left_side, right_side, (((1,), (1,)), ((), ())), preferred_element_type=jnp.float32
    )


def row_total(array_in):
    return jnp.sum(array_in.astype(jnp.float32), axis=0)


def unpack_weights(gathered, model_width, ff_width):
    matrix, vector = gathered
    vector = vector.astype(jnp.float32)
    pieces = tuple(
        (vector[offset * model_width : (offset + 1) * model_width] for offset in range(8))
    )
    return (
        (
            matrix[:, : 3 * model_width],
            matrix[:, 3 * model_width : 4 * model_width],
            matrix[:, 4 * model_width : 4 * model_width + ff_width],
            matrix[:, 4 * model_width + ff_width :],
        )
        + pieces
        + (vector[8 * model_width :],)
    )


def norm_forward(summed, gain_vec, shift_vec):
    row_mean = jnp.mean(summed, axis=-1, keepdims=True)
    centered = summed - row_mean
    inv_dev = lax.rsqrt(jnp.mean(centered * centered, axis=-1, keepdims=True) + NORM_EPS)
    normed = centered * inv_dev
    return (normed * gain_vec + shift_vec, normed, inv_dev)


def norm_backward(grad_out, normed, inv_dev, gain_vec):
    scaled = grad_out * gain_vec
    mean_one = jnp.mean(scaled, axis=-1, keepdims=True)
    mean_two = jnp.mean(scaled * normed, axis=-1, keepdims=True)
    grad_in = inv_dev * (scaled - mean_one - normed * mean_two)
    return (grad_in, jnp.sum(grad_out * normed, axis=0), jnp.sum(grad_out, axis=0))


def gelu_value(before):
    return 0.5 * before * (1.0 + lax.erf(before * SQRT_HALF))


def gelu_slope(before):
    return (
        0.5 * (1.0 + lax.erf(before * SQRT_HALF))
        + before * jnp.exp(-0.5 * before * before) * INV_SQRT_TWO_PI
    )


def attention_scores(queries, keys_in, allowed, score_scale):
    raw_scores = (
        jnp.einsum("bqhe,bkhe->bhqk", queries, keys_in, preferred_element_type=jnp.float32)
        * score_scale
    )
    return jnp.where(allowed, raw_scores, MASK_FILL)


def attention_forward(queries, keys_in, values, allowed, score_scale):
    scores = attention_scores(queries, keys_in, allowed, score_scale)
    row_top = jnp.max(scores, axis=-1, keepdims=True)
    log_total = row_top + jnp.log(jnp.sum(jnp.exp(scores - row_top), axis=-1, keepdims=True))
    weights = jnp.exp(scores - log_total).astype(jnp.bfloat16)
    mixed_rows = jnp.einsum("bhqk,bkhe->bqhe", weights, values, preferred_element_type=jnp.float32)
    return (mixed_rows, log_total)


def attention_backward(queries, keys_in, values, allowed, score_scale, log_total, grad_mixed):
    probabilities = jnp.exp(attention_scores(queries, keys_in, allowed, score_scale) - log_total)
    grad_probs = jnp.einsum(
        "bqhe,bkhe->bhqk", grad_mixed, values, preferred_element_type=jnp.float32
    )
    inner_sum = jnp.sum(grad_probs * probabilities, axis=-1, keepdims=True)
    grad_scores = (probabilities * (grad_probs - inner_sum)).astype(jnp.bfloat16)
    grad_query = (
        jnp.einsum("bhqk,bkhe->bqhe", grad_scores, keys_in, preferred_element_type=jnp.float32)
        * score_scale
    )
    grad_key = (
        jnp.einsum("bhqk,bqhe->bkhe", grad_scores, queries, preferred_element_type=jnp.float32)
        * score_scale
    )
    grad_value = jnp.einsum(
        "bhqk,bqhe->bkhe",
        probabilities.astype(jnp.bfloat16),
        grad_mixed,
        preferred_element_type=jnp.float32,
    )
    return (grad_query, grad_key, grad_value)


def block_forward(rows_in, unpacked, attend):
    (
        qkv_weight,
        out_weight,
        up_weight,
        down_weight,
        query_bias,
        value_bias,
        out_bias,
        down_bias,
        gain_first,
        shift_first,
        gain_second,
        shift_second,
        up_bias,
    ) = unpacked
    model_width = rows_in.shape[1]
    inputs = rows_in.astype(jnp.bfloat16)
    projected = product_plain(inputs, qkv_weight)
    queries = (projected[:, :model_width] + query_bias).astype(jnp.bfloat16)
    keys_in = projected[:, model_width : 2 * model_width].astype(jnp.bfloat16)
    values = (projected[:, 2 * model_width :] + value_bias).astype(jnp.bfloat16)
    mixed_rows, attend_kept = attend(queries, keys_in, values)
    mixed_rows = mixed_rows.astype(jnp.bfloat16)
    summed_first = rows_in + product_plain(mixed_rows, out_weight) + out_bias
    first_out, normed_first, inv_first = norm_forward(summed_first, gain_first, shift_first)
    first_low = first_out.astype(jnp.bfloat16)
    pre_act = product_plain(first_low, up_weight) + up_bias
    activated = gelu_value(pre_act).astype(jnp.bfloat16)
    summed_second = first_out + product_right(activated, down_weight) + down_bias
    block_out, normed_second, inv_second = norm_forward(summed_second, gain_second, shift_second)
    saved_state = (
        inputs,
        queries,
        keys_in,
        values,
        attend_kept,
        mixed_rows,
        normed_first,
        inv_first,
        first_low,
        pre_act,
        activated,
        normed_second,
        inv_second,
    )
    return (block_out, saved_state)


def block_backward(grad_out, unpacked, saved_state, attend_back):
    (
        qkv_weight,
        out_weight,
        up_weight,
        down_weight,
        query_bias,
        value_bias,
        out_bias,
        down_bias,
        gain_first,
        shift_first,
        gain_second,
        shift_second,
        up_bias,
    ) = unpacked
    (
        inputs,
        queries,
        keys_in,
        values,
        attend_kept,
        mixed_rows,
        normed_first,
        inv_first,
        first_low,
        pre_act,
        activated,
        normed_second,
        inv_second,
    ) = saved_state
    grad_second, grad_gain_second, grad_shift_second = norm_backward(
        grad_out, normed_second, inv_second, gain_second
    )
    second_low = grad_second.astype(jnp.bfloat16)
    grad_pre = (product_plain(second_low, down_weight) * gelu_slope(pre_act)).astype(jnp.bfloat16)
    grad_first = grad_second + product_right(grad_pre, up_weight)
    grad_summed, grad_gain_first, grad_shift_first = norm_backward(
        grad_first, normed_first, inv_first, gain_first
    )
    branch_low = grad_summed.astype(jnp.bfloat16)
    grad_mixed = product_right(branch_low, out_weight).astype(jnp.bfloat16)
    grad_query, grad_key, grad_value = attend_back(
        queries, keys_in, values, attend_kept, grad_mixed
    )
    grad_proj = jnp.concatenate([grad_query, grad_key, grad_value], axis=1)
    grad_rows = grad_summed + product_right(grad_proj, qkv_weight)
    vector_grad = jnp.concatenate(
        [
            row_total(grad_query),
            row_total(grad_value),
            row_total(branch_low),
            row_total(second_low),
            grad_gain_first,
            grad_shift_first,
            grad_gain_second,
            grad_shift_second,
            row_total(grad_pre),
        ]
    )
    weight_rows = (
        inputs,
        grad_proj,
        mixed_rows,
        branch_low,
        first_low,
        grad_pre,
        second_low,
        activated,
    )
    return (grad_rows, weight_rows, vector_grad)


def weight_products(weight_rows):
    inputs, grad_proj, mixed_rows, branch_low, first_low, grad_pre, second_low, activated = (
        weight_rows
    )
    return (
        product_left(inputs, grad_proj),
        product_left(mixed_rows, branch_low),
        product_left(first_low, grad_pre),
        product_left(second_low, activated),
    )


def local(
    hidden_in,
    targets,
    doc_ids,
    seg_nums,
    valid_flags,
    seg_mats,
    seg_vecs,
    cls_mats,
    cls_vecs,
    seg_pos,
):
    tok_rows, model_width = hidden_in.shape
    ff_width = FF
    seg_len = SEG
    group_span = SEQ // tok_rows
    seg_count = tok_rows // seg_len
    score_scale = HEAD_DIM ** (-0.5)
    head_shape = (HEADS, HEAD_DIM)
    live_rows = valid_flags.astype(jnp.float32)
    rank_full = lax.axis_index("fsdp")
    seg_gathered = (
        lax.all_gather(seg_mats, "fsdp", axis=0, tiled=True),
        lax.all_gather(seg_vecs, "fsdp", axis=0, tiled=True),
    )
    seg_unpacked = unpack_weights(seg_gathered, model_width, ff_width)
    cls_gathered = (
        lax.all_gather(cls_mats, "fsdp", axis=0, tiled=True),
        lax.all_gather(cls_vecs, "fsdp", axis=0, tiled=True),
    )
    cls_unpacked = unpack_weights(cls_gathered, model_width, ff_width)
    seg_allowed = (live_rows.reshape(seg_count, 1, 1, seg_len) > 0.5) | jnp.eye(seg_len, dtype=bool)
    seg_shape = (seg_count, seg_len) + head_shape

    def seg_attend(queries, keys_in, values):
        mixed_rows, log_total = attention_forward(
            queries.reshape(seg_shape),
            keys_in.reshape(seg_shape),
            values.reshape(seg_shape),
            seg_allowed,
            score_scale,
        )
        return (mixed_rows.reshape(tok_rows, model_width), log_total)

    def seg_attend_back(queries, keys_in, values, log_total, grad_mixed):
        grad_parts = attention_backward(
            queries.reshape(seg_shape),
            keys_in.reshape(seg_shape),
            values.reshape(seg_shape),
            seg_allowed,
            score_scale,
            log_total,
            grad_mixed.reshape(seg_shape),
        )
        return tuple(
            (
                grad_part.reshape(tok_rows, model_width).astype(jnp.bfloat16)
                for grad_part in grad_parts
            )
        )

    first_out, seg_saved = block_forward(hidden_in.astype(jnp.float32), seg_unpacked, seg_attend)
    first_grid = first_out.reshape(seg_count, seg_len, model_width)
    position_hot = (seg_nums[:, None] == jnp.arange(seg_pos.shape[0])[None, :]).astype(jnp.float32)
    position_rows = jnp.sum(
        position_hot[:, :, None] * seg_pos.astype(jnp.float32)[None, :, :], axis=1
    )
    heads_in = first_grid[:, 0, :] + position_rows
    lead_live = live_rows.reshape(seg_count, seg_len)[:, 0]
    lead_doc = doc_ids.reshape(seg_count, seg_len)[:, 0]
    lead_labels = jnp.where(lead_live > 0.5, lead_doc, -1).astype(jnp.bfloat16)
    lead_doc_low = lead_doc.astype(jnp.bfloat16)
    bit_count = group_span.bit_length() - 1
    key_total = group_span * seg_count
    own_slot = rank_full % group_span * seg_count + jnp.arange(seg_count)
    query_shape = (1, seg_count) + head_shape
    key_shape = (1, key_total) + head_shape

    def cls_attend(queries, keys_in, values):
        paired = jnp.concatenate([keys_in, values], axis=1)
        labels = lead_labels
        for bit_level in range(bit_count):
            other_pair, other_labels = swapped((paired, labels), "fsdp", bit_level)
            upper_half = rank_full // (1 << bit_level) % 2 == 1
            paired = jnp.where(
                upper_half,
                jnp.concatenate([other_pair, paired]),
                jnp.concatenate([paired, other_pair]),
            )
            labels = jnp.where(
                upper_half,
                jnp.concatenate([other_labels, labels]),
                jnp.concatenate([labels, other_labels]),
            )
        allowed = (labels[None, :] == lead_doc_low[:, None]) | (
            jnp.arange(key_total)[None, :] == own_slot[:, None]
        )
        allowed = allowed[None, None]
        mixed_rows, log_total = attention_forward(
            queries.reshape(query_shape),
            paired[:, :model_width].reshape(key_shape),
            paired[:, model_width:].reshape(key_shape),
            allowed,
            score_scale,
        )
        return (mixed_rows.reshape(seg_count, model_width), (paired, allowed, log_total))

    def cls_attend_back(queries, keys_in, values, attend_kept, grad_mixed):
        paired, allowed, log_total = attend_kept
        grad_query, grad_key, grad_value = attention_backward(
            queries.reshape(query_shape),
            paired[:, :model_width].reshape(key_shape),
            paired[:, model_width:].reshape(key_shape),
            allowed,
            score_scale,
            log_total,
            grad_mixed.reshape(query_shape),
        )
        grad_pair = jnp.concatenate(
            [grad_key.reshape(key_total, model_width), grad_value.reshape(key_total, model_width)],
            axis=1,
        )
        for bit_level in reversed(range(bit_count)):
            half_rows = grad_pair.shape[0] // 2
            upper_half = rank_full // (1 << bit_level) % 2 == 1
            kept_half = jnp.where(upper_half, grad_pair[half_rows:], grad_pair[:half_rows])
            sent_half = jnp.where(upper_half, grad_pair[:half_rows], grad_pair[half_rows:])
            grad_pair = kept_half + swapped(
                sent_half.astype(jnp.bfloat16), "fsdp", bit_level
            ).astype(sent_half.dtype)
        grad_pair = grad_pair.astype(jnp.bfloat16)
        return (
            grad_query.reshape(seg_count, model_width).astype(jnp.bfloat16),
            grad_pair[:, :model_width],
            grad_pair[:, model_width:],
        )

    top_out, cls_saved = block_forward(heads_in, cls_unpacked, cls_attend)
    combined = jnp.concatenate([top_out[:, None, :], first_grid[:, 1:, :]], axis=1).reshape(
        tok_rows, model_width
    )
    output_rows = combined * live_rows[:, None]
    diff_rows = (output_rows - targets.astype(jnp.float32)) * live_rows[:, None]
    count_all, square_all = lax.psum(
        (jnp.sum(live_rows), jnp.sum(diff_rows * diff_rows)), ("rep", "fsdp")
    )
    loss_value = square_all / (count_all * model_width)
    slots_all = tok_rows * lax.axis_size("rep") * lax.axis_size("fsdp")
    grad_grid = (diff_rows * (slots_all / count_all)).reshape(seg_count, seg_len, model_width)
    cls_back = unpack_weights(
        (
            lax.all_gather(cls_mats, "fsdp", axis=0, tiled=True),
            lax.all_gather(cls_vecs, "fsdp", axis=0, tiled=True),
        ),
        model_width,
        ff_width,
    )
    heads_grad, cls_weight_rows, cls_g_vec = block_backward(
        grad_grid[:, 0, :], cls_back, cls_saved, cls_attend_back
    )
    cls_g_qkv, cls_g_out, cls_g_up, cls_g_down = weight_products(cls_weight_rows)
    pos_local = jnp.sum(position_hot[:, :, None] * heads_grad[:, None, :], axis=0)
    seg_grad_out = jnp.concatenate([heads_grad[:, None, :], grad_grid[:, 1:, :]], axis=1).reshape(
        tok_rows, model_width
    )
    seg_back = unpack_weights(
        (
            lax.all_gather(seg_mats, "fsdp", axis=0, tiled=True),
            lax.all_gather(seg_vecs, "fsdp", axis=0, tiled=True),
        ),
        model_width,
        ff_width,
    )
    input_grad, seg_weight_rows, seg_g_vec = block_backward(
        seg_grad_out, seg_back, seg_saved, seg_attend_back
    )
    seg_g_qkv, seg_g_out, seg_g_up, seg_g_down = weight_products(seg_weight_rows)
    owner_rows = tuple(
        (
            lax.psum_scatter(seg_g_qkv, "fsdp", scatter_dimension=0, tiled=True),
            lax.psum_scatter(seg_g_out, "fsdp", scatter_dimension=0, tiled=True),
            lax.psum_scatter(seg_g_up, "fsdp", scatter_dimension=0, tiled=True),
            lax.psum_scatter(seg_g_down, "fsdp", scatter_dimension=0, tiled=True),
            lax.psum_scatter(seg_g_vec, "fsdp", scatter_dimension=0, tiled=True),
            lax.psum_scatter(cls_g_qkv, "fsdp", scatter_dimension=0, tiled=True),
            lax.psum_scatter(cls_g_out, "fsdp", scatter_dimension=0, tiled=True),
            lax.psum_scatter(cls_g_up, "fsdp", scatter_dimension=0, tiled=True),
            lax.psum_scatter(cls_g_down, "fsdp", scatter_dimension=0, tiled=True),
            lax.psum_scatter(cls_g_vec, "fsdp", scatter_dimension=0, tiled=True),
        )
    )
    replica_share = (
        lax.psum_scatter(
            owner_rows[0].astype(jnp.bfloat16), "rep", scatter_dimension=1, tiled=True
        ).astype(jnp.float32),
        lax.psum_scatter(
            owner_rows[1].astype(jnp.bfloat16), "rep", scatter_dimension=1, tiled=True
        ).astype(jnp.float32),
        lax.psum_scatter(
            owner_rows[2].astype(jnp.bfloat16), "rep", scatter_dimension=1, tiled=True
        ).astype(jnp.float32),
        lax.psum_scatter(
            owner_rows[3].astype(jnp.bfloat16), "rep", scatter_dimension=1, tiled=True
        ).astype(jnp.float32),
        lax.psum_scatter(
            owner_rows[4].astype(jnp.bfloat16), "rep", scatter_dimension=0, tiled=True
        ).astype(jnp.float32),
        lax.psum_scatter(
            owner_rows[5].astype(jnp.bfloat16), "rep", scatter_dimension=1, tiled=True
        ).astype(jnp.float32),
        lax.psum_scatter(
            owner_rows[6].astype(jnp.bfloat16), "rep", scatter_dimension=1, tiled=True
        ).astype(jnp.float32),
        lax.psum_scatter(
            owner_rows[7].astype(jnp.bfloat16), "rep", scatter_dimension=1, tiled=True
        ).astype(jnp.float32),
        lax.psum_scatter(
            owner_rows[8].astype(jnp.bfloat16), "rep", scatter_dimension=1, tiled=True
        ).astype(jnp.float32),
        lax.psum_scatter(
            owner_rows[9].astype(jnp.bfloat16), "rep", scatter_dimension=0, tiled=True
        ).astype(jnp.float32),
    )
    all_summed = (
        lax.all_gather(replica_share[0].astype(jnp.bfloat16), "rep", axis=1, tiled=True).astype(
            jnp.float32
        ),
        lax.all_gather(replica_share[1].astype(jnp.bfloat16), "rep", axis=1, tiled=True).astype(
            jnp.float32
        ),
        lax.all_gather(replica_share[2].astype(jnp.bfloat16), "rep", axis=1, tiled=True).astype(
            jnp.float32
        ),
        lax.all_gather(replica_share[3].astype(jnp.bfloat16), "rep", axis=1, tiled=True).astype(
            jnp.float32
        ),
        lax.all_gather(replica_share[4].astype(jnp.bfloat16), "rep", axis=0, tiled=True).astype(
            jnp.float32
        ),
        lax.all_gather(replica_share[5].astype(jnp.bfloat16), "rep", axis=1, tiled=True).astype(
            jnp.float32
        ),
        lax.all_gather(replica_share[6].astype(jnp.bfloat16), "rep", axis=1, tiled=True).astype(
            jnp.float32
        ),
        lax.all_gather(replica_share[7].astype(jnp.bfloat16), "rep", axis=1, tiled=True).astype(
            jnp.float32
        ),
        lax.all_gather(replica_share[8].astype(jnp.bfloat16), "rep", axis=1, tiled=True).astype(
            jnp.float32
        ),
        lax.all_gather(replica_share[9].astype(jnp.bfloat16), "rep", axis=0, tiled=True).astype(
            jnp.float32
        ),
    )
    seg_summed = all_summed[:5]
    cls_summed = all_summed[5:]
    pos_total = lax.psum(pos_local, ("rep", "fsdp"))
    seg_mat_grad = jnp.concatenate(
        [seg_summed[0], seg_summed[1], seg_summed[2], seg_summed[3]], axis=1
    )
    cls_mat_grad = jnp.concatenate(
        [cls_summed[0], cls_summed[1], cls_summed[2], cls_summed[3]], axis=1
    )
    return (
        output_rows.astype(jnp.bfloat16),
        input_grad.astype(jnp.bfloat16),
        seg_mat_grad,
        seg_summed[4],
        cls_mat_grad,
        cls_summed[4],
        pos_total,
        loss_value,
    )


LINE = 4
PLANE = 4
CORES = 2
LANES = 128
GROUP = LINE * PLANE
LOW, WIDE = jnp.bfloat16, jnp.float32
MODEL = HEADS * HEAD_DIM
SPAN = 2 * LANES
TILE_START = (0, 1, 3, 4)


def line_pairs(apart):
    return [(source, (source + apart * PLANE) % GROUP) for source in range(GROUP)]


def plane_pairs(mask):
    return [(source, source ^ mask) for source in range(GROUP)]


def along_line(value, apart):
    return lax.ppermute(value, "fsdp", line_pairs(apart))


def in_plane(value, mask):
    return lax.ppermute(value, "fsdp", plane_pairs(mask))


def other_core(value):
    return lax.ppermute(value, "rep", [(0, 1), (1, 0)])


def after(value, *events):
    return lax.optimization_barrier((value,) + events)[0]


def shape_of(dims, dtype=WIDE):
    return jax.ShapeDtypeStruct(dims, dtype)


def run_kernel(body, name, outs, where, blocks, arrays, scratch=(), outs_far=False, flops=0):
    in_specs = [pl.BlockSpec(memory_space=pltpu.SMEM)]
    in_specs += [pl.BlockSpec(memory_space=pl.ANY)] * len(blocks)
    in_specs += [pl.BlockSpec(memory_space=pltpu.VMEM)] * len(arrays)
    out_space = pl.ANY if outs_far else pltpu.VMEM
    moved = sum(x.size * x.dtype.itemsize for x in list(blocks) + list(arrays))
    moved += sum(math.prod(o.shape) * jnp.dtype(o.dtype).itemsize for o in outs)
    return pl.pallas_call(
        body,
        name=name,
        out_shape=tuple(outs),
        in_specs=in_specs,
        out_specs=tuple(pl.BlockSpec(memory_space=out_space) for _ in outs),
        scratch_shapes=list(scratch),
        cost_estimate=pl.CostEstimate(flops=flops, bytes_accessed=moved, transcendentals=0),
        compiler_params=pltpu.CompilerParams(vmem_limit_bytes=VMEM_BYTES),
    )(where, *blocks, *arrays)


VMEM_BYTES = 24 * 1024 * 1024
HALF = MODEL // CORES
FF_HALF = FF // CORES
OWN = MODEL // GROUP
QUARTER = 3 * SPAN + 2 * FF // LINE
QUARTER_HALF = QUARTER // CORES


def aligned(start):
    return pl.multiple_of(start, LANES)


def wait_all(copies):
    for copy in copies:
        copy.wait()


def run_copies(pairs, sems):
    copies = [
        pltpu.make_async_copy(source, target, sems.at[at])
        for at, (source, target) in enumerate(pairs)
    ]
    for copy in copies:
        copy.start()
    wait_all(copies)


def gather_blocks(where, refs, base, width, targets):
    line_at, plane_at = where[0], where[1]
    half = LINE // 2
    for mask in range(PLANE):
        for step in range(LINE):
            if mask == 0:
                ref, offset = refs[step], 0
            elif mask == 3:
                ref = refs[LINE + 3] if step < half else refs[LINE + 2]
                offset = step % half * width
            else:
                ref, offset = refs[LINE + mask - 1], base + step * width
            chip = (line_at + LINE - step) % LINE * PLANE + (plane_at ^ mask)
            for whole, first, last in targets:
                whole[chip] = ref[:, offset + first : offset + last]


def whole_rows(ref):
    value = ref[...]
    return value.reshape(value.shape[0] * value.shape[1], value.shape[2])


def prepare_first_kernel(where, seg, seg_vec, cls_vec, live_row, out, sems):
    core_at = where[2]
    pairs = []
    for piece in range(4):
        source = seg.at[:, pl.ds(aligned(piece * MODEL + core_at * HALF), HALF)]
        pairs.append((source, out.at[:, piece * HALF : (piece + 1) * HALF]))
    run_copies(pairs, sems)
    size = seg_vec.shape[1]
    lines = -(-size // LANES)
    block = jnp.zeros((OWN, LANES), WIDE)
    row_at = lax.broadcasted_iota(jnp.int32, (OWN, LANES), 0)
    for which, vec in enumerate((seg_vec, cls_vec)):
        for line in range(lines):
            width = min(LANES, size - line * LANES)
            value = vec[:, line * LANES : line * LANES + width].astype(WIDE)
            if width < LANES:
                value = jnp.concatenate([value, jnp.zeros((1, LANES - width), WIDE)], axis=1)
            block = jnp.where(row_at == which * lines + line, value, block)
    count = jnp.sum(live_row[...], axis=1, keepdims=True)
    block = jnp.where(row_at == 2 * lines, count, block)
    out[:, 4 * HALF :] = block.astype(LOW)


def prepare_rest_kernel(where, seg, cls, *refs):
    second_out, third_out = refs[:2]
    step_outs, out_half = refs[2 : 2 + LINE], refs[2 + LINE]
    quarters, sems = refs[3 + LINE :]
    line_at, core_at = where[0], where[2]
    start = core_at * FF_HALF
    pairs = [
        (seg.at[:, pl.ds(aligned(4 * MODEL + start), FF_HALF)], second_out),
        (seg.at[:, pl.ds(aligned(4 * MODEL + FF + start), FF_HALF)], third_out),
        (cls.at[:, pl.ds(aligned(3 * MODEL + core_at * HALF), HALF)], out_half),
    ]
    part = FF // LINE
    for at in range(LINE):
        first = TILE_START[at] * LANES
        plan = [(piece * MODEL + first, SPAN, piece * SPAN) for piece in range(3)]
        plan += [
            (4 * MODEL + piece * FF + at * part, part, 3 * SPAN + piece * part)
            for piece in range(2)
        ]
        for source, size, target in plan:
            pairs.append(
                (
                    cls.at[:, source : source + size],
                    quarters.at[at, :, target : target + size],
                )
            )
    run_copies(pairs, sems)
    lanes = pl.ds(aligned(core_at * QUARTER_HALF), QUARTER_HALF)
    for step, out in enumerate(step_outs):
        out[...] = quarters[(line_at + step) % LINE, :, lanes]


def lane_mask(rows, head):
    lane = lax.broadcasted_iota(jnp.int32, (rows, LANES), 1)
    return (lane < HEAD_DIM) if head == 0 else (lane >= HEAD_DIM)


def masked(value, mask):
    return jnp.where(mask, value, jnp.zeros_like(value))


def head_probabilities(query, key, allowed):
    scores = product_right(query, key) * HEAD_DIM ** (-0.5)
    scores = jnp.where(allowed, scores, MASK_FILL)
    raised = jnp.exp(scores - jnp.max(scores, axis=-1, keepdims=True))
    return raised / jnp.sum(raised, axis=-1, keepdims=True)


def attend_tiles(qkv, width, allowed):
    rows = qkv.shape[0]
    mixed = []
    for tile in range(width // LANES):
        at = tile * LANES
        query, key, value = (
            qkv[:, piece * width + at : piece * width + at + LANES] for piece in range(3)
        )
        total = jnp.zeros((rows, LANES), WIDE)
        for head in range(2):
            mask = lane_mask(rows, head)
            weights = head_probabilities(masked(query, mask), key, allowed).astype(LOW)
            total = total + product_plain(weights, masked(value, mask))
        mixed.append(total.astype(LOW))
    return mixed


def attend_tiles_back(qkv, grad_mixed, width, allowed):
    rows = qkv.shape[0]
    scale = HEAD_DIM ** (-0.5)
    results = ([], [], [])
    for tile in range(width // LANES):
        at = tile * LANES
        query, key, value = (
            qkv[:, piece * width + at : piece * width + at + LANES] for piece in range(3)
        )
        grad = grad_mixed[:, at : at + LANES]
        totals = [jnp.zeros((rows, LANES), WIDE) for _ in range(3)]
        for head in range(2):
            mask = lane_mask(rows, head)
            query_low, key_low, grad_low = (masked(x, mask) for x in (query, key, grad))
            chance = head_probabilities(query_low, key, allowed)
            grad_chance = product_right(grad_low, value)
            inner = jnp.sum(grad_chance * chance, axis=-1, keepdims=True)
            grad_scores = (chance * (grad_chance - inner)).astype(LOW)
            totals[0] = totals[0] + product_plain(grad_scores, key_low)
            totals[1] = totals[1] + product_left(grad_scores, query_low)
            totals[2] = totals[2] + product_left(chance.astype(LOW), grad_low)
        results[0].append((totals[0] * scale).astype(LOW))
        results[1].append((totals[1] * scale).astype(LOW))
        results[2].append(totals[2].astype(LOW))
    return results[0] + results[1] + results[2]


def token_allowed(live_row):
    shape = (SEG, SEG)
    same = lax.broadcasted_iota(jnp.int32, shape, 0) == lax.broadcasted_iota(jnp.int32, shape, 1)
    return (live_row > 0.5) | same


def qkv_kernel(where, *refs):
    blocks = refs[:8]
    hidden, hidden_got, live_row, live_got = refs[8:12]
    weight, out_half, qkv_out, mixed_out, vectors_out, count_out = refs[12:18]
    vec_rows, flat, inputs = refs[18:]
    core_at = where[2]
    gather_blocks(
        where,
        blocks,
        0,
        4 * HALF + LANES,
        (
            (weight, 0, 3 * HALF),
            (out_half, 3 * HALF, 4 * HALF),
            (vec_rows, 4 * HALF, 4 * HALF + LANES),
        ),
    )
    piece = (8 * MODEL + FF) // GROUP
    lines = -(-piece // LANES)
    count = jnp.zeros((1, LANES), WIDE)
    for chip in range(GROUP):
        rows = vec_rows[chip, 0:16, :].astype(WIDE)
        for block in range(2):
            joined = jnp.concatenate(
                [rows[block * lines + r : block * lines + r + 1] for r in range(lines)], axis=1
            )
            flat[block : block + 1, chip * piece : (chip + 1) * piece] = joined[:, :piece]
        count = count + rows[2 * lines : 2 * lines + 1]
    rows_each = (8 * MODEL + FF) // MODEL
    for block in range(2):
        for row in range(rows_each):
            vectors_out[block * rows_each + row : block * rows_each + row + 1, :] = flat[
                block : block + 1, row * MODEL : (row + 1) * MODEL
            ]
    count_out[...] = jnp.broadcast_to(count, count_out.shape)
    inputs[:SEG] = hidden[...]
    inputs[SEG:] = hidden_got[...]
    projected = product_plain(inputs[...], whole_rows(weight))
    lanes = pl.ds(aligned(core_at * HALF), HALF)
    qkv_out[:, :HALF] = (projected[:, :HALF] + vectors_out[0:1, lanes]).astype(LOW)
    qkv_out[:, HALF : 2 * HALF] = projected[:, HALF : 2 * HALF].astype(LOW)
    qkv_out[:, 2 * HALF :] = (projected[:, 2 * HALF :] + vectors_out[1:2, lanes]).astype(LOW)
    for part, live in enumerate((live_row, live_got)):
        rows = slice(part * SEG, (part + 1) * SEG)
        tiles = attend_tiles(qkv_out[rows, :], HALF, token_allowed(live[...]))
        for tile, value in enumerate(tiles):
            mixed_out[rows, tile * LANES : (tile + 1) * LANES] = value


def norm_rows(summed):
    row_mean = jnp.mean(summed, axis=-1, keepdims=True)
    centered = summed - row_mean
    inv_dev = lax.rsqrt(jnp.mean(centered * centered, axis=-1, keepdims=True) + NORM_EPS)
    return centered * inv_dev, inv_dev


def norm_rows_back(grad_out, normed, inv_dev, gain):
    scaled = grad_out * gain
    mean_one = jnp.mean(scaled, axis=-1, keepdims=True)
    mean_two = jnp.mean(scaled * normed, axis=-1, keepdims=True)
    return inv_dev * (scaled - mean_one - normed * mean_two)


def column_sum(value):
    return jnp.sum(value.astype(WIDE), axis=0, keepdims=True)


def four_rows(vectors, first):
    return jnp.concatenate([vectors[first + at : first + at + 1, :] for at in range(4)], axis=1)


def gelu_both(before):
    half = 0.5 * (1.0 + lax.erf(before * SQRT_HALF))
    slope = half + before * jnp.exp(-0.5 * before * before) * INV_SQRT_TWO_PI
    return before * half, slope


def out_kernel(where, hidden, mixed, mixed_got, half, half_got, vectors, *outs):
    full_out, mixed_full, normed_out, inv_out, low_out = outs
    core_at = where[2]
    own, other = aligned(core_at * HALF), aligned((1 - core_at) * HALF)
    full_out[:, pl.ds(own, HALF)] = half[...]
    full_out[:, pl.ds(other, HALF)] = half_got[...]
    mixed_full[:, pl.ds(own, HALF)] = mixed[...]
    mixed_full[:SEG, pl.ds(other, HALF)] = mixed_got[SEG:, :]
    mixed_full[SEG:, pl.ds(other, HALF)] = mixed_got[:SEG, :]
    branch = product_plain(mixed_full[:SEG, :], full_out[...])
    normed, inv_dev = norm_rows(hidden[...].astype(WIDE) + branch + vectors[2:3, :])
    normed_out[...] = normed
    inv_out[...] = inv_dev
    low_out[...] = (normed * vectors[4:5, :] + vectors[5:6, :]).astype(LOW)


def up_kernel(where, *refs):
    blocks = refs[:8]
    low, low_got, vectors = refs[8:11]
    weight, act_out, slope_out, both = refs[11:]
    core_at = where[2]
    gather_blocks(where, blocks, 2 * (4 * HALF + LANES), FF_HALF, ((weight, 0, FF_HALF),))
    both[:SEG] = low[...]
    both[SEG:] = low_got[...]
    for at in range(FF_HALF // MODEL):
        columns = slice(at * MODEL, (at + 1) * MODEL)
        held = weight[:, :, columns]
        before = product_plain(both[...], held.reshape(MODEL, MODEL))
        bias = vectors[pl.ds(8 + core_at * (FF_HALF // MODEL) + at, 1), :]
        value, slope = gelu_both(before + bias)
        act_out[:, columns] = value.astype(LOW)
        slope_out[:, columns] = slope


def down_kernel(where, *refs):
    blocks, act = refs[:8], refs[8]
    weight, own_out, send_out = refs[9:]
    gather_blocks(where, blocks, 2 * FF_HALF, FF_HALF, ((weight, 0, FF_HALF),))
    partial = product_right(act[...], whole_rows(weight))
    own_out[...] = partial[:SEG]
    send_out[...] = partial[SEG:]


def seg_rows_kernel(where, *refs):
    own, got, normed_first, vectors, targets, live, seg_pos = refs[:7]
    normed_out, inv_out, diff_out, rows_out, head_out = refs[7:]
    doc, number = where[3], where[4]
    first = normed_first[...] * vectors[4:5, :] + vectors[5:6, :]
    normed, inv_dev = norm_rows(first + own[...] + got[...] + vectors[3:4, :])
    normed_out[...] = normed
    inv_out[...] = inv_dev
    rows = normed * vectors[6:7, :] + vectors[7:8, :]
    live_rows = live[...]
    target_rows = targets[...].astype(WIDE)
    output = rows * live_rows
    rows_out[...] = output
    diff = (output - target_rows) * live_rows
    row_at = lax.broadcasted_iota(jnp.int32, (SEG, 1), 0)
    diff = jnp.where(row_at > 0, diff, 0.0)
    diff_out[...] = diff
    table = seg_pos[...].astype(WIDE)
    chosen = lax.broadcasted_iota(jnp.int32, table.shape, 0) == number
    position = jnp.sum(jnp.where(chosen, table, 0.0), axis=0, keepdims=True)
    head_out[:, :MODEL] = rows[0:1, :] + position
    head_out[:, MODEL : 2 * MODEL] = target_rows[0:1, :]
    square = jnp.sum(column_sum(diff * diff), axis=1, keepdims=True)
    lane = lax.broadcasted_iota(jnp.int32, (1, LANES), 1)
    facts = jnp.where(lane == 0, live_rows[0:1, :], 0.0)
    facts = jnp.where(lane == 1, doc.astype(WIDE), facts)
    facts = jnp.where(lane == 2, number.astype(WIDE), facts)
    facts = jnp.where(lane == 3, square, facts)
    head_out[:, 2 * MODEL :] = facts


def second_norm_kernel(where, diff, count, normed, inv_dev, vectors, grad_out, low_out, sums_out):
    grad_top = diff[...] * ((SEG * GROUP * CORES) / count[0:1, 0:1])
    normed_rows = normed[...]
    grad = norm_rows_back(grad_top, normed_rows, inv_dev[...], vectors[6:7, :])
    low = grad.astype(LOW)
    grad_out[...] = grad
    low_out[...] = low
    sums_out[0:1, :] = column_sum(low)
    sums_out[1:2, :] = column_sum(grad_top * normed_rows)
    sums_out[2:3, :] = column_sum(grad_top)


def mlp_back_kernel(where, *refs):
    low, low_got, down_weight, up_weight, slope = refs[:5]
    pre_out, own_out, send_out, sums_out, both = refs[5:]
    both[:SEG] = low[...]
    both[SEG:] = low_got[...]
    for at in range(FF_HALF // MODEL):
        columns = slice(at * MODEL, (at + 1) * MODEL)
        held = down_weight[:, :, columns]
        before = product_plain(both[...], held.reshape(MODEL, MODEL))
        pre = (before * slope[:, columns]).astype(LOW)
        pre_out[:, columns] = pre
        sums_out[at : at + 1, :] = column_sum(pre)
    partial = product_right(pre_out[...], whole_rows(up_weight))
    own_out[...] = partial[:SEG]
    send_out[...] = partial[SEG:]


def scatter_parts(where, parts, outs, sems):
    line_at, plane_at = where[0], where[1]
    far_low, far_high, to_x, to_y, kept = outs
    half = LINE // 2
    copies = []
    for mask in range(PLANE):
        for step in range(LINE):
            source = parts.at[(line_at + step) % LINE * PLANE + (plane_at ^ mask)]
            if mask == 3:
                target = far_low.at[step] if step < half else far_high.at[step - half]
            else:
                target = (kept, to_x, to_y)[mask].at[step]
            copies.append(pltpu.make_async_copy(source, target, sems.at[len(copies)]))
    for copy in copies:
        copy.start()
    wait_all(copies)


def mlp_weight_kernel(where, *refs):
    first, first_got, second, second_got, pre, act = refs[:6]
    outs = refs[6:11]
    left, parts, sems = refs[11:]
    for at, (own, got, right) in enumerate(((first, first_got, pre), (second, second_got, act))):
        left[:SEG] = own[...]
        left[SEG:] = got[...]
        for piece in range(FF_HALF // MODEL):
            start = piece * MODEL
            product = product_left(left[...], right[:, start : start + MODEL]).astype(LOW)
            target = at * FF_HALF + start
            parts[:, :, target : target + MODEL] = product.reshape(GROUP, OWN, MODEL)
    scatter_parts(where, parts, outs, sems)


def attn_weight_kernel(where, *refs):
    hidden, hidden_got, mixed, proj, branch, got = refs[:6]
    outs = refs[6:11]
    left, right, parts, sems = refs[11:]
    core_at = where[2]
    left[:SEG] = hidden[...]
    left[SEG:] = hidden_got[...]
    right[:SEG] = branch[:, pl.ds(aligned(core_at * HALF), HALF)]
    right[SEG:] = got[:, HALF:]
    for piece in range(4):
        start = piece * HALF
        if piece < 3:
            product = product_left(left[...], proj[:, start : start + HALF])
        else:
            product = product_left(mixed[...], right[...])
        parts[:, :, start : start + HALF] = product.astype(LOW).reshape(GROUP, OWN, HALF)
    scatter_parts(where, parts, outs, sems)


def fold_kernel(where, kept, got_x, got_y, *refs):
    extra, own_out, sent = refs[: -LINE], refs[-LINE], refs[1 - LINE :]
    rows = kept.shape[1]
    for step in range(LINE):
        total = kept[step].astype(WIDE) + got_x[step].astype(WIDE) + got_y[step].astype(WIDE)
        if step == 0:
            own_out[...] = total
            continue
        out = sent[step - 1]
        out[:rows, :] = total.astype(LOW)
        if extra:
            out[rows:, :] = jnp.zeros_like(out[rows:, :])
            out[rows:, : extra[0].shape[1]] = extra[0][...]


def reduce_far(parts):
    return in_plane(parts[0], 2), in_plane(parts[1], 1)


def reduce_add(where, parts, far):
    shape = parts[2].shape
    return run_kernel(
        add_far_kernel,
        "add_far",
        [shape_of(shape, LOW)] * 2,
        where,
        (),
        tuple(far) + (parts[2], parts[3]),
    )


def reduce_fold(where, kept, got, *extra):
    _, rows, columns = kept.shape
    more = sum(value.shape[0] for value in extra)
    return run_kernel(
        fold_kernel,
        "fold",
        [shape_of((rows, columns))] + [shape_of((rows + more, columns), LOW)] * (LINE - 1),
        where,
        (),
        (kept,) + tuple(got) + extra,
    )


def reduce_line(own, pieces):
    total = own
    for piece in pieces:
        total = total + piece[: own.shape[0]].astype(WIDE)
    return total


def head_back_kernel(where, *refs):
    grad, grad_got, down_weight, up_weight, slope, act, low, low_got = refs[:8]
    own_out, send_out, data_out = refs[8:]
    few = 16
    row_at = lax.broadcasted_iota(jnp.int32, (few, 1), 0)

    def two_rows(first, second):
        return jnp.where(row_at == 0, first, jnp.where(row_at == 1, second, 0.0))

    second = two_rows(grad[...], grad_got[...]).astype(LOW)
    data_out[0:1, :] = low[0:1, :].astype(WIDE)
    data_out[1:2, :] = low_got[0:1, :].astype(WIDE)
    data_out[2:4, :] = second[0:2].astype(WIDE)
    partial = jnp.zeros((few, MODEL), WIDE)
    for at in range(FF_HALF // MODEL):
        columns = slice(at * MODEL, (at + 1) * MODEL)
        before = product_plain(second, down_weight[:, :, columns].reshape(MODEL, MODEL))
        slopes = two_rows(slope[0:1, columns], slope[SEG : SEG + 1, columns])
        pre = (before * slopes).astype(LOW)
        partial = partial + product_right(pre, up_weight[:, :, columns].reshape(MODEL, MODEL))
        data_out[4 + 2 * at : 6 + 2 * at, :] = pre[0:2].astype(WIDE)
        data_out[8 + 2 * at : 9 + 2 * at, :] = act[0:1, columns].astype(WIDE)
        data_out[9 + 2 * at : 10 + 2 * at, :] = act[SEG : SEG + 1, columns].astype(WIDE)
    own_out[...] = partial[0:1]
    send_out[...] = partial[1:2]


def first_norm_kernel(where, *refs):
    second_grad, own, got, head_grad, head_own, head_got = refs[:6]
    normed_rows, inv_dev, vectors, out_weight = refs[6:10]
    grad_out, branch_out, mixed_out, send_out, sums_out = refs[10:]
    core_at = where[2]
    grad_rows = second_grad[...] + own[...] + got[...]
    head = head_grad[...] + head_own[...] + head_got[...]
    row_at = lax.broadcasted_iota(jnp.int32, (SEG, 1), 0)
    grad_rows = jnp.where(row_at == 0, head, grad_rows)
    normed = normed_rows[...]
    grad = norm_rows_back(grad_rows, normed, inv_dev[...], vectors[4:5, :])
    grad_out[...] = grad
    branch = grad.astype(LOW)
    branch_out[...] = branch
    mixed_out[...] = product_right(branch, out_weight[...]).astype(LOW)
    other = pl.ds(aligned((1 - core_at) * HALF), HALF)
    send_out[:, :HALF] = mixed_out[:, other]
    send_out[:, HALF:] = branch_out[:, other]
    sums_out[0:1, :] = column_sum(branch)
    sums_out[1:2, :] = column_sum(grad_rows * normed)
    sums_out[2:3, :] = column_sum(grad_rows)


def attn_back_kernel(where, *refs):
    qkv, mixed_grad, got, live_row, live_got, weight = refs[:6]
    sums_first, sums_second, sums_up, head_top, head_normed, data = refs[6:12]
    proj_out, own_out, send_out, payload_out, rows = refs[12:]
    core_at = where[2]
    lanes = pl.ds(aligned(core_at * HALF), HALF)
    for part, live in enumerate((live_row, live_got)):
        at = slice(part * SEG, (part + 1) * SEG)
        grad = mixed_grad[:, lanes] if part == 0 else got[:, :HALF]
        pieces = attend_tiles_back(qkv[at, :], grad, HALF, token_allowed(live[...]))
        for tile, value in enumerate(pieces):
            proj_out[at, tile * LANES : (tile + 1) * LANES] = value
    partial = product_right(proj_out[...], whole_rows(weight))
    own_out[...] = partial[:SEG]
    send_out[...] = partial[SEG:]
    rows[...] = jnp.zeros_like(rows)
    rows[0:12, :] = data[0:12, :]
    rows[12:13, lanes] = column_sum(proj_out[:, :HALF])
    rows[13:14, lanes] = column_sum(proj_out[:, 2 * HALF :])
    rows[14:15, :] = sums_first[0:1, :]
    rows[15:16, :] = sums_second[0:1, :] + data[2:3, :]
    rows[16:18, :] = sums_first[1:3, :]
    rows[18:19, :] = sums_second[1:2, :] + head_top[...] * head_normed[0:1, :]
    rows[19:20, :] = sums_second[2:3, :] + head_top[...]
    for at in range(FF_HALF // MODEL):
        total = sums_up[at : at + 1, :] + data[4 + 2 * at : 5 + 2 * at, :]
        total = total + data[5 + 2 * at : 6 + 2 * at, :]
        rows[pl.ds(20 + core_at * (FF_HALF // MODEL) + at, 1), :] = total
    payload_out[...] = rows[...].astype(LOW)


def cls_gather_kernel(where, *refs):
    blocks = refs[:8]
    own_out, from_x, from_y, far_x = refs[8], refs[4], refs[5], refs[6]
    weight_out, out_rows = refs[9:]
    plane_at = where[1]
    gather_blocks(where, blocks, 0, QUARTER_HALF, ((weight_out, 0, QUARTER_HALF),))
    first = LINE * QUARTER_HALF
    out_rows[plane_at] = own_out[...]
    out_rows[plane_at ^ 1] = from_x[:, first : first + HALF]
    out_rows[plane_at ^ 2] = from_y[:, first : first + HALF]
    first = LINE // 2 * QUARTER_HALF
    out_rows[plane_at ^ 3] = far_x[:, first : first + HALF]


def cls_weight_kernel(where, own, got, out_half, out_got, weight_out, out_full):
    line_at, core_at = where[0], where[2]
    out_full[...] = jnp.zeros_like(out_full)
    for value, part, core in ((own, out_half, core_at), (got, out_got, 1 - core_at)):
        weight_out[:, :, pl.ds(aligned(core * QUARTER_HALF), QUARTER_HALF)] = value[...]
        rows = part[...].reshape(3, HEAD_DIM, HALF)
        out_full[pl.ds(line_at % 2, 3), :, pl.ds(aligned(core * HALF), HALF)] = rows


def add_far_kernel(where, far_low, far_high, to_x, to_y, x_out, y_out):
    half = LINE // 2
    x_out[:half] = to_x[:half] + far_low[...]
    x_out[half:] = to_x[half:]
    y_out[:half] = to_y[:half]
    y_out[half:] = to_y[half:] + far_high[...]


def row_from_column(column, size):
    shape = (size, size)
    same = lax.broadcasted_iota(jnp.int32, shape, 0) == lax.broadcasted_iota(jnp.int32, shape, 1)
    return jnp.sum(jnp.where(same, column, 0.0), axis=0, keepdims=True)


def head_allowed(heads):
    facts = heads[:, 2 * MODEL :]
    live, doc = facts[:, 0:1], facts[:, 1:2]
    shape = (GROUP, GROUP)
    same = lax.broadcasted_iota(jnp.int32, shape, 0) == lax.broadcasted_iota(jnp.int32, shape, 1)
    live_row, doc_row = row_from_column(live, GROUP), row_from_column(doc, GROUP)
    return ((live_row > 0.5) & (doc == doc_row)) | same


def quarter_mask(quarter):
    lane = lax.broadcasted_iota(jnp.int32, (GROUP, SPAN), 1)
    first = (quarter % 2) * HEAD_DIM
    return (lane >= first) & (lane < first + 3 * HEAD_DIM)


def quarter_piece(vectors, row, quarter):
    value = jnp.zeros((1, SPAN), WIDE)
    for at in range(LINE):
        first = TILE_START[at] * LANES
        value = jnp.where(quarter == at, vectors[row : row + 1, first : first + SPAN], value)
    return value


def cls_attend_kernel(where, *refs):
    stacks, vectors, weight, out_weight = refs[:4], refs[4], refs[5], refs[6]
    heads_out, qkv_out, mixed_out, part_out = refs[7:]
    line_at, plane_at = where[0], where[1]
    for step, stack in enumerate(stacks):
        for mask in range(PLANE):
            row = (line_at + LINE - step) % LINE * PLANE + (plane_at ^ mask)
            heads_out[pl.ds(row, 1), :] = stack[mask : mask + 1, :]
    heads = heads_out[...]
    inputs = heads[:, :MODEL].astype(LOW)
    projected = product_plain(inputs, weight[:, : 3 * SPAN])
    query = projected[:, :SPAN] + quarter_piece(vectors, 12, line_at)
    value = projected[:, 2 * SPAN :] + quarter_piece(vectors, 13, line_at)
    qkv_out[:, :SPAN] = query.astype(LOW)
    qkv_out[:, SPAN : 2 * SPAN] = projected[:, SPAN : 2 * SPAN].astype(LOW)
    qkv_out[:, 2 * SPAN :] = value.astype(LOW)
    mixed = attend_tiles(qkv_out[...], SPAN, head_allowed(heads))
    mixed = masked(jnp.concatenate(mixed, axis=1), quarter_mask(line_at))
    mixed_out[...] = mixed
    part_out[...] = product_plain(mixed, out_weight[...])


def cls_mlp_kernel(where, *refs):
    heads, own, got_one, got_two, got_three, vectors, weight = refs[:7]
    normed_out, inv_out, low_out, act_out, slope_out, part_out = refs[7:]
    line_at = where[0]
    branch = own[...] + got_one[...] + got_two[...] + got_three[...]
    normed, inv_dev = norm_rows(heads[:, :MODEL] + branch + vectors[14:15, :])
    normed_out[...] = normed
    inv_out[...] = inv_dev
    low = (normed * vectors[16:17, :] + vectors[17:18, :]).astype(LOW)
    low_out[...] = low
    part = FF // LINE
    first = 3 * SPAN
    bias = vectors[pl.ds(20 + line_at, 1), :]
    before = product_plain(low, weight[:, first : first + part]) + bias
    value, slope = gelu_both(before)
    act = value.astype(LOW)
    act_out[...] = act
    slope_out[...] = slope
    part_out[...] = product_right(act, weight[:, first + part :])


def cls_top_kernel(where, *refs):
    heads, own, got_one, got_two, got_three, vectors, weight = refs[:7]
    normed_first, count, slope = refs[7:10]
    top_out, square_out, grad_out, second_out, pre_out, part_out, sums_out = refs[10:17]
    held = refs[17]
    rank = where[0] * PLANE + where[1]
    first = normed_first[...] * vectors[16:17, :] + vectors[17:18, :]
    down = own[...] + got_one[...] + got_two[...] + got_three[...]
    normed, inv_dev = norm_rows(first + down + vectors[15:16, :])
    rows = normed * vectors[18:19, :] + vectors[19:20, :]
    held[...] = rows
    top_out[...] = held[pl.ds(rank, 1), :]
    facts = heads[:, 2 * MODEL :]
    live = facts[:, 0:1]
    diff = (rows * live - heads[:, MODEL : 2 * MODEL]) * live
    square = jnp.sum(column_sum(diff * diff), axis=1, keepdims=True)
    square = square + jnp.sum(facts[:, 3:4], axis=0, keepdims=True)
    square_out[...] = jnp.broadcast_to(square, square_out.shape)
    grad_top = diff * ((SEG * GROUP * CORES) / count[0:1, 0:1])
    grad = norm_rows_back(grad_top, normed, inv_dev, vectors[18:19, :])
    sums_out[0:1, :] = column_sum(grad_top * normed)
    sums_out[1:2, :] = column_sum(grad_top)
    grad_out[...] = grad
    second = grad.astype(LOW)
    second_out[...] = second
    part = FF // LINE
    at = 3 * SPAN
    pre = (product_plain(second, weight[:, at + part :]) * slope[...]).astype(LOW)
    pre_out[...] = pre
    part_out[...] = product_right(pre, weight[:, at : at + part])


def cls_attend_back_kernel(where, *refs):
    heads, own, got_one, got_two, got_three, vectors, weight, out_weight = refs[:8]
    grad_in, normed_first, inv_first, qkv = refs[8:12]
    grad_out, branch_out, proj_out, part_out, sums_out = refs[12:]
    line_at = where[0]
    grad_first = grad_in[...] + own[...] + got_one[...] + got_two[...] + got_three[...]
    normed = normed_first[...]
    grad = norm_rows_back(grad_first, normed, inv_first[...], vectors[16:17, :])
    sums_out[0:1, :] = column_sum(grad_first * normed)
    sums_out[1:2, :] = column_sum(grad_first)
    grad_out[...] = grad
    branch = grad.astype(LOW)
    branch_out[...] = branch
    mask = quarter_mask(line_at)
    mixed_grad = masked(product_right(branch, out_weight[...]).astype(LOW), mask)
    pieces = attend_tiles_back(qkv[...], mixed_grad, SPAN, head_allowed(heads[...]))
    tiles = SPAN // LANES
    for piece in range(3):
        joined = jnp.concatenate(pieces[piece * tiles : (piece + 1) * tiles], axis=1)
        proj_out[:, piece * SPAN : (piece + 1) * SPAN] = masked(joined, mask)
    part_out[...] = product_right(proj_out[...], weight[:, : 3 * SPAN])


def cls_end_kernel(where, *refs):
    heads, grad, own, got_one, got_two, got_three = refs[:6]
    square, sums_back, sums_top = refs[6:9]
    normed_second, inv_second, vectors = refs[9:12]
    row_out, second_out, shared_out, held = refs[12:]
    rank = where[0] * PLANE + where[1]
    total = grad[...] + own[...] + got_one[...] + got_two[...] + got_three[...]
    held[...] = total
    row = held[pl.ds(rank, 1), :]
    row_out[...] = row
    second_out[...] = norm_rows_back(
        row, normed_second[0:1, :], inv_second[0:1, :], vectors[6:7, :]
    )
    number = row_from_column(heads[:, 2 * MODEL + 2 : 2 * MODEL + 3], GROUP)
    entry = lax.broadcasted_iota(jnp.int32, (GROUP, GROUP), 0).astype(WIDE)
    hot = (entry == number).astype(WIDE)
    shared_out[0:GROUP, :] = jnp.dot(hot, total, precision=lax.Precision.HIGHEST)
    shared_out[GROUP : GROUP + 1, 0:LANES] = square[0:1, :]
    shared_out[GROUP + 1 : GROUP + 3, :] = sums_back[0:2, :]
    shared_out[GROUP + 3 : GROUP + 5, :] = sums_top[0:2, :]


def cls_rows_kernel(where, *refs):
    packs = refs[:4]
    heads, branch, low, second = refs[4:8]
    out, kept = refs[8:]
    line_at = where[0]
    rows, width = kept.shape[1:]
    for step, pack in enumerate(packs):
        first = pack.shape[0] - rows
        kept[(line_at + LINE - step) % LINE] = pack[first:, :width]
    starts = (MODEL, 2 * MODEL, 3 * MODEL, 4 * MODEL)
    out[:, 0:MODEL] = heads[:, :MODEL].astype(LOW)
    for piece, start in enumerate(starts):
        from_at = piece * SPAN
        for tile in range(MODEL // LANES):
            total = None
            for at in range(PLANE):
                inner = tile - TILE_START[at]
                if inner in (0, 1):
                    first = from_at + inner * LANES
                    value = kept[at, :, first : first + LANES]
                    total = value if total is None else total + value
            out[:, start + tile * LANES : start + (tile + 1) * LANES] = total
    out[:, 5 * MODEL : 6 * MODEL] = branch[...]
    out[:, 6 * MODEL : 7 * MODEL] = low[...]
    out[:, 7 * MODEL + FF : 8 * MODEL + FF] = second[...]
    part = FF // LINE
    for at in range(PLANE):
        first = 4 * SPAN
        out[:, 7 * MODEL + at * part : 7 * MODEL + (at + 1) * part] = kept[
            at, :, first : first + part
        ]
        out[:, 8 * MODEL + FF + at * part : 8 * MODEL + FF + (at + 1) * part] = kept[
            at, :, first + part : first + 2 * part
        ]


def own_features(rank, width):
    shape = (MODEL, width)
    feature = lax.broadcasted_iota(jnp.int32, shape, 0)
    column = lax.broadcasted_iota(jnp.int32, shape, 1)
    return (feature == rank * width + column).astype(LOW)


def cls_owner_kernel(where, *refs):
    own, got, mats_out, vecs_out, rows = refs
    rank = where[0] * PLANE + where[1]
    width = mats_out.shape[0]
    rows[:GROUP] = own[...]
    rows[GROUP:] = got[...]
    chosen = own_features(rank, width)
    plan = (
        (0, MODEL, 3 * MODEL, 0),
        (4 * MODEL, 5 * MODEL, MODEL, 3 * MODEL),
        (6 * MODEL, 7 * MODEL, FF, 4 * MODEL),
        (7 * MODEL + FF, 8 * MODEL + FF, FF, 4 * MODEL + FF),
    )
    for left, right, size, target in plan:
        side = product_plain(rows[:, left : left + MODEL], chosen).astype(LOW)
        mats_out[:, target : target + size] = product_left(side, rows[:, right : right + size])
    vecs_out[...] = jnp.zeros_like(vecs_out)
    for at, start in ((0, MODEL), (1, 3 * MODEL), (2, 5 * MODEL), (3, 7 * MODEL + FF)):
        vecs_out[at : at + 1, :] = column_sum(rows[:, start : start + MODEL])
    for at in range(FF // MODEL):
        start = 7 * MODEL + at * MODEL
        vecs_out[8 + at : 9 + at, :] = column_sum(rows[:, start : start + MODEL])


def head_share_kernel(where, *refs):
    packs, mlp = refs[:4], refs[4]
    mine_out, vecs_out, rows = refs[5:]
    rank = where[0] * PLANE + where[1]
    count = LINE * 24
    for at, pack in enumerate(packs):
        rows[at * count : (at + 1) * count] = pack[...]
    total = PLANE * count

    def chosen(base, apart):
        shape = (CORES * GROUP, total)
        row = lax.broadcasted_iota(jnp.int32, shape, 0)
        column = lax.broadcasted_iota(jnp.int32, shape, 1)
        hot = (column == row // 2 * 24 + base + row % 2 * apart).astype(LOW)
        return product_plain(hot, rows[...]).astype(LOW)

    own = own_features(rank, OWN)
    for at, (left, right) in enumerate(((0, 4), (2, 8))):
        side = product_plain(chosen(left, 1), own).astype(LOW)
        for piece in range(FF_HALF // MODEL):
            columns = slice(at * FF_HALF + piece * MODEL, at * FF_HALF + (piece + 1) * MODEL)
            share = product_left(side, chosen(right + 2 * piece, 1))
            mine_out[:, columns] = mlp[:, columns] + share
    shape = (16, total)
    row = lax.broadcasted_iota(jnp.int32, shape, 0)
    column = lax.broadcasted_iota(jnp.int32, shape, 1)
    hot = ((column % 24 == row + 12) & (row < 12)).astype(LOW)
    vecs_out[...] = product_plain(hot, rows[...])


def seg_owner_kernel(where, attn, attn_got, mlp, mlp_got, mats_out):
    core_at = where[2]

    def put(base, size, own, got):
        mats_out[:, pl.ds(aligned(base + core_at * size), size)] = own
        mats_out[:, pl.ds(aligned(base + (1 - core_at) * size), size)] = got

    for piece in range(4):
        columns = slice(piece * HALF, (piece + 1) * HALF)
        put(piece * MODEL, HALF, attn[:, columns], attn_got[:, columns])
    for piece in range(2):
        columns = slice(piece * FF_HALF, (piece + 1) * FF_HALF)
        put(4 * MODEL + piece * FF, FF_HALF, mlp[:, columns], mlp_got[:, columns])


def plane_parts(part):
    return (part,) + tuple(in_plane(part, mask) for mask in range(1, PLANE))


def line_parts(part):
    return (part,) + tuple(along_line(part, apart) for apart in range(1, LINE))


def slice_local(
    hidden_in,
    targets,
    doc_ids,
    seg_nums,
    valid_flags,
    seg_mats,
    seg_vecs,
    cls_mats,
    cls_vecs,
    seg_pos,
):
    rank, core_at = lax.axis_index("fsdp"), lax.axis_index("rep")
    line_at, plane_at = rank // PLANE, rank % PLANE
    where = jnp.stack([line_at, plane_at, core_at, doc_ids[0], seg_nums[0]]).astype(jnp.int32)
    own_rows, total_columns = seg_mats.shape
    vec_size = seg_vecs.shape[0]
    live = valid_flags.astype(WIDE)
    live_row, live_column = live[None, :], live[:, None]
    both_rows = CORES * SEG
    first_columns = 4 * HALF + LANES

    first_piece = run_kernel(
        prepare_first_kernel,
        "prepare_first",
        [shape_of((own_rows, first_columns), LOW)],
        where,
        (seg_mats,),
        (seg_vecs[None], cls_vecs[None], live_row),
        [pltpu.SemaphoreType.DMA((4,))],
    )[0]
    first_line = line_parts(first_piece)
    rest = run_kernel(
        prepare_rest_kernel,
        "prepare_rest",
        [shape_of((own_rows, FF_HALF), LOW)] * 2
        + [shape_of((own_rows, QUARTER_HALF), LOW)] * LINE
        + [shape_of((own_rows, HALF), LOW)],
        where,
        (seg_mats, cls_mats),
        (),
        [
            pltpu.VMEM((LINE, own_rows, QUARTER), LOW),
            pltpu.SemaphoreType.DMA((3 + 5 * LINE,)),
        ],
    )
    second_piece, third_piece, quarters, cls_out_piece = rest[0], rest[1], rest[2:-1], rest[-1]

    def joined(*pieces):
        return jnp.concatenate(pieces, axis=1)

    def sent_both(to_x, to_y):
        return in_plane(to_x, 1), in_plane(to_y, 2)

    first_sent = joined(*first_line)
    first_x, first_y = sent_both(first_sent, first_sent)
    second_line = line_parts(after(second_piece, *first_line[1:]))
    size = 2 * first_columns
    second_x, second_y = sent_both(
        joined(first_y[:, size:], *second_line), joined(first_x[:, :size], *second_line)
    )
    third_line = line_parts(after(third_piece, first_x, first_y, *second_line[1:]))
    start, size = size, 2 * FF_HALF
    third_x, third_y = sent_both(
        joined(second_y[:, start + size :], *third_line),
        joined(second_x[:, start : start + size], *third_line),
    )
    cls_line = (quarters[0],) + tuple(
        along_line(after(quarters[apart], second_x, second_y, *third_line[1:]), apart)
        for apart in range(1, LINE)
    )

    hidden_got, live_got = other_core(hidden_in), other_core(live_row)
    qkv_weight, out_half, qkv, mixed, vectors, count = run_kernel(
        qkv_kernel,
        "seg_qkv",
        [
            shape_of((GROUP, own_rows, 3 * HALF), LOW),
            shape_of((GROUP, own_rows, HALF), LOW),
            shape_of((both_rows, 3 * HALF), LOW),
            shape_of((both_rows, HALF), LOW),
            shape_of((2 * (8 * MODEL + FF) // MODEL, MODEL)),
            shape_of((8, LANES)),
        ],
        where,
        (),
        first_line
        + (first_x, first_y, second_x, second_y)
        + (hidden_in, hidden_got, live_row, live_got),
        [
            pltpu.VMEM((GROUP, own_rows, LANES), LOW),
            pltpu.VMEM((2, 8 * MODEL + FF), WIDE),
            pltpu.VMEM((both_rows, MODEL), LOW),
        ],
        flops=2 * SEG * MODEL * 3 * MODEL,
    )
    count = count + other_core(count)
    out_half = out_half.reshape(MODEL, HALF)
    out_weight, mixed_full, normed_first, inv_first, first_low = run_kernel(
        out_kernel,
        "seg_out",
        [
            shape_of((MODEL, MODEL), LOW),
            shape_of((both_rows, MODEL), LOW),
            shape_of((SEG, MODEL)),
            shape_of((SEG, 1)),
            shape_of((SEG, MODEL), LOW),
        ],
        where,
        (),
        (hidden_in, mixed, other_core(mixed), out_half, other_core(out_half), vectors),
        flops=2 * SEG * MODEL * MODEL,
    )
    first_got = other_core(first_low)
    third_x, third_y = after(third_x, first_low), after(third_y, first_low)
    up_weight, act, slope = run_kernel(
        up_kernel,
        "seg_up",
        [
            shape_of((GROUP, own_rows, FF_HALF), LOW),
            shape_of((both_rows, FF_HALF), LOW),
            shape_of((both_rows, FF_HALF)),
        ],
        where,
        (),
        second_line
        + (second_x, second_y, third_x, third_y)
        + (first_low, first_got, vectors),
        [pltpu.VMEM((both_rows, MODEL), LOW)],
        flops=2 * SEG * MODEL * FF,
    )
    fourth_x, fourth_y = sent_both(third_y[:, 2 * size :], third_x[:, size : 2 * size])
    fourth_x, fourth_y = after(fourth_x, act), after(fourth_y, act)
    cls_sent = joined(*cls_line, cls_out_piece)
    cls_sent = after(cls_sent, fourth_x, fourth_y)
    cls_x, cls_y = sent_both(cls_sent, cls_sent)
    down_weight, down_own, down_send = run_kernel(
        down_kernel,
        "seg_down",
        [
            shape_of((GROUP, own_rows, FF_HALF), LOW),
            shape_of((SEG, MODEL)),
            shape_of((SEG, MODEL)),
        ],
        where,
        (),
        third_line + (third_x, third_y, fourth_x, fourth_y) + (act,),
        flops=2 * SEG * MODEL * FF,
    )
    normed_second, inv_second, diff, out_rows, head_row = run_kernel(
        seg_rows_kernel,
        "seg_rows",
        [
            shape_of((SEG, MODEL)),
            shape_of((SEG, 1)),
            shape_of((SEG, MODEL)),
            shape_of((SEG, MODEL)),
            shape_of((1, 2 * MODEL + LANES)),
        ],
        where,
        (),
        (
            down_own,
            other_core(down_send),
            normed_first,
            vectors,
            targets,
            live_column,
            seg_pos,
        ),
    )
    head_planes = plane_parts(head_row)
    size = LINE // 2 * QUARTER_HALF
    cls_far = sent_both(
        after(cls_y[:, size:], *head_planes[1:]), after(cls_x[:, :size], *head_planes[1:])
    )

    second_grad, second_low, second_sums = run_kernel(
        second_norm_kernel,
        "seg_second_norm",
        [shape_of((SEG, MODEL)), shape_of((SEG, MODEL), LOW), shape_of((3, MODEL))],
        where,
        (),
        (diff, count, normed_second, inv_second, vectors),
    )
    second_got = after(other_core(second_low), head_planes[1])
    pre, first_grad_own, first_grad_send, up_sums = run_kernel(
        mlp_back_kernel,
        "seg_mlp_back",
        [
            shape_of((both_rows, FF_HALF), LOW),
            shape_of((SEG, MODEL)),
            shape_of((SEG, MODEL)),
            shape_of((FF_HALF // MODEL, MODEL)),
        ],
        where,
        (),
        (second_low, second_got, down_weight, up_weight, slope),
        [pltpu.VMEM((both_rows, MODEL), LOW)],
        flops=4 * SEG * MODEL * FF,
    )
    head_stack = jnp.concatenate([head_planes[0]] + [after(got, pre) for got in head_planes[1:]])
    head_lines = line_parts(head_stack)
    cls_half, cls_out_half = run_kernel(
        cls_gather_kernel,
        "head_gather",
        [
            shape_of((GROUP, own_rows, QUARTER_HALF), LOW),
            shape_of((PLANE, own_rows, HALF), LOW),
        ],
        where,
        (),
        cls_line + (cls_x, cls_y) + cls_far + (cls_out_piece,),
    )
    cls_weight, cls_out = run_kernel(
        cls_weight_kernel,
        "head_weight",
        [
            shape_of((GROUP, own_rows, QUARTER), LOW),
            shape_of((4, HEAD_DIM, MODEL), LOW),
        ],
        where,
        (),
        (cls_half, other_core(cls_half), cls_out_half, other_core(cls_out_half)),
    )
    cls_weight = cls_weight.reshape(MODEL, QUARTER)
    cls_out = cls_out.reshape(SPAN, MODEL)
    first_grad_got = other_core(first_grad_send)

    def part_shapes(columns):
        return [
            shape_of((count_of, own_rows, columns), LOW)
            for count_of in (LINE // 2, LINE // 2, LINE, LINE, LINE)
        ]

    mlp_parts = run_kernel(
        mlp_weight_kernel,
        "seg_mlp_weight",
        part_shapes(FF),
        where,
        (),
        (first_low, first_got, second_low, second_got, after(pre, head_lines[1]), act),
        [
            pltpu.VMEM((both_rows, MODEL), LOW),
            pltpu.VMEM((GROUP, own_rows, FF), LOW),
            pltpu.SemaphoreType.DMA((GROUP,)),
        ],
        outs_far=True,
        flops=4 * SEG * MODEL * FF,
    )
    mlp_far = reduce_far(tuple(after(part, *cls_far) for part in mlp_parts[:2]))
    heads, cls_qkv, cls_mixed, part = run_kernel(
        cls_attend_kernel,
        "head_attend",
        [
            shape_of((GROUP, 2 * MODEL + LANES)),
            shape_of((GROUP, 3 * SPAN), LOW),
            shape_of((GROUP, SPAN), LOW),
            shape_of((GROUP, MODEL)),
        ],
        where,
        (),
        tuple(after(got, mlp_parts[0], first_grad_got) for got in head_lines)
        + (vectors, cls_weight, cls_out),
    )
    cls_normed, cls_inv, cls_low, cls_act, cls_slope, part = run_kernel(
        cls_mlp_kernel,
        "head_mlp",
        [
            shape_of((GROUP, MODEL)),
            shape_of((GROUP, 1)),
            shape_of((GROUP, MODEL), LOW),
            shape_of((GROUP, FF // LINE), LOW),
            shape_of((GROUP, FF // LINE)),
            shape_of((GROUP, MODEL)),
        ],
        where,
        (),
        (heads,) + line_parts(part) + (vectors, cls_weight),
    )
    cls_parts = line_parts(part)
    mlp_far = tuple(after(got, cls_low) for got in mlp_far)
    mlp_sent = reduce_add(where, mlp_parts, mlp_far)
    mlp_plane = sent_both(*mlp_sent)
    top_row, square, cls_grad, cls_second, cls_pre, part, top_sums = run_kernel(
        cls_top_kernel,
        "head_top",
        [
            shape_of((1, MODEL)),
            shape_of((8, LANES)),
            shape_of((GROUP, MODEL)),
            shape_of((GROUP, MODEL), LOW),
            shape_of((GROUP, FF // LINE), LOW),
            shape_of((GROUP, MODEL)),
            shape_of((2, MODEL)),
        ],
        where,
        (),
        (heads, cls_parts[0], cls_parts[1])
        + tuple(after(got, *mlp_sent) for got in cls_parts[2:])
        + (vectors, cls_weight, cls_normed, count, cls_slope),
        [pltpu.VMEM((GROUP, MODEL), WIDE)],
    )
    cls_grad, cls_branch, cls_proj, part, back_sums = run_kernel(
        cls_attend_back_kernel,
        "head_attend_back",
        [
            shape_of((GROUP, MODEL)),
            shape_of((GROUP, MODEL), LOW),
            shape_of((GROUP, 3 * SPAN), LOW),
            shape_of((GROUP, MODEL)),
            shape_of((2, MODEL)),
        ],
        where,
        (),
        (heads,)
        + line_parts(part)
        + (vectors, cls_weight, cls_out, cls_grad, cls_normed, cls_inv, cls_qkv),
    )
    dheads, head_grad, shared = run_kernel(
        cls_end_kernel,
        "head_end",
        [shape_of((1, MODEL)), shape_of((1, MODEL)), shape_of((GROUP + 8, MODEL))],
        where,
        (),
        (heads, cls_grad)
        + line_parts(part)
        + (square, back_sums, top_sums, normed_second, inv_second, vectors),
        [pltpu.VMEM((GROUP, MODEL), WIDE)],
    )

    head_own, head_send, head_data = run_kernel(
        head_back_kernel,
        "seg_head_back",
        [shape_of((1, MODEL)), shape_of((1, MODEL)), shape_of((12, MODEL))],
        where,
        (),
        (
            head_grad,
            other_core(head_grad),
            down_weight,
            up_weight,
            slope,
            act,
            first_low,
            first_got,
        ),
    )
    grad_summed, branch, mixed_grad, attn_send, first_sums = run_kernel(
        first_norm_kernel,
        "seg_first_norm",
        [
            shape_of((SEG, MODEL)),
            shape_of((SEG, MODEL), LOW),
            shape_of((SEG, MODEL), LOW),
            shape_of((SEG, MODEL), LOW),
            shape_of((3, MODEL)),
        ],
        where,
        (),
        (
            second_grad,
            first_grad_own,
            first_grad_got,
            head_grad,
            head_own,
            other_core(head_send),
            normed_first,
            inv_first,
            vectors,
            out_weight,
        ),
    )
    pack = jnp.concatenate([cls_proj, cls_mixed, cls_pre, cls_act], axis=1)
    mlp_plane = [after(got, branch) for got in mlp_plane]
    mlp_own, *mlp_sent = reduce_fold(where, mlp_parts[4], mlp_plane, pack)
    mlp_got = [along_line(mlp_sent[apart - 1], apart) for apart in range(1, LINE)]
    shared = shared + other_core(shared)
    attn_got = after(other_core(attn_send), mlp_own, shared)
    proj, input_own, input_send, payload = run_kernel(
        attn_back_kernel,
        "seg_attn_back",
        [
            shape_of((both_rows, 3 * HALF), LOW),
            shape_of((SEG, MODEL)),
            shape_of((SEG, MODEL)),
            shape_of((24, MODEL), LOW),
        ],
        where,
        (),
        (
            qkv,
            mixed_grad,
            attn_got,
            live_row,
            live_got,
            qkv_weight,
            first_sums,
            second_sums,
            up_sums,
            dheads,
            normed_second,
            head_data,
        ),
        [pltpu.VMEM((24, MODEL), WIDE)],
        flops=4 * SEG * MODEL * 3 * MODEL,
    )
    attn_parts = run_kernel(
        attn_weight_kernel,
        "seg_attn_weight",
        part_shapes(4 * HALF),
        where,
        (),
        (hidden_in, hidden_got, mixed_full, proj, branch, attn_got),
        [
            pltpu.VMEM((both_rows, MODEL), LOW),
            pltpu.VMEM((both_rows, HALF), LOW),
            pltpu.VMEM((GROUP, own_rows, 4 * HALF), LOW),
            pltpu.SemaphoreType.DMA((GROUP,)),
        ],
        outs_far=True,
        flops=4 * SEG * MODEL * 2 * MODEL,
    )
    attn_far = reduce_far(tuple(after(part, mlp_got[-1]) for part in attn_parts[:2]))
    input_grad = (grad_summed + input_own + other_core(input_send)).astype(LOW)
    row_at = jnp.arange(SEG)[:, None]
    output = jnp.where(row_at == 0, top_row * live_row[:, :1], out_rows).astype(LOW)
    attn_sent = reduce_add(where, attn_parts, attn_far)
    attn_plane = sent_both(*(after(part, mlp_got[1]) for part in attn_sent))
    mlp_got = [after(got, attn_plane[0]) for got in mlp_got]
    mlp_sum = reduce_line(mlp_own, mlp_got)
    payload_line = jnp.concatenate(line_parts(after(payload, *attn_plane)))
    mlp_mine, own_vecs = run_kernel(
        head_share_kernel,
        "seg_head_share",
        [shape_of((own_rows, FF)), shape_of((16, MODEL))],
        where,
        (),
        plane_parts(payload_line) + (mlp_sum,),
        [pltpu.VMEM((GROUP * 24, MODEL), LOW)],
    )
    attn_own, *attn_sent = reduce_fold(where, attn_parts[4], attn_plane)
    attn_sum = reduce_line(
        attn_own, [along_line(attn_sent[apart - 1], apart) for apart in range(1, LINE)]
    )
    seg_mats_grad = run_kernel(
        seg_owner_kernel,
        "seg_owner",
        [shape_of((own_rows, total_columns))],
        where,
        (),
        (attn_sum, other_core(attn_sum), mlp_mine, other_core(mlp_mine)),
    )[0]

    row_width = 8 * MODEL + 2 * FF
    cls_rows = run_kernel(
        cls_rows_kernel,
        "head_rows",
        [shape_of((GROUP, row_width), LOW)],
        where,
        (),
        (pack,) + tuple(mlp_got) + (heads, cls_branch, cls_low, cls_second),
        [pltpu.VMEM((LINE,) + pack.shape, LOW)],
    )[0]
    vec_rows = (8 * MODEL + FF) // MODEL
    cls_mats_grad, cls_vec_rows = run_kernel(
        cls_owner_kernel,
        "head_owner",
        [shape_of((own_rows, total_columns)), shape_of((vec_rows, MODEL))],
        where,
        (),
        (cls_rows, other_core(cls_rows)),
        [pltpu.VMEM((CORES * GROUP, row_width), LOW)],
        flops=64 * own_rows * total_columns,
    )
    pos_total = shared[:GROUP]
    loss_value = shared[GROUP, 0] / (count[0, 0] * MODEL)
    cls_vec_rows = jnp.concatenate(
        [cls_vec_rows[:4], shared[GROUP + 1 : GROUP + 5], cls_vec_rows[8:]]
    )
    seg_vec_rows = (own_vecs + other_core(own_vecs))[:vec_rows]

    def own_vector(rows):
        return lax.dynamic_index_in_dim(rows.reshape(GROUP, vec_size), rank, 0, keepdims=False)

    return (
        output,
        input_grad,
        seg_mats_grad,
        own_vector(seg_vec_rows),
        cls_mats_grad,
        own_vector(cls_vec_rows),
        pos_total,
        loss_value,
    )


def solution(mesh):
    in_specs = (
        P(("rep", "fsdp"), None),
        P(("rep", "fsdp"), None),
        P(("rep", "fsdp")),
        P(("rep", "fsdp")),
        P(("rep", "fsdp")),
        P("fsdp", None),
        P("fsdp"),
        P("fsdp", None),
        P("fsdp"),
        P(),
    )
    out_specs = (
        P(("rep", "fsdp"), None),
        P(("rep", "fsdp"), None),
        P("fsdp", None),
        P("fsdp"),
        P("fsdp", None),
        P("fsdp"),
        P(),
        P(),
    )
    one_slice = dict(mesh.shape) == {"rep": CORES, "fsdp": LINE * PLANE}
    body = slice_local if one_slice else local
    return jax.shard_map(body, mesh=mesh, in_specs=in_specs, out_specs=out_specs, check_vma=False)
```

```python
import math

import jax
import jax.numpy as jnp
from jax import lax
from jax.experimental import pallas as pl
from jax.experimental.pallas import tpu as pltpu
from jax.sharding import PartitionSpec as P

HEADS = 12
HEAD_DIM = 64
FF = 3072
SEG = 128
SEQ = 2048


NORM_EPS = 1e-05
MASK_FILL = -1e30
SQRT_HALF = 0.7071067811865476
INV_SQRT_TWO_PI = 0.3989422804014327


def swapped(value, axis, apart):
    mask = 2**apart
    pairs = [(source, source ^ mask) for source in range(lax.axis_size(axis))]
    return lax.ppermute(value, axis, pairs)


def product_plain(left_side, right_side):
    return jnp.dot(left_side, right_side, preferred_element_type=jnp.float32)


def product_left(left_side, right_side):
    return lax.dot_general(
        left_side, right_side, (((0,), (0,)), ((), ())), preferred_element_type=jnp.float32
    )


def product_right(left_side, right_side):
    return lax.dot_general(
        left_side, right_side, (((1,), (1,)), ((), ())), preferred_element_type=jnp.float32
    )


def row_total(array_in):
    return jnp.sum(array_in.astype(jnp.float32), axis=0)


def unpack_weights(gathered, model_width, ff_width):
    matrix, vector = gathered
    vector = vector.astype(jnp.float32)
    pieces = tuple(
        (vector[offset * model_width : (offset + 1) * model_width] for offset in range(8))
    )
    return (
        (
            matrix[:, : 3 * model_width],
            matrix[:, 3 * model_width : 4 * model_width],
            matrix[:, 4 * model_width : 4 * model_width + ff_width],
            matrix[:, 4 * model_width + ff_width :],
        )
        + pieces
        + (vector[8 * model_width :],)
    )


def norm_forward(summed, gain_vec, shift_vec):
    row_mean = jnp.mean(summed, axis=-1, keepdims=True)
    centered = summed - row_mean
    inv_dev = lax.rsqrt(jnp.mean(centered * centered, axis=-1, keepdims=True) + NORM_EPS)
    normed = centered * inv_dev
    return (normed * gain_vec + shift_vec, normed, inv_dev)


def norm_backward(grad_out, normed, inv_dev, gain_vec):
    scaled = grad_out * gain_vec
    mean_one = jnp.mean(scaled, axis=-1, keepdims=True)
    mean_two = jnp.mean(scaled * normed, axis=-1, keepdims=True)
    grad_in = inv_dev * (scaled - mean_one - normed * mean_two)
    return (grad_in, jnp.sum(grad_out * normed, axis=0), jnp.sum(grad_out, axis=0))


def gelu_value(before):
    return 0.5 * before * (1.0 + lax.erf(before * SQRT_HALF))


def gelu_slope(before):
    return (
        0.5 * (1.0 + lax.erf(before * SQRT_HALF))
        + before * jnp.exp(-0.5 * before * before) * INV_SQRT_TWO_PI
    )


def attention_scores(queries, keys_in, allowed, score_scale):
    raw_scores = (
        jnp.einsum("bqhe,bkhe->bhqk", queries, keys_in, preferred_element_type=jnp.float32)
        * score_scale
    )
    return jnp.where(allowed, raw_scores, MASK_FILL)


def attention_forward(queries, keys_in, values, allowed, score_scale):
    scores = attention_scores(queries, keys_in, allowed, score_scale)
    row_top = jnp.max(scores, axis=-1, keepdims=True)
    log_total = row_top + jnp.log(jnp.sum(jnp.exp(scores - row_top), axis=-1, keepdims=True))
    weights = jnp.exp(scores - log_total).astype(jnp.bfloat16)
    mixed_rows = jnp.einsum("bhqk,bkhe->bqhe", weights, values, preferred_element_type=jnp.float32)
    return (mixed_rows, log_total)


def attention_backward(queries, keys_in, values, allowed, score_scale, log_total, grad_mixed):
    probabilities = jnp.exp(attention_scores(queries, keys_in, allowed, score_scale) - log_total)
    grad_probs = jnp.einsum(
        "bqhe,bkhe->bhqk", grad_mixed, values, preferred_element_type=jnp.float32
    )
    inner_sum = jnp.sum(grad_probs * probabilities, axis=-1, keepdims=True)
    grad_scores = (probabilities * (grad_probs - inner_sum)).astype(jnp.bfloat16)
    grad_query = (
        jnp.einsum("bhqk,bkhe->bqhe", grad_scores, keys_in, preferred_element_type=jnp.float32)
        * score_scale
    )
    grad_key = (
        jnp.einsum("bhqk,bqhe->bkhe", grad_scores, queries, preferred_element_type=jnp.float32)
        * score_scale
    )
    grad_value = jnp.einsum(
        "bhqk,bqhe->bkhe",
        probabilities.astype(jnp.bfloat16),
        grad_mixed,
        preferred_element_type=jnp.float32,
    )
    return (grad_query, grad_key, grad_value)


def block_forward(rows_in, unpacked, attend):
    (
        qkv_weight,
        out_weight,
        up_weight,
        down_weight,
        query_bias,
        value_bias,
        out_bias,
        down_bias,
        gain_first,
        shift_first,
        gain_second,
        shift_second,
        up_bias,
    ) = unpacked
    model_width = rows_in.shape[1]
    inputs = rows_in.astype(jnp.bfloat16)
    projected = product_plain(inputs, qkv_weight)
    queries = (projected[:, :model_width] + query_bias).astype(jnp.bfloat16)
    keys_in = projected[:, model_width : 2 * model_width].astype(jnp.bfloat16)
    values = (projected[:, 2 * model_width :] + value_bias).astype(jnp.bfloat16)
    mixed_rows, attend_kept = attend(queries, keys_in, values)
    mixed_rows = mixed_rows.astype(jnp.bfloat16)
    summed_first = rows_in + product_plain(mixed_rows, out_weight) + out_bias
    first_out, normed_first, inv_first = norm_forward(summed_first, gain_first, shift_first)
    first_low = first_out.astype(jnp.bfloat16)
    pre_act = product_plain(first_low, up_weight) + up_bias
    activated = gelu_value(pre_act).astype(jnp.bfloat16)
    summed_second = first_out + product_right(activated, down_weight) + down_bias
    block_out, normed_second, inv_second = norm_forward(summed_second, gain_second, shift_second)
    saved_state = (
        inputs,
        queries,
        keys_in,
        values,
        attend_kept,
        mixed_rows,
        normed_first,
        inv_first,
        first_low,
        pre_act,
        activated,
        normed_second,
        inv_second,
    )
    return (block_out, saved_state)


def block_backward(grad_out, unpacked, saved_state, attend_back):
    (
        qkv_weight,
        out_weight,
        up_weight,
        down_weight,
        query_bias,
        value_bias,
        out_bias,
        down_bias,
        gain_first,
        shift_first,
        gain_second,
        shift_second,
        up_bias,
    ) = unpacked
    (
        inputs,
        queries,
        keys_in,
        values,
        attend_kept,
        mixed_rows,
        normed_first,
        inv_first,
        first_low,
        pre_act,
        activated,
        normed_second,
        inv_second,
    ) = saved_state
    grad_second, grad_gain_second, grad_shift_second = norm_backward(
        grad_out, normed_second, inv_second, gain_second
    )
    second_low = grad_second.astype(jnp.bfloat16)
    grad_pre = (product_plain(second_low, down_weight) * gelu_slope(pre_act)).astype(jnp.bfloat16)
    grad_first = grad_second + product_right(grad_pre, up_weight)
    grad_summed, grad_gain_first, grad_shift_first = norm_backward(
        grad_first, normed_first, inv_first, gain_first
    )
    branch_low = grad_summed.astype(jnp.bfloat16)
    grad_mixed = product_right(branch_low, out_weight).astype(jnp.bfloat16)
    grad_query, grad_key, grad_value = attend_back(
        queries, keys_in, values, attend_kept, grad_mixed
    )
    grad_proj = jnp.concatenate([grad_query, grad_key, grad_value], axis=1)
    grad_rows = grad_summed + product_right(grad_proj, qkv_weight)
    vector_grad = jnp.concatenate(
        [
            row_total(grad_query),
            row_total(grad_value),
            row_total(branch_low),
            row_total(second_low),
            grad_gain_first,
            grad_shift_first,
            grad_gain_second,
            grad_shift_second,
            row_total(grad_pre),
        ]
    )
    weight_rows = (
        inputs,
        grad_proj,
        mixed_rows,
        branch_low,
        first_low,
        grad_pre,
        second_low,
        activated,
    )
    return (grad_rows, weight_rows, vector_grad)


def weight_products(weight_rows):
    inputs, grad_proj, mixed_rows, branch_low, first_low, grad_pre, second_low, activated = (
        weight_rows
    )
    return (
        product_left(inputs, grad_proj),
        product_left(mixed_rows, branch_low),
        product_left(first_low, grad_pre),
        product_left(second_low, activated),
    )


def local(
    hidden_in,
    targets,
    doc_ids,
    seg_nums,
    valid_flags,
    seg_mats,
    seg_vecs,
    cls_mats,
    cls_vecs,
    seg_pos,
):
    tok_rows, model_width = hidden_in.shape
    ff_width = FF
    seg_len = SEG
    group_span = SEQ // tok_rows
    seg_count = tok_rows // seg_len
    score_scale = HEAD_DIM ** (-0.5)
    head_shape = (HEADS, HEAD_DIM)
    live_rows = valid_flags.astype(jnp.float32)
    rank_full = lax.axis_index("fsdp")
    seg_gathered = (
        lax.all_gather(seg_mats, "fsdp", axis=0, tiled=True),
        lax.all_gather(seg_vecs, "fsdp", axis=0, tiled=True),
    )
    seg_unpacked = unpack_weights(seg_gathered, model_width, ff_width)
    cls_gathered = (
        lax.all_gather(cls_mats, "fsdp", axis=0, tiled=True),
        lax.all_gather(cls_vecs, "fsdp", axis=0, tiled=True),
    )
    cls_unpacked = unpack_weights(cls_gathered, model_width, ff_width)
    seg_allowed = (live_rows.reshape(seg_count, 1, 1, seg_len) > 0.5) | jnp.eye(seg_len, dtype=bool)
    seg_shape = (seg_count, seg_len) + head_shape

    def seg_attend(queries, keys_in, values):
        mixed_rows, log_total = attention_forward(
            queries.reshape(seg_shape),
            keys_in.reshape(seg_shape),
            values.reshape(seg_shape),
            seg_allowed,
            score_scale,
        )
        return (mixed_rows.reshape(tok_rows, model_width), log_total)

    def seg_attend_back(queries, keys_in, values, log_total, grad_mixed):
        grad_parts = attention_backward(
            queries.reshape(seg_shape),
            keys_in.reshape(seg_shape),
            values.reshape(seg_shape),
            seg_allowed,
            score_scale,
            log_total,
            grad_mixed.reshape(seg_shape),
        )
        return tuple(
            (
                grad_part.reshape(tok_rows, model_width).astype(jnp.bfloat16)
                for grad_part in grad_parts
            )
        )

    first_out, seg_saved = block_forward(hidden_in.astype(jnp.float32), seg_unpacked, seg_attend)
    first_grid = first_out.reshape(seg_count, seg_len, model_width)
    position_hot = (seg_nums[:, None] == jnp.arange(seg_pos.shape[0])[None, :]).astype(jnp.float32)
    position_rows = jnp.sum(
        position_hot[:, :, None] * seg_pos.astype(jnp.float32)[None, :, :], axis=1
    )
    heads_in = first_grid[:, 0, :] + position_rows
    lead_live = live_rows.reshape(seg_count, seg_len)[:, 0]
    lead_doc = doc_ids.reshape(seg_count, seg_len)[:, 0]
    lead_labels = jnp.where(lead_live > 0.5, lead_doc, -1).astype(jnp.bfloat16)
    lead_doc_low = lead_doc.astype(jnp.bfloat16)
    bit_count = group_span.bit_length() - 1
    key_total = group_span * seg_count
    own_slot = rank_full % group_span * seg_count + jnp.arange(seg_count)
    query_shape = (1, seg_count) + head_shape
    key_shape = (1, key_total) + head_shape

    def cls_attend(queries, keys_in, values):
        paired = jnp.concatenate([keys_in, values], axis=1)
        labels = lead_labels
        for bit_level in range(bit_count):
            other_pair, other_labels = swapped((paired, labels), "fsdp", bit_level)
            upper_half = rank_full // (1 << bit_level) % 2 == 1
            paired = jnp.where(
                upper_half,
                jnp.concatenate([other_pair, paired]),
                jnp.concatenate([paired, other_pair]),
            )
            labels = jnp.where(
                upper_half,
                jnp.concatenate([other_labels, labels]),
                jnp.concatenate([labels, other_labels]),
            )
        allowed = (labels[None, :] == lead_doc_low[:, None]) | (
            jnp.arange(key_total)[None, :] == own_slot[:, None]
        )
        allowed = allowed[None, None]
        mixed_rows, log_total = attention_forward(
            queries.reshape(query_shape),
            paired[:, :model_width].reshape(key_shape),
            paired[:, model_width:].reshape(key_shape),
            allowed,
            score_scale,
        )
        return (mixed_rows.reshape(seg_count, model_width), (paired, allowed, log_total))

    def cls_attend_back(queries, keys_in, values, attend_kept, grad_mixed):
        paired, allowed, log_total = attend_kept
        grad_query, grad_key, grad_value = attention_backward(
            queries.reshape(query_shape),
            paired[:, :model_width].reshape(key_shape),
            paired[:, model_width:].reshape(key_shape),
            allowed,
            score_scale,
            log_total,
            grad_mixed.reshape(query_shape),
        )
        grad_pair = jnp.concatenate(
            [grad_key.reshape(key_total, model_width), grad_value.reshape(key_total, model_width)],
            axis=1,
        )
        for bit_level in reversed(range(bit_count)):
            half_rows = grad_pair.shape[0] // 2
            upper_half = rank_full // (1 << bit_level) % 2 == 1
            kept_half = jnp.where(upper_half, grad_pair[half_rows:], grad_pair[:half_rows])
            sent_half = jnp.where(upper_half, grad_pair[:half_rows], grad_pair[half_rows:])
            grad_pair = kept_half + swapped(
                sent_half.astype(jnp.bfloat16), "fsdp", bit_level
            ).astype(sent_half.dtype)
        grad_pair = grad_pair.astype(jnp.bfloat16)
        return (
            grad_query.reshape(seg_count, model_width).astype(jnp.bfloat16),
            grad_pair[:, :model_width],
            grad_pair[:, model_width:],
        )

    top_out, cls_saved = block_forward(heads_in, cls_unpacked, cls_attend)
    combined = jnp.concatenate([top_out[:, None, :], first_grid[:, 1:, :]], axis=1).reshape(
        tok_rows, model_width
    )
    output_rows = combined * live_rows[:, None]
    diff_rows = (output_rows - targets.astype(jnp.float32)) * live_rows[:, None]
    count_all, square_all = lax.psum(
        (jnp.sum(live_rows), jnp.sum(diff_rows * diff_rows)), ("rep", "fsdp")
    )
    loss_value = square_all / (count_all * model_width)
    slots_all = tok_rows * lax.axis_size("rep") * lax.axis_size("fsdp")
    grad_grid = (diff_rows * (slots_all / count_all)).reshape(seg_count, seg_len, model_width)
    cls_back = unpack_weights(
        (
            lax.all_gather(cls_mats, "fsdp", axis=0, tiled=True),
            lax.all_gather(cls_vecs, "fsdp", axis=0, tiled=True),
        ),
        model_width,
        ff_width,
    )
    heads_grad, cls_weight_rows, cls_g_vec = block_backward(
        grad_grid[:, 0, :], cls_back, cls_saved, cls_attend_back
    )
    cls_g_qkv, cls_g_out, cls_g_up, cls_g_down = weight_products(cls_weight_rows)
    pos_local = jnp.sum(position_hot[:, :, None] * heads_grad[:, None, :], axis=0)
    seg_grad_out = jnp.concatenate([heads_grad[:, None, :], grad_grid[:, 1:, :]], axis=1).reshape(
        tok_rows, model_width
    )
    seg_back = unpack_weights(
        (
            lax.all_gather(seg_mats, "fsdp", axis=0, tiled=True),
            lax.all_gather(seg_vecs, "fsdp", axis=0, tiled=True),
        ),
        model_width,
        ff_width,
    )
    input_grad, seg_weight_rows, seg_g_vec = block_backward(
        seg_grad_out, seg_back, seg_saved, seg_attend_back
    )
    seg_g_qkv, seg_g_out, seg_g_up, seg_g_down = weight_products(seg_weight_rows)
    owner_rows = tuple(
        (
            lax.psum_scatter(seg_g_qkv, "fsdp", scatter_dimension=0, tiled=True),
            lax.psum_scatter(seg_g_out, "fsdp", scatter_dimension=0, tiled=True),
            lax.psum_scatter(seg_g_up, "fsdp", scatter_dimension=0, tiled=True),
            lax.psum_scatter(seg_g_down, "fsdp", scatter_dimension=0, tiled=True),
            lax.psum_scatter(seg_g_vec, "fsdp", scatter_dimension=0, tiled=True),
            lax.psum_scatter(cls_g_qkv, "fsdp", scatter_dimension=0, tiled=True),
            lax.psum_scatter(cls_g_out, "fsdp", scatter_dimension=0, tiled=True),
            lax.psum_scatter(cls_g_up, "fsdp", scatter_dimension=0, tiled=True),
            lax.psum_scatter(cls_g_down, "fsdp", scatter_dimension=0, tiled=True),
            lax.psum_scatter(cls_g_vec, "fsdp", scatter_dimension=0, tiled=True),
        )
    )
    replica_share = (
        lax.psum_scatter(
            owner_rows[0].astype(jnp.bfloat16), "rep", scatter_dimension=1, tiled=True
        ).astype(jnp.float32),
        lax.psum_scatter(
            owner_rows[1].astype(jnp.bfloat16), "rep", scatter_dimension=1, tiled=True
        ).astype(jnp.float32),
        lax.psum_scatter(
            owner_rows[2].astype(jnp.bfloat16), "rep", scatter_dimension=1, tiled=True
        ).astype(jnp.float32),
        lax.psum_scatter(
            owner_rows[3].astype(jnp.bfloat16), "rep", scatter_dimension=1, tiled=True
        ).astype(jnp.float32),
        lax.psum_scatter(
            owner_rows[4].astype(jnp.bfloat16), "rep", scatter_dimension=0, tiled=True
        ).astype(jnp.float32),
        lax.psum_scatter(
            owner_rows[5].astype(jnp.bfloat16), "rep", scatter_dimension=1, tiled=True
        ).astype(jnp.float32),
        lax.psum_scatter(
            owner_rows[6].astype(jnp.bfloat16), "rep", scatter_dimension=1, tiled=True
        ).astype(jnp.float32),
        lax.psum_scatter(
            owner_rows[7].astype(jnp.bfloat16), "rep", scatter_dimension=1, tiled=True
        ).astype(jnp.float32),
        lax.psum_scatter(
            owner_rows[8].astype(jnp.bfloat16), "rep", scatter_dimension=1, tiled=True
        ).astype(jnp.float32),
        lax.psum_scatter(
            owner_rows[9].astype(jnp.bfloat16), "rep", scatter_dimension=0, tiled=True
        ).astype(jnp.float32),
    )
    all_summed = (
        lax.all_gather(replica_share[0].astype(jnp.bfloat16), "rep", axis=1, tiled=True).astype(
            jnp.float32
        ),
        lax.all_gather(replica_share[1].astype(jnp.bfloat16), "rep", axis=1, tiled=True).astype(
            jnp.float32
        ),
        lax.all_gather(replica_share[2].astype(jnp.bfloat16), "rep", axis=1, tiled=True).astype(
            jnp.float32
        ),
        lax.all_gather(replica_share[3].astype(jnp.bfloat16), "rep", axis=1, tiled=True).astype(
            jnp.float32
        ),
        lax.all_gather(replica_share[4].astype(jnp.bfloat16), "rep", axis=0, tiled=True).astype(
            jnp.float32
        ),
        lax.all_gather(replica_share[5].astype(jnp.bfloat16), "rep", axis=1, tiled=True).astype(
            jnp.float32
        ),
        lax.all_gather(replica_share[6].astype(jnp.bfloat16), "rep", axis=1, tiled=True).astype(
            jnp.float32
        ),
        lax.all_gather(replica_share[7].astype(jnp.bfloat16), "rep", axis=1, tiled=True).astype(
            jnp.float32
        ),
        lax.all_gather(replica_share[8].astype(jnp.bfloat16), "rep", axis=1, tiled=True).astype(
            jnp.float32
        ),
        lax.all_gather(replica_share[9].astype(jnp.bfloat16), "rep", axis=0, tiled=True).astype(
            jnp.float32
        ),
    )
    seg_summed = all_summed[:5]
    cls_summed = all_summed[5:]
    pos_total = lax.psum(pos_local, ("rep", "fsdp"))
    seg_mat_grad = jnp.concatenate(
        [seg_summed[0], seg_summed[1], seg_summed[2], seg_summed[3]], axis=1
    )
    cls_mat_grad = jnp.concatenate(
        [cls_summed[0], cls_summed[1], cls_summed[2], cls_summed[3]], axis=1
    )
    return (
        output_rows.astype(jnp.bfloat16),
        input_grad.astype(jnp.bfloat16),
        seg_mat_grad,
        seg_summed[4],
        cls_mat_grad,
        cls_summed[4],
        pos_total,
        loss_value,
    )


LINE = 4
PLANE = 4
CORES = 2
LANES = 128
GROUP = LINE * PLANE
LOW, WIDE = jnp.bfloat16, jnp.float32
MODEL = HEADS * HEAD_DIM
SPAN = 2 * LANES
TILE_START = (0, 1, 3, 4)


def line_pairs(apart):
    return [(source, (source + apart * PLANE) % GROUP) for source in range(GROUP)]


def plane_pairs(mask):
    return [(source, source ^ mask) for source in range(GROUP)]


def along_line(value, apart):
    return lax.ppermute(value, "fsdp", line_pairs(apart))


def in_plane(value, mask):
    return lax.ppermute(value, "fsdp", plane_pairs(mask))


def other_core(value):
    return lax.ppermute(value, "rep", [(0, 1), (1, 0)])


def after(value, *events):
    return lax.optimization_barrier((value,) + events)[0]


def shape_of(dims, dtype=WIDE):
    return jax.ShapeDtypeStruct(dims, dtype)


def run_kernel(body, name, outs, where, blocks, arrays, scratch=(), far=(), flops=0):
    in_specs = [pl.BlockSpec(memory_space=pltpu.SMEM)]
    in_specs += [pl.BlockSpec(memory_space=pltpu.HBM)] * len(blocks)
    in_specs += [pl.BlockSpec(memory_space=pltpu.VMEM)] * len(arrays)
    spaces = [pltpu.HBM if at in far else pltpu.VMEM for at in range(len(outs))]
    moved = sum(x.size * x.dtype.itemsize for x in list(blocks) + list(arrays))
    moved += sum(math.prod(o.shape) * jnp.dtype(o.dtype).itemsize for o in outs)
    return pl.pallas_call(
        body,
        name=name,
        out_shape=tuple(outs),
        in_specs=in_specs,
        out_specs=tuple(pl.BlockSpec(memory_space=space) for space in spaces),
        scratch_shapes=list(scratch),
        cost_estimate=pl.CostEstimate(flops=flops, bytes_accessed=moved, transcendentals=0),
        compiler_params=pltpu.CompilerParams(vmem_limit_bytes=VMEM_BYTES),
    )(where, *blocks, *arrays)


VMEM_BYTES = 24 * 1024 * 1024
HALF = MODEL // CORES
FF_HALF = FF // CORES
OWN = MODEL // GROUP
QUARTER = 3 * SPAN + 2 * FF // LINE
QUARTER_HALF = QUARTER // CORES


def aligned(start):
    return pl.multiple_of(start, LANES)


def wait_all(copies):
    for copy in copies:
        copy.wait()


def run_copies(pairs, sems):
    copies = [
        pltpu.make_async_copy(source, target, sems.at[at])
        for at, (source, target) in enumerate(pairs)
    ]
    for copy in copies:
        copy.start()
    wait_all(copies)


def gather_blocks(where, refs, base, width, targets):
    line_at, plane_at = where[0], where[1]
    half = LINE // 2
    for mask in range(PLANE):
        for step in range(LINE):
            if mask == 0:
                ref, offset = refs[step], 0
            elif mask == 3:
                ref = refs[LINE + 3] if step < half else refs[LINE + 2]
                offset = step % half * width
            else:
                ref, offset = refs[LINE + mask - 1], base + step * width
            chip = (line_at + LINE - step) % LINE * PLANE + (plane_at ^ mask)
            for whole, first, last in targets:
                whole[chip] = ref[:, offset + first : offset + last]


def whole_rows(ref):
    value = ref[...]
    return value.reshape(value.shape[0] * value.shape[1], value.shape[2])


def prepare_first_kernel(where, seg, vecs, flags, out, live_out, sems):
    core_at = where[2]
    pairs = []
    for piece in range(4):
        source = seg.at[:, pl.ds(aligned(piece * MODEL + core_at * HALF), HALF)]
        pairs.append((source, out.at[:, piece * HALF : (piece + 1) * HALF]))
    run_copies(pairs, sems)
    size = vecs.shape[1]
    lines = -(-size // LANES)
    block = jnp.zeros((OWN, LANES), WIDE)
    row_at = lax.broadcasted_iota(jnp.int32, (OWN, LANES), 0)
    for which in range(2):
        for line in range(lines):
            width = min(LANES, size - line * LANES)
            value = vecs[which : which + 1, line * LANES : line * LANES + width]
            if width < LANES:
                value = jnp.concatenate([value, jnp.zeros((1, LANES - width), WIDE)], axis=1)
            block = jnp.where(row_at == which * lines + line, value, block)
    live = flags[...].astype(WIDE)
    live_out[...] = live
    count = jnp.sum(live, axis=1, keepdims=True)
    block = jnp.where(row_at == 2 * lines, count, block)
    out[:, 4 * HALF :] = block.astype(LOW)


def prepare_rest_kernel(where, seg, cls, *refs):
    second_out, third_out = refs[:2]
    step_outs, out_half = refs[2 : 2 + LINE], refs[2 + LINE]
    quarters, sems = refs[3 + LINE :]
    line_at, core_at = where[0], where[2]
    start = core_at * FF_HALF
    pairs = [
        (seg.at[:, pl.ds(aligned(4 * MODEL + start), FF_HALF)], second_out),
        (seg.at[:, pl.ds(aligned(4 * MODEL + FF + start), FF_HALF)], third_out),
        (cls.at[:, pl.ds(aligned(3 * MODEL + core_at * HALF), HALF)], out_half),
    ]
    part = FF // LINE
    for at in range(LINE):
        first = TILE_START[at] * LANES
        plan = [(piece * MODEL + first, SPAN, piece * SPAN) for piece in range(3)]
        plan += [
            (4 * MODEL + piece * FF + at * part, part, 3 * SPAN + piece * part)
            for piece in range(2)
        ]
        for source, size, target in plan:
            pairs.append(
                (
                    cls.at[:, source : source + size],
                    quarters.at[at, :, target : target + size],
                )
            )
    run_copies(pairs, sems)
    lanes = pl.ds(aligned(core_at * QUARTER_HALF), QUARTER_HALF)
    for step, out in enumerate(step_outs):
        out[...] = quarters[(line_at + step) % LINE, :, lanes]


def lane_mask(rows, head):
    lane = lax.broadcasted_iota(jnp.int32, (rows, LANES), 1)
    return (lane < HEAD_DIM) if head == 0 else (lane >= HEAD_DIM)


def masked(value, mask):
    return jnp.where(mask, value, jnp.zeros_like(value))


def head_probabilities(query, key, allowed):
    scores = product_right(query, key) * HEAD_DIM ** (-0.5)
    scores = jnp.where(allowed, scores, MASK_FILL)
    raised = jnp.exp(scores - jnp.max(scores, axis=-1, keepdims=True))
    return raised / jnp.sum(raised, axis=-1, keepdims=True)


def attend_tiles(qkv, width, allowed):
    rows = qkv.shape[0]
    mixed = []
    for tile in range(width // LANES):
        at = tile * LANES
        query, key, value = (
            qkv[:, piece * width + at : piece * width + at + LANES] for piece in range(3)
        )
        total = jnp.zeros((rows, LANES), WIDE)
        for head in range(2):
            mask = lane_mask(rows, head)
            weights = head_probabilities(masked(query, mask), key, allowed).astype(LOW)
            total = total + product_plain(weights, masked(value, mask))
        mixed.append(total.astype(LOW))
    return mixed


def attend_tiles_back(qkv, grad_mixed, width, allowed):
    rows = qkv.shape[0]
    scale = HEAD_DIM ** (-0.5)
    results = ([], [], [])
    for tile in range(width // LANES):
        at = tile * LANES
        query, key, value = (
            qkv[:, piece * width + at : piece * width + at + LANES] for piece in range(3)
        )
        grad = grad_mixed[:, at : at + LANES]
        totals = [jnp.zeros((rows, LANES), WIDE) for _ in range(3)]
        for head in range(2):
            mask = lane_mask(rows, head)
            query_low, key_low, grad_low = (masked(x, mask) for x in (query, key, grad))
            chance = head_probabilities(query_low, key, allowed)
            grad_chance = product_right(grad_low, value)
            inner = jnp.sum(grad_chance * chance, axis=-1, keepdims=True)
            grad_scores = (chance * (grad_chance - inner)).astype(LOW)
            totals[0] = totals[0] + product_plain(grad_scores, key_low)
            totals[1] = totals[1] + product_left(grad_scores, query_low)
            totals[2] = totals[2] + product_left(chance.astype(LOW), grad_low)
        results[0].append((totals[0] * scale).astype(LOW))
        results[1].append((totals[1] * scale).astype(LOW))
        results[2].append(totals[2].astype(LOW))
    return results[0] + results[1] + results[2]


def token_allowed(live_row):
    shape = (SEG, SEG)
    same = lax.broadcasted_iota(jnp.int32, shape, 0) == lax.broadcasted_iota(jnp.int32, shape, 1)
    return (live_row > 0.5) | same


def qkv_kernel(where, *refs):
    blocks = refs[:8]
    hidden, hidden_got, live_row, live_got = refs[8:12]
    weight_out, out_half, qkv_out, mixed_out, vectors_out, count_out = refs[12:18]
    vec_rows, flat, inputs, weight, sem = refs[18:]
    core_at = where[2]
    gather_blocks(
        where,
        blocks,
        0,
        4 * HALF + LANES,
        (
            (weight, 0, 3 * HALF),
            (out_half, 3 * HALF, 4 * HALF),
            (vec_rows, 4 * HALF, 4 * HALF + LANES),
        ),
    )
    stored = pltpu.make_async_copy(weight, weight_out, sem)
    stored.start()
    piece = (8 * MODEL + FF) // GROUP
    lines = -(-piece // LANES)
    count = jnp.zeros((1, LANES), WIDE)
    for chip in range(GROUP):
        rows = vec_rows[chip, 0:16, :].astype(WIDE)
        for block in range(2):
            joined = jnp.concatenate(
                [rows[block * lines + r : block * lines + r + 1] for r in range(lines)], axis=1
            )
            flat[block : block + 1, chip * piece : (chip + 1) * piece] = joined[:, :piece]
        count = count + rows[2 * lines : 2 * lines + 1]
    rows_each = (8 * MODEL + FF) // MODEL
    for block in range(2):
        for row in range(rows_each):
            vectors_out[block * rows_each + row : block * rows_each + row + 1, :] = flat[
                block : block + 1, row * MODEL : (row + 1) * MODEL
            ]
    count_out[...] = jnp.broadcast_to(count, count_out.shape)
    inputs[:SEG] = hidden[...]
    inputs[SEG:] = hidden_got[...]
    projected = product_plain(inputs[...], whole_rows(weight))
    lanes = pl.ds(aligned(core_at * HALF), HALF)
    qkv_out[:, :HALF] = (projected[:, :HALF] + vectors_out[0:1, lanes]).astype(LOW)
    qkv_out[:, HALF : 2 * HALF] = projected[:, HALF : 2 * HALF].astype(LOW)
    qkv_out[:, 2 * HALF :] = (projected[:, 2 * HALF :] + vectors_out[1:2, lanes]).astype(LOW)
    for part, live in enumerate((live_row, live_got)):
        rows = slice(part * SEG, (part + 1) * SEG)
        tiles = attend_tiles(qkv_out[rows, :], HALF, token_allowed(live[...]))
        for tile, value in enumerate(tiles):
            mixed_out[rows, tile * LANES : (tile + 1) * LANES] = value
    stored.wait()


def norm_rows(summed):
    row_mean = jnp.mean(summed, axis=-1, keepdims=True)
    centered = summed - row_mean
    inv_dev = lax.rsqrt(jnp.mean(centered * centered, axis=-1, keepdims=True) + NORM_EPS)
    return centered * inv_dev, inv_dev


def norm_rows_back(grad_out, normed, inv_dev, gain):
    scaled = grad_out * gain
    mean_one = jnp.mean(scaled, axis=-1, keepdims=True)
    mean_two = jnp.mean(scaled * normed, axis=-1, keepdims=True)
    return inv_dev * (scaled - mean_one - normed * mean_two)


def column_sum(value):
    return jnp.sum(value.astype(WIDE), axis=0, keepdims=True)


def four_rows(vectors, first):
    return jnp.concatenate([vectors[first + at : first + at + 1, :] for at in range(4)], axis=1)


def gelu_both(before):
    half = 0.5 * (1.0 + lax.erf(before * SQRT_HALF))
    slope = half + before * jnp.exp(-0.5 * before * before) * INV_SQRT_TWO_PI
    return before * half, slope


def out_kernel(where, hidden, mixed, mixed_got, half, half_got, vectors, *outs):
    full_store, mixed_full, normed_out, inv_out, low_out, full_out, sem = outs
    core_at = where[2]
    own, other = aligned(core_at * HALF), aligned((1 - core_at) * HALF)
    full_out[:, pl.ds(own, HALF)] = half[...]
    full_out[:, pl.ds(other, HALF)] = half_got[...]
    stored = pltpu.make_async_copy(full_out, full_store, sem)
    stored.start()
    mixed_full[:, pl.ds(own, HALF)] = mixed[...]
    mixed_full[:SEG, pl.ds(other, HALF)] = mixed_got[SEG:, :]
    mixed_full[SEG:, pl.ds(other, HALF)] = mixed_got[:SEG, :]
    branch = product_plain(mixed_full[:SEG, :], full_out[...])
    normed, inv_dev = norm_rows(hidden[...].astype(WIDE) + branch + vectors[2:3, :])
    normed_out[...] = normed
    inv_out[...] = inv_dev
    low_out[...] = (normed * vectors[4:5, :] + vectors[5:6, :]).astype(LOW)
    stored.wait()


def up_kernel(where, *refs):
    blocks = refs[:8]
    low, low_got, vectors = refs[8:11]
    weight, act_out, slope_store, both, slope_out, sems = refs[11:]
    core_at = where[2]
    gather_blocks(where, blocks, 2 * (4 * HALF + LANES), FF_HALF, ((weight, 0, FF_HALF),))
    both[:SEG] = low[...]
    both[SEG:] = low_got[...]
    stored = []
    for at in range(FF_HALF // MODEL):
        columns = slice(at * MODEL, (at + 1) * MODEL)
        held = weight[:, :, columns]
        before = product_plain(both[...], held.reshape(MODEL, MODEL))
        bias = vectors[pl.ds(8 + core_at * (FF_HALF // MODEL) + at, 1), :]
        value, slope = gelu_both(before + bias)
        act_out[:, columns] = value.astype(LOW)
        slope_out[:, columns] = slope
        stored.append(
            pltpu.make_async_copy(
                slope_out.at[:, columns], slope_store.at[:, columns], sems.at[at]
            )
        )
        stored[-1].start()
    wait_all(stored)


def down_kernel(where, *refs):
    blocks, act = refs[:8], refs[8]
    store, own_out, send_out, weight, sem = refs[9:]
    gather_blocks(where, blocks, 2 * FF_HALF, FF_HALF, ((weight, 0, FF_HALF),))
    stored = pltpu.make_async_copy(weight, store, sem)
    stored.start()
    partial = product_right(act[...], whole_rows(weight))
    own_out[...] = partial[:SEG]
    send_out[...] = partial[SEG:]
    stored.wait()


def seg_rows_kernel(where, *refs):
    own, got, normed_first, vectors, targets, live, seg_pos = refs[:7]
    normed_out, inv_out, diff_out, rows_out, head_out = refs[7:]
    doc, number = where[3], where[4]
    first = normed_first[...] * vectors[4:5, :] + vectors[5:6, :]
    normed, inv_dev = norm_rows(first + own[...] + got[...] + vectors[3:4, :])
    normed_out[...] = normed
    inv_out[...] = inv_dev
    rows = normed * vectors[6:7, :] + vectors[7:8, :]
    shape = (SEG, SEG)
    same = lax.broadcasted_iota(jnp.int32, shape, 0) == lax.broadcasted_iota(jnp.int32, shape, 1)
    live_rows = jnp.sum(jnp.where(same, live[...], 0.0), axis=1, keepdims=True)
    target_rows = targets[...].astype(WIDE)
    output = rows * live_rows
    rows_out[...] = output
    diff = (output - target_rows) * live_rows
    row_at = lax.broadcasted_iota(jnp.int32, (SEG, 1), 0)
    diff = jnp.where(row_at > 0, diff, 0.0)
    diff_out[...] = diff
    table = seg_pos[...].astype(WIDE)
    chosen = lax.broadcasted_iota(jnp.int32, table.shape, 0) == number
    position = jnp.sum(jnp.where(chosen, table, 0.0), axis=0, keepdims=True)
    head_out[:, :MODEL] = rows[0:1, :] + position
    head_out[:, MODEL : 2 * MODEL] = target_rows[0:1, :]
    square = jnp.sum(column_sum(diff * diff), axis=1, keepdims=True)
    lane = lax.broadcasted_iota(jnp.int32, (1, LANES), 1)
    facts = jnp.where(lane == 0, live_rows[0:1, :], 0.0)
    facts = jnp.where(lane == 1, doc.astype(WIDE), facts)
    facts = jnp.where(lane == 2, number.astype(WIDE), facts)
    facts = jnp.where(lane == 3, square, facts)
    head_out[:, 2 * MODEL :] = facts


def second_norm_kernel(where, diff, count, normed, inv_dev, vectors, grad_out, low_out, sums_out):
    grad_top = diff[...] * ((SEG * GROUP * CORES) / count[0:1, 0:1])
    normed_rows = normed[...]
    grad = norm_rows_back(grad_top, normed_rows, inv_dev[...], vectors[6:7, :])
    low = grad.astype(LOW)
    grad_out[...] = grad
    low_out[...] = low
    sums_out[0:1, :] = column_sum(low)
    sums_out[1:2, :] = column_sum(grad_top * normed_rows)
    sums_out[2:3, :] = column_sum(grad_top)


def mlp_back_kernel(where, *refs):
    low, low_got, down_weight, up_weight, slope = refs[:5]
    pre_out, own_out, send_out, sums_out, both = refs[5:]
    both[:SEG] = low[...]
    both[SEG:] = low_got[...]
    for at in range(FF_HALF // MODEL):
        columns = slice(at * MODEL, (at + 1) * MODEL)
        held = down_weight[:, :, columns]
        before = product_plain(both[...], held.reshape(MODEL, MODEL))
        pre = (before * slope[:, columns]).astype(LOW)
        pre_out[:, columns] = pre
        sums_out[at : at + 1, :] = column_sum(pre)
    partial = product_right(pre_out[...], whole_rows(up_weight))
    own_out[...] = partial[:SEG]
    send_out[...] = partial[SEG:]


def scatter_parts(where, parts, outs, sems):
    line_at, plane_at = where[0], where[1]
    far_low, far_high, to_x, to_y, kept = outs
    half = LINE // 2
    copies = []
    for mask in range(PLANE):
        for step in range(LINE):
            source = parts.at[(line_at + step) % LINE * PLANE + (plane_at ^ mask)]
            if mask == 3:
                target = far_low.at[step] if step < half else far_high.at[step - half]
            else:
                target = (kept, to_x, to_y)[mask].at[step]
            copies.append(pltpu.make_async_copy(source, target, sems.at[len(copies)]))
    for copy in copies:
        copy.start()
    wait_all(copies)


def mlp_weight_kernel(where, *refs):
    first, first_got, second, second_got, pre, act = refs[:6]
    outs = refs[6:11]
    left, parts, sems = refs[11:]
    for at, (own, got, right) in enumerate(((first, first_got, pre), (second, second_got, act))):
        left[:SEG] = own[...]
        left[SEG:] = got[...]
        for piece in range(FF_HALF // MODEL):
            start = piece * MODEL
            product = product_left(left[...], right[:, start : start + MODEL]).astype(LOW)
            target = at * FF_HALF + start
            parts[:, :, target : target + MODEL] = product.reshape(GROUP, OWN, MODEL)
    scatter_parts(where, parts, outs, sems)


def attn_weight_kernel(where, *refs):
    hidden, hidden_got, mixed, proj, branch, got = refs[:6]
    outs = refs[6:11]
    left, right, parts, sems = refs[11:]
    core_at = where[2]
    left[:SEG] = hidden[...]
    left[SEG:] = hidden_got[...]
    right[:SEG] = branch[:, pl.ds(aligned(core_at * HALF), HALF)]
    right[SEG:] = got[:, HALF:]
    for piece in range(4):
        start = piece * HALF
        if piece < 3:
            product = product_left(left[...], proj[:, start : start + HALF])
        else:
            product = product_left(mixed[...], right[...])
        parts[:, :, start : start + HALF] = product.astype(LOW).reshape(GROUP, OWN, HALF)
    scatter_parts(where, parts, outs, sems)


def fold_kernel(where, kept, got_x, got_y, *refs):
    extra, own_out, sent = refs[: -LINE], refs[-LINE], refs[1 - LINE :]
    rows = kept.shape[1]
    for step in range(LINE):
        total = kept[step].astype(WIDE) + got_x[step].astype(WIDE) + got_y[step].astype(WIDE)
        if step == 0:
            own_out[...] = total
            continue
        out = sent[step - 1]
        out[:rows, :] = total.astype(LOW)
        if extra:
            out[rows:, :] = jnp.zeros_like(out[rows:, :])
            out[rows:, : extra[0].shape[1]] = extra[0][...]


def reduce_far(parts):
    return in_plane(parts[0], 2), in_plane(parts[1], 1)


def reduce_add(where, parts, far):
    shape = parts[2].shape
    return run_kernel(
        add_far_kernel,
        "add_far",
        [shape_of(shape, LOW)] * 2,
        where,
        (),
        tuple(far) + (parts[2], parts[3]),
    )


def reduce_fold(where, kept, got, *extra):
    _, rows, columns = kept.shape
    more = sum(value.shape[0] for value in extra)
    return run_kernel(
        fold_kernel,
        "fold",
        [shape_of((rows, columns))] + [shape_of((rows + more, columns), LOW)] * (LINE - 1),
        where,
        (),
        (kept,) + tuple(got) + extra,
    )


def reduce_line(own, pieces):
    total = own
    for piece in pieces:
        total = total + piece[: own.shape[0]].astype(WIDE)
    return total


def head_back_kernel(where, *refs):
    grad, grad_got, down_weight, up_weight, slope, act, low, low_got = refs[:8]
    own_out, send_out, data_out = refs[8:]
    few = 16
    row_at = lax.broadcasted_iota(jnp.int32, (few, 1), 0)

    def two_rows(first, second):
        return jnp.where(row_at == 0, first, jnp.where(row_at == 1, second, 0.0))

    second = two_rows(grad[...], grad_got[...]).astype(LOW)
    data_out[0:1, :] = low[0:1, :].astype(WIDE)
    data_out[1:2, :] = low_got[0:1, :].astype(WIDE)
    data_out[2:4, :] = second[0:2].astype(WIDE)
    partial = jnp.zeros((few, MODEL), WIDE)
    for at in range(FF_HALF // MODEL):
        columns = slice(at * MODEL, (at + 1) * MODEL)
        before = product_plain(second, down_weight[:, :, columns].reshape(MODEL, MODEL))
        slopes = two_rows(slope[0:1, columns], slope[SEG : SEG + 1, columns])
        pre = (before * slopes).astype(LOW)
        partial = partial + product_right(pre, up_weight[:, :, columns].reshape(MODEL, MODEL))
        data_out[4 + 2 * at : 6 + 2 * at, :] = pre[0:2].astype(WIDE)
        data_out[8 + 2 * at : 9 + 2 * at, :] = act[0:1, columns].astype(WIDE)
        data_out[9 + 2 * at : 10 + 2 * at, :] = act[SEG : SEG + 1, columns].astype(WIDE)
    own_out[...] = partial[0:1]
    send_out[...] = partial[1:2]


def first_norm_kernel(where, *refs):
    second_grad, own, got, head_grad, head_own, head_got = refs[:6]
    normed_rows, inv_dev, vectors, out_weight = refs[6:10]
    grad_out, branch_out, mixed_out, send_out, sums_out = refs[10:]
    core_at = where[2]
    grad_rows = second_grad[...] + own[...] + got[...]
    head = head_grad[...] + head_own[...] + head_got[...]
    row_at = lax.broadcasted_iota(jnp.int32, (SEG, 1), 0)
    grad_rows = jnp.where(row_at == 0, head, grad_rows)
    normed = normed_rows[...]
    grad = norm_rows_back(grad_rows, normed, inv_dev[...], vectors[4:5, :])
    grad_out[...] = grad
    branch = grad.astype(LOW)
    branch_out[...] = branch
    mixed_out[...] = product_right(branch, out_weight[...]).astype(LOW)
    other = pl.ds(aligned((1 - core_at) * HALF), HALF)
    send_out[:, :HALF] = mixed_out[:, other]
    send_out[:, HALF:] = branch_out[:, other]
    sums_out[0:1, :] = column_sum(branch)
    sums_out[1:2, :] = column_sum(grad_rows * normed)
    sums_out[2:3, :] = column_sum(grad_rows)


def attn_back_kernel(where, *refs):
    qkv, mixed_grad, got, live_row, live_got, weight = refs[:6]
    sums_first, sums_second, sums_up, head_top, head_normed, data = refs[6:12]
    proj_out, own_out, send_out, payload_out, rows = refs[12:]
    core_at = where[2]
    lanes = pl.ds(aligned(core_at * HALF), HALF)
    for part, live in enumerate((live_row, live_got)):
        at = slice(part * SEG, (part + 1) * SEG)
        grad = mixed_grad[:, lanes] if part == 0 else got[:, :HALF]
        pieces = attend_tiles_back(qkv[at, :], grad, HALF, token_allowed(live[...]))
        for tile, value in enumerate(pieces):
            proj_out[at, tile * LANES : (tile + 1) * LANES] = value
    partial = product_right(proj_out[...], whole_rows(weight))
    own_out[...] = partial[:SEG]
    send_out[...] = partial[SEG:]
    rows[...] = jnp.zeros_like(rows)
    rows[0:12, :] = data[0:12, :]
    rows[12:13, lanes] = column_sum(proj_out[:, :HALF])
    rows[13:14, lanes] = column_sum(proj_out[:, 2 * HALF :])
    rows[14:15, :] = sums_first[0:1, :]
    rows[15:16, :] = sums_second[0:1, :] + data[2:3, :]
    rows[16:18, :] = sums_first[1:3, :]
    rows[18:19, :] = sums_second[1:2, :] + head_top[...] * head_normed[0:1, :]
    rows[19:20, :] = sums_second[2:3, :] + head_top[...]
    for at in range(FF_HALF // MODEL):
        total = sums_up[at : at + 1, :] + data[4 + 2 * at : 5 + 2 * at, :]
        total = total + data[5 + 2 * at : 6 + 2 * at, :]
        rows[pl.ds(20 + core_at * (FF_HALF // MODEL) + at, 1), :] = total
    payload_out[...] = rows[...].astype(LOW)


def cls_gather_kernel(where, *refs):
    blocks = refs[:8]
    own_out, from_x, from_y, far_x = refs[8], refs[4], refs[5], refs[6]
    weight_out, out_rows = refs[9:]
    plane_at = where[1]
    gather_blocks(where, blocks, 0, QUARTER_HALF, ((weight_out, 0, QUARTER_HALF),))
    first = LINE * QUARTER_HALF
    out_rows[plane_at] = own_out[...]
    out_rows[plane_at ^ 1] = from_x[:, first : first + HALF]
    out_rows[plane_at ^ 2] = from_y[:, first : first + HALF]
    first = LINE // 2 * QUARTER_HALF
    out_rows[plane_at ^ 3] = far_x[:, first : first + HALF]


def cls_weight_kernel(where, own, got, out_half, out_got, weight_out, out_full):
    line_at, core_at = where[0], where[2]
    out_full[...] = jnp.zeros_like(out_full)
    for value, part, core in ((own, out_half, core_at), (got, out_got, 1 - core_at)):
        weight_out[:, :, pl.ds(aligned(core * QUARTER_HALF), QUARTER_HALF)] = value[...]
        rows = part[...].reshape(3, HEAD_DIM, HALF)
        out_full[pl.ds(line_at % 2, 3), :, pl.ds(aligned(core * HALF), HALF)] = rows


def add_far_kernel(where, far_low, far_high, to_x, to_y, x_out, y_out):
    half = LINE // 2
    x_out[:half] = to_x[:half] + far_low[...]
    x_out[half:] = to_x[half:]
    y_out[:half] = to_y[:half]
    y_out[half:] = to_y[half:] + far_high[...]


def row_from_column(column, size):
    shape = (size, size)
    same = lax.broadcasted_iota(jnp.int32, shape, 0) == lax.broadcasted_iota(jnp.int32, shape, 1)
    return jnp.sum(jnp.where(same, column, 0.0), axis=0, keepdims=True)


def head_allowed(heads):
    facts = heads[:, 2 * MODEL :]
    live, doc = facts[:, 0:1], facts[:, 1:2]
    shape = (GROUP, GROUP)
    same = lax.broadcasted_iota(jnp.int32, shape, 0) == lax.broadcasted_iota(jnp.int32, shape, 1)
    live_row, doc_row = row_from_column(live, GROUP), row_from_column(doc, GROUP)
    return ((live_row > 0.5) & (doc == doc_row)) | same


def quarter_mask(quarter):
    lane = lax.broadcasted_iota(jnp.int32, (GROUP, SPAN), 1)
    first = (quarter % 2) * HEAD_DIM
    return (lane >= first) & (lane < first + 3 * HEAD_DIM)


def quarter_piece(vectors, row, quarter):
    value = jnp.zeros((1, SPAN), WIDE)
    for at in range(LINE):
        first = TILE_START[at] * LANES
        value = jnp.where(quarter == at, vectors[row : row + 1, first : first + SPAN], value)
    return value


def cls_attend_kernel(where, *refs):
    stacks, vectors, weight, out_weight = refs[:4], refs[4], refs[5], refs[6]
    heads_out, qkv_out, mixed_out, part_out = refs[7:]
    line_at, plane_at = where[0], where[1]
    for step, stack in enumerate(stacks):
        for mask in range(PLANE):
            row = (line_at + LINE - step) % LINE * PLANE + (plane_at ^ mask)
            heads_out[pl.ds(row, 1), :] = stack[mask : mask + 1, :]
    heads = heads_out[...]
    inputs = heads[:, :MODEL].astype(LOW)
    projected = product_plain(inputs, weight[:, : 3 * SPAN])
    query = projected[:, :SPAN] + quarter_piece(vectors, 12, line_at)
    value = projected[:, 2 * SPAN :] + quarter_piece(vectors, 13, line_at)
    qkv_out[:, :SPAN] = query.astype(LOW)
    qkv_out[:, SPAN : 2 * SPAN] = projected[:, SPAN : 2 * SPAN].astype(LOW)
    qkv_out[:, 2 * SPAN :] = value.astype(LOW)
    mixed = attend_tiles(qkv_out[...], SPAN, head_allowed(heads))
    mixed = masked(jnp.concatenate(mixed, axis=1), quarter_mask(line_at))
    mixed_out[...] = mixed
    part_out[...] = product_plain(mixed, out_weight[...])


def cls_mlp_kernel(where, *refs):
    heads, own, got_one, got_two, got_three, vectors, weight = refs[:7]
    normed_out, inv_out, low_out, act_out, slope_out, part_out = refs[7:]
    line_at = where[0]
    branch = own[...] + got_one[...] + got_two[...] + got_three[...]
    normed, inv_dev = norm_rows(heads[:, :MODEL] + branch + vectors[14:15, :])
    normed_out[...] = normed
    inv_out[...] = inv_dev
    low = (normed * vectors[16:17, :] + vectors[17:18, :]).astype(LOW)
    low_out[...] = low
    part = FF // LINE
    first = 3 * SPAN
    bias = vectors[pl.ds(20 + line_at, 1), :]
    before = product_plain(low, weight[:, first : first + part]) + bias
    value, slope = gelu_both(before)
    act = value.astype(LOW)
    act_out[...] = act
    slope_out[...] = slope
    part_out[...] = product_right(act, weight[:, first + part :])


def cls_top_kernel(where, *refs):
    heads, own, got_one, got_two, got_three, vectors, weight = refs[:7]
    normed_first, count, slope = refs[7:10]
    top_out, square_out, grad_out, second_out, pre_out, part_out, sums_out = refs[10:17]
    held = refs[17]
    rank = where[0] * PLANE + where[1]
    first = normed_first[...] * vectors[16:17, :] + vectors[17:18, :]
    down = own[...] + got_one[...] + got_two[...] + got_three[...]
    normed, inv_dev = norm_rows(first + down + vectors[15:16, :])
    rows = normed * vectors[18:19, :] + vectors[19:20, :]
    held[...] = rows
    top_out[...] = held[pl.ds(rank, 1), :]
    facts = heads[:, 2 * MODEL :]
    live = facts[:, 0:1]
    diff = (rows * live - heads[:, MODEL : 2 * MODEL]) * live
    square = jnp.sum(column_sum(diff * diff), axis=1, keepdims=True)
    square = square + jnp.sum(facts[:, 3:4], axis=0, keepdims=True)
    square_out[...] = jnp.broadcast_to(square, square_out.shape)
    grad_top = diff * ((SEG * GROUP * CORES) / count[0:1, 0:1])
    grad = norm_rows_back(grad_top, normed, inv_dev, vectors[18:19, :])
    sums_out[0:1, :] = column_sum(grad_top * normed)
    sums_out[1:2, :] = column_sum(grad_top)
    grad_out[...] = grad
    second = grad.astype(LOW)
    second_out[...] = second
    part = FF // LINE
    at = 3 * SPAN
    pre = (product_plain(second, weight[:, at + part :]) * slope[...]).astype(LOW)
    pre_out[...] = pre
    part_out[...] = product_right(pre, weight[:, at : at + part])


def cls_attend_back_kernel(where, *refs):
    heads, own, got_one, got_two, got_three, vectors, weight, out_weight = refs[:8]
    grad_in, normed_first, inv_first, qkv = refs[8:12]
    grad_out, branch_out, proj_out, part_out, sums_out = refs[12:]
    line_at = where[0]
    grad_first = grad_in[...] + own[...] + got_one[...] + got_two[...] + got_three[...]
    normed = normed_first[...]
    grad = norm_rows_back(grad_first, normed, inv_first[...], vectors[16:17, :])
    sums_out[0:1, :] = column_sum(grad_first * normed)
    sums_out[1:2, :] = column_sum(grad_first)
    grad_out[...] = grad
    branch = grad.astype(LOW)
    branch_out[...] = branch
    mask = quarter_mask(line_at)
    mixed_grad = masked(product_right(branch, out_weight[...]).astype(LOW), mask)
    pieces = attend_tiles_back(qkv[...], mixed_grad, SPAN, head_allowed(heads[...]))
    tiles = SPAN // LANES
    for piece in range(3):
        joined = jnp.concatenate(pieces[piece * tiles : (piece + 1) * tiles], axis=1)
        proj_out[:, piece * SPAN : (piece + 1) * SPAN] = masked(joined, mask)
    part_out[...] = product_right(proj_out[...], weight[:, : 3 * SPAN])


def cls_end_kernel(where, *refs):
    heads, grad, own, got_one, got_two, got_three = refs[:6]
    square, sums_back, sums_top = refs[6:9]
    normed_second, inv_second, vectors = refs[9:12]
    row_out, second_out, shared_out, held = refs[12:]
    rank = where[0] * PLANE + where[1]
    total = grad[...] + own[...] + got_one[...] + got_two[...] + got_three[...]
    held[...] = total
    row = held[pl.ds(rank, 1), :]
    row_out[...] = row
    second_out[...] = norm_rows_back(
        row, normed_second[0:1, :], inv_second[0:1, :], vectors[6:7, :]
    )
    number = row_from_column(heads[:, 2 * MODEL + 2 : 2 * MODEL + 3], GROUP)
    entry = lax.broadcasted_iota(jnp.int32, (GROUP, GROUP), 0).astype(WIDE)
    hot = (entry == number).astype(WIDE)
    shared_out[0:GROUP, :] = jnp.dot(hot, total, precision=lax.Precision.HIGHEST)
    shared_out[GROUP : GROUP + 1, 0:LANES] = square[0:1, :]
    shared_out[GROUP + 1 : GROUP + 3, :] = sums_back[0:2, :]
    shared_out[GROUP + 3 : GROUP + 5, :] = sums_top[0:2, :]


def cls_rows_kernel(where, *refs):
    packs = refs[:4]
    heads, branch, low, second = refs[4:8]
    out, kept = refs[8:]
    line_at = where[0]
    rows, width = kept.shape[1:]
    for step, pack in enumerate(packs):
        first = pack.shape[0] - rows
        kept[(line_at + LINE - step) % LINE] = pack[first:, :width]
    starts = (MODEL, 2 * MODEL, 3 * MODEL, 4 * MODEL)
    out[:, 0:MODEL] = heads[:, :MODEL].astype(LOW)
    for piece, start in enumerate(starts):
        from_at = piece * SPAN
        for tile in range(MODEL // LANES):
            total = None
            for at in range(PLANE):
                inner = tile - TILE_START[at]
                if inner in (0, 1):
                    first = from_at + inner * LANES
                    value = kept[at, :, first : first + LANES]
                    total = value if total is None else total + value
            out[:, start + tile * LANES : start + (tile + 1) * LANES] = total
    out[:, 5 * MODEL : 6 * MODEL] = branch[...]
    out[:, 6 * MODEL : 7 * MODEL] = low[...]
    out[:, 7 * MODEL + FF : 8 * MODEL + FF] = second[...]
    part = FF // LINE
    for at in range(PLANE):
        first = 4 * SPAN
        out[:, 7 * MODEL + at * part : 7 * MODEL + (at + 1) * part] = kept[
            at, :, first : first + part
        ]
        out[:, 8 * MODEL + FF + at * part : 8 * MODEL + FF + (at + 1) * part] = kept[
            at, :, first + part : first + 2 * part
        ]


def own_features(rank, width):
    shape = (MODEL, width)
    feature = lax.broadcasted_iota(jnp.int32, shape, 0)
    column = lax.broadcasted_iota(jnp.int32, shape, 1)
    return (feature == rank * width + column).astype(LOW)


def own_vector(rank, pieces, out, flat):
    size = out.shape[1]
    for at, piece in enumerate(pieces):
        flat[:, at * MODEL : (at + 1) * MODEL] = piece
    value = jnp.zeros((1, size), WIDE)
    for chip in range(GROUP):
        value = jnp.where(rank == chip, flat[:, chip * size : (chip + 1) * size], value)
    out[...] = value


def cls_owner_kernel(where, *refs):
    own, got, shared, mats_out, vec_out, rows, flat = refs
    rank = where[0] * PLANE + where[1]
    width = mats_out.shape[0]
    rows[:GROUP] = own[...]
    rows[GROUP:] = got[...]
    chosen = own_features(rank, width)
    plan = (
        (0, MODEL, 3 * MODEL, 0),
        (4 * MODEL, 5 * MODEL, MODEL, 3 * MODEL),
        (6 * MODEL, 7 * MODEL, FF, 4 * MODEL),
        (7 * MODEL + FF, 8 * MODEL + FF, FF, 4 * MODEL + FF),
    )
    for left, right, size, target in plan:
        side = product_plain(rows[:, left : left + MODEL], chosen).astype(LOW)
        mats_out[:, target : target + size] = product_left(side, rows[:, right : right + size])
    starts = (MODEL, 3 * MODEL, 5 * MODEL, 7 * MODEL + FF)
    pieces = [column_sum(rows[:, start : start + MODEL]) for start in starts]
    pieces += [shared[GROUP + 1 + at : GROUP + 2 + at, :] for at in range(4)]
    starts = [7 * MODEL + at * MODEL for at in range(FF // MODEL)]
    pieces += [column_sum(rows[:, start : start + MODEL]) for start in starts]
    own_vector(rank, pieces, vec_out, flat)


def head_share_kernel(where, *refs):
    packs, mlp = refs[:4], refs[4]
    mine_out, vecs_out, rows = refs[5:]
    rank = where[0] * PLANE + where[1]
    count = LINE * 24
    for at, pack in enumerate(packs):
        rows[at * count : (at + 1) * count] = pack[...]
    total = PLANE * count

    def chosen(base, apart):
        shape = (CORES * GROUP, total)
        row = lax.broadcasted_iota(jnp.int32, shape, 0)
        column = lax.broadcasted_iota(jnp.int32, shape, 1)
        hot = (column == row // 2 * 24 + base + row % 2 * apart).astype(LOW)
        return product_plain(hot, rows[...]).astype(LOW)

    own = own_features(rank, OWN)
    for at, (left, right) in enumerate(((0, 4), (2, 8))):
        side = product_plain(chosen(left, 1), own).astype(LOW)
        for piece in range(FF_HALF // MODEL):
            columns = slice(at * FF_HALF + piece * MODEL, at * FF_HALF + (piece + 1) * MODEL)
            share = product_left(side, chosen(right + 2 * piece, 1))
            mine_out[:, columns] = mlp[:, columns] + share
    shape = (16, total)
    row = lax.broadcasted_iota(jnp.int32, shape, 0)
    column = lax.broadcasted_iota(jnp.int32, shape, 1)
    hot = ((column % 24 == row + 12) & (row < 12)).astype(LOW)
    vecs_out[...] = product_plain(hot, rows[...])


def seg_owner_kernel(where, *refs):
    attn, attn_got, mlp, mlp_got, vecs, vecs_got, mats_out, vec_out, flat = refs
    core_at = where[2]
    rank = where[0] * PLANE + where[1]
    rows = (8 * MODEL + FF) // MODEL
    pieces = [vecs[at : at + 1, :] + vecs_got[at : at + 1, :] for at in range(rows)]
    own_vector(rank, pieces, vec_out, flat)

    def put(base, size, own, got):
        mats_out[:, pl.ds(aligned(base + core_at * size), size)] = own
        mats_out[:, pl.ds(aligned(base + (1 - core_at) * size), size)] = got

    for piece in range(4):
        columns = slice(piece * HALF, (piece + 1) * HALF)
        put(piece * MODEL, HALF, attn[:, columns], attn_got[:, columns])
    for piece in range(2):
        columns = slice(piece * FF_HALF, (piece + 1) * FF_HALF)
        put(4 * MODEL + piece * FF, FF_HALF, mlp[:, columns], mlp_got[:, columns])


def plane_parts(part):
    return (part,) + tuple(in_plane(part, mask) for mask in range(1, PLANE))


def line_parts(part):
    return (part,) + tuple(along_line(part, apart) for apart in range(1, LINE))


def slice_local(
    hidden_in,
    targets,
    doc_ids,
    seg_nums,
    valid_flags,
    seg_mats,
    seg_vecs,
    cls_mats,
    cls_vecs,
    seg_pos,
):
    rank, core_at = lax.axis_index("fsdp"), lax.axis_index("rep")
    line_at, plane_at = rank // PLANE, rank % PLANE
    where = jnp.stack([line_at, plane_at, core_at, doc_ids[0], seg_nums[0]]).astype(jnp.int32)
    own_rows, total_columns = seg_mats.shape
    vec_size = seg_vecs.shape[0]
    both_rows = CORES * SEG
    first_columns = 4 * HALF + LANES

    first_piece, live_row = run_kernel(
        prepare_first_kernel,
        "prepare_first",
        [shape_of((own_rows, first_columns), LOW), shape_of((1, SEG))],
        where,
        (seg_mats,),
        (jnp.stack([seg_vecs, cls_vecs]).astype(WIDE), valid_flags[None]),
        [pltpu.SemaphoreType.DMA((4,))],
    )
    first_line = line_parts(first_piece)
    rest = run_kernel(
        prepare_rest_kernel,
        "prepare_rest",
        [shape_of((own_rows, FF_HALF), LOW)] * 2
        + [shape_of((own_rows, QUARTER_HALF), LOW)] * LINE
        + [shape_of((own_rows, HALF), LOW)],
        where,
        (seg_mats, cls_mats),
        (),
        [
            pltpu.VMEM((LINE, own_rows, QUARTER), LOW),
            pltpu.SemaphoreType.DMA((3 + 5 * LINE,)),
        ],
    )
    second_piece, third_piece, quarters, cls_out_piece = rest[0], rest[1], rest[2:-1], rest[-1]

    def joined(*pieces):
        return jnp.concatenate(pieces, axis=1)

    def sent_both(to_x, to_y):
        return in_plane(to_x, 1), in_plane(to_y, 2)

    hidden_got, live_got = other_core(hidden_in), other_core(live_row)
    first_sent = joined(*first_line)
    first_x, first_y = sent_both(first_sent, first_sent)
    second_line = line_parts(after(second_piece, hidden_got, live_got, *first_line[1:]))
    size = 2 * first_columns
    second_x, second_y = sent_both(
        joined(first_y[:, size:], *second_line), joined(first_x[:, :size], *second_line)
    )
    third_line = line_parts(after(third_piece, first_x, first_y, *second_line[1:]))
    start, size = size, 2 * FF_HALF
    third_x, third_y = sent_both(
        joined(second_y[:, start + size :], *third_line),
        joined(second_x[:, start : start + size], *third_line),
    )
    cls_line = (quarters[0],) + tuple(
        along_line(after(quarters[apart], second_x, second_y, *third_line[1:]), apart)
        for apart in range(1, LINE)
    )

    qkv_weight, out_half, qkv, mixed, vectors, count = run_kernel(
        qkv_kernel,
        "seg_qkv",
        [
            shape_of((GROUP, own_rows, 3 * HALF), LOW),
            shape_of((GROUP, own_rows, HALF), LOW),
            shape_of((both_rows, 3 * HALF), LOW),
            shape_of((both_rows, HALF), LOW),
            shape_of((2 * (8 * MODEL + FF) // MODEL, MODEL)),
            shape_of((8, LANES)),
        ],
        where,
        (),
        first_line
        + (first_x, first_y, second_x, second_y)
        + (hidden_in, hidden_got, live_row, live_got),
        [
            pltpu.VMEM((GROUP, own_rows, LANES), LOW),
            pltpu.VMEM((2, 8 * MODEL + FF), WIDE),
            pltpu.VMEM((both_rows, MODEL), LOW),
            pltpu.VMEM((GROUP, own_rows, 3 * HALF), LOW),
            pltpu.SemaphoreType.DMA(()),
        ],
        far=(0,),
        flops=2 * SEG * MODEL * 3 * MODEL,
    )
    count = count + other_core(count)
    out_half = out_half.reshape(MODEL, HALF)
    out_weight, mixed_full, normed_first, inv_first, first_low = run_kernel(
        out_kernel,
        "seg_out",
        [
            shape_of((MODEL, MODEL), LOW),
            shape_of((both_rows, MODEL), LOW),
            shape_of((SEG, MODEL)),
            shape_of((SEG, 1)),
            shape_of((SEG, MODEL), LOW),
        ],
        where,
        (),
        (hidden_in, mixed, other_core(mixed), out_half, other_core(out_half), vectors),
        [pltpu.VMEM((MODEL, MODEL), LOW), pltpu.SemaphoreType.DMA(())],
        far=(0,),
        flops=2 * SEG * MODEL * MODEL,
    )
    first_got = after(other_core(first_low), count)
    third_x, third_y = after(third_x, first_low), after(third_y, first_low)
    up_weight, act, slope = run_kernel(
        up_kernel,
        "seg_up",
        [
            shape_of((GROUP, own_rows, FF_HALF), LOW),
            shape_of((both_rows, FF_HALF), LOW),
            shape_of((both_rows, FF_HALF)),
        ],
        where,
        (),
        second_line
        + (second_x, second_y, third_x, third_y)
        + (first_low, first_got, vectors),
        [
            pltpu.VMEM((both_rows, MODEL), LOW),
            pltpu.VMEM((both_rows, FF_HALF), WIDE),
            pltpu.SemaphoreType.DMA((FF_HALF // MODEL,)),
        ],
        far=(2,),
        flops=2 * SEG * MODEL * FF,
    )
    fourth_x, fourth_y = sent_both(third_y[:, 2 * size :], third_x[:, size : 2 * size])
    fourth_x, fourth_y = after(fourth_x, act), after(fourth_y, act)
    cls_sent = joined(*cls_line, cls_out_piece)
    cls_sent = after(cls_sent, fourth_x, fourth_y)
    cls_x, cls_y = sent_both(cls_sent, cls_sent)
    down_weight, down_own, down_send = run_kernel(
        down_kernel,
        "seg_down",
        [
            shape_of((GROUP, own_rows, FF_HALF), LOW),
            shape_of((SEG, MODEL)),
            shape_of((SEG, MODEL)),
        ],
        where,
        (),
        third_line + (third_x, third_y, fourth_x, fourth_y) + (act,),
        [pltpu.VMEM((GROUP, own_rows, FF_HALF), LOW), pltpu.SemaphoreType.DMA(())],
        far=(0,),
        flops=2 * SEG * MODEL * FF,
    )
    normed_second, inv_second, diff, out_rows, head_row = run_kernel(
        seg_rows_kernel,
        "seg_rows",
        [
            shape_of((SEG, MODEL)),
            shape_of((SEG, 1)),
            shape_of((SEG, MODEL)),
            shape_of((SEG, MODEL)),
            shape_of((1, 2 * MODEL + LANES)),
        ],
        where,
        (),
        (
            down_own,
            other_core(down_send),
            normed_first,
            vectors,
            targets,
            live_row,
            seg_pos,
        ),
    )
    head_planes = plane_parts(head_row)
    head_lines = line_parts(jnp.concatenate(head_planes))
    size = LINE // 2 * QUARTER_HALF
    cls_far = sent_both(
        after(cls_y[:, size:], *head_planes[1:]), after(cls_x[:, :size], *head_planes[1:])
    )

    second_grad, second_low, second_sums = run_kernel(
        second_norm_kernel,
        "seg_second_norm",
        [shape_of((SEG, MODEL)), shape_of((SEG, MODEL), LOW), shape_of((3, MODEL))],
        where,
        (),
        (diff, count, normed_second, inv_second, vectors),
    )
    cls_half, cls_out_half = run_kernel(
        cls_gather_kernel,
        "head_gather",
        [
            shape_of((GROUP, own_rows, QUARTER_HALF), LOW),
            shape_of((PLANE, own_rows, HALF), LOW),
        ],
        where,
        (),
        cls_line + (cls_x, cls_y) + cls_far + (cls_out_piece,),
    )
    second_got = after(other_core(second_low), head_lines[2], head_lines[3], cls_half)
    pre, first_grad_own, first_grad_send, up_sums = run_kernel(
        mlp_back_kernel,
        "seg_mlp_back",
        [
            shape_of((both_rows, FF_HALF), LOW),
            shape_of((SEG, MODEL)),
            shape_of((SEG, MODEL)),
            shape_of((FF_HALF // MODEL, MODEL)),
        ],
        where,
        (),
        (second_low, second_got, down_weight, up_weight, slope),
        [pltpu.VMEM((both_rows, MODEL), LOW)],
        flops=4 * SEG * MODEL * FF,
    )
    cls_weight, cls_out = run_kernel(
        cls_weight_kernel,
        "head_weight",
        [
            shape_of((GROUP, own_rows, QUARTER), LOW),
            shape_of((4, HEAD_DIM, MODEL), LOW),
        ],
        where,
        (),
        (cls_half, other_core(cls_half), cls_out_half, other_core(cls_out_half)),
    )
    cls_weight = cls_weight.reshape(MODEL, QUARTER)
    cls_out = cls_out.reshape(SPAN, MODEL)
    first_grad_got = other_core(first_grad_send)

    def part_shapes(columns):
        return [
            shape_of((count_of, own_rows, columns), LOW)
            for count_of in (LINE // 2, LINE // 2, LINE, LINE, LINE)
        ]

    mlp_parts = run_kernel(
        mlp_weight_kernel,
        "seg_mlp_weight",
        part_shapes(FF),
        where,
        (),
        (first_low, first_got, second_low, second_got, pre, act),
        [
            pltpu.VMEM((both_rows, MODEL), LOW),
            pltpu.VMEM((GROUP, own_rows, FF), LOW),
            pltpu.SemaphoreType.DMA((GROUP,)),
        ],
        far=range(5),
        flops=4 * SEG * MODEL * FF,
    )
    mlp_far = reduce_far(tuple(after(part, *cls_far) for part in mlp_parts[:2]))
    heads, cls_qkv, cls_mixed, part = run_kernel(
        cls_attend_kernel,
        "head_attend",
        [
            shape_of((GROUP, 2 * MODEL + LANES)),
            shape_of((GROUP, 3 * SPAN), LOW),
            shape_of((GROUP, SPAN), LOW),
            shape_of((GROUP, MODEL)),
        ],
        where,
        (),
        tuple(after(got, mlp_parts[0], first_grad_got) for got in head_lines)
        + (vectors, cls_weight, cls_out),
    )
    cls_normed, cls_inv, cls_low, cls_act, cls_slope, part = run_kernel(
        cls_mlp_kernel,
        "head_mlp",
        [
            shape_of((GROUP, MODEL)),
            shape_of((GROUP, 1)),
            shape_of((GROUP, MODEL), LOW),
            shape_of((GROUP, FF // LINE), LOW),
            shape_of((GROUP, FF // LINE)),
            shape_of((GROUP, MODEL)),
        ],
        where,
        (),
        (heads,) + line_parts(part) + (vectors, cls_weight),
    )
    cls_parts = line_parts(part)
    mlp_far = tuple(after(got, cls_low) for got in mlp_far)
    mlp_sent = reduce_add(where, mlp_parts, mlp_far)
    mlp_plane = sent_both(*mlp_sent)
    top_row, square, cls_grad, cls_second, cls_pre, part, top_sums = run_kernel(
        cls_top_kernel,
        "head_top",
        [
            shape_of((1, MODEL)),
            shape_of((8, LANES)),
            shape_of((GROUP, MODEL)),
            shape_of((GROUP, MODEL), LOW),
            shape_of((GROUP, FF // LINE), LOW),
            shape_of((GROUP, MODEL)),
            shape_of((2, MODEL)),
        ],
        where,
        (),
        (heads, cls_parts[0], cls_parts[1])
        + tuple(after(got, *mlp_sent) for got in cls_parts[2:])
        + (vectors, cls_weight, cls_normed, count, cls_slope),
        [pltpu.VMEM((GROUP, MODEL), WIDE)],
    )
    cls_grad, cls_branch, cls_proj, part, back_sums = run_kernel(
        cls_attend_back_kernel,
        "head_attend_back",
        [
            shape_of((GROUP, MODEL)),
            shape_of((GROUP, MODEL), LOW),
            shape_of((GROUP, 3 * SPAN), LOW),
            shape_of((GROUP, MODEL)),
            shape_of((2, MODEL)),
        ],
        where,
        (),
        (heads,)
        + line_parts(part)
        + (vectors, cls_weight, cls_out, cls_grad, cls_normed, cls_inv, cls_qkv),
    )
    dheads, head_grad, shared = run_kernel(
        cls_end_kernel,
        "head_end",
        [shape_of((1, MODEL)), shape_of((1, MODEL)), shape_of((GROUP + 8, MODEL))],
        where,
        (),
        (heads, cls_grad)
        + line_parts(part)
        + (square, back_sums, top_sums, normed_second, inv_second, vectors),
        [pltpu.VMEM((GROUP, MODEL), WIDE)],
    )

    head_own, head_send, head_data = run_kernel(
        head_back_kernel,
        "seg_head_back",
        [shape_of((1, MODEL)), shape_of((1, MODEL)), shape_of((12, MODEL))],
        where,
        (),
        (
            head_grad,
            other_core(head_grad),
            down_weight,
            up_weight,
            slope,
            act,
            first_low,
            first_got,
        ),
    )
    grad_summed, branch, mixed_grad, attn_send, first_sums = run_kernel(
        first_norm_kernel,
        "seg_first_norm",
        [
            shape_of((SEG, MODEL)),
            shape_of((SEG, MODEL), LOW),
            shape_of((SEG, MODEL), LOW),
            shape_of((SEG, MODEL), LOW),
            shape_of((3, MODEL)),
        ],
        where,
        (),
        (
            second_grad,
            first_grad_own,
            first_grad_got,
            head_grad,
            head_own,
            other_core(head_send),
            normed_first,
            inv_first,
            vectors,
            out_weight,
        ),
    )
    pack = jnp.concatenate([cls_proj, cls_mixed, cls_pre, cls_act], axis=1)
    mlp_plane = [after(got, branch) for got in mlp_plane]
    mlp_own, *mlp_sent = reduce_fold(where, mlp_parts[4], mlp_plane, pack)
    mlp_got = [along_line(mlp_sent[apart - 1], apart) for apart in range(1, LINE)]
    shared = shared + other_core(shared)
    attn_got = after(other_core(attn_send), mlp_own, shared)
    proj, input_own, input_send, payload = run_kernel(
        attn_back_kernel,
        "seg_attn_back",
        [
            shape_of((both_rows, 3 * HALF), LOW),
            shape_of((SEG, MODEL)),
            shape_of((SEG, MODEL)),
            shape_of((24, MODEL), LOW),
        ],
        where,
        (),
        (
            qkv,
            mixed_grad,
            attn_got,
            live_row,
            live_got,
            qkv_weight,
            first_sums,
            second_sums,
            up_sums,
            dheads,
            normed_second,
            head_data,
        ),
        [pltpu.VMEM((24, MODEL), WIDE)],
        flops=4 * SEG * MODEL * 3 * MODEL,
    )
    attn_parts = run_kernel(
        attn_weight_kernel,
        "seg_attn_weight",
        part_shapes(4 * HALF),
        where,
        (),
        (hidden_in, hidden_got, mixed_full, proj, branch, attn_got),
        [
            pltpu.VMEM((both_rows, MODEL), LOW),
            pltpu.VMEM((both_rows, HALF), LOW),
            pltpu.VMEM((GROUP, own_rows, 4 * HALF), LOW),
            pltpu.SemaphoreType.DMA((GROUP,)),
        ],
        far=range(5),
        flops=4 * SEG * MODEL * 2 * MODEL,
    )
    attn_far = reduce_far(tuple(after(part, mlp_got[-1]) for part in attn_parts[:2]))
    input_grad = (grad_summed + input_own + other_core(input_send)).astype(LOW)
    row_at = jnp.arange(SEG)[:, None]
    output = jnp.where(row_at == 0, top_row * live_row[:, :1], out_rows).astype(LOW)
    payload_parts = line_parts(after(payload, attn_parts[0]))
    attn_far = tuple(after(got, payload_parts[1]) for got in attn_far)
    attn_sent = reduce_add(where, attn_parts, attn_far)
    attn_plane = sent_both(*(after(part, mlp_got[1]) for part in attn_sent))
    mlp_got = [after(got, attn_plane[0]) for got in mlp_got]
    mlp_sum = reduce_line(mlp_own, mlp_got)
    payload_line = jnp.concatenate(payload_parts)
    mlp_mine, own_vecs = run_kernel(
        head_share_kernel,
        "seg_head_share",
        [shape_of((own_rows, FF)), shape_of((16, MODEL))],
        where,
        (),
        plane_parts(after(payload_line, *attn_plane)) + (mlp_sum,),
        [pltpu.VMEM((GROUP * 24, MODEL), LOW)],
    )
    attn_own, *attn_sent = reduce_fold(where, attn_parts[4], attn_plane)
    attn_sum = reduce_line(
        attn_own, [along_line(attn_sent[apart - 1], apart) for apart in range(1, LINE)]
    )
    flat = pltpu.VMEM((1, 8 * MODEL + FF), WIDE)
    seg_mats_grad, seg_vec_grad = run_kernel(
        seg_owner_kernel,
        "seg_owner",
        [shape_of((own_rows, total_columns)), shape_of((1, vec_size))],
        where,
        (),
        (attn_sum, other_core(attn_sum), mlp_mine, other_core(mlp_mine))
        + (own_vecs, other_core(own_vecs)),
        [flat],
    )

    row_width = 8 * MODEL + 2 * FF
    cls_rows = run_kernel(
        cls_rows_kernel,
        "head_rows",
        [shape_of((GROUP, row_width), LOW)],
        where,
        (),
        (pack,) + tuple(mlp_got) + (heads, cls_branch, cls_low, cls_second),
        [pltpu.VMEM((LINE,) + pack.shape, LOW)],
    )[0]
    cls_mats_grad, cls_vec_grad = run_kernel(
        cls_owner_kernel,
        "head_owner",
        [shape_of((own_rows, total_columns)), shape_of((1, vec_size))],
        where,
        (),
        (cls_rows, other_core(cls_rows), shared),
        [pltpu.VMEM((CORES * GROUP, row_width), LOW), flat],
        flops=64 * own_rows * total_columns,
    )
    pos_total = shared[:GROUP]
    loss_value = shared[GROUP, 0] / (count[0, 0] * MODEL)

    return (
        output,
        input_grad,
        seg_mats_grad,
        seg_vec_grad.reshape(vec_size),
        cls_mats_grad,
        cls_vec_grad.reshape(vec_size),
        pos_total,
        loss_value,
    )


def solution(mesh):
    in_specs = (
        P(("rep", "fsdp"), None),
        P(("rep", "fsdp"), None),
        P(("rep", "fsdp")),
        P(("rep", "fsdp")),
        P(("rep", "fsdp")),
        P("fsdp", None),
        P("fsdp"),
        P("fsdp", None),
        P("fsdp"),
        P(),
    )
    out_specs = (
        P(("rep", "fsdp"), None),
        P(("rep", "fsdp"), None),
        P("fsdp", None),
        P("fsdp"),
        P("fsdp", None),
        P("fsdp"),
        P(),
        P(),
    )
    one_slice = dict(mesh.shape) == {"rep": CORES, "fsdp": LINE * PLANE}
    body = slice_local if one_slice else local
    return jax.shard_map(body, mesh=mesh, in_specs=in_specs, out_specs=out_specs, check_vma=False)
```

```python
import math

import jax
import jax.numpy as jnp
from jax import lax
from jax.experimental import pallas as pl
from jax.experimental.pallas import tpu as pltpu
from jax.sharding import PartitionSpec as P

HEADS = 12
HEAD_DIM = 64
FF = 3072
SEG = 128
SEQ = 2048


NORM_EPS = 1e-05
MASK_FILL = -1e30
SQRT_HALF = 0.7071067811865476
INV_SQRT_TWO_PI = 0.3989422804014327


def swapped(value, axis, apart):
    mask = 2**apart
    pairs = [(source, source ^ mask) for source in range(lax.axis_size(axis))]
    return lax.ppermute(value, axis, pairs)


def product_plain(left_side, right_side):
    return jnp.dot(left_side, right_side, preferred_element_type=jnp.float32)


def product_left(left_side, right_side):
    return lax.dot_general(
        left_side, right_side, (((0,), (0,)), ((), ())), preferred_element_type=jnp.float32
    )


def product_right(left_side, right_side):
    return lax.dot_general(
        left_side, right_side, (((1,), (1,)), ((), ())), preferred_element_type=jnp.float32
    )


def row_total(array_in):
    return jnp.sum(array_in.astype(jnp.float32), axis=0)


def unpack_weights(gathered, model_width, ff_width):
    matrix, vector = gathered
    vector = vector.astype(jnp.float32)
    pieces = tuple(
        (vector[offset * model_width : (offset + 1) * model_width] for offset in range(8))
    )
    return (
        (
            matrix[:, : 3 * model_width],
            matrix[:, 3 * model_width : 4 * model_width],
            matrix[:, 4 * model_width : 4 * model_width + ff_width],
            matrix[:, 4 * model_width + ff_width :],
        )
        + pieces
        + (vector[8 * model_width :],)
    )


def norm_forward(summed, gain_vec, shift_vec):
    row_mean = jnp.mean(summed, axis=-1, keepdims=True)
    centered = summed - row_mean
    inv_dev = lax.rsqrt(jnp.mean(centered * centered, axis=-1, keepdims=True) + NORM_EPS)
    normed = centered * inv_dev
    return (normed * gain_vec + shift_vec, normed, inv_dev)


def norm_backward(grad_out, normed, inv_dev, gain_vec):
    scaled = grad_out * gain_vec
    mean_one = jnp.mean(scaled, axis=-1, keepdims=True)
    mean_two = jnp.mean(scaled * normed, axis=-1, keepdims=True)
    grad_in = inv_dev * (scaled - mean_one - normed * mean_two)
    return (grad_in, jnp.sum(grad_out * normed, axis=0), jnp.sum(grad_out, axis=0))


def gelu_value(before):
    return 0.5 * before * (1.0 + lax.erf(before * SQRT_HALF))


def gelu_slope(before):
    return (
        0.5 * (1.0 + lax.erf(before * SQRT_HALF))
        + before * jnp.exp(-0.5 * before * before) * INV_SQRT_TWO_PI
    )


def attention_scores(queries, keys_in, allowed, score_scale):
    raw_scores = (
        jnp.einsum("bqhe,bkhe->bhqk", queries, keys_in, preferred_element_type=jnp.float32)
        * score_scale
    )
    return jnp.where(allowed, raw_scores, MASK_FILL)


def attention_forward(queries, keys_in, values, allowed, score_scale):
    scores = attention_scores(queries, keys_in, allowed, score_scale)
    row_top = jnp.max(scores, axis=-1, keepdims=True)
    log_total = row_top + jnp.log(jnp.sum(jnp.exp(scores - row_top), axis=-1, keepdims=True))
    weights = jnp.exp(scores - log_total).astype(jnp.bfloat16)
    mixed_rows = jnp.einsum("bhqk,bkhe->bqhe", weights, values, preferred_element_type=jnp.float32)
    return (mixed_rows, log_total)


def attention_backward(queries, keys_in, values, allowed, score_scale, log_total, grad_mixed):
    probabilities = jnp.exp(attention_scores(queries, keys_in, allowed, score_scale) - log_total)
    grad_probs = jnp.einsum(
        "bqhe,bkhe->bhqk", grad_mixed, values, preferred_element_type=jnp.float32
    )
    inner_sum = jnp.sum(grad_probs * probabilities, axis=-1, keepdims=True)
    grad_scores = (probabilities * (grad_probs - inner_sum)).astype(jnp.bfloat16)
    grad_query = (
        jnp.einsum("bhqk,bkhe->bqhe", grad_scores, keys_in, preferred_element_type=jnp.float32)
        * score_scale
    )
    grad_key = (
        jnp.einsum("bhqk,bqhe->bkhe", grad_scores, queries, preferred_element_type=jnp.float32)
        * score_scale
    )
    grad_value = jnp.einsum(
        "bhqk,bqhe->bkhe",
        probabilities.astype(jnp.bfloat16),
        grad_mixed,
        preferred_element_type=jnp.float32,
    )
    return (grad_query, grad_key, grad_value)


def block_forward(rows_in, unpacked, attend):
    (
        qkv_weight,
        out_weight,
        up_weight,
        down_weight,
        query_bias,
        value_bias,
        out_bias,
        down_bias,
        gain_first,
        shift_first,
        gain_second,
        shift_second,
        up_bias,
    ) = unpacked
    model_width = rows_in.shape[1]
    inputs = rows_in.astype(jnp.bfloat16)
    projected = product_plain(inputs, qkv_weight)
    queries = (projected[:, :model_width] + query_bias).astype(jnp.bfloat16)
    keys_in = projected[:, model_width : 2 * model_width].astype(jnp.bfloat16)
    values = (projected[:, 2 * model_width :] + value_bias).astype(jnp.bfloat16)
    mixed_rows, attend_kept = attend(queries, keys_in, values)
    mixed_rows = mixed_rows.astype(jnp.bfloat16)
    summed_first = rows_in + product_plain(mixed_rows, out_weight) + out_bias
    first_out, normed_first, inv_first = norm_forward(summed_first, gain_first, shift_first)
    first_low = first_out.astype(jnp.bfloat16)
    pre_act = product_plain(first_low, up_weight) + up_bias
    activated = gelu_value(pre_act).astype(jnp.bfloat16)
    summed_second = first_out + product_right(activated, down_weight) + down_bias
    block_out, normed_second, inv_second = norm_forward(summed_second, gain_second, shift_second)
    saved_state = (
        inputs,
        queries,
        keys_in,
        values,
        attend_kept,
        mixed_rows,
        normed_first,
        inv_first,
        first_low,
        pre_act,
        activated,
        normed_second,
        inv_second,
    )
    return (block_out, saved_state)


def block_backward(grad_out, unpacked, saved_state, attend_back):
    (
        qkv_weight,
        out_weight,
        up_weight,
        down_weight,
        query_bias,
        value_bias,
        out_bias,
        down_bias,
        gain_first,
        shift_first,
        gain_second,
        shift_second,
        up_bias,
    ) = unpacked
    (
        inputs,
        queries,
        keys_in,
        values,
        attend_kept,
        mixed_rows,
        normed_first,
        inv_first,
        first_low,
        pre_act,
        activated,
        normed_second,
        inv_second,
    ) = saved_state
    grad_second, grad_gain_second, grad_shift_second = norm_backward(
        grad_out, normed_second, inv_second, gain_second
    )
    second_low = grad_second.astype(jnp.bfloat16)
    grad_pre = (product_plain(second_low, down_weight) * gelu_slope(pre_act)).astype(jnp.bfloat16)
    grad_first = grad_second + product_right(grad_pre, up_weight)
    grad_summed, grad_gain_first, grad_shift_first = norm_backward(
        grad_first, normed_first, inv_first, gain_first
    )
    branch_low = grad_summed.astype(jnp.bfloat16)
    grad_mixed = product_right(branch_low, out_weight).astype(jnp.bfloat16)
    grad_query, grad_key, grad_value = attend_back(
        queries, keys_in, values, attend_kept, grad_mixed
    )
    grad_proj = jnp.concatenate([grad_query, grad_key, grad_value], axis=1)
    grad_rows = grad_summed + product_right(grad_proj, qkv_weight)
    vector_grad = jnp.concatenate(
        [
            row_total(grad_query),
            row_total(grad_value),
            row_total(branch_low),
            row_total(second_low),
            grad_gain_first,
            grad_shift_first,
            grad_gain_second,
            grad_shift_second,
            row_total(grad_pre),
        ]
    )
    weight_rows = (
        inputs,
        grad_proj,
        mixed_rows,
        branch_low,
        first_low,
        grad_pre,
        second_low,
        activated,
    )
    return (grad_rows, weight_rows, vector_grad)


def weight_products(weight_rows):
    inputs, grad_proj, mixed_rows, branch_low, first_low, grad_pre, second_low, activated = (
        weight_rows
    )
    return (
        product_left(inputs, grad_proj),
        product_left(mixed_rows, branch_low),
        product_left(first_low, grad_pre),
        product_left(second_low, activated),
    )


def local(
    hidden_in,
    targets,
    doc_ids,
    seg_nums,
    valid_flags,
    seg_mats,
    seg_vecs,
    cls_mats,
    cls_vecs,
    seg_pos,
):
    tok_rows, model_width = hidden_in.shape
    ff_width = FF
    seg_len = SEG
    group_span = SEQ // tok_rows
    seg_count = tok_rows // seg_len
    score_scale = HEAD_DIM ** (-0.5)
    head_shape = (HEADS, HEAD_DIM)
    live_rows = valid_flags.astype(jnp.float32)
    rank_full = lax.axis_index("fsdp")
    seg_gathered = (
        lax.all_gather(seg_mats, "fsdp", axis=0, tiled=True),
        lax.all_gather(seg_vecs, "fsdp", axis=0, tiled=True),
    )
    seg_unpacked = unpack_weights(seg_gathered, model_width, ff_width)
    cls_gathered = (
        lax.all_gather(cls_mats, "fsdp", axis=0, tiled=True),
        lax.all_gather(cls_vecs, "fsdp", axis=0, tiled=True),
    )
    cls_unpacked = unpack_weights(cls_gathered, model_width, ff_width)
    seg_allowed = (live_rows.reshape(seg_count, 1, 1, seg_len) > 0.5) | jnp.eye(seg_len, dtype=bool)
    seg_shape = (seg_count, seg_len) + head_shape

    def seg_attend(queries, keys_in, values):
        mixed_rows, log_total = attention_forward(
            queries.reshape(seg_shape),
            keys_in.reshape(seg_shape),
            values.reshape(seg_shape),
            seg_allowed,
            score_scale,
        )
        return (mixed_rows.reshape(tok_rows, model_width), log_total)

    def seg_attend_back(queries, keys_in, values, log_total, grad_mixed):
        grad_parts = attention_backward(
            queries.reshape(seg_shape),
            keys_in.reshape(seg_shape),
            values.reshape(seg_shape),
            seg_allowed,
            score_scale,
            log_total,
            grad_mixed.reshape(seg_shape),
        )
        return tuple(
            (
                grad_part.reshape(tok_rows, model_width).astype(jnp.bfloat16)
                for grad_part in grad_parts
            )
        )

    first_out, seg_saved = block_forward(hidden_in.astype(jnp.float32), seg_unpacked, seg_attend)
    first_grid = first_out.reshape(seg_count, seg_len, model_width)
    position_hot = (seg_nums[:, None] == jnp.arange(seg_pos.shape[0])[None, :]).astype(jnp.float32)
    position_rows = jnp.sum(
        position_hot[:, :, None] * seg_pos.astype(jnp.float32)[None, :, :], axis=1
    )
    heads_in = first_grid[:, 0, :] + position_rows
    lead_live = live_rows.reshape(seg_count, seg_len)[:, 0]
    lead_doc = doc_ids.reshape(seg_count, seg_len)[:, 0]
    lead_labels = jnp.where(lead_live > 0.5, lead_doc, -1).astype(jnp.bfloat16)
    lead_doc_low = lead_doc.astype(jnp.bfloat16)
    bit_count = group_span.bit_length() - 1
    key_total = group_span * seg_count
    own_slot = rank_full % group_span * seg_count + jnp.arange(seg_count)
    query_shape = (1, seg_count) + head_shape
    key_shape = (1, key_total) + head_shape

    def cls_attend(queries, keys_in, values):
        paired = jnp.concatenate([keys_in, values], axis=1)
        labels = lead_labels
        for bit_level in range(bit_count):
            other_pair, other_labels = swapped((paired, labels), "fsdp", bit_level)
            upper_half = rank_full // (1 << bit_level) % 2 == 1
            paired = jnp.where(
                upper_half,
                jnp.concatenate([other_pair, paired]),
                jnp.concatenate([paired, other_pair]),
            )
            labels = jnp.where(
                upper_half,
                jnp.concatenate([other_labels, labels]),
                jnp.concatenate([labels, other_labels]),
            )
        allowed = (labels[None, :] == lead_doc_low[:, None]) | (
            jnp.arange(key_total)[None, :] == own_slot[:, None]
        )
        allowed = allowed[None, None]
        mixed_rows, log_total = attention_forward(
            queries.reshape(query_shape),
            paired[:, :model_width].reshape(key_shape),
            paired[:, model_width:].reshape(key_shape),
            allowed,
            score_scale,
        )
        return (mixed_rows.reshape(seg_count, model_width), (paired, allowed, log_total))

    def cls_attend_back(queries, keys_in, values, attend_kept, grad_mixed):
        paired, allowed, log_total = attend_kept
        grad_query, grad_key, grad_value = attention_backward(
            queries.reshape(query_shape),
            paired[:, :model_width].reshape(key_shape),
            paired[:, model_width:].reshape(key_shape),
            allowed,
            score_scale,
            log_total,
            grad_mixed.reshape(query_shape),
        )
        grad_pair = jnp.concatenate(
            [grad_key.reshape(key_total, model_width), grad_value.reshape(key_total, model_width)],
            axis=1,
        )
        for bit_level in reversed(range(bit_count)):
            half_rows = grad_pair.shape[0] // 2
            upper_half = rank_full // (1 << bit_level) % 2 == 1
            kept_half = jnp.where(upper_half, grad_pair[half_rows:], grad_pair[:half_rows])
            sent_half = jnp.where(upper_half, grad_pair[:half_rows], grad_pair[half_rows:])
            grad_pair = kept_half + swapped(
                sent_half.astype(jnp.bfloat16), "fsdp", bit_level
            ).astype(sent_half.dtype)
        grad_pair = grad_pair.astype(jnp.bfloat16)
        return (
            grad_query.reshape(seg_count, model_width).astype(jnp.bfloat16),
            grad_pair[:, :model_width],
            grad_pair[:, model_width:],
        )

    top_out, cls_saved = block_forward(heads_in, cls_unpacked, cls_attend)
    combined = jnp.concatenate([top_out[:, None, :], first_grid[:, 1:, :]], axis=1).reshape(
        tok_rows, model_width
    )
    output_rows = combined * live_rows[:, None]
    diff_rows = (output_rows - targets.astype(jnp.float32)) * live_rows[:, None]
    count_all, square_all = lax.psum(
        (jnp.sum(live_rows), jnp.sum(diff_rows * diff_rows)), ("rep", "fsdp")
    )
    loss_value = square_all / (count_all * model_width)
    slots_all = tok_rows * lax.axis_size("rep") * lax.axis_size("fsdp")
    grad_grid = (diff_rows * (slots_all / count_all)).reshape(seg_count, seg_len, model_width)
    cls_back = unpack_weights(
        (
            lax.all_gather(cls_mats, "fsdp", axis=0, tiled=True),
            lax.all_gather(cls_vecs, "fsdp", axis=0, tiled=True),
        ),
        model_width,
        ff_width,
    )
    heads_grad, cls_weight_rows, cls_g_vec = block_backward(
        grad_grid[:, 0, :], cls_back, cls_saved, cls_attend_back
    )
    cls_g_qkv, cls_g_out, cls_g_up, cls_g_down = weight_products(cls_weight_rows)
    pos_local = jnp.sum(position_hot[:, :, None] * heads_grad[:, None, :], axis=0)
    seg_grad_out = jnp.concatenate([heads_grad[:, None, :], grad_grid[:, 1:, :]], axis=1).reshape(
        tok_rows, model_width
    )
    seg_back = unpack_weights(
        (
            lax.all_gather(seg_mats, "fsdp", axis=0, tiled=True),
            lax.all_gather(seg_vecs, "fsdp", axis=0, tiled=True),
        ),
        model_width,
        ff_width,
    )
    input_grad, seg_weight_rows, seg_g_vec = block_backward(
        seg_grad_out, seg_back, seg_saved, seg_attend_back
    )
    seg_g_qkv, seg_g_out, seg_g_up, seg_g_down = weight_products(seg_weight_rows)
    owner_rows = tuple(
        (
            lax.psum_scatter(seg_g_qkv, "fsdp", scatter_dimension=0, tiled=True),
            lax.psum_scatter(seg_g_out, "fsdp", scatter_dimension=0, tiled=True),
            lax.psum_scatter(seg_g_up, "fsdp", scatter_dimension=0, tiled=True),
            lax.psum_scatter(seg_g_down, "fsdp", scatter_dimension=0, tiled=True),
            lax.psum_scatter(seg_g_vec, "fsdp", scatter_dimension=0, tiled=True),
            lax.psum_scatter(cls_g_qkv, "fsdp", scatter_dimension=0, tiled=True),
            lax.psum_scatter(cls_g_out, "fsdp", scatter_dimension=0, tiled=True),
            lax.psum_scatter(cls_g_up, "fsdp", scatter_dimension=0, tiled=True),
            lax.psum_scatter(cls_g_down, "fsdp", scatter_dimension=0, tiled=True),
            lax.psum_scatter(cls_g_vec, "fsdp", scatter_dimension=0, tiled=True),
        )
    )
    replica_share = (
        lax.psum_scatter(
            owner_rows[0].astype(jnp.bfloat16), "rep", scatter_dimension=1, tiled=True
        ).astype(jnp.float32),
        lax.psum_scatter(
            owner_rows[1].astype(jnp.bfloat16), "rep", scatter_dimension=1, tiled=True
        ).astype(jnp.float32),
        lax.psum_scatter(
            owner_rows[2].astype(jnp.bfloat16), "rep", scatter_dimension=1, tiled=True
        ).astype(jnp.float32),
        lax.psum_scatter(
            owner_rows[3].astype(jnp.bfloat16), "rep", scatter_dimension=1, tiled=True
        ).astype(jnp.float32),
        lax.psum_scatter(
            owner_rows[4].astype(jnp.bfloat16), "rep", scatter_dimension=0, tiled=True
        ).astype(jnp.float32),
        lax.psum_scatter(
            owner_rows[5].astype(jnp.bfloat16), "rep", scatter_dimension=1, tiled=True
        ).astype(jnp.float32),
        lax.psum_scatter(
            owner_rows[6].astype(jnp.bfloat16), "rep", scatter_dimension=1, tiled=True
        ).astype(jnp.float32),
        lax.psum_scatter(
            owner_rows[7].astype(jnp.bfloat16), "rep", scatter_dimension=1, tiled=True
        ).astype(jnp.float32),
        lax.psum_scatter(
            owner_rows[8].astype(jnp.bfloat16), "rep", scatter_dimension=1, tiled=True
        ).astype(jnp.float32),
        lax.psum_scatter(
            owner_rows[9].astype(jnp.bfloat16), "rep", scatter_dimension=0, tiled=True
        ).astype(jnp.float32),
    )
    all_summed = (
        lax.all_gather(replica_share[0].astype(jnp.bfloat16), "rep", axis=1, tiled=True).astype(
            jnp.float32
        ),
        lax.all_gather(replica_share[1].astype(jnp.bfloat16), "rep", axis=1, tiled=True).astype(
            jnp.float32
        ),
        lax.all_gather(replica_share[2].astype(jnp.bfloat16), "rep", axis=1, tiled=True).astype(
            jnp.float32
        ),
        lax.all_gather(replica_share[3].astype(jnp.bfloat16), "rep", axis=1, tiled=True).astype(
            jnp.float32
        ),
        lax.all_gather(replica_share[4].astype(jnp.bfloat16), "rep", axis=0, tiled=True).astype(
            jnp.float32
        ),
        lax.all_gather(replica_share[5].astype(jnp.bfloat16), "rep", axis=1, tiled=True).astype(
            jnp.float32
        ),
        lax.all_gather(replica_share[6].astype(jnp.bfloat16), "rep", axis=1, tiled=True).astype(
            jnp.float32
        ),
        lax.all_gather(replica_share[7].astype(jnp.bfloat16), "rep", axis=1, tiled=True).astype(
            jnp.float32
        ),
        lax.all_gather(replica_share[8].astype(jnp.bfloat16), "rep", axis=1, tiled=True).astype(
            jnp.float32
        ),
        lax.all_gather(replica_share[9].astype(jnp.bfloat16), "rep", axis=0, tiled=True).astype(
            jnp.float32
        ),
    )
    seg_summed = all_summed[:5]
    cls_summed = all_summed[5:]
    pos_total = lax.psum(pos_local, ("rep", "fsdp"))
    seg_mat_grad = jnp.concatenate(
        [seg_summed[0], seg_summed[1], seg_summed[2], seg_summed[3]], axis=1
    )
    cls_mat_grad = jnp.concatenate(
        [cls_summed[0], cls_summed[1], cls_summed[2], cls_summed[3]], axis=1
    )
    return (
        output_rows.astype(jnp.bfloat16),
        input_grad.astype(jnp.bfloat16),
        seg_mat_grad,
        seg_summed[4],
        cls_mat_grad,
        cls_summed[4],
        pos_total,
        loss_value,
    )


LINE = 4
PLANE = 4
CORES = 2
LANES = 128
GROUP = LINE * PLANE
LOW, WIDE = jnp.bfloat16, jnp.float32
MODEL = HEADS * HEAD_DIM
SPAN = 2 * LANES
TILE_START = (0, 1, 3, 4)


def line_pairs(apart):
    return [(source, (source + apart * PLANE) % GROUP) for source in range(GROUP)]


def plane_pairs(mask):
    return [(source, source ^ mask) for source in range(GROUP)]


def along_line(value, apart):
    return lax.ppermute(value, "fsdp", line_pairs(apart))


def in_plane(value, mask):
    return lax.ppermute(value, "fsdp", plane_pairs(mask))


def other_core(value):
    return lax.ppermute(value, "rep", [(0, 1), (1, 0)])


def after(value, *events):
    return lax.optimization_barrier((value,) + events)[0]


def shape_of(dims, dtype=WIDE):
    return jax.ShapeDtypeStruct(dims, dtype)


def run_kernel(body, name, outs, where, blocks, arrays, scratch=(), far=(), flops=0):
    in_specs = [pl.BlockSpec(memory_space=pltpu.SMEM)]
    in_specs += [pl.BlockSpec(memory_space=pltpu.HBM)] * len(blocks)
    in_specs += [pl.BlockSpec(memory_space=pltpu.VMEM)] * len(arrays)
    spaces = [pltpu.HBM if at in far else pltpu.VMEM for at in range(len(outs))]
    moved = sum(x.size * x.dtype.itemsize for x in list(blocks) + list(arrays))
    moved += sum(math.prod(o.shape) * jnp.dtype(o.dtype).itemsize for o in outs)
    return pl.pallas_call(
        body,
        name=name,
        out_shape=tuple(outs),
        in_specs=in_specs,
        out_specs=tuple(pl.BlockSpec(memory_space=space) for space in spaces),
        scratch_shapes=list(scratch),
        cost_estimate=pl.CostEstimate(flops=flops, bytes_accessed=moved, transcendentals=0),
        compiler_params=pltpu.CompilerParams(vmem_limit_bytes=VMEM_BYTES),
    )(where, *blocks, *arrays)


VMEM_BYTES = 24 * 1024 * 1024
HALF = MODEL // CORES
FF_HALF = FF // CORES
OWN = MODEL // GROUP
QUARTER = 3 * SPAN + 2 * FF // LINE
QUARTER_HALF = QUARTER // CORES


def aligned(start):
    return pl.multiple_of(start, LANES)


def wait_all(copies):
    for copy in copies:
        copy.wait()


def run_copies(pairs, sems):
    copies = [
        pltpu.make_async_copy(source, target, sems.at[at])
        for at, (source, target) in enumerate(pairs)
    ]
    for copy in copies:
        copy.start()
    wait_all(copies)


def gather_blocks(where, refs, base, width, targets):
    line_at, plane_at = where[0], where[1]
    half = LINE // 2
    for mask in range(PLANE):
        for step in range(LINE):
            if mask == 0:
                ref, offset = refs[step], 0
            elif mask == 3:
                ref = refs[LINE + 3] if step < half else refs[LINE + 2]
                offset = step % half * width
            else:
                ref, offset = refs[LINE + mask - 1], base + step * width
            chip = (line_at + LINE - step) % LINE * PLANE + (plane_at ^ mask)
            for whole, first, last in targets:
                whole[chip] = ref[:, offset + first : offset + last]


def whole_rows(ref):
    value = ref[...]
    return value.reshape(value.shape[0] * value.shape[1], value.shape[2])


def prepare_first_kernel(where, seg, vecs, flags, out, live_out, sems):
    core_at = where[2]
    pairs = []
    for piece in range(4):
        source = seg.at[:, pl.ds(aligned(piece * MODEL + core_at * HALF), HALF)]
        pairs.append((source, out.at[:, piece * HALF : (piece + 1) * HALF]))
    run_copies(pairs, sems)
    size = vecs.shape[1]
    lines = -(-size // LANES)
    block = jnp.zeros((OWN, LANES), WIDE)
    row_at = lax.broadcasted_iota(jnp.int32, (OWN, LANES), 0)
    for which in range(2):
        for line in range(lines):
            width = min(LANES, size - line * LANES)
            value = vecs[which : which + 1, line * LANES : line * LANES + width]
            if width < LANES:
                value = jnp.concatenate([value, jnp.zeros((1, LANES - width), WIDE)], axis=1)
            block = jnp.where(row_at == which * lines + line, value, block)
    live = flags[...].astype(WIDE)
    live_out[...] = live
    count = jnp.sum(live, axis=1, keepdims=True)
    block = jnp.where(row_at == 2 * lines, count, block)
    out[:, 4 * HALF :] = block.astype(LOW)


def prepare_rest_kernel(where, seg, cls, *refs):
    second_out, third_out = refs[:2]
    step_outs, out_half, order_out = refs[2 : 2 + LINE], refs[2 + LINE], refs[3 + LINE]
    quarters, sems = refs[4 + LINE :]
    line_at, plane_at, core_at = where[0], where[1], where[2]
    start = core_at * FF_HALF
    pairs = [
        (seg.at[:, pl.ds(aligned(4 * MODEL + start), FF_HALF)], second_out),
        (seg.at[:, pl.ds(aligned(4 * MODEL + FF + start), FF_HALF)], third_out),
        (cls.at[:, pl.ds(aligned(3 * MODEL + core_at * HALF), HALF)], out_half),
    ]
    part = FF // LINE
    for at in range(LINE):
        first = TILE_START[at] * LANES
        plan = [(piece * MODEL + first, SPAN, piece * SPAN) for piece in range(3)]
        plan += [
            (4 * MODEL + piece * FF + at * part, part, 3 * SPAN + piece * part)
            for piece in range(2)
        ]
        for source, size, target in plan:
            pairs.append(
                (
                    cls.at[:, source : source + size],
                    quarters.at[at, :, target : target + size],
                )
            )
    run_copies(pairs, sems)
    lanes = pl.ds(aligned(core_at * QUARTER_HALF), QUARTER_HALF)
    for step, out in enumerate(step_outs):
        out[...] = quarters[(line_at + step) % LINE, :, lanes]
    column = lax.broadcasted_iota(jnp.int32, (1, SPAN), 1)
    feature = lax.broadcasted_iota(jnp.int32, (MODEL, SPAN), 0)
    turn = sum((column >= OWN * step).astype(jnp.int32) for step in range(1, LINE))
    held = column - OWN * turn
    turn = (line_at + turn) % LINE
    for mask in range(PLANE):
        source = (turn * PLANE + (plane_at ^ mask)) * OWN + held
        source = jnp.where(column < OWN * LINE, source, -1)
        order_out[:, mask * SPAN : (mask + 1) * SPAN] = (feature == source).astype(LOW)


def lane_mask(rows, head):
    lane = lax.broadcasted_iota(jnp.int32, (rows, LANES), 1)
    return (lane < HEAD_DIM) if head == 0 else (lane >= HEAD_DIM)


def masked(value, mask):
    return jnp.where(mask, value, jnp.zeros_like(value))


def head_probabilities(query, key, allowed):
    scores = product_right(query, key) * HEAD_DIM ** (-0.5)
    scores = jnp.where(allowed, scores, MASK_FILL)
    raised = jnp.exp(scores - jnp.max(scores, axis=-1, keepdims=True))
    return raised / jnp.sum(raised, axis=-1, keepdims=True)


def attend_tiles(qkv, width, allowed):
    rows = qkv.shape[0]
    mixed = []
    for tile in range(width // LANES):
        at = tile * LANES
        query, key, value = (
            qkv[:, piece * width + at : piece * width + at + LANES] for piece in range(3)
        )
        total = jnp.zeros((rows, LANES), WIDE)
        for head in range(2):
            mask = lane_mask(rows, head)
            weights = head_probabilities(masked(query, mask), key, allowed).astype(LOW)
            total = total + product_plain(weights, masked(value, mask))
        mixed.append(total.astype(LOW))
    return mixed


def attend_tiles_back(qkv, grad_mixed, width, allowed):
    rows = qkv.shape[0]
    scale = HEAD_DIM ** (-0.5)
    results = ([], [], [])
    for tile in range(width // LANES):
        at = tile * LANES
        query, key, value = (
            qkv[:, piece * width + at : piece * width + at + LANES] for piece in range(3)
        )
        grad = grad_mixed[:, at : at + LANES]
        totals = [jnp.zeros((rows, LANES), WIDE) for _ in range(3)]
        for head in range(2):
            mask = lane_mask(rows, head)
            query_low, key_low, grad_low = (masked(x, mask) for x in (query, key, grad))
            chance = head_probabilities(query_low, key, allowed)
            grad_chance = product_right(grad_low, value)
            inner = jnp.sum(grad_chance * chance, axis=-1, keepdims=True)
            grad_scores = (chance * (grad_chance - inner)).astype(LOW)
            totals[0] = totals[0] + product_plain(grad_scores, key_low)
            totals[1] = totals[1] + product_left(grad_scores, query_low)
            totals[2] = totals[2] + product_left(chance.astype(LOW), grad_low)
        results[0].append((totals[0] * scale).astype(LOW))
        results[1].append((totals[1] * scale).astype(LOW))
        results[2].append(totals[2].astype(LOW))
    return results[0] + results[1] + results[2]


def token_allowed(live_row):
    shape = (SEG, SEG)
    same = lax.broadcasted_iota(jnp.int32, shape, 0) == lax.broadcasted_iota(jnp.int32, shape, 1)
    return (live_row > 0.5) | same


def qkv_kernel(where, *refs):
    blocks = refs[:8]
    hidden, hidden_got, live_row, live_got, order = refs[8:13]
    weight, out_half, qkv_out, mixed_out, vectors_out, count_out, ordered_out = refs[13:20]
    vec_rows, flat, inputs = refs[20:]
    core_at = where[2]
    gather_blocks(
        where,
        blocks,
        0,
        4 * HALF + LANES,
        (
            (weight, 0, 3 * HALF),
            (out_half, 3 * HALF, 4 * HALF),
            (vec_rows, 4 * HALF, 4 * HALF + LANES),
        ),
    )
    piece = (8 * MODEL + FF) // GROUP
    lines = -(-piece // LANES)
    count = jnp.zeros((1, LANES), WIDE)
    for chip in range(GROUP):
        rows = vec_rows[chip, 0:16, :].astype(WIDE)
        for block in range(2):
            joined = jnp.concatenate(
                [rows[block * lines + r : block * lines + r + 1] for r in range(lines)], axis=1
            )
            flat[block : block + 1, chip * piece : (chip + 1) * piece] = joined[:, :piece]
        count = count + rows[2 * lines : 2 * lines + 1]
    rows_each = (8 * MODEL + FF) // MODEL
    for block in range(2):
        for row in range(rows_each):
            vectors_out[block * rows_each + row : block * rows_each + row + 1, :] = flat[
                block : block + 1, row * MODEL : (row + 1) * MODEL
            ]
    count_out[...] = jnp.broadcast_to(count, count_out.shape)
    inputs[:SEG] = hidden[...]
    inputs[SEG:] = hidden_got[...]
    projected = product_plain(inputs[...], whole_rows(weight))
    lanes = pl.ds(aligned(core_at * HALF), HALF)
    qkv_out[:, :HALF] = (projected[:, :HALF] + vectors_out[0:1, lanes]).astype(LOW)
    qkv_out[:, HALF : 2 * HALF] = projected[:, HALF : 2 * HALF].astype(LOW)
    qkv_out[:, 2 * HALF :] = (projected[:, 2 * HALF :] + vectors_out[1:2, lanes]).astype(LOW)
    for part, live in enumerate((live_row, live_got)):
        rows = slice(part * SEG, (part + 1) * SEG)
        tiles = attend_tiles(qkv_out[rows, :], HALF, token_allowed(live[...]))
        for tile, value in enumerate(tiles):
            mixed_out[rows, tile * LANES : (tile + 1) * LANES] = value
    ordered_out[...] = product_plain(inputs[...], order[...]).astype(LOW)


def norm_rows(summed):
    row_mean = jnp.mean(summed, axis=-1, keepdims=True)
    centered = summed - row_mean
    inv_dev = lax.rsqrt(jnp.mean(centered * centered, axis=-1, keepdims=True) + NORM_EPS)
    return centered * inv_dev, inv_dev


def norm_rows_back(grad_out, normed, inv_dev, gain):
    scaled = grad_out * gain
    mean_one = jnp.mean(scaled, axis=-1, keepdims=True)
    mean_two = jnp.mean(scaled * normed, axis=-1, keepdims=True)
    return inv_dev * (scaled - mean_one - normed * mean_two)


def column_sum(value):
    return jnp.sum(value.astype(WIDE), axis=0, keepdims=True)


def four_rows(vectors, first):
    return jnp.concatenate([vectors[first + at : first + at + 1, :] for at in range(4)], axis=1)


def gelu_both(before):
    half = 0.5 * (1.0 + lax.erf(before * SQRT_HALF))
    slope = half + before * jnp.exp(-0.5 * before * before) * INV_SQRT_TWO_PI
    return before * half, slope


def out_kernel(where, hidden, mixed, mixed_got, half, half_got, vectors, order, *outs):
    full_out, ordered_out, normed_out, inv_out, low_out, mixed_full = outs
    core_at = where[2]
    own, other = aligned(core_at * HALF), aligned((1 - core_at) * HALF)
    full_out[:, pl.ds(own, HALF)] = half[...]
    full_out[:, pl.ds(other, HALF)] = half_got[...]
    mixed_full[:, pl.ds(own, HALF)] = mixed[...]
    mixed_full[:SEG, pl.ds(other, HALF)] = mixed_got[SEG:, :]
    mixed_full[SEG:, pl.ds(other, HALF)] = mixed_got[:SEG, :]
    branch = product_plain(mixed_full[:SEG, :], full_out[...])
    normed, inv_dev = norm_rows(hidden[...].astype(WIDE) + branch + vectors[2:3, :])
    normed_out[...] = normed
    inv_out[...] = inv_dev
    low_out[...] = (normed * vectors[4:5, :] + vectors[5:6, :]).astype(LOW)
    ordered_out[...] = product_plain(mixed_full[...], order[...]).astype(LOW)


def up_kernel(where, *refs):
    blocks = refs[:8]
    low, low_got, vectors = refs[8:11]
    weight, act_out, slope_out, both = refs[11:]
    core_at = where[2]
    gather_blocks(where, blocks, 2 * (4 * HALF + LANES), FF_HALF, ((weight, 0, FF_HALF),))
    both[:SEG] = low[...]
    both[SEG:] = low_got[...]
    for at in range(FF_HALF // MODEL):
        columns = slice(at * MODEL, (at + 1) * MODEL)
        held = weight[:, :, columns]
        before = product_plain(both[...], held.reshape(MODEL, MODEL))
        bias = vectors[pl.ds(8 + core_at * (FF_HALF // MODEL) + at, 1), :]
        value, slope = gelu_both(before + bias)
        act_out[:, columns] = value.astype(LOW)
        slope_out[:, columns] = slope


def down_kernel(where, *refs):
    blocks, act = refs[:8], refs[8]
    weight, own_out, send_out = refs[9:]
    gather_blocks(where, blocks, 2 * FF_HALF, FF_HALF, ((weight, 0, FF_HALF),))
    partial = product_right(act[...], whole_rows(weight))
    own_out[...] = partial[:SEG]
    send_out[...] = partial[SEG:]


def seg_rows_kernel(where, *refs):
    own, got, normed_first, vectors, targets, live, seg_pos = refs[:7]
    normed_out, inv_out, diff_out, rows_out, head_out = refs[7:]
    doc, number = where[3], where[4]
    first = normed_first[...] * vectors[4:5, :] + vectors[5:6, :]
    normed, inv_dev = norm_rows(first + own[...] + got[...] + vectors[3:4, :])
    normed_out[...] = normed
    inv_out[...] = inv_dev
    rows = normed * vectors[6:7, :] + vectors[7:8, :]
    shape = (SEG, SEG)
    same = lax.broadcasted_iota(jnp.int32, shape, 0) == lax.broadcasted_iota(jnp.int32, shape, 1)
    live_rows = jnp.sum(jnp.where(same, live[...], 0.0), axis=1, keepdims=True)
    target_rows = targets[...].astype(WIDE)
    output = rows * live_rows
    rows_out[...] = output
    diff = (output - target_rows) * live_rows
    row_at = lax.broadcasted_iota(jnp.int32, (SEG, 1), 0)
    diff = jnp.where(row_at > 0, diff, 0.0)
    diff_out[...] = diff
    table = seg_pos[...].astype(WIDE)
    chosen = lax.broadcasted_iota(jnp.int32, table.shape, 0) == number
    position = jnp.sum(jnp.where(chosen, table, 0.0), axis=0, keepdims=True)
    head_out[:, :MODEL] = rows[0:1, :] + position
    head_out[:, MODEL : 2 * MODEL] = target_rows[0:1, :]
    square = jnp.sum(column_sum(diff * diff), axis=1, keepdims=True)
    lane = lax.broadcasted_iota(jnp.int32, (1, LANES), 1)
    facts = jnp.where(lane == 0, live_rows[0:1, :], 0.0)
    facts = jnp.where(lane == 1, doc.astype(WIDE), facts)
    facts = jnp.where(lane == 2, number.astype(WIDE), facts)
    facts = jnp.where(lane == 3, square, facts)
    head_out[:, 2 * MODEL :] = facts


def second_norm_kernel(where, diff, count, normed, inv_dev, vectors, grad_out, low_out, sums_out):
    grad_top = diff[...] * ((SEG * GROUP * CORES) / count[0:1, 0:1])
    normed_rows = normed[...]
    grad = norm_rows_back(grad_top, normed_rows, inv_dev[...], vectors[6:7, :])
    low = grad.astype(LOW)
    grad_out[...] = grad
    low_out[...] = low
    sums_out[0:1, :] = column_sum(low)
    sums_out[1:2, :] = column_sum(grad_top * normed_rows)
    sums_out[2:3, :] = column_sum(grad_top)


def mlp_back_kernel(where, *refs):
    low, low_got, down_weight, up_weight, slope = refs[:5]
    pre_out, own_out, send_out, sums_out, both = refs[5:]
    both[:SEG] = low[...]
    both[SEG:] = low_got[...]
    for at in range(FF_HALF // MODEL):
        columns = slice(at * MODEL, (at + 1) * MODEL)
        held = down_weight[:, :, columns]
        before = product_plain(both[...], held.reshape(MODEL, MODEL))
        pre = (before * slope[:, columns]).astype(LOW)
        pre_out[:, columns] = pre
        sums_out[at : at + 1, :] = column_sum(pre)
    partial = product_right(pre_out[...], whole_rows(up_weight))
    own_out[...] = partial[:SEG]
    send_out[...] = partial[SEG:]


def scatter_parts(where, parts, outs, sems):
    line_at, plane_at = where[0], where[1]
    far_low, far_high, to_x, to_y, kept = outs
    half = LINE // 2
    copies = []
    for mask in range(PLANE):
        for step in range(LINE):
            source = parts.at[(line_at + step) % LINE * PLANE + (plane_at ^ mask)]
            if mask == 3:
                target = far_low.at[step] if step < half else far_high.at[step - half]
            else:
                target = (kept, to_x, to_y)[mask].at[step]
            copies.append(pltpu.make_async_copy(source, target, sems.at[len(copies)]))
    for copy in copies:
        copy.start()
    wait_all(copies)


def mlp_weight_kernel(where, *refs):
    first, first_got, second, second_got, pre, act = refs[:6]
    outs = refs[6:11]
    left, parts, sems = refs[11:]
    for at, (own, got, right) in enumerate(((first, first_got, pre), (second, second_got, act))):
        left[:SEG] = own[...]
        left[SEG:] = got[...]
        for piece in range(FF_HALF // MODEL):
            start = piece * MODEL
            product = product_left(left[...], right[:, start : start + MODEL]).astype(LOW)
            target = at * FF_HALF + start
            parts[:, :, target : target + MODEL] = product.reshape(GROUP, OWN, MODEL)
    scatter_parts(where, parts, outs, sems)


def attn_product(where, refs, mask, piece):
    hidden, mixed, proj, branch, got = refs
    lanes = slice(mask * SPAN, (mask + 1) * SPAN)
    if piece < 3:
        right = proj[:, piece * HALF : (piece + 1) * HALF]
        product = product_left(hidden[:, lanes], right)
    else:
        own = branch[:, pl.ds(aligned(where[2] * HALF), HALF)]
        product = product_left(mixed[:SEG, lanes], own)
        product = product + product_left(mixed[SEG:, lanes], got[:, HALF:])
    return product[: LINE * OWN].astype(LOW).reshape(LINE, OWN, HALF)


def attn_far_kernel(where, *refs):
    low_out, high_out = refs[5:]
    half = LINE // 2
    for piece in range(4):
        columns = slice(piece * HALF, (piece + 1) * HALF)
        product = attn_product(where, refs[:5], 3, piece)
        low_out[:, :, columns] = product[:half]
        high_out[:, :, columns] = product[half:]


def attn_near_kernel(where, *refs):
    for mask, out in ((1, refs[5]), (2, refs[6]), (0, refs[7])):
        for piece in range(4):
            columns = slice(piece * HALF, (piece + 1) * HALF)
            out[:, :, columns] = attn_product(where, refs[:5], mask, piece)


def fold_kernel(where, kept, got_x, got_y, *refs):
    extra, own_out, sent = refs[: -LINE], refs[-LINE], refs[1 - LINE :]
    rows = kept.shape[1]
    for step in range(LINE):
        total = kept[step].astype(WIDE) + got_x[step].astype(WIDE) + got_y[step].astype(WIDE)
        if step == 0:
            own_out[...] = total
            continue
        out = sent[step - 1]
        out[:rows, :] = total.astype(LOW)
        if extra:
            out[rows:, :] = jnp.zeros_like(out[rows:, :])
            out[rows:, : extra[0].shape[1]] = extra[0][...]


def reduce_far(parts):
    return in_plane(parts[0], 2), in_plane(parts[1], 1)


def reduce_add(where, parts, far):
    shape = parts[2].shape
    return run_kernel(
        add_far_kernel,
        "add_far",
        [shape_of(shape, LOW)] * 2,
        where,
        (),
        tuple(far) + (parts[2], parts[3]),
    )


def reduce_fold(where, kept, got, *extra):
    _, rows, columns = kept.shape
    more = sum(value.shape[0] for value in extra)
    return run_kernel(
        fold_kernel,
        "fold",
        [shape_of((rows, columns))] + [shape_of((rows + more, columns), LOW)] * (LINE - 1),
        where,
        (),
        (kept,) + tuple(got) + extra,
    )


def reduce_line(own, pieces):
    total = own
    for piece in pieces:
        total = total + piece[: own.shape[0]].astype(WIDE)
    return total


def head_back_kernel(where, *refs):
    grad, grad_got, down_weight, up_weight, slope, act, low, low_got = refs[:8]
    own_out, send_out, data_out = refs[8:]
    few = 16
    row_at = lax.broadcasted_iota(jnp.int32, (few, 1), 0)

    def two_rows(first, second):
        return jnp.where(row_at == 0, first, jnp.where(row_at == 1, second, 0.0))

    second = two_rows(grad[...], grad_got[...]).astype(LOW)
    data_out[0:1, :] = low[0:1, :].astype(WIDE)
    data_out[1:2, :] = low_got[0:1, :].astype(WIDE)
    data_out[2:4, :] = second[0:2].astype(WIDE)
    partial = jnp.zeros((few, MODEL), WIDE)
    for at in range(FF_HALF // MODEL):
        columns = slice(at * MODEL, (at + 1) * MODEL)
        before = product_plain(second, down_weight[:, :, columns].reshape(MODEL, MODEL))
        slopes = two_rows(slope[0:1, columns], slope[SEG : SEG + 1, columns])
        pre = (before * slopes).astype(LOW)
        partial = partial + product_right(pre, up_weight[:, :, columns].reshape(MODEL, MODEL))
        data_out[4 + 2 * at : 6 + 2 * at, :] = pre[0:2].astype(WIDE)
        data_out[8 + 2 * at : 9 + 2 * at, :] = act[0:1, columns].astype(WIDE)
        data_out[9 + 2 * at : 10 + 2 * at, :] = act[SEG : SEG + 1, columns].astype(WIDE)
    own_out[...] = partial[0:1]
    send_out[...] = partial[1:2]


def first_norm_kernel(where, *refs):
    second_grad, own, got, head_grad, head_own, head_got = refs[:6]
    normed_rows, inv_dev, vectors, out_weight = refs[6:10]
    grad_out, branch_out, mixed_out, send_out, sums_out = refs[10:]
    core_at = where[2]
    grad_rows = second_grad[...] + own[...] + got[...]
    head = head_grad[...] + head_own[...] + head_got[...]
    row_at = lax.broadcasted_iota(jnp.int32, (SEG, 1), 0)
    grad_rows = jnp.where(row_at == 0, head, grad_rows)
    normed = normed_rows[...]
    grad = norm_rows_back(grad_rows, normed, inv_dev[...], vectors[4:5, :])
    grad_out[...] = grad
    branch = grad.astype(LOW)
    branch_out[...] = branch
    mixed_out[...] = product_right(branch, out_weight[...]).astype(LOW)
    other = pl.ds(aligned((1 - core_at) * HALF), HALF)
    send_out[:, :HALF] = mixed_out[:, other]
    send_out[:, HALF:] = branch_out[:, other]
    sums_out[0:1, :] = column_sum(branch)
    sums_out[1:2, :] = column_sum(grad_rows * normed)
    sums_out[2:3, :] = column_sum(grad_rows)


def attn_back_kernel(where, *refs):
    qkv, mixed_grad, got, live_row, live_got, weight = refs[:6]
    sums_first, sums_second, sums_up, head_top, head_normed, data = refs[6:12]
    proj_out, own_out, send_out, payload_out, rows = refs[12:]
    core_at = where[2]
    lanes = pl.ds(aligned(core_at * HALF), HALF)
    for part, live in enumerate((live_row, live_got)):
        at = slice(part * SEG, (part + 1) * SEG)
        grad = mixed_grad[:, lanes] if part == 0 else got[:, :HALF]
        pieces = attend_tiles_back(qkv[at, :], grad, HALF, token_allowed(live[...]))
        for tile, value in enumerate(pieces):
            proj_out[at, tile * LANES : (tile + 1) * LANES] = value
    partial = product_right(proj_out[...], whole_rows(weight))
    own_out[...] = partial[:SEG]
    send_out[...] = partial[SEG:]
    rows[...] = jnp.zeros_like(rows)
    rows[0:12, :] = data[0:12, :]
    rows[12:13, lanes] = column_sum(proj_out[:, :HALF])
    rows[13:14, lanes] = column_sum(proj_out[:, 2 * HALF :])
    rows[14:15, :] = sums_first[0:1, :]
    rows[15:16, :] = sums_second[0:1, :] + data[2:3, :]
    rows[16:18, :] = sums_first[1:3, :]
    rows[18:19, :] = sums_second[1:2, :] + head_top[...] * head_normed[0:1, :]
    rows[19:20, :] = sums_second[2:3, :] + head_top[...]
    for at in range(FF_HALF // MODEL):
        total = sums_up[at : at + 1, :] + data[4 + 2 * at : 5 + 2 * at, :]
        total = total + data[5 + 2 * at : 6 + 2 * at, :]
        rows[pl.ds(20 + core_at * (FF_HALF // MODEL) + at, 1), :] = total
    payload_out[...] = rows[...].astype(LOW)


def cls_gather_kernel(where, *refs):
    blocks = refs[:8]
    own_out, from_x, from_y, far_x = refs[8], refs[4], refs[5], refs[6]
    weight_out, out_rows = refs[9:]
    plane_at = where[1]
    gather_blocks(where, blocks, 0, QUARTER_HALF, ((weight_out, 0, QUARTER_HALF),))
    first = LINE * QUARTER_HALF
    out_rows[plane_at] = own_out[...]
    out_rows[plane_at ^ 1] = from_x[:, first : first + HALF]
    out_rows[plane_at ^ 2] = from_y[:, first : first + HALF]
    first = LINE // 2 * QUARTER_HALF
    out_rows[plane_at ^ 3] = far_x[:, first : first + HALF]


def cls_weight_kernel(where, own, got, out_half, out_got, weight_out, out_full):
    line_at, core_at = where[0], where[2]
    out_full[...] = jnp.zeros_like(out_full)
    for value, part, core in ((own, out_half, core_at), (got, out_got, 1 - core_at)):
        weight_out[:, :, pl.ds(aligned(core * QUARTER_HALF), QUARTER_HALF)] = value[...]
        rows = part[...].reshape(3, HEAD_DIM, HALF)
        out_full[pl.ds(line_at % 2, 3), :, pl.ds(aligned(core * HALF), HALF)] = rows


def add_far_kernel(where, far_low, far_high, to_x, to_y, x_out, y_out):
    half = LINE // 2
    x_out[:half] = to_x[:half] + far_low[...]
    x_out[half:] = to_x[half:]
    y_out[:half] = to_y[:half]
    y_out[half:] = to_y[half:] + far_high[...]


def row_from_column(column, size):
    shape = (size, size)
    same = lax.broadcasted_iota(jnp.int32, shape, 0) == lax.broadcasted_iota(jnp.int32, shape, 1)
    return jnp.sum(jnp.where(same, column, 0.0), axis=0, keepdims=True)


def head_allowed(heads):
    facts = heads[:, 2 * MODEL :]
    live, doc = facts[:, 0:1], facts[:, 1:2]
    shape = (GROUP, GROUP)
    same = lax.broadcasted_iota(jnp.int32, shape, 0) == lax.broadcasted_iota(jnp.int32, shape, 1)
    live_row, doc_row = row_from_column(live, GROUP), row_from_column(doc, GROUP)
    return ((live_row > 0.5) & (doc == doc_row)) | same


def quarter_mask(quarter):
    lane = lax.broadcasted_iota(jnp.int32, (GROUP, SPAN), 1)
    first = (quarter % 2) * HEAD_DIM
    return (lane >= first) & (lane < first + 3 * HEAD_DIM)


def quarter_piece(vectors, row, quarter):
    value = jnp.zeros((1, SPAN), WIDE)
    for at in range(LINE):
        first = TILE_START[at] * LANES
        value = jnp.where(quarter == at, vectors[row : row + 1, first : first + SPAN], value)
    return value


def cls_attend_kernel(where, *refs):
    stacks, vectors, weight, out_weight = refs[:4], refs[4], refs[5], refs[6]
    heads_out, qkv_out, mixed_out, part_out = refs[7:]
    line_at, plane_at = where[0], where[1]
    for step, stack in enumerate(stacks):
        for mask in range(PLANE):
            row = (line_at + LINE - step) % LINE * PLANE + (plane_at ^ mask)
            heads_out[pl.ds(row, 1), :] = stack[mask : mask + 1, :]
    heads = heads_out[...]
    inputs = heads[:, :MODEL].astype(LOW)
    projected = product_plain(inputs, weight[:, : 3 * SPAN])
    query = projected[:, :SPAN] + quarter_piece(vectors, 12, line_at)
    value = projected[:, 2 * SPAN :] + quarter_piece(vectors, 13, line_at)
    qkv_out[:, :SPAN] = query.astype(LOW)
    qkv_out[:, SPAN : 2 * SPAN] = projected[:, SPAN : 2 * SPAN].astype(LOW)
    qkv_out[:, 2 * SPAN :] = value.astype(LOW)
    mixed = attend_tiles(qkv_out[...], SPAN, head_allowed(heads))
    mixed = masked(jnp.concatenate(mixed, axis=1), quarter_mask(line_at))
    mixed_out[...] = mixed
    part_out[...] = product_plain(mixed, out_weight[...])


def cls_mlp_kernel(where, *refs):
    heads, own, got_one, got_two, got_three, vectors, weight = refs[:7]
    normed_out, inv_out, low_out, act_out, slope_out, part_out = refs[7:]
    line_at = where[0]
    branch = own[...] + got_one[...] + got_two[...] + got_three[...]
    normed, inv_dev = norm_rows(heads[:, :MODEL] + branch + vectors[14:15, :])
    normed_out[...] = normed
    inv_out[...] = inv_dev
    low = (normed * vectors[16:17, :] + vectors[17:18, :]).astype(LOW)
    low_out[...] = low
    part = FF // LINE
    first = 3 * SPAN
    bias = vectors[pl.ds(20 + line_at, 1), :]
    before = product_plain(low, weight[:, first : first + part]) + bias
    value, slope = gelu_both(before)
    act = value.astype(LOW)
    act_out[...] = act
    slope_out[...] = slope
    part_out[...] = product_right(act, weight[:, first + part :])


def cls_top_kernel(where, *refs):
    heads, own, got_one, got_two, got_three, vectors, weight = refs[:7]
    normed_first, count, slope = refs[7:10]
    top_out, square_out, grad_out, second_out, pre_out, part_out, sums_out = refs[10:17]
    held = refs[17]
    rank = where[0] * PLANE + where[1]
    first = normed_first[...] * vectors[16:17, :] + vectors[17:18, :]
    down = own[...] + got_one[...] + got_two[...] + got_three[...]
    normed, inv_dev = norm_rows(first + down + vectors[15:16, :])
    rows = normed * vectors[18:19, :] + vectors[19:20, :]
    held[...] = rows
    top_out[...] = held[pl.ds(rank, 1), :]
    facts = heads[:, 2 * MODEL :]
    live = facts[:, 0:1]
    diff = (rows * live - heads[:, MODEL : 2 * MODEL]) * live
    square = jnp.sum(column_sum(diff * diff), axis=1, keepdims=True)
    square = square + jnp.sum(facts[:, 3:4], axis=0, keepdims=True)
    square_out[...] = jnp.broadcast_to(square, square_out.shape)
    grad_top = diff * ((SEG * GROUP * CORES) / count[0:1, 0:1])
    grad = norm_rows_back(grad_top, normed, inv_dev, vectors[18:19, :])
    sums_out[0:1, :] = column_sum(grad_top * normed)
    sums_out[1:2, :] = column_sum(grad_top)
    grad_out[...] = grad
    second = grad.astype(LOW)
    second_out[...] = second
    part = FF // LINE
    at = 3 * SPAN
    pre = (product_plain(second, weight[:, at + part :]) * slope[...]).astype(LOW)
    pre_out[...] = pre
    part_out[...] = product_right(pre, weight[:, at : at + part])


def cls_attend_back_kernel(where, *refs):
    heads, own, got_one, got_two, got_three, vectors, weight, out_weight = refs[:8]
    grad_in, normed_first, inv_first, qkv = refs[8:12]
    grad_out, branch_out, proj_out, part_out, sums_out = refs[12:]
    line_at = where[0]
    grad_first = grad_in[...] + own[...] + got_one[...] + got_two[...] + got_three[...]
    normed = normed_first[...]
    grad = norm_rows_back(grad_first, normed, inv_first[...], vectors[16:17, :])
    sums_out[0:1, :] = column_sum(grad_first * normed)
    sums_out[1:2, :] = column_sum(grad_first)
    grad_out[...] = grad
    branch = grad.astype(LOW)
    branch_out[...] = branch
    mask = quarter_mask(line_at)
    mixed_grad = masked(product_right(branch, out_weight[...]).astype(LOW), mask)
    pieces = attend_tiles_back(qkv[...], mixed_grad, SPAN, head_allowed(heads[...]))
    tiles = SPAN // LANES
    for piece in range(3):
        joined = jnp.concatenate(pieces[piece * tiles : (piece + 1) * tiles], axis=1)
        proj_out[:, piece * SPAN : (piece + 1) * SPAN] = masked(joined, mask)
    part_out[...] = product_right(proj_out[...], weight[:, : 3 * SPAN])


def cls_end_kernel(where, *refs):
    heads, grad, own, got_one, got_two, got_three = refs[:6]
    square, sums_back, sums_top = refs[6:9]
    normed_second, inv_second, vectors = refs[9:12]
    row_out, second_out, shared_out, held = refs[12:]
    rank = where[0] * PLANE + where[1]
    total = grad[...] + own[...] + got_one[...] + got_two[...] + got_three[...]
    held[...] = total
    row = held[pl.ds(rank, 1), :]
    row_out[...] = row
    second_out[...] = norm_rows_back(
        row, normed_second[0:1, :], inv_second[0:1, :], vectors[6:7, :]
    )
    number = row_from_column(heads[:, 2 * MODEL + 2 : 2 * MODEL + 3], GROUP)
    entry = lax.broadcasted_iota(jnp.int32, (GROUP, GROUP), 0).astype(WIDE)
    hot = (entry == number).astype(WIDE)
    shared_out[0:GROUP, :] = jnp.dot(hot, total, precision=lax.Precision.HIGHEST)
    shared_out[GROUP : GROUP + 1, 0:LANES] = square[0:1, :]
    shared_out[GROUP + 1 : GROUP + 3, :] = sums_back[0:2, :]
    shared_out[GROUP + 3 : GROUP + 5, :] = sums_top[0:2, :]


def cls_rows_kernel(where, *refs):
    packs = refs[:4]
    heads, branch, low, second = refs[4:8]
    out, kept = refs[8:]
    line_at = where[0]
    rows, width = kept.shape[1:]
    for step, pack in enumerate(packs):
        first = pack.shape[0] - rows
        kept[(line_at + LINE - step) % LINE] = pack[first:, :width]
    starts = (MODEL, 2 * MODEL, 3 * MODEL, 4 * MODEL)
    out[:, 0:MODEL] = heads[:, :MODEL].astype(LOW)
    for piece, start in enumerate(starts):
        from_at = piece * SPAN
        for tile in range(MODEL // LANES):
            total = None
            for at in range(PLANE):
                inner = tile - TILE_START[at]
                if inner in (0, 1):
                    first = from_at + inner * LANES
                    value = kept[at, :, first : first + LANES]
                    total = value if total is None else total + value
            out[:, start + tile * LANES : start + (tile + 1) * LANES] = total
    out[:, 5 * MODEL : 6 * MODEL] = branch[...]
    out[:, 6 * MODEL : 7 * MODEL] = low[...]
    out[:, 7 * MODEL + FF : 8 * MODEL + FF] = second[...]
    part = FF // LINE
    for at in range(PLANE):
        first = 4 * SPAN
        out[:, 7 * MODEL + at * part : 7 * MODEL + (at + 1) * part] = kept[
            at, :, first : first + part
        ]
        out[:, 8 * MODEL + FF + at * part : 8 * MODEL + FF + (at + 1) * part] = kept[
            at, :, first + part : first + 2 * part
        ]


def own_features(rank, width):
    shape = (MODEL, width)
    feature = lax.broadcasted_iota(jnp.int32, shape, 0)
    column = lax.broadcasted_iota(jnp.int32, shape, 1)
    return (feature == rank * width + column).astype(LOW)


def own_vector(rank, pieces, out, flat):
    size = out.shape[1]
    for at, piece in enumerate(pieces):
        flat[:, at * MODEL : (at + 1) * MODEL] = piece
    value = jnp.zeros((1, size), WIDE)
    for chip in range(GROUP):
        value = jnp.where(rank == chip, flat[:, chip * size : (chip + 1) * size], value)
    out[...] = value


def cls_owner_kernel(where, *refs):
    own, got, shared, mats_out, vec_out, rows, flat = refs
    rank = where[0] * PLANE + where[1]
    width = mats_out.shape[0]
    rows[:GROUP] = own[...]
    rows[GROUP:] = got[...]
    chosen = own_features(rank, width)
    plan = (
        (0, MODEL, 3 * MODEL, 0),
        (4 * MODEL, 5 * MODEL, MODEL, 3 * MODEL),
        (6 * MODEL, 7 * MODEL, FF, 4 * MODEL),
        (7 * MODEL + FF, 8 * MODEL + FF, FF, 4 * MODEL + FF),
    )
    for left, right, size, target in plan:
        side = product_plain(rows[:, left : left + MODEL], chosen).astype(LOW)
        mats_out[:, target : target + size] = product_left(side, rows[:, right : right + size])
    starts = (MODEL, 3 * MODEL, 5 * MODEL, 7 * MODEL + FF)
    pieces = [column_sum(rows[:, start : start + MODEL]) for start in starts]
    pieces += [shared[GROUP + 1 + at : GROUP + 2 + at, :] for at in range(4)]
    starts = [7 * MODEL + at * MODEL for at in range(FF // MODEL)]
    pieces += [column_sum(rows[:, start : start + MODEL]) for start in starts]
    own_vector(rank, pieces, vec_out, flat)


def head_share_kernel(where, *refs):
    packs, mlp = refs[:4], refs[4]
    mine_out, vecs_out, rows = refs[5:]
    rank = where[0] * PLANE + where[1]
    count = LINE * 24
    for at, pack in enumerate(packs):
        rows[at * count : (at + 1) * count] = pack[...]
    total = PLANE * count

    def chosen(base, apart):
        shape = (CORES * GROUP, total)
        row = lax.broadcasted_iota(jnp.int32, shape, 0)
        column = lax.broadcasted_iota(jnp.int32, shape, 1)
        hot = (column == row // 2 * 24 + base + row % 2 * apart).astype(LOW)
        return product_plain(hot, rows[...]).astype(LOW)

    own = own_features(rank, OWN)
    for at, (left, right) in enumerate(((0, 4), (2, 8))):
        side = product_plain(chosen(left, 1), own).astype(LOW)
        for piece in range(FF_HALF // MODEL):
            columns = slice(at * FF_HALF + piece * MODEL, at * FF_HALF + (piece + 1) * MODEL)
            share = product_left(side, chosen(right + 2 * piece, 1))
            mine_out[:, columns] = mlp[:, columns] + share
    shape = (16, total)
    row = lax.broadcasted_iota(jnp.int32, shape, 0)
    column = lax.broadcasted_iota(jnp.int32, shape, 1)
    hot = ((column % 24 == row + 12) & (row < 12)).astype(LOW)
    vecs_out[...] = product_plain(hot, rows[...])


def seg_vec_kernel(where, vecs, vecs_got, vec_out, flat):
    rank = where[0] * PLANE + where[1]
    rows = (8 * MODEL + FF) // MODEL
    pieces = [vecs[at : at + 1, :] + vecs_got[at : at + 1, :] for at in range(rows)]
    own_vector(rank, pieces, vec_out, flat)


def column_copies(where, out, base, size, own, got, first):
    core_at = where[2]
    lanes = slice(first, first + size)
    return [
        (own.at[:, lanes], out.at[:, pl.ds(aligned(base + core_at * size), size)]),
        (got.at[:, lanes], out.at[:, pl.ds(aligned(base + (1 - core_at) * size), size)]),
    ]


def mlp_store_kernel(where, mlp, mlp_got, out, sems):
    pairs = []
    for piece in range(2):
        base = 4 * MODEL + piece * FF
        pairs += column_copies(where, out, base, FF_HALF, mlp, mlp_got, piece * FF_HALF)
    run_copies(pairs, sems)


def attn_store_kernel(where, attn, attn_got, filled, out, sems):
    pairs = []
    for piece in range(4):
        pairs += column_copies(where, out, piece * MODEL, HALF, attn, attn_got, piece * HALF)
    run_copies(pairs, sems)


def store_attn(where, attn, attn_got, filled):
    far = pl.BlockSpec(memory_space=pl.ANY)
    near = pl.BlockSpec(memory_space=pltpu.VMEM)
    return pl.pallas_call(
        attn_store_kernel,
        name="seg_attn_store",
        out_shape=shape_of(filled.shape),
        in_specs=[pl.BlockSpec(memory_space=pltpu.SMEM), near, near, far],
        out_specs=far,
        scratch_shapes=[pltpu.SemaphoreType.DMA((8,))],
        input_output_aliases={3: 0},
        compiler_params=pltpu.CompilerParams(vmem_limit_bytes=VMEM_BYTES),
    )(where, attn, attn_got, filled)


def plane_parts(part):
    return (part,) + tuple(in_plane(part, mask) for mask in range(1, PLANE))


def line_parts(part):
    return (part,) + tuple(along_line(part, apart) for apart in range(1, LINE))


def slice_local(
    hidden_in,
    targets,
    doc_ids,
    seg_nums,
    valid_flags,
    seg_mats,
    seg_vecs,
    cls_mats,
    cls_vecs,
    seg_pos,
):
    rank, core_at = lax.axis_index("fsdp"), lax.axis_index("rep")
    line_at, plane_at = rank // PLANE, rank % PLANE
    where = jnp.stack([line_at, plane_at, core_at, doc_ids[0], seg_nums[0]]).astype(jnp.int32)
    own_rows, total_columns = seg_mats.shape
    vec_size = seg_vecs.shape[0]
    both_rows = CORES * SEG
    first_columns = 4 * HALF + LANES

    first_piece, live_row = run_kernel(
        prepare_first_kernel,
        "prepare_first",
        [shape_of((own_rows, first_columns), LOW), shape_of((1, SEG))],
        where,
        (seg_mats,),
        (jnp.stack([seg_vecs, cls_vecs]).astype(WIDE), valid_flags[None]),
        [pltpu.SemaphoreType.DMA((4,))],
    )
    first_line = line_parts(first_piece)
    rest = run_kernel(
        prepare_rest_kernel,
        "prepare_rest",
        [shape_of((own_rows, FF_HALF), LOW)] * 2
        + [shape_of((own_rows, QUARTER_HALF), LOW)] * LINE
        + [shape_of((own_rows, HALF), LOW), shape_of((MODEL, PLANE * SPAN), LOW)],
        where,
        (seg_mats, cls_mats),
        (),
        [
            pltpu.VMEM((LINE, own_rows, QUARTER), LOW),
            pltpu.SemaphoreType.DMA((3 + 5 * LINE,)),
        ],
    )
    second_piece, third_piece, quarters, cls_out_piece, order = (
        rest[0],
        rest[1],
        rest[2:-2],
        rest[-2],
        rest[-1],
    )

    def joined(*pieces):
        return jnp.concatenate(pieces, axis=1)

    def sent_both(to_x, to_y):
        return in_plane(to_x, 1), in_plane(to_y, 2)

    hidden_got, live_got = other_core(hidden_in), other_core(live_row)
    first_sent = after(joined(*first_line), second_piece)
    first_x, first_y = sent_both(first_sent, first_sent)
    second_line = line_parts(after(second_piece, hidden_got, live_got, *first_line[1:]))
    size = 2 * first_columns
    second_x, second_y = sent_both(
        joined(first_y[:, size:], *second_line), joined(first_x[:, :size], *second_line)
    )
    third_line = line_parts(after(third_piece, first_x, first_y, *second_line[1:]))
    start, size = size, 2 * FF_HALF
    third_x, third_y = sent_both(
        joined(second_y[:, start + size :], *third_line),
        joined(second_x[:, start : start + size], *third_line),
    )
    cls_line = (quarters[0],) + tuple(
        along_line(after(quarters[apart], second_x, second_y, *third_line[1:]), apart)
        for apart in range(1, LINE)
    )

    qkv_weight, out_half, qkv, mixed, vectors, count, hidden_ordered = run_kernel(
        qkv_kernel,
        "seg_qkv",
        [
            shape_of((GROUP, own_rows, 3 * HALF), LOW),
            shape_of((GROUP, own_rows, HALF), LOW),
            shape_of((both_rows, 3 * HALF), LOW),
            shape_of((both_rows, HALF), LOW),
            shape_of((2 * (8 * MODEL + FF) // MODEL, MODEL)),
            shape_of((8, LANES)),
            shape_of((both_rows, PLANE * SPAN), LOW),
        ],
        where,
        (),
        first_line
        + (first_x, first_y, second_x, second_y)
        + (hidden_in, hidden_got, live_row, live_got, order),
        [
            pltpu.VMEM((GROUP, own_rows, LANES), LOW),
            pltpu.VMEM((2, 8 * MODEL + FF), WIDE),
            pltpu.VMEM((both_rows, MODEL), LOW),
        ],
        flops=2 * SEG * MODEL * 3 * MODEL,
    )
    count = count + other_core(count)
    out_half = out_half.reshape(MODEL, HALF)
    out_weight, mixed_ordered, normed_first, inv_first, first_low = run_kernel(
        out_kernel,
        "seg_out",
        [
            shape_of((MODEL, MODEL), LOW),
            shape_of((both_rows, PLANE * SPAN), LOW),
            shape_of((SEG, MODEL)),
            shape_of((SEG, 1)),
            shape_of((SEG, MODEL), LOW),
        ],
        where,
        (),
        (hidden_in, mixed, other_core(mixed), out_half, other_core(out_half), vectors, order),
        [pltpu.VMEM((both_rows, MODEL), LOW)],
        flops=2 * SEG * MODEL * MODEL,
    )
    first_got = after(other_core(first_low), count)
    third_x, third_y = after(third_x, first_low), after(third_y, first_low)
    up_weight, act, slope = run_kernel(
        up_kernel,
        "seg_up",
        [
            shape_of((GROUP, own_rows, FF_HALF), LOW),
            shape_of((both_rows, FF_HALF), LOW),
            shape_of((both_rows, FF_HALF)),
        ],
        where,
        (),
        second_line
        + (second_x, second_y, third_x, third_y)
        + (first_low, first_got, vectors),
        [pltpu.VMEM((both_rows, MODEL), LOW)],
        flops=2 * SEG * MODEL * FF,
    )
    fourth_x, fourth_y = sent_both(third_y[:, 2 * size :], third_x[:, size : 2 * size])
    fourth_x, fourth_y = after(fourth_x, act), after(fourth_y, act)
    cls_sent = joined(*cls_line, cls_out_piece)
    cls_sent = after(cls_sent, fourth_x, fourth_y)
    cls_x, cls_y = sent_both(cls_sent, cls_sent)
    down_weight, down_own, down_send = run_kernel(
        down_kernel,
        "seg_down",
        [
            shape_of((GROUP, own_rows, FF_HALF), LOW),
            shape_of((SEG, MODEL)),
            shape_of((SEG, MODEL)),
        ],
        where,
        (),
        third_line + (third_x, third_y, fourth_x, fourth_y) + (act,),
        flops=2 * SEG * MODEL * FF,
    )
    normed_second, inv_second, diff, out_rows, head_row = run_kernel(
        seg_rows_kernel,
        "seg_rows",
        [
            shape_of((SEG, MODEL)),
            shape_of((SEG, 1)),
            shape_of((SEG, MODEL)),
            shape_of((SEG, MODEL)),
            shape_of((1, 2 * MODEL + LANES)),
        ],
        where,
        (),
        (
            down_own,
            other_core(down_send),
            normed_first,
            vectors,
            targets,
            live_row,
            seg_pos,
        ),
    )
    head_planes = plane_parts(head_row)
    head_lines = line_parts(jnp.concatenate(head_planes))
    size = LINE // 2 * QUARTER_HALF
    cls_far = sent_both(
        after(cls_y[:, size:], *head_planes[1:]), after(cls_x[:, :size], *head_planes[1:])
    )

    second_grad, second_low, second_sums = run_kernel(
        second_norm_kernel,
        "seg_second_norm",
        [shape_of((SEG, MODEL)), shape_of((SEG, MODEL), LOW), shape_of((3, MODEL))],
        where,
        (),
        (diff, count, normed_second, inv_second, vectors),
    )
    second_got = other_core(second_low)
    cls_far = tuple(after(got, second_got, *head_lines[1:]) for got in cls_far)
    cls_half, cls_out_half = run_kernel(
        cls_gather_kernel,
        "head_gather",
        [
            shape_of((GROUP, own_rows, QUARTER_HALF), LOW),
            shape_of((PLANE, own_rows, HALF), LOW),
        ],
        where,
        (),
        cls_line + (cls_x, cls_y) + cls_far + (cls_out_piece,),
    )
    second_got = after(second_got, cls_half)
    pre, first_grad_own, first_grad_send, up_sums = run_kernel(
        mlp_back_kernel,
        "seg_mlp_back",
        [
            shape_of((both_rows, FF_HALF), LOW),
            shape_of((SEG, MODEL)),
            shape_of((SEG, MODEL)),
            shape_of((FF_HALF // MODEL, MODEL)),
        ],
        where,
        (),
        (second_low, second_got, down_weight, up_weight, slope),
        [pltpu.VMEM((both_rows, MODEL), LOW)],
        flops=4 * SEG * MODEL * FF,
    )
    cls_weight, cls_out = run_kernel(
        cls_weight_kernel,
        "head_weight",
        [
            shape_of((GROUP, own_rows, QUARTER), LOW),
            shape_of((4, HEAD_DIM, MODEL), LOW),
        ],
        where,
        (),
        (cls_half, other_core(cls_half), cls_out_half, other_core(cls_out_half)),
    )
    cls_weight = cls_weight.reshape(MODEL, QUARTER)
    cls_out = cls_out.reshape(SPAN, MODEL)
    first_grad_got = other_core(first_grad_send)

    def part_shapes(columns):
        return [
            shape_of((count_of, own_rows, columns), LOW)
            for count_of in (LINE // 2, LINE // 2, LINE, LINE, LINE)
        ]

    mlp_parts = run_kernel(
        mlp_weight_kernel,
        "seg_mlp_weight",
        part_shapes(FF),
        where,
        (),
        (first_low, first_got, second_low, second_got, pre, act),
        [
            pltpu.VMEM((both_rows, MODEL), LOW),
            pltpu.VMEM((GROUP, own_rows, FF), LOW),
            pltpu.SemaphoreType.DMA((GROUP,)),
        ],
        far=range(5),
        flops=4 * SEG * MODEL * FF,
    )
    mlp_far = reduce_far(tuple(after(part, *cls_far) for part in mlp_parts[:2]))
    heads, cls_qkv, cls_mixed, part = run_kernel(
        cls_attend_kernel,
        "head_attend",
        [
            shape_of((GROUP, 2 * MODEL + LANES)),
            shape_of((GROUP, 3 * SPAN), LOW),
            shape_of((GROUP, SPAN), LOW),
            shape_of((GROUP, MODEL)),
        ],
        where,
        (),
        tuple(after(got, mlp_parts[0], first_grad_got) for got in head_lines)
        + (vectors, cls_weight, cls_out),
    )
    cls_normed, cls_inv, cls_low, cls_act, cls_slope, part = run_kernel(
        cls_mlp_kernel,
        "head_mlp",
        [
            shape_of((GROUP, MODEL)),
            shape_of((GROUP, 1)),
            shape_of((GROUP, MODEL), LOW),
            shape_of((GROUP, FF // LINE), LOW),
            shape_of((GROUP, FF // LINE)),
            shape_of((GROUP, MODEL)),
        ],
        where,
        (),
        (heads,) + line_parts(part) + (vectors, cls_weight),
    )
    cls_parts = line_parts(part)
    mlp_far = tuple(after(got, cls_low) for got in mlp_far)
    mlp_sent = reduce_add(where, mlp_parts, mlp_far)
    mlp_plane = sent_both(*mlp_sent)
    top_row, square, cls_grad, cls_second, cls_pre, part, top_sums = run_kernel(
        cls_top_kernel,
        "head_top",
        [
            shape_of((1, MODEL)),
            shape_of((8, LANES)),
            shape_of((GROUP, MODEL)),
            shape_of((GROUP, MODEL), LOW),
            shape_of((GROUP, FF // LINE), LOW),
            shape_of((GROUP, MODEL)),
            shape_of((2, MODEL)),
        ],
        where,
        (),
        (heads, cls_parts[0], cls_parts[1])
        + tuple(after(got, *mlp_sent) for got in cls_parts[2:])
        + (vectors, cls_weight, cls_normed, count, cls_slope),
        [pltpu.VMEM((GROUP, MODEL), WIDE)],
    )
    cls_grad, cls_branch, cls_proj, part, back_sums = run_kernel(
        cls_attend_back_kernel,
        "head_attend_back",
        [
            shape_of((GROUP, MODEL)),
            shape_of((GROUP, MODEL), LOW),
            shape_of((GROUP, 3 * SPAN), LOW),
            shape_of((GROUP, MODEL)),
            shape_of((2, MODEL)),
        ],
        where,
        (),
        (heads,)
        + line_parts(part)
        + (vectors, cls_weight, cls_out, cls_grad, cls_normed, cls_inv, cls_qkv),
    )
    end_parts = line_parts(part)
    pack = jnp.concatenate([cls_proj, cls_mixed, cls_pre, cls_act], axis=1)
    mlp_plane = [after(got, *end_parts[1:]) for got in mlp_plane]
    mlp_own, *mlp_sent = reduce_fold(where, mlp_parts[4], mlp_plane, pack)
    mlp_got = [along_line(mlp_sent[apart - 1], apart) for apart in range(1, LINE)]
    dheads, head_grad, shared = run_kernel(
        cls_end_kernel,
        "head_end",
        [shape_of((1, MODEL)), shape_of((1, MODEL)), shape_of((GROUP + 8, MODEL))],
        where,
        (),
        (heads, cls_grad)
        + (after(end_parts[0], mlp_own),)
        + end_parts[1:]
        + (square, back_sums, top_sums, normed_second, inv_second, vectors),
        [pltpu.VMEM((GROUP, MODEL), WIDE)],
    )

    head_own, head_send, head_data = run_kernel(
        head_back_kernel,
        "seg_head_back",
        [shape_of((1, MODEL)), shape_of((1, MODEL)), shape_of((12, MODEL))],
        where,
        (),
        (
            head_grad,
            other_core(head_grad),
            down_weight,
            up_weight,
            slope,
            act,
            first_low,
            first_got,
        ),
    )
    grad_summed, branch, mixed_grad, attn_send, first_sums = run_kernel(
        first_norm_kernel,
        "seg_first_norm",
        [
            shape_of((SEG, MODEL)),
            shape_of((SEG, MODEL), LOW),
            shape_of((SEG, MODEL), LOW),
            shape_of((SEG, MODEL), LOW),
            shape_of((3, MODEL)),
        ],
        where,
        (),
        (
            second_grad,
            first_grad_own,
            first_grad_got,
            head_grad,
            head_own,
            other_core(head_send),
            normed_first,
            inv_first,
            vectors,
            out_weight,
        ),
    )
    attn_got = after(other_core(attn_send), mlp_own)
    proj, input_own, input_send, payload = run_kernel(
        attn_back_kernel,
        "seg_attn_back",
        [
            shape_of((both_rows, 3 * HALF), LOW),
            shape_of((SEG, MODEL)),
            shape_of((SEG, MODEL)),
            shape_of((24, MODEL), LOW),
        ],
        where,
        (),
        (
            qkv,
            mixed_grad,
            attn_got,
            live_row,
            live_got,
            qkv_weight,
            first_sums,
            second_sums,
            up_sums,
            dheads,
            normed_second,
            head_data,
        ),
        [pltpu.VMEM((24, MODEL), WIDE)],
        flops=4 * SEG * MODEL * 3 * MODEL,
    )
    attn_data = (hidden_ordered, mixed_ordered, proj, branch, attn_got)
    attn_far = run_kernel(
        attn_far_kernel,
        "seg_attn_far",
        part_shapes(4 * HALF)[:2],
        where,
        (),
        attn_data,
        flops=SEG * MODEL * 2 * MODEL,
    )
    attn_far = reduce_far(tuple(after(part, mlp_got[-1]) for part in attn_far))
    attn_near = run_kernel(
        attn_near_kernel,
        "seg_attn_near",
        part_shapes(4 * HALF)[2:],
        where,
        (),
        attn_data,
        flops=3 * SEG * MODEL * 2 * MODEL,
    )
    input_grad = (grad_summed + input_own + other_core(input_send)).astype(LOW)
    row_at = jnp.arange(SEG)[:, None]
    output = jnp.where(row_at == 0, top_row * live_row[:, :1], out_rows).astype(LOW)
    payload_parts = line_parts(after(payload, attn_near[0]))
    attn_far = tuple(after(got, payload_parts[1]) for got in attn_far)
    attn_sent = reduce_add(where, (None, None) + tuple(attn_near), attn_far)
    attn_plane = sent_both(*(after(part, mlp_got[1]) for part in attn_sent))
    mlp_got = [after(got, attn_plane[0]) for got in mlp_got]
    mlp_sum = reduce_line(mlp_own, mlp_got)
    shared = after(shared, attn_sent[0])
    shared = shared + other_core(shared)
    row_width = 8 * MODEL + 2 * FF
    cls_rows = run_kernel(
        cls_rows_kernel,
        "head_rows",
        [shape_of((GROUP, row_width), LOW)],
        where,
        (),
        (pack,) + tuple(mlp_got) + (heads, cls_branch, cls_low, cls_second),
        [pltpu.VMEM((LINE,) + pack.shape, LOW)],
    )[0]
    attn_plane = tuple(after(got, cls_rows) for got in attn_plane)
    attn_own, *attn_sent = reduce_fold(where, attn_near[2], attn_plane)
    attn_lines = [along_line(attn_sent[apart - 1], apart) for apart in range(1, LINE)]
    payload_line = jnp.concatenate(payload_parts)
    mlp_mine, own_vecs = run_kernel(
        head_share_kernel,
        "seg_head_share",
        [shape_of((own_rows, FF)), shape_of((16, MODEL))],
        where,
        (),
        tuple(
            after(got, attn_lines[0]) for got in plane_parts(after(payload_line, *attn_plane))
        )
        + (mlp_sum,),
        [pltpu.VMEM((GROUP * 24, MODEL), LOW)],
    )
    flat = pltpu.VMEM((1, 8 * MODEL + FF), WIDE)
    seg_vec_grad = run_kernel(
        seg_vec_kernel,
        "seg_vector",
        [shape_of((1, vec_size))],
        where,
        (),
        (own_vecs, other_core(own_vecs)),
        [flat],
    )[0].reshape(vec_size)
    seg_mats_grad = run_kernel(
        mlp_store_kernel,
        "seg_mlp_store",
        [shape_of((own_rows, total_columns))],
        where,
        (),
        (mlp_mine, other_core(mlp_mine)),
        [pltpu.SemaphoreType.DMA((4,))],
        far=(0,),
    )[0]

    cls_mats_grad, cls_vec_grad = run_kernel(
        cls_owner_kernel,
        "head_owner",
        [shape_of((own_rows, total_columns)), shape_of((1, vec_size))],
        where,
        (),
        (cls_rows, other_core(cls_rows), after(shared, attn_lines[1])),
        [pltpu.VMEM((CORES * GROUP, row_width), LOW), flat],
        flops=64 * own_rows * total_columns,
    )
    cls_vec_grad = cls_vec_grad.reshape(vec_size)
    pos_total = shared[:GROUP]
    loss_value = shared[GROUP, 0] / (count[0, 0] * MODEL)
    ready = (output, input_grad, cls_mats_grad, cls_vec_grad, pos_total, seg_vec_grad)
    attn_lines[-1] = after(attn_lines[-1], seg_mats_grad, *ready)
    attn_sum = reduce_line(attn_own, attn_lines)
    seg_mats_grad = store_attn(where, attn_sum, other_core(attn_sum), seg_mats_grad)

    return (
        output,
        input_grad,
        seg_mats_grad,
        seg_vec_grad,
        cls_mats_grad,
        cls_vec_grad,
        pos_total,
        loss_value,
    )


def solution(mesh):
    in_specs = (
        P(("rep", "fsdp"), None),
        P(("rep", "fsdp"), None),
        P(("rep", "fsdp")),
        P(("rep", "fsdp")),
        P(("rep", "fsdp")),
        P("fsdp", None),
        P("fsdp"),
        P("fsdp", None),
        P("fsdp"),
        P(),
    )
    out_specs = (
        P(("rep", "fsdp"), None),
        P(("rep", "fsdp"), None),
        P("fsdp", None),
        P("fsdp"),
        P("fsdp", None),
        P("fsdp"),
        P(),
        P(),
    )
    one_slice = dict(mesh.shape) == {"rep": CORES, "fsdp": LINE * PLANE}
    body = slice_local if one_slice else local
    return jax.shard_map(body, mesh=mesh, in_specs=in_specs, out_specs=out_specs, check_vma=False)
```

```python
import math

import jax
import jax.numpy as jnp
from jax import lax
from jax.experimental import pallas as pl
from jax.experimental.pallas import tpu as pltpu
from jax.sharding import PartitionSpec as P

HEADS = 12
HEAD_DIM = 64
FF = 3072
SEG = 128
SEQ = 2048


NORM_EPS = 1e-05
MASK_FILL = -1e30
SQRT_HALF = 0.7071067811865476
INV_SQRT_TWO_PI = 0.3989422804014327


def swapped(value, axis, apart):
    mask = 2**apart
    pairs = [(source, source ^ mask) for source in range(lax.axis_size(axis))]
    return lax.ppermute(value, axis, pairs)


def product_plain(left_side, right_side):
    return jnp.dot(left_side, right_side, preferred_element_type=jnp.float32)


def product_left(left_side, right_side):
    return lax.dot_general(
        left_side, right_side, (((0,), (0,)), ((), ())), preferred_element_type=jnp.float32
    )


def product_right(left_side, right_side):
    return lax.dot_general(
        left_side, right_side, (((1,), (1,)), ((), ())), preferred_element_type=jnp.float32
    )


def row_total(array_in):
    return jnp.sum(array_in.astype(jnp.float32), axis=0)


def unpack_weights(gathered, model_width, ff_width):
    matrix, vector = gathered
    vector = vector.astype(jnp.float32)
    pieces = tuple(
        (vector[offset * model_width : (offset + 1) * model_width] for offset in range(8))
    )
    return (
        (
            matrix[:, : 3 * model_width],
            matrix[:, 3 * model_width : 4 * model_width],
            matrix[:, 4 * model_width : 4 * model_width + ff_width],
            matrix[:, 4 * model_width + ff_width :],
        )
        + pieces
        + (vector[8 * model_width :],)
    )


def norm_forward(summed, gain_vec, shift_vec):
    row_mean = jnp.mean(summed, axis=-1, keepdims=True)
    centered = summed - row_mean
    inv_dev = lax.rsqrt(jnp.mean(centered * centered, axis=-1, keepdims=True) + NORM_EPS)
    normed = centered * inv_dev
    return (normed * gain_vec + shift_vec, normed, inv_dev)


def norm_backward(grad_out, normed, inv_dev, gain_vec):
    scaled = grad_out * gain_vec
    mean_one = jnp.mean(scaled, axis=-1, keepdims=True)
    mean_two = jnp.mean(scaled * normed, axis=-1, keepdims=True)
    grad_in = inv_dev * (scaled - mean_one - normed * mean_two)
    return (grad_in, jnp.sum(grad_out * normed, axis=0), jnp.sum(grad_out, axis=0))


def gelu_value(before):
    return 0.5 * before * (1.0 + lax.erf(before * SQRT_HALF))


def gelu_slope(before):
    return (
        0.5 * (1.0 + lax.erf(before * SQRT_HALF))
        + before * jnp.exp(-0.5 * before * before) * INV_SQRT_TWO_PI
    )


def attention_scores(queries, keys_in, allowed, score_scale):
    raw_scores = (
        jnp.einsum("bqhe,bkhe->bhqk", queries, keys_in, preferred_element_type=jnp.float32)
        * score_scale
    )
    return jnp.where(allowed, raw_scores, MASK_FILL)


def attention_forward(queries, keys_in, values, allowed, score_scale):
    scores = attention_scores(queries, keys_in, allowed, score_scale)
    row_top = jnp.max(scores, axis=-1, keepdims=True)
    log_total = row_top + jnp.log(jnp.sum(jnp.exp(scores - row_top), axis=-1, keepdims=True))
    weights = jnp.exp(scores - log_total).astype(jnp.bfloat16)
    mixed_rows = jnp.einsum("bhqk,bkhe->bqhe", weights, values, preferred_element_type=jnp.float32)
    return (mixed_rows, log_total)


def attention_backward(queries, keys_in, values, allowed, score_scale, log_total, grad_mixed):
    probabilities = jnp.exp(attention_scores(queries, keys_in, allowed, score_scale) - log_total)
    grad_probs = jnp.einsum(
        "bqhe,bkhe->bhqk", grad_mixed, values, preferred_element_type=jnp.float32
    )
    inner_sum = jnp.sum(grad_probs * probabilities, axis=-1, keepdims=True)
    grad_scores = (probabilities * (grad_probs - inner_sum)).astype(jnp.bfloat16)
    grad_query = (
        jnp.einsum("bhqk,bkhe->bqhe", grad_scores, keys_in, preferred_element_type=jnp.float32)
        * score_scale
    )
    grad_key = (
        jnp.einsum("bhqk,bqhe->bkhe", grad_scores, queries, preferred_element_type=jnp.float32)
        * score_scale
    )
    grad_value = jnp.einsum(
        "bhqk,bqhe->bkhe",
        probabilities.astype(jnp.bfloat16),
        grad_mixed,
        preferred_element_type=jnp.float32,
    )
    return (grad_query, grad_key, grad_value)


def block_forward(rows_in, unpacked, attend):
    (
        qkv_weight,
        out_weight,
        up_weight,
        down_weight,
        query_bias,
        value_bias,
        out_bias,
        down_bias,
        gain_first,
        shift_first,
        gain_second,
        shift_second,
        up_bias,
    ) = unpacked
    model_width = rows_in.shape[1]
    inputs = rows_in.astype(jnp.bfloat16)
    projected = product_plain(inputs, qkv_weight)
    queries = (projected[:, :model_width] + query_bias).astype(jnp.bfloat16)
    keys_in = projected[:, model_width : 2 * model_width].astype(jnp.bfloat16)
    values = (projected[:, 2 * model_width :] + value_bias).astype(jnp.bfloat16)
    mixed_rows, attend_kept = attend(queries, keys_in, values)
    mixed_rows = mixed_rows.astype(jnp.bfloat16)
    summed_first = rows_in + product_plain(mixed_rows, out_weight) + out_bias
    first_out, normed_first, inv_first = norm_forward(summed_first, gain_first, shift_first)
    first_low = first_out.astype(jnp.bfloat16)
    pre_act = product_plain(first_low, up_weight) + up_bias
    activated = gelu_value(pre_act).astype(jnp.bfloat16)
    summed_second = first_out + product_right(activated, down_weight) + down_bias
    block_out, normed_second, inv_second = norm_forward(summed_second, gain_second, shift_second)
    saved_state = (
        inputs,
        queries,
        keys_in,
        values,
        attend_kept,
        mixed_rows,
        normed_first,
        inv_first,
        first_low,
        pre_act,
        activated,
        normed_second,
        inv_second,
    )
    return (block_out, saved_state)


def block_backward(grad_out, unpacked, saved_state, attend_back):
    (
        qkv_weight,
        out_weight,
        up_weight,
        down_weight,
        query_bias,
        value_bias,
        out_bias,
        down_bias,
        gain_first,
        shift_first,
        gain_second,
        shift_second,
        up_bias,
    ) = unpacked
    (
        inputs,
        queries,
        keys_in,
        values,
        attend_kept,
        mixed_rows,
        normed_first,
        inv_first,
        first_low,
        pre_act,
        activated,
        normed_second,
        inv_second,
    ) = saved_state
    grad_second, grad_gain_second, grad_shift_second = norm_backward(
        grad_out, normed_second, inv_second, gain_second
    )
    second_low = grad_second.astype(jnp.bfloat16)
    grad_pre = (product_plain(second_low, down_weight) * gelu_slope(pre_act)).astype(jnp.bfloat16)
    grad_first = grad_second + product_right(grad_pre, up_weight)
    grad_summed, grad_gain_first, grad_shift_first = norm_backward(
        grad_first, normed_first, inv_first, gain_first
    )
    branch_low = grad_summed.astype(jnp.bfloat16)
    grad_mixed = product_right(branch_low, out_weight).astype(jnp.bfloat16)
    grad_query, grad_key, grad_value = attend_back(
        queries, keys_in, values, attend_kept, grad_mixed
    )
    grad_proj = jnp.concatenate([grad_query, grad_key, grad_value], axis=1)
    grad_rows = grad_summed + product_right(grad_proj, qkv_weight)
    vector_grad = jnp.concatenate(
        [
            row_total(grad_query),
            row_total(grad_value),
            row_total(branch_low),
            row_total(second_low),
            grad_gain_first,
            grad_shift_first,
            grad_gain_second,
            grad_shift_second,
            row_total(grad_pre),
        ]
    )
    weight_rows = (
        inputs,
        grad_proj,
        mixed_rows,
        branch_low,
        first_low,
        grad_pre,
        second_low,
        activated,
    )
    return (grad_rows, weight_rows, vector_grad)


def weight_products(weight_rows):
    inputs, grad_proj, mixed_rows, branch_low, first_low, grad_pre, second_low, activated = (
        weight_rows
    )
    return (
        product_left(inputs, grad_proj),
        product_left(mixed_rows, branch_low),
        product_left(first_low, grad_pre),
        product_left(second_low, activated),
    )


def local(
    hidden_in,
    targets,
    doc_ids,
    seg_nums,
    valid_flags,
    seg_mats,
    seg_vecs,
    cls_mats,
    cls_vecs,
    seg_pos,
):
    tok_rows, model_width = hidden_in.shape
    ff_width = FF
    seg_len = SEG
    group_span = SEQ // tok_rows
    seg_count = tok_rows // seg_len
    score_scale = HEAD_DIM ** (-0.5)
    head_shape = (HEADS, HEAD_DIM)
    live_rows = valid_flags.astype(jnp.float32)
    rank_full = lax.axis_index("fsdp")
    seg_gathered = (
        lax.all_gather(seg_mats, "fsdp", axis=0, tiled=True),
        lax.all_gather(seg_vecs, "fsdp", axis=0, tiled=True),
    )
    seg_unpacked = unpack_weights(seg_gathered, model_width, ff_width)
    cls_gathered = (
        lax.all_gather(cls_mats, "fsdp", axis=0, tiled=True),
        lax.all_gather(cls_vecs, "fsdp", axis=0, tiled=True),
    )
    cls_unpacked = unpack_weights(cls_gathered, model_width, ff_width)
    seg_allowed = (live_rows.reshape(seg_count, 1, 1, seg_len) > 0.5) | jnp.eye(seg_len, dtype=bool)
    seg_shape = (seg_count, seg_len) + head_shape

    def seg_attend(queries, keys_in, values):
        mixed_rows, log_total = attention_forward(
            queries.reshape(seg_shape),
            keys_in.reshape(seg_shape),
            values.reshape(seg_shape),
            seg_allowed,
            score_scale,
        )
        return (mixed_rows.reshape(tok_rows, model_width), log_total)

    def seg_attend_back(queries, keys_in, values, log_total, grad_mixed):
        grad_parts = attention_backward(
            queries.reshape(seg_shape),
            keys_in.reshape(seg_shape),
            values.reshape(seg_shape),
            seg_allowed,
            score_scale,
            log_total,
            grad_mixed.reshape(seg_shape),
        )
        return tuple(
            (
                grad_part.reshape(tok_rows, model_width).astype(jnp.bfloat16)
                for grad_part in grad_parts
            )
        )

    first_out, seg_saved = block_forward(hidden_in.astype(jnp.float32), seg_unpacked, seg_attend)
    first_grid = first_out.reshape(seg_count, seg_len, model_width)
    position_hot = (seg_nums[:, None] == jnp.arange(seg_pos.shape[0])[None, :]).astype(jnp.float32)
    position_rows = jnp.sum(
        position_hot[:, :, None] * seg_pos.astype(jnp.float32)[None, :, :], axis=1
    )
    heads_in = first_grid[:, 0, :] + position_rows
    lead_live = live_rows.reshape(seg_count, seg_len)[:, 0]
    lead_doc = doc_ids.reshape(seg_count, seg_len)[:, 0]
    lead_labels = jnp.where(lead_live > 0.5, lead_doc, -1).astype(jnp.bfloat16)
    lead_doc_low = lead_doc.astype(jnp.bfloat16)
    bit_count = group_span.bit_length() - 1
    key_total = group_span * seg_count
    own_slot = rank_full % group_span * seg_count + jnp.arange(seg_count)
    query_shape = (1, seg_count) + head_shape
    key_shape = (1, key_total) + head_shape

    def cls_attend(queries, keys_in, values):
        paired = jnp.concatenate([keys_in, values], axis=1)
        labels = lead_labels
        for bit_level in range(bit_count):
            other_pair, other_labels = swapped((paired, labels), "fsdp", bit_level)
            upper_half = rank_full // (1 << bit_level) % 2 == 1
            paired = jnp.where(
                upper_half,
                jnp.concatenate([other_pair, paired]),
                jnp.concatenate([paired, other_pair]),
            )
            labels = jnp.where(
                upper_half,
                jnp.concatenate([other_labels, labels]),
                jnp.concatenate([labels, other_labels]),
            )
        allowed = (labels[None, :] == lead_doc_low[:, None]) | (
            jnp.arange(key_total)[None, :] == own_slot[:, None]
        )
        allowed = allowed[None, None]
        mixed_rows, log_total = attention_forward(
            queries.reshape(query_shape),
            paired[:, :model_width].reshape(key_shape),
            paired[:, model_width:].reshape(key_shape),
            allowed,
            score_scale,
        )
        return (mixed_rows.reshape(seg_count, model_width), (paired, allowed, log_total))

    def cls_attend_back(queries, keys_in, values, attend_kept, grad_mixed):
        paired, allowed, log_total = attend_kept
        grad_query, grad_key, grad_value = attention_backward(
            queries.reshape(query_shape),
            paired[:, :model_width].reshape(key_shape),
            paired[:, model_width:].reshape(key_shape),
            allowed,
            score_scale,
            log_total,
            grad_mixed.reshape(query_shape),
        )
        grad_pair = jnp.concatenate(
            [grad_key.reshape(key_total, model_width), grad_value.reshape(key_total, model_width)],
            axis=1,
        )
        for bit_level in reversed(range(bit_count)):
            half_rows = grad_pair.shape[0] // 2
            upper_half = rank_full // (1 << bit_level) % 2 == 1
            kept_half = jnp.where(upper_half, grad_pair[half_rows:], grad_pair[:half_rows])
            sent_half = jnp.where(upper_half, grad_pair[:half_rows], grad_pair[half_rows:])
            grad_pair = kept_half + swapped(
                sent_half.astype(jnp.bfloat16), "fsdp", bit_level
            ).astype(sent_half.dtype)
        grad_pair = grad_pair.astype(jnp.bfloat16)
        return (
            grad_query.reshape(seg_count, model_width).astype(jnp.bfloat16),
            grad_pair[:, :model_width],
            grad_pair[:, model_width:],
        )

    top_out, cls_saved = block_forward(heads_in, cls_unpacked, cls_attend)
    combined = jnp.concatenate([top_out[:, None, :], first_grid[:, 1:, :]], axis=1).reshape(
        tok_rows, model_width
    )
    output_rows = combined * live_rows[:, None]
    diff_rows = (output_rows - targets.astype(jnp.float32)) * live_rows[:, None]
    count_all, square_all = lax.psum(
        (jnp.sum(live_rows), jnp.sum(diff_rows * diff_rows)), ("rep", "fsdp")
    )
    loss_value = square_all / (count_all * model_width)
    slots_all = tok_rows * lax.axis_size("rep") * lax.axis_size("fsdp")
    grad_grid = (diff_rows * (slots_all / count_all)).reshape(seg_count, seg_len, model_width)
    cls_back = unpack_weights(
        (
            lax.all_gather(cls_mats, "fsdp", axis=0, tiled=True),
            lax.all_gather(cls_vecs, "fsdp", axis=0, tiled=True),
        ),
        model_width,
        ff_width,
    )
    heads_grad, cls_weight_rows, cls_g_vec = block_backward(
        grad_grid[:, 0, :], cls_back, cls_saved, cls_attend_back
    )
    cls_g_qkv, cls_g_out, cls_g_up, cls_g_down = weight_products(cls_weight_rows)
    pos_local = jnp.sum(position_hot[:, :, None] * heads_grad[:, None, :], axis=0)
    seg_grad_out = jnp.concatenate([heads_grad[:, None, :], grad_grid[:, 1:, :]], axis=1).reshape(
        tok_rows, model_width
    )
    seg_back = unpack_weights(
        (
            lax.all_gather(seg_mats, "fsdp", axis=0, tiled=True),
            lax.all_gather(seg_vecs, "fsdp", axis=0, tiled=True),
        ),
        model_width,
        ff_width,
    )
    input_grad, seg_weight_rows, seg_g_vec = block_backward(
        seg_grad_out, seg_back, seg_saved, seg_attend_back
    )
    seg_g_qkv, seg_g_out, seg_g_up, seg_g_down = weight_products(seg_weight_rows)
    owner_rows = tuple(
        (
            lax.psum_scatter(seg_g_qkv, "fsdp", scatter_dimension=0, tiled=True),
            lax.psum_scatter(seg_g_out, "fsdp", scatter_dimension=0, tiled=True),
            lax.psum_scatter(seg_g_up, "fsdp", scatter_dimension=0, tiled=True),
            lax.psum_scatter(seg_g_down, "fsdp", scatter_dimension=0, tiled=True),
            lax.psum_scatter(seg_g_vec, "fsdp", scatter_dimension=0, tiled=True),
            lax.psum_scatter(cls_g_qkv, "fsdp", scatter_dimension=0, tiled=True),
            lax.psum_scatter(cls_g_out, "fsdp", scatter_dimension=0, tiled=True),
            lax.psum_scatter(cls_g_up, "fsdp", scatter_dimension=0, tiled=True),
            lax.psum_scatter(cls_g_down, "fsdp", scatter_dimension=0, tiled=True),
            lax.psum_scatter(cls_g_vec, "fsdp", scatter_dimension=0, tiled=True),
        )
    )
    replica_share = (
        lax.psum_scatter(
            owner_rows[0].astype(jnp.bfloat16), "rep", scatter_dimension=1, tiled=True
        ).astype(jnp.float32),
        lax.psum_scatter(
            owner_rows[1].astype(jnp.bfloat16), "rep", scatter_dimension=1, tiled=True
        ).astype(jnp.float32),
        lax.psum_scatter(
            owner_rows[2].astype(jnp.bfloat16), "rep", scatter_dimension=1, tiled=True
        ).astype(jnp.float32),
        lax.psum_scatter(
            owner_rows[3].astype(jnp.bfloat16), "rep", scatter_dimension=1, tiled=True
        ).astype(jnp.float32),
        lax.psum_scatter(
            owner_rows[4].astype(jnp.bfloat16), "rep", scatter_dimension=0, tiled=True
        ).astype(jnp.float32),
        lax.psum_scatter(
            owner_rows[5].astype(jnp.bfloat16), "rep", scatter_dimension=1, tiled=True
        ).astype(jnp.float32),
        lax.psum_scatter(
            owner_rows[6].astype(jnp.bfloat16), "rep", scatter_dimension=1, tiled=True
        ).astype(jnp.float32),
        lax.psum_scatter(
            owner_rows[7].astype(jnp.bfloat16), "rep", scatter_dimension=1, tiled=True
        ).astype(jnp.float32),
        lax.psum_scatter(
            owner_rows[8].astype(jnp.bfloat16), "rep", scatter_dimension=1, tiled=True
        ).astype(jnp.float32),
        lax.psum_scatter(
            owner_rows[9].astype(jnp.bfloat16), "rep", scatter_dimension=0, tiled=True
        ).astype(jnp.float32),
    )
    all_summed = (
        lax.all_gather(replica_share[0].astype(jnp.bfloat16), "rep", axis=1, tiled=True).astype(
            jnp.float32
        ),
        lax.all_gather(replica_share[1].astype(jnp.bfloat16), "rep", axis=1, tiled=True).astype(
            jnp.float32
        ),
        lax.all_gather(replica_share[2].astype(jnp.bfloat16), "rep", axis=1, tiled=True).astype(
            jnp.float32
        ),
        lax.all_gather(replica_share[3].astype(jnp.bfloat16), "rep", axis=1, tiled=True).astype(
            jnp.float32
        ),
        lax.all_gather(replica_share[4].astype(jnp.bfloat16), "rep", axis=0, tiled=True).astype(
            jnp.float32
        ),
        lax.all_gather(replica_share[5].astype(jnp.bfloat16), "rep", axis=1, tiled=True).astype(
            jnp.float32
        ),
        lax.all_gather(replica_share[6].astype(jnp.bfloat16), "rep", axis=1, tiled=True).astype(
            jnp.float32
        ),
        lax.all_gather(replica_share[7].astype(jnp.bfloat16), "rep", axis=1, tiled=True).astype(
            jnp.float32
        ),
        lax.all_gather(replica_share[8].astype(jnp.bfloat16), "rep", axis=1, tiled=True).astype(
            jnp.float32
        ),
        lax.all_gather(replica_share[9].astype(jnp.bfloat16), "rep", axis=0, tiled=True).astype(
            jnp.float32
        ),
    )
    seg_summed = all_summed[:5]
    cls_summed = all_summed[5:]
    pos_total = lax.psum(pos_local, ("rep", "fsdp"))
    seg_mat_grad = jnp.concatenate(
        [seg_summed[0], seg_summed[1], seg_summed[2], seg_summed[3]], axis=1
    )
    cls_mat_grad = jnp.concatenate(
        [cls_summed[0], cls_summed[1], cls_summed[2], cls_summed[3]], axis=1
    )
    return (
        output_rows.astype(jnp.bfloat16),
        input_grad.astype(jnp.bfloat16),
        seg_mat_grad,
        seg_summed[4],
        cls_mat_grad,
        cls_summed[4],
        pos_total,
        loss_value,
    )


LINE = 4
PLANE = 4
CORES = 2
LANES = 128
GROUP = LINE * PLANE
LOW, WIDE = jnp.bfloat16, jnp.float32
MODEL = HEADS * HEAD_DIM
SPAN = 2 * LANES
TILE_START = (0, 1, 3, 4)


def line_pairs(apart):
    return [(source, (source + apart * PLANE) % GROUP) for source in range(GROUP)]


def plane_pairs(mask):
    return [(source, source ^ mask) for source in range(GROUP)]


def along_line(value, apart):
    return lax.ppermute(value, "fsdp", line_pairs(apart))


def in_plane(value, mask):
    return lax.ppermute(value, "fsdp", plane_pairs(mask))


def other_core(value):
    return lax.ppermute(value, "rep", [(0, 1), (1, 0)])


def after(value, *events):
    return lax.optimization_barrier((value,) + events)[0]


def together(*values):
    return tuple(lax.optimization_barrier(values))


def shape_of(dims, dtype=WIDE):
    return jax.ShapeDtypeStruct(dims, dtype)


def run_kernel(body, name, outs, where, blocks, arrays, scratch=(), far=(), flops=0):
    in_specs = [pl.BlockSpec(memory_space=pltpu.SMEM)]
    in_specs += [pl.BlockSpec(memory_space=pltpu.HBM)] * len(blocks)
    in_specs += [pl.BlockSpec(memory_space=pltpu.VMEM)] * len(arrays)
    spaces = [pltpu.HBM if at in far else pltpu.VMEM for at in range(len(outs))]
    moved = sum(x.size * x.dtype.itemsize for x in list(blocks) + list(arrays))
    moved += sum(math.prod(o.shape) * jnp.dtype(o.dtype).itemsize for o in outs)
    return pl.pallas_call(
        body,
        name=name,
        out_shape=tuple(outs),
        in_specs=in_specs,
        out_specs=tuple(pl.BlockSpec(memory_space=space) for space in spaces),
        scratch_shapes=list(scratch),
        cost_estimate=pl.CostEstimate(flops=flops, bytes_accessed=moved, transcendentals=0),
        compiler_params=pltpu.CompilerParams(vmem_limit_bytes=VMEM_BYTES),
    )(where, *blocks, *arrays)


VMEM_BYTES = 24 * 1024 * 1024
HALF = MODEL // CORES
FF_HALF = FF // CORES
OWN = MODEL // GROUP
QUARTER = 3 * SPAN + 2 * FF // LINE
QUARTER_HALF = QUARTER // CORES


def aligned(start):
    return pl.multiple_of(start, LANES)


def wait_all(copies):
    for copy in copies:
        copy.wait()


def run_copies(pairs, sems):
    copies = [
        pltpu.make_async_copy(source, target, sems.at[at])
        for at, (source, target) in enumerate(pairs)
    ]
    for copy in copies:
        copy.start()
    wait_all(copies)


FIRST = 4 * HALF + LANES
OWN_CUT = FIRST + FF_HALF // 2
LINE_CUTS = (7 * LANES, FF_HALF // 2, FF_HALF // 2)
WIDTHS = (FIRST, FF_HALF, FF_HALF)


def group_pieces(group, refs):
    own, rest = refs[:LINE], refs[LINE:]
    own_x, own_y, far_x, far_y, line_x, line_y, late_x, late_y = rest
    width, cut = WIDTHS[group], LINE_CUTS[group]
    start = sum(WIDTHS[:group])
    if group == 0:
        bases = (sum(WIDTHS) - OWN_CUT, OWN_CUT)
    else:
        before, before_cut = WIDTHS[group - 1], LINE_CUTS[group - 1]
        bases = (2 * before - before_cut, before + before_cut)
    pieces = {(0, step): [(own[step], 0, 0, width)] for step in range(LINE)}
    for mask, whole, line, base in ((1, own_x, line_x, bases[0]), (2, own_y, line_y, bases[1])):
        pieces[mask, 0] = [(whole, start, 0, width)]
        for step in range(1, LINE):
            pieces[mask, step] = [(line, base + (step - 1) * width, 0, width)]
    middle = min(max(OWN_CUT - start, 0), width)
    far = []
    if middle > 0:
        far.append((far_y, start, 0, middle))
    if middle < width:
        far.append((far_x, start + middle - OWN_CUT, middle, width))
    pieces[3, 0] = far
    pieces[3, 1] = [(late_y, 0, 0, width)]
    pieces[3, 2] = [(late_y, width, 0, cut), (late_x, 0, cut, width)]
    pieces[3, 3] = [(late_x, width - cut, 0, width)]
    return pieces


def gather_group(where, group, refs, targets):
    line_at, plane_at = where[0], where[1]
    for (mask, step), parts in group_pieces(group, refs).items():
        chip = (line_at + LINE - step) % LINE * PLANE + (plane_at ^ mask)
        for whole, first, last in targets:
            for ref, offset, begin, end in parts:
                low, high = max(first, begin), min(last, end)
                if low < high:
                    source = slice(offset + low - begin, offset + high - begin)
                    whole[chip, :, low - first : high - first] = ref[:, source]


def gather_blocks(where, refs, base, width, targets):
    line_at, plane_at = where[0], where[1]
    half = LINE // 2
    for mask in range(PLANE):
        for step in range(LINE):
            if mask == 0:
                ref, offset = refs[step], 0
            elif mask == 3:
                ref = refs[LINE + 3] if step < half else refs[LINE + 2]
                offset = step % half * width
            else:
                ref, offset = refs[LINE + mask - 1], base + step * width
            chip = (line_at + LINE - step) % LINE * PLANE + (plane_at ^ mask)
            for whole, first, last in targets:
                whole[chip] = ref[:, offset + first : offset + last]


def whole_rows(ref):
    value = ref[...]
    return value.reshape(value.shape[0] * value.shape[1], value.shape[2])


def prepare_first_kernel(where, seg, vecs, flags, out, live_out, sems):
    core_at = where[2]
    pairs = []
    for piece in range(4):
        source = seg.at[:, pl.ds(aligned(piece * MODEL + core_at * HALF), HALF)]
        pairs.append((source, out.at[:, piece * HALF : (piece + 1) * HALF]))
    run_copies(pairs, sems)
    size = vecs.shape[1]
    lines = -(-size // LANES)
    block = jnp.zeros((OWN, LANES), WIDE)
    row_at = lax.broadcasted_iota(jnp.int32, (OWN, LANES), 0)
    for which in range(2):
        for line in range(lines):
            width = min(LANES, size - line * LANES)
            value = vecs[which : which + 1, line * LANES : line * LANES + width]
            if width < LANES:
                value = jnp.concatenate([value, jnp.zeros((1, LANES - width), WIDE)], axis=1)
            block = jnp.where(row_at == which * lines + line, value, block)
    live = flags[...].astype(WIDE)
    live_out[...] = live
    count = jnp.sum(live, axis=1, keepdims=True)
    block = jnp.where(row_at == 2 * lines, count, block)
    out[:, 4 * HALF :] = block.astype(LOW)


def prepare_rest_kernel(where, seg, cls, *refs):
    second_out, third_out = refs[:2]
    step_outs, out_half, order_out = refs[2 : 2 + LINE], refs[2 + LINE], refs[3 + LINE]
    quarters, sems = refs[4 + LINE :]
    line_at, plane_at, core_at = where[0], where[1], where[2]
    start = core_at * FF_HALF
    pairs = [
        (seg.at[:, pl.ds(aligned(4 * MODEL + start), FF_HALF)], second_out),
        (seg.at[:, pl.ds(aligned(4 * MODEL + FF + start), FF_HALF)], third_out),
        (cls.at[:, pl.ds(aligned(3 * MODEL + core_at * HALF), HALF)], out_half),
    ]
    part = FF // LINE
    for at in range(LINE):
        first = TILE_START[at] * LANES
        plan = [(piece * MODEL + first, SPAN, piece * SPAN) for piece in range(3)]
        plan += [
            (4 * MODEL + piece * FF + at * part, part, 3 * SPAN + piece * part)
            for piece in range(2)
        ]
        for source, size, target in plan:
            pairs.append(
                (
                    cls.at[:, source : source + size],
                    quarters.at[at, :, target : target + size],
                )
            )
    run_copies(pairs, sems)
    lanes = pl.ds(aligned(core_at * QUARTER_HALF), QUARTER_HALF)
    for step, out in enumerate(step_outs):
        out[...] = quarters[(line_at + step) % LINE, :, lanes]
    column = lax.broadcasted_iota(jnp.int32, (1, SPAN), 1)
    feature = lax.broadcasted_iota(jnp.int32, (MODEL, SPAN), 0)
    turn = sum((column >= OWN * step).astype(jnp.int32) for step in range(1, LINE))
    held = column - OWN * turn
    turn = (line_at + turn) % LINE
    for mask in range(PLANE):
        source = (turn * PLANE + (plane_at ^ mask)) * OWN + held
        source = jnp.where(column < OWN * LINE, source, -1)
        order_out[:, mask * SPAN : (mask + 1) * SPAN] = (feature == source).astype(LOW)


def lane_mask(rows, head):
    lane = lax.broadcasted_iota(jnp.int32, (rows, LANES), 1)
    return (lane < HEAD_DIM) if head == 0 else (lane >= HEAD_DIM)


def masked(value, mask):
    return jnp.where(mask, value, jnp.zeros_like(value))


def head_probabilities(query, key, allowed):
    scores = product_right(query, key) * HEAD_DIM ** (-0.5)
    scores = jnp.where(allowed, scores, MASK_FILL)
    raised = jnp.exp(scores - jnp.max(scores, axis=-1, keepdims=True))
    return raised / jnp.sum(raised, axis=-1, keepdims=True)


def attend_tiles(qkv, width, allowed):
    rows = qkv.shape[0]
    mixed = []
    for tile in range(width // LANES):
        at = tile * LANES
        query, key, value = (
            qkv[:, piece * width + at : piece * width + at + LANES] for piece in range(3)
        )
        total = jnp.zeros((rows, LANES), WIDE)
        for head in range(2):
            mask = lane_mask(rows, head)
            weights = head_probabilities(masked(query, mask), key, allowed).astype(LOW)
            total = total + product_plain(weights, masked(value, mask))
        mixed.append(total.astype(LOW))
    return mixed


def attend_tiles_back(qkv, grad_mixed, width, allowed):
    rows = qkv.shape[0]
    scale = HEAD_DIM ** (-0.5)
    results = ([], [], [])
    for tile in range(width // LANES):
        at = tile * LANES
        query, key, value = (
            qkv[:, piece * width + at : piece * width + at + LANES] for piece in range(3)
        )
        grad = grad_mixed[:, at : at + LANES]
        totals = [jnp.zeros((rows, LANES), WIDE) for _ in range(3)]
        for head in range(2):
            mask = lane_mask(rows, head)
            query_low, key_low, grad_low = (masked(x, mask) for x in (query, key, grad))
            chance = head_probabilities(query_low, key, allowed)
            grad_chance = product_right(grad_low, value)
            inner = jnp.sum(grad_chance * chance, axis=-1, keepdims=True)
            grad_scores = (chance * (grad_chance - inner)).astype(LOW)
            totals[0] = totals[0] + product_plain(grad_scores, key_low)
            totals[1] = totals[1] + product_left(grad_scores, query_low)
            totals[2] = totals[2] + product_left(chance.astype(LOW), grad_low)
        results[0].append((totals[0] * scale).astype(LOW))
        results[1].append((totals[1] * scale).astype(LOW))
        results[2].append(totals[2].astype(LOW))
    return results[0] + results[1] + results[2]


def token_allowed(live_row):
    shape = (SEG, SEG)
    same = lax.broadcasted_iota(jnp.int32, shape, 0) == lax.broadcasted_iota(jnp.int32, shape, 1)
    return (live_row > 0.5) | same


def qkv_kernel(where, *refs):
    blocks = refs[:12]
    hidden, hidden_got, live_row, live_got, order = refs[12:17]
    weight, out_low, out_high, qkv_out, mixed_out = refs[17:22]
    vectors_out, count_out, ordered_out = refs[22:25]
    vec_rows, flat, inputs, out_half = refs[25:]
    core_at = where[2]
    gather_group(
        where,
        0,
        blocks,
        (
            (weight, 0, 3 * HALF),
            (out_half, 3 * HALF, 4 * HALF),
            (vec_rows, 4 * HALF, 4 * HALF + LANES),
        ),
    )
    out_low[...] = out_half[: GROUP // 2]
    out_high[...] = out_half[GROUP // 2 :]
    piece = (8 * MODEL + FF) // GROUP
    lines = -(-piece // LANES)
    count = jnp.zeros((1, LANES), WIDE)
    for chip in range(GROUP):
        rows = vec_rows[chip, 0:16, :].astype(WIDE)
        for block in range(2):
            joined = jnp.concatenate(
                [rows[block * lines + r : block * lines + r + 1] for r in range(lines)], axis=1
            )
            flat[block : block + 1, chip * piece : (chip + 1) * piece] = joined[:, :piece]
        count = count + rows[2 * lines : 2 * lines + 1]
    rows_each = (8 * MODEL + FF) // MODEL
    for block in range(2):
        for row in range(rows_each):
            vectors_out[block * rows_each + row : block * rows_each + row + 1, :] = flat[
                block : block + 1, row * MODEL : (row + 1) * MODEL
            ]
    count_out[...] = jnp.broadcast_to(count, count_out.shape)
    inputs[:SEG] = hidden[...]
    inputs[SEG:] = hidden_got[...]
    projected = product_plain(inputs[...], whole_rows(weight))
    lanes = pl.ds(aligned(core_at * HALF), HALF)
    qkv_out[:, :HALF] = (projected[:, :HALF] + vectors_out[0:1, lanes]).astype(LOW)
    qkv_out[:, HALF : 2 * HALF] = projected[:, HALF : 2 * HALF].astype(LOW)
    qkv_out[:, 2 * HALF :] = (projected[:, 2 * HALF :] + vectors_out[1:2, lanes]).astype(LOW)
    for part, live in enumerate((live_row, live_got)):
        rows = slice(part * SEG, (part + 1) * SEG)
        tiles = attend_tiles(qkv_out[rows, :], HALF, token_allowed(live[...]))
        for tile, value in enumerate(tiles):
            mixed_out[rows, tile * LANES : (tile + 1) * LANES] = value
    ordered_out[...] = product_plain(inputs[...], order[...]).astype(LOW)


def norm_rows(summed):
    row_mean = jnp.mean(summed, axis=-1, keepdims=True)
    centered = summed - row_mean
    inv_dev = lax.rsqrt(jnp.mean(centered * centered, axis=-1, keepdims=True) + NORM_EPS)
    return centered * inv_dev, inv_dev


def norm_rows_back(grad_out, normed, inv_dev, gain):
    scaled = grad_out * gain
    mean_one = jnp.mean(scaled, axis=-1, keepdims=True)
    mean_two = jnp.mean(scaled * normed, axis=-1, keepdims=True)
    return inv_dev * (scaled - mean_one - normed * mean_two)


def column_sum(value):
    return jnp.sum(value.astype(WIDE), axis=0, keepdims=True)


def four_rows(vectors, first):
    return jnp.concatenate([vectors[first + at : first + at + 1, :] for at in range(4)], axis=1)


def gelu_both(before):
    half = 0.5 * (1.0 + lax.erf(before * SQRT_HALF))
    slope = half + before * jnp.exp(-0.5 * before * before) * INV_SQRT_TWO_PI
    return before * half, slope


def out_kernel(where, hidden, mixed, mixed_got, low, high, low_got, high_got, *refs):
    vectors, order, full_out, ordered_out, normed_out, inv_out, low_out, mixed_full = refs
    core_at = where[2]
    own, other = aligned(core_at * HALF), aligned((1 - core_at) * HALF)
    rows = MODEL // 2
    full_out[:rows, pl.ds(own, HALF)] = whole_rows(low)
    full_out[rows:, pl.ds(own, HALF)] = whole_rows(high)
    full_out[:rows, pl.ds(other, HALF)] = whole_rows(low_got)
    full_out[rows:, pl.ds(other, HALF)] = whole_rows(high_got)
    mixed_full[:, pl.ds(own, HALF)] = mixed[...]
    mixed_full[:SEG, pl.ds(other, HALF)] = mixed_got[SEG:, :]
    mixed_full[SEG:, pl.ds(other, HALF)] = mixed_got[:SEG, :]
    branch = product_plain(mixed_full[:SEG, :], full_out[...])
    normed, inv_dev = norm_rows(hidden[...].astype(WIDE) + branch + vectors[2:3, :])
    normed_out[...] = normed
    inv_out[...] = inv_dev
    low_out[...] = (normed * vectors[4:5, :] + vectors[5:6, :]).astype(LOW)
    ordered_out[...] = product_plain(mixed_full[...], order[...]).astype(LOW)


def up_kernel(where, *refs):
    blocks = refs[:12]
    low, low_got, vectors = refs[12:15]
    weight, act_out, slope_out, both = refs[15:]
    core_at = where[2]
    gather_group(where, 1, blocks, ((weight, 0, FF_HALF),))
    both[:SEG] = low[...]
    both[SEG:] = low_got[...]
    for at in range(FF_HALF // MODEL):
        columns = slice(at * MODEL, (at + 1) * MODEL)
        held = weight[:, :, columns]
        before = product_plain(both[...], held.reshape(MODEL, MODEL))
        bias = vectors[pl.ds(8 + core_at * (FF_HALF // MODEL) + at, 1), :]
        value, slope = gelu_both(before + bias)
        act_out[:, columns] = value.astype(LOW)
        slope_out[:, columns] = slope


def down_kernel(where, *refs):
    blocks, act = refs[:12], refs[12]
    weight, own_out, send_out = refs[13:]
    gather_group(where, 2, blocks, ((weight, 0, FF_HALF),))
    partial = product_right(act[...], whole_rows(weight))
    own_out[...] = partial[:SEG]
    send_out[...] = partial[SEG:]


def seg_rows_kernel(where, *refs):
    own, got, normed_first, vectors, targets, live, seg_pos = refs[:7]
    normed_out, inv_out, diff_out, rows_out, head_out = refs[7:]
    doc, number = where[3], where[4]
    first = normed_first[...] * vectors[4:5, :] + vectors[5:6, :]
    normed, inv_dev = norm_rows(first + own[...] + got[...] + vectors[3:4, :])
    normed_out[...] = normed
    inv_out[...] = inv_dev
    rows = normed * vectors[6:7, :] + vectors[7:8, :]
    shape = (SEG, SEG)
    same = lax.broadcasted_iota(jnp.int32, shape, 0) == lax.broadcasted_iota(jnp.int32, shape, 1)
    live_rows = jnp.sum(jnp.where(same, live[...], 0.0), axis=1, keepdims=True)
    target_rows = targets[...].astype(WIDE)
    output = rows * live_rows
    rows_out[...] = output
    diff = (output - target_rows) * live_rows
    row_at = lax.broadcasted_iota(jnp.int32, (SEG, 1), 0)
    diff = jnp.where(row_at > 0, diff, 0.0)
    diff_out[...] = diff
    table = seg_pos[...].astype(WIDE)
    chosen = lax.broadcasted_iota(jnp.int32, table.shape, 0) == number
    position = jnp.sum(jnp.where(chosen, table, 0.0), axis=0, keepdims=True)
    head_out[:, :MODEL] = rows[0:1, :] + position
    head_out[:, MODEL : 2 * MODEL] = target_rows[0:1, :]
    square = jnp.sum(column_sum(diff * diff), axis=1, keepdims=True)
    lane = lax.broadcasted_iota(jnp.int32, (1, LANES), 1)
    facts = jnp.where(lane == 0, live_rows[0:1, :], 0.0)
    facts = jnp.where(lane == 1, doc.astype(WIDE), facts)
    facts = jnp.where(lane == 2, number.astype(WIDE), facts)
    facts = jnp.where(lane == 3, square, facts)
    head_out[:, 2 * MODEL :] = facts


def second_norm_kernel(where, diff, count, normed, inv_dev, vectors, grad_out, low_out, sums_out):
    grad_top = diff[...] * ((SEG * GROUP * CORES) / count[0:1, 0:1])
    normed_rows = normed[...]
    grad = norm_rows_back(grad_top, normed_rows, inv_dev[...], vectors[6:7, :])
    low = grad.astype(LOW)
    grad_out[...] = grad
    low_out[...] = low
    sums_out[0:1, :] = column_sum(low)
    sums_out[1:2, :] = column_sum(grad_top * normed_rows)
    sums_out[2:3, :] = column_sum(grad_top)


def mlp_back_kernel(where, *refs):
    low, low_got, down_weight, up_weight, slope = refs[:5]
    pre_out, own_out, send_out, sums_out, both = refs[5:]
    both[:SEG] = low[...]
    both[SEG:] = low_got[...]
    for at in range(FF_HALF // MODEL):
        columns = slice(at * MODEL, (at + 1) * MODEL)
        held = down_weight[:, :, columns]
        before = product_plain(both[...], held.reshape(MODEL, MODEL))
        pre = (before * slope[:, columns]).astype(LOW)
        pre_out[:, columns] = pre
        sums_out[at : at + 1, :] = column_sum(pre)
    partial = product_right(pre_out[...], whole_rows(up_weight))
    own_out[...] = partial[:SEG]
    send_out[...] = partial[SEG:]


def scatter_parts(where, parts, outs, sems):
    line_at, plane_at = where[0], where[1]
    far_low, far_high, to_x, to_y, kept = outs
    half = LINE // 2
    copies = []
    for mask in range(PLANE):
        for step in range(LINE):
            source = parts.at[(line_at + step) % LINE * PLANE + (plane_at ^ mask)]
            if mask == 3:
                target = far_low.at[step] if step < half else far_high.at[step - half]
            else:
                target = (kept, to_x, to_y)[mask].at[step]
            copies.append(pltpu.make_async_copy(source, target, sems.at[len(copies)]))
    for copy in copies:
        copy.start()
    wait_all(copies)


def mlp_weight_kernel(where, *refs):
    first, first_got, second, second_got, pre, act = refs[:6]
    outs = refs[6:11]
    left, parts, sems = refs[11:]
    for at, (own, got, right) in enumerate(((first, first_got, pre), (second, second_got, act))):
        left[:SEG] = own[...]
        left[SEG:] = got[...]
        for piece in range(FF_HALF // MODEL):
            start = piece * MODEL
            product = product_left(left[...], right[:, start : start + MODEL]).astype(LOW)
            target = at * FF_HALF + start
            parts[:, :, target : target + MODEL] = product.reshape(GROUP, OWN, MODEL)
    scatter_parts(where, parts, outs, sems)


def attn_product(where, refs, mask, piece):
    hidden, mixed, proj, branch, got = refs
    lanes = slice(mask * SPAN, (mask + 1) * SPAN)
    if piece < 3:
        right = proj[:, piece * HALF : (piece + 1) * HALF]
        product = product_left(hidden[:, lanes], right)
    else:
        own = branch[:, pl.ds(aligned(where[2] * HALF), HALF)]
        product = product_left(mixed[:SEG, lanes], own)
        product = product + product_left(mixed[SEG:, lanes], got[:, HALF:])
    return product[: LINE * OWN].astype(LOW).reshape(LINE, OWN, HALF)


def attn_far_kernel(where, *refs):
    low_out, high_out = refs[5:]
    half = LINE // 2
    for piece in range(4):
        columns = slice(piece * HALF, (piece + 1) * HALF)
        product = attn_product(where, refs[:5], 3, piece)
        low_out[:, :, columns] = product[:half]
        high_out[:, :, columns] = product[half:]


def attn_near_kernel(where, *refs):
    top_row, out_rows, live_row = refs[5:8]
    row_at = lax.broadcasted_iota(jnp.int32, (SEG, 1), 0)
    output = jnp.where(row_at == 0, top_row[...] * live_row[:, 0:1], out_rows[...])
    refs[11][...] = output.astype(LOW)
    for mask, out in ((1, refs[8]), (2, refs[9]), (0, refs[10])):
        for piece in range(4):
            columns = slice(piece * HALF, (piece + 1) * HALF)
            out[:, :, columns] = attn_product(where, refs[:5], mask, piece)


def fold_kernel(where, kept, got_x, got_y, *refs):
    extra, own_out, sent = refs[: -LINE], refs[-LINE], refs[1 - LINE :]
    rows = kept.shape[1]
    for step in range(LINE):
        total = kept[step].astype(WIDE) + got_x[step].astype(WIDE) + got_y[step].astype(WIDE)
        if step == 0:
            own_out[...] = total
            continue
        out = sent[step - 1]
        out[:rows, :] = total.astype(LOW)
        if extra:
            out[rows:, :] = jnp.zeros_like(out[rows:, :])
            out[rows:, : extra[0].shape[1]] = extra[0][...]


def reduce_far(parts):
    return together(in_plane(parts[0], 2), in_plane(parts[1], 1))


def reduce_add(where, parts, far):
    shape = parts[2].shape
    return run_kernel(
        add_far_kernel,
        "add_far",
        [shape_of(shape, LOW)] * 2,
        where,
        (),
        tuple(far) + (parts[2], parts[3]),
    )


def reduce_fold(where, kept, got, *extra):
    _, rows, columns = kept.shape
    more = sum(value.shape[0] for value in extra)
    return run_kernel(
        fold_kernel,
        "fold",
        [shape_of((rows, columns))] + [shape_of((rows + more, columns), LOW)] * (LINE - 1),
        where,
        (),
        (kept,) + tuple(got) + extra,
    )


def reduce_line(own, pieces):
    total = own
    for piece in pieces:
        total = total + piece[: own.shape[0]].astype(WIDE)
    return total


def head_back_kernel(where, *refs):
    grad, grad_got, down_weight, up_weight, slope, act, low, low_got = refs[:8]
    own_out, send_out, data_out = refs[8:]
    few = 16
    row_at = lax.broadcasted_iota(jnp.int32, (few, 1), 0)

    def two_rows(first, second):
        return jnp.where(row_at == 0, first, jnp.where(row_at == 1, second, 0.0))

    second = two_rows(grad[...], grad_got[...]).astype(LOW)
    data_out[0:1, :] = low[0:1, :].astype(WIDE)
    data_out[1:2, :] = low_got[0:1, :].astype(WIDE)
    data_out[2:4, :] = second[0:2].astype(WIDE)
    partial = jnp.zeros((few, MODEL), WIDE)
    for at in range(FF_HALF // MODEL):
        columns = slice(at * MODEL, (at + 1) * MODEL)
        before = product_plain(second, down_weight[:, :, columns].reshape(MODEL, MODEL))
        slopes = two_rows(slope[0:1, columns], slope[SEG : SEG + 1, columns])
        pre = (before * slopes).astype(LOW)
        partial = partial + product_right(pre, up_weight[:, :, columns].reshape(MODEL, MODEL))
        data_out[4 + 2 * at : 6 + 2 * at, :] = pre[0:2].astype(WIDE)
        data_out[8 + 2 * at : 9 + 2 * at, :] = act[0:1, columns].astype(WIDE)
        data_out[9 + 2 * at : 10 + 2 * at, :] = act[SEG : SEG + 1, columns].astype(WIDE)
    own_out[...] = partial[0:1]
    send_out[...] = partial[1:2]


def first_norm_kernel(where, *refs):
    second_grad, own, got, head_grad, head_own, head_got = refs[:6]
    normed_rows, inv_dev, vectors, out_weight = refs[6:10]
    grad_out, branch_out, mixed_out, send_out, sums_out = refs[10:]
    core_at = where[2]
    grad_rows = second_grad[...] + own[...] + got[...]
    head = head_grad[...] + head_own[...] + head_got[...]
    row_at = lax.broadcasted_iota(jnp.int32, (SEG, 1), 0)
    grad_rows = jnp.where(row_at == 0, head, grad_rows)
    normed = normed_rows[...]
    grad = norm_rows_back(grad_rows, normed, inv_dev[...], vectors[4:5, :])
    grad_out[...] = grad
    branch = grad.astype(LOW)
    branch_out[...] = branch
    mixed_out[...] = product_right(branch, out_weight[...]).astype(LOW)
    other = pl.ds(aligned((1 - core_at) * HALF), HALF)
    send_out[:, :HALF] = mixed_out[:, other]
    send_out[:, HALF:] = branch_out[:, other]
    sums_out[0:1, :] = column_sum(branch)
    sums_out[1:2, :] = column_sum(grad_rows * normed)
    sums_out[2:3, :] = column_sum(grad_rows)


def attn_back_kernel(where, *refs):
    qkv, mixed_grad, got, live_row, live_got, weight = refs[:6]
    sums_first, sums_second, sums_up, head_top, head_normed, data = refs[6:12]
    proj_out, own_out, send_out, payload_out, rows = refs[12:]
    core_at = where[2]
    lanes = pl.ds(aligned(core_at * HALF), HALF)
    for part, live in enumerate((live_row, live_got)):
        at = slice(part * SEG, (part + 1) * SEG)
        grad = mixed_grad[:, lanes] if part == 0 else got[:, :HALF]
        pieces = attend_tiles_back(qkv[at, :], grad, HALF, token_allowed(live[...]))
        for tile, value in enumerate(pieces):
            proj_out[at, tile * LANES : (tile + 1) * LANES] = value
    partial = product_right(proj_out[...], whole_rows(weight))
    own_out[...] = partial[:SEG]
    send_out[...] = partial[SEG:]
    rows[...] = jnp.zeros_like(rows)
    rows[0:12, :] = data[0:12, :]
    rows[12:13, lanes] = column_sum(proj_out[:, :HALF])
    rows[13:14, lanes] = column_sum(proj_out[:, 2 * HALF :])
    rows[14:15, :] = sums_first[0:1, :]
    rows[15:16, :] = sums_second[0:1, :] + data[2:3, :]
    rows[16:18, :] = sums_first[1:3, :]
    rows[18:19, :] = sums_second[1:2, :] + head_top[...] * head_normed[0:1, :]
    rows[19:20, :] = sums_second[2:3, :] + head_top[...]
    for at in range(FF_HALF // MODEL):
        total = sums_up[at : at + 1, :] + data[4 + 2 * at : 5 + 2 * at, :]
        total = total + data[5 + 2 * at : 6 + 2 * at, :]
        rows[pl.ds(20 + core_at * (FF_HALF // MODEL) + at, 1), :] = total
    payload_out[...] = rows[...].astype(LOW)


def cls_gather_kernel(where, *refs):
    blocks = refs[:8]
    own_out, from_x, from_y, far_x = refs[8], refs[4], refs[5], refs[6]
    weight_out, out_rows = refs[9:]
    plane_at = where[1]
    gather_blocks(where, blocks, 0, QUARTER_HALF, ((weight_out, 0, QUARTER_HALF),))
    first = LINE * QUARTER_HALF
    out_rows[plane_at] = own_out[...]
    out_rows[plane_at ^ 1] = from_x[:, first : first + HALF]
    out_rows[plane_at ^ 2] = from_y[:, first : first + HALF]
    first = LINE // 2 * QUARTER_HALF
    out_rows[plane_at ^ 3] = far_x[:, first : first + HALF]


def cls_weight_kernel(where, own, got, out_half, out_got, weight_out, out_full):
    line_at, core_at = where[0], where[2]
    out_full[...] = jnp.zeros_like(out_full)
    for value, part, core in ((own, out_half, core_at), (got, out_got, 1 - core_at)):
        weight_out[:, :, pl.ds(aligned(core * QUARTER_HALF), QUARTER_HALF)] = value[...]
        rows = part[...].reshape(3, HEAD_DIM, HALF)
        out_full[pl.ds(line_at % 2, 3), :, pl.ds(aligned(core * HALF), HALF)] = rows


def add_far_kernel(where, far_low, far_high, to_x, to_y, x_out, y_out):
    half = LINE // 2
    x_out[:half] = to_x[:half] + far_low[...]
    x_out[half:] = to_x[half:]
    y_out[:half] = to_y[:half]
    y_out[half:] = to_y[half:] + far_high[...]


def row_from_column(column, size):
    shape = (size, size)
    same = lax.broadcasted_iota(jnp.int32, shape, 0) == lax.broadcasted_iota(jnp.int32, shape, 1)
    return jnp.sum(jnp.where(same, column, 0.0), axis=0, keepdims=True)


def head_allowed(heads):
    facts = heads[:, 2 * MODEL :]
    live, doc = facts[:, 0:1], facts[:, 1:2]
    shape = (GROUP, GROUP)
    same = lax.broadcasted_iota(jnp.int32, shape, 0) == lax.broadcasted_iota(jnp.int32, shape, 1)
    live_row, doc_row = row_from_column(live, GROUP), row_from_column(doc, GROUP)
    return ((live_row > 0.5) & (doc == doc_row)) | same


def quarter_mask(quarter):
    lane = lax.broadcasted_iota(jnp.int32, (GROUP, SPAN), 1)
    first = (quarter % 2) * HEAD_DIM
    return (lane >= first) & (lane < first + 3 * HEAD_DIM)


def quarter_piece(vectors, row, quarter):
    value = jnp.zeros((1, SPAN), WIDE)
    for at in range(LINE):
        first = TILE_START[at] * LANES
        value = jnp.where(quarter == at, vectors[row : row + 1, first : first + SPAN], value)
    return value


def cls_attend_kernel(where, *refs):
    stacks, vectors, weight, out_weight = refs[:4], refs[4], refs[5], refs[6]
    heads_out, qkv_out, mixed_out, part_out = refs[7:]
    line_at, plane_at = where[0], where[1]
    for step, stack in enumerate(stacks):
        for mask in range(PLANE):
            row = (line_at + LINE - step) % LINE * PLANE + (plane_at ^ mask)
            heads_out[pl.ds(row, 1), :] = stack[mask : mask + 1, :]
    heads = heads_out[...]
    inputs = heads[:, :MODEL].astype(LOW)
    projected = product_plain(inputs, weight[:, : 3 * SPAN])
    query = projected[:, :SPAN] + quarter_piece(vectors, 12, line_at)
    value = projected[:, 2 * SPAN :] + quarter_piece(vectors, 13, line_at)
    qkv_out[:, :SPAN] = query.astype(LOW)
    qkv_out[:, SPAN : 2 * SPAN] = projected[:, SPAN : 2 * SPAN].astype(LOW)
    qkv_out[:, 2 * SPAN :] = value.astype(LOW)
    mixed = attend_tiles(qkv_out[...], SPAN, head_allowed(heads))
    mixed = masked(jnp.concatenate(mixed, axis=1), quarter_mask(line_at))
    mixed_out[...] = mixed
    part_out[...] = product_plain(mixed, out_weight[...])


def cls_mlp_kernel(where, *refs):
    heads, own, got_one, got_two, got_three, vectors, weight = refs[:7]
    normed_out, inv_out, low_out, act_out, slope_out, part_out = refs[7:]
    line_at = where[0]
    branch = own[...] + got_one[...] + got_two[...] + got_three[...]
    normed, inv_dev = norm_rows(heads[:, :MODEL] + branch + vectors[14:15, :])
    normed_out[...] = normed
    inv_out[...] = inv_dev
    low = (normed * vectors[16:17, :] + vectors[17:18, :]).astype(LOW)
    low_out[...] = low
    part = FF // LINE
    first = 3 * SPAN
    bias = vectors[pl.ds(20 + line_at, 1), :]
    before = product_plain(low, weight[:, first : first + part]) + bias
    value, slope = gelu_both(before)
    act = value.astype(LOW)
    act_out[...] = act
    slope_out[...] = slope
    part_out[...] = product_right(act, weight[:, first + part :])


def cls_top_kernel(where, *refs):
    heads, own, got_one, got_two, got_three, vectors, weight = refs[:7]
    normed_first, count, slope = refs[7:10]
    top_out, square_out, grad_out, second_out, pre_out, part_out, sums_out = refs[10:17]
    held = refs[17]
    rank = where[0] * PLANE + where[1]
    first = normed_first[...] * vectors[16:17, :] + vectors[17:18, :]
    down = own[...] + got_one[...] + got_two[...] + got_three[...]
    normed, inv_dev = norm_rows(first + down + vectors[15:16, :])
    rows = normed * vectors[18:19, :] + vectors[19:20, :]
    held[...] = rows
    top_out[...] = held[pl.ds(rank, 1), :]
    facts = heads[:, 2 * MODEL :]
    live = facts[:, 0:1]
    diff = (rows * live - heads[:, MODEL : 2 * MODEL]) * live
    square = jnp.sum(column_sum(diff * diff), axis=1, keepdims=True)
    square = square + jnp.sum(facts[:, 3:4], axis=0, keepdims=True)
    square_out[...] = jnp.broadcast_to(square, square_out.shape)
    grad_top = diff * ((SEG * GROUP * CORES) / count[0:1, 0:1])
    grad = norm_rows_back(grad_top, normed, inv_dev, vectors[18:19, :])
    sums_out[0:1, :] = column_sum(grad_top * normed)
    sums_out[1:2, :] = column_sum(grad_top)
    grad_out[...] = grad
    second = grad.astype(LOW)
    second_out[...] = second
    part = FF // LINE
    at = 3 * SPAN
    pre = (product_plain(second, weight[:, at + part :]) * slope[...]).astype(LOW)
    pre_out[...] = pre
    part_out[...] = product_right(pre, weight[:, at : at + part])


def cls_attend_back_kernel(where, *refs):
    heads, own, got_one, got_two, got_three, vectors, weight, out_weight = refs[:8]
    grad_in, normed_first, inv_first, qkv = refs[8:12]
    grad_out, branch_out, proj_out, part_out, sums_out = refs[12:]
    line_at = where[0]
    grad_first = grad_in[...] + own[...] + got_one[...] + got_two[...] + got_three[...]
    normed = normed_first[...]
    grad = norm_rows_back(grad_first, normed, inv_first[...], vectors[16:17, :])
    sums_out[0:1, :] = column_sum(grad_first * normed)
    sums_out[1:2, :] = column_sum(grad_first)
    grad_out[...] = grad
    branch = grad.astype(LOW)
    branch_out[...] = branch
    mask = quarter_mask(line_at)
    mixed_grad = masked(product_right(branch, out_weight[...]).astype(LOW), mask)
    pieces = attend_tiles_back(qkv[...], mixed_grad, SPAN, head_allowed(heads[...]))
    tiles = SPAN // LANES
    for piece in range(3):
        joined = jnp.concatenate(pieces[piece * tiles : (piece + 1) * tiles], axis=1)
        proj_out[:, piece * SPAN : (piece + 1) * SPAN] = masked(joined, mask)
    part_out[...] = product_right(proj_out[...], weight[:, : 3 * SPAN])


def cls_end_kernel(where, *refs):
    heads, grad, own, got_one, got_two, got_three = refs[:6]
    square, sums_back, sums_top = refs[6:9]
    normed_second, inv_second, vectors = refs[9:12]
    row_out, second_out, shared_out, held = refs[12:]
    rank = where[0] * PLANE + where[1]
    total = grad[...] + own[...] + got_one[...] + got_two[...] + got_three[...]
    held[...] = total
    row = held[pl.ds(rank, 1), :]
    row_out[...] = row
    second_out[...] = norm_rows_back(
        row, normed_second[0:1, :], inv_second[0:1, :], vectors[6:7, :]
    )
    number = row_from_column(heads[:, 2 * MODEL + 2 : 2 * MODEL + 3], GROUP)
    entry = lax.broadcasted_iota(jnp.int32, (GROUP, GROUP), 0).astype(WIDE)
    hot = (entry == number).astype(WIDE)
    shared_out[0:GROUP, :] = jnp.dot(hot, total, precision=lax.Precision.HIGHEST)
    shared_out[GROUP : GROUP + 1, 0:LANES] = square[0:1, :]
    shared_out[GROUP + 1 : GROUP + 3, :] = sums_back[0:2, :]
    shared_out[GROUP + 3 : GROUP + 5, :] = sums_top[0:2, :]


def head_mlp_kernel(where, *refs):
    cls_mlp_kernel(where, *refs[:7], *refs[11:17])
    add_far_kernel(where, *refs[7:11], *refs[17:])


def head_end_kernel(where, *refs):
    cls_end_kernel(where, *refs[:12], *refs[16:19], refs[23])
    fold_kernel(where, *refs[12:16], *refs[19:23])


def attn_add_kernel(where, *refs):
    far_low, far_high, to_x, to_y, grad, own, got, x_out, y_out, input_out = refs
    add_far_kernel(where, far_low, far_high, to_x, to_y, x_out, y_out)
    input_out[...] = (grad[...] + own[...] + got[...]).astype(LOW)


def cls_rows_kernel(where, *refs):
    packs = refs[:4]
    heads, branch, low, second = refs[4:8]
    out, kept = refs[8:]
    line_at = where[0]
    rows, width = kept.shape[1:]
    for step, pack in enumerate(packs):
        first = pack.shape[0] - rows
        kept[(line_at + LINE - step) % LINE] = pack[first:, :width]
    starts = (MODEL, 2 * MODEL, 3 * MODEL, 4 * MODEL)
    out[:, 0:MODEL] = heads[:, :MODEL].astype(LOW)
    for piece, start in enumerate(starts):
        from_at = piece * SPAN
        for tile in range(MODEL // LANES):
            total = None
            for at in range(PLANE):
                inner = tile - TILE_START[at]
                if inner in (0, 1):
                    first = from_at + inner * LANES
                    value = kept[at, :, first : first + LANES]
                    total = value if total is None else total + value
            out[:, start + tile * LANES : start + (tile + 1) * LANES] = total
    out[:, 5 * MODEL : 6 * MODEL] = branch[...]
    out[:, 6 * MODEL : 7 * MODEL] = low[...]
    out[:, 7 * MODEL + FF : 8 * MODEL + FF] = second[...]
    part = FF // LINE
    for at in range(PLANE):
        first = 4 * SPAN
        out[:, 7 * MODEL + at * part : 7 * MODEL + (at + 1) * part] = kept[
            at, :, first : first + part
        ]
        out[:, 8 * MODEL + FF + at * part : 8 * MODEL + FF + (at + 1) * part] = kept[
            at, :, first + part : first + 2 * part
        ]


def own_features(rank, width):
    shape = (MODEL, width)
    feature = lax.broadcasted_iota(jnp.int32, shape, 0)
    column = lax.broadcasted_iota(jnp.int32, shape, 1)
    return (feature == rank * width + column).astype(LOW)


def own_vector(rank, pieces, out, flat):
    size = out.shape[0]
    for at, piece in enumerate(pieces):
        flat[:, at * MODEL : (at + 1) * MODEL] = piece
    value = jnp.zeros((1, size), WIDE)
    for chip in range(GROUP):
        value = jnp.where(rank == chip, flat[:, chip * size : (chip + 1) * size], value)
    out[...] = value.reshape(size)


def cls_owner_kernel(where, *refs):
    own, got, shared, mats_out, vec_out, rows, flat = refs
    rank = where[0] * PLANE + where[1]
    width = mats_out.shape[0]
    rows[:GROUP] = own[...]
    rows[GROUP:] = got[...]
    chosen = own_features(rank, width)
    plan = (
        (0, MODEL, 3 * MODEL, 0),
        (4 * MODEL, 5 * MODEL, MODEL, 3 * MODEL),
        (6 * MODEL, 7 * MODEL, FF, 4 * MODEL),
        (7 * MODEL + FF, 8 * MODEL + FF, FF, 4 * MODEL + FF),
    )
    for left, right, size, target in plan:
        side = product_plain(rows[:, left : left + MODEL], chosen).astype(LOW)
        mats_out[:, target : target + size] = product_left(side, rows[:, right : right + size])
    starts = (MODEL, 3 * MODEL, 5 * MODEL, 7 * MODEL + FF)
    pieces = [column_sum(rows[:, start : start + MODEL]) for start in starts]
    pieces += [shared[GROUP + 1 + at : GROUP + 2 + at, :] for at in range(4)]
    starts = [7 * MODEL + at * MODEL for at in range(FF // MODEL)]
    pieces += [column_sum(rows[:, start : start + MODEL]) for start in starts]
    own_vector(rank, pieces, vec_out, flat)


def head_share_kernel(where, *refs):
    packs, mlp = refs[:4], refs[4]
    mine_out, vecs_out, rows = refs[5:]
    rank = where[0] * PLANE + where[1]
    count = LINE * 24
    for at, pack in enumerate(packs):
        rows[at * count : (at + 1) * count] = pack[...]
    total = PLANE * count

    def chosen(base, apart):
        shape = (CORES * GROUP, total)
        row = lax.broadcasted_iota(jnp.int32, shape, 0)
        column = lax.broadcasted_iota(jnp.int32, shape, 1)
        hot = (column == row // 2 * 24 + base + row % 2 * apart).astype(LOW)
        return product_plain(hot, rows[...]).astype(LOW)

    own = own_features(rank, OWN)
    for at, (left, right) in enumerate(((0, 4), (2, 8))):
        side = product_plain(chosen(left, 1), own).astype(LOW)
        for piece in range(FF_HALF // MODEL):
            columns = slice(at * FF_HALF + piece * MODEL, at * FF_HALF + (piece + 1) * MODEL)
            share = product_left(side, chosen(right + 2 * piece, 1))
            mine_out[:, columns] = mlp[:, columns] + share
    shape = (16, total)
    row = lax.broadcasted_iota(jnp.int32, shape, 0)
    column = lax.broadcasted_iota(jnp.int32, shape, 1)
    hot = ((column % 24 == row + 12) & (row < 12)).astype(LOW)
    vecs_out[...] = product_plain(hot, rows[...])


def share_owner_kernel(where, *refs):
    head_share_kernel(where, *refs[:5], *refs[9:11], refs[15])
    cls_owner_kernel(where, *refs[5:8], *refs[11:13], *refs[16:])
    shared, count, pos_out, loss_out = refs[7], refs[8], refs[13], refs[14]
    pos_out[...] = shared[:GROUP, :]
    loss_out[...] = shared[GROUP : GROUP + 1, 0:1] / (count[0:1, 0:1] * MODEL)


def seg_vec_kernel(where, vecs, vecs_got, vec_out, flat):
    rank = where[0] * PLANE + where[1]
    rows = (8 * MODEL + FF) // MODEL
    pieces = [vecs[at : at + 1, :] + vecs_got[at : at + 1, :] for at in range(rows)]
    own_vector(rank, pieces, vec_out, flat)


def column_copies(where, out, base, size, own, got, first):
    core_at = where[2]
    lanes = slice(first, first + size)
    return [
        (own.at[:, lanes], out.at[:, pl.ds(aligned(base + core_at * size), size)]),
        (got.at[:, lanes], out.at[:, pl.ds(aligned(base + (1 - core_at) * size), size)]),
    ]


def store_kernel(where, attn, attn_got, mlp, mlp_got, vecs, vecs_got, out, vec_out, flat, sems):
    pairs = []
    for piece in range(4):
        pairs += column_copies(where, out, piece * MODEL, HALF, attn, attn_got, piece * HALF)
    for piece in range(2):
        base = 4 * MODEL + piece * FF
        pairs += column_copies(where, out, base, FF_HALF, mlp, mlp_got, piece * FF_HALF)
    copies = [
        pltpu.make_async_copy(source, target, sems.at[at])
        for at, (source, target) in enumerate(pairs)
    ]
    for copy in copies:
        copy.start()
    seg_vec_kernel(where, vecs, vecs_got, vec_out, flat)
    wait_all(copies)


def plane_parts(part):
    return (part,) + together(*(in_plane(part, mask) for mask in range(1, PLANE)))


def line_parts(part):
    return (part,) + together(*(along_line(part, apart) for apart in range(1, LINE)))


def slice_local(
    hidden_in,
    targets,
    doc_ids,
    seg_nums,
    valid_flags,
    seg_mats,
    seg_vecs,
    cls_mats,
    cls_vecs,
    seg_pos,
):
    rank, core_at = lax.axis_index("fsdp"), lax.axis_index("rep")
    line_at, plane_at = rank // PLANE, rank % PLANE
    where = jnp.stack([line_at, plane_at, core_at, doc_ids[0], seg_nums[0]]).astype(jnp.int32)
    own_rows, total_columns = seg_mats.shape
    vec_size = seg_vecs.shape[0]
    both_rows = CORES * SEG

    first_piece, live_row = run_kernel(
        prepare_first_kernel,
        "prepare_first",
        [shape_of((own_rows, FIRST), LOW), shape_of((1, SEG))],
        where,
        (seg_mats,),
        (jnp.stack([seg_vecs, cls_vecs]).astype(WIDE), valid_flags[None]),
        [pltpu.SemaphoreType.DMA((4,))],
    )
    first_line = line_parts(first_piece)
    rest = run_kernel(
        prepare_rest_kernel,
        "prepare_rest",
        [shape_of((own_rows, FF_HALF), LOW)] * 2
        + [shape_of((own_rows, QUARTER_HALF), LOW)] * LINE
        + [shape_of((own_rows, HALF), LOW), shape_of((MODEL, PLANE * SPAN), LOW)],
        where,
        (seg_mats, cls_mats),
        (),
        [
            pltpu.VMEM((LINE, own_rows, QUARTER), LOW),
            pltpu.SemaphoreType.DMA((3 + 5 * LINE,)),
        ],
    )
    second_piece, third_piece, quarters, cls_out_piece, order = (
        rest[0],
        rest[1],
        rest[2:-2],
        rest[-2],
        rest[-1],
    )

    def joined(*pieces):
        return jnp.concatenate(pieces, axis=1)

    def sent_both(to_x, to_y):
        to_x, to_y = together(to_x, to_y)
        return together(in_plane(to_x, 1), in_plane(to_y, 2))

    own_sent = joined(first_piece, second_piece, third_piece)
    own_x, own_y = sent_both(own_sent, own_sent)
    first_line = first_line[:1] + tuple(after(got, own_x, own_y) for got in first_line[1:])
    to_x = joined(own_y[:, OWN_CUT:], *first_line[1:])
    to_y = joined(own_x[:, :OWN_CUT], *first_line[1:])
    first_x, first_y = sent_both(to_x, to_y)
    hidden_got = other_core(after(hidden_in, to_x, to_y))
    live_got = other_core(after(live_row, to_x, to_y))
    second_line = line_parts(after(second_piece, hidden_got, live_got, to_x, to_y))

    def halves(group, from_x, from_y):
        width, cut = WIDTHS[group], LINE_CUTS[group]
        if group == 0:
            base_x, base_y = sum(WIDTHS) - OWN_CUT, OWN_CUT
        else:
            before, before_cut = WIDTHS[group - 1], LINE_CUTS[group - 1]
            base_x, base_y = 2 * before - before_cut, before + before_cut
        return (
            from_y[:, base_y + width + cut : base_y + 3 * width],
            from_x[:, base_x : base_x + width + cut],
        )

    high, low = halves(0, first_x, first_y)
    to_x, to_y = joined(high, *second_line[1:]), joined(low, *second_line[1:])
    second_x, second_y = sent_both(to_x, to_y)
    third_line = line_parts(after(third_piece, to_x, to_y))
    high, low = halves(1, second_x, second_y)
    to_x, to_y = joined(high, *third_line[1:]), joined(low, *third_line[1:])
    third_x, third_y = sent_both(to_x, to_y)
    own_parts = (own_x, own_y, first_x, first_y)
    cls_line = (quarters[0],) + tuple(
        along_line(after(quarters[apart], to_x, to_y), apart)
        for apart in range(1, LINE)
    )

    qkv_weight, out_low, out_high, qkv, mixed, vectors, count, hidden_ordered = run_kernel(
        qkv_kernel,
        "seg_qkv",
        [
            shape_of((GROUP, own_rows, 3 * HALF), LOW),
            shape_of((GROUP // 2, own_rows, HALF), LOW),
            shape_of((GROUP // 2, own_rows, HALF), LOW),
            shape_of((both_rows, 3 * HALF), LOW),
            shape_of((both_rows, HALF), LOW),
            shape_of((2 * (8 * MODEL + FF) // MODEL, MODEL)),
            shape_of((8, LANES)),
            shape_of((both_rows, PLANE * SPAN), LOW),
        ],
        where,
        (),
        first_line
        + own_parts
        + (first_x, first_y, second_x, second_y)
        + (hidden_in, hidden_got, live_row, live_got, order),
        [
            pltpu.VMEM((GROUP, own_rows, LANES), LOW),
            pltpu.VMEM((2, 8 * MODEL + FF), WIDE),
            pltpu.VMEM((both_rows, MODEL), LOW),
            pltpu.VMEM((GROUP, own_rows, HALF), LOW),
        ],
        flops=2 * SEG * MODEL * 3 * MODEL,
    )
    out_weight, mixed_ordered, normed_first, inv_first, first_low = run_kernel(
        out_kernel,
        "seg_out",
        [
            shape_of((MODEL, MODEL), LOW),
            shape_of((both_rows, PLANE * SPAN), LOW),
            shape_of((SEG, MODEL)),
            shape_of((SEG, 1)),
            shape_of((SEG, MODEL), LOW),
        ],
        where,
        (),
        (
            hidden_in,
            mixed,
            after(other_core(mixed), third_x, third_y),
            out_low,
            out_high,
            other_core(out_low),
            other_core(out_high),
            vectors,
            order,
        ),
        [pltpu.VMEM((both_rows, MODEL), LOW)],
        flops=2 * SEG * MODEL * MODEL,
    )
    fourth_x, fourth_y = sent_both(*halves(2, third_x, third_y))
    first_got = after(other_core(first_low), fourth_x, fourth_y)
    count = count + other_core(after(count, first_got))
    up_weight, act, slope = run_kernel(
        up_kernel,
        "seg_up",
        [
            shape_of((GROUP, own_rows, FF_HALF), LOW),
            shape_of((both_rows, FF_HALF), LOW),
            shape_of((both_rows, FF_HALF)),
        ],
        where,
        (),
        second_line
        + own_parts
        + (second_x, second_y, third_x, third_y)
        + (first_low, first_got, vectors),
        [pltpu.VMEM((both_rows, MODEL), LOW)],
        flops=2 * SEG * MODEL * FF,
    )
    cls_sent = joined(*cls_line, cls_out_piece)
    cls_sent = after(cls_sent, act)
    cls_x, cls_y = sent_both(cls_sent, cls_sent)
    down_weight, down_own, down_send = run_kernel(
        down_kernel,
        "seg_down",
        [
            shape_of((GROUP, own_rows, FF_HALF), LOW),
            shape_of((SEG, MODEL)),
            shape_of((SEG, MODEL)),
        ],
        where,
        (),
        third_line + own_parts + (third_x, third_y, fourth_x, fourth_y) + (act,),
        flops=2 * SEG * MODEL * FF,
    )
    normed_second, inv_second, diff, out_rows, head_row = run_kernel(
        seg_rows_kernel,
        "seg_rows",
        [
            shape_of((SEG, MODEL)),
            shape_of((SEG, 1)),
            shape_of((SEG, MODEL)),
            shape_of((SEG, MODEL)),
            shape_of((1, 2 * MODEL + LANES)),
        ],
        where,
        (),
        (
            down_own,
            other_core(down_send),
            normed_first,
            vectors,
            targets,
            live_row,
            seg_pos,
        ),
    )
    head_planes = plane_parts(head_row)
    head_lines = line_parts(jnp.concatenate(head_planes))
    size = LINE // 2 * QUARTER_HALF
    cls_far = sent_both(
        after(cls_y[:, size:], *head_planes[1:]), after(cls_x[:, :size], *head_planes[1:])
    )

    second_grad, second_low, second_sums = run_kernel(
        second_norm_kernel,
        "seg_second_norm",
        [shape_of((SEG, MODEL)), shape_of((SEG, MODEL), LOW), shape_of((3, MODEL))],
        where,
        (),
        (diff, count, normed_second, inv_second, vectors),
    )
    second_got = other_core(second_low)
    pre, first_grad_own, first_grad_send, up_sums = run_kernel(
        mlp_back_kernel,
        "seg_mlp_back",
        [
            shape_of((both_rows, FF_HALF), LOW),
            shape_of((SEG, MODEL)),
            shape_of((SEG, MODEL)),
            shape_of((FF_HALF // MODEL, MODEL)),
        ],
        where,
        (),
        (second_low, second_got, down_weight, up_weight, slope),
        [pltpu.VMEM((both_rows, MODEL), LOW)],
        flops=4 * SEG * MODEL * FF,
    )
    first_grad_got = other_core(first_grad_send)

    def part_shapes(columns):
        return [
            shape_of((count_of, own_rows, columns), LOW)
            for count_of in (LINE // 2, LINE // 2, LINE, LINE, LINE)
        ]

    head_lines = head_lines[:1] + together(*(after(got, pre) for got in head_lines[1:]))
    cls_far = together(*(after(got, *head_lines[1:]) for got in cls_far))
    cls_half, cls_out_half = run_kernel(
        cls_gather_kernel,
        "head_gather",
        [
            shape_of((GROUP, own_rows, QUARTER_HALF), LOW),
            shape_of((PLANE, own_rows, HALF), LOW),
        ],
        where,
        (),
        cls_line + (cls_x, cls_y) + cls_far + (cls_out_piece,),
    )
    mlp_parts = run_kernel(
        mlp_weight_kernel,
        "seg_mlp_weight",
        part_shapes(FF),
        where,
        (),
        (first_low, first_got, second_low, second_got, after(pre, cls_half), act),
        [
            pltpu.VMEM((both_rows, MODEL), LOW),
            pltpu.VMEM((GROUP, own_rows, FF), LOW),
            pltpu.SemaphoreType.DMA((GROUP,)),
        ],
        far=range(5),
        flops=4 * SEG * MODEL * FF,
    )
    mlp_far = reduce_far(tuple(after(part, *cls_far) for part in mlp_parts[:2]))
    cls_weight, cls_out = run_kernel(
        cls_weight_kernel,
        "head_weight",
        [
            shape_of((GROUP, own_rows, QUARTER), LOW),
            shape_of((4, HEAD_DIM, MODEL), LOW),
        ],
        where,
        (),
        (cls_half, other_core(cls_half), cls_out_half, other_core(cls_out_half)),
    )
    cls_weight = cls_weight.reshape(MODEL, QUARTER)
    cls_out = cls_out.reshape(SPAN, MODEL)
    heads, cls_qkv, cls_mixed, part = run_kernel(
        cls_attend_kernel,
        "head_attend",
        [
            shape_of((GROUP, 2 * MODEL + LANES)),
            shape_of((GROUP, 3 * SPAN), LOW),
            shape_of((GROUP, SPAN), LOW),
            shape_of((GROUP, MODEL)),
        ],
        where,
        (),
        tuple(after(got, mlp_parts[0], first_grad_got) for got in head_lines)
        + (vectors, cls_weight, cls_out),
    )
    cls_normed, cls_inv, cls_low, cls_act, cls_slope, part, *mlp_sent = run_kernel(
        head_mlp_kernel,
        "head_mlp",
        [
            shape_of((GROUP, MODEL)),
            shape_of((GROUP, 1)),
            shape_of((GROUP, MODEL), LOW),
            shape_of((GROUP, FF // LINE), LOW),
            shape_of((GROUP, FF // LINE)),
            shape_of((GROUP, MODEL)),
            shape_of(mlp_parts[2].shape, LOW),
            shape_of(mlp_parts[2].shape, LOW),
        ],
        where,
        (),
        (heads,) + line_parts(part) + (vectors, cls_weight) + mlp_far + tuple(mlp_parts[2:4]),
    )
    mlp_plane = sent_both(*mlp_sent)
    cls_parts = line_parts(part)
    top_row, square, cls_grad, cls_second, cls_pre, part, top_sums = run_kernel(
        cls_top_kernel,
        "head_top",
        [
            shape_of((1, MODEL)),
            shape_of((8, LANES)),
            shape_of((GROUP, MODEL)),
            shape_of((GROUP, MODEL), LOW),
            shape_of((GROUP, FF // LINE), LOW),
            shape_of((GROUP, MODEL)),
            shape_of((2, MODEL)),
        ],
        where,
        (),
        (heads,)
        + cls_parts
        + (vectors, cls_weight, cls_normed, count, cls_slope),
        [pltpu.VMEM((GROUP, MODEL), WIDE)],
    )
    top_parts = line_parts(part)
    cls_grad, cls_branch, cls_proj, part, back_sums = run_kernel(
        cls_attend_back_kernel,
        "head_attend_back",
        [
            shape_of((GROUP, MODEL)),
            shape_of((GROUP, MODEL), LOW),
            shape_of((GROUP, 3 * SPAN), LOW),
            shape_of((GROUP, MODEL)),
            shape_of((2, MODEL)),
        ],
        where,
        (),
        (heads,)
        + top_parts
        + (vectors, cls_weight, cls_out, cls_grad, cls_normed, cls_inv, cls_qkv),
    )
    end_parts = line_parts(part)
    pack = jnp.concatenate([cls_proj, cls_mixed, cls_pre, cls_act], axis=1)
    folded = [shape_of((own_rows, FF))] + [shape_of((own_rows + GROUP, FF), LOW)] * (LINE - 1)
    dheads, head_grad, shared, mlp_own, *mlp_sent = run_kernel(
        head_end_kernel,
        "head_end",
        [shape_of((1, MODEL)), shape_of((1, MODEL)), shape_of((GROUP + 8, MODEL))] + folded,
        where,
        (),
        (heads, cls_grad)
        + end_parts
        + (square, back_sums, top_sums, normed_second, inv_second, vectors)
        + (mlp_parts[4],)
        + mlp_plane
        + (pack,),
        [pltpu.VMEM((GROUP, MODEL), WIDE)],
    )
    got_three, got_two = along_line(mlp_sent[2], 3), along_line(mlp_sent[1], 2)
    got_one = along_line(after(mlp_sent[0], got_two), 1)
    mlp_got = [got_one, got_two, got_three]

    head_own, head_send, head_data = run_kernel(
        head_back_kernel,
        "seg_head_back",
        [shape_of((1, MODEL)), shape_of((1, MODEL)), shape_of((12, MODEL))],
        where,
        (),
        (
            head_grad,
            other_core(head_grad),
            down_weight,
            up_weight,
            slope,
            act,
            first_low,
            first_got,
        ),
    )
    grad_summed, branch, mixed_grad, attn_send, first_sums = run_kernel(
        first_norm_kernel,
        "seg_first_norm",
        [
            shape_of((SEG, MODEL)),
            shape_of((SEG, MODEL), LOW),
            shape_of((SEG, MODEL), LOW),
            shape_of((SEG, MODEL), LOW),
            shape_of((3, MODEL)),
        ],
        where,
        (),
        (
            second_grad,
            first_grad_own,
            first_grad_got,
            head_grad,
            head_own,
            other_core(head_send),
            normed_first,
            inv_first,
            vectors,
            out_weight,
        ),
    )
    attn_got = other_core(attn_send)
    proj, input_own, input_send, payload = run_kernel(
        attn_back_kernel,
        "seg_attn_back",
        [
            shape_of((both_rows, 3 * HALF), LOW),
            shape_of((SEG, MODEL)),
            shape_of((SEG, MODEL)),
            shape_of((24, MODEL), LOW),
        ],
        where,
        (),
        (
            qkv,
            mixed_grad,
            attn_got,
            live_row,
            live_got,
            qkv_weight,
            first_sums,
            second_sums,
            up_sums,
            dheads,
            normed_second,
            head_data,
        ),
        [pltpu.VMEM((24, MODEL), WIDE)],
        flops=4 * SEG * MODEL * 3 * MODEL,
    )
    attn_data = (hidden_ordered, mixed_ordered, proj, branch, attn_got)
    attn_far = run_kernel(
        attn_far_kernel,
        "seg_attn_far",
        part_shapes(4 * HALF)[:2],
        where,
        (),
        attn_data,
        flops=SEG * MODEL * 2 * MODEL,
    )
    attn_far = reduce_far(tuple(after(part, mlp_got[-1]) for part in attn_far))
    attn_near = run_kernel(
        attn_near_kernel,
        "seg_attn_near",
        part_shapes(4 * HALF)[2:] + [shape_of((SEG, MODEL), LOW)],
        where,
        (),
        attn_data + (after(top_row, got_two), out_rows, live_row),
        flops=3 * SEG * MODEL * 2 * MODEL,
    )
    output = attn_near[3]
    *attn_sent, input_grad = run_kernel(
        attn_add_kernel,
        "seg_attn_add",
        [shape_of(attn_near[0].shape, LOW)] * 2 + [shape_of((SEG, MODEL), LOW)],
        where,
        (),
        attn_far + tuple(attn_near[:2]) + (grad_summed, input_own, other_core(input_send)),
    )
    attn_plane = sent_both(*attn_sent)
    payload_parts = line_parts(after(payload, *attn_sent))
    mlp_got = [after(got, attn_plane[0]) for got in mlp_got]
    mlp_sum = reduce_line(mlp_own, mlp_got)
    shared = shared + other_core(after(shared, attn_sent[0]))
    row_width = 8 * MODEL + 2 * FF
    cls_rows = run_kernel(
        cls_rows_kernel,
        "head_rows",
        [shape_of((GROUP, row_width), LOW)],
        where,
        (),
        (pack,) + tuple(mlp_got) + (heads, cls_branch, cls_low, cls_second),
        [pltpu.VMEM((LINE,) + pack.shape, LOW)],
    )[0]
    cls_got = other_core(cls_rows)
    attn_plane = tuple(after(got, cls_got, output, input_grad, shared) for got in attn_plane)
    attn_own, *attn_sent = reduce_fold(where, attn_near[2], attn_plane)
    attn_lines = list(
        together(*(along_line(attn_sent[apart - 1], apart) for apart in range(1, LINE)))
    )
    flat = pltpu.VMEM((1, 8 * MODEL + FF), WIDE)
    payload_line = jnp.concatenate(payload_parts)
    mlp_mine, own_vecs, cls_mats_grad, cls_vec_grad, pos_total, loss_value = run_kernel(
        share_owner_kernel,
        "head_owner",
        [
            shape_of((own_rows, FF)),
            shape_of((16, MODEL)),
            shape_of((own_rows, total_columns)),
            shape_of((vec_size,)),
            shape_of((GROUP, MODEL)),
            shape_of((1, 1)),
        ],
        where,
        (),
        tuple(after(got, attn_own) for got in plane_parts(after(payload_line, *attn_plane)))
        + (mlp_sum, cls_rows, cls_got, shared, count),
        [
            pltpu.VMEM((GROUP * 24, MODEL), LOW),
            pltpu.VMEM((CORES * GROUP, row_width), LOW),
            flat,
        ],
        flops=64 * own_rows * total_columns,
    )
    loss_value = loss_value.reshape(())
    attn_lines = together(*(after(got, mlp_mine) for got in attn_lines))
    attn_sum = reduce_line(attn_own, attn_lines)
    seg_mats_grad, seg_vec_grad = run_kernel(
        store_kernel,
        "seg_owner",
        [shape_of((own_rows, total_columns)), shape_of((vec_size,))],
        where,
        (),
        (attn_sum, other_core(attn_sum), mlp_mine, other_core(mlp_mine))
        + (own_vecs, other_core(own_vecs)),
        [flat, pltpu.SemaphoreType.DMA((12,))],
        far=(0,),
    )

    return (
        output,
        input_grad,
        seg_mats_grad,
        seg_vec_grad,
        cls_mats_grad,
        cls_vec_grad,
        pos_total,
        loss_value,
    )


def solution(mesh):
    in_specs = (
        P(("rep", "fsdp"), None),
        P(("rep", "fsdp"), None),
        P(("rep", "fsdp")),
        P(("rep", "fsdp")),
        P(("rep", "fsdp")),
        P("fsdp", None),
        P("fsdp"),
        P("fsdp", None),
        P("fsdp"),
        P(),
    )
    out_specs = (
        P(("rep", "fsdp"), None),
        P(("rep", "fsdp"), None),
        P("fsdp", None),
        P("fsdp"),
        P("fsdp", None),
        P("fsdp"),
        P(),
        P(),
    )
    one_slice = dict(mesh.shape) == {"rep": CORES, "fsdp": LINE * PLANE}
    body = slice_local if one_slice else local
    return jax.shard_map(body, mesh=mesh, in_specs=in_specs, out_specs=out_specs, check_vma=False)
```

```python
import math

import jax
import jax.numpy as jnp
from jax import lax
from jax.experimental import pallas as pl
from jax.experimental.pallas import tpu as pltpu
from jax.sharding import PartitionSpec as P

HEADS = 12
HEAD_DIM = 64
FF = 3072
SEG = 128
SEQ = 2048


NORM_EPS = 1e-05
MASK_FILL = -1e30
SQRT_HALF = 0.7071067811865476
INV_SQRT_TWO_PI = 0.3989422804014327


def swapped(value, axis, apart):
    mask = 2**apart
    pairs = [(source, source ^ mask) for source in range(lax.axis_size(axis))]
    return lax.ppermute(value, axis, pairs)


def product_plain(left_side, right_side):
    return jnp.dot(left_side, right_side, preferred_element_type=jnp.float32)


def product_left(left_side, right_side):
    return lax.dot_general(
        left_side, right_side, (((0,), (0,)), ((), ())), preferred_element_type=jnp.float32
    )


def product_right(left_side, right_side):
    return lax.dot_general(
        left_side, right_side, (((1,), (1,)), ((), ())), preferred_element_type=jnp.float32
    )


def row_total(array_in):
    return jnp.sum(array_in.astype(jnp.float32), axis=0)


def unpack_weights(gathered, model_width, ff_width):
    matrix, vector = gathered
    vector = vector.astype(jnp.float32)
    pieces = tuple(
        (vector[offset * model_width : (offset + 1) * model_width] for offset in range(8))
    )
    return (
        (
            matrix[:, : 3 * model_width],
            matrix[:, 3 * model_width : 4 * model_width],
            matrix[:, 4 * model_width : 4 * model_width + ff_width],
            matrix[:, 4 * model_width + ff_width :],
        )
        + pieces
        + (vector[8 * model_width :],)
    )


def norm_forward(summed, gain_vec, shift_vec):
    row_mean = jnp.mean(summed, axis=-1, keepdims=True)
    centered = summed - row_mean
    inv_dev = lax.rsqrt(jnp.mean(centered * centered, axis=-1, keepdims=True) + NORM_EPS)
    normed = centered * inv_dev
    return (normed * gain_vec + shift_vec, normed, inv_dev)


def norm_backward(grad_out, normed, inv_dev, gain_vec):
    scaled = grad_out * gain_vec
    mean_one = jnp.mean(scaled, axis=-1, keepdims=True)
    mean_two = jnp.mean(scaled * normed, axis=-1, keepdims=True)
    grad_in = inv_dev * (scaled - mean_one - normed * mean_two)
    return (grad_in, jnp.sum(grad_out * normed, axis=0), jnp.sum(grad_out, axis=0))


def gelu_value(before):
    return 0.5 * before * (1.0 + lax.erf(before * SQRT_HALF))


def gelu_slope(before):
    return (
        0.5 * (1.0 + lax.erf(before * SQRT_HALF))
        + before * jnp.exp(-0.5 * before * before) * INV_SQRT_TWO_PI
    )


def attention_scores(queries, keys_in, allowed, score_scale):
    raw_scores = (
        jnp.einsum("bqhe,bkhe->bhqk", queries, keys_in, preferred_element_type=jnp.float32)
        * score_scale
    )
    return jnp.where(allowed, raw_scores, MASK_FILL)


def attention_forward(queries, keys_in, values, allowed, score_scale):
    scores = attention_scores(queries, keys_in, allowed, score_scale)
    row_top = jnp.max(scores, axis=-1, keepdims=True)
    log_total = row_top + jnp.log(jnp.sum(jnp.exp(scores - row_top), axis=-1, keepdims=True))
    weights = jnp.exp(scores - log_total).astype(jnp.bfloat16)
    mixed_rows = jnp.einsum("bhqk,bkhe->bqhe", weights, values, preferred_element_type=jnp.float32)
    return (mixed_rows, log_total)


def attention_backward(queries, keys_in, values, allowed, score_scale, log_total, grad_mixed):
    probabilities = jnp.exp(attention_scores(queries, keys_in, allowed, score_scale) - log_total)
    grad_probs = jnp.einsum(
        "bqhe,bkhe->bhqk", grad_mixed, values, preferred_element_type=jnp.float32
    )
    inner_sum = jnp.sum(grad_probs * probabilities, axis=-1, keepdims=True)
    grad_scores = (probabilities * (grad_probs - inner_sum)).astype(jnp.bfloat16)
    grad_query = (
        jnp.einsum("bhqk,bkhe->bqhe", grad_scores, keys_in, preferred_element_type=jnp.float32)
        * score_scale
    )
    grad_key = (
        jnp.einsum("bhqk,bqhe->bkhe", grad_scores, queries, preferred_element_type=jnp.float32)
        * score_scale
    )
    grad_value = jnp.einsum(
        "bhqk,bqhe->bkhe",
        probabilities.astype(jnp.bfloat16),
        grad_mixed,
        preferred_element_type=jnp.float32,
    )
    return (grad_query, grad_key, grad_value)


def block_forward(rows_in, unpacked, attend):
    (
        qkv_weight,
        out_weight,
        up_weight,
        down_weight,
        query_bias,
        value_bias,
        out_bias,
        down_bias,
        gain_first,
        shift_first,
        gain_second,
        shift_second,
        up_bias,
    ) = unpacked
    model_width = rows_in.shape[1]
    inputs = rows_in.astype(jnp.bfloat16)
    projected = product_plain(inputs, qkv_weight)
    queries = (projected[:, :model_width] + query_bias).astype(jnp.bfloat16)
    keys_in = projected[:, model_width : 2 * model_width].astype(jnp.bfloat16)
    values = (projected[:, 2 * model_width :] + value_bias).astype(jnp.bfloat16)
    mixed_rows, attend_kept = attend(queries, keys_in, values)
    mixed_rows = mixed_rows.astype(jnp.bfloat16)
    summed_first = rows_in + product_plain(mixed_rows, out_weight) + out_bias
    first_out, normed_first, inv_first = norm_forward(summed_first, gain_first, shift_first)
    first_low = first_out.astype(jnp.bfloat16)
    pre_act = product_plain(first_low, up_weight) + up_bias
    activated = gelu_value(pre_act).astype(jnp.bfloat16)
    summed_second = first_out + product_right(activated, down_weight) + down_bias
    block_out, normed_second, inv_second = norm_forward(summed_second, gain_second, shift_second)
    saved_state = (
        inputs,
        queries,
        keys_in,
        values,
        attend_kept,
        mixed_rows,
        normed_first,
        inv_first,
        first_low,
        pre_act,
        activated,
        normed_second,
        inv_second,
    )
    return (block_out, saved_state)


def block_backward(grad_out, unpacked, saved_state, attend_back):
    (
        qkv_weight,
        out_weight,
        up_weight,
        down_weight,
        query_bias,
        value_bias,
        out_bias,
        down_bias,
        gain_first,
        shift_first,
        gain_second,
        shift_second,
        up_bias,
    ) = unpacked
    (
        inputs,
        queries,
        keys_in,
        values,
        attend_kept,
        mixed_rows,
        normed_first,
        inv_first,
        first_low,
        pre_act,
        activated,
        normed_second,
        inv_second,
    ) = saved_state
    grad_second, grad_gain_second, grad_shift_second = norm_backward(
        grad_out, normed_second, inv_second, gain_second
    )
    second_low = grad_second.astype(jnp.bfloat16)
    grad_pre = (product_plain(second_low, down_weight) * gelu_slope(pre_act)).astype(jnp.bfloat16)
    grad_first = grad_second + product_right(grad_pre, up_weight)
    grad_summed, grad_gain_first, grad_shift_first = norm_backward(
        grad_first, normed_first, inv_first, gain_first
    )
    branch_low = grad_summed.astype(jnp.bfloat16)
    grad_mixed = product_right(branch_low, out_weight).astype(jnp.bfloat16)
    grad_query, grad_key, grad_value = attend_back(
        queries, keys_in, values, attend_kept, grad_mixed
    )
    grad_proj = jnp.concatenate([grad_query, grad_key, grad_value], axis=1)
    grad_rows = grad_summed + product_right(grad_proj, qkv_weight)
    vector_grad = jnp.concatenate(
        [
            row_total(grad_query),
            row_total(grad_value),
            row_total(branch_low),
            row_total(second_low),
            grad_gain_first,
            grad_shift_first,
            grad_gain_second,
            grad_shift_second,
            row_total(grad_pre),
        ]
    )
    weight_rows = (
        inputs,
        grad_proj,
        mixed_rows,
        branch_low,
        first_low,
        grad_pre,
        second_low,
        activated,
    )
    return (grad_rows, weight_rows, vector_grad)


def weight_products(weight_rows):
    inputs, grad_proj, mixed_rows, branch_low, first_low, grad_pre, second_low, activated = (
        weight_rows
    )
    return (
        product_left(inputs, grad_proj),
        product_left(mixed_rows, branch_low),
        product_left(first_low, grad_pre),
        product_left(second_low, activated),
    )


def local(
    hidden_in,
    targets,
    doc_ids,
    seg_nums,
    valid_flags,
    seg_mats,
    seg_vecs,
    cls_mats,
    cls_vecs,
    seg_pos,
):
    tok_rows, model_width = hidden_in.shape
    ff_width = FF
    seg_len = SEG
    group_span = SEQ // tok_rows
    seg_count = tok_rows // seg_len
    score_scale = HEAD_DIM ** (-0.5)
    head_shape = (HEADS, HEAD_DIM)
    live_rows = valid_flags.astype(jnp.float32)
    rank_full = lax.axis_index("fsdp")
    seg_gathered = (
        lax.all_gather(seg_mats, "fsdp", axis=0, tiled=True),
        lax.all_gather(seg_vecs, "fsdp", axis=0, tiled=True),
    )
    seg_unpacked = unpack_weights(seg_gathered, model_width, ff_width)
    cls_gathered = (
        lax.all_gather(cls_mats, "fsdp", axis=0, tiled=True),
        lax.all_gather(cls_vecs, "fsdp", axis=0, tiled=True),
    )
    cls_unpacked = unpack_weights(cls_gathered, model_width, ff_width)
    seg_allowed = (live_rows.reshape(seg_count, 1, 1, seg_len) > 0.5) | jnp.eye(seg_len, dtype=bool)
    seg_shape = (seg_count, seg_len) + head_shape

    def seg_attend(queries, keys_in, values):
        mixed_rows, log_total = attention_forward(
            queries.reshape(seg_shape),
            keys_in.reshape(seg_shape),
            values.reshape(seg_shape),
            seg_allowed,
            score_scale,
        )
        return (mixed_rows.reshape(tok_rows, model_width), log_total)

    def seg_attend_back(queries, keys_in, values, log_total, grad_mixed):
        grad_parts = attention_backward(
            queries.reshape(seg_shape),
            keys_in.reshape(seg_shape),
            values.reshape(seg_shape),
            seg_allowed,
            score_scale,
            log_total,
            grad_mixed.reshape(seg_shape),
        )
        return tuple(
            (
                grad_part.reshape(tok_rows, model_width).astype(jnp.bfloat16)
                for grad_part in grad_parts
            )
        )

    first_out, seg_saved = block_forward(hidden_in.astype(jnp.float32), seg_unpacked, seg_attend)
    first_grid = first_out.reshape(seg_count, seg_len, model_width)
    position_hot = (seg_nums[:, None] == jnp.arange(seg_pos.shape[0])[None, :]).astype(jnp.float32)
    position_rows = jnp.sum(
        position_hot[:, :, None] * seg_pos.astype(jnp.float32)[None, :, :], axis=1
    )
    heads_in = first_grid[:, 0, :] + position_rows
    lead_live = live_rows.reshape(seg_count, seg_len)[:, 0]
    lead_doc = doc_ids.reshape(seg_count, seg_len)[:, 0]
    lead_labels = jnp.where(lead_live > 0.5, lead_doc, -1).astype(jnp.bfloat16)
    lead_doc_low = lead_doc.astype(jnp.bfloat16)
    bit_count = group_span.bit_length() - 1
    key_total = group_span * seg_count
    own_slot = rank_full % group_span * seg_count + jnp.arange(seg_count)
    query_shape = (1, seg_count) + head_shape
    key_shape = (1, key_total) + head_shape

    def cls_attend(queries, keys_in, values):
        paired = jnp.concatenate([keys_in, values], axis=1)
        labels = lead_labels
        for bit_level in range(bit_count):
            other_pair, other_labels = swapped((paired, labels), "fsdp", bit_level)
            upper_half = rank_full // (1 << bit_level) % 2 == 1
            paired = jnp.where(
                upper_half,
                jnp.concatenate([other_pair, paired]),
                jnp.concatenate([paired, other_pair]),
            )
            labels = jnp.where(
                upper_half,
                jnp.concatenate([other_labels, labels]),
                jnp.concatenate([labels, other_labels]),
            )
        allowed = (labels[None, :] == lead_doc_low[:, None]) | (
            jnp.arange(key_total)[None, :] == own_slot[:, None]
        )
        allowed = allowed[None, None]
        mixed_rows, log_total = attention_forward(
            queries.reshape(query_shape),
            paired[:, :model_width].reshape(key_shape),
            paired[:, model_width:].reshape(key_shape),
            allowed,
            score_scale,
        )
        return (mixed_rows.reshape(seg_count, model_width), (paired, allowed, log_total))

    def cls_attend_back(queries, keys_in, values, attend_kept, grad_mixed):
        paired, allowed, log_total = attend_kept
        grad_query, grad_key, grad_value = attention_backward(
            queries.reshape(query_shape),
            paired[:, :model_width].reshape(key_shape),
            paired[:, model_width:].reshape(key_shape),
            allowed,
            score_scale,
            log_total,
            grad_mixed.reshape(query_shape),
        )
        grad_pair = jnp.concatenate(
            [grad_key.reshape(key_total, model_width), grad_value.reshape(key_total, model_width)],
            axis=1,
        )
        for bit_level in reversed(range(bit_count)):
            half_rows = grad_pair.shape[0] // 2
            upper_half = rank_full // (1 << bit_level) % 2 == 1
            kept_half = jnp.where(upper_half, grad_pair[half_rows:], grad_pair[:half_rows])
            sent_half = jnp.where(upper_half, grad_pair[:half_rows], grad_pair[half_rows:])
            grad_pair = kept_half + swapped(
                sent_half.astype(jnp.bfloat16), "fsdp", bit_level
            ).astype(sent_half.dtype)
        grad_pair = grad_pair.astype(jnp.bfloat16)
        return (
            grad_query.reshape(seg_count, model_width).astype(jnp.bfloat16),
            grad_pair[:, :model_width],
            grad_pair[:, model_width:],
        )

    top_out, cls_saved = block_forward(heads_in, cls_unpacked, cls_attend)
    combined = jnp.concatenate([top_out[:, None, :], first_grid[:, 1:, :]], axis=1).reshape(
        tok_rows, model_width
    )
    output_rows = combined * live_rows[:, None]
    diff_rows = (output_rows - targets.astype(jnp.float32)) * live_rows[:, None]
    count_all, square_all = lax.psum(
        (jnp.sum(live_rows), jnp.sum(diff_rows * diff_rows)), ("rep", "fsdp")
    )
    loss_value = square_all / (count_all * model_width)
    slots_all = tok_rows * lax.axis_size("rep") * lax.axis_size("fsdp")
    grad_grid = (diff_rows * (slots_all / count_all)).reshape(seg_count, seg_len, model_width)
    cls_back = unpack_weights(
        (
            lax.all_gather(cls_mats, "fsdp", axis=0, tiled=True),
            lax.all_gather(cls_vecs, "fsdp", axis=0, tiled=True),
        ),
        model_width,
        ff_width,
    )
    heads_grad, cls_weight_rows, cls_g_vec = block_backward(
        grad_grid[:, 0, :], cls_back, cls_saved, cls_attend_back
    )
    cls_g_qkv, cls_g_out, cls_g_up, cls_g_down = weight_products(cls_weight_rows)
    pos_local = jnp.sum(position_hot[:, :, None] * heads_grad[:, None, :], axis=0)
    seg_grad_out = jnp.concatenate([heads_grad[:, None, :], grad_grid[:, 1:, :]], axis=1).reshape(
        tok_rows, model_width
    )
    seg_back = unpack_weights(
        (
            lax.all_gather(seg_mats, "fsdp", axis=0, tiled=True),
            lax.all_gather(seg_vecs, "fsdp", axis=0, tiled=True),
        ),
        model_width,
        ff_width,
    )
    input_grad, seg_weight_rows, seg_g_vec = block_backward(
        seg_grad_out, seg_back, seg_saved, seg_attend_back
    )
    seg_g_qkv, seg_g_out, seg_g_up, seg_g_down = weight_products(seg_weight_rows)
    owner_rows = tuple(
        (
            lax.psum_scatter(seg_g_qkv, "fsdp", scatter_dimension=0, tiled=True),
            lax.psum_scatter(seg_g_out, "fsdp", scatter_dimension=0, tiled=True),
            lax.psum_scatter(seg_g_up, "fsdp", scatter_dimension=0, tiled=True),
            lax.psum_scatter(seg_g_down, "fsdp", scatter_dimension=0, tiled=True),
            lax.psum_scatter(seg_g_vec, "fsdp", scatter_dimension=0, tiled=True),
            lax.psum_scatter(cls_g_qkv, "fsdp", scatter_dimension=0, tiled=True),
            lax.psum_scatter(cls_g_out, "fsdp", scatter_dimension=0, tiled=True),
            lax.psum_scatter(cls_g_up, "fsdp", scatter_dimension=0, tiled=True),
            lax.psum_scatter(cls_g_down, "fsdp", scatter_dimension=0, tiled=True),
            lax.psum_scatter(cls_g_vec, "fsdp", scatter_dimension=0, tiled=True),
        )
    )
    replica_share = (
        lax.psum_scatter(
            owner_rows[0].astype(jnp.bfloat16), "rep", scatter_dimension=1, tiled=True
        ).astype(jnp.float32),
        lax.psum_scatter(
            owner_rows[1].astype(jnp.bfloat16), "rep", scatter_dimension=1, tiled=True
        ).astype(jnp.float32),
        lax.psum_scatter(
            owner_rows[2].astype(jnp.bfloat16), "rep", scatter_dimension=1, tiled=True
        ).astype(jnp.float32),
        lax.psum_scatter(
            owner_rows[3].astype(jnp.bfloat16), "rep", scatter_dimension=1, tiled=True
        ).astype(jnp.float32),
        lax.psum_scatter(
            owner_rows[4].astype(jnp.bfloat16), "rep", scatter_dimension=0, tiled=True
        ).astype(jnp.float32),
        lax.psum_scatter(
            owner_rows[5].astype(jnp.bfloat16), "rep", scatter_dimension=1, tiled=True
        ).astype(jnp.float32),
        lax.psum_scatter(
            owner_rows[6].astype(jnp.bfloat16), "rep", scatter_dimension=1, tiled=True
        ).astype(jnp.float32),
        lax.psum_scatter(
            owner_rows[7].astype(jnp.bfloat16), "rep", scatter_dimension=1, tiled=True
        ).astype(jnp.float32),
        lax.psum_scatter(
            owner_rows[8].astype(jnp.bfloat16), "rep", scatter_dimension=1, tiled=True
        ).astype(jnp.float32),
        lax.psum_scatter(
            owner_rows[9].astype(jnp.bfloat16), "rep", scatter_dimension=0, tiled=True
        ).astype(jnp.float32),
    )
    all_summed = (
        lax.all_gather(replica_share[0].astype(jnp.bfloat16), "rep", axis=1, tiled=True).astype(
            jnp.float32
        ),
        lax.all_gather(replica_share[1].astype(jnp.bfloat16), "rep", axis=1, tiled=True).astype(
            jnp.float32
        ),
        lax.all_gather(replica_share[2].astype(jnp.bfloat16), "rep", axis=1, tiled=True).astype(
            jnp.float32
        ),
        lax.all_gather(replica_share[3].astype(jnp.bfloat16), "rep", axis=1, tiled=True).astype(
            jnp.float32
        ),
        lax.all_gather(replica_share[4].astype(jnp.bfloat16), "rep", axis=0, tiled=True).astype(
            jnp.float32
        ),
        lax.all_gather(replica_share[5].astype(jnp.bfloat16), "rep", axis=1, tiled=True).astype(
            jnp.float32
        ),
        lax.all_gather(replica_share[6].astype(jnp.bfloat16), "rep", axis=1, tiled=True).astype(
            jnp.float32
        ),
        lax.all_gather(replica_share[7].astype(jnp.bfloat16), "rep", axis=1, tiled=True).astype(
            jnp.float32
        ),
        lax.all_gather(replica_share[8].astype(jnp.bfloat16), "rep", axis=1, tiled=True).astype(
            jnp.float32
        ),
        lax.all_gather(replica_share[9].astype(jnp.bfloat16), "rep", axis=0, tiled=True).astype(
            jnp.float32
        ),
    )
    seg_summed = all_summed[:5]
    cls_summed = all_summed[5:]
    pos_total = lax.psum(pos_local, ("rep", "fsdp"))
    seg_mat_grad = jnp.concatenate(
        [seg_summed[0], seg_summed[1], seg_summed[2], seg_summed[3]], axis=1
    )
    cls_mat_grad = jnp.concatenate(
        [cls_summed[0], cls_summed[1], cls_summed[2], cls_summed[3]], axis=1
    )
    return (
        output_rows.astype(jnp.bfloat16),
        input_grad.astype(jnp.bfloat16),
        seg_mat_grad,
        seg_summed[4],
        cls_mat_grad,
        cls_summed[4],
        pos_total,
        loss_value,
    )


LINE = 4
PLANE = 4
CORES = 2
LANES = 128
GROUP = LINE * PLANE
LOW, WIDE = jnp.bfloat16, jnp.float32
MODEL = HEADS * HEAD_DIM
SPAN = 2 * LANES
TILE_START = (0, 1, 3, 4)


def line_pairs(apart):
    return [(source, (source + apart * PLANE) % GROUP) for source in range(GROUP)]


def plane_pairs(mask):
    return [(source, source ^ mask) for source in range(GROUP)]


def along_line(value, apart):
    return lax.ppermute(value, "fsdp", line_pairs(apart))


def in_plane(value, mask):
    return lax.ppermute(value, "fsdp", plane_pairs(mask))


def other_core(value):
    return lax.ppermute(value, "rep", [(0, 1), (1, 0)])


def after(value, *events):
    return lax.optimization_barrier((value,) + events)[0]


def together(*values):
    return tuple(lax.optimization_barrier(values))


def shape_of(dims, dtype=WIDE):
    return jax.ShapeDtypeStruct(dims, dtype)


def run_kernel(body, name, outs, where, blocks, arrays, scratch=(), far=(), flops=0):
    in_specs = [pl.BlockSpec(memory_space=pltpu.SMEM)]
    in_specs += [pl.BlockSpec(memory_space=pltpu.HBM)] * len(blocks)
    in_specs += [pl.BlockSpec(memory_space=pltpu.VMEM)] * len(arrays)
    spaces = [pltpu.HBM if at in far else pltpu.VMEM for at in range(len(outs))]
    moved = sum(x.size * x.dtype.itemsize for x in list(blocks) + list(arrays))
    moved += sum(math.prod(o.shape) * jnp.dtype(o.dtype).itemsize for o in outs)
    return pl.pallas_call(
        body,
        name=name,
        out_shape=tuple(outs),
        in_specs=in_specs,
        out_specs=tuple(pl.BlockSpec(memory_space=space) for space in spaces),
        scratch_shapes=list(scratch),
        cost_estimate=pl.CostEstimate(flops=flops, bytes_accessed=moved, transcendentals=0),
        compiler_params=pltpu.CompilerParams(vmem_limit_bytes=VMEM_BYTES),
    )(where, *blocks, *arrays)


VMEM_BYTES = 24 * 1024 * 1024
HALF = MODEL // CORES
FF_HALF = FF // CORES
OWN = MODEL // GROUP
QUARTER = 3 * SPAN + 2 * FF // LINE
QUARTER_HALF = QUARTER // CORES


def aligned(start):
    return pl.multiple_of(start, LANES)


def wait_all(copies):
    for copy in copies:
        copy.wait()


def run_copies(pairs, sems):
    copies = [
        pltpu.make_async_copy(source, target, sems.at[at])
        for at, (source, target) in enumerate(pairs)
    ]
    for copy in copies:
        copy.start()
    wait_all(copies)


FIRST = 4 * HALF + LANES
OWN_CUT = FIRST + FF_HALF // 2
LINE_CUTS = (7 * LANES, FF_HALF // 2, FF_HALF // 2)
WIDTHS = (FIRST, FF_HALF, FF_HALF)


def group_pieces(group, refs):
    own, rest = refs[:LINE], refs[LINE:]
    own_x, own_y, far_x, far_y, line_x, line_y, late_x, late_y = rest
    width, cut = WIDTHS[group], LINE_CUTS[group]
    start = sum(WIDTHS[:group])
    if group == 0:
        bases = (sum(WIDTHS) - OWN_CUT, OWN_CUT)
    else:
        before, before_cut = WIDTHS[group - 1], LINE_CUTS[group - 1]
        bases = (2 * before - before_cut, before + before_cut)
    pieces = {(0, step): [(own[step], 0, 0, width)] for step in range(LINE)}
    for mask, whole, line, base in ((1, own_x, line_x, bases[0]), (2, own_y, line_y, bases[1])):
        pieces[mask, 0] = [(whole, start, 0, width)]
        for step in range(1, LINE):
            pieces[mask, step] = [(line, base + (step - 1) * width, 0, width)]
    middle = min(max(OWN_CUT - start, 0), width)
    far = []
    if middle > 0:
        far.append((far_y, start, 0, middle))
    if middle < width:
        far.append((far_x, start + middle - OWN_CUT, middle, width))
    pieces[3, 0] = far
    pieces[3, 1] = [(late_y, 0, 0, width)]
    pieces[3, 2] = [(late_y, width, 0, cut), (late_x, 0, cut, width)]
    pieces[3, 3] = [(late_x, width - cut, 0, width)]
    return pieces


def gather_group(where, group, refs, targets):
    line_at, plane_at = where[0], where[1]
    for (mask, step), parts in group_pieces(group, refs).items():
        chip = (line_at + LINE - step) % LINE * PLANE + (plane_at ^ mask)
        for whole, first, last in targets:
            for ref, offset, begin, end in parts:
                low, high = max(first, begin), min(last, end)
                if low < high:
                    source = slice(offset + low - begin, offset + high - begin)
                    whole[chip, :, low - first : high - first] = ref[:, source]


def gather_blocks(where, refs, base, width, targets):
    line_at, plane_at = where[0], where[1]
    half = LINE // 2
    for mask in range(PLANE):
        for step in range(LINE):
            if mask == 0:
                ref, offset = refs[step], 0
            elif mask == 3:
                ref = refs[LINE + 3] if step < half else refs[LINE + 2]
                offset = step % half * width
            else:
                ref, offset = refs[LINE + mask - 1], base + step * width
            chip = (line_at + LINE - step) % LINE * PLANE + (plane_at ^ mask)
            for whole, first, last in targets:
                whole[chip] = ref[:, offset + first : offset + last]


def whole_rows(ref):
    value = ref[...]
    return value.reshape(value.shape[0] * value.shape[1], value.shape[2])


def prepare_first_kernel(where, seg, vecs, flags, out, live_out, sems):
    core_at = where[2]
    pairs = []
    for piece in range(4):
        source = seg.at[:, pl.ds(aligned(piece * MODEL + core_at * HALF), HALF)]
        pairs.append((source, out.at[:, piece * HALF : (piece + 1) * HALF]))
    run_copies(pairs, sems)
    size = vecs.shape[1]
    lines = -(-size // LANES)
    block = jnp.zeros((OWN, LANES), WIDE)
    row_at = lax.broadcasted_iota(jnp.int32, (OWN, LANES), 0)
    for which in range(2):
        for line in range(lines):
            width = min(LANES, size - line * LANES)
            value = vecs[which : which + 1, line * LANES : line * LANES + width]
            if width < LANES:
                value = jnp.concatenate([value, jnp.zeros((1, LANES - width), WIDE)], axis=1)
            block = jnp.where(row_at == which * lines + line, value, block)
    live = flags[...].astype(WIDE)
    live_out[...] = live
    count = jnp.sum(live, axis=1, keepdims=True)
    block = jnp.where(row_at == 2 * lines, count, block)
    out[:, 4 * HALF :] = block.astype(LOW)


def prepare_rest_kernel(where, seg, cls, *refs):
    second_out, third_out = refs[:2]
    step_outs, out_half, order_out = refs[2 : 2 + LINE], refs[2 + LINE], refs[3 + LINE]
    quarters, sems = refs[4 + LINE :]
    line_at, plane_at, core_at = where[0], where[1], where[2]
    start = core_at * FF_HALF
    pairs = [
        (seg.at[:, pl.ds(aligned(4 * MODEL + start), FF_HALF)], second_out),
        (seg.at[:, pl.ds(aligned(4 * MODEL + FF + start), FF_HALF)], third_out),
        (cls.at[:, pl.ds(aligned(3 * MODEL + core_at * HALF), HALF)], out_half),
    ]
    part = FF // LINE
    for at in range(LINE):
        first = TILE_START[at] * LANES
        plan = [(piece * MODEL + first, SPAN, piece * SPAN) for piece in range(3)]
        plan += [
            (4 * MODEL + piece * FF + at * part, part, 3 * SPAN + piece * part)
            for piece in range(2)
        ]
        for source, size, target in plan:
            pairs.append(
                (
                    cls.at[:, source : source + size],
                    quarters.at[at, :, target : target + size],
                )
            )
    run_copies(pairs, sems)
    lanes = pl.ds(aligned(core_at * QUARTER_HALF), QUARTER_HALF)
    for step, out in enumerate(step_outs):
        out[...] = quarters[(line_at + step) % LINE, :, lanes]
    column = lax.broadcasted_iota(jnp.int32, (1, SPAN), 1)
    feature = lax.broadcasted_iota(jnp.int32, (MODEL, SPAN), 0)
    turn = sum((column >= OWN * step).astype(jnp.int32) for step in range(1, LINE))
    held = column - OWN * turn
    turn = (line_at + turn) % LINE
    for mask in range(PLANE):
        source = (turn * PLANE + (plane_at ^ mask)) * OWN + held
        source = jnp.where(column < OWN * LINE, source, -1)
        order_out[:, mask * SPAN : (mask + 1) * SPAN] = (feature == source).astype(LOW)


def prepare_kernel(where, seg, cls, vecs, flags, first_out, live_out, *refs):
    rest, (first_sems, quarters, sems) = refs[:-3], refs[-3:]
    prepare_first_kernel(where, seg, vecs, flags, first_out, live_out, first_sems)
    prepare_rest_kernel(where, seg, cls, *rest, quarters, sems)


def lane_mask(rows, head):
    lane = lax.broadcasted_iota(jnp.int32, (rows, LANES), 1)
    return (lane < HEAD_DIM) if head == 0 else (lane >= HEAD_DIM)


def masked(value, mask):
    return jnp.where(mask, value, jnp.zeros_like(value))


def head_probabilities(query, key, allowed):
    scores = product_right(query, key) * HEAD_DIM ** (-0.5)
    scores = jnp.where(allowed, scores, MASK_FILL)
    raised = jnp.exp(scores - jnp.max(scores, axis=-1, keepdims=True))
    return raised / jnp.sum(raised, axis=-1, keepdims=True)


def attend_tiles(qkv, width, allowed):
    rows = qkv.shape[0]
    mixed = []
    for tile in range(width // LANES):
        at = tile * LANES
        query, key, value = (
            qkv[:, piece * width + at : piece * width + at + LANES] for piece in range(3)
        )
        total = jnp.zeros((rows, LANES), WIDE)
        for head in range(2):
            mask = lane_mask(rows, head)
            weights = head_probabilities(masked(query, mask), key, allowed).astype(LOW)
            total = total + product_plain(weights, masked(value, mask))
        mixed.append(total.astype(LOW))
    return mixed


def attend_tiles_back(qkv, grad_mixed, width, allowed):
    rows = qkv.shape[0]
    scale = HEAD_DIM ** (-0.5)
    results = ([], [], [])
    for tile in range(width // LANES):
        at = tile * LANES
        query, key, value = (
            qkv[:, piece * width + at : piece * width + at + LANES] for piece in range(3)
        )
        grad = grad_mixed[:, at : at + LANES]
        totals = [jnp.zeros((rows, LANES), WIDE) for _ in range(3)]
        for head in range(2):
            mask = lane_mask(rows, head)
            query_low, key_low, grad_low = (masked(x, mask) for x in (query, key, grad))
            chance = head_probabilities(query_low, key, allowed)
            grad_chance = product_right(grad_low, value)
            inner = jnp.sum(grad_chance * chance, axis=-1, keepdims=True)
            grad_scores = (chance * (grad_chance - inner)).astype(LOW)
            totals[0] = totals[0] + product_plain(grad_scores, key_low)
            totals[1] = totals[1] + product_left(grad_scores, query_low)
            totals[2] = totals[2] + product_left(chance.astype(LOW), grad_low)
        results[0].append((totals[0] * scale).astype(LOW))
        results[1].append((totals[1] * scale).astype(LOW))
        results[2].append(totals[2].astype(LOW))
    return results[0] + results[1] + results[2]


def token_allowed(live_row):
    shape = (SEG, SEG)
    same = lax.broadcasted_iota(jnp.int32, shape, 0) == lax.broadcasted_iota(jnp.int32, shape, 1)
    return (live_row > 0.5) | same


def qkv_kernel(where, *refs):
    blocks = refs[:12]
    hidden, hidden_got, live_row, live_got, order = refs[12:17]
    weight, out_low, out_high, qkv_out, mixed_out = refs[17:22]
    vectors_out, count_out, ordered_out = refs[22:25]
    vec_rows, flat, inputs, out_half = refs[25:]
    core_at = where[2]
    gather_group(
        where,
        0,
        blocks,
        (
            (weight, 0, 3 * HALF),
            (out_half, 3 * HALF, 4 * HALF),
            (vec_rows, 4 * HALF, 4 * HALF + LANES),
        ),
    )
    out_low[...] = out_half[: GROUP // 2]
    out_high[...] = out_half[GROUP // 2 :]
    piece = (8 * MODEL + FF) // GROUP
    lines = -(-piece // LANES)
    count = jnp.zeros((1, LANES), WIDE)
    for chip in range(GROUP):
        rows = vec_rows[chip, 0:16, :].astype(WIDE)
        for block in range(2):
            joined = jnp.concatenate(
                [rows[block * lines + r : block * lines + r + 1] for r in range(lines)], axis=1
            )
            flat[block : block + 1, chip * piece : (chip + 1) * piece] = joined[:, :piece]
        count = count + rows[2 * lines : 2 * lines + 1]
    rows_each = (8 * MODEL + FF) // MODEL
    for block in range(2):
        for row in range(rows_each):
            vectors_out[block * rows_each + row : block * rows_each + row + 1, :] = flat[
                block : block + 1, row * MODEL : (row + 1) * MODEL
            ]
    count_out[...] = jnp.broadcast_to(count, count_out.shape)
    inputs[:SEG] = hidden[...]
    inputs[SEG:] = hidden_got[...]
    projected = product_plain(inputs[...], whole_rows(weight))
    lanes = pl.ds(aligned(core_at * HALF), HALF)
    qkv_out[:, :HALF] = (projected[:, :HALF] + vectors_out[0:1, lanes]).astype(LOW)
    qkv_out[:, HALF : 2 * HALF] = projected[:, HALF : 2 * HALF].astype(LOW)
    qkv_out[:, 2 * HALF :] = (projected[:, 2 * HALF :] + vectors_out[1:2, lanes]).astype(LOW)
    for part, live in enumerate((live_row, live_got)):
        rows = slice(part * SEG, (part + 1) * SEG)
        tiles = attend_tiles(qkv_out[rows, :], HALF, token_allowed(live[...]))
        for tile, value in enumerate(tiles):
            mixed_out[rows, tile * LANES : (tile + 1) * LANES] = value
    ordered_out[...] = product_plain(inputs[...], order[...]).astype(LOW)


def norm_rows(summed):
    row_mean = jnp.mean(summed, axis=-1, keepdims=True)
    centered = summed - row_mean
    inv_dev = lax.rsqrt(jnp.mean(centered * centered, axis=-1, keepdims=True) + NORM_EPS)
    return centered * inv_dev, inv_dev


def norm_rows_back(grad_out, normed, inv_dev, gain):
    scaled = grad_out * gain
    mean_one = jnp.mean(scaled, axis=-1, keepdims=True)
    mean_two = jnp.mean(scaled * normed, axis=-1, keepdims=True)
    return inv_dev * (scaled - mean_one - normed * mean_two)


def column_sum(value):
    return jnp.sum(value.astype(WIDE), axis=0, keepdims=True)


def four_rows(vectors, first):
    return jnp.concatenate([vectors[first + at : first + at + 1, :] for at in range(4)], axis=1)


def gelu_both(before):
    half = 0.5 * (1.0 + lax.erf(before * SQRT_HALF))
    slope = half + before * jnp.exp(-0.5 * before * before) * INV_SQRT_TWO_PI
    return before * half, slope


def out_kernel(where, hidden, mixed, mixed_got, low, high, low_got, high_got, *refs):
    vectors, order, full_out, ordered_out, normed_out, inv_out, low_out, mixed_full = refs
    core_at = where[2]
    own, other = aligned(core_at * HALF), aligned((1 - core_at) * HALF)
    rows = MODEL // 2
    full_out[:rows, pl.ds(own, HALF)] = whole_rows(low)
    full_out[rows:, pl.ds(own, HALF)] = whole_rows(high)
    full_out[:rows, pl.ds(other, HALF)] = whole_rows(low_got)
    full_out[rows:, pl.ds(other, HALF)] = whole_rows(high_got)
    mixed_full[:, pl.ds(own, HALF)] = mixed[...]
    mixed_full[:SEG, pl.ds(other, HALF)] = mixed_got[SEG:, :]
    mixed_full[SEG:, pl.ds(other, HALF)] = mixed_got[:SEG, :]
    branch = product_plain(mixed_full[:SEG, :], full_out[...])
    normed, inv_dev = norm_rows(hidden[...].astype(WIDE) + branch + vectors[2:3, :])
    normed_out[...] = normed
    inv_out[...] = inv_dev
    low_out[...] = (normed * vectors[4:5, :] + vectors[5:6, :]).astype(LOW)
    ordered_out[...] = product_plain(mixed_full[...], order[...]).astype(LOW)


def up_kernel(where, *refs):
    blocks = refs[:12]
    low, low_got, vectors = refs[12:15]
    weight, act_out, slope_out, both = refs[15:]
    core_at = where[2]
    gather_group(where, 1, blocks, ((weight, 0, FF_HALF),))
    both[:SEG] = low[...]
    both[SEG:] = low_got[...]
    for at in range(FF_HALF // MODEL):
        columns = slice(at * MODEL, (at + 1) * MODEL)
        held = weight[:, :, columns]
        before = product_plain(both[...], held.reshape(MODEL, MODEL))
        bias = vectors[pl.ds(8 + core_at * (FF_HALF // MODEL) + at, 1), :]
        value, slope = gelu_both(before + bias)
        act_out[:, columns] = value.astype(LOW)
        slope_out[:, columns] = slope


def down_kernel(where, *refs):
    blocks, act = refs[:12], refs[12]
    weight, own_out, send_out = refs[13:]
    gather_group(where, 2, blocks, ((weight, 0, FF_HALF),))
    partial = product_right(act[...], whole_rows(weight))
    own_out[...] = partial[:SEG]
    send_out[...] = partial[SEG:]


def seg_rows_kernel(where, *refs):
    own, got, normed_first, vectors, targets, live, seg_pos = refs[:7]
    normed_out, inv_out, diff_out, rows_out, head_out = refs[7:]
    doc, number = where[3], where[4]
    first = normed_first[...] * vectors[4:5, :] + vectors[5:6, :]
    normed, inv_dev = norm_rows(first + own[...] + got[...] + vectors[3:4, :])
    normed_out[...] = normed
    inv_out[...] = inv_dev
    rows = normed * vectors[6:7, :] + vectors[7:8, :]
    shape = (SEG, SEG)
    same = lax.broadcasted_iota(jnp.int32, shape, 0) == lax.broadcasted_iota(jnp.int32, shape, 1)
    live_rows = jnp.sum(jnp.where(same, live[...], 0.0), axis=1, keepdims=True)
    target_rows = targets[...].astype(WIDE)
    output = rows * live_rows
    rows_out[...] = output
    diff = (output - target_rows) * live_rows
    row_at = lax.broadcasted_iota(jnp.int32, (SEG, 1), 0)
    diff = jnp.where(row_at > 0, diff, 0.0)
    diff_out[...] = diff
    table = seg_pos[...].astype(WIDE)
    chosen = lax.broadcasted_iota(jnp.int32, table.shape, 0) == number
    position = jnp.sum(jnp.where(chosen, table, 0.0), axis=0, keepdims=True)
    head_out[:, :MODEL] = rows[0:1, :] + position
    head_out[:, MODEL : 2 * MODEL] = target_rows[0:1, :]
    square = jnp.sum(column_sum(diff * diff), axis=1, keepdims=True)
    lane = lax.broadcasted_iota(jnp.int32, (1, LANES), 1)
    facts = jnp.where(lane == 0, live_rows[0:1, :], 0.0)
    facts = jnp.where(lane == 1, doc.astype(WIDE), facts)
    facts = jnp.where(lane == 2, number.astype(WIDE), facts)
    facts = jnp.where(lane == 3, square, facts)
    head_out[:, 2 * MODEL :] = facts


def second_norm_kernel(where, diff, count, normed, inv_dev, vectors, grad_out, low_out, sums_out):
    grad_top = diff[...] * ((SEG * GROUP * CORES) / count[0:1, 0:1])
    normed_rows = normed[...]
    grad = norm_rows_back(grad_top, normed_rows, inv_dev[...], vectors[6:7, :])
    low = grad.astype(LOW)
    grad_out[...] = grad
    low_out[...] = low
    sums_out[0:1, :] = column_sum(low)
    sums_out[1:2, :] = column_sum(grad_top * normed_rows)
    sums_out[2:3, :] = column_sum(grad_top)


def mlp_back_kernel(where, *refs):
    low, low_got, down_weight, up_weight, slope = refs[:5]
    pre_out, own_out, send_out, sums_out, both = refs[5:]
    both[:SEG] = low[...]
    both[SEG:] = low_got[...]
    for at in range(FF_HALF // MODEL):
        columns = slice(at * MODEL, (at + 1) * MODEL)
        held = down_weight[:, :, columns]
        before = product_plain(both[...], held.reshape(MODEL, MODEL))
        pre = (before * slope[:, columns]).astype(LOW)
        pre_out[:, columns] = pre
        sums_out[at : at + 1, :] = column_sum(pre)
    partial = product_right(pre_out[...], whole_rows(up_weight))
    own_out[...] = partial[:SEG]
    send_out[...] = partial[SEG:]


def scatter_parts(where, parts, outs, sems):
    line_at, plane_at = where[0], where[1]
    far_low, far_high, to_x, to_y, kept = outs
    half = LINE // 2
    copies = []
    for mask in range(PLANE):
        for step in range(LINE):
            source = parts.at[(line_at + step) % LINE * PLANE + (plane_at ^ mask)]
            if mask == 3:
                target = far_low.at[step] if step < half else far_high.at[step - half]
            else:
                target = (kept, to_x, to_y)[mask].at[step]
            copies.append(pltpu.make_async_copy(source, target, sems.at[len(copies)]))
    for copy in copies:
        copy.start()
    wait_all(copies)


def mlp_weight_kernel(where, *refs):
    first, first_got, second, second_got, pre, act = refs[:6]
    outs = refs[6:11]
    left, parts, sems = refs[11:]
    for at, (own, got, right) in enumerate(((first, first_got, pre), (second, second_got, act))):
        left[:SEG] = own[...]
        left[SEG:] = got[...]
        for piece in range(FF_HALF // MODEL):
            start = piece * MODEL
            product = product_left(left[...], right[:, start : start + MODEL]).astype(LOW)
            target = at * FF_HALF + start
            parts[:, :, target : target + MODEL] = product.reshape(GROUP, OWN, MODEL)
    scatter_parts(where, parts, outs, sems)


def attn_product(where, refs, mask, piece):
    hidden, mixed, proj, branch, got = refs
    lanes = slice(mask * SPAN, (mask + 1) * SPAN)
    if piece < 3:
        right = proj[:, piece * HALF : (piece + 1) * HALF]
        product = product_left(hidden[:, lanes], right)
    else:
        own = branch[:, pl.ds(aligned(where[2] * HALF), HALF)]
        product = product_left(mixed[:SEG, lanes], own)
        product = product + product_left(mixed[SEG:, lanes], got[:, HALF:])
    return product[: LINE * OWN].astype(LOW).reshape(LINE, OWN, HALF)


def attn_far_kernel(where, *refs):
    low_out, high_out = refs[5:]
    half = LINE // 2
    for piece in range(4):
        columns = slice(piece * HALF, (piece + 1) * HALF)
        product = attn_product(where, refs[:5], 3, piece)
        low_out[:, :, columns] = product[:half]
        high_out[:, :, columns] = product[half:]


def attn_near_kernel(where, *refs):
    top_row, out_rows, live_row = refs[5:8]
    row_at = lax.broadcasted_iota(jnp.int32, (SEG, 1), 0)
    output = jnp.where(row_at == 0, top_row[...] * live_row[:, 0:1], out_rows[...])
    refs[11][...] = output.astype(LOW)
    for mask, out in ((1, refs[8]), (2, refs[9]), (0, refs[10])):
        for piece in range(4):
            columns = slice(piece * HALF, (piece + 1) * HALF)
            out[:, :, columns] = attn_product(where, refs[:5], mask, piece)


def fold_kernel(where, kept, got_x, got_y, *refs):
    extra, own_out, sent = refs[: -LINE], refs[-LINE], refs[1 - LINE :]
    rows = kept.shape[1]
    for step in range(LINE):
        total = kept[step].astype(WIDE) + got_x[step].astype(WIDE) + got_y[step].astype(WIDE)
        if step == 0:
            own_out[...] = total
            continue
        out = sent[step - 1]
        out[:rows, :] = total.astype(LOW)
        if extra:
            out[rows:, :] = jnp.zeros_like(out[rows:, :])
            out[rows:, : extra[0].shape[1]] = extra[0][...]


def reduce_far(parts):
    return together(in_plane(parts[0], 2), in_plane(parts[1], 1))


def reduce_add(where, parts, far):
    shape = parts[2].shape
    return run_kernel(
        add_far_kernel,
        "add_far",
        [shape_of(shape, LOW)] * 2,
        where,
        (),
        tuple(far) + (parts[2], parts[3]),
    )


def reduce_fold(where, kept, got, *extra):
    _, rows, columns = kept.shape
    more = sum(value.shape[0] for value in extra)
    return run_kernel(
        fold_kernel,
        "fold",
        [shape_of((rows, columns))] + [shape_of((rows + more, columns), LOW)] * (LINE - 1),
        where,
        (),
        (kept,) + tuple(got) + extra,
    )


def reduce_line(own, pieces):
    total = own
    for piece in pieces:
        total = total + piece[: own.shape[0]].astype(WIDE)
    return total


def head_back_kernel(where, *refs):
    grad, grad_got, down_weight, up_weight, slope, act, low, low_got = refs[:8]
    own_out, send_out, data_out = refs[8:]
    few = 16
    row_at = lax.broadcasted_iota(jnp.int32, (few, 1), 0)

    def two_rows(first, second):
        return jnp.where(row_at == 0, first, jnp.where(row_at == 1, second, 0.0))

    second = two_rows(grad[...], grad_got[...]).astype(LOW)
    data_out[0:1, :] = low[0:1, :].astype(WIDE)
    data_out[1:2, :] = low_got[0:1, :].astype(WIDE)
    data_out[2:4, :] = second[0:2].astype(WIDE)
    partial = jnp.zeros((few, MODEL), WIDE)
    for at in range(FF_HALF // MODEL):
        columns = slice(at * MODEL, (at + 1) * MODEL)
        before = product_plain(second, down_weight[:, :, columns].reshape(MODEL, MODEL))
        slopes = two_rows(slope[0:1, columns], slope[SEG : SEG + 1, columns])
        pre = (before * slopes).astype(LOW)
        partial = partial + product_right(pre, up_weight[:, :, columns].reshape(MODEL, MODEL))
        data_out[4 + 2 * at : 6 + 2 * at, :] = pre[0:2].astype(WIDE)
        data_out[8 + 2 * at : 9 + 2 * at, :] = act[0:1, columns].astype(WIDE)
        data_out[9 + 2 * at : 10 + 2 * at, :] = act[SEG : SEG + 1, columns].astype(WIDE)
    own_out[...] = partial[0:1]
    send_out[...] = partial[1:2]


def first_norm_kernel(where, *refs):
    second_grad, own, got, head_grad, head_own, head_got = refs[:6]
    normed_rows, inv_dev, vectors, out_weight = refs[6:10]
    grad_out, branch_out, mixed_out, send_out, sums_out = refs[10:]
    core_at = where[2]
    grad_rows = second_grad[...] + own[...] + got[...]
    head = head_grad[...] + head_own[...] + head_got[...]
    row_at = lax.broadcasted_iota(jnp.int32, (SEG, 1), 0)
    grad_rows = jnp.where(row_at == 0, head, grad_rows)
    normed = normed_rows[...]
    grad = norm_rows_back(grad_rows, normed, inv_dev[...], vectors[4:5, :])
    grad_out[...] = grad
    branch = grad.astype(LOW)
    branch_out[...] = branch
    mixed_out[...] = product_right(branch, out_weight[...]).astype(LOW)
    other = pl.ds(aligned((1 - core_at) * HALF), HALF)
    send_out[:, :HALF] = mixed_out[:, other]
    send_out[:, HALF:] = branch_out[:, other]
    sums_out[0:1, :] = column_sum(branch)
    sums_out[1:2, :] = column_sum(grad_rows * normed)
    sums_out[2:3, :] = column_sum(grad_rows)


def attn_back_kernel(where, *refs):
    qkv, mixed_grad, got, live_row, live_got, weight = refs[:6]
    sums_first, sums_second, sums_up, head_top, head_normed, data = refs[6:12]
    proj_out, own_out, send_out, payload_out, rows = refs[12:]
    core_at = where[2]
    lanes = pl.ds(aligned(core_at * HALF), HALF)
    for part, live in enumerate((live_row, live_got)):
        at = slice(part * SEG, (part + 1) * SEG)
        grad = mixed_grad[:, lanes] if part == 0 else got[:, :HALF]
        pieces = attend_tiles_back(qkv[at, :], grad, HALF, token_allowed(live[...]))
        for tile, value in enumerate(pieces):
            proj_out[at, tile * LANES : (tile + 1) * LANES] = value
    partial = product_right(proj_out[...], whole_rows(weight))
    own_out[...] = partial[:SEG]
    send_out[...] = partial[SEG:]
    rows[...] = jnp.zeros_like(rows)
    rows[0:12, :] = data[0:12, :]
    rows[12:13, lanes] = column_sum(proj_out[:, :HALF])
    rows[13:14, lanes] = column_sum(proj_out[:, 2 * HALF :])
    rows[14:15, :] = sums_first[0:1, :]
    rows[15:16, :] = sums_second[0:1, :] + data[2:3, :]
    rows[16:18, :] = sums_first[1:3, :]
    rows[18:19, :] = sums_second[1:2, :] + head_top[...] * head_normed[0:1, :]
    rows[19:20, :] = sums_second[2:3, :] + head_top[...]
    for at in range(FF_HALF // MODEL):
        total = sums_up[at : at + 1, :] + data[4 + 2 * at : 5 + 2 * at, :]
        total = total + data[5 + 2 * at : 6 + 2 * at, :]
        rows[pl.ds(20 + core_at * (FF_HALF // MODEL) + at, 1), :] = total
    payload_out[...] = rows[...].astype(LOW)


def cls_gather_kernel(where, *refs):
    blocks = refs[:8]
    own_out, from_x, from_y, far_x = refs[8], refs[4], refs[5], refs[6]
    weight_out, out_rows = refs[9:]
    plane_at = where[1]
    gather_blocks(where, blocks, 0, QUARTER_HALF, ((weight_out, 0, QUARTER_HALF),))
    first = LINE * QUARTER_HALF
    out_rows[plane_at] = own_out[...]
    out_rows[plane_at ^ 1] = from_x[:, first : first + HALF]
    out_rows[plane_at ^ 2] = from_y[:, first : first + HALF]
    first = LINE // 2 * QUARTER_HALF
    out_rows[plane_at ^ 3] = far_x[:, first : first + HALF]


def cls_weight_kernel(where, own, got, out_half, out_got, weight_out, out_full):
    line_at, core_at = where[0], where[2]
    out_full[...] = jnp.zeros_like(out_full)
    for value, part, core in ((own, out_half, core_at), (got, out_got, 1 - core_at)):
        weight_out[:, :, pl.ds(aligned(core * QUARTER_HALF), QUARTER_HALF)] = value[...]
        rows = part[...].reshape(3, HEAD_DIM, HALF)
        out_full[pl.ds(line_at % 2, 3), :, pl.ds(aligned(core * HALF), HALF)] = rows


def add_far_kernel(where, far_low, far_high, to_x, to_y, x_out, y_out):
    half = LINE // 2
    x_out[:half] = to_x[:half] + far_low[...]
    x_out[half:] = to_x[half:]
    y_out[:half] = to_y[:half]
    y_out[half:] = to_y[half:] + far_high[...]


def row_from_column(column, size):
    shape = (size, size)
    same = lax.broadcasted_iota(jnp.int32, shape, 0) == lax.broadcasted_iota(jnp.int32, shape, 1)
    return jnp.sum(jnp.where(same, column, 0.0), axis=0, keepdims=True)


def head_allowed(heads):
    facts = heads[:, 2 * MODEL :]
    live, doc = facts[:, 0:1], facts[:, 1:2]
    shape = (GROUP, GROUP)
    same = lax.broadcasted_iota(jnp.int32, shape, 0) == lax.broadcasted_iota(jnp.int32, shape, 1)
    live_row, doc_row = row_from_column(live, GROUP), row_from_column(doc, GROUP)
    return ((live_row > 0.5) & (doc == doc_row)) | same


def quarter_mask(quarter):
    lane = lax.broadcasted_iota(jnp.int32, (GROUP, SPAN), 1)
    first = (quarter % 2) * HEAD_DIM
    return (lane >= first) & (lane < first + 3 * HEAD_DIM)


def quarter_piece(vectors, row, quarter):
    value = jnp.zeros((1, SPAN), WIDE)
    for at in range(LINE):
        first = TILE_START[at] * LANES
        value = jnp.where(quarter == at, vectors[row : row + 1, first : first + SPAN], value)
    return value


def cls_attend_kernel(where, *refs):
    stacks, vectors, weight, out_weight = refs[:4], refs[4], refs[5], refs[6]
    heads_out, qkv_out, mixed_out, part_out = refs[7:]
    line_at, plane_at = where[0], where[1]
    for step, stack in enumerate(stacks):
        for mask in range(PLANE):
            row = (line_at + LINE - step) % LINE * PLANE + (plane_at ^ mask)
            heads_out[pl.ds(row, 1), :] = stack[mask : mask + 1, :]
    heads = heads_out[...]
    inputs = heads[:, :MODEL].astype(LOW)
    projected = product_plain(inputs, weight[:, : 3 * SPAN])
    query = projected[:, :SPAN] + quarter_piece(vectors, 12, line_at)
    value = projected[:, 2 * SPAN :] + quarter_piece(vectors, 13, line_at)
    qkv_out[:, :SPAN] = query.astype(LOW)
    qkv_out[:, SPAN : 2 * SPAN] = projected[:, SPAN : 2 * SPAN].astype(LOW)
    qkv_out[:, 2 * SPAN :] = value.astype(LOW)
    mixed = attend_tiles(qkv_out[...], SPAN, head_allowed(heads))
    mixed = masked(jnp.concatenate(mixed, axis=1), quarter_mask(line_at))
    mixed_out[...] = mixed
    part_out[...] = product_plain(mixed, out_weight[...])


def cls_mlp_kernel(where, *refs):
    heads, own, got_one, got_two, got_three, vectors, weight = refs[:7]
    normed_out, inv_out, low_out, act_out, slope_out, part_out = refs[7:]
    line_at = where[0]
    branch = own[...] + got_one[...] + got_two[...] + got_three[...]
    normed, inv_dev = norm_rows(heads[:, :MODEL] + branch + vectors[14:15, :])
    normed_out[...] = normed
    inv_out[...] = inv_dev
    low = (normed * vectors[16:17, :] + vectors[17:18, :]).astype(LOW)
    low_out[...] = low
    part = FF // LINE
    first = 3 * SPAN
    bias = vectors[pl.ds(20 + line_at, 1), :]
    before = product_plain(low, weight[:, first : first + part]) + bias
    value, slope = gelu_both(before)
    act = value.astype(LOW)
    act_out[...] = act
    slope_out[...] = slope
    part_out[...] = product_right(act, weight[:, first + part :])


def cls_top_kernel(where, *refs):
    heads, own, got_one, got_two, got_three, vectors, weight = refs[:7]
    normed_first, count, slope = refs[7:10]
    top_out, square_out, grad_out, second_out, pre_out, part_out, sums_out = refs[10:17]
    held = refs[17]
    rank = where[0] * PLANE + where[1]
    first = normed_first[...] * vectors[16:17, :] + vectors[17:18, :]
    down = own[...] + got_one[...] + got_two[...] + got_three[...]
    normed, inv_dev = norm_rows(first + down + vectors[15:16, :])
    rows = normed * vectors[18:19, :] + vectors[19:20, :]
    held[...] = rows
    top_out[...] = held[pl.ds(rank, 1), :]
    facts = heads[:, 2 * MODEL :]
    live = facts[:, 0:1]
    diff = (rows * live - heads[:, MODEL : 2 * MODEL]) * live
    square = jnp.sum(column_sum(diff * diff), axis=1, keepdims=True)
    square = square + jnp.sum(facts[:, 3:4], axis=0, keepdims=True)
    square_out[...] = jnp.broadcast_to(square, square_out.shape)
    grad_top = diff * ((SEG * GROUP * CORES) / count[0:1, 0:1])
    grad = norm_rows_back(grad_top, normed, inv_dev, vectors[18:19, :])
    sums_out[0:1, :] = column_sum(grad_top * normed)
    sums_out[1:2, :] = column_sum(grad_top)
    grad_out[...] = grad
    second = grad.astype(LOW)
    second_out[...] = second
    part = FF // LINE
    at = 3 * SPAN
    pre = (product_plain(second, weight[:, at + part :]) * slope[...]).astype(LOW)
    pre_out[...] = pre
    part_out[...] = product_right(pre, weight[:, at : at + part])


def cls_attend_back_kernel(where, *refs):
    heads, own, got_one, got_two, got_three, vectors, weight, out_weight = refs[:8]
    grad_in, normed_first, inv_first, qkv = refs[8:12]
    grad_out, branch_out, proj_out, part_out, sums_out = refs[12:]
    line_at = where[0]
    grad_first = grad_in[...] + own[...] + got_one[...] + got_two[...] + got_three[...]
    normed = normed_first[...]
    grad = norm_rows_back(grad_first, normed, inv_first[...], vectors[16:17, :])
    sums_out[0:1, :] = column_sum(grad_first * normed)
    sums_out[1:2, :] = column_sum(grad_first)
    grad_out[...] = grad
    branch = grad.astype(LOW)
    branch_out[...] = branch
    mask = quarter_mask(line_at)
    mixed_grad = masked(product_right(branch, out_weight[...]).astype(LOW), mask)
    pieces = attend_tiles_back(qkv[...], mixed_grad, SPAN, head_allowed(heads[...]))
    tiles = SPAN // LANES
    for piece in range(3):
        joined = jnp.concatenate(pieces[piece * tiles : (piece + 1) * tiles], axis=1)
        proj_out[:, piece * SPAN : (piece + 1) * SPAN] = masked(joined, mask)
    part_out[...] = product_right(proj_out[...], weight[:, : 3 * SPAN])


def cls_end_kernel(where, *refs):
    heads, grad, own, got_one, got_two, got_three = refs[:6]
    square, sums_back, sums_top = refs[6:9]
    normed_second, inv_second, vectors = refs[9:12]
    row_out, second_out, shared_out, held = refs[12:]
    rank = where[0] * PLANE + where[1]
    total = grad[...] + own[...] + got_one[...] + got_two[...] + got_three[...]
    held[...] = total
    row = held[pl.ds(rank, 1), :]
    row_out[...] = row
    second_out[...] = norm_rows_back(
        row, normed_second[0:1, :], inv_second[0:1, :], vectors[6:7, :]
    )
    number = row_from_column(heads[:, 2 * MODEL + 2 : 2 * MODEL + 3], GROUP)
    entry = lax.broadcasted_iota(jnp.int32, (GROUP, GROUP), 0).astype(WIDE)
    hot = (entry == number).astype(WIDE)
    shared_out[0:GROUP, :] = jnp.dot(hot, total, precision=lax.Precision.HIGHEST)
    shared_out[GROUP : GROUP + 1, 0:LANES] = square[0:1, :]
    shared_out[GROUP + 1 : GROUP + 3, :] = sums_back[0:2, :]
    shared_out[GROUP + 3 : GROUP + 5, :] = sums_top[0:2, :]


def head_mlp_kernel(where, *refs):
    cls_mlp_kernel(where, *refs[:7], *refs[11:17])
    add_far_kernel(where, *refs[7:11], *refs[17:])


def head_end_kernel(where, *refs):
    cls_end_kernel(where, *refs[:12], *refs[16:19], refs[23])
    fold_kernel(where, *refs[12:16], *refs[19:23])


def attn_add_kernel(where, *refs):
    far_low, far_high, to_x, to_y, grad, own, got, x_out, y_out, input_out = refs
    add_far_kernel(where, far_low, far_high, to_x, to_y, x_out, y_out)
    input_out[...] = (grad[...] + own[...] + got[...]).astype(LOW)


def cls_rows_kernel(where, *refs):
    packs = refs[:4]
    heads, branch, low, second = refs[4:8]
    out, kept = refs[8:]
    line_at = where[0]
    rows, width = kept.shape[1:]
    for step, pack in enumerate(packs):
        first = pack.shape[0] - rows
        kept[(line_at + LINE - step) % LINE] = pack[first:, :width]
    starts = (MODEL, 2 * MODEL, 3 * MODEL, 4 * MODEL)
    out[:, 0:MODEL] = heads[:, :MODEL].astype(LOW)
    for piece, start in enumerate(starts):
        from_at = piece * SPAN
        for tile in range(MODEL // LANES):
            total = None
            for at in range(PLANE):
                inner = tile - TILE_START[at]
                if inner in (0, 1):
                    first = from_at + inner * LANES
                    value = kept[at, :, first : first + LANES]
                    total = value if total is None else total + value
            out[:, start + tile * LANES : start + (tile + 1) * LANES] = total
    out[:, 5 * MODEL : 6 * MODEL] = branch[...]
    out[:, 6 * MODEL : 7 * MODEL] = low[...]
    out[:, 7 * MODEL + FF : 8 * MODEL + FF] = second[...]
    part = FF // LINE
    for at in range(PLANE):
        first = 4 * SPAN
        out[:, 7 * MODEL + at * part : 7 * MODEL + (at + 1) * part] = kept[
            at, :, first : first + part
        ]
        out[:, 8 * MODEL + FF + at * part : 8 * MODEL + FF + (at + 1) * part] = kept[
            at, :, first + part : first + 2 * part
        ]


def own_features(rank, width):
    shape = (MODEL, width)
    feature = lax.broadcasted_iota(jnp.int32, shape, 0)
    column = lax.broadcasted_iota(jnp.int32, shape, 1)
    return (feature == rank * width + column).astype(LOW)


def own_vector(rank, pieces, out, flat):
    size = out.shape[0]
    for at, piece in enumerate(pieces):
        flat[:, at * MODEL : (at + 1) * MODEL] = piece
    value = jnp.zeros((1, size), WIDE)
    for chip in range(GROUP):
        value = jnp.where(rank == chip, flat[:, chip * size : (chip + 1) * size], value)
    out[...] = value.reshape(size)


def cls_owner_kernel(where, *refs):
    own, got, shared, mats_out, vec_out, rows, flat = refs
    rank = where[0] * PLANE + where[1]
    width = mats_out.shape[0]
    rows[:GROUP] = own[...]
    rows[GROUP:] = got[...]
    chosen = own_features(rank, width)
    plan = (
        (0, MODEL, 3 * MODEL, 0),
        (4 * MODEL, 5 * MODEL, MODEL, 3 * MODEL),
        (6 * MODEL, 7 * MODEL, FF, 4 * MODEL),
        (7 * MODEL + FF, 8 * MODEL + FF, FF, 4 * MODEL + FF),
    )
    for left, right, size, target in plan:
        side = product_plain(rows[:, left : left + MODEL], chosen).astype(LOW)
        mats_out[:, target : target + size] = product_left(side, rows[:, right : right + size])
    starts = (MODEL, 3 * MODEL, 5 * MODEL, 7 * MODEL + FF)
    pieces = [column_sum(rows[:, start : start + MODEL]) for start in starts]
    pieces += [shared[GROUP + 1 + at : GROUP + 2 + at, :] for at in range(4)]
    starts = [7 * MODEL + at * MODEL for at in range(FF // MODEL)]
    pieces += [column_sum(rows[:, start : start + MODEL]) for start in starts]
    own_vector(rank, pieces, vec_out, flat)


def head_share_kernel(where, *refs):
    packs, mlp = refs[:4], refs[4]
    mine_out, vecs_out, rows = refs[5:]
    rank = where[0] * PLANE + where[1]
    count = LINE * 24
    for at, pack in enumerate(packs):
        rows[at * count : (at + 1) * count] = pack[...]
    total = PLANE * count

    def chosen(base, apart):
        shape = (CORES * GROUP, total)
        row = lax.broadcasted_iota(jnp.int32, shape, 0)
        column = lax.broadcasted_iota(jnp.int32, shape, 1)
        hot = (column == row // 2 * 24 + base + row % 2 * apart).astype(LOW)
        return product_plain(hot, rows[...]).astype(LOW)

    own = own_features(rank, OWN)
    for at, (left, right) in enumerate(((0, 4), (2, 8))):
        side = product_plain(chosen(left, 1), own).astype(LOW)
        for piece in range(FF_HALF // MODEL):
            columns = slice(at * FF_HALF + piece * MODEL, at * FF_HALF + (piece + 1) * MODEL)
            share = product_left(side, chosen(right + 2 * piece, 1))
            mine_out[:, columns] = mlp[:, columns] + share
    shape = (16, total)
    row = lax.broadcasted_iota(jnp.int32, shape, 0)
    column = lax.broadcasted_iota(jnp.int32, shape, 1)
    hot = ((column % 24 == row + 12) & (row < 12)).astype(LOW)
    vecs_out[...] = product_plain(hot, rows[...])


def share_owner_kernel(where, *refs):
    head_share_kernel(where, *refs[:5], *refs[9:11], refs[15])
    cls_owner_kernel(where, *refs[5:8], *refs[11:13], *refs[16:])
    shared, count, pos_out, loss_out = refs[7], refs[8], refs[13], refs[14]
    pos_out[...] = shared[:GROUP, :]
    loss_out[...] = shared[GROUP : GROUP + 1, 0:1] / (count[0:1, 0:1] * MODEL)


def seg_vec_kernel(where, vecs, vecs_got, vec_out, flat):
    rank = where[0] * PLANE + where[1]
    rows = (8 * MODEL + FF) // MODEL
    pieces = [vecs[at : at + 1, :] + vecs_got[at : at + 1, :] for at in range(rows)]
    own_vector(rank, pieces, vec_out, flat)


def column_copies(where, out, base, size, own, got, first):
    core_at = where[2]
    lanes = slice(first, first + size)
    return [
        (own.at[:, lanes], out.at[:, pl.ds(aligned(base + core_at * size), size)]),
        (got.at[:, lanes], out.at[:, pl.ds(aligned(base + (1 - core_at) * size), size)]),
    ]


def store_kernel(where, attn, attn_got, mlp, mlp_got, vecs, vecs_got, out, vec_out, flat, sems):
    pairs = []
    for piece in range(4):
        pairs += column_copies(where, out, piece * MODEL, HALF, attn, attn_got, piece * HALF)
    for piece in range(2):
        base = 4 * MODEL + piece * FF
        pairs += column_copies(where, out, base, FF_HALF, mlp, mlp_got, piece * FF_HALF)
    copies = [
        pltpu.make_async_copy(source, target, sems.at[at])
        for at, (source, target) in enumerate(pairs)
    ]
    for copy in copies:
        copy.start()
    seg_vec_kernel(where, vecs, vecs_got, vec_out, flat)
    wait_all(copies)


def plane_parts(part):
    return (part,) + together(*(in_plane(part, mask) for mask in range(1, PLANE)))


def line_parts(part):
    return (part,) + together(*(along_line(part, apart) for apart in range(1, LINE)))


def slice_local(
    hidden_in,
    targets,
    doc_ids,
    seg_nums,
    valid_flags,
    seg_mats,
    seg_vecs,
    cls_mats,
    cls_vecs,
    seg_pos,
):
    rank, core_at = lax.axis_index("fsdp"), lax.axis_index("rep")
    line_at, plane_at = rank // PLANE, rank % PLANE
    where = jnp.stack([line_at, plane_at, core_at, doc_ids[0], seg_nums[0]]).astype(jnp.int32)
    own_rows, total_columns = seg_mats.shape
    vec_size = seg_vecs.shape[0]
    both_rows = CORES * SEG

    first_piece, live_row, *rest = run_kernel(
        prepare_kernel,
        "prepare",
        [shape_of((own_rows, FIRST), LOW), shape_of((1, SEG))]
        + [shape_of((own_rows, FF_HALF), LOW)] * 2
        + [shape_of((own_rows, QUARTER_HALF), LOW)] * LINE
        + [shape_of((own_rows, HALF), LOW), shape_of((MODEL, PLANE * SPAN), LOW)],
        where,
        (seg_mats, cls_mats),
        (jnp.stack([seg_vecs, cls_vecs]).astype(WIDE), valid_flags[None]),
        [
            pltpu.SemaphoreType.DMA((4,)),
            pltpu.VMEM((LINE, own_rows, QUARTER), LOW),
            pltpu.SemaphoreType.DMA((3 + 5 * LINE,)),
        ],
    )
    first_line = line_parts(first_piece)
    second_piece, third_piece, quarters, cls_out_piece, order = (
        rest[0],
        rest[1],
        rest[2:-2],
        rest[-2],
        rest[-1],
    )

    def joined(*pieces):
        return jnp.concatenate(pieces, axis=1)

    def sent_both(to_x, to_y):
        to_x, to_y = together(to_x, to_y)
        return together(in_plane(to_x, 1), in_plane(to_y, 2))

    own_sent = joined(first_piece, second_piece, third_piece)
    own_x, own_y = sent_both(own_sent, own_sent)
    first_line = first_line[:1] + tuple(after(got, own_x, own_y) for got in first_line[1:])
    to_x = joined(own_y[:, OWN_CUT:], *first_line[1:])
    to_y = joined(own_x[:, :OWN_CUT], *first_line[1:])
    first_x, first_y = sent_both(to_x, to_y)
    hidden_got = other_core(after(hidden_in, to_x, to_y))
    live_got = other_core(after(live_row, to_x, to_y))
    second_line = line_parts(after(second_piece, hidden_got, live_got, to_x, to_y))

    def halves(group, from_x, from_y):
        width, cut = WIDTHS[group], LINE_CUTS[group]
        if group == 0:
            base_x, base_y = sum(WIDTHS) - OWN_CUT, OWN_CUT
        else:
            before, before_cut = WIDTHS[group - 1], LINE_CUTS[group - 1]
            base_x, base_y = 2 * before - before_cut, before + before_cut
        return (
            from_y[:, base_y + width + cut : base_y + 3 * width],
            from_x[:, base_x : base_x + width + cut],
        )

    high, low = halves(0, first_x, first_y)
    to_x, to_y = joined(high, *second_line[1:]), joined(low, *second_line[1:])
    second_x, second_y = sent_both(to_x, to_y)
    third_line = line_parts(after(third_piece, to_x, to_y))
    high, low = halves(1, second_x, second_y)
    to_x, to_y = joined(high, *third_line[1:]), joined(low, *third_line[1:])
    third_x, third_y = sent_both(to_x, to_y)
    own_parts = (own_x, own_y, first_x, first_y)
    cls_line = (quarters[0],) + tuple(
        along_line(after(quarters[apart], to_x, to_y), apart)
        for apart in range(1, LINE)
    )

    qkv_weight, out_low, out_high, qkv, mixed, vectors, count, hidden_ordered = run_kernel(
        qkv_kernel,
        "seg_qkv",
        [
            shape_of((GROUP, own_rows, 3 * HALF), LOW),
            shape_of((GROUP // 2, own_rows, HALF), LOW),
            shape_of((GROUP // 2, own_rows, HALF), LOW),
            shape_of((both_rows, 3 * HALF), LOW),
            shape_of((both_rows, HALF), LOW),
            shape_of((2 * (8 * MODEL + FF) // MODEL, MODEL)),
            shape_of((8, LANES)),
            shape_of((both_rows, PLANE * SPAN), LOW),
        ],
        where,
        (),
        first_line
        + own_parts
        + (first_x, first_y, second_x, second_y)
        + (hidden_in, hidden_got, live_row, live_got, order),
        [
            pltpu.VMEM((GROUP, own_rows, LANES), LOW),
            pltpu.VMEM((2, 8 * MODEL + FF), WIDE),
            pltpu.VMEM((both_rows, MODEL), LOW),
            pltpu.VMEM((GROUP, own_rows, HALF), LOW),
        ],
        flops=2 * SEG * MODEL * 3 * MODEL,
    )
    out_weight, mixed_ordered, normed_first, inv_first, first_low = run_kernel(
        out_kernel,
        "seg_out",
        [
            shape_of((MODEL, MODEL), LOW),
            shape_of((both_rows, PLANE * SPAN), LOW),
            shape_of((SEG, MODEL)),
            shape_of((SEG, 1)),
            shape_of((SEG, MODEL), LOW),
        ],
        where,
        (),
        (
            hidden_in,
            mixed,
            after(other_core(mixed), third_x, third_y),
            out_low,
            out_high,
            other_core(out_low),
            other_core(out_high),
            vectors,
            order,
        ),
        [pltpu.VMEM((both_rows, MODEL), LOW)],
        flops=2 * SEG * MODEL * MODEL,
    )
    fourth_x, fourth_y = sent_both(*halves(2, third_x, third_y))
    first_got = after(other_core(first_low), fourth_x, fourth_y)
    count = count + other_core(after(count, first_got))
    up_weight, act, slope = run_kernel(
        up_kernel,
        "seg_up",
        [
            shape_of((GROUP, own_rows, FF_HALF), LOW),
            shape_of((both_rows, FF_HALF), LOW),
            shape_of((both_rows, FF_HALF)),
        ],
        where,
        (),
        second_line
        + own_parts
        + (second_x, second_y, third_x, third_y)
        + (first_low, first_got, vectors),
        [pltpu.VMEM((both_rows, MODEL), LOW)],
        flops=2 * SEG * MODEL * FF,
    )
    cls_sent = joined(*cls_line, cls_out_piece)
    cls_sent = after(cls_sent, act)
    cls_x, cls_y = sent_both(cls_sent, cls_sent)
    down_weight, down_own, down_send = run_kernel(
        down_kernel,
        "seg_down",
        [
            shape_of((GROUP, own_rows, FF_HALF), LOW),
            shape_of((SEG, MODEL)),
            shape_of((SEG, MODEL)),
        ],
        where,
        (),
        third_line + own_parts + (third_x, third_y, fourth_x, fourth_y) + (act,),
        flops=2 * SEG * MODEL * FF,
    )
    normed_second, inv_second, diff, out_rows, head_row = run_kernel(
        seg_rows_kernel,
        "seg_rows",
        [
            shape_of((SEG, MODEL)),
            shape_of((SEG, 1)),
            shape_of((SEG, MODEL)),
            shape_of((SEG, MODEL)),
            shape_of((1, 2 * MODEL + LANES)),
        ],
        where,
        (),
        (
            down_own,
            other_core(down_send),
            normed_first,
            vectors,
            targets,
            live_row,
            seg_pos,
        ),
    )
    head_planes = plane_parts(head_row)
    head_lines = line_parts(jnp.concatenate(head_planes))
    size = LINE // 2 * QUARTER_HALF
    cls_far = sent_both(
        after(cls_y[:, size:], head_lines[3]), after(cls_x[:, :size], head_lines[3])
    )

    second_grad, second_low, second_sums = run_kernel(
        second_norm_kernel,
        "seg_second_norm",
        [shape_of((SEG, MODEL)), shape_of((SEG, MODEL), LOW), shape_of((3, MODEL))],
        where,
        (),
        (diff, count, normed_second, inv_second, vectors),
    )
    second_got = other_core(second_low)
    pre, first_grad_own, first_grad_send, up_sums = run_kernel(
        mlp_back_kernel,
        "seg_mlp_back",
        [
            shape_of((both_rows, FF_HALF), LOW),
            shape_of((SEG, MODEL)),
            shape_of((SEG, MODEL)),
            shape_of((FF_HALF // MODEL, MODEL)),
        ],
        where,
        (),
        (second_low, second_got, down_weight, up_weight, slope),
        [pltpu.VMEM((both_rows, MODEL), LOW)],
        flops=4 * SEG * MODEL * FF,
    )
    first_grad_got = other_core(first_grad_send)

    def part_shapes(columns):
        return [
            shape_of((count_of, own_rows, columns), LOW)
            for count_of in (LINE // 2, LINE // 2, LINE, LINE, LINE)
        ]

    head_lines = head_lines[:1] + together(*(after(got, pre) for got in head_lines[1:]))
    cls_far = together(*(after(got, *head_lines[1:]) for got in cls_far))
    cls_half, cls_out_half = run_kernel(
        cls_gather_kernel,
        "head_gather",
        [
            shape_of((GROUP, own_rows, QUARTER_HALF), LOW),
            shape_of((PLANE, own_rows, HALF), LOW),
        ],
        where,
        (),
        cls_line + (cls_x, cls_y) + cls_far + (cls_out_piece,),
    )
    mlp_parts = run_kernel(
        mlp_weight_kernel,
        "seg_mlp_weight",
        part_shapes(FF),
        where,
        (),
        (first_low, first_got, second_low, second_got, after(pre, cls_half), act),
        [
            pltpu.VMEM((both_rows, MODEL), LOW),
            pltpu.VMEM((GROUP, own_rows, FF), LOW),
            pltpu.SemaphoreType.DMA((GROUP,)),
        ],
        far=range(5),
        flops=4 * SEG * MODEL * FF,
    )
    mlp_far = reduce_far(tuple(after(part, *cls_far) for part in mlp_parts[:2]))
    cls_weight, cls_out = run_kernel(
        cls_weight_kernel,
        "head_weight",
        [
            shape_of((GROUP, own_rows, QUARTER), LOW),
            shape_of((4, HEAD_DIM, MODEL), LOW),
        ],
        where,
        (),
        (cls_half, other_core(cls_half), cls_out_half, other_core(cls_out_half)),
    )
    cls_weight = cls_weight.reshape(MODEL, QUARTER)
    cls_out = cls_out.reshape(SPAN, MODEL)
    heads, cls_qkv, cls_mixed, part = run_kernel(
        cls_attend_kernel,
        "head_attend",
        [
            shape_of((GROUP, 2 * MODEL + LANES)),
            shape_of((GROUP, 3 * SPAN), LOW),
            shape_of((GROUP, SPAN), LOW),
            shape_of((GROUP, MODEL)),
        ],
        where,
        (),
        tuple(after(got, mlp_parts[0], first_grad_got) for got in head_lines)
        + (vectors, cls_weight, cls_out),
    )
    cls_normed, cls_inv, cls_low, cls_act, cls_slope, part, *mlp_sent = run_kernel(
        head_mlp_kernel,
        "head_mlp",
        [
            shape_of((GROUP, MODEL)),
            shape_of((GROUP, 1)),
            shape_of((GROUP, MODEL), LOW),
            shape_of((GROUP, FF // LINE), LOW),
            shape_of((GROUP, FF // LINE)),
            shape_of((GROUP, MODEL)),
            shape_of(mlp_parts[2].shape, LOW),
            shape_of(mlp_parts[2].shape, LOW),
        ],
        where,
        (),
        (heads,) + line_parts(part) + (vectors, cls_weight) + mlp_far + tuple(mlp_parts[2:4]),
    )
    mlp_plane = sent_both(*mlp_sent)
    cls_parts = line_parts(part)
    top_row, square, cls_grad, cls_second, cls_pre, part, top_sums = run_kernel(
        cls_top_kernel,
        "head_top",
        [
            shape_of((1, MODEL)),
            shape_of((8, LANES)),
            shape_of((GROUP, MODEL)),
            shape_of((GROUP, MODEL), LOW),
            shape_of((GROUP, FF // LINE), LOW),
            shape_of((GROUP, MODEL)),
            shape_of((2, MODEL)),
        ],
        where,
        (),
        (heads,)
        + cls_parts
        + (vectors, cls_weight, cls_normed, count, cls_slope),
        [pltpu.VMEM((GROUP, MODEL), WIDE)],
    )
    top_parts = line_parts(part)
    cls_grad, cls_branch, cls_proj, part, back_sums = run_kernel(
        cls_attend_back_kernel,
        "head_attend_back",
        [
            shape_of((GROUP, MODEL)),
            shape_of((GROUP, MODEL), LOW),
            shape_of((GROUP, 3 * SPAN), LOW),
            shape_of((GROUP, MODEL)),
            shape_of((2, MODEL)),
        ],
        where,
        (),
        (heads,)
        + top_parts
        + (vectors, cls_weight, cls_out, cls_grad, cls_normed, cls_inv, cls_qkv),
    )
    end_parts = line_parts(part)
    pack = jnp.concatenate([cls_proj, cls_mixed, cls_pre, cls_act], axis=1)
    folded = [shape_of((own_rows, FF))] + [shape_of((own_rows + GROUP, FF), LOW)] * (LINE - 1)
    dheads, head_grad, shared, mlp_own, *mlp_sent = run_kernel(
        head_end_kernel,
        "head_end",
        [shape_of((1, MODEL)), shape_of((1, MODEL)), shape_of((GROUP + 8, MODEL))] + folded,
        where,
        (),
        (heads, cls_grad)
        + end_parts
        + (square, back_sums, top_sums, normed_second, inv_second, vectors)
        + (mlp_parts[4],)
        + mlp_plane
        + (pack,),
        [pltpu.VMEM((GROUP, MODEL), WIDE)],
    )
    got_three, got_two = along_line(mlp_sent[2], 3), along_line(mlp_sent[1], 2)
    mlp_last = mlp_sent[0]
    mlp_got = [None, got_two, got_three]

    head_own, head_send, head_data = run_kernel(
        head_back_kernel,
        "seg_head_back",
        [shape_of((1, MODEL)), shape_of((1, MODEL)), shape_of((12, MODEL))],
        where,
        (),
        (
            head_grad,
            other_core(head_grad),
            down_weight,
            up_weight,
            slope,
            act,
            first_low,
            first_got,
        ),
    )
    grad_summed, branch, mixed_grad, attn_send, first_sums = run_kernel(
        first_norm_kernel,
        "seg_first_norm",
        [
            shape_of((SEG, MODEL)),
            shape_of((SEG, MODEL), LOW),
            shape_of((SEG, MODEL), LOW),
            shape_of((SEG, MODEL), LOW),
            shape_of((3, MODEL)),
        ],
        where,
        (),
        (
            second_grad,
            first_grad_own,
            first_grad_got,
            head_grad,
            head_own,
            other_core(head_send),
            normed_first,
            inv_first,
            vectors,
            out_weight,
        ),
    )
    attn_got = other_core(attn_send)
    proj, input_own, input_send, payload = run_kernel(
        attn_back_kernel,
        "seg_attn_back",
        [
            shape_of((both_rows, 3 * HALF), LOW),
            shape_of((SEG, MODEL)),
            shape_of((SEG, MODEL)),
            shape_of((24, MODEL), LOW),
        ],
        where,
        (),
        (
            qkv,
            mixed_grad,
            attn_got,
            live_row,
            live_got,
            qkv_weight,
            first_sums,
            second_sums,
            up_sums,
            dheads,
            normed_second,
            head_data,
        ),
        [pltpu.VMEM((24, MODEL), WIDE)],
        flops=4 * SEG * MODEL * 3 * MODEL,
    )
    attn_data = (hidden_ordered, mixed_ordered, proj, branch, attn_got)
    attn_far = run_kernel(
        attn_far_kernel,
        "seg_attn_far",
        part_shapes(4 * HALF)[:2],
        where,
        (),
        attn_data,
        flops=SEG * MODEL * 2 * MODEL,
    )
    attn_far = reduce_far(tuple(after(part, mlp_got[-1]) for part in attn_far))
    attn_near = run_kernel(
        attn_near_kernel,
        "seg_attn_near",
        part_shapes(4 * HALF)[2:] + [shape_of((SEG, MODEL), LOW)],
        where,
        (),
        attn_data + (top_row, out_rows, live_row),
        flops=3 * SEG * MODEL * 2 * MODEL,
    )
    output = attn_near[3]
    *attn_sent, input_grad = run_kernel(
        attn_add_kernel,
        "seg_attn_add",
        [shape_of(attn_near[0].shape, LOW)] * 2 + [shape_of((SEG, MODEL), LOW)],
        where,
        (),
        attn_far
        + tuple(attn_near[:2])
        + (after(grad_summed, got_two), input_own, other_core(input_send)),
    )
    attn_plane = sent_both(*attn_sent)
    payload_parts = line_parts(after(payload, *attn_sent))
    mlp_got[0] = along_line(after(mlp_last, *payload_parts[1:]), 1)
    mlp_got = [after(got, attn_plane[0]) for got in mlp_got]
    mlp_sum = reduce_line(mlp_own, mlp_got)
    shared = shared + other_core(after(shared, attn_sent[0]))
    row_width = 8 * MODEL + 2 * FF
    cls_rows = run_kernel(
        cls_rows_kernel,
        "head_rows",
        [shape_of((GROUP, row_width), LOW)],
        where,
        (),
        (pack,) + tuple(mlp_got) + (heads, cls_branch, cls_low, cls_second),
        [pltpu.VMEM((LINE,) + pack.shape, LOW)],
    )[0]
    cls_got = other_core(cls_rows)
    attn_plane = tuple(after(got, cls_got, output, input_grad, shared) for got in attn_plane)
    attn_own, *attn_sent = reduce_fold(where, attn_near[2], attn_plane)
    attn_lines = list(
        together(*(along_line(attn_sent[apart - 1], apart) for apart in range(1, LINE)))
    )
    flat = pltpu.VMEM((1, 8 * MODEL + FF), WIDE)
    payload_line = jnp.concatenate(payload_parts)
    mlp_mine, own_vecs, cls_mats_grad, cls_vec_grad, pos_total, loss_value = run_kernel(
        share_owner_kernel,
        "head_owner",
        [
            shape_of((own_rows, FF)),
            shape_of((16, MODEL)),
            shape_of((own_rows, total_columns)),
            shape_of((vec_size,)),
            shape_of((GROUP, MODEL)),
            shape_of((1, 1)),
        ],
        where,
        (),
        tuple(after(got, attn_own) for got in plane_parts(after(payload_line, *attn_plane)))
        + (mlp_sum, cls_rows, cls_got, shared, count),
        [
            pltpu.VMEM((GROUP * 24, MODEL), LOW),
            pltpu.VMEM((CORES * GROUP, row_width), LOW),
            flat,
        ],
        flops=64 * own_rows * total_columns,
    )
    loss_value = loss_value.reshape(())
    attn_lines = together(*(after(got, mlp_mine) for got in attn_lines))
    attn_sum = reduce_line(attn_own, attn_lines)
    seg_mats_grad, seg_vec_grad = run_kernel(
        store_kernel,
        "seg_owner",
        [shape_of((own_rows, total_columns)), shape_of((vec_size,))],
        where,
        (),
        (attn_sum, other_core(attn_sum), mlp_mine, other_core(mlp_mine))
        + (own_vecs, other_core(own_vecs)),
        [flat, pltpu.SemaphoreType.DMA((12,))],
        far=(0,),
    )

    return (
        output,
        input_grad,
        seg_mats_grad,
        seg_vec_grad,
        cls_mats_grad,
        cls_vec_grad,
        pos_total,
        loss_value,
    )


def solution(mesh):
    in_specs = (
        P(("rep", "fsdp"), None),
        P(("rep", "fsdp"), None),
        P(("rep", "fsdp")),
        P(("rep", "fsdp")),
        P(("rep", "fsdp")),
        P("fsdp", None),
        P("fsdp"),
        P("fsdp", None),
        P("fsdp"),
        P(),
    )
    out_specs = (
        P(("rep", "fsdp"), None),
        P(("rep", "fsdp"), None),
        P("fsdp", None),
        P("fsdp"),
        P("fsdp", None),
        P("fsdp"),
        P(),
        P(),
    )
    one_slice = dict(mesh.shape) == {"rep": CORES, "fsdp": LINE * PLANE}
    body = slice_local if one_slice else local
    return jax.shard_map(body, mesh=mesh, in_specs=in_specs, out_specs=out_specs, check_vma=False)
```

```python
import math

import jax
import jax.numpy as jnp
from jax import lax
from jax.experimental import pallas as pl
from jax.experimental.pallas import tpu as pltpu
from jax.sharding import PartitionSpec as P

HEADS = 12
HEAD_DIM = 64
FF = 3072
SEG = 128
SEQ = 2048


NORM_EPS = 1e-05
MASK_FILL = -1e30
SQRT_HALF = 0.7071067811865476
INV_SQRT_TWO_PI = 0.3989422804014327


def swapped(value, axis, apart):
    mask = 2**apart
    pairs = [(source, source ^ mask) for source in range(lax.axis_size(axis))]
    return lax.ppermute(value, axis, pairs)


def product_plain(left_side, right_side):
    return jnp.dot(left_side, right_side, preferred_element_type=jnp.float32)


def product_left(left_side, right_side):
    return lax.dot_general(
        left_side, right_side, (((0,), (0,)), ((), ())), preferred_element_type=jnp.float32
    )


def product_right(left_side, right_side):
    return lax.dot_general(
        left_side, right_side, (((1,), (1,)), ((), ())), preferred_element_type=jnp.float32
    )


def row_total(array_in):
    return jnp.sum(array_in.astype(jnp.float32), axis=0)


def unpack_weights(gathered, model_width, ff_width):
    matrix, vector = gathered
    vector = vector.astype(jnp.float32)
    pieces = tuple(
        (vector[offset * model_width : (offset + 1) * model_width] for offset in range(8))
    )
    return (
        (
            matrix[:, : 3 * model_width],
            matrix[:, 3 * model_width : 4 * model_width],
            matrix[:, 4 * model_width : 4 * model_width + ff_width],
            matrix[:, 4 * model_width + ff_width :],
        )
        + pieces
        + (vector[8 * model_width :],)
    )


def norm_forward(summed, gain_vec, shift_vec):
    row_mean = jnp.mean(summed, axis=-1, keepdims=True)
    centered = summed - row_mean
    inv_dev = lax.rsqrt(jnp.mean(centered * centered, axis=-1, keepdims=True) + NORM_EPS)
    normed = centered * inv_dev
    return (normed * gain_vec + shift_vec, normed, inv_dev)


def norm_backward(grad_out, normed, inv_dev, gain_vec):
    scaled = grad_out * gain_vec
    mean_one = jnp.mean(scaled, axis=-1, keepdims=True)
    mean_two = jnp.mean(scaled * normed, axis=-1, keepdims=True)
    grad_in = inv_dev * (scaled - mean_one - normed * mean_two)
    return (grad_in, jnp.sum(grad_out * normed, axis=0), jnp.sum(grad_out, axis=0))


def gelu_value(before):
    return 0.5 * before * (1.0 + lax.erf(before * SQRT_HALF))


def gelu_slope(before):
    return (
        0.5 * (1.0 + lax.erf(before * SQRT_HALF))
        + before * jnp.exp(-0.5 * before * before) * INV_SQRT_TWO_PI
    )


def attention_scores(queries, keys_in, allowed, score_scale):
    raw_scores = (
        jnp.einsum("bqhe,bkhe->bhqk", queries, keys_in, preferred_element_type=jnp.float32)
        * score_scale
    )
    return jnp.where(allowed, raw_scores, MASK_FILL)


def attention_forward(queries, keys_in, values, allowed, score_scale):
    scores = attention_scores(queries, keys_in, allowed, score_scale)
    row_top = jnp.max(scores, axis=-1, keepdims=True)
    log_total = row_top + jnp.log(jnp.sum(jnp.exp(scores - row_top), axis=-1, keepdims=True))
    weights = jnp.exp(scores - log_total).astype(jnp.bfloat16)
    mixed_rows = jnp.einsum("bhqk,bkhe->bqhe", weights, values, preferred_element_type=jnp.float32)
    return (mixed_rows, log_total)


def attention_backward(queries, keys_in, values, allowed, score_scale, log_total, grad_mixed):
    probabilities = jnp.exp(attention_scores(queries, keys_in, allowed, score_scale) - log_total)
    grad_probs = jnp.einsum(
        "bqhe,bkhe->bhqk", grad_mixed, values, preferred_element_type=jnp.float32
    )
    inner_sum = jnp.sum(grad_probs * probabilities, axis=-1, keepdims=True)
    grad_scores = (probabilities * (grad_probs - inner_sum)).astype(jnp.bfloat16)
    grad_query = (
        jnp.einsum("bhqk,bkhe->bqhe", grad_scores, keys_in, preferred_element_type=jnp.float32)
        * score_scale
    )
    grad_key = (
        jnp.einsum("bhqk,bqhe->bkhe", grad_scores, queries, preferred_element_type=jnp.float32)
        * score_scale
    )
    grad_value = jnp.einsum(
        "bhqk,bqhe->bkhe",
        probabilities.astype(jnp.bfloat16),
        grad_mixed,
        preferred_element_type=jnp.float32,
    )
    return (grad_query, grad_key, grad_value)


def block_forward(rows_in, unpacked, attend):
    (
        qkv_weight,
        out_weight,
        up_weight,
        down_weight,
        query_bias,
        value_bias,
        out_bias,
        down_bias,
        gain_first,
        shift_first,
        gain_second,
        shift_second,
        up_bias,
    ) = unpacked
    model_width = rows_in.shape[1]
    inputs = rows_in.astype(jnp.bfloat16)
    projected = product_plain(inputs, qkv_weight)
    queries = (projected[:, :model_width] + query_bias).astype(jnp.bfloat16)
    keys_in = projected[:, model_width : 2 * model_width].astype(jnp.bfloat16)
    values = (projected[:, 2 * model_width :] + value_bias).astype(jnp.bfloat16)
    mixed_rows, attend_kept = attend(queries, keys_in, values)
    mixed_rows = mixed_rows.astype(jnp.bfloat16)
    summed_first = rows_in + product_plain(mixed_rows, out_weight) + out_bias
    first_out, normed_first, inv_first = norm_forward(summed_first, gain_first, shift_first)
    first_low = first_out.astype(jnp.bfloat16)
    pre_act = product_plain(first_low, up_weight) + up_bias
    activated = gelu_value(pre_act).astype(jnp.bfloat16)
    summed_second = first_out + product_right(activated, down_weight) + down_bias
    block_out, normed_second, inv_second = norm_forward(summed_second, gain_second, shift_second)
    saved_state = (
        inputs,
        queries,
        keys_in,
        values,
        attend_kept,
        mixed_rows,
        normed_first,
        inv_first,
        first_low,
        pre_act,
        activated,
        normed_second,
        inv_second,
    )
    return (block_out, saved_state)


def block_backward(grad_out, unpacked, saved_state, attend_back):
    (
        qkv_weight,
        out_weight,
        up_weight,
        down_weight,
        query_bias,
        value_bias,
        out_bias,
        down_bias,
        gain_first,
        shift_first,
        gain_second,
        shift_second,
        up_bias,
    ) = unpacked
    (
        inputs,
        queries,
        keys_in,
        values,
        attend_kept,
        mixed_rows,
        normed_first,
        inv_first,
        first_low,
        pre_act,
        activated,
        normed_second,
        inv_second,
    ) = saved_state
    grad_second, grad_gain_second, grad_shift_second = norm_backward(
        grad_out, normed_second, inv_second, gain_second
    )
    second_low = grad_second.astype(jnp.bfloat16)
    grad_pre = (product_plain(second_low, down_weight) * gelu_slope(pre_act)).astype(jnp.bfloat16)
    grad_first = grad_second + product_right(grad_pre, up_weight)
    grad_summed, grad_gain_first, grad_shift_first = norm_backward(
        grad_first, normed_first, inv_first, gain_first
    )
    branch_low = grad_summed.astype(jnp.bfloat16)
    grad_mixed = product_right(branch_low, out_weight).astype(jnp.bfloat16)
    grad_query, grad_key, grad_value = attend_back(
        queries, keys_in, values, attend_kept, grad_mixed
    )
    grad_proj = jnp.concatenate([grad_query, grad_key, grad_value], axis=1)
    grad_rows = grad_summed + product_right(grad_proj, qkv_weight)
    vector_grad = jnp.concatenate(
        [
            row_total(grad_query),
            row_total(grad_value),
            row_total(branch_low),
            row_total(second_low),
            grad_gain_first,
            grad_shift_first,
            grad_gain_second,
            grad_shift_second,
            row_total(grad_pre),
        ]
    )
    weight_rows = (
        inputs,
        grad_proj,
        mixed_rows,
        branch_low,
        first_low,
        grad_pre,
        second_low,
        activated,
    )
    return (grad_rows, weight_rows, vector_grad)


def weight_products(weight_rows):
    inputs, grad_proj, mixed_rows, branch_low, first_low, grad_pre, second_low, activated = (
        weight_rows
    )
    return (
        product_left(inputs, grad_proj),
        product_left(mixed_rows, branch_low),
        product_left(first_low, grad_pre),
        product_left(second_low, activated),
    )


def local(
    hidden_in,
    targets,
    doc_ids,
    seg_nums,
    valid_flags,
    seg_mats,
    seg_vecs,
    cls_mats,
    cls_vecs,
    seg_pos,
):
    tok_rows, model_width = hidden_in.shape
    ff_width = FF
    seg_len = SEG
    group_span = SEQ // tok_rows
    seg_count = tok_rows // seg_len
    score_scale = HEAD_DIM ** (-0.5)
    head_shape = (HEADS, HEAD_DIM)
    live_rows = valid_flags.astype(jnp.float32)
    rank_full = lax.axis_index("fsdp")
    seg_gathered = (
        lax.all_gather(seg_mats, "fsdp", axis=0, tiled=True),
        lax.all_gather(seg_vecs, "fsdp", axis=0, tiled=True),
    )
    seg_unpacked = unpack_weights(seg_gathered, model_width, ff_width)
    cls_gathered = (
        lax.all_gather(cls_mats, "fsdp", axis=0, tiled=True),
        lax.all_gather(cls_vecs, "fsdp", axis=0, tiled=True),
    )
    cls_unpacked = unpack_weights(cls_gathered, model_width, ff_width)
    seg_allowed = (live_rows.reshape(seg_count, 1, 1, seg_len) > 0.5) | jnp.eye(seg_len, dtype=bool)
    seg_shape = (seg_count, seg_len) + head_shape

    def seg_attend(queries, keys_in, values):
        mixed_rows, log_total = attention_forward(
            queries.reshape(seg_shape),
            keys_in.reshape(seg_shape),
            values.reshape(seg_shape),
            seg_allowed,
            score_scale,
        )
        return (mixed_rows.reshape(tok_rows, model_width), log_total)

    def seg_attend_back(queries, keys_in, values, log_total, grad_mixed):
        grad_parts = attention_backward(
            queries.reshape(seg_shape),
            keys_in.reshape(seg_shape),
            values.reshape(seg_shape),
            seg_allowed,
            score_scale,
            log_total,
            grad_mixed.reshape(seg_shape),
        )
        return tuple(
            (
                grad_part.reshape(tok_rows, model_width).astype(jnp.bfloat16)
                for grad_part in grad_parts
            )
        )

    first_out, seg_saved = block_forward(hidden_in.astype(jnp.float32), seg_unpacked, seg_attend)
    first_grid = first_out.reshape(seg_count, seg_len, model_width)
    position_hot = (seg_nums[:, None] == jnp.arange(seg_pos.shape[0])[None, :]).astype(jnp.float32)
    position_rows = jnp.sum(
        position_hot[:, :, None] * seg_pos.astype(jnp.float32)[None, :, :], axis=1
    )
    heads_in = first_grid[:, 0, :] + position_rows
    lead_live = live_rows.reshape(seg_count, seg_len)[:, 0]
    lead_doc = doc_ids.reshape(seg_count, seg_len)[:, 0]
    lead_labels = jnp.where(lead_live > 0.5, lead_doc, -1).astype(jnp.bfloat16)
    lead_doc_low = lead_doc.astype(jnp.bfloat16)
    bit_count = group_span.bit_length() - 1
    key_total = group_span * seg_count
    own_slot = rank_full % group_span * seg_count + jnp.arange(seg_count)
    query_shape = (1, seg_count) + head_shape
    key_shape = (1, key_total) + head_shape

    def cls_attend(queries, keys_in, values):
        paired = jnp.concatenate([keys_in, values], axis=1)
        labels = lead_labels
        for bit_level in range(bit_count):
            other_pair, other_labels = swapped((paired, labels), "fsdp", bit_level)
            upper_half = rank_full // (1 << bit_level) % 2 == 1
            paired = jnp.where(
                upper_half,
                jnp.concatenate([other_pair, paired]),
                jnp.concatenate([paired, other_pair]),
            )
            labels = jnp.where(
                upper_half,
                jnp.concatenate([other_labels, labels]),
                jnp.concatenate([labels, other_labels]),
            )
        allowed = (labels[None, :] == lead_doc_low[:, None]) | (
            jnp.arange(key_total)[None, :] == own_slot[:, None]
        )
        allowed = allowed[None, None]
        mixed_rows, log_total = attention_forward(
            queries.reshape(query_shape),
            paired[:, :model_width].reshape(key_shape),
            paired[:, model_width:].reshape(key_shape),
            allowed,
            score_scale,
        )
        return (mixed_rows.reshape(seg_count, model_width), (paired, allowed, log_total))

    def cls_attend_back(queries, keys_in, values, attend_kept, grad_mixed):
        paired, allowed, log_total = attend_kept
        grad_query, grad_key, grad_value = attention_backward(
            queries.reshape(query_shape),
            paired[:, :model_width].reshape(key_shape),
            paired[:, model_width:].reshape(key_shape),
            allowed,
            score_scale,
            log_total,
            grad_mixed.reshape(query_shape),
        )
        grad_pair = jnp.concatenate(
            [grad_key.reshape(key_total, model_width), grad_value.reshape(key_total, model_width)],
            axis=1,
        )
        for bit_level in reversed(range(bit_count)):
            half_rows = grad_pair.shape[0] // 2
            upper_half = rank_full // (1 << bit_level) % 2 == 1
            kept_half = jnp.where(upper_half, grad_pair[half_rows:], grad_pair[:half_rows])
            sent_half = jnp.where(upper_half, grad_pair[:half_rows], grad_pair[half_rows:])
            grad_pair = kept_half + swapped(
                sent_half.astype(jnp.bfloat16), "fsdp", bit_level
            ).astype(sent_half.dtype)
        grad_pair = grad_pair.astype(jnp.bfloat16)
        return (
            grad_query.reshape(seg_count, model_width).astype(jnp.bfloat16),
            grad_pair[:, :model_width],
            grad_pair[:, model_width:],
        )

    top_out, cls_saved = block_forward(heads_in, cls_unpacked, cls_attend)
    combined = jnp.concatenate([top_out[:, None, :], first_grid[:, 1:, :]], axis=1).reshape(
        tok_rows, model_width
    )
    output_rows = combined * live_rows[:, None]
    diff_rows = (output_rows - targets.astype(jnp.float32)) * live_rows[:, None]
    count_all, square_all = lax.psum(
        (jnp.sum(live_rows), jnp.sum(diff_rows * diff_rows)), ("rep", "fsdp")
    )
    loss_value = square_all / (count_all * model_width)
    slots_all = tok_rows * lax.axis_size("rep") * lax.axis_size("fsdp")
    grad_grid = (diff_rows * (slots_all / count_all)).reshape(seg_count, seg_len, model_width)
    cls_back = unpack_weights(
        (
            lax.all_gather(cls_mats, "fsdp", axis=0, tiled=True),
            lax.all_gather(cls_vecs, "fsdp", axis=0, tiled=True),
        ),
        model_width,
        ff_width,
    )
    heads_grad, cls_weight_rows, cls_g_vec = block_backward(
        grad_grid[:, 0, :], cls_back, cls_saved, cls_attend_back
    )
    cls_g_qkv, cls_g_out, cls_g_up, cls_g_down = weight_products(cls_weight_rows)
    pos_local = jnp.sum(position_hot[:, :, None] * heads_grad[:, None, :], axis=0)
    seg_grad_out = jnp.concatenate([heads_grad[:, None, :], grad_grid[:, 1:, :]], axis=1).reshape(
        tok_rows, model_width
    )
    seg_back = unpack_weights(
        (
            lax.all_gather(seg_mats, "fsdp", axis=0, tiled=True),
            lax.all_gather(seg_vecs, "fsdp", axis=0, tiled=True),
        ),
        model_width,
        ff_width,
    )
    input_grad, seg_weight_rows, seg_g_vec = block_backward(
        seg_grad_out, seg_back, seg_saved, seg_attend_back
    )
    seg_g_qkv, seg_g_out, seg_g_up, seg_g_down = weight_products(seg_weight_rows)
    owner_rows = tuple(
        (
            lax.psum_scatter(seg_g_qkv, "fsdp", scatter_dimension=0, tiled=True),
            lax.psum_scatter(seg_g_out, "fsdp", scatter_dimension=0, tiled=True),
            lax.psum_scatter(seg_g_up, "fsdp", scatter_dimension=0, tiled=True),
            lax.psum_scatter(seg_g_down, "fsdp", scatter_dimension=0, tiled=True),
            lax.psum_scatter(seg_g_vec, "fsdp", scatter_dimension=0, tiled=True),
            lax.psum_scatter(cls_g_qkv, "fsdp", scatter_dimension=0, tiled=True),
            lax.psum_scatter(cls_g_out, "fsdp", scatter_dimension=0, tiled=True),
            lax.psum_scatter(cls_g_up, "fsdp", scatter_dimension=0, tiled=True),
            lax.psum_scatter(cls_g_down, "fsdp", scatter_dimension=0, tiled=True),
            lax.psum_scatter(cls_g_vec, "fsdp", scatter_dimension=0, tiled=True),
        )
    )
    replica_share = (
        lax.psum_scatter(
            owner_rows[0].astype(jnp.bfloat16), "rep", scatter_dimension=1, tiled=True
        ).astype(jnp.float32),
        lax.psum_scatter(
            owner_rows[1].astype(jnp.bfloat16), "rep", scatter_dimension=1, tiled=True
        ).astype(jnp.float32),
        lax.psum_scatter(
            owner_rows[2].astype(jnp.bfloat16), "rep", scatter_dimension=1, tiled=True
        ).astype(jnp.float32),
        lax.psum_scatter(
            owner_rows[3].astype(jnp.bfloat16), "rep", scatter_dimension=1, tiled=True
        ).astype(jnp.float32),
        lax.psum_scatter(
            owner_rows[4].astype(jnp.bfloat16), "rep", scatter_dimension=0, tiled=True
        ).astype(jnp.float32),
        lax.psum_scatter(
            owner_rows[5].astype(jnp.bfloat16), "rep", scatter_dimension=1, tiled=True
        ).astype(jnp.float32),
        lax.psum_scatter(
            owner_rows[6].astype(jnp.bfloat16), "rep", scatter_dimension=1, tiled=True
        ).astype(jnp.float32),
        lax.psum_scatter(
            owner_rows[7].astype(jnp.bfloat16), "rep", scatter_dimension=1, tiled=True
        ).astype(jnp.float32),
        lax.psum_scatter(
            owner_rows[8].astype(jnp.bfloat16), "rep", scatter_dimension=1, tiled=True
        ).astype(jnp.float32),
        lax.psum_scatter(
            owner_rows[9].astype(jnp.bfloat16), "rep", scatter_dimension=0, tiled=True
        ).astype(jnp.float32),
    )
    all_summed = (
        lax.all_gather(replica_share[0].astype(jnp.bfloat16), "rep", axis=1, tiled=True).astype(
            jnp.float32
        ),
        lax.all_gather(replica_share[1].astype(jnp.bfloat16), "rep", axis=1, tiled=True).astype(
            jnp.float32
        ),
        lax.all_gather(replica_share[2].astype(jnp.bfloat16), "rep", axis=1, tiled=True).astype(
            jnp.float32
        ),
        lax.all_gather(replica_share[3].astype(jnp.bfloat16), "rep", axis=1, tiled=True).astype(
            jnp.float32
        ),
        lax.all_gather(replica_share[4].astype(jnp.bfloat16), "rep", axis=0, tiled=True).astype(
            jnp.float32
        ),
        lax.all_gather(replica_share[5].astype(jnp.bfloat16), "rep", axis=1, tiled=True).astype(
            jnp.float32
        ),
        lax.all_gather(replica_share[6].astype(jnp.bfloat16), "rep", axis=1, tiled=True).astype(
            jnp.float32
        ),
        lax.all_gather(replica_share[7].astype(jnp.bfloat16), "rep", axis=1, tiled=True).astype(
            jnp.float32
        ),
        lax.all_gather(replica_share[8].astype(jnp.bfloat16), "rep", axis=1, tiled=True).astype(
            jnp.float32
        ),
        lax.all_gather(replica_share[9].astype(jnp.bfloat16), "rep", axis=0, tiled=True).astype(
            jnp.float32
        ),
    )
    seg_summed = all_summed[:5]
    cls_summed = all_summed[5:]
    pos_total = lax.psum(pos_local, ("rep", "fsdp"))
    seg_mat_grad = jnp.concatenate(
        [seg_summed[0], seg_summed[1], seg_summed[2], seg_summed[3]], axis=1
    )
    cls_mat_grad = jnp.concatenate(
        [cls_summed[0], cls_summed[1], cls_summed[2], cls_summed[3]], axis=1
    )
    return (
        output_rows.astype(jnp.bfloat16),
        input_grad.astype(jnp.bfloat16),
        seg_mat_grad,
        seg_summed[4],
        cls_mat_grad,
        cls_summed[4],
        pos_total,
        loss_value,
    )


LINE = 4
PLANE = 4
CORES = 2
LANES = 128
GROUP = LINE * PLANE
LOW, WIDE = jnp.bfloat16, jnp.float32
MODEL = HEADS * HEAD_DIM
SPAN = 2 * LANES
TILE_START = (0, 1, 3, 4)


def line_pairs(apart):
    return [(source, (source + apart * PLANE) % GROUP) for source in range(GROUP)]


def plane_pairs(mask):
    return [(source, source ^ mask) for source in range(GROUP)]


def along_line(value, apart):
    return lax.ppermute(value, "fsdp", line_pairs(apart))


def in_plane(value, mask):
    return lax.ppermute(value, "fsdp", plane_pairs(mask))


def other_core(value):
    return lax.ppermute(value, "rep", [(0, 1), (1, 0)])


def after(value, *events):
    return lax.optimization_barrier((value,) + events)[0]


def together(*values):
    return tuple(lax.optimization_barrier(values))


def shape_of(dims, dtype=WIDE):
    return jax.ShapeDtypeStruct(dims, dtype)


def run_kernel(body, name, outs, where, blocks, arrays, scratch=(), far=(), flops=0):
    in_specs = [pl.BlockSpec(memory_space=pltpu.SMEM)]
    in_specs += [pl.BlockSpec(memory_space=pltpu.HBM)] * len(blocks)
    in_specs += [pl.BlockSpec(memory_space=pltpu.VMEM)] * len(arrays)
    spaces = [pltpu.HBM if at in far else pltpu.VMEM for at in range(len(outs))]
    moved = sum(x.size * x.dtype.itemsize for x in list(blocks) + list(arrays))
    moved += sum(math.prod(o.shape) * jnp.dtype(o.dtype).itemsize for o in outs)
    return pl.pallas_call(
        body,
        name=name,
        out_shape=tuple(outs),
        in_specs=in_specs,
        out_specs=tuple(pl.BlockSpec(memory_space=space) for space in spaces),
        scratch_shapes=list(scratch),
        cost_estimate=pl.CostEstimate(flops=flops, bytes_accessed=moved, transcendentals=0),
        compiler_params=pltpu.CompilerParams(vmem_limit_bytes=VMEM_BYTES),
    )(where, *blocks, *arrays)


VMEM_BYTES = 24 * 1024 * 1024
HALF = MODEL // CORES
FF_HALF = FF // CORES
OWN = MODEL // GROUP
QUARTER = 3 * SPAN + 2 * FF // LINE
QUARTER_HALF = QUARTER // CORES


def aligned(start):
    return pl.multiple_of(start, LANES)


def wait_all(copies):
    for copy in copies:
        copy.wait()


def run_copies(pairs, sems):
    copies = [
        pltpu.make_async_copy(source, target, sems.at[at])
        for at, (source, target) in enumerate(pairs)
    ]
    for copy in copies:
        copy.start()
    wait_all(copies)


FIRST = 4 * HALF + LANES
OWN_CUT = FIRST + FF_HALF // 2
LINE_CUTS = (7 * LANES, FF_HALF // 2, FF_HALF // 2)
WIDTHS = (FIRST, FF_HALF, FF_HALF)


def group_pieces(group, refs):
    own, rest = refs[:LINE], refs[LINE:]
    own_x, own_y, far_x, far_y, line_x, line_y, late_x, late_y = rest
    width, cut = WIDTHS[group], LINE_CUTS[group]
    start = sum(WIDTHS[:group])
    if group == 0:
        bases = (sum(WIDTHS) - OWN_CUT, OWN_CUT)
    else:
        before, before_cut = WIDTHS[group - 1], LINE_CUTS[group - 1]
        bases = (2 * before - before_cut, before + before_cut)
    pieces = {(0, step): [(own[step], 0, 0, width)] for step in range(LINE)}
    for mask, whole, line, base in ((1, own_x, line_x, bases[0]), (2, own_y, line_y, bases[1])):
        pieces[mask, 0] = [(whole, start, 0, width)]
        for step in range(1, LINE):
            pieces[mask, step] = [(line, base + (step - 1) * width, 0, width)]
    middle = min(max(OWN_CUT - start, 0), width)
    far = []
    if middle > 0:
        far.append((far_y, start, 0, middle))
    if middle < width:
        far.append((far_x, start + middle - OWN_CUT, middle, width))
    pieces[3, 0] = far
    pieces[3, 1] = [(late_y, 0, 0, width)]
    pieces[3, 2] = [(late_y, width, 0, cut), (late_x, 0, cut, width)]
    pieces[3, 3] = [(late_x, width - cut, 0, width)]
    return pieces


def gather_group(where, group, refs, targets):
    line_at, plane_at = where[0], where[1]
    for (mask, step), parts in group_pieces(group, refs).items():
        chip = (line_at + LINE - step) % LINE * PLANE + (plane_at ^ mask)
        for whole, first, last in targets:
            for ref, offset, begin, end in parts:
                low, high = max(first, begin), min(last, end)
                if low < high:
                    source = slice(offset + low - begin, offset + high - begin)
                    whole[chip, :, low - first : high - first] = ref[:, source]


def gather_blocks(where, refs, base, width, targets):
    line_at, plane_at = where[0], where[1]
    half = LINE // 2
    for mask in range(PLANE):
        for step in range(LINE):
            if mask == 0:
                ref, offset = refs[step], 0
            elif mask == 3:
                ref = refs[LINE + 3] if step < half else refs[LINE + 2]
                offset = step % half * width
            else:
                ref, offset = refs[LINE + mask - 1], base + step * width
            chip = (line_at + LINE - step) % LINE * PLANE + (plane_at ^ mask)
            for whole, first, last in targets:
                whole[chip] = ref[:, offset + first : offset + last]


def whole_rows(ref):
    value = ref[...]
    return value.reshape(value.shape[0] * value.shape[1], value.shape[2])


def prepare_first_kernel(where, seg, vecs, flags, out, live_out, sems):
    core_at = where[2]
    pairs = []
    for piece in range(4):
        source = seg.at[:, pl.ds(aligned(piece * MODEL + core_at * HALF), HALF)]
        pairs.append((source, out.at[:, piece * HALF : (piece + 1) * HALF]))
    run_copies(pairs, sems)
    size = vecs.shape[1]
    lines = -(-size // LANES)
    block = jnp.zeros((OWN, LANES), WIDE)
    row_at = lax.broadcasted_iota(jnp.int32, (OWN, LANES), 0)
    for which in range(2):
        for line in range(lines):
            width = min(LANES, size - line * LANES)
            value = vecs[which : which + 1, line * LANES : line * LANES + width]
            if width < LANES:
                value = jnp.concatenate([value, jnp.zeros((1, LANES - width), WIDE)], axis=1)
            block = jnp.where(row_at == which * lines + line, value, block)
    live = flags[...].astype(WIDE)
    live_out[...] = live
    count = jnp.sum(live, axis=1, keepdims=True)
    block = jnp.where(row_at == 2 * lines, count, block)
    out[:, 4 * HALF :] = block.astype(LOW)


def prepare_rest_kernel(where, seg, cls, *refs):
    second_out, third_out = refs[:2]
    step_outs, out_half, order_out = refs[2 : 2 + LINE], refs[2 + LINE], refs[3 + LINE]
    quarters, sems = refs[4 + LINE :]
    line_at, plane_at, core_at = where[0], where[1], where[2]
    start = core_at * FF_HALF
    pairs = [
        (seg.at[:, pl.ds(aligned(4 * MODEL + start), FF_HALF)], second_out),
        (seg.at[:, pl.ds(aligned(4 * MODEL + FF + start), FF_HALF)], third_out),
        (cls.at[:, pl.ds(aligned(3 * MODEL + core_at * HALF), HALF)], out_half),
    ]
    part = FF // LINE
    for at in range(LINE):
        first = TILE_START[at] * LANES
        plan = [(piece * MODEL + first, SPAN, piece * SPAN) for piece in range(3)]
        plan += [
            (4 * MODEL + piece * FF + at * part, part, 3 * SPAN + piece * part)
            for piece in range(2)
        ]
        for source, size, target in plan:
            pairs.append(
                (
                    cls.at[:, source : source + size],
                    quarters.at[at, :, target : target + size],
                )
            )
    run_copies(pairs, sems)
    lanes = pl.ds(aligned(core_at * QUARTER_HALF), QUARTER_HALF)
    for step, out in enumerate(step_outs):
        out[...] = quarters[(line_at + step) % LINE, :, lanes]
    column = lax.broadcasted_iota(jnp.int32, (1, SPAN), 1)
    feature = lax.broadcasted_iota(jnp.int32, (MODEL, SPAN), 0)
    turn = sum((column >= OWN * step).astype(jnp.int32) for step in range(1, LINE))
    held = column - OWN * turn
    turn = (line_at + turn) % LINE
    for mask in range(PLANE):
        source = (turn * PLANE + (plane_at ^ mask)) * OWN + held
        source = jnp.where(column < OWN * LINE, source, -1)
        order_out[:, mask * SPAN : (mask + 1) * SPAN] = (feature == source).astype(LOW)


def prepare_kernel(where, seg, cls, vecs, flags, first_out, live_out, *refs):
    rest, (first_sems, quarters, sems) = refs[:-3], refs[-3:]
    prepare_first_kernel(where, seg, vecs, flags, first_out, live_out, first_sems)
    prepare_rest_kernel(where, seg, cls, *rest, quarters, sems)


def lane_mask(rows, head):
    lane = lax.broadcasted_iota(jnp.int32, (rows, LANES), 1)
    return (lane < HEAD_DIM) if head == 0 else (lane >= HEAD_DIM)


def masked(value, mask):
    return jnp.where(mask, value, jnp.zeros_like(value))


def head_probabilities(query, key, allowed):
    scores = product_right(query, key) * HEAD_DIM ** (-0.5)
    scores = jnp.where(allowed, scores, MASK_FILL)
    raised = jnp.exp(scores - jnp.max(scores, axis=-1, keepdims=True))
    return raised / jnp.sum(raised, axis=-1, keepdims=True)


def attend_tiles(qkv, width, allowed):
    rows = qkv.shape[0]
    mixed = []
    for tile in range(width // LANES):
        at = tile * LANES
        query, key, value = (
            qkv[:, piece * width + at : piece * width + at + LANES] for piece in range(3)
        )
        total = jnp.zeros((rows, LANES), WIDE)
        for head in range(2):
            mask = lane_mask(rows, head)
            weights = head_probabilities(masked(query, mask), key, allowed).astype(LOW)
            total = total + product_plain(weights, masked(value, mask))
        mixed.append(total.astype(LOW))
    return mixed


def attend_tiles_back(qkv, grad_mixed, width, allowed):
    rows = qkv.shape[0]
    scale = HEAD_DIM ** (-0.5)
    results = ([], [], [])
    for tile in range(width // LANES):
        at = tile * LANES
        query, key, value = (
            qkv[:, piece * width + at : piece * width + at + LANES] for piece in range(3)
        )
        grad = grad_mixed[:, at : at + LANES]
        totals = [jnp.zeros((rows, LANES), WIDE) for _ in range(3)]
        for head in range(2):
            mask = lane_mask(rows, head)
            query_low, key_low, grad_low = (masked(x, mask) for x in (query, key, grad))
            chance = head_probabilities(query_low, key, allowed)
            grad_chance = product_right(grad_low, value)
            inner = jnp.sum(grad_chance * chance, axis=-1, keepdims=True)
            grad_scores = (chance * (grad_chance - inner)).astype(LOW)
            totals[0] = totals[0] + product_plain(grad_scores, key_low)
            totals[1] = totals[1] + product_left(grad_scores, query_low)
            totals[2] = totals[2] + product_left(chance.astype(LOW), grad_low)
        results[0].append((totals[0] * scale).astype(LOW))
        results[1].append((totals[1] * scale).astype(LOW))
        results[2].append(totals[2].astype(LOW))
    return results[0] + results[1] + results[2]


def token_allowed(live_row):
    shape = (SEG, SEG)
    same = lax.broadcasted_iota(jnp.int32, shape, 0) == lax.broadcasted_iota(jnp.int32, shape, 1)
    return (live_row > 0.5) | same


def qkv_kernel(where, *refs):
    blocks = refs[:12]
    hidden, hidden_got, live_row, live_got, order = refs[12:17]
    weight, out_low, out_high, qkv_out, mixed_out = refs[17:22]
    vectors_out, count_out, ordered_out = refs[22:25]
    vec_rows, flat, inputs, out_half = refs[25:]
    core_at = where[2]
    gather_group(
        where,
        0,
        blocks,
        (
            (weight, 0, 3 * HALF),
            (out_half, 3 * HALF, 4 * HALF),
            (vec_rows, 4 * HALF, 4 * HALF + LANES),
        ),
    )
    out_low[...] = out_half[: GROUP // 2]
    out_high[...] = out_half[GROUP // 2 :]
    piece = (8 * MODEL + FF) // GROUP
    lines = -(-piece // LANES)
    count = jnp.zeros((1, LANES), WIDE)
    for chip in range(GROUP):
        rows = vec_rows[chip, 0:16, :].astype(WIDE)
        for block in range(2):
            joined = jnp.concatenate(
                [rows[block * lines + r : block * lines + r + 1] for r in range(lines)], axis=1
            )
            flat[block : block + 1, chip * piece : (chip + 1) * piece] = joined[:, :piece]
        count = count + rows[2 * lines : 2 * lines + 1]
    rows_each = (8 * MODEL + FF) // MODEL
    for block in range(2):
        for row in range(rows_each):
            vectors_out[block * rows_each + row : block * rows_each + row + 1, :] = flat[
                block : block + 1, row * MODEL : (row + 1) * MODEL
            ]
    count_out[...] = jnp.broadcast_to(count, count_out.shape)
    inputs[:SEG] = hidden[...]
    inputs[SEG:] = hidden_got[...]
    projected = product_plain(inputs[...], whole_rows(weight))
    lanes = pl.ds(aligned(core_at * HALF), HALF)
    qkv_out[:, :HALF] = (projected[:, :HALF] + vectors_out[0:1, lanes]).astype(LOW)
    qkv_out[:, HALF : 2 * HALF] = projected[:, HALF : 2 * HALF].astype(LOW)
    qkv_out[:, 2 * HALF :] = (projected[:, 2 * HALF :] + vectors_out[1:2, lanes]).astype(LOW)
    for part, live in enumerate((live_row, live_got)):
        rows = slice(part * SEG, (part + 1) * SEG)
        tiles = attend_tiles(qkv_out[rows, :], HALF, token_allowed(live[...]))
        for tile, value in enumerate(tiles):
            mixed_out[rows, tile * LANES : (tile + 1) * LANES] = value
    ordered_out[...] = product_plain(inputs[...], order[...]).astype(LOW)


def norm_rows(summed):
    row_mean = jnp.mean(summed, axis=-1, keepdims=True)
    centered = summed - row_mean
    inv_dev = lax.rsqrt(jnp.mean(centered * centered, axis=-1, keepdims=True) + NORM_EPS)
    return centered * inv_dev, inv_dev


def norm_rows_back(grad_out, normed, inv_dev, gain):
    scaled = grad_out * gain
    mean_one = jnp.mean(scaled, axis=-1, keepdims=True)
    mean_two = jnp.mean(scaled * normed, axis=-1, keepdims=True)
    return inv_dev * (scaled - mean_one - normed * mean_two)


def column_sum(value):
    return jnp.sum(value.astype(WIDE), axis=0, keepdims=True)


def four_rows(vectors, first):
    return jnp.concatenate([vectors[first + at : first + at + 1, :] for at in range(4)], axis=1)


def gelu_both(before):
    half = 0.5 * (1.0 + lax.erf(before * SQRT_HALF))
    slope = half + before * jnp.exp(-0.5 * before * before) * INV_SQRT_TWO_PI
    return before * half, slope


def out_kernel(where, hidden, mixed, mixed_got, low, high, low_got, high_got, *refs):
    vectors, order, full_out, ordered_out, normed_out, inv_out, low_out, mixed_full = refs
    core_at = where[2]
    own, other = aligned(core_at * HALF), aligned((1 - core_at) * HALF)
    rows = MODEL // 2
    full_out[:rows, pl.ds(own, HALF)] = whole_rows(low)
    full_out[rows:, pl.ds(own, HALF)] = whole_rows(high)
    full_out[:rows, pl.ds(other, HALF)] = whole_rows(low_got)
    full_out[rows:, pl.ds(other, HALF)] = whole_rows(high_got)
    mixed_full[:, pl.ds(own, HALF)] = mixed[...]
    mixed_full[:SEG, pl.ds(other, HALF)] = mixed_got[SEG:, :]
    mixed_full[SEG:, pl.ds(other, HALF)] = mixed_got[:SEG, :]
    branch = product_plain(mixed_full[:SEG, :], full_out[...])
    normed, inv_dev = norm_rows(hidden[...].astype(WIDE) + branch + vectors[2:3, :])
    normed_out[...] = normed
    inv_out[...] = inv_dev
    low_out[...] = (normed * vectors[4:5, :] + vectors[5:6, :]).astype(LOW)
    ordered_out[...] = product_plain(mixed_full[...], order[...]).astype(LOW)


def up_kernel(where, *refs):
    blocks = refs[:12]
    low, low_got, vectors = refs[12:15]
    weight, act_out, slope_out, both = refs[15:]
    core_at = where[2]
    gather_group(where, 1, blocks, ((weight, 0, FF_HALF),))
    both[:SEG] = low[...]
    both[SEG:] = low_got[...]
    for at in range(FF_HALF // MODEL):
        columns = slice(at * MODEL, (at + 1) * MODEL)
        held = weight[:, :, columns]
        before = product_plain(both[...], held.reshape(MODEL, MODEL))
        bias = vectors[pl.ds(8 + core_at * (FF_HALF // MODEL) + at, 1), :]
        value, slope = gelu_both(before + bias)
        act_out[:, columns] = value.astype(LOW)
        slope_out[:, columns] = slope


def down_kernel(where, *refs):
    blocks, act = refs[:12], refs[12]
    weight, own_out, send_out = refs[13:]
    gather_group(where, 2, blocks, ((weight, 0, FF_HALF),))
    partial = product_right(act[...], whole_rows(weight))
    own_out[...] = partial[:SEG]
    send_out[...] = partial[SEG:]


def seg_rows_kernel(where, *refs):
    own, got, normed_first, vectors, targets, live, seg_pos = refs[:7]
    normed_out, inv_out, diff_out, rows_out, head_out = refs[7:]
    doc, number = where[3], where[4]
    first = normed_first[...] * vectors[4:5, :] + vectors[5:6, :]
    normed, inv_dev = norm_rows(first + own[...] + got[...] + vectors[3:4, :])
    normed_out[...] = normed
    inv_out[...] = inv_dev
    rows = normed * vectors[6:7, :] + vectors[7:8, :]
    shape = (SEG, SEG)
    same = lax.broadcasted_iota(jnp.int32, shape, 0) == lax.broadcasted_iota(jnp.int32, shape, 1)
    live_rows = jnp.sum(jnp.where(same, live[...], 0.0), axis=1, keepdims=True)
    target_rows = targets[...].astype(WIDE)
    output = rows * live_rows
    rows_out[...] = output
    diff = (output - target_rows) * live_rows
    row_at = lax.broadcasted_iota(jnp.int32, (SEG, 1), 0)
    diff = jnp.where(row_at > 0, diff, 0.0)
    diff_out[...] = diff
    table = seg_pos[...].astype(WIDE)
    chosen = lax.broadcasted_iota(jnp.int32, table.shape, 0) == number
    position = jnp.sum(jnp.where(chosen, table, 0.0), axis=0, keepdims=True)
    head_out[:, :MODEL] = rows[0:1, :] + position
    head_out[:, MODEL : 2 * MODEL] = target_rows[0:1, :]
    square = jnp.sum(column_sum(diff * diff), axis=1, keepdims=True)
    lane = lax.broadcasted_iota(jnp.int32, (1, LANES), 1)
    facts = jnp.where(lane == 0, live_rows[0:1, :], 0.0)
    facts = jnp.where(lane == 1, doc.astype(WIDE), facts)
    facts = jnp.where(lane == 2, number.astype(WIDE), facts)
    facts = jnp.where(lane == 3, square, facts)
    head_out[:, 2 * MODEL :] = facts


def second_norm_kernel(where, diff, count, normed, inv_dev, vectors, grad_out, low_out, sums_out):
    grad_top = diff[...] * ((SEG * GROUP * CORES) / count[0:1, 0:1])
    normed_rows = normed[...]
    grad = norm_rows_back(grad_top, normed_rows, inv_dev[...], vectors[6:7, :])
    low = grad.astype(LOW)
    grad_out[...] = grad
    low_out[...] = low
    sums_out[0:1, :] = column_sum(low)
    sums_out[1:2, :] = column_sum(grad_top * normed_rows)
    sums_out[2:3, :] = column_sum(grad_top)


def mlp_back_kernel(where, *refs):
    low, low_got, down_weight, up_weight, slope = refs[:5]
    pre_out, own_out, send_out, sums_out, both = refs[5:]
    both[:SEG] = low[...]
    both[SEG:] = low_got[...]
    for at in range(FF_HALF // MODEL):
        columns = slice(at * MODEL, (at + 1) * MODEL)
        held = down_weight[:, :, columns]
        before = product_plain(both[...], held.reshape(MODEL, MODEL))
        pre = (before * slope[:, columns]).astype(LOW)
        pre_out[:, columns] = pre
        sums_out[at : at + 1, :] = column_sum(pre)
    partial = product_right(pre_out[...], whole_rows(up_weight))
    own_out[...] = partial[:SEG]
    send_out[...] = partial[SEG:]


def scatter_parts(where, parts, outs, sems):
    line_at, plane_at = where[0], where[1]
    far_low, far_high, to_x, to_y, kept = outs
    half = LINE // 2
    copies = []
    for mask in range(PLANE):
        for step in range(LINE):
            source = parts.at[(line_at + step) % LINE * PLANE + (plane_at ^ mask)]
            if mask == 3:
                target = far_low.at[step] if step < half else far_high.at[step - half]
            else:
                target = (kept, to_x, to_y)[mask].at[step]
            copies.append(pltpu.make_async_copy(source, target, sems.at[len(copies)]))
    for copy in copies:
        copy.start()
    wait_all(copies)


def mlp_weight_kernel(where, *refs):
    first, first_got, second, second_got, pre, act = refs[:6]
    outs = refs[6:11]
    left, parts, sems = refs[11:]
    for at, (own, got, right) in enumerate(((first, first_got, pre), (second, second_got, act))):
        left[:SEG] = own[...]
        left[SEG:] = got[...]
        for piece in range(FF_HALF // MODEL):
            start = piece * MODEL
            product = product_left(left[...], right[:, start : start + MODEL]).astype(LOW)
            target = at * FF_HALF + start
            parts[:, :, target : target + MODEL] = product.reshape(GROUP, OWN, MODEL)
    scatter_parts(where, parts, outs, sems)


def attn_product(where, refs, mask, piece):
    hidden, mixed, proj, branch, got = refs
    lanes = slice(mask * SPAN, (mask + 1) * SPAN)
    if piece < 3:
        right = proj[:, piece * HALF : (piece + 1) * HALF]
        product = product_left(hidden[:, lanes], right)
    else:
        own = branch[:, pl.ds(aligned(where[2] * HALF), HALF)]
        product = product_left(mixed[:SEG, lanes], own)
        product = product + product_left(mixed[SEG:, lanes], got[:, HALF:])
    return product[: LINE * OWN].astype(LOW).reshape(LINE, OWN, HALF)


def attn_far_kernel(where, *refs):
    low_out, high_out = refs[5:]
    half = LINE // 2
    for piece in range(4):
        columns = slice(piece * HALF, (piece + 1) * HALF)
        product = attn_product(where, refs[:5], 3, piece)
        low_out[:, :, columns] = product[:half]
        high_out[:, :, columns] = product[half:]


def attn_near_kernel(where, *refs):
    top_row, out_rows, live_row = refs[5:8]
    row_at = lax.broadcasted_iota(jnp.int32, (SEG, 1), 0)
    output = jnp.where(row_at == 0, top_row[...] * live_row[:, 0:1], out_rows[...])
    refs[11][...] = output.astype(LOW)
    for mask, out in ((1, refs[8]), (2, refs[9]), (0, refs[10])):
        for piece in range(4):
            columns = slice(piece * HALF, (piece + 1) * HALF)
            out[:, :, columns] = attn_product(where, refs[:5], mask, piece)


def fold_kernel(where, kept, got_x, got_y, *refs):
    extra, own_out, sent = refs[: -LINE], refs[-LINE], refs[1 - LINE :]
    rows = kept.shape[1]
    for step in range(LINE):
        total = kept[step].astype(WIDE) + got_x[step].astype(WIDE) + got_y[step].astype(WIDE)
        if step == 0:
            own_out[...] = total
            continue
        out = sent[step - 1]
        out[:rows, :] = total.astype(LOW)
        if extra:
            out[rows:, :] = jnp.zeros_like(out[rows:, :])
            out[rows:, : extra[0].shape[1]] = extra[0][...]


def reduce_far(parts):
    return together(in_plane(parts[0], 2), in_plane(parts[1], 1))


def reduce_add(where, parts, far):
    shape = parts[2].shape
    return run_kernel(
        add_far_kernel,
        "add_far",
        [shape_of(shape, LOW)] * 2,
        where,
        (),
        tuple(far) + (parts[2], parts[3]),
    )


def reduce_fold(where, kept, got, *extra):
    _, rows, columns = kept.shape
    more = sum(value.shape[0] for value in extra)
    return run_kernel(
        fold_kernel,
        "fold",
        [shape_of((rows, columns))] + [shape_of((rows + more, columns), LOW)] * (LINE - 1),
        where,
        (),
        (kept,) + tuple(got) + extra,
    )


def reduce_line(own, pieces):
    total = own
    for piece in pieces:
        total = total + piece[: own.shape[0]].astype(WIDE)
    return total


def head_back_kernel(where, *refs):
    grad, grad_got, down_weight, up_weight, slope, act, low, low_got = refs[:8]
    own_out, send_out, data_out = refs[8:]
    few = 16
    row_at = lax.broadcasted_iota(jnp.int32, (few, 1), 0)

    def two_rows(first, second):
        return jnp.where(row_at == 0, first, jnp.where(row_at == 1, second, 0.0))

    second = two_rows(grad[...], grad_got[...]).astype(LOW)
    data_out[0:1, :] = low[0:1, :].astype(WIDE)
    data_out[1:2, :] = low_got[0:1, :].astype(WIDE)
    data_out[2:4, :] = second[0:2].astype(WIDE)
    partial = jnp.zeros((few, MODEL), WIDE)
    for at in range(FF_HALF // MODEL):
        columns = slice(at * MODEL, (at + 1) * MODEL)
        before = product_plain(second, down_weight[:, :, columns].reshape(MODEL, MODEL))
        slopes = two_rows(slope[0:1, columns], slope[SEG : SEG + 1, columns])
        pre = (before * slopes).astype(LOW)
        partial = partial + product_right(pre, up_weight[:, :, columns].reshape(MODEL, MODEL))
        data_out[4 + 2 * at : 6 + 2 * at, :] = pre[0:2].astype(WIDE)
        data_out[8 + 2 * at : 9 + 2 * at, :] = act[0:1, columns].astype(WIDE)
        data_out[9 + 2 * at : 10 + 2 * at, :] = act[SEG : SEG + 1, columns].astype(WIDE)
    own_out[...] = partial[0:1]
    send_out[...] = partial[1:2]


def first_norm_kernel(where, *refs):
    second_grad, own, got, head_grad, head_own, head_got = refs[:6]
    normed_rows, inv_dev, vectors, out_weight = refs[6:10]
    grad_out, branch_out, mixed_out, send_out, sums_out = refs[10:]
    core_at = where[2]
    grad_rows = second_grad[...] + own[...] + got[...]
    head = head_grad[...] + head_own[...] + head_got[...]
    row_at = lax.broadcasted_iota(jnp.int32, (SEG, 1), 0)
    grad_rows = jnp.where(row_at == 0, head, grad_rows)
    normed = normed_rows[...]
    grad = norm_rows_back(grad_rows, normed, inv_dev[...], vectors[4:5, :])
    grad_out[...] = grad
    branch = grad.astype(LOW)
    branch_out[...] = branch
    mixed_out[...] = product_right(branch, out_weight[...]).astype(LOW)
    other = pl.ds(aligned((1 - core_at) * HALF), HALF)
    send_out[:, :HALF] = mixed_out[:, other]
    send_out[:, HALF:] = branch_out[:, other]
    sums_out[0:1, :] = column_sum(branch)
    sums_out[1:2, :] = column_sum(grad_rows * normed)
    sums_out[2:3, :] = column_sum(grad_rows)


def attn_back_kernel(where, *refs):
    qkv, mixed_grad, got, live_row, live_got, weight = refs[:6]
    sums_first, sums_second, sums_up, head_top, head_normed, data = refs[6:12]
    proj_out, own_out, send_out, payload_out, rows = refs[12:]
    core_at = where[2]
    lanes = pl.ds(aligned(core_at * HALF), HALF)
    for part, live in enumerate((live_row, live_got)):
        at = slice(part * SEG, (part + 1) * SEG)
        grad = mixed_grad[:, lanes] if part == 0 else got[:, :HALF]
        pieces = attend_tiles_back(qkv[at, :], grad, HALF, token_allowed(live[...]))
        for tile, value in enumerate(pieces):
            proj_out[at, tile * LANES : (tile + 1) * LANES] = value
    partial = product_right(proj_out[...], whole_rows(weight))
    own_out[...] = partial[:SEG]
    send_out[...] = partial[SEG:]
    rows[...] = jnp.zeros_like(rows)
    rows[0:12, :] = data[0:12, :]
    rows[12:13, lanes] = column_sum(proj_out[:, :HALF])
    rows[13:14, lanes] = column_sum(proj_out[:, 2 * HALF :])
    rows[14:15, :] = sums_first[0:1, :]
    rows[15:16, :] = sums_second[0:1, :] + data[2:3, :]
    rows[16:18, :] = sums_first[1:3, :]
    rows[18:19, :] = sums_second[1:2, :] + head_top[...] * head_normed[0:1, :]
    rows[19:20, :] = sums_second[2:3, :] + head_top[...]
    for at in range(FF_HALF // MODEL):
        total = sums_up[at : at + 1, :] + data[4 + 2 * at : 5 + 2 * at, :]
        total = total + data[5 + 2 * at : 6 + 2 * at, :]
        rows[pl.ds(20 + core_at * (FF_HALF // MODEL) + at, 1), :] = total
    payload_out[...] = rows[...].astype(LOW)


def cls_gather_kernel(where, *refs):
    blocks = refs[:8]
    own_out, from_x, from_y, far_x = refs[8], refs[4], refs[5], refs[6]
    weight_out, out_rows = refs[9:]
    plane_at = where[1]
    gather_blocks(where, blocks, 0, QUARTER_HALF, ((weight_out, 0, QUARTER_HALF),))
    first = LINE * QUARTER_HALF
    out_rows[plane_at] = own_out[...]
    out_rows[plane_at ^ 1] = from_x[:, first : first + HALF]
    out_rows[plane_at ^ 2] = from_y[:, first : first + HALF]
    first = LINE // 2 * QUARTER_HALF
    out_rows[plane_at ^ 3] = far_x[:, first : first + HALF]


def cls_weight_kernel(where, own, got, out_half, out_got, weight_out, out_full):
    line_at, core_at = where[0], where[2]
    out_full[...] = jnp.zeros_like(out_full)
    for value, part, core in ((own, out_half, core_at), (got, out_got, 1 - core_at)):
        weight_out[:, :, pl.ds(aligned(core * QUARTER_HALF), QUARTER_HALF)] = value[...]
        rows = part[...].reshape(3, HEAD_DIM, HALF)
        out_full[pl.ds(line_at % 2, 3), :, pl.ds(aligned(core * HALF), HALF)] = rows


def add_far_kernel(where, far_low, far_high, to_x, to_y, x_out, y_out):
    half = LINE // 2
    x_out[:half] = to_x[:half] + far_low[...]
    x_out[half:] = to_x[half:]
    y_out[:half] = to_y[:half]
    y_out[half:] = to_y[half:] + far_high[...]


def row_from_column(column, size):
    shape = (size, size)
    same = lax.broadcasted_iota(jnp.int32, shape, 0) == lax.broadcasted_iota(jnp.int32, shape, 1)
    return jnp.sum(jnp.where(same, column, 0.0), axis=0, keepdims=True)


def head_allowed(heads):
    facts = heads[:, 2 * MODEL :]
    live, doc = facts[:, 0:1], facts[:, 1:2]
    shape = (GROUP, GROUP)
    same = lax.broadcasted_iota(jnp.int32, shape, 0) == lax.broadcasted_iota(jnp.int32, shape, 1)
    live_row, doc_row = row_from_column(live, GROUP), row_from_column(doc, GROUP)
    return ((live_row > 0.5) & (doc == doc_row)) | same


def quarter_mask(quarter):
    lane = lax.broadcasted_iota(jnp.int32, (GROUP, SPAN), 1)
    first = (quarter % 2) * HEAD_DIM
    return (lane >= first) & (lane < first + 3 * HEAD_DIM)


def quarter_piece(vectors, row, quarter):
    value = jnp.zeros((1, SPAN), WIDE)
    for at in range(LINE):
        first = TILE_START[at] * LANES
        value = jnp.where(quarter == at, vectors[row : row + 1, first : first + SPAN], value)
    return value


def cls_attend_kernel(where, *refs):
    stacks, vectors, weight, out_weight = refs[:4], refs[4], refs[5], refs[6]
    heads_out, qkv_out, mixed_out, part_out = refs[7:]
    line_at, plane_at = where[0], where[1]
    for step, stack in enumerate(stacks):
        for mask in range(PLANE):
            row = (line_at + LINE - step) % LINE * PLANE + (plane_at ^ mask)
            heads_out[pl.ds(row, 1), :] = stack[mask : mask + 1, :]
    heads = heads_out[...]
    inputs = heads[:, :MODEL].astype(LOW)
    projected = product_plain(inputs, weight[:, : 3 * SPAN])
    query = projected[:, :SPAN] + quarter_piece(vectors, 12, line_at)
    value = projected[:, 2 * SPAN :] + quarter_piece(vectors, 13, line_at)
    qkv_out[:, :SPAN] = query.astype(LOW)
    qkv_out[:, SPAN : 2 * SPAN] = projected[:, SPAN : 2 * SPAN].astype(LOW)
    qkv_out[:, 2 * SPAN :] = value.astype(LOW)
    mixed = attend_tiles(qkv_out[...], SPAN, head_allowed(heads))
    mixed = masked(jnp.concatenate(mixed, axis=1), quarter_mask(line_at))
    mixed_out[...] = mixed
    part_out[...] = product_plain(mixed, out_weight[...])


def cls_mlp_kernel(where, *refs):
    heads, own, got_one, got_two, got_three, vectors, weight = refs[:7]
    normed_out, inv_out, low_out, act_out, slope_out, part_out = refs[7:]
    line_at = where[0]
    branch = own[...] + got_one[...] + got_two[...] + got_three[...]
    normed, inv_dev = norm_rows(heads[:, :MODEL] + branch + vectors[14:15, :])
    normed_out[...] = normed
    inv_out[...] = inv_dev
    low = (normed * vectors[16:17, :] + vectors[17:18, :]).astype(LOW)
    low_out[...] = low
    part = FF // LINE
    first = 3 * SPAN
    bias = vectors[pl.ds(20 + line_at, 1), :]
    before = product_plain(low, weight[:, first : first + part]) + bias
    value, slope = gelu_both(before)
    act = value.astype(LOW)
    act_out[...] = act
    slope_out[...] = slope
    part_out[...] = product_right(act, weight[:, first + part :])


def cls_top_kernel(where, *refs):
    heads, own, got_one, got_two, got_three, vectors, weight = refs[:7]
    normed_first, count, slope = refs[7:10]
    top_out, square_out, grad_out, second_out, pre_out, part_out, sums_out = refs[10:17]
    held = refs[17]
    rank = where[0] * PLANE + where[1]
    first = normed_first[...] * vectors[16:17, :] + vectors[17:18, :]
    down = own[...] + got_one[...] + got_two[...] + got_three[...]
    normed, inv_dev = norm_rows(first + down + vectors[15:16, :])
    rows = normed * vectors[18:19, :] + vectors[19:20, :]
    held[...] = rows
    top_out[...] = held[pl.ds(rank, 1), :]
    facts = heads[:, 2 * MODEL :]
    live = facts[:, 0:1]
    diff = (rows * live - heads[:, MODEL : 2 * MODEL]) * live
    square = jnp.sum(column_sum(diff * diff), axis=1, keepdims=True)
    square = square + jnp.sum(facts[:, 3:4], axis=0, keepdims=True)
    square_out[...] = jnp.broadcast_to(square, square_out.shape)
    grad_top = diff * ((SEG * GROUP * CORES) / count[0:1, 0:1])
    grad = norm_rows_back(grad_top, normed, inv_dev, vectors[18:19, :])
    sums_out[0:1, :] = column_sum(grad_top * normed)
    sums_out[1:2, :] = column_sum(grad_top)
    grad_out[...] = grad
    second = grad.astype(LOW)
    second_out[...] = second
    part = FF // LINE
    at = 3 * SPAN
    pre = (product_plain(second, weight[:, at + part :]) * slope[...]).astype(LOW)
    pre_out[...] = pre
    part_out[...] = product_right(pre, weight[:, at : at + part])


def cls_attend_back_kernel(where, *refs):
    heads, own, got_one, got_two, got_three, vectors, weight, out_weight = refs[:8]
    grad_in, normed_first, inv_first, qkv = refs[8:12]
    grad_out, branch_out, proj_out, part_out, sums_out = refs[12:]
    line_at = where[0]
    grad_first = grad_in[...] + own[...] + got_one[...] + got_two[...] + got_three[...]
    normed = normed_first[...]
    grad = norm_rows_back(grad_first, normed, inv_first[...], vectors[16:17, :])
    sums_out[0:1, :] = column_sum(grad_first * normed)
    sums_out[1:2, :] = column_sum(grad_first)
    grad_out[...] = grad
    branch = grad.astype(LOW)
    branch_out[...] = branch
    mask = quarter_mask(line_at)
    mixed_grad = masked(product_right(branch, out_weight[...]).astype(LOW), mask)
    pieces = attend_tiles_back(qkv[...], mixed_grad, SPAN, head_allowed(heads[...]))
    tiles = SPAN // LANES
    for piece in range(3):
        joined = jnp.concatenate(pieces[piece * tiles : (piece + 1) * tiles], axis=1)
        proj_out[:, piece * SPAN : (piece + 1) * SPAN] = masked(joined, mask)
    part_out[...] = product_right(proj_out[...], weight[:, : 3 * SPAN])


def cls_end_kernel(where, *refs):
    heads, grad, own, got_one, got_two, got_three = refs[:6]
    square, sums_back, sums_top = refs[6:9]
    normed_second, inv_second, vectors = refs[9:12]
    row_out, second_out, shared_out, held = refs[12:]
    rank = where[0] * PLANE + where[1]
    total = grad[...] + own[...] + got_one[...] + got_two[...] + got_three[...]
    held[...] = total
    row = held[pl.ds(rank, 1), :]
    row_out[...] = row
    second_out[...] = norm_rows_back(
        row, normed_second[0:1, :], inv_second[0:1, :], vectors[6:7, :]
    )
    number = row_from_column(heads[:, 2 * MODEL + 2 : 2 * MODEL + 3], GROUP)
    entry = lax.broadcasted_iota(jnp.int32, (GROUP, GROUP), 0).astype(WIDE)
    hot = (entry == number).astype(WIDE)
    shared_out[0:GROUP, :] = jnp.dot(hot, total, precision=lax.Precision.HIGHEST)
    shared_out[GROUP : GROUP + 1, 0:LANES] = square[0:1, :]
    shared_out[GROUP + 1 : GROUP + 3, :] = sums_back[0:2, :]
    shared_out[GROUP + 3 : GROUP + 5, :] = sums_top[0:2, :]


def head_mlp_kernel(where, *refs):
    cls_mlp_kernel(where, *refs[:7], *refs[11:17])
    add_far_kernel(where, *refs[7:11], *refs[17:])


def head_end_kernel(where, *refs):
    cls_end_kernel(where, *refs[:12], *refs[16:19], refs[23])
    fold_kernel(where, *refs[12:16], *refs[19:23])


def attn_add_kernel(where, *refs):
    far_low, far_high, to_x, to_y, grad, own, got, x_out, y_out, input_out = refs
    add_far_kernel(where, far_low, far_high, to_x, to_y, x_out, y_out)
    input_out[...] = (grad[...] + own[...] + got[...]).astype(LOW)


def cls_rows_kernel(where, *refs):
    packs = refs[:4]
    heads, branch, low, second = refs[4:8]
    out, kept = refs[8:]
    line_at = where[0]
    rows, width = kept.shape[1:]
    for step, pack in enumerate(packs):
        first = pack.shape[0] - rows
        kept[(line_at + LINE - step) % LINE] = pack[first:, :width]
    starts = (MODEL, 2 * MODEL, 3 * MODEL, 4 * MODEL)
    out[:, 0:MODEL] = heads[:, :MODEL].astype(LOW)
    for piece, start in enumerate(starts):
        from_at = piece * SPAN
        for tile in range(MODEL // LANES):
            total = None
            for at in range(PLANE):
                inner = tile - TILE_START[at]
                if inner in (0, 1):
                    first = from_at + inner * LANES
                    value = kept[at, :, first : first + LANES]
                    total = value if total is None else total + value
            out[:, start + tile * LANES : start + (tile + 1) * LANES] = total
    out[:, 5 * MODEL : 6 * MODEL] = branch[...]
    out[:, 6 * MODEL : 7 * MODEL] = low[...]
    out[:, 7 * MODEL + FF : 8 * MODEL + FF] = second[...]
    part = FF // LINE
    for at in range(PLANE):
        first = 4 * SPAN
        out[:, 7 * MODEL + at * part : 7 * MODEL + (at + 1) * part] = kept[
            at, :, first : first + part
        ]
        out[:, 8 * MODEL + FF + at * part : 8 * MODEL + FF + (at + 1) * part] = kept[
            at, :, first + part : first + 2 * part
        ]


def own_features(rank, width):
    shape = (MODEL, width)
    feature = lax.broadcasted_iota(jnp.int32, shape, 0)
    column = lax.broadcasted_iota(jnp.int32, shape, 1)
    return (feature == rank * width + column).astype(LOW)


def own_vector(rank, pieces, out, flat):
    size = out.shape[0]
    for at, piece in enumerate(pieces):
        flat[:, at * MODEL : (at + 1) * MODEL] = piece
    value = jnp.zeros((1, size), WIDE)
    for chip in range(GROUP):
        value = jnp.where(rank == chip, flat[:, chip * size : (chip + 1) * size], value)
    out[...] = value.reshape(size)


def cls_owner_kernel(where, *refs):
    own, got, shared, mats_out, vec_out, rows, flat = refs
    rank = where[0] * PLANE + where[1]
    width = mats_out.shape[0]
    rows[:GROUP] = own[...]
    rows[GROUP:] = got[...]
    chosen = own_features(rank, width)
    plan = (
        (0, MODEL, 3 * MODEL, 0),
        (4 * MODEL, 5 * MODEL, MODEL, 3 * MODEL),
        (6 * MODEL, 7 * MODEL, FF, 4 * MODEL),
        (7 * MODEL + FF, 8 * MODEL + FF, FF, 4 * MODEL + FF),
    )
    for left, right, size, target in plan:
        side = product_plain(rows[:, left : left + MODEL], chosen).astype(LOW)
        mats_out[:, target : target + size] = product_left(side, rows[:, right : right + size])
    starts = (MODEL, 3 * MODEL, 5 * MODEL, 7 * MODEL + FF)
    pieces = [column_sum(rows[:, start : start + MODEL]) for start in starts]
    pieces += [shared[GROUP + 1 + at : GROUP + 2 + at, :] for at in range(4)]
    starts = [7 * MODEL + at * MODEL for at in range(FF // MODEL)]
    pieces += [column_sum(rows[:, start : start + MODEL]) for start in starts]
    own_vector(rank, pieces, vec_out, flat)


def head_share_kernel(where, *refs):
    packs, mlp = refs[:4], refs[4]
    mine_out, vecs_out, rows = refs[5:]
    rank = where[0] * PLANE + where[1]
    count = LINE * 24
    for at, pack in enumerate(packs):
        rows[at * count : (at + 1) * count] = pack[...]
    total = PLANE * count

    def chosen(base, apart):
        shape = (CORES * GROUP, total)
        row = lax.broadcasted_iota(jnp.int32, shape, 0)
        column = lax.broadcasted_iota(jnp.int32, shape, 1)
        hot = (column == row // 2 * 24 + base + row % 2 * apart).astype(LOW)
        return product_plain(hot, rows[...]).astype(LOW)

    own = own_features(rank, OWN)
    for at, (left, right) in enumerate(((0, 4), (2, 8))):
        side = product_plain(chosen(left, 1), own).astype(LOW)
        for piece in range(FF_HALF // MODEL):
            columns = slice(at * FF_HALF + piece * MODEL, at * FF_HALF + (piece + 1) * MODEL)
            share = product_left(side, chosen(right + 2 * piece, 1))
            mine_out[:, columns] = mlp[:, columns] + share
    shape = (16, total)
    row = lax.broadcasted_iota(jnp.int32, shape, 0)
    column = lax.broadcasted_iota(jnp.int32, shape, 1)
    hot = ((column % 24 == row + 12) & (row < 12)).astype(LOW)
    vecs_out[...] = product_plain(hot, rows[...])


def share_owner_kernel(where, *refs):
    head_share_kernel(where, *refs[:5], *refs[9:11], refs[15])
    cls_owner_kernel(where, *refs[5:8], *refs[11:13], *refs[16:])
    shared, count, pos_out, loss_out = refs[7], refs[8], refs[13], refs[14]
    pos_out[...] = shared[:GROUP, :]
    loss_out[...] = shared[GROUP : GROUP + 1, 0:1] / (count[0:1, 0:1] * MODEL)


def seg_vec_kernel(where, vecs, vecs_got, vec_out, flat):
    rank = where[0] * PLANE + where[1]
    rows = (8 * MODEL + FF) // MODEL
    pieces = [vecs[at : at + 1, :] + vecs_got[at : at + 1, :] for at in range(rows)]
    own_vector(rank, pieces, vec_out, flat)


def column_copies(where, out, base, size, own, got, first):
    core_at = where[2]
    lanes = slice(first, first + size)
    return [
        (own.at[:, lanes], out.at[:, pl.ds(aligned(base + core_at * size), size)]),
        (got.at[:, lanes], out.at[:, pl.ds(aligned(base + (1 - core_at) * size), size)]),
    ]


def store_kernel(where, attn, attn_got, mlp, mlp_got, vecs, vecs_got, out, vec_out, flat, sems):
    pairs = []
    for piece in range(4):
        pairs += column_copies(where, out, piece * MODEL, HALF, attn, attn_got, piece * HALF)
    for piece in range(2):
        base = 4 * MODEL + piece * FF
        pairs += column_copies(where, out, base, FF_HALF, mlp, mlp_got, piece * FF_HALF)
    copies = [
        pltpu.make_async_copy(source, target, sems.at[at])
        for at, (source, target) in enumerate(pairs)
    ]
    for copy in copies:
        copy.start()
    seg_vec_kernel(where, vecs, vecs_got, vec_out, flat)
    wait_all(copies)


def plane_parts(part):
    return (part,) + together(*(in_plane(part, mask) for mask in range(1, PLANE)))


def line_parts(part):
    return (part,) + together(*(along_line(part, apart) for apart in range(1, LINE)))


def slice_local(
    hidden_in,
    targets,
    doc_ids,
    seg_nums,
    valid_flags,
    seg_mats,
    seg_vecs,
    cls_mats,
    cls_vecs,
    seg_pos,
):
    rank, core_at = lax.axis_index("fsdp"), lax.axis_index("rep")
    line_at, plane_at = rank // PLANE, rank % PLANE
    where = jnp.stack([line_at, plane_at, core_at, doc_ids[0], seg_nums[0]]).astype(jnp.int32)
    own_rows, total_columns = seg_mats.shape
    vec_size = seg_vecs.shape[0]
    both_rows = CORES * SEG

    first_piece, live_row, *rest = run_kernel(
        prepare_kernel,
        "prepare",
        [shape_of((own_rows, FIRST), LOW), shape_of((1, SEG))]
        + [shape_of((own_rows, FF_HALF), LOW)] * 2
        + [shape_of((own_rows, QUARTER_HALF), LOW)] * LINE
        + [shape_of((own_rows, HALF), LOW), shape_of((MODEL, PLANE * SPAN), LOW)],
        where,
        (seg_mats, cls_mats),
        (jnp.stack([seg_vecs, cls_vecs]).astype(WIDE), valid_flags[None]),
        [
            pltpu.SemaphoreType.DMA((4,)),
            pltpu.VMEM((LINE, own_rows, QUARTER), LOW),
            pltpu.SemaphoreType.DMA((3 + 5 * LINE,)),
        ],
    )
    first_line = line_parts(first_piece)
    second_piece, third_piece, quarters, cls_out_piece, order = (
        rest[0],
        rest[1],
        rest[2:-2],
        rest[-2],
        rest[-1],
    )

    def joined(*pieces):
        return jnp.concatenate(pieces, axis=1)

    def sent_both(to_x, to_y):
        to_x, to_y = together(to_x, to_y)
        return together(in_plane(to_x, 1), in_plane(to_y, 2))

    own_sent = joined(first_piece, second_piece, third_piece)
    own_x, own_y = sent_both(own_sent, own_sent)
    first_line = first_line[:1] + tuple(after(got, own_x, own_y) for got in first_line[1:])
    to_x = joined(own_y[:, OWN_CUT:], *first_line[1:])
    to_y = joined(own_x[:, :OWN_CUT], *first_line[1:])
    first_x, first_y = sent_both(to_x, to_y)
    hidden_got = other_core(after(hidden_in, to_x, to_y))
    live_got = other_core(after(live_row, to_x, to_y))
    second_line = line_parts(after(second_piece, hidden_got, live_got, to_x, to_y))

    def halves(group, from_x, from_y):
        width, cut = WIDTHS[group], LINE_CUTS[group]
        if group == 0:
            base_x, base_y = sum(WIDTHS) - OWN_CUT, OWN_CUT
        else:
            before, before_cut = WIDTHS[group - 1], LINE_CUTS[group - 1]
            base_x, base_y = 2 * before - before_cut, before + before_cut
        return (
            from_y[:, base_y + width + cut : base_y + 3 * width],
            from_x[:, base_x : base_x + width + cut],
        )

    high, low = halves(0, first_x, first_y)
    to_x, to_y = joined(high, *second_line[1:]), joined(low, *second_line[1:])
    second_x, second_y = sent_both(to_x, to_y)
    third_line = line_parts(after(third_piece, to_x, to_y))
    high, low = halves(1, second_x, second_y)
    to_x, to_y = joined(high, *third_line[1:]), joined(low, *third_line[1:])
    third_x, third_y = sent_both(to_x, to_y)
    own_parts = (own_x, own_y, first_x, first_y)
    cls_line = (quarters[0],) + tuple(
        along_line(after(quarters[apart], to_x, to_y), apart)
        for apart in range(1, LINE)
    )

    qkv_weight, out_low, out_high, qkv, mixed, vectors, count, hidden_ordered = run_kernel(
        qkv_kernel,
        "seg_qkv",
        [
            shape_of((GROUP, own_rows, 3 * HALF), LOW),
            shape_of((GROUP // 2, own_rows, HALF), LOW),
            shape_of((GROUP // 2, own_rows, HALF), LOW),
            shape_of((both_rows, 3 * HALF), LOW),
            shape_of((both_rows, HALF), LOW),
            shape_of((2 * (8 * MODEL + FF) // MODEL, MODEL)),
            shape_of((8, LANES)),
            shape_of((both_rows, PLANE * SPAN), LOW),
        ],
        where,
        (),
        first_line
        + own_parts
        + (first_x, first_y, second_x, second_y)
        + (hidden_in, hidden_got, live_row, live_got, order),
        [
            pltpu.VMEM((GROUP, own_rows, LANES), LOW),
            pltpu.VMEM((2, 8 * MODEL + FF), WIDE),
            pltpu.VMEM((both_rows, MODEL), LOW),
            pltpu.VMEM((GROUP, own_rows, HALF), LOW),
        ],
        flops=2 * SEG * MODEL * 3 * MODEL,
    )
    out_weight, mixed_ordered, normed_first, inv_first, first_low = run_kernel(
        out_kernel,
        "seg_out",
        [
            shape_of((MODEL, MODEL), LOW),
            shape_of((both_rows, PLANE * SPAN), LOW),
            shape_of((SEG, MODEL)),
            shape_of((SEG, 1)),
            shape_of((SEG, MODEL), LOW),
        ],
        where,
        (),
        (
            hidden_in,
            mixed,
            after(other_core(mixed), third_x, third_y),
            out_low,
            out_high,
            other_core(out_low),
            other_core(out_high),
            vectors,
            order,
        ),
        [pltpu.VMEM((both_rows, MODEL), LOW)],
        flops=2 * SEG * MODEL * MODEL,
    )
    fourth_x, fourth_y = sent_both(*halves(2, third_x, third_y))
    first_got = after(other_core(first_low), fourth_x, fourth_y)
    count = count + other_core(after(count, first_got))
    up_weight, act, slope = run_kernel(
        up_kernel,
        "seg_up",
        [
            shape_of((GROUP, own_rows, FF_HALF), LOW),
            shape_of((both_rows, FF_HALF), LOW),
            shape_of((both_rows, FF_HALF)),
        ],
        where,
        (),
        second_line
        + own_parts
        + (second_x, second_y, third_x, third_y)
        + (first_low, first_got, vectors),
        [pltpu.VMEM((both_rows, MODEL), LOW)],
        flops=2 * SEG * MODEL * FF,
    )
    cls_sent = joined(*cls_line, cls_out_piece)
    cls_sent = after(cls_sent, act)
    cls_x, cls_y = sent_both(cls_sent, cls_sent)
    down_weight, down_own, down_send = run_kernel(
        down_kernel,
        "seg_down",
        [
            shape_of((GROUP, own_rows, FF_HALF), LOW),
            shape_of((SEG, MODEL)),
            shape_of((SEG, MODEL)),
        ],
        where,
        (),
        third_line + own_parts + (third_x, third_y, fourth_x, fourth_y) + (act,),
        flops=2 * SEG * MODEL * FF,
    )
    normed_second, inv_second, diff, out_rows, head_row = run_kernel(
        seg_rows_kernel,
        "seg_rows",
        [
            shape_of((SEG, MODEL)),
            shape_of((SEG, 1)),
            shape_of((SEG, MODEL)),
            shape_of((SEG, MODEL)),
            shape_of((1, 2 * MODEL + LANES)),
        ],
        where,
        (),
        (
            down_own,
            other_core(down_send),
            normed_first,
            vectors,
            targets,
            live_row,
            seg_pos,
        ),
    )
    head_planes = plane_parts(head_row)
    head_lines = line_parts(jnp.concatenate(head_planes))
    size = LINE // 2 * QUARTER_HALF
    cls_far = sent_both(
        after(cls_y[:, size:], *head_planes[1:]), after(cls_x[:, :size], *head_planes[1:])
    )

    second_grad, second_low, second_sums = run_kernel(
        second_norm_kernel,
        "seg_second_norm",
        [shape_of((SEG, MODEL)), shape_of((SEG, MODEL), LOW), shape_of((3, MODEL))],
        where,
        (),
        (diff, count, normed_second, inv_second, vectors),
    )
    second_got = other_core(second_low)
    pre, first_grad_own, first_grad_send, up_sums = run_kernel(
        mlp_back_kernel,
        "seg_mlp_back",
        [
            shape_of((both_rows, FF_HALF), LOW),
            shape_of((SEG, MODEL)),
            shape_of((SEG, MODEL)),
            shape_of((FF_HALF // MODEL, MODEL)),
        ],
        where,
        (),
        (second_low, second_got, down_weight, up_weight, slope),
        [pltpu.VMEM((both_rows, MODEL), LOW)],
        flops=4 * SEG * MODEL * FF,
    )
    first_grad_got = other_core(first_grad_send)

    def part_shapes(columns):
        return [
            shape_of((count_of, own_rows, columns), LOW)
            for count_of in (LINE // 2, LINE // 2, LINE, LINE, LINE)
        ]

    head_lines = head_lines[:1] + together(*(after(got, pre) for got in head_lines[1:]))
    cls_far = together(*(after(got, *head_lines[1:]) for got in cls_far))
    cls_half, cls_out_half = run_kernel(
        cls_gather_kernel,
        "head_gather",
        [
            shape_of((GROUP, own_rows, QUARTER_HALF), LOW),
            shape_of((PLANE, own_rows, HALF), LOW),
        ],
        where,
        (),
        cls_line + (cls_x, cls_y) + cls_far + (cls_out_piece,),
    )
    mlp_parts = run_kernel(
        mlp_weight_kernel,
        "seg_mlp_weight",
        part_shapes(FF),
        where,
        (),
        (first_low, first_got, second_low, second_got, after(pre, cls_half), act),
        [
            pltpu.VMEM((both_rows, MODEL), LOW),
            pltpu.VMEM((GROUP, own_rows, FF), LOW),
            pltpu.SemaphoreType.DMA((GROUP,)),
        ],
        far=range(5),
        flops=4 * SEG * MODEL * FF,
    )
    mlp_far = reduce_far(tuple(after(part, *cls_far) for part in mlp_parts[:2]))
    cls_weight, cls_out = run_kernel(
        cls_weight_kernel,
        "head_weight",
        [
            shape_of((GROUP, own_rows, QUARTER), LOW),
            shape_of((4, HEAD_DIM, MODEL), LOW),
        ],
        where,
        (),
        (cls_half, other_core(cls_half), cls_out_half, other_core(cls_out_half)),
    )
    cls_weight = cls_weight.reshape(MODEL, QUARTER)
    cls_out = cls_out.reshape(SPAN, MODEL)
    heads, cls_qkv, cls_mixed, part = run_kernel(
        cls_attend_kernel,
        "head_attend",
        [
            shape_of((GROUP, 2 * MODEL + LANES)),
            shape_of((GROUP, 3 * SPAN), LOW),
            shape_of((GROUP, SPAN), LOW),
            shape_of((GROUP, MODEL)),
        ],
        where,
        (),
        tuple(after(got, mlp_parts[0], first_grad_got) for got in head_lines)
        + (vectors, cls_weight, cls_out),
    )
    cls_normed, cls_inv, cls_low, cls_act, cls_slope, part, *mlp_sent = run_kernel(
        head_mlp_kernel,
        "head_mlp",
        [
            shape_of((GROUP, MODEL)),
            shape_of((GROUP, 1)),
            shape_of((GROUP, MODEL), LOW),
            shape_of((GROUP, FF // LINE), LOW),
            shape_of((GROUP, FF // LINE)),
            shape_of((GROUP, MODEL)),
            shape_of(mlp_parts[2].shape, LOW),
            shape_of(mlp_parts[2].shape, LOW),
        ],
        where,
        (),
        (heads,) + line_parts(part) + (vectors, cls_weight) + mlp_far + tuple(mlp_parts[2:4]),
    )
    mlp_plane = sent_both(*mlp_sent)
    cls_parts = line_parts(part)
    top_row, square, cls_grad, cls_second, cls_pre, part, top_sums = run_kernel(
        cls_top_kernel,
        "head_top",
        [
            shape_of((1, MODEL)),
            shape_of((8, LANES)),
            shape_of((GROUP, MODEL)),
            shape_of((GROUP, MODEL), LOW),
            shape_of((GROUP, FF // LINE), LOW),
            shape_of((GROUP, MODEL)),
            shape_of((2, MODEL)),
        ],
        where,
        (),
        (heads,)
        + cls_parts
        + (vectors, cls_weight, cls_normed, count, cls_slope),
        [pltpu.VMEM((GROUP, MODEL), WIDE)],
    )
    top_parts = line_parts(part)
    cls_grad, cls_branch, cls_proj, part, back_sums = run_kernel(
        cls_attend_back_kernel,
        "head_attend_back",
        [
            shape_of((GROUP, MODEL)),
            shape_of((GROUP, MODEL), LOW),
            shape_of((GROUP, 3 * SPAN), LOW),
            shape_of((GROUP, MODEL)),
            shape_of((2, MODEL)),
        ],
        where,
        (),
        (heads,)
        + top_parts
        + (vectors, cls_weight, cls_out, cls_grad, cls_normed, cls_inv, cls_qkv),
    )
    end_parts = line_parts(part)
    pack = jnp.concatenate([cls_proj, cls_mixed, cls_pre, cls_act], axis=1)
    folded = [shape_of((own_rows, FF))] + [shape_of((own_rows + GROUP, FF), LOW)] * (LINE - 1)
    dheads, head_grad, shared, mlp_own, *mlp_sent = run_kernel(
        head_end_kernel,
        "head_end",
        [shape_of((1, MODEL)), shape_of((1, MODEL)), shape_of((GROUP + 8, MODEL))] + folded,
        where,
        (),
        (heads, cls_grad)
        + end_parts
        + (square, back_sums, top_sums, normed_second, inv_second, vectors)
        + (mlp_parts[4],)
        + mlp_plane
        + (pack,),
        [pltpu.VMEM((GROUP, MODEL), WIDE)],
    )
    got_three = along_line(mlp_sent[2], 3)
    mlp_last = mlp_sent[0]
    mlp_middle = mlp_sent[1]
    mlp_got = [None, None, got_three]

    head_own, head_send, head_data = run_kernel(
        head_back_kernel,
        "seg_head_back",
        [shape_of((1, MODEL)), shape_of((1, MODEL)), shape_of((12, MODEL))],
        where,
        (),
        (
            head_grad,
            other_core(head_grad),
            down_weight,
            up_weight,
            slope,
            act,
            first_low,
            first_got,
        ),
    )
    grad_summed, branch, mixed_grad, attn_send, first_sums = run_kernel(
        first_norm_kernel,
        "seg_first_norm",
        [
            shape_of((SEG, MODEL)),
            shape_of((SEG, MODEL), LOW),
            shape_of((SEG, MODEL), LOW),
            shape_of((SEG, MODEL), LOW),
            shape_of((3, MODEL)),
        ],
        where,
        (),
        (
            second_grad,
            first_grad_own,
            first_grad_got,
            head_grad,
            head_own,
            other_core(head_send),
            normed_first,
            inv_first,
            vectors,
            out_weight,
        ),
    )
    attn_got = other_core(attn_send)
    proj, input_own, input_send, payload = run_kernel(
        attn_back_kernel,
        "seg_attn_back",
        [
            shape_of((both_rows, 3 * HALF), LOW),
            shape_of((SEG, MODEL)),
            shape_of((SEG, MODEL)),
            shape_of((24, MODEL), LOW),
        ],
        where,
        (),
        (
            qkv,
            mixed_grad,
            attn_got,
            live_row,
            live_got,
            qkv_weight,
            first_sums,
            second_sums,
            up_sums,
            dheads,
            normed_second,
            head_data,
        ),
        [pltpu.VMEM((24, MODEL), WIDE)],
        flops=4 * SEG * MODEL * 3 * MODEL,
    )
    attn_data = (hidden_ordered, mixed_ordered, proj, branch, attn_got)
    attn_far = run_kernel(
        attn_far_kernel,
        "seg_attn_far",
        part_shapes(4 * HALF)[:2],
        where,
        (),
        attn_data,
        flops=SEG * MODEL * 2 * MODEL,
    )
    attn_far = reduce_far(tuple(after(part, mlp_got[-1]) for part in attn_far))
    attn_near = run_kernel(
        attn_near_kernel,
        "seg_attn_near",
        part_shapes(4 * HALF)[2:] + [shape_of((SEG, MODEL), LOW)],
        where,
        (),
        attn_data + (top_row, out_rows, live_row),
        flops=3 * SEG * MODEL * 2 * MODEL,
    )
    payload_parts = line_parts(after(payload, proj))
    got_two = along_line(after(mlp_middle, *payload_parts[1:]), 2)
    mlp_got[:2] = [along_line(after(mlp_last, got_two), 1), got_two]
    output = attn_near[3]
    *attn_sent, input_grad = run_kernel(
        attn_add_kernel,
        "seg_attn_add",
        [shape_of(attn_near[0].shape, LOW)] * 2 + [shape_of((SEG, MODEL), LOW)],
        where,
        (),
        attn_far
        + tuple(attn_near[:2])
        + (grad_summed, input_own, other_core(input_send)),
    )
    attn_plane = sent_both(*attn_sent)
    mlp_got = [after(got, attn_plane[0]) for got in mlp_got]
    mlp_sum = reduce_line(mlp_own, mlp_got)
    shared = shared + other_core(after(shared, attn_sent[0]))
    row_width = 8 * MODEL + 2 * FF
    cls_rows = run_kernel(
        cls_rows_kernel,
        "head_rows",
        [shape_of((GROUP, row_width), LOW)],
        where,
        (),
        (pack,) + tuple(mlp_got) + (heads, cls_branch, cls_low, cls_second),
        [pltpu.VMEM((LINE,) + pack.shape, LOW)],
    )[0]
    cls_got = other_core(cls_rows)
    attn_plane = tuple(after(got, output, input_grad, shared) for got in attn_plane)
    attn_own, *attn_sent = reduce_fold(where, attn_near[2], attn_plane)
    attn_lines = list(
        together(*(along_line(attn_sent[apart - 1], apart) for apart in range(1, LINE)))
    )
    flat = pltpu.VMEM((1, 8 * MODEL + FF), WIDE)
    payload_line = jnp.concatenate(payload_parts)
    mlp_mine, own_vecs, cls_mats_grad, cls_vec_grad, pos_total, loss_value = run_kernel(
        share_owner_kernel,
        "head_owner",
        [
            shape_of((own_rows, FF)),
            shape_of((16, MODEL)),
            shape_of((own_rows, total_columns)),
            shape_of((vec_size,)),
            shape_of((GROUP, MODEL)),
            shape_of((1, 1)),
        ],
        where,
        (),
        tuple(after(got, attn_own) for got in plane_parts(after(payload_line, *attn_plane)))
        + (mlp_sum, cls_rows, cls_got, shared, count),
        [
            pltpu.VMEM((GROUP * 24, MODEL), LOW),
            pltpu.VMEM((CORES * GROUP, row_width), LOW),
            flat,
        ],
        flops=64 * own_rows * total_columns,
    )
    loss_value = loss_value.reshape(())
    attn_lines = together(*(after(got, mlp_mine) for got in attn_lines))
    attn_sum = reduce_line(attn_own, attn_lines)
    seg_mats_grad, seg_vec_grad = run_kernel(
        store_kernel,
        "seg_owner",
        [shape_of((own_rows, total_columns)), shape_of((vec_size,))],
        where,
        (),
        (attn_sum, other_core(attn_sum), mlp_mine, other_core(mlp_mine))
        + (own_vecs, other_core(own_vecs)),
        [flat, pltpu.SemaphoreType.DMA((12,))],
        far=(0,),
    )

    return (
        output,
        input_grad,
        seg_mats_grad,
        seg_vec_grad,
        cls_mats_grad,
        cls_vec_grad,
        pos_total,
        loss_value,
    )


def solution(mesh):
    in_specs = (
        P(("rep", "fsdp"), None),
        P(("rep", "fsdp"), None),
        P(("rep", "fsdp")),
        P(("rep", "fsdp")),
        P(("rep", "fsdp")),
        P("fsdp", None),
        P("fsdp"),
        P("fsdp", None),
        P("fsdp"),
        P(),
    )
    out_specs = (
        P(("rep", "fsdp"), None),
        P(("rep", "fsdp"), None),
        P("fsdp", None),
        P("fsdp"),
        P("fsdp", None),
        P("fsdp"),
        P(),
        P(),
    )
    one_slice = dict(mesh.shape) == {"rep": CORES, "fsdp": LINE * PLANE}
    body = slice_local if one_slice else local
    return jax.shard_map(body, mesh=mesh, in_specs=in_specs, out_specs=out_specs, check_vma=False)
```

```python
import math

import jax
import jax.numpy as jnp
from jax import lax
from jax.experimental import pallas as pl
from jax.experimental.pallas import tpu as pltpu
from jax.sharding import PartitionSpec as P

HEADS = 12
HEAD_DIM = 64
FF = 3072
SEG = 128
SEQ = 2048


NORM_EPS = 1e-05
MASK_FILL = -1e30
SQRT_HALF = 0.7071067811865476
INV_SQRT_TWO_PI = 0.3989422804014327


def swapped(value, axis, apart):
    mask = 2**apart
    pairs = [(source, source ^ mask) for source in range(lax.axis_size(axis))]
    return lax.ppermute(value, axis, pairs)


def product_plain(left_side, right_side):
    return jnp.dot(left_side, right_side, preferred_element_type=jnp.float32)


def product_left(left_side, right_side):
    return lax.dot_general(
        left_side, right_side, (((0,), (0,)), ((), ())), preferred_element_type=jnp.float32
    )


def product_right(left_side, right_side):
    return lax.dot_general(
        left_side, right_side, (((1,), (1,)), ((), ())), preferred_element_type=jnp.float32
    )


def row_total(array_in):
    return jnp.sum(array_in.astype(jnp.float32), axis=0)


def unpack_weights(gathered, model_width, ff_width):
    matrix, vector = gathered
    vector = vector.astype(jnp.float32)
    pieces = tuple(
        (vector[offset * model_width : (offset + 1) * model_width] for offset in range(8))
    )
    return (
        (
            matrix[:, : 3 * model_width],
            matrix[:, 3 * model_width : 4 * model_width],
            matrix[:, 4 * model_width : 4 * model_width + ff_width],
            matrix[:, 4 * model_width + ff_width :],
        )
        + pieces
        + (vector[8 * model_width :],)
    )


def norm_forward(summed, gain_vec, shift_vec):
    row_mean = jnp.mean(summed, axis=-1, keepdims=True)
    centered = summed - row_mean
    inv_dev = lax.rsqrt(jnp.mean(centered * centered, axis=-1, keepdims=True) + NORM_EPS)
    normed = centered * inv_dev
    return (normed * gain_vec + shift_vec, normed, inv_dev)


def norm_backward(grad_out, normed, inv_dev, gain_vec):
    scaled = grad_out * gain_vec
    mean_one = jnp.mean(scaled, axis=-1, keepdims=True)
    mean_two = jnp.mean(scaled * normed, axis=-1, keepdims=True)
    grad_in = inv_dev * (scaled - mean_one - normed * mean_two)
    return (grad_in, jnp.sum(grad_out * normed, axis=0), jnp.sum(grad_out, axis=0))


def gelu_value(before):
    return 0.5 * before * (1.0 + lax.erf(before * SQRT_HALF))


def gelu_slope(before):
    return (
        0.5 * (1.0 + lax.erf(before * SQRT_HALF))
        + before * jnp.exp(-0.5 * before * before) * INV_SQRT_TWO_PI
    )


def attention_scores(queries, keys_in, allowed, score_scale):
    raw_scores = (
        jnp.einsum("bqhe,bkhe->bhqk", queries, keys_in, preferred_element_type=jnp.float32)
        * score_scale
    )
    return jnp.where(allowed, raw_scores, MASK_FILL)


def attention_forward(queries, keys_in, values, allowed, score_scale):
    scores = attention_scores(queries, keys_in, allowed, score_scale)
    row_top = jnp.max(scores, axis=-1, keepdims=True)
    log_total = row_top + jnp.log(jnp.sum(jnp.exp(scores - row_top), axis=-1, keepdims=True))
    weights = jnp.exp(scores - log_total).astype(jnp.bfloat16)
    mixed_rows = jnp.einsum("bhqk,bkhe->bqhe", weights, values, preferred_element_type=jnp.float32)
    return (mixed_rows, log_total)


def attention_backward(queries, keys_in, values, allowed, score_scale, log_total, grad_mixed):
    probabilities = jnp.exp(attention_scores(queries, keys_in, allowed, score_scale) - log_total)
    grad_probs = jnp.einsum(
        "bqhe,bkhe->bhqk", grad_mixed, values, preferred_element_type=jnp.float32
    )
    inner_sum = jnp.sum(grad_probs * probabilities, axis=-1, keepdims=True)
    grad_scores = (probabilities * (grad_probs - inner_sum)).astype(jnp.bfloat16)
    grad_query = (
        jnp.einsum("bhqk,bkhe->bqhe", grad_scores, keys_in, preferred_element_type=jnp.float32)
        * score_scale
    )
    grad_key = (
        jnp.einsum("bhqk,bqhe->bkhe", grad_scores, queries, preferred_element_type=jnp.float32)
        * score_scale
    )
    grad_value = jnp.einsum(
        "bhqk,bqhe->bkhe",
        probabilities.astype(jnp.bfloat16),
        grad_mixed,
        preferred_element_type=jnp.float32,
    )
    return (grad_query, grad_key, grad_value)


def block_forward(rows_in, unpacked, attend):
    (
        qkv_weight,
        out_weight,
        up_weight,
        down_weight,
        query_bias,
        value_bias,
        out_bias,
        down_bias,
        gain_first,
        shift_first,
        gain_second,
        shift_second,
        up_bias,
    ) = unpacked
    model_width = rows_in.shape[1]
    inputs = rows_in.astype(jnp.bfloat16)
    projected = product_plain(inputs, qkv_weight)
    queries = (projected[:, :model_width] + query_bias).astype(jnp.bfloat16)
    keys_in = projected[:, model_width : 2 * model_width].astype(jnp.bfloat16)
    values = (projected[:, 2 * model_width :] + value_bias).astype(jnp.bfloat16)
    mixed_rows, attend_kept = attend(queries, keys_in, values)
    mixed_rows = mixed_rows.astype(jnp.bfloat16)
    summed_first = rows_in + product_plain(mixed_rows, out_weight) + out_bias
    first_out, normed_first, inv_first = norm_forward(summed_first, gain_first, shift_first)
    first_low = first_out.astype(jnp.bfloat16)
    pre_act = product_plain(first_low, up_weight) + up_bias
    activated = gelu_value(pre_act).astype(jnp.bfloat16)
    summed_second = first_out + product_right(activated, down_weight) + down_bias
    block_out, normed_second, inv_second = norm_forward(summed_second, gain_second, shift_second)
    saved_state = (
        inputs,
        queries,
        keys_in,
        values,
        attend_kept,
        mixed_rows,
        normed_first,
        inv_first,
        first_low,
        pre_act,
        activated,
        normed_second,
        inv_second,
    )
    return (block_out, saved_state)


def block_backward(grad_out, unpacked, saved_state, attend_back):
    (
        qkv_weight,
        out_weight,
        up_weight,
        down_weight,
        query_bias,
        value_bias,
        out_bias,
        down_bias,
        gain_first,
        shift_first,
        gain_second,
        shift_second,
        up_bias,
    ) = unpacked
    (
        inputs,
        queries,
        keys_in,
        values,
        attend_kept,
        mixed_rows,
        normed_first,
        inv_first,
        first_low,
        pre_act,
        activated,
        normed_second,
        inv_second,
    ) = saved_state
    grad_second, grad_gain_second, grad_shift_second = norm_backward(
        grad_out, normed_second, inv_second, gain_second
    )
    second_low = grad_second.astype(jnp.bfloat16)
    grad_pre = (product_plain(second_low, down_weight) * gelu_slope(pre_act)).astype(jnp.bfloat16)
    grad_first = grad_second + product_right(grad_pre, up_weight)
    grad_summed, grad_gain_first, grad_shift_first = norm_backward(
        grad_first, normed_first, inv_first, gain_first
    )
    branch_low = grad_summed.astype(jnp.bfloat16)
    grad_mixed = product_right(branch_low, out_weight).astype(jnp.bfloat16)
    grad_query, grad_key, grad_value = attend_back(
        queries, keys_in, values, attend_kept, grad_mixed
    )
    grad_proj = jnp.concatenate([grad_query, grad_key, grad_value], axis=1)
    grad_rows = grad_summed + product_right(grad_proj, qkv_weight)
    vector_grad = jnp.concatenate(
        [
            row_total(grad_query),
            row_total(grad_value),
            row_total(branch_low),
            row_total(second_low),
            grad_gain_first,
            grad_shift_first,
            grad_gain_second,
            grad_shift_second,
            row_total(grad_pre),
        ]
    )
    weight_rows = (
        inputs,
        grad_proj,
        mixed_rows,
        branch_low,
        first_low,
        grad_pre,
        second_low,
        activated,
    )
    return (grad_rows, weight_rows, vector_grad)


def weight_products(weight_rows):
    inputs, grad_proj, mixed_rows, branch_low, first_low, grad_pre, second_low, activated = (
        weight_rows
    )
    return (
        product_left(inputs, grad_proj),
        product_left(mixed_rows, branch_low),
        product_left(first_low, grad_pre),
        product_left(second_low, activated),
    )


def local(
    hidden_in,
    targets,
    doc_ids,
    seg_nums,
    valid_flags,
    seg_mats,
    seg_vecs,
    cls_mats,
    cls_vecs,
    seg_pos,
):
    tok_rows, model_width = hidden_in.shape
    ff_width = FF
    seg_len = SEG
    group_span = SEQ // tok_rows
    seg_count = tok_rows // seg_len
    score_scale = HEAD_DIM ** (-0.5)
    head_shape = (HEADS, HEAD_DIM)
    live_rows = valid_flags.astype(jnp.float32)
    rank_full = lax.axis_index("fsdp")
    seg_gathered = (
        lax.all_gather(seg_mats, "fsdp", axis=0, tiled=True),
        lax.all_gather(seg_vecs, "fsdp", axis=0, tiled=True),
    )
    seg_unpacked = unpack_weights(seg_gathered, model_width, ff_width)
    cls_gathered = (
        lax.all_gather(cls_mats, "fsdp", axis=0, tiled=True),
        lax.all_gather(cls_vecs, "fsdp", axis=0, tiled=True),
    )
    cls_unpacked = unpack_weights(cls_gathered, model_width, ff_width)
    seg_allowed = (live_rows.reshape(seg_count, 1, 1, seg_len) > 0.5) | jnp.eye(seg_len, dtype=bool)
    seg_shape = (seg_count, seg_len) + head_shape

    def seg_attend(queries, keys_in, values):
        mixed_rows, log_total = attention_forward(
            queries.reshape(seg_shape),
            keys_in.reshape(seg_shape),
            values.reshape(seg_shape),
            seg_allowed,
            score_scale,
        )
        return (mixed_rows.reshape(tok_rows, model_width), log_total)

    def seg_attend_back(queries, keys_in, values, log_total, grad_mixed):
        grad_parts = attention_backward(
            queries.reshape(seg_shape),
            keys_in.reshape(seg_shape),
            values.reshape(seg_shape),
            seg_allowed,
            score_scale,
            log_total,
            grad_mixed.reshape(seg_shape),
        )
        return tuple(
            (
                grad_part.reshape(tok_rows, model_width).astype(jnp.bfloat16)
                for grad_part in grad_parts
            )
        )

    first_out, seg_saved = block_forward(hidden_in.astype(jnp.float32), seg_unpacked, seg_attend)
    first_grid = first_out.reshape(seg_count, seg_len, model_width)
    position_hot = (seg_nums[:, None] == jnp.arange(seg_pos.shape[0])[None, :]).astype(jnp.float32)
    position_rows = jnp.sum(
        position_hot[:, :, None] * seg_pos.astype(jnp.float32)[None, :, :], axis=1
    )
    heads_in = first_grid[:, 0, :] + position_rows
    lead_live = live_rows.reshape(seg_count, seg_len)[:, 0]
    lead_doc = doc_ids.reshape(seg_count, seg_len)[:, 0]
    lead_labels = jnp.where(lead_live > 0.5, lead_doc, -1).astype(jnp.bfloat16)
    lead_doc_low = lead_doc.astype(jnp.bfloat16)
    bit_count = group_span.bit_length() - 1
    key_total = group_span * seg_count
    own_slot = rank_full % group_span * seg_count + jnp.arange(seg_count)
    query_shape = (1, seg_count) + head_shape
    key_shape = (1, key_total) + head_shape

    def cls_attend(queries, keys_in, values):
        paired = jnp.concatenate([keys_in, values], axis=1)
        labels = lead_labels
        for bit_level in range(bit_count):
            other_pair, other_labels = swapped((paired, labels), "fsdp", bit_level)
            upper_half = rank_full // (1 << bit_level) % 2 == 1
            paired = jnp.where(
                upper_half,
                jnp.concatenate([other_pair, paired]),
                jnp.concatenate([paired, other_pair]),
            )
            labels = jnp.where(
                upper_half,
                jnp.concatenate([other_labels, labels]),
                jnp.concatenate([labels, other_labels]),
            )
        allowed = (labels[None, :] == lead_doc_low[:, None]) | (
            jnp.arange(key_total)[None, :] == own_slot[:, None]
        )
        allowed = allowed[None, None]
        mixed_rows, log_total = attention_forward(
            queries.reshape(query_shape),
            paired[:, :model_width].reshape(key_shape),
            paired[:, model_width:].reshape(key_shape),
            allowed,
            score_scale,
        )
        return (mixed_rows.reshape(seg_count, model_width), (paired, allowed, log_total))

    def cls_attend_back(queries, keys_in, values, attend_kept, grad_mixed):
        paired, allowed, log_total = attend_kept
        grad_query, grad_key, grad_value = attention_backward(
            queries.reshape(query_shape),
            paired[:, :model_width].reshape(key_shape),
            paired[:, model_width:].reshape(key_shape),
            allowed,
            score_scale,
            log_total,
            grad_mixed.reshape(query_shape),
        )
        grad_pair = jnp.concatenate(
            [grad_key.reshape(key_total, model_width), grad_value.reshape(key_total, model_width)],
            axis=1,
        )
        for bit_level in reversed(range(bit_count)):
            half_rows = grad_pair.shape[0] // 2
            upper_half = rank_full // (1 << bit_level) % 2 == 1
            kept_half = jnp.where(upper_half, grad_pair[half_rows:], grad_pair[:half_rows])
            sent_half = jnp.where(upper_half, grad_pair[:half_rows], grad_pair[half_rows:])
            grad_pair = kept_half + swapped(
                sent_half.astype(jnp.bfloat16), "fsdp", bit_level
            ).astype(sent_half.dtype)
        grad_pair = grad_pair.astype(jnp.bfloat16)
        return (
            grad_query.reshape(seg_count, model_width).astype(jnp.bfloat16),
            grad_pair[:, :model_width],
            grad_pair[:, model_width:],
        )

    top_out, cls_saved = block_forward(heads_in, cls_unpacked, cls_attend)
    combined = jnp.concatenate([top_out[:, None, :], first_grid[:, 1:, :]], axis=1).reshape(
        tok_rows, model_width
    )
    output_rows = combined * live_rows[:, None]
    diff_rows = (output_rows - targets.astype(jnp.float32)) * live_rows[:, None]
    count_all, square_all = lax.psum(
        (jnp.sum(live_rows), jnp.sum(diff_rows * diff_rows)), ("rep", "fsdp")
    )
    loss_value = square_all / (count_all * model_width)
    slots_all = tok_rows * lax.axis_size("rep") * lax.axis_size("fsdp")
    grad_grid = (diff_rows * (slots_all / count_all)).reshape(seg_count, seg_len, model_width)
    cls_back = unpack_weights(
        (
            lax.all_gather(cls_mats, "fsdp", axis=0, tiled=True),
            lax.all_gather(cls_vecs, "fsdp", axis=0, tiled=True),
        ),
        model_width,
        ff_width,
    )
    heads_grad, cls_weight_rows, cls_g_vec = block_backward(
        grad_grid[:, 0, :], cls_back, cls_saved, cls_attend_back
    )
    cls_g_qkv, cls_g_out, cls_g_up, cls_g_down = weight_products(cls_weight_rows)
    pos_local = jnp.sum(position_hot[:, :, None] * heads_grad[:, None, :], axis=0)
    seg_grad_out = jnp.concatenate([heads_grad[:, None, :], grad_grid[:, 1:, :]], axis=1).reshape(
        tok_rows, model_width
    )
    seg_back = unpack_weights(
        (
            lax.all_gather(seg_mats, "fsdp", axis=0, tiled=True),
            lax.all_gather(seg_vecs, "fsdp", axis=0, tiled=True),
        ),
        model_width,
        ff_width,
    )
    input_grad, seg_weight_rows, seg_g_vec = block_backward(
        seg_grad_out, seg_back, seg_saved, seg_attend_back
    )
    seg_g_qkv, seg_g_out, seg_g_up, seg_g_down = weight_products(seg_weight_rows)
    owner_rows = tuple(
        (
            lax.psum_scatter(seg_g_qkv, "fsdp", scatter_dimension=0, tiled=True),
            lax.psum_scatter(seg_g_out, "fsdp", scatter_dimension=0, tiled=True),
            lax.psum_scatter(seg_g_up, "fsdp", scatter_dimension=0, tiled=True),
            lax.psum_scatter(seg_g_down, "fsdp", scatter_dimension=0, tiled=True),
            lax.psum_scatter(seg_g_vec, "fsdp", scatter_dimension=0, tiled=True),
            lax.psum_scatter(cls_g_qkv, "fsdp", scatter_dimension=0, tiled=True),
            lax.psum_scatter(cls_g_out, "fsdp", scatter_dimension=0, tiled=True),
            lax.psum_scatter(cls_g_up, "fsdp", scatter_dimension=0, tiled=True),
            lax.psum_scatter(cls_g_down, "fsdp", scatter_dimension=0, tiled=True),
            lax.psum_scatter(cls_g_vec, "fsdp", scatter_dimension=0, tiled=True),
        )
    )
    replica_share = (
        lax.psum_scatter(
            owner_rows[0].astype(jnp.bfloat16), "rep", scatter_dimension=1, tiled=True
        ).astype(jnp.float32),
        lax.psum_scatter(
            owner_rows[1].astype(jnp.bfloat16), "rep", scatter_dimension=1, tiled=True
        ).astype(jnp.float32),
        lax.psum_scatter(
            owner_rows[2].astype(jnp.bfloat16), "rep", scatter_dimension=1, tiled=True
        ).astype(jnp.float32),
        lax.psum_scatter(
            owner_rows[3].astype(jnp.bfloat16), "rep", scatter_dimension=1, tiled=True
        ).astype(jnp.float32),
        lax.psum_scatter(
            owner_rows[4].astype(jnp.bfloat16), "rep", scatter_dimension=0, tiled=True
        ).astype(jnp.float32),
        lax.psum_scatter(
            owner_rows[5].astype(jnp.bfloat16), "rep", scatter_dimension=1, tiled=True
        ).astype(jnp.float32),
        lax.psum_scatter(
            owner_rows[6].astype(jnp.bfloat16), "rep", scatter_dimension=1, tiled=True
        ).astype(jnp.float32),
        lax.psum_scatter(
            owner_rows[7].astype(jnp.bfloat16), "rep", scatter_dimension=1, tiled=True
        ).astype(jnp.float32),
        lax.psum_scatter(
            owner_rows[8].astype(jnp.bfloat16), "rep", scatter_dimension=1, tiled=True
        ).astype(jnp.float32),
        lax.psum_scatter(
            owner_rows[9].astype(jnp.bfloat16), "rep", scatter_dimension=0, tiled=True
        ).astype(jnp.float32),
    )
    all_summed = (
        lax.all_gather(replica_share[0].astype(jnp.bfloat16), "rep", axis=1, tiled=True).astype(
            jnp.float32
        ),
        lax.all_gather(replica_share[1].astype(jnp.bfloat16), "rep", axis=1, tiled=True).astype(
            jnp.float32
        ),
        lax.all_gather(replica_share[2].astype(jnp.bfloat16), "rep", axis=1, tiled=True).astype(
            jnp.float32
        ),
        lax.all_gather(replica_share[3].astype(jnp.bfloat16), "rep", axis=1, tiled=True).astype(
            jnp.float32
        ),
        lax.all_gather(replica_share[4].astype(jnp.bfloat16), "rep", axis=0, tiled=True).astype(
            jnp.float32
        ),
        lax.all_gather(replica_share[5].astype(jnp.bfloat16), "rep", axis=1, tiled=True).astype(
            jnp.float32
        ),
        lax.all_gather(replica_share[6].astype(jnp.bfloat16), "rep", axis=1, tiled=True).astype(
            jnp.float32
        ),
        lax.all_gather(replica_share[7].astype(jnp.bfloat16), "rep", axis=1, tiled=True).astype(
            jnp.float32
        ),
        lax.all_gather(replica_share[8].astype(jnp.bfloat16), "rep", axis=1, tiled=True).astype(
            jnp.float32
        ),
        lax.all_gather(replica_share[9].astype(jnp.bfloat16), "rep", axis=0, tiled=True).astype(
            jnp.float32
        ),
    )
    seg_summed = all_summed[:5]
    cls_summed = all_summed[5:]
    pos_total = lax.psum(pos_local, ("rep", "fsdp"))
    seg_mat_grad = jnp.concatenate(
        [seg_summed[0], seg_summed[1], seg_summed[2], seg_summed[3]], axis=1
    )
    cls_mat_grad = jnp.concatenate(
        [cls_summed[0], cls_summed[1], cls_summed[2], cls_summed[3]], axis=1
    )
    return (
        output_rows.astype(jnp.bfloat16),
        input_grad.astype(jnp.bfloat16),
        seg_mat_grad,
        seg_summed[4],
        cls_mat_grad,
        cls_summed[4],
        pos_total,
        loss_value,
    )


LINE = 4
PLANE = 4
CORES = 2
LANES = 128
GROUP = LINE * PLANE
LOW, WIDE = jnp.bfloat16, jnp.float32
MODEL = HEADS * HEAD_DIM
SPAN = 2 * LANES
TILE_START = (0, 1, 3, 4)


def line_pairs(apart):
    return [(source, (source + apart * PLANE) % GROUP) for source in range(GROUP)]


def plane_pairs(mask):
    return [(source, source ^ mask) for source in range(GROUP)]


def along_line(value, apart):
    return lax.ppermute(value, "fsdp", line_pairs(apart))


def in_plane(value, mask):
    return lax.ppermute(value, "fsdp", plane_pairs(mask))


def other_core(value):
    return lax.ppermute(value, "rep", [(0, 1), (1, 0)])


def after(value, *events):
    return lax.optimization_barrier((value,) + events)[0]


def together(*values):
    return tuple(lax.optimization_barrier(values))


def shape_of(dims, dtype=WIDE):
    return jax.ShapeDtypeStruct(dims, dtype)


def run_kernel(body, name, outs, where, blocks, arrays, scratch=(), far=(), flops=0):
    in_specs = [pl.BlockSpec(memory_space=pltpu.SMEM)]
    in_specs += [pl.BlockSpec(memory_space=pltpu.HBM)] * len(blocks)
    in_specs += [pl.BlockSpec(memory_space=pltpu.VMEM)] * len(arrays)
    spaces = [pltpu.HBM if at in far else pltpu.VMEM for at in range(len(outs))]
    moved = sum(x.size * x.dtype.itemsize for x in list(blocks) + list(arrays))
    moved += sum(math.prod(o.shape) * jnp.dtype(o.dtype).itemsize for o in outs)
    return pl.pallas_call(
        body,
        name=name,
        out_shape=tuple(outs),
        in_specs=in_specs,
        out_specs=tuple(pl.BlockSpec(memory_space=space) for space in spaces),
        scratch_shapes=list(scratch),
        cost_estimate=pl.CostEstimate(flops=flops, bytes_accessed=moved, transcendentals=0),
        compiler_params=pltpu.CompilerParams(vmem_limit_bytes=VMEM_BYTES),
    )(where, *blocks, *arrays)


VMEM_BYTES = 24 * 1024 * 1024
HALF = MODEL // CORES
FF_HALF = FF // CORES
OWN = MODEL // GROUP
QUARTER = 3 * SPAN + 2 * FF // LINE
QUARTER_HALF = QUARTER // CORES


def aligned(start):
    return pl.multiple_of(start, LANES)


def wait_all(copies):
    for copy in copies:
        copy.wait()


def run_copies(pairs, sems):
    copies = [
        pltpu.make_async_copy(source, target, sems.at[at])
        for at, (source, target) in enumerate(pairs)
    ]
    for copy in copies:
        copy.start()
    wait_all(copies)


FIRST = 4 * HALF + LANES
OWN_CUT = FIRST + FF_HALF // 2
LINE_CUTS = (7 * LANES, FF_HALF // 2, FF_HALF // 2)
WIDTHS = (FIRST, FF_HALF, FF_HALF)


def group_pieces(group, refs):
    own, rest = refs[:LINE], refs[LINE:]
    own_x, own_y, far_x, far_y, line_x, line_y, late_x, late_y = rest
    width, cut = WIDTHS[group], LINE_CUTS[group]
    start = sum(WIDTHS[:group])
    if group == 0:
        bases = (sum(WIDTHS) - OWN_CUT, OWN_CUT)
    else:
        before, before_cut = WIDTHS[group - 1], LINE_CUTS[group - 1]
        bases = (2 * before - before_cut, before + before_cut)
    pieces = {(0, step): [(own[step], 0, 0, width)] for step in range(LINE)}
    for mask, whole, line, base in ((1, own_x, line_x, bases[0]), (2, own_y, line_y, bases[1])):
        pieces[mask, 0] = [(whole, start, 0, width)]
        for step in range(1, LINE):
            pieces[mask, step] = [(line, base + (step - 1) * width, 0, width)]
    middle = min(max(OWN_CUT - start, 0), width)
    far = []
    if middle > 0:
        far.append((far_y, start, 0, middle))
    if middle < width:
        far.append((far_x, start + middle - OWN_CUT, middle, width))
    pieces[3, 0] = far
    pieces[3, 1] = [(late_y, 0, 0, width)]
    pieces[3, 2] = [(late_y, width, 0, cut), (late_x, 0, cut, width)]
    pieces[3, 3] = [(late_x, width - cut, 0, width)]
    return pieces


def gather_group(where, group, refs, targets):
    line_at, plane_at = where[0], where[1]
    for (mask, step), parts in group_pieces(group, refs).items():
        chip = (line_at + LINE - step) % LINE * PLANE + (plane_at ^ mask)
        for whole, first, last in targets:
            for ref, offset, begin, end in parts:
                low, high = max(first, begin), min(last, end)
                if low < high:
                    source = slice(offset + low - begin, offset + high - begin)
                    whole[chip, :, low - first : high - first] = ref[:, source]


def gather_blocks(where, refs, base, width, targets):
    line_at, plane_at = where[0], where[1]
    half = LINE // 2
    for mask in range(PLANE):
        for step in range(LINE):
            if mask == 0:
                ref, offset = refs[step], 0
            elif mask == 3:
                ref = refs[LINE + 3] if step < half else refs[LINE + 2]
                offset = step % half * width
            else:
                ref, offset = refs[LINE + mask - 1], base + step * width
            chip = (line_at + LINE - step) % LINE * PLANE + (plane_at ^ mask)
            for whole, first, last in targets:
                whole[chip] = ref[:, offset + first : offset + last]


def whole_rows(ref):
    value = ref[...]
    return value.reshape(value.shape[0] * value.shape[1], value.shape[2])


def prepare_first_kernel(where, seg, vecs, flags, out, live_out, sems):
    core_at = where[2]
    pairs = []
    for piece in range(4):
        source = seg.at[:, pl.ds(aligned(piece * MODEL + core_at * HALF), HALF)]
        pairs.append((source, out.at[:, piece * HALF : (piece + 1) * HALF]))
    run_copies(pairs, sems)
    size = vecs.shape[1]
    lines = -(-size // LANES)
    block = jnp.zeros((OWN, LANES), WIDE)
    row_at = lax.broadcasted_iota(jnp.int32, (OWN, LANES), 0)
    for which in range(2):
        for line in range(lines):
            width = min(LANES, size - line * LANES)
            value = vecs[which : which + 1, line * LANES : line * LANES + width]
            if width < LANES:
                value = jnp.concatenate([value, jnp.zeros((1, LANES - width), WIDE)], axis=1)
            block = jnp.where(row_at == which * lines + line, value, block)
    live = flags[...].astype(WIDE)
    live_out[...] = live
    count = jnp.sum(live, axis=1, keepdims=True)
    block = jnp.where(row_at == 2 * lines, count, block)
    out[:, 4 * HALF :] = block.astype(LOW)


def prepare_rest_kernel(where, seg, cls, *refs):
    second_out, third_out = refs[:2]
    step_outs, out_half, order_out = refs[2 : 2 + LINE], refs[2 + LINE], refs[3 + LINE]
    quarters, sems = refs[4 + LINE :]
    line_at, plane_at, core_at = where[0], where[1], where[2]
    start = core_at * FF_HALF
    pairs = [
        (seg.at[:, pl.ds(aligned(4 * MODEL + start), FF_HALF)], second_out),
        (seg.at[:, pl.ds(aligned(4 * MODEL + FF + start), FF_HALF)], third_out),
        (cls.at[:, pl.ds(aligned(3 * MODEL + core_at * HALF), HALF)], out_half),
    ]
    part = FF // LINE
    for at in range(LINE):
        first = TILE_START[at] * LANES
        plan = [(piece * MODEL + first, SPAN, piece * SPAN) for piece in range(3)]
        plan += [
            (4 * MODEL + piece * FF + at * part, part, 3 * SPAN + piece * part)
            for piece in range(2)
        ]
        for source, size, target in plan:
            pairs.append(
                (
                    cls.at[:, source : source + size],
                    quarters.at[at, :, target : target + size],
                )
            )
    run_copies(pairs, sems)
    lanes = pl.ds(aligned(core_at * QUARTER_HALF), QUARTER_HALF)
    for step, out in enumerate(step_outs):
        out[...] = quarters[(line_at + step) % LINE, :, lanes]
    column = lax.broadcasted_iota(jnp.int32, (1, SPAN), 1)
    feature = lax.broadcasted_iota(jnp.int32, (MODEL, SPAN), 0)
    turn = sum((column >= OWN * step).astype(jnp.int32) for step in range(1, LINE))
    held = column - OWN * turn
    turn = (line_at + turn) % LINE
    for mask in range(PLANE):
        source = (turn * PLANE + (plane_at ^ mask)) * OWN + held
        source = jnp.where(column < OWN * LINE, source, -1)
        order_out[:, mask * SPAN : (mask + 1) * SPAN] = (feature == source).astype(LOW)


def prepare_kernel(where, seg, cls, vecs, flags, first_out, live_out, *refs):
    rest, (first_sems, quarters, sems) = refs[:-3], refs[-3:]
    prepare_first_kernel(where, seg, vecs, flags, first_out, live_out, first_sems)
    prepare_rest_kernel(where, seg, cls, *rest, quarters, sems)


def lane_mask(rows, head):
    lane = lax.broadcasted_iota(jnp.int32, (rows, LANES), 1)
    return (lane < HEAD_DIM) if head == 0 else (lane >= HEAD_DIM)


def masked(value, mask):
    return jnp.where(mask, value, jnp.zeros_like(value))


def head_probabilities(query, key, allowed):
    scores = product_right(query, key) * HEAD_DIM ** (-0.5)
    scores = jnp.where(allowed, scores, MASK_FILL)
    raised = jnp.exp(scores - jnp.max(scores, axis=-1, keepdims=True))
    return raised / jnp.sum(raised, axis=-1, keepdims=True)


def attend_tiles(qkv, width, allowed):
    rows = qkv.shape[0]
    mixed = []
    for tile in range(width // LANES):
        at = tile * LANES
        query, key, value = (
            qkv[:, piece * width + at : piece * width + at + LANES] for piece in range(3)
        )
        total = jnp.zeros((rows, LANES), WIDE)
        for head in range(2):
            mask = lane_mask(rows, head)
            weights = head_probabilities(masked(query, mask), key, allowed).astype(LOW)
            total = total + product_plain(weights, masked(value, mask))
        mixed.append(total.astype(LOW))
    return mixed


def attend_tiles_back(qkv, grad_mixed, width, allowed):
    rows = qkv.shape[0]
    scale = HEAD_DIM ** (-0.5)
    results = ([], [], [])
    for tile in range(width // LANES):
        at = tile * LANES
        query, key, value = (
            qkv[:, piece * width + at : piece * width + at + LANES] for piece in range(3)
        )
        grad = grad_mixed[:, at : at + LANES]
        totals = [jnp.zeros((rows, LANES), WIDE) for _ in range(3)]
        for head in range(2):
            mask = lane_mask(rows, head)
            query_low, key_low, grad_low = (masked(x, mask) for x in (query, key, grad))
            chance = head_probabilities(query_low, key, allowed)
            grad_chance = product_right(grad_low, value)
            inner = jnp.sum(grad_chance * chance, axis=-1, keepdims=True)
            grad_scores = (chance * (grad_chance - inner)).astype(LOW)
            totals[0] = totals[0] + product_plain(grad_scores, key_low)
            totals[1] = totals[1] + product_left(grad_scores, query_low)
            totals[2] = totals[2] + product_left(chance.astype(LOW), grad_low)
        results[0].append((totals[0] * scale).astype(LOW))
        results[1].append((totals[1] * scale).astype(LOW))
        results[2].append(totals[2].astype(LOW))
    return results[0] + results[1] + results[2]


def token_allowed(live_row):
    shape = (SEG, SEG)
    same = lax.broadcasted_iota(jnp.int32, shape, 0) == lax.broadcasted_iota(jnp.int32, shape, 1)
    return (live_row > 0.5) | same


def qkv_kernel(where, *refs):
    blocks = refs[:12]
    hidden, hidden_got, live_row, live_got, order = refs[12:17]
    weight, out_low, out_high, qkv_out, mixed_out = refs[17:22]
    vectors_out, count_out, ordered_out = refs[22:25]
    vec_rows, flat, inputs, out_half = refs[25:]
    core_at = where[2]
    gather_group(
        where,
        0,
        blocks,
        (
            (weight, 0, 3 * HALF),
            (out_half, 3 * HALF, 4 * HALF),
            (vec_rows, 4 * HALF, 4 * HALF + LANES),
        ),
    )
    out_low[...] = out_half[: GROUP // 2]
    out_high[...] = out_half[GROUP // 2 :]
    piece = (8 * MODEL + FF) // GROUP
    lines = -(-piece // LANES)
    count = jnp.zeros((1, LANES), WIDE)
    for chip in range(GROUP):
        rows = vec_rows[chip, 0:16, :].astype(WIDE)
        for block in range(2):
            joined = jnp.concatenate(
                [rows[block * lines + r : block * lines + r + 1] for r in range(lines)], axis=1
            )
            flat[block : block + 1, chip * piece : (chip + 1) * piece] = joined[:, :piece]
        count = count + rows[2 * lines : 2 * lines + 1]
    rows_each = (8 * MODEL + FF) // MODEL
    for block in range(2):
        for row in range(rows_each):
            vectors_out[block * rows_each + row : block * rows_each + row + 1, :] = flat[
                block : block + 1, row * MODEL : (row + 1) * MODEL
            ]
    count_out[...] = jnp.broadcast_to(count, count_out.shape)
    inputs[:SEG] = hidden[...]
    inputs[SEG:] = hidden_got[...]
    projected = product_plain(inputs[...], whole_rows(weight))
    lanes = pl.ds(aligned(core_at * HALF), HALF)
    qkv_out[:, :HALF] = (projected[:, :HALF] + vectors_out[0:1, lanes]).astype(LOW)
    qkv_out[:, HALF : 2 * HALF] = projected[:, HALF : 2 * HALF].astype(LOW)
    qkv_out[:, 2 * HALF :] = (projected[:, 2 * HALF :] + vectors_out[1:2, lanes]).astype(LOW)
    for part, live in enumerate((live_row, live_got)):
        rows = slice(part * SEG, (part + 1) * SEG)
        tiles = attend_tiles(qkv_out[rows, :], HALF, token_allowed(live[...]))
        for tile, value in enumerate(tiles):
            mixed_out[rows, tile * LANES : (tile + 1) * LANES] = value
    ordered_out[...] = product_plain(inputs[...], order[...]).astype(LOW)


def norm_rows(summed):
    row_mean = jnp.mean(summed, axis=-1, keepdims=True)
    centered = summed - row_mean
    inv_dev = lax.rsqrt(jnp.mean(centered * centered, axis=-1, keepdims=True) + NORM_EPS)
    return centered * inv_dev, inv_dev


def norm_rows_back(grad_out, normed, inv_dev, gain):
    scaled = grad_out * gain
    mean_one = jnp.mean(scaled, axis=-1, keepdims=True)
    mean_two = jnp.mean(scaled * normed, axis=-1, keepdims=True)
    return inv_dev * (scaled - mean_one - normed * mean_two)


def column_sum(value):
    return jnp.sum(value.astype(WIDE), axis=0, keepdims=True)


def four_rows(vectors, first):
    return jnp.concatenate([vectors[first + at : first + at + 1, :] for at in range(4)], axis=1)


def gelu_both(before):
    half = 0.5 * (1.0 + lax.erf(before * SQRT_HALF))
    slope = half + before * jnp.exp(-0.5 * before * before) * INV_SQRT_TWO_PI
    return before * half, slope


def out_kernel(where, hidden, mixed, mixed_got, low, high, low_got, high_got, *refs):
    vectors, order, full_out, ordered_out, normed_out, inv_out, low_out, mixed_full = refs
    core_at = where[2]
    own, other = aligned(core_at * HALF), aligned((1 - core_at) * HALF)
    rows = MODEL // 2
    full_out[:rows, pl.ds(own, HALF)] = whole_rows(low)
    full_out[rows:, pl.ds(own, HALF)] = whole_rows(high)
    full_out[:rows, pl.ds(other, HALF)] = whole_rows(low_got)
    full_out[rows:, pl.ds(other, HALF)] = whole_rows(high_got)
    mixed_full[:, pl.ds(own, HALF)] = mixed[...]
    mixed_full[:SEG, pl.ds(other, HALF)] = mixed_got[SEG:, :]
    mixed_full[SEG:, pl.ds(other, HALF)] = mixed_got[:SEG, :]
    branch = product_plain(mixed_full[:SEG, :], full_out[...])
    normed, inv_dev = norm_rows(hidden[...].astype(WIDE) + branch + vectors[2:3, :])
    normed_out[...] = normed
    inv_out[...] = inv_dev
    low_out[...] = (normed * vectors[4:5, :] + vectors[5:6, :]).astype(LOW)
    ordered_out[...] = product_plain(mixed_full[...], order[...]).astype(LOW)


def up_kernel(where, *refs):
    blocks = refs[:12]
    low, low_got, vectors = refs[12:15]
    weight, act_out, slope_out, both = refs[15:]
    core_at = where[2]
    gather_group(where, 1, blocks, ((weight, 0, FF_HALF),))
    both[:SEG] = low[...]
    both[SEG:] = low_got[...]
    for at in range(FF_HALF // MODEL):
        columns = slice(at * MODEL, (at + 1) * MODEL)
        held = weight[:, :, columns]
        before = product_plain(both[...], held.reshape(MODEL, MODEL))
        bias = vectors[pl.ds(8 + core_at * (FF_HALF // MODEL) + at, 1), :]
        value, slope = gelu_both(before + bias)
        act_out[:, columns] = value.astype(LOW)
        slope_out[:, columns] = slope


def down_kernel(where, *refs):
    blocks, act = refs[:12], refs[12]
    weight, own_out, send_out = refs[13:]
    gather_group(where, 2, blocks, ((weight, 0, FF_HALF),))
    partial = product_right(act[...], whole_rows(weight))
    own_out[...] = partial[:SEG]
    send_out[...] = partial[SEG:]


def seg_rows_kernel(where, *refs):
    own, got, normed_first, vectors, targets, live, seg_pos = refs[:7]
    normed_out, inv_out, diff_out, rows_out, head_out = refs[7:]
    doc, number = where[3], where[4]
    first = normed_first[...] * vectors[4:5, :] + vectors[5:6, :]
    normed, inv_dev = norm_rows(first + own[...] + got[...] + vectors[3:4, :])
    normed_out[...] = normed
    inv_out[...] = inv_dev
    rows = normed * vectors[6:7, :] + vectors[7:8, :]
    shape = (SEG, SEG)
    same = lax.broadcasted_iota(jnp.int32, shape, 0) == lax.broadcasted_iota(jnp.int32, shape, 1)
    live_rows = jnp.sum(jnp.where(same, live[...], 0.0), axis=1, keepdims=True)
    target_rows = targets[...].astype(WIDE)
    output = rows * live_rows
    rows_out[...] = output
    diff = (output - target_rows) * live_rows
    row_at = lax.broadcasted_iota(jnp.int32, (SEG, 1), 0)
    diff = jnp.where(row_at > 0, diff, 0.0)
    diff_out[...] = diff
    table = seg_pos[...].astype(WIDE)
    chosen = lax.broadcasted_iota(jnp.int32, table.shape, 0) == number
    position = jnp.sum(jnp.where(chosen, table, 0.0), axis=0, keepdims=True)
    head_out[:, :MODEL] = rows[0:1, :] + position
    head_out[:, MODEL : 2 * MODEL] = target_rows[0:1, :]
    square = jnp.sum(column_sum(diff * diff), axis=1, keepdims=True)
    lane = lax.broadcasted_iota(jnp.int32, (1, LANES), 1)
    facts = jnp.where(lane == 0, live_rows[0:1, :], 0.0)
    facts = jnp.where(lane == 1, doc.astype(WIDE), facts)
    facts = jnp.where(lane == 2, number.astype(WIDE), facts)
    facts = jnp.where(lane == 3, square, facts)
    head_out[:, 2 * MODEL :] = facts


def second_norm_kernel(where, diff, count, normed, inv_dev, vectors, grad_out, low_out, sums_out):
    grad_top = diff[...] * ((SEG * GROUP * CORES) / count[0:1, 0:1])
    normed_rows = normed[...]
    grad = norm_rows_back(grad_top, normed_rows, inv_dev[...], vectors[6:7, :])
    low = grad.astype(LOW)
    grad_out[...] = grad
    low_out[...] = low
    sums_out[0:1, :] = column_sum(low)
    sums_out[1:2, :] = column_sum(grad_top * normed_rows)
    sums_out[2:3, :] = column_sum(grad_top)


def mlp_back_kernel(where, *refs):
    low, low_got, down_weight, up_weight, slope = refs[:5]
    pre_out, own_out, send_out, sums_out, both = refs[5:]
    both[:SEG] = low[...]
    both[SEG:] = low_got[...]
    for at in range(FF_HALF // MODEL):
        columns = slice(at * MODEL, (at + 1) * MODEL)
        held = down_weight[:, :, columns]
        before = product_plain(both[...], held.reshape(MODEL, MODEL))
        pre = (before * slope[:, columns]).astype(LOW)
        pre_out[:, columns] = pre
        sums_out[at : at + 1, :] = column_sum(pre)
    partial = product_right(pre_out[...], whole_rows(up_weight))
    own_out[...] = partial[:SEG]
    send_out[...] = partial[SEG:]


def scatter_parts(where, parts, outs, sems):
    line_at, plane_at = where[0], where[1]
    far_low, far_high, to_x, to_y, kept = outs
    half = LINE // 2
    copies = []
    for mask in range(PLANE):
        for step in range(LINE):
            source = parts.at[(line_at + step) % LINE * PLANE + (plane_at ^ mask)]
            if mask == 3:
                target = far_low.at[step] if step < half else far_high.at[step - half]
            else:
                target = (kept, to_x, to_y)[mask].at[step]
            copies.append(pltpu.make_async_copy(source, target, sems.at[len(copies)]))
    for copy in copies:
        copy.start()
    wait_all(copies)


def mlp_weight_kernel(where, *refs):
    first, first_got, second, second_got, pre, act = refs[:6]
    outs = refs[6:11]
    left, parts, sems = refs[11:]
    for at, (own, got, right) in enumerate(((first, first_got, pre), (second, second_got, act))):
        left[:SEG] = own[...]
        left[SEG:] = got[...]
        for piece in range(FF_HALF // MODEL):
            start = piece * MODEL
            product = product_left(left[...], right[:, start : start + MODEL]).astype(LOW)
            target = at * FF_HALF + start
            parts[:, :, target : target + MODEL] = product.reshape(GROUP, OWN, MODEL)
    scatter_parts(where, parts, outs, sems)


def attn_product(where, refs, mask, piece):
    hidden, mixed, proj, branch, got = refs
    lanes = slice(mask * SPAN, (mask + 1) * SPAN)
    if piece < 3:
        right = proj[:, piece * HALF : (piece + 1) * HALF]
        product = product_left(hidden[:, lanes], right)
    else:
        own = branch[:, pl.ds(aligned(where[2] * HALF), HALF)]
        product = product_left(mixed[:SEG, lanes], own)
        product = product + product_left(mixed[SEG:, lanes], got[:, HALF:])
    return product[: LINE * OWN].astype(LOW).reshape(LINE, OWN, HALF)


def attn_far_kernel(where, *refs):
    low_out, high_out = refs[5:]
    half = LINE // 2
    for piece in range(4):
        columns = slice(piece * HALF, (piece + 1) * HALF)
        product = attn_product(where, refs[:5], 3, piece)
        low_out[:, :, columns] = product[:half]
        high_out[:, :, columns] = product[half:]


def attn_near_kernel(where, *refs):
    top_row, out_rows, live_row = refs[5:8]
    row_at = lax.broadcasted_iota(jnp.int32, (SEG, 1), 0)
    output = jnp.where(row_at == 0, top_row[...] * live_row[:, 0:1], out_rows[...])
    refs[11][...] = output.astype(LOW)
    for mask, out in ((1, refs[8]), (2, refs[9]), (0, refs[10])):
        for piece in range(4):
            columns = slice(piece * HALF, (piece + 1) * HALF)
            out[:, :, columns] = attn_product(where, refs[:5], mask, piece)


def fold_kernel(where, kept, got_x, got_y, *refs):
    extra, own_out, sent = refs[: -LINE], refs[-LINE], refs[1 - LINE :]
    rows = kept.shape[1]
    for step in range(LINE):
        total = kept[step].astype(WIDE) + got_x[step].astype(WIDE) + got_y[step].astype(WIDE)
        if step == 0:
            own_out[...] = total
            continue
        out = sent[step - 1]
        out[:rows, :] = total.astype(LOW)
        if extra:
            out[rows:, :] = jnp.zeros_like(out[rows:, :])
            out[rows:, : extra[0].shape[1]] = extra[0][...]


def reduce_far(parts):
    return together(in_plane(parts[0], 2), in_plane(parts[1], 1))


def reduce_add(where, parts, far):
    shape = parts[2].shape
    return run_kernel(
        add_far_kernel,
        "add_far",
        [shape_of(shape, LOW)] * 2,
        where,
        (),
        tuple(far) + (parts[2], parts[3]),
    )


def reduce_fold(where, kept, got, *extra):
    _, rows, columns = kept.shape
    more = sum(value.shape[0] for value in extra)
    return run_kernel(
        fold_kernel,
        "fold",
        [shape_of((rows, columns))] + [shape_of((rows + more, columns), LOW)] * (LINE - 1),
        where,
        (),
        (kept,) + tuple(got) + extra,
    )


def reduce_line(own, pieces):
    total = own
    for piece in pieces:
        total = total + piece[: own.shape[0]].astype(WIDE)
    return total


def head_back_kernel(where, *refs):
    grad, grad_got, down_weight, up_weight, slope, act, low, low_got = refs[:8]
    own_out, send_out, data_out = refs[8:]
    few = 16
    row_at = lax.broadcasted_iota(jnp.int32, (few, 1), 0)

    def two_rows(first, second):
        return jnp.where(row_at == 0, first, jnp.where(row_at == 1, second, 0.0))

    second = two_rows(grad[...], grad_got[...]).astype(LOW)
    data_out[0:1, :] = low[0:1, :].astype(WIDE)
    data_out[1:2, :] = low_got[0:1, :].astype(WIDE)
    data_out[2:4, :] = second[0:2].astype(WIDE)
    partial = jnp.zeros((few, MODEL), WIDE)
    for at in range(FF_HALF // MODEL):
        columns = slice(at * MODEL, (at + 1) * MODEL)
        before = product_plain(second, down_weight[:, :, columns].reshape(MODEL, MODEL))
        slopes = two_rows(slope[0:1, columns], slope[SEG : SEG + 1, columns])
        pre = (before * slopes).astype(LOW)
        partial = partial + product_right(pre, up_weight[:, :, columns].reshape(MODEL, MODEL))
        data_out[4 + 2 * at : 6 + 2 * at, :] = pre[0:2].astype(WIDE)
        data_out[8 + 2 * at : 9 + 2 * at, :] = act[0:1, columns].astype(WIDE)
        data_out[9 + 2 * at : 10 + 2 * at, :] = act[SEG : SEG + 1, columns].astype(WIDE)
    own_out[...] = partial[0:1]
    send_out[...] = partial[1:2]


def first_norm_kernel(where, *refs):
    second_grad, own, got, head_grad, head_own, head_got = refs[:6]
    normed_rows, inv_dev, vectors, out_weight = refs[6:10]
    grad_out, branch_out, mixed_out, send_out, sums_out = refs[10:]
    core_at = where[2]
    grad_rows = second_grad[...] + own[...] + got[...]
    head = head_grad[...] + head_own[...] + head_got[...]
    row_at = lax.broadcasted_iota(jnp.int32, (SEG, 1), 0)
    grad_rows = jnp.where(row_at == 0, head, grad_rows)
    normed = normed_rows[...]
    grad = norm_rows_back(grad_rows, normed, inv_dev[...], vectors[4:5, :])
    grad_out[...] = grad
    branch = grad.astype(LOW)
    branch_out[...] = branch
    mixed_out[...] = product_right(branch, out_weight[...]).astype(LOW)
    other = pl.ds(aligned((1 - core_at) * HALF), HALF)
    send_out[:, :HALF] = mixed_out[:, other]
    send_out[:, HALF:] = branch_out[:, other]
    sums_out[0:1, :] = column_sum(branch)
    sums_out[1:2, :] = column_sum(grad_rows * normed)
    sums_out[2:3, :] = column_sum(grad_rows)


def attn_back_kernel(where, *refs):
    qkv, mixed_grad, got, live_row, live_got, weight = refs[:6]
    sums_first, sums_second, sums_up, head_top, head_normed, data = refs[6:12]
    proj_out, own_out, send_out, payload_out, rows = refs[12:]
    core_at = where[2]
    lanes = pl.ds(aligned(core_at * HALF), HALF)
    for part, live in enumerate((live_row, live_got)):
        at = slice(part * SEG, (part + 1) * SEG)
        grad = mixed_grad[:, lanes] if part == 0 else got[:, :HALF]
        pieces = attend_tiles_back(qkv[at, :], grad, HALF, token_allowed(live[...]))
        for tile, value in enumerate(pieces):
            proj_out[at, tile * LANES : (tile + 1) * LANES] = value
    partial = product_right(proj_out[...], whole_rows(weight))
    own_out[...] = partial[:SEG]
    send_out[...] = partial[SEG:]
    rows[...] = jnp.zeros_like(rows)
    rows[0:12, :] = data[0:12, :]
    rows[12:13, lanes] = column_sum(proj_out[:, :HALF])
    rows[13:14, lanes] = column_sum(proj_out[:, 2 * HALF :])
    rows[14:15, :] = sums_first[0:1, :]
    rows[15:16, :] = sums_second[0:1, :] + data[2:3, :]
    rows[16:18, :] = sums_first[1:3, :]
    rows[18:19, :] = sums_second[1:2, :] + head_top[...] * head_normed[0:1, :]
    rows[19:20, :] = sums_second[2:3, :] + head_top[...]
    for at in range(FF_HALF // MODEL):
        total = sums_up[at : at + 1, :] + data[4 + 2 * at : 5 + 2 * at, :]
        total = total + data[5 + 2 * at : 6 + 2 * at, :]
        rows[pl.ds(20 + core_at * (FF_HALF // MODEL) + at, 1), :] = total
    payload_out[...] = rows[...].astype(LOW)


def cls_gather_kernel(where, *refs):
    blocks = refs[:8]
    own_out, from_x, from_y, far_x = refs[8], refs[4], refs[5], refs[6]
    weight_out, out_rows = refs[9:]
    plane_at = where[1]
    gather_blocks(where, blocks, 0, QUARTER_HALF, ((weight_out, 0, QUARTER_HALF),))
    first = LINE * QUARTER_HALF
    out_rows[plane_at] = own_out[...]
    out_rows[plane_at ^ 1] = from_x[:, first : first + HALF]
    out_rows[plane_at ^ 2] = from_y[:, first : first + HALF]
    first = LINE // 2 * QUARTER_HALF
    out_rows[plane_at ^ 3] = far_x[:, first : first + HALF]


def cls_weight_kernel(where, own, got, out_half, out_got, weight_out, out_full):
    line_at, core_at = where[0], where[2]
    out_full[...] = jnp.zeros_like(out_full)
    for value, part, core in ((own, out_half, core_at), (got, out_got, 1 - core_at)):
        weight_out[:, :, pl.ds(aligned(core * QUARTER_HALF), QUARTER_HALF)] = value[...]
        rows = part[...].reshape(3, HEAD_DIM, HALF)
        out_full[pl.ds(line_at % 2, 3), :, pl.ds(aligned(core * HALF), HALF)] = rows


def add_far_kernel(where, far_low, far_high, to_x, to_y, x_out, y_out):
    half = LINE // 2
    x_out[:half] = to_x[:half] + far_low[...]
    x_out[half:] = to_x[half:]
    y_out[:half] = to_y[:half]
    y_out[half:] = to_y[half:] + far_high[...]


def row_from_column(column, size):
    shape = (size, size)
    same = lax.broadcasted_iota(jnp.int32, shape, 0) == lax.broadcasted_iota(jnp.int32, shape, 1)
    return jnp.sum(jnp.where(same, column, 0.0), axis=0, keepdims=True)


def head_allowed(heads):
    facts = heads[:, 2 * MODEL :]
    live, doc = facts[:, 0:1], facts[:, 1:2]
    shape = (GROUP, GROUP)
    same = lax.broadcasted_iota(jnp.int32, shape, 0) == lax.broadcasted_iota(jnp.int32, shape, 1)
    live_row, doc_row = row_from_column(live, GROUP), row_from_column(doc, GROUP)
    return ((live_row > 0.5) & (doc == doc_row)) | same


def quarter_mask(quarter):
    lane = lax.broadcasted_iota(jnp.int32, (GROUP, SPAN), 1)
    first = (quarter % 2) * HEAD_DIM
    return (lane >= first) & (lane < first + 3 * HEAD_DIM)


def quarter_piece(vectors, row, quarter):
    value = jnp.zeros((1, SPAN), WIDE)
    for at in range(LINE):
        first = TILE_START[at] * LANES
        value = jnp.where(quarter == at, vectors[row : row + 1, first : first + SPAN], value)
    return value


def cls_attend_kernel(where, *refs):
    stacks, vectors, weight, out_weight = refs[:4], refs[4], refs[5], refs[6]
    heads_out, qkv_out, mixed_out, part_out = refs[7:]
    line_at, plane_at = where[0], where[1]
    for step, stack in enumerate(stacks):
        for mask in range(PLANE):
            row = (line_at + LINE - step) % LINE * PLANE + (plane_at ^ mask)
            heads_out[pl.ds(row, 1), :] = stack[mask : mask + 1, :]
    heads = heads_out[...]
    inputs = heads[:, :MODEL].astype(LOW)
    projected = product_plain(inputs, weight[:, : 3 * SPAN])
    query = projected[:, :SPAN] + quarter_piece(vectors, 12, line_at)
    value = projected[:, 2 * SPAN :] + quarter_piece(vectors, 13, line_at)
    qkv_out[:, :SPAN] = query.astype(LOW)
    qkv_out[:, SPAN : 2 * SPAN] = projected[:, SPAN : 2 * SPAN].astype(LOW)
    qkv_out[:, 2 * SPAN :] = value.astype(LOW)
    mixed = attend_tiles(qkv_out[...], SPAN, head_allowed(heads))
    mixed = masked(jnp.concatenate(mixed, axis=1), quarter_mask(line_at))
    mixed_out[...] = mixed
    part_out[...] = product_plain(mixed, out_weight[...])


def cls_mlp_kernel(where, *refs):
    heads, own, got_one, got_two, got_three, vectors, weight = refs[:7]
    normed_out, inv_out, low_out, act_out, slope_out, part_out = refs[7:]
    line_at = where[0]
    branch = own[...] + got_one[...] + got_two[...] + got_three[...]
    normed, inv_dev = norm_rows(heads[:, :MODEL] + branch + vectors[14:15, :])
    normed_out[...] = normed
    inv_out[...] = inv_dev
    low = (normed * vectors[16:17, :] + vectors[17:18, :]).astype(LOW)
    low_out[...] = low
    part = FF // LINE
    first = 3 * SPAN
    bias = vectors[pl.ds(20 + line_at, 1), :]
    before = product_plain(low, weight[:, first : first + part]) + bias
    value, slope = gelu_both(before)
    act = value.astype(LOW)
    act_out[...] = act
    slope_out[...] = slope
    part_out[...] = product_right(act, weight[:, first + part :])


def cls_top_kernel(where, *refs):
    heads, own, got_one, got_two, got_three, vectors, weight = refs[:7]
    normed_first, count, slope = refs[7:10]
    top_out, square_out, grad_out, second_out, pre_out, part_out, sums_out = refs[10:17]
    held = refs[17]
    rank = where[0] * PLANE + where[1]
    first = normed_first[...] * vectors[16:17, :] + vectors[17:18, :]
    down = own[...] + got_one[...] + got_two[...] + got_three[...]
    normed, inv_dev = norm_rows(first + down + vectors[15:16, :])
    rows = normed * vectors[18:19, :] + vectors[19:20, :]
    held[...] = rows
    top_out[...] = held[pl.ds(rank, 1), :]
    facts = heads[:, 2 * MODEL :]
    live = facts[:, 0:1]
    diff = (rows * live - heads[:, MODEL : 2 * MODEL]) * live
    square = jnp.sum(column_sum(diff * diff), axis=1, keepdims=True)
    square = square + jnp.sum(facts[:, 3:4], axis=0, keepdims=True)
    square_out[...] = jnp.broadcast_to(square, square_out.shape)
    grad_top = diff * ((SEG * GROUP * CORES) / count[0:1, 0:1])
    grad = norm_rows_back(grad_top, normed, inv_dev, vectors[18:19, :])
    sums_out[0:1, :] = column_sum(grad_top * normed)
    sums_out[1:2, :] = column_sum(grad_top)
    grad_out[...] = grad
    second = grad.astype(LOW)
    second_out[...] = second
    part = FF // LINE
    at = 3 * SPAN
    pre = (product_plain(second, weight[:, at + part :]) * slope[...]).astype(LOW)
    pre_out[...] = pre
    part_out[...] = product_right(pre, weight[:, at : at + part])


def cls_attend_back_kernel(where, *refs):
    heads, own, got_one, got_two, got_three, vectors, weight, out_weight = refs[:8]
    grad_in, normed_first, inv_first, qkv = refs[8:12]
    grad_out, branch_out, proj_out, part_out, sums_out = refs[12:]
    line_at = where[0]
    grad_first = grad_in[...] + own[...] + got_one[...] + got_two[...] + got_three[...]
    normed = normed_first[...]
    grad = norm_rows_back(grad_first, normed, inv_first[...], vectors[16:17, :])
    sums_out[0:1, :] = column_sum(grad_first * normed)
    sums_out[1:2, :] = column_sum(grad_first)
    grad_out[...] = grad
    branch = grad.astype(LOW)
    branch_out[...] = branch
    mask = quarter_mask(line_at)
    mixed_grad = masked(product_right(branch, out_weight[...]).astype(LOW), mask)
    pieces = attend_tiles_back(qkv[...], mixed_grad, SPAN, head_allowed(heads[...]))
    tiles = SPAN // LANES
    for piece in range(3):
        joined = jnp.concatenate(pieces[piece * tiles : (piece + 1) * tiles], axis=1)
        proj_out[:, piece * SPAN : (piece + 1) * SPAN] = masked(joined, mask)
    part_out[...] = product_right(proj_out[...], weight[:, : 3 * SPAN])


def cls_end_kernel(where, *refs):
    heads, grad, own, got_one, got_two, got_three = refs[:6]
    square, sums_back, sums_top = refs[6:9]
    normed_second, inv_second, vectors = refs[9:12]
    row_out, second_out, shared_out, held = refs[12:]
    rank = where[0] * PLANE + where[1]
    total = grad[...] + own[...] + got_one[...] + got_two[...] + got_three[...]
    held[...] = total
    row = held[pl.ds(rank, 1), :]
    row_out[...] = row
    second_out[...] = norm_rows_back(
        row, normed_second[0:1, :], inv_second[0:1, :], vectors[6:7, :]
    )
    number = row_from_column(heads[:, 2 * MODEL + 2 : 2 * MODEL + 3], GROUP)
    entry = lax.broadcasted_iota(jnp.int32, (GROUP, GROUP), 0).astype(WIDE)
    hot = (entry == number).astype(WIDE)
    shared_out[0:GROUP, :] = jnp.dot(hot, total, precision=lax.Precision.HIGHEST)
    shared_out[GROUP : GROUP + 1, 0:LANES] = square[0:1, :]
    shared_out[GROUP + 1 : GROUP + 3, :] = sums_back[0:2, :]
    shared_out[GROUP + 3 : GROUP + 5, :] = sums_top[0:2, :]


def head_mlp_kernel(where, *refs):
    cls_mlp_kernel(where, *refs[:7], *refs[11:17])
    add_far_kernel(where, *refs[7:11], *refs[17:])


def head_end_kernel(where, *refs):
    cls_end_kernel(where, *refs[:12], *refs[16:19], refs[23])
    fold_kernel(where, *refs[12:16], *refs[19:23])


def attn_add_kernel(where, *refs):
    far_low, far_high, to_x, to_y, grad, own, got, x_out, y_out, input_out = refs
    add_far_kernel(where, far_low, far_high, to_x, to_y, x_out, y_out)
    input_out[...] = (grad[...] + own[...] + got[...]).astype(LOW)


def cls_rows_kernel(where, *refs):
    packs = refs[:4]
    heads, branch, low, second = refs[4:8]
    out, kept = refs[8:]
    line_at = where[0]
    rows, width = kept.shape[1:]
    for step, pack in enumerate(packs):
        first = pack.shape[0] - rows
        kept[(line_at + LINE - step) % LINE] = pack[first:, :width]
    starts = (MODEL, 2 * MODEL, 3 * MODEL, 4 * MODEL)
    out[:, 0:MODEL] = heads[:, :MODEL].astype(LOW)
    for piece, start in enumerate(starts):
        from_at = piece * SPAN
        for tile in range(MODEL // LANES):
            total = None
            for at in range(PLANE):
                inner = tile - TILE_START[at]
                if inner in (0, 1):
                    first = from_at + inner * LANES
                    value = kept[at, :, first : first + LANES]
                    total = value if total is None else total + value
            out[:, start + tile * LANES : start + (tile + 1) * LANES] = total
    out[:, 5 * MODEL : 6 * MODEL] = branch[...]
    out[:, 6 * MODEL : 7 * MODEL] = low[...]
    out[:, 7 * MODEL + FF : 8 * MODEL + FF] = second[...]
    part = FF // LINE
    for at in range(PLANE):
        first = 4 * SPAN
        out[:, 7 * MODEL + at * part : 7 * MODEL + (at + 1) * part] = kept[
            at, :, first : first + part
        ]
        out[:, 8 * MODEL + FF + at * part : 8 * MODEL + FF + (at + 1) * part] = kept[
            at, :, first + part : first + 2 * part
        ]


def own_features(rank, width):
    shape = (MODEL, width)
    feature = lax.broadcasted_iota(jnp.int32, shape, 0)
    column = lax.broadcasted_iota(jnp.int32, shape, 1)
    return (feature == rank * width + column).astype(LOW)


def own_vector(rank, pieces, out, flat):
    size = out.shape[0]
    for at, piece in enumerate(pieces):
        flat[:, at * MODEL : (at + 1) * MODEL] = piece
    value = jnp.zeros((1, size), WIDE)
    for chip in range(GROUP):
        value = jnp.where(rank == chip, flat[:, chip * size : (chip + 1) * size], value)
    out[...] = value.reshape(size)


def cls_owner_kernel(where, *refs):
    own, got, shared, mats_out, vec_out, rows, flat = refs
    rank = where[0] * PLANE + where[1]
    width = mats_out.shape[0]
    rows[:GROUP] = own[...]
    rows[GROUP:] = got[...]
    chosen = own_features(rank, width)
    plan = (
        (0, MODEL, 3 * MODEL, 0),
        (4 * MODEL, 5 * MODEL, MODEL, 3 * MODEL),
        (6 * MODEL, 7 * MODEL, FF, 4 * MODEL),
        (7 * MODEL + FF, 8 * MODEL + FF, FF, 4 * MODEL + FF),
    )
    for left, right, size, target in plan:
        side = product_plain(rows[:, left : left + MODEL], chosen).astype(LOW)
        mats_out[:, target : target + size] = product_left(side, rows[:, right : right + size])
    starts = (MODEL, 3 * MODEL, 5 * MODEL, 7 * MODEL + FF)
    pieces = [column_sum(rows[:, start : start + MODEL]) for start in starts]
    pieces += [shared[GROUP + 1 + at : GROUP + 2 + at, :] for at in range(4)]
    starts = [7 * MODEL + at * MODEL for at in range(FF // MODEL)]
    pieces += [column_sum(rows[:, start : start + MODEL]) for start in starts]
    own_vector(rank, pieces, vec_out, flat)


def head_share_kernel(where, *refs):
    packs, mlp = refs[:4], refs[4]
    mine_out, vecs_out, rows = refs[5:]
    rank = where[0] * PLANE + where[1]
    count = LINE * 24
    for at, pack in enumerate(packs):
        rows[at * count : (at + 1) * count] = pack[...]
    total = PLANE * count

    def chosen(base, apart):
        shape = (CORES * GROUP, total)
        row = lax.broadcasted_iota(jnp.int32, shape, 0)
        column = lax.broadcasted_iota(jnp.int32, shape, 1)
        hot = (column == row // 2 * 24 + base + row % 2 * apart).astype(LOW)
        return product_plain(hot, rows[...]).astype(LOW)

    own = own_features(rank, OWN)
    for at, (left, right) in enumerate(((0, 4), (2, 8))):
        side = product_plain(chosen(left, 1), own).astype(LOW)
        for piece in range(FF_HALF // MODEL):
            columns = slice(at * FF_HALF + piece * MODEL, at * FF_HALF + (piece + 1) * MODEL)
            share = product_left(side, chosen(right + 2 * piece, 1))
            mine_out[:, columns] = mlp[:, columns] + share
    shape = (16, total)
    row = lax.broadcasted_iota(jnp.int32, shape, 0)
    column = lax.broadcasted_iota(jnp.int32, shape, 1)
    hot = ((column % 24 == row + 12) & (row < 12)).astype(LOW)
    vecs_out[...] = product_plain(hot, rows[...])


def share_owner_kernel(where, *refs):
    head_share_kernel(where, *refs[:5], *refs[9:11], refs[15])
    cls_owner_kernel(where, *refs[5:8], *refs[11:13], *refs[16:])
    shared, count, pos_out, loss_out = refs[7], refs[8], refs[13], refs[14]
    pos_out[...] = shared[:GROUP, :]
    loss_out[...] = shared[GROUP : GROUP + 1, 0:1] / (count[0:1, 0:1] * MODEL)


def seg_vec_kernel(where, vecs, vecs_got, vec_out, flat):
    rank = where[0] * PLANE + where[1]
    rows = (8 * MODEL + FF) // MODEL
    pieces = [vecs[at : at + 1, :] + vecs_got[at : at + 1, :] for at in range(rows)]
    own_vector(rank, pieces, vec_out, flat)


def column_copies(where, out, base, size, own, got, first):
    core_at = where[2]
    lanes = slice(first, first + size)
    return [
        (own.at[:, lanes], out.at[:, pl.ds(aligned(base + core_at * size), size)]),
        (got.at[:, lanes], out.at[:, pl.ds(aligned(base + (1 - core_at) * size), size)]),
    ]


def store_kernel(where, attn, attn_got, mlp, mlp_got, vecs, vecs_got, out, vec_out, flat, sems):
    pairs = []
    for piece in range(4):
        pairs += column_copies(where, out, piece * MODEL, HALF, attn, attn_got, piece * HALF)
    for piece in range(2):
        base = 4 * MODEL + piece * FF
        pairs += column_copies(where, out, base, FF_HALF, mlp, mlp_got, piece * FF_HALF)
    copies = [
        pltpu.make_async_copy(source, target, sems.at[at])
        for at, (source, target) in enumerate(pairs)
    ]
    for copy in copies:
        copy.start()
    seg_vec_kernel(where, vecs, vecs_got, vec_out, flat)
    wait_all(copies)


def plane_parts(part):
    return (part,) + together(*(in_plane(part, mask) for mask in range(1, PLANE)))


def line_parts(part):
    return (part,) + together(*(along_line(part, apart) for apart in range(1, LINE)))


def slice_local(
    hidden_in,
    targets,
    doc_ids,
    seg_nums,
    valid_flags,
    seg_mats,
    seg_vecs,
    cls_mats,
    cls_vecs,
    seg_pos,
):
    rank, core_at = lax.axis_index("fsdp"), lax.axis_index("rep")
    line_at, plane_at = rank // PLANE, rank % PLANE
    where = jnp.stack([line_at, plane_at, core_at, doc_ids[0], seg_nums[0]]).astype(jnp.int32)
    own_rows, total_columns = seg_mats.shape
    vec_size = seg_vecs.shape[0]
    both_rows = CORES * SEG

    first_piece, live_row, *rest = run_kernel(
        prepare_kernel,
        "prepare",
        [shape_of((own_rows, FIRST), LOW), shape_of((1, SEG))]
        + [shape_of((own_rows, FF_HALF), LOW)] * 2
        + [shape_of((own_rows, QUARTER_HALF), LOW)] * LINE
        + [shape_of((own_rows, HALF), LOW), shape_of((MODEL, PLANE * SPAN), LOW)],
        where,
        (seg_mats, cls_mats),
        (jnp.stack([seg_vecs, cls_vecs]).astype(WIDE), valid_flags[None]),
        [
            pltpu.SemaphoreType.DMA((4,)),
            pltpu.VMEM((LINE, own_rows, QUARTER), LOW),
            pltpu.SemaphoreType.DMA((3 + 5 * LINE,)),
        ],
    )
    first_line = line_parts(first_piece)
    second_piece, third_piece, quarters, cls_out_piece, order = (
        rest[0],
        rest[1],
        rest[2:-2],
        rest[-2],
        rest[-1],
    )

    def joined(*pieces):
        return jnp.concatenate(pieces, axis=1)

    def sent_both(to_x, to_y):
        to_x, to_y = together(to_x, to_y)
        return together(in_plane(to_x, 1), in_plane(to_y, 2))

    own_sent = joined(first_piece, second_piece, third_piece)
    own_x, own_y = sent_both(own_sent, own_sent)
    first_line = first_line[:1] + tuple(after(got, own_x, own_y) for got in first_line[1:])
    to_x = joined(own_y[:, OWN_CUT:], *first_line[1:])
    to_y = joined(own_x[:, :OWN_CUT], *first_line[1:])
    first_x, first_y = sent_both(to_x, to_y)
    hidden_got = other_core(after(hidden_in, to_x, to_y))
    live_got = other_core(after(live_row, to_x, to_y))
    second_line = line_parts(after(second_piece, hidden_got, live_got, to_x, to_y))

    def halves(group, from_x, from_y):
        width, cut = WIDTHS[group], LINE_CUTS[group]
        if group == 0:
            base_x, base_y = sum(WIDTHS) - OWN_CUT, OWN_CUT
        else:
            before, before_cut = WIDTHS[group - 1], LINE_CUTS[group - 1]
            base_x, base_y = 2 * before - before_cut, before + before_cut
        return (
            from_y[:, base_y + width + cut : base_y + 3 * width],
            from_x[:, base_x : base_x + width + cut],
        )

    high, low = halves(0, first_x, first_y)
    to_x, to_y = joined(high, *second_line[1:]), joined(low, *second_line[1:])
    second_x, second_y = sent_both(to_x, to_y)
    third_line = line_parts(after(third_piece, to_x, to_y))
    high, low = halves(1, second_x, second_y)
    to_x, to_y = joined(high, *third_line[1:]), joined(low, *third_line[1:])
    third_x, third_y = sent_both(to_x, to_y)
    own_parts = (own_x, own_y, first_x, first_y)
    cls_line = (quarters[0],) + tuple(
        along_line(after(quarters[apart], to_x, to_y), apart)
        for apart in range(1, LINE)
    )

    qkv_weight, out_low, out_high, qkv, mixed, vectors, count, hidden_ordered = run_kernel(
        qkv_kernel,
        "seg_qkv",
        [
            shape_of((GROUP, own_rows, 3 * HALF), LOW),
            shape_of((GROUP // 2, own_rows, HALF), LOW),
            shape_of((GROUP // 2, own_rows, HALF), LOW),
            shape_of((both_rows, 3 * HALF), LOW),
            shape_of((both_rows, HALF), LOW),
            shape_of((2 * (8 * MODEL + FF) // MODEL, MODEL)),
            shape_of((8, LANES)),
            shape_of((both_rows, PLANE * SPAN), LOW),
        ],
        where,
        (),
        first_line
        + own_parts
        + (first_x, first_y, second_x, second_y)
        + (hidden_in, hidden_got, live_row, live_got, order),
        [
            pltpu.VMEM((GROUP, own_rows, LANES), LOW),
            pltpu.VMEM((2, 8 * MODEL + FF), WIDE),
            pltpu.VMEM((both_rows, MODEL), LOW),
            pltpu.VMEM((GROUP, own_rows, HALF), LOW),
        ],
        flops=2 * SEG * MODEL * 3 * MODEL,
    )
    out_weight, mixed_ordered, normed_first, inv_first, first_low = run_kernel(
        out_kernel,
        "seg_out",
        [
            shape_of((MODEL, MODEL), LOW),
            shape_of((both_rows, PLANE * SPAN), LOW),
            shape_of((SEG, MODEL)),
            shape_of((SEG, 1)),
            shape_of((SEG, MODEL), LOW),
        ],
        where,
        (),
        (
            hidden_in,
            mixed,
            after(other_core(mixed), third_x, third_y),
            out_low,
            out_high,
            other_core(out_low),
            other_core(out_high),
            vectors,
            order,
        ),
        [pltpu.VMEM((both_rows, MODEL), LOW)],
        flops=2 * SEG * MODEL * MODEL,
    )
    fourth_x, fourth_y = sent_both(*halves(2, third_x, third_y))
    first_got = after(other_core(first_low), fourth_x, fourth_y)
    count = count + other_core(after(count, first_got))
    up_weight, act, slope = run_kernel(
        up_kernel,
        "seg_up",
        [
            shape_of((GROUP, own_rows, FF_HALF), LOW),
            shape_of((both_rows, FF_HALF), LOW),
            shape_of((both_rows, FF_HALF)),
        ],
        where,
        (),
        second_line
        + own_parts
        + (second_x, second_y, third_x, third_y)
        + (first_low, first_got, vectors),
        [pltpu.VMEM((both_rows, MODEL), LOW)],
        flops=2 * SEG * MODEL * FF,
    )
    cls_sent = joined(*cls_line, cls_out_piece)
    cls_sent = after(cls_sent, act)
    cls_x, cls_y = sent_both(cls_sent, cls_sent)
    down_weight, down_own, down_send = run_kernel(
        down_kernel,
        "seg_down",
        [
            shape_of((GROUP, own_rows, FF_HALF), LOW),
            shape_of((SEG, MODEL)),
            shape_of((SEG, MODEL)),
        ],
        where,
        (),
        third_line + own_parts + (third_x, third_y, fourth_x, fourth_y) + (act,),
        flops=2 * SEG * MODEL * FF,
    )
    normed_second, inv_second, diff, out_rows, head_row = run_kernel(
        seg_rows_kernel,
        "seg_rows",
        [
            shape_of((SEG, MODEL)),
            shape_of((SEG, 1)),
            shape_of((SEG, MODEL)),
            shape_of((SEG, MODEL)),
            shape_of((1, 2 * MODEL + LANES)),
        ],
        where,
        (),
        (
            down_own,
            other_core(down_send),
            normed_first,
            vectors,
            targets,
            live_row,
            seg_pos,
        ),
    )
    head_planes = plane_parts(head_row)
    head_lines = line_parts(jnp.concatenate(head_planes))
    size = LINE // 2 * QUARTER_HALF
    cls_far = sent_both(
        after(cls_y[:, size:], *head_planes[1:]), after(cls_x[:, :size], *head_planes[1:])
    )

    second_grad, second_low, second_sums = run_kernel(
        second_norm_kernel,
        "seg_second_norm",
        [shape_of((SEG, MODEL)), shape_of((SEG, MODEL), LOW), shape_of((3, MODEL))],
        where,
        (),
        (diff, count, normed_second, inv_second, vectors),
    )
    second_got = other_core(second_low)
    pre, first_grad_own, first_grad_send, up_sums = run_kernel(
        mlp_back_kernel,
        "seg_mlp_back",
        [
            shape_of((both_rows, FF_HALF), LOW),
            shape_of((SEG, MODEL)),
            shape_of((SEG, MODEL)),
            shape_of((FF_HALF // MODEL, MODEL)),
        ],
        where,
        (),
        (second_low, second_got, down_weight, up_weight, slope),
        [pltpu.VMEM((both_rows, MODEL), LOW)],
        flops=4 * SEG * MODEL * FF,
    )
    first_grad_got = other_core(first_grad_send)

    def part_shapes(columns):
        return [
            shape_of((count_of, own_rows, columns), LOW)
            for count_of in (LINE // 2, LINE // 2, LINE, LINE, LINE)
        ]

    head_lines = head_lines[:1] + together(*(after(got, pre) for got in head_lines[1:]))
    cls_far = together(*(after(got, *head_lines[1:]) for got in cls_far))
    cls_half, cls_out_half = run_kernel(
        cls_gather_kernel,
        "head_gather",
        [
            shape_of((GROUP, own_rows, QUARTER_HALF), LOW),
            shape_of((PLANE, own_rows, HALF), LOW),
        ],
        where,
        (),
        cls_line + (cls_x, cls_y) + cls_far + (cls_out_piece,),
    )
    mlp_parts = run_kernel(
        mlp_weight_kernel,
        "seg_mlp_weight",
        part_shapes(FF),
        where,
        (),
        (first_low, first_got, second_low, second_got, after(pre, cls_half), act),
        [
            pltpu.VMEM((both_rows, MODEL), LOW),
            pltpu.VMEM((GROUP, own_rows, FF), LOW),
            pltpu.SemaphoreType.DMA((GROUP,)),
        ],
        far=range(5),
        flops=4 * SEG * MODEL * FF,
    )
    mlp_far = reduce_far(tuple(after(part, *cls_far) for part in mlp_parts[:2]))
    cls_weight, cls_out = run_kernel(
        cls_weight_kernel,
        "head_weight",
        [
            shape_of((GROUP, own_rows, QUARTER), LOW),
            shape_of((4, HEAD_DIM, MODEL), LOW),
        ],
        where,
        (),
        (cls_half, other_core(cls_half), cls_out_half, other_core(cls_out_half)),
    )
    cls_weight = cls_weight.reshape(MODEL, QUARTER)
    cls_out = cls_out.reshape(SPAN, MODEL)
    heads, cls_qkv, cls_mixed, part = run_kernel(
        cls_attend_kernel,
        "head_attend",
        [
            shape_of((GROUP, 2 * MODEL + LANES)),
            shape_of((GROUP, 3 * SPAN), LOW),
            shape_of((GROUP, SPAN), LOW),
            shape_of((GROUP, MODEL)),
        ],
        where,
        (),
        tuple(after(got, mlp_parts[0], first_grad_got) for got in head_lines)
        + (vectors, cls_weight, cls_out),
    )
    cls_normed, cls_inv, cls_low, cls_act, cls_slope, part, *mlp_sent = run_kernel(
        head_mlp_kernel,
        "head_mlp",
        [
            shape_of((GROUP, MODEL)),
            shape_of((GROUP, 1)),
            shape_of((GROUP, MODEL), LOW),
            shape_of((GROUP, FF // LINE), LOW),
            shape_of((GROUP, FF // LINE)),
            shape_of((GROUP, MODEL)),
            shape_of(mlp_parts[2].shape, LOW),
            shape_of(mlp_parts[2].shape, LOW),
        ],
        where,
        (),
        (heads,) + line_parts(part) + (vectors, cls_weight) + mlp_far + tuple(mlp_parts[2:4]),
    )
    mlp_plane = sent_both(*mlp_sent)
    cls_parts = line_parts(part)
    top_row, square, cls_grad, cls_second, cls_pre, part, top_sums = run_kernel(
        cls_top_kernel,
        "head_top",
        [
            shape_of((1, MODEL)),
            shape_of((8, LANES)),
            shape_of((GROUP, MODEL)),
            shape_of((GROUP, MODEL), LOW),
            shape_of((GROUP, FF // LINE), LOW),
            shape_of((GROUP, MODEL)),
            shape_of((2, MODEL)),
        ],
        where,
        (),
        (heads,)
        + cls_parts
        + (vectors, cls_weight, cls_normed, count, cls_slope),
        [pltpu.VMEM((GROUP, MODEL), WIDE)],
    )
    top_parts = line_parts(part)
    cls_grad, cls_branch, cls_proj, part, back_sums = run_kernel(
        cls_attend_back_kernel,
        "head_attend_back",
        [
            shape_of((GROUP, MODEL)),
            shape_of((GROUP, MODEL), LOW),
            shape_of((GROUP, 3 * SPAN), LOW),
            shape_of((GROUP, MODEL)),
            shape_of((2, MODEL)),
        ],
        where,
        (),
        (heads,)
        + top_parts
        + (vectors, cls_weight, cls_out, cls_grad, cls_normed, cls_inv, cls_qkv),
    )
    end_parts = line_parts(part)
    pack = jnp.concatenate([cls_proj, cls_mixed, cls_pre, cls_act], axis=1)
    folded = [shape_of((own_rows, FF))] + [shape_of((own_rows + GROUP, FF), LOW)] * (LINE - 1)
    dheads, head_grad, shared, mlp_own, *mlp_sent = run_kernel(
        head_end_kernel,
        "head_end",
        [shape_of((1, MODEL)), shape_of((1, MODEL)), shape_of((GROUP + 8, MODEL))] + folded,
        where,
        (),
        (heads, cls_grad)
        + end_parts
        + (square, back_sums, top_sums, normed_second, inv_second, vectors)
        + (mlp_parts[4],)
        + mlp_plane
        + (pack,),
        [pltpu.VMEM((GROUP, MODEL), WIDE)],
    )
    got_three, got_two = along_line(mlp_sent[2], 3), along_line(mlp_sent[1], 2)
    mlp_last = mlp_sent[0]
    mlp_got = [None, got_two, got_three]

    head_own, head_send, head_data = run_kernel(
        head_back_kernel,
        "seg_head_back",
        [shape_of((1, MODEL)), shape_of((1, MODEL)), shape_of((12, MODEL))],
        where,
        (),
        (
            head_grad,
            other_core(head_grad),
            down_weight,
            up_weight,
            slope,
            act,
            first_low,
            first_got,
        ),
    )
    grad_summed, branch, mixed_grad, attn_send, first_sums = run_kernel(
        first_norm_kernel,
        "seg_first_norm",
        [
            shape_of((SEG, MODEL)),
            shape_of((SEG, MODEL), LOW),
            shape_of((SEG, MODEL), LOW),
            shape_of((SEG, MODEL), LOW),
            shape_of((3, MODEL)),
        ],
        where,
        (),
        (
            second_grad,
            first_grad_own,
            first_grad_got,
            head_grad,
            head_own,
            other_core(head_send),
            normed_first,
            inv_first,
            vectors,
            out_weight,
        ),
    )
    attn_got = other_core(attn_send)
    proj, input_own, input_send, payload = run_kernel(
        attn_back_kernel,
        "seg_attn_back",
        [
            shape_of((both_rows, 3 * HALF), LOW),
            shape_of((SEG, MODEL)),
            shape_of((SEG, MODEL)),
            shape_of((24, MODEL), LOW),
        ],
        where,
        (),
        (
            qkv,
            mixed_grad,
            attn_got,
            live_row,
            live_got,
            qkv_weight,
            first_sums,
            second_sums,
            up_sums,
            dheads,
            normed_second,
            head_data,
        ),
        [pltpu.VMEM((24, MODEL), WIDE)],
        flops=4 * SEG * MODEL * 3 * MODEL,
    )
    attn_data = (hidden_ordered, mixed_ordered, proj, branch, attn_got)
    attn_far = run_kernel(
        attn_far_kernel,
        "seg_attn_far",
        part_shapes(4 * HALF)[:2],
        where,
        (),
        attn_data,
        flops=SEG * MODEL * 2 * MODEL,
    )
    attn_far = reduce_far(tuple(after(part, mlp_got[-1]) for part in attn_far))
    attn_near = run_kernel(
        attn_near_kernel,
        "seg_attn_near",
        part_shapes(4 * HALF)[2:] + [shape_of((SEG, MODEL), LOW)],
        where,
        (),
        attn_data + (top_row, out_rows, live_row),
        flops=3 * SEG * MODEL * 2 * MODEL,
    )
    output = attn_near[3]
    *attn_sent, input_grad = run_kernel(
        attn_add_kernel,
        "seg_attn_add",
        [shape_of(attn_near[0].shape, LOW)] * 2 + [shape_of((SEG, MODEL), LOW)],
        where,
        (),
        attn_far
        + tuple(attn_near[:2])
        + (after(grad_summed, got_two), input_own, other_core(input_send)),
    )
    attn_plane = sent_both(*attn_sent)
    payload_parts = line_parts(after(payload, *attn_sent))
    mlp_got[0] = along_line(after(mlp_last, *payload_parts[1:]), 1)
    mlp_got = [after(got, attn_plane[0]) for got in mlp_got]
    mlp_sum = reduce_line(mlp_own, mlp_got)
    shared = shared + other_core(after(shared, attn_sent[0]))
    row_width = 8 * MODEL + 2 * FF
    cls_rows = run_kernel(
        cls_rows_kernel,
        "head_rows",
        [shape_of((GROUP, row_width), LOW)],
        where,
        (),
        (pack,) + tuple(mlp_got) + (heads, cls_branch, cls_low, cls_second),
        [pltpu.VMEM((LINE,) + pack.shape, LOW)],
    )[0]
    cls_got = other_core(cls_rows)
    attn_plane = tuple(after(got, output, input_grad, shared) for got in attn_plane)
    attn_own, *attn_sent = reduce_fold(where, attn_near[2], attn_plane)
    attn_lines = list(
        together(*(along_line(attn_sent[apart - 1], apart) for apart in range(1, LINE)))
    )
    flat = pltpu.VMEM((1, 8 * MODEL + FF), WIDE)
    payload_line = jnp.concatenate(payload_parts)
    mlp_mine, own_vecs, cls_mats_grad, cls_vec_grad, pos_total, loss_value = run_kernel(
        share_owner_kernel,
        "head_owner",
        [
            shape_of((own_rows, FF)),
            shape_of((16, MODEL)),
            shape_of((own_rows, total_columns)),
            shape_of((vec_size,)),
            shape_of((GROUP, MODEL)),
            shape_of((1, 1)),
        ],
        where,
        (),
        tuple(after(got, attn_own) for got in plane_parts(after(payload_line, *attn_plane)))
        + (mlp_sum, cls_rows, cls_got, shared, count),
        [
            pltpu.VMEM((GROUP * 24, MODEL), LOW),
            pltpu.VMEM((CORES * GROUP, row_width), LOW),
            flat,
        ],
        flops=64 * own_rows * total_columns,
    )
    loss_value = loss_value.reshape(())
    attn_lines = together(*(after(got, mlp_mine) for got in attn_lines))
    attn_sum = reduce_line(attn_own, attn_lines)
    seg_mats_grad, seg_vec_grad = run_kernel(
        store_kernel,
        "seg_owner",
        [shape_of((own_rows, total_columns)), shape_of((vec_size,))],
        where,
        (),
        (attn_sum, other_core(attn_sum), mlp_mine, other_core(mlp_mine))
        + (own_vecs, other_core(own_vecs)),
        [flat, pltpu.SemaphoreType.DMA((12,))],
        far=(0,),
    )

    return (
        output,
        input_grad,
        seg_mats_grad,
        seg_vec_grad,
        cls_mats_grad,
        cls_vec_grad,
        pos_total,
        loss_value,
    )


def solution(mesh):
    in_specs = (
        P(("rep", "fsdp"), None),
        P(("rep", "fsdp"), None),
        P(("rep", "fsdp")),
        P(("rep", "fsdp")),
        P(("rep", "fsdp")),
        P("fsdp", None),
        P("fsdp"),
        P("fsdp", None),
        P("fsdp"),
        P(),
    )
    out_specs = (
        P(("rep", "fsdp"), None),
        P(("rep", "fsdp"), None),
        P("fsdp", None),
        P("fsdp"),
        P("fsdp", None),
        P("fsdp"),
        P(),
        P(),
    )
    one_slice = dict(mesh.shape) == {"rep": CORES, "fsdp": LINE * PLANE}
    body = slice_local if one_slice else local
    return jax.shard_map(body, mesh=mesh, in_specs=in_specs, out_specs=out_specs, check_vma=False)
```

```python
import math

import jax
import jax.numpy as jnp
from jax import lax
from jax.experimental import pallas as pl
from jax.experimental.pallas import tpu as pltpu
from jax.sharding import PartitionSpec as P

HEADS = 12
HEAD_DIM = 64
FF = 3072
SEG = 128
SEQ = 2048


NORM_EPS = 1e-05
MASK_FILL = -1e30
SQRT_HALF = 0.7071067811865476
INV_SQRT_TWO_PI = 0.3989422804014327


def swapped(value, axis, apart):
    mask = 2**apart
    pairs = [(source, source ^ mask) for source in range(lax.axis_size(axis))]
    return lax.ppermute(value, axis, pairs)


def product_plain(left_side, right_side):
    return jnp.dot(left_side, right_side, preferred_element_type=jnp.float32)


def product_left(left_side, right_side):
    return lax.dot_general(
        left_side, right_side, (((0,), (0,)), ((), ())), preferred_element_type=jnp.float32
    )


def product_right(left_side, right_side):
    return lax.dot_general(
        left_side, right_side, (((1,), (1,)), ((), ())), preferred_element_type=jnp.float32
    )


def row_total(array_in):
    return jnp.sum(array_in.astype(jnp.float32), axis=0)


def unpack_weights(gathered, model_width, ff_width):
    matrix, vector = gathered
    vector = vector.astype(jnp.float32)
    pieces = tuple(
        (vector[offset * model_width : (offset + 1) * model_width] for offset in range(8))
    )
    return (
        (
            matrix[:, : 3 * model_width],
            matrix[:, 3 * model_width : 4 * model_width],
            matrix[:, 4 * model_width : 4 * model_width + ff_width],
            matrix[:, 4 * model_width + ff_width :],
        )
        + pieces
        + (vector[8 * model_width :],)
    )


def norm_forward(summed, gain_vec, shift_vec):
    row_mean = jnp.mean(summed, axis=-1, keepdims=True)
    centered = summed - row_mean
    inv_dev = lax.rsqrt(jnp.mean(centered * centered, axis=-1, keepdims=True) + NORM_EPS)
    normed = centered * inv_dev
    return (normed * gain_vec + shift_vec, normed, inv_dev)


def norm_backward(grad_out, normed, inv_dev, gain_vec):
    scaled = grad_out * gain_vec
    mean_one = jnp.mean(scaled, axis=-1, keepdims=True)
    mean_two = jnp.mean(scaled * normed, axis=-1, keepdims=True)
    grad_in = inv_dev * (scaled - mean_one - normed * mean_two)
    return (grad_in, jnp.sum(grad_out * normed, axis=0), jnp.sum(grad_out, axis=0))


def gelu_value(before):
    return 0.5 * before * (1.0 + lax.erf(before * SQRT_HALF))


def gelu_slope(before):
    return (
        0.5 * (1.0 + lax.erf(before * SQRT_HALF))
        + before * jnp.exp(-0.5 * before * before) * INV_SQRT_TWO_PI
    )


def attention_scores(queries, keys_in, allowed, score_scale):
    raw_scores = (
        jnp.einsum("bqhe,bkhe->bhqk", queries, keys_in, preferred_element_type=jnp.float32)
        * score_scale
    )
    return jnp.where(allowed, raw_scores, MASK_FILL)


def attention_forward(queries, keys_in, values, allowed, score_scale):
    scores = attention_scores(queries, keys_in, allowed, score_scale)
    row_top = jnp.max(scores, axis=-1, keepdims=True)
    log_total = row_top + jnp.log(jnp.sum(jnp.exp(scores - row_top), axis=-1, keepdims=True))
    weights = jnp.exp(scores - log_total).astype(jnp.bfloat16)
    mixed_rows = jnp.einsum("bhqk,bkhe->bqhe", weights, values, preferred_element_type=jnp.float32)
    return (mixed_rows, log_total)


def attention_backward(queries, keys_in, values, allowed, score_scale, log_total, grad_mixed):
    probabilities = jnp.exp(attention_scores(queries, keys_in, allowed, score_scale) - log_total)
    grad_probs = jnp.einsum(
        "bqhe,bkhe->bhqk", grad_mixed, values, preferred_element_type=jnp.float32
    )
    inner_sum = jnp.sum(grad_probs * probabilities, axis=-1, keepdims=True)
    grad_scores = (probabilities * (grad_probs - inner_sum)).astype(jnp.bfloat16)
    grad_query = (
        jnp.einsum("bhqk,bkhe->bqhe", grad_scores, keys_in, preferred_element_type=jnp.float32)
        * score_scale
    )
    grad_key = (
        jnp.einsum("bhqk,bqhe->bkhe", grad_scores, queries, preferred_element_type=jnp.float32)
        * score_scale
    )
    grad_value = jnp.einsum(
        "bhqk,bqhe->bkhe",
        probabilities.astype(jnp.bfloat16),
        grad_mixed,
        preferred_element_type=jnp.float32,
    )
    return (grad_query, grad_key, grad_value)


def block_forward(rows_in, unpacked, attend):
    (
        qkv_weight,
        out_weight,
        up_weight,
        down_weight,
        query_bias,
        value_bias,
        out_bias,
        down_bias,
        gain_first,
        shift_first,
        gain_second,
        shift_second,
        up_bias,
    ) = unpacked
    model_width = rows_in.shape[1]
    inputs = rows_in.astype(jnp.bfloat16)
    projected = product_plain(inputs, qkv_weight)
    queries = (projected[:, :model_width] + query_bias).astype(jnp.bfloat16)
    keys_in = projected[:, model_width : 2 * model_width].astype(jnp.bfloat16)
    values = (projected[:, 2 * model_width :] + value_bias).astype(jnp.bfloat16)
    mixed_rows, attend_kept = attend(queries, keys_in, values)
    mixed_rows = mixed_rows.astype(jnp.bfloat16)
    summed_first = rows_in + product_plain(mixed_rows, out_weight) + out_bias
    first_out, normed_first, inv_first = norm_forward(summed_first, gain_first, shift_first)
    first_low = first_out.astype(jnp.bfloat16)
    pre_act = product_plain(first_low, up_weight) + up_bias
    activated = gelu_value(pre_act).astype(jnp.bfloat16)
    summed_second = first_out + product_right(activated, down_weight) + down_bias
    block_out, normed_second, inv_second = norm_forward(summed_second, gain_second, shift_second)
    saved_state = (
        inputs,
        queries,
        keys_in,
        values,
        attend_kept,
        mixed_rows,
        normed_first,
        inv_first,
        first_low,
        pre_act,
        activated,
        normed_second,
        inv_second,
    )
    return (block_out, saved_state)


def block_backward(grad_out, unpacked, saved_state, attend_back):
    (
        qkv_weight,
        out_weight,
        up_weight,
        down_weight,
        query_bias,
        value_bias,
        out_bias,
        down_bias,
        gain_first,
        shift_first,
        gain_second,
        shift_second,
        up_bias,
    ) = unpacked
    (
        inputs,
        queries,
        keys_in,
        values,
        attend_kept,
        mixed_rows,
        normed_first,
        inv_first,
        first_low,
        pre_act,
        activated,
        normed_second,
        inv_second,
    ) = saved_state
    grad_second, grad_gain_second, grad_shift_second = norm_backward(
        grad_out, normed_second, inv_second, gain_second
    )
    second_low = grad_second.astype(jnp.bfloat16)
    grad_pre = (product_plain(second_low, down_weight) * gelu_slope(pre_act)).astype(jnp.bfloat16)
    grad_first = grad_second + product_right(grad_pre, up_weight)
    grad_summed, grad_gain_first, grad_shift_first = norm_backward(
        grad_first, normed_first, inv_first, gain_first
    )
    branch_low = grad_summed.astype(jnp.bfloat16)
    grad_mixed = product_right(branch_low, out_weight).astype(jnp.bfloat16)
    grad_query, grad_key, grad_value = attend_back(
        queries, keys_in, values, attend_kept, grad_mixed
    )
    grad_proj = jnp.concatenate([grad_query, grad_key, grad_value], axis=1)
    grad_rows = grad_summed + product_right(grad_proj, qkv_weight)
    vector_grad = jnp.concatenate(
        [
            row_total(grad_query),
            row_total(grad_value),
            row_total(branch_low),
            row_total(second_low),
            grad_gain_first,
            grad_shift_first,
            grad_gain_second,
            grad_shift_second,
            row_total(grad_pre),
        ]
    )
    weight_rows = (
        inputs,
        grad_proj,
        mixed_rows,
        branch_low,
        first_low,
        grad_pre,
        second_low,
        activated,
    )
    return (grad_rows, weight_rows, vector_grad)


def weight_products(weight_rows):
    inputs, grad_proj, mixed_rows, branch_low, first_low, grad_pre, second_low, activated = (
        weight_rows
    )
    return (
        product_left(inputs, grad_proj),
        product_left(mixed_rows, branch_low),
        product_left(first_low, grad_pre),
        product_left(second_low, activated),
    )


def local(
    hidden_in,
    targets,
    doc_ids,
    seg_nums,
    valid_flags,
    seg_mats,
    seg_vecs,
    cls_mats,
    cls_vecs,
    seg_pos,
):
    tok_rows, model_width = hidden_in.shape
    ff_width = FF
    seg_len = SEG
    group_span = SEQ // tok_rows
    seg_count = tok_rows // seg_len
    score_scale = HEAD_DIM ** (-0.5)
    head_shape = (HEADS, HEAD_DIM)
    live_rows = valid_flags.astype(jnp.float32)
    rank_full = lax.axis_index("fsdp")
    seg_gathered = (
        lax.all_gather(seg_mats, "fsdp", axis=0, tiled=True),
        lax.all_gather(seg_vecs, "fsdp", axis=0, tiled=True),
    )
    seg_unpacked = unpack_weights(seg_gathered, model_width, ff_width)
    cls_gathered = (
        lax.all_gather(cls_mats, "fsdp", axis=0, tiled=True),
        lax.all_gather(cls_vecs, "fsdp", axis=0, tiled=True),
    )
    cls_unpacked = unpack_weights(cls_gathered, model_width, ff_width)
    seg_allowed = (live_rows.reshape(seg_count, 1, 1, seg_len) > 0.5) | jnp.eye(seg_len, dtype=bool)
    seg_shape = (seg_count, seg_len) + head_shape

    def seg_attend(queries, keys_in, values):
        mixed_rows, log_total = attention_forward(
            queries.reshape(seg_shape),
            keys_in.reshape(seg_shape),
            values.reshape(seg_shape),
            seg_allowed,
            score_scale,
        )
        return (mixed_rows.reshape(tok_rows, model_width), log_total)

    def seg_attend_back(queries, keys_in, values, log_total, grad_mixed):
        grad_parts = attention_backward(
            queries.reshape(seg_shape),
            keys_in.reshape(seg_shape),
            values.reshape(seg_shape),
            seg_allowed,
            score_scale,
            log_total,
            grad_mixed.reshape(seg_shape),
        )
        return tuple(
            (
                grad_part.reshape(tok_rows, model_width).astype(jnp.bfloat16)
                for grad_part in grad_parts
            )
        )

    first_out, seg_saved = block_forward(hidden_in.astype(jnp.float32), seg_unpacked, seg_attend)
    first_grid = first_out.reshape(seg_count, seg_len, model_width)
    position_hot = (seg_nums[:, None] == jnp.arange(seg_pos.shape[0])[None, :]).astype(jnp.float32)
    position_rows = jnp.sum(
        position_hot[:, :, None] * seg_pos.astype(jnp.float32)[None, :, :], axis=1
    )
    heads_in = first_grid[:, 0, :] + position_rows
    lead_live = live_rows.reshape(seg_count, seg_len)[:, 0]
    lead_doc = doc_ids.reshape(seg_count, seg_len)[:, 0]
    lead_labels = jnp.where(lead_live > 0.5, lead_doc, -1).astype(jnp.bfloat16)
    lead_doc_low = lead_doc.astype(jnp.bfloat16)
    bit_count = group_span.bit_length() - 1
    key_total = group_span * seg_count
    own_slot = rank_full % group_span * seg_count + jnp.arange(seg_count)
    query_shape = (1, seg_count) + head_shape
    key_shape = (1, key_total) + head_shape

    def cls_attend(queries, keys_in, values):
        paired = jnp.concatenate([keys_in, values], axis=1)
        labels = lead_labels
        for bit_level in range(bit_count):
            other_pair, other_labels = swapped((paired, labels), "fsdp", bit_level)
            upper_half = rank_full // (1 << bit_level) % 2 == 1
            paired = jnp.where(
                upper_half,
                jnp.concatenate([other_pair, paired]),
                jnp.concatenate([paired, other_pair]),
            )
            labels = jnp.where(
                upper_half,
                jnp.concatenate([other_labels, labels]),
                jnp.concatenate([labels, other_labels]),
            )
        allowed = (labels[None, :] == lead_doc_low[:, None]) | (
            jnp.arange(key_total)[None, :] == own_slot[:, None]
        )
        allowed = allowed[None, None]
        mixed_rows, log_total = attention_forward(
            queries.reshape(query_shape),
            paired[:, :model_width].reshape(key_shape),
            paired[:, model_width:].reshape(key_shape),
            allowed,
            score_scale,
        )
        return (mixed_rows.reshape(seg_count, model_width), (paired, allowed, log_total))

    def cls_attend_back(queries, keys_in, values, attend_kept, grad_mixed):
        paired, allowed, log_total = attend_kept
        grad_query, grad_key, grad_value = attention_backward(
            queries.reshape(query_shape),
            paired[:, :model_width].reshape(key_shape),
            paired[:, model_width:].reshape(key_shape),
            allowed,
            score_scale,
            log_total,
            grad_mixed.reshape(query_shape),
        )
        grad_pair = jnp.concatenate(
            [grad_key.reshape(key_total, model_width), grad_value.reshape(key_total, model_width)],
            axis=1,
        )
        for bit_level in reversed(range(bit_count)):
            half_rows = grad_pair.shape[0] // 2
            upper_half = rank_full // (1 << bit_level) % 2 == 1
            kept_half = jnp.where(upper_half, grad_pair[half_rows:], grad_pair[:half_rows])
            sent_half = jnp.where(upper_half, grad_pair[:half_rows], grad_pair[half_rows:])
            grad_pair = kept_half + swapped(
                sent_half.astype(jnp.bfloat16), "fsdp", bit_level
            ).astype(sent_half.dtype)
        grad_pair = grad_pair.astype(jnp.bfloat16)
        return (
            grad_query.reshape(seg_count, model_width).astype(jnp.bfloat16),
            grad_pair[:, :model_width],
            grad_pair[:, model_width:],
        )

    top_out, cls_saved = block_forward(heads_in, cls_unpacked, cls_attend)
    combined = jnp.concatenate([top_out[:, None, :], first_grid[:, 1:, :]], axis=1).reshape(
        tok_rows, model_width
    )
    output_rows = combined * live_rows[:, None]
    diff_rows = (output_rows - targets.astype(jnp.float32)) * live_rows[:, None]
    count_all, square_all = lax.psum(
        (jnp.sum(live_rows), jnp.sum(diff_rows * diff_rows)), ("rep", "fsdp")
    )
    loss_value = square_all / (count_all * model_width)
    slots_all = tok_rows * lax.axis_size("rep") * lax.axis_size("fsdp")
    grad_grid = (diff_rows * (slots_all / count_all)).reshape(seg_count, seg_len, model_width)
    cls_back = unpack_weights(
        (
            lax.all_gather(cls_mats, "fsdp", axis=0, tiled=True),
            lax.all_gather(cls_vecs, "fsdp", axis=0, tiled=True),
        ),
        model_width,
        ff_width,
    )
    heads_grad, cls_weight_rows, cls_g_vec = block_backward(
        grad_grid[:, 0, :], cls_back, cls_saved, cls_attend_back
    )
    cls_g_qkv, cls_g_out, cls_g_up, cls_g_down = weight_products(cls_weight_rows)
    pos_local = jnp.sum(position_hot[:, :, None] * heads_grad[:, None, :], axis=0)
    seg_grad_out = jnp.concatenate([heads_grad[:, None, :], grad_grid[:, 1:, :]], axis=1).reshape(
        tok_rows, model_width
    )
    seg_back = unpack_weights(
        (
            lax.all_gather(seg_mats, "fsdp", axis=0, tiled=True),
            lax.all_gather(seg_vecs, "fsdp", axis=0, tiled=True),
        ),
        model_width,
        ff_width,
    )
    input_grad, seg_weight_rows, seg_g_vec = block_backward(
        seg_grad_out, seg_back, seg_saved, seg_attend_back
    )
    seg_g_qkv, seg_g_out, seg_g_up, seg_g_down = weight_products(seg_weight_rows)
    owner_rows = tuple(
        (
            lax.psum_scatter(seg_g_qkv, "fsdp", scatter_dimension=0, tiled=True),
            lax.psum_scatter(seg_g_out, "fsdp", scatter_dimension=0, tiled=True),
            lax.psum_scatter(seg_g_up, "fsdp", scatter_dimension=0, tiled=True),
            lax.psum_scatter(seg_g_down, "fsdp", scatter_dimension=0, tiled=True),
            lax.psum_scatter(seg_g_vec, "fsdp", scatter_dimension=0, tiled=True),
            lax.psum_scatter(cls_g_qkv, "fsdp", scatter_dimension=0, tiled=True),
            lax.psum_scatter(cls_g_out, "fsdp", scatter_dimension=0, tiled=True),
            lax.psum_scatter(cls_g_up, "fsdp", scatter_dimension=0, tiled=True),
            lax.psum_scatter(cls_g_down, "fsdp", scatter_dimension=0, tiled=True),
            lax.psum_scatter(cls_g_vec, "fsdp", scatter_dimension=0, tiled=True),
        )
    )
    replica_share = (
        lax.psum_scatter(
            owner_rows[0].astype(jnp.bfloat16), "rep", scatter_dimension=1, tiled=True
        ).astype(jnp.float32),
        lax.psum_scatter(
            owner_rows[1].astype(jnp.bfloat16), "rep", scatter_dimension=1, tiled=True
        ).astype(jnp.float32),
        lax.psum_scatter(
            owner_rows[2].astype(jnp.bfloat16), "rep", scatter_dimension=1, tiled=True
        ).astype(jnp.float32),
        lax.psum_scatter(
            owner_rows[3].astype(jnp.bfloat16), "rep", scatter_dimension=1, tiled=True
        ).astype(jnp.float32),
        lax.psum_scatter(
            owner_rows[4].astype(jnp.bfloat16), "rep", scatter_dimension=0, tiled=True
        ).astype(jnp.float32),
        lax.psum_scatter(
            owner_rows[5].astype(jnp.bfloat16), "rep", scatter_dimension=1, tiled=True
        ).astype(jnp.float32),
        lax.psum_scatter(
            owner_rows[6].astype(jnp.bfloat16), "rep", scatter_dimension=1, tiled=True
        ).astype(jnp.float32),
        lax.psum_scatter(
            owner_rows[7].astype(jnp.bfloat16), "rep", scatter_dimension=1, tiled=True
        ).astype(jnp.float32),
        lax.psum_scatter(
            owner_rows[8].astype(jnp.bfloat16), "rep", scatter_dimension=1, tiled=True
        ).astype(jnp.float32),
        lax.psum_scatter(
            owner_rows[9].astype(jnp.bfloat16), "rep", scatter_dimension=0, tiled=True
        ).astype(jnp.float32),
    )
    all_summed = (
        lax.all_gather(replica_share[0].astype(jnp.bfloat16), "rep", axis=1, tiled=True).astype(
            jnp.float32
        ),
        lax.all_gather(replica_share[1].astype(jnp.bfloat16), "rep", axis=1, tiled=True).astype(
            jnp.float32
        ),
        lax.all_gather(replica_share[2].astype(jnp.bfloat16), "rep", axis=1, tiled=True).astype(
            jnp.float32
        ),
        lax.all_gather(replica_share[3].astype(jnp.bfloat16), "rep", axis=1, tiled=True).astype(
            jnp.float32
        ),
        lax.all_gather(replica_share[4].astype(jnp.bfloat16), "rep", axis=0, tiled=True).astype(
            jnp.float32
        ),
        lax.all_gather(replica_share[5].astype(jnp.bfloat16), "rep", axis=1, tiled=True).astype(
            jnp.float32
        ),
        lax.all_gather(replica_share[6].astype(jnp.bfloat16), "rep", axis=1, tiled=True).astype(
            jnp.float32
        ),
        lax.all_gather(replica_share[7].astype(jnp.bfloat16), "rep", axis=1, tiled=True).astype(
            jnp.float32
        ),
        lax.all_gather(replica_share[8].astype(jnp.bfloat16), "rep", axis=1, tiled=True).astype(
            jnp.float32
        ),
        lax.all_gather(replica_share[9].astype(jnp.bfloat16), "rep", axis=0, tiled=True).astype(
            jnp.float32
        ),
    )
    seg_summed = all_summed[:5]
    cls_summed = all_summed[5:]
    pos_total = lax.psum(pos_local, ("rep", "fsdp"))
    seg_mat_grad = jnp.concatenate(
        [seg_summed[0], seg_summed[1], seg_summed[2], seg_summed[3]], axis=1
    )
    cls_mat_grad = jnp.concatenate(
        [cls_summed[0], cls_summed[1], cls_summed[2], cls_summed[3]], axis=1
    )
    return (
        output_rows.astype(jnp.bfloat16),
        input_grad.astype(jnp.bfloat16),
        seg_mat_grad,
        seg_summed[4],
        cls_mat_grad,
        cls_summed[4],
        pos_total,
        loss_value,
    )


LINE = 4
PLANE = 4
CORES = 2
LANES = 128
GROUP = LINE * PLANE
LOW, WIDE = jnp.bfloat16, jnp.float32
MODEL = HEADS * HEAD_DIM
SPAN = 2 * LANES
TILE_START = (0, 1, 3, 4)


def line_pairs(apart):
    return [(source, (source + apart * PLANE) % GROUP) for source in range(GROUP)]


def plane_pairs(mask):
    return [(source, source ^ mask) for source in range(GROUP)]


def along_line(value, apart):
    return lax.ppermute(value, "fsdp", line_pairs(apart))


def in_plane(value, mask):
    return lax.ppermute(value, "fsdp", plane_pairs(mask))


def other_core(value):
    return lax.ppermute(value, "rep", [(0, 1), (1, 0)])


def after(value, *events):
    return lax.optimization_barrier((value,) + events)[0]


def together(*values):
    return tuple(lax.optimization_barrier(values))


def shape_of(dims, dtype=WIDE):
    return jax.ShapeDtypeStruct(dims, dtype)


def run_kernel(body, name, outs, where, blocks, arrays, scratch=(), far=(), flops=0):
    in_specs = [pl.BlockSpec(memory_space=pltpu.SMEM)]
    in_specs += [pl.BlockSpec(memory_space=pltpu.HBM)] * len(blocks)
    in_specs += [pl.BlockSpec(memory_space=pltpu.VMEM)] * len(arrays)
    spaces = [pltpu.HBM if at in far else pltpu.VMEM for at in range(len(outs))]
    moved = sum(x.size * x.dtype.itemsize for x in list(blocks) + list(arrays))
    moved += sum(math.prod(o.shape) * jnp.dtype(o.dtype).itemsize for o in outs)
    return pl.pallas_call(
        body,
        name=name,
        out_shape=tuple(outs),
        in_specs=in_specs,
        out_specs=tuple(pl.BlockSpec(memory_space=space) for space in spaces),
        scratch_shapes=list(scratch),
        cost_estimate=pl.CostEstimate(flops=flops, bytes_accessed=moved, transcendentals=0),
        compiler_params=pltpu.CompilerParams(vmem_limit_bytes=VMEM_BYTES),
    )(where, *blocks, *arrays)


VMEM_BYTES = 24 * 1024 * 1024
HALF = MODEL // CORES
FF_HALF = FF // CORES
OWN = MODEL // GROUP
QUARTER = 3 * SPAN + 2 * FF // LINE
QUARTER_HALF = QUARTER // CORES


def aligned(start):
    return pl.multiple_of(start, LANES)


def wait_all(copies):
    for copy in copies:
        copy.wait()


def run_copies(pairs, sems):
    copies = [
        pltpu.make_async_copy(source, target, sems.at[at])
        for at, (source, target) in enumerate(pairs)
    ]
    for copy in copies:
        copy.start()
    wait_all(copies)


FIRST = 4 * HALF + LANES
OWN_CUT = FIRST + FF_HALF // 2
LINE_CUTS = (7 * LANES, FF_HALF // 2, FF_HALF // 2)
WIDTHS = (FIRST, FF_HALF, FF_HALF)


def group_pieces(group, refs):
    own, rest = refs[:LINE], refs[LINE:]
    own_x, own_y, far_x, far_y, line_x, line_y, late_x, late_y = rest
    width, cut = WIDTHS[group], LINE_CUTS[group]
    start = sum(WIDTHS[:group])
    if group == 0:
        bases = (sum(WIDTHS) - OWN_CUT, OWN_CUT)
    else:
        before, before_cut = WIDTHS[group - 1], LINE_CUTS[group - 1]
        bases = (2 * before - before_cut, before + before_cut)
    pieces = {(0, step): [(own[step], 0, 0, width)] for step in range(LINE)}
    for mask, whole, line, base in ((1, own_x, line_x, bases[0]), (2, own_y, line_y, bases[1])):
        pieces[mask, 0] = [(whole, start, 0, width)]
        for step in range(1, LINE):
            pieces[mask, step] = [(line, base + (step - 1) * width, 0, width)]
    middle = min(max(OWN_CUT - start, 0), width)
    far = []
    if middle > 0:
        far.append((far_y, start, 0, middle))
    if middle < width:
        far.append((far_x, start + middle - OWN_CUT, middle, width))
    pieces[3, 0] = far
    pieces[3, 1] = [(late_y, 0, 0, width)]
    pieces[3, 2] = [(late_y, width, 0, cut), (late_x, 0, cut, width)]
    pieces[3, 3] = [(late_x, width - cut, 0, width)]
    return pieces


def gather_group(where, group, refs, targets):
    line_at, plane_at = where[0], where[1]
    for (mask, step), parts in group_pieces(group, refs).items():
        chip = (line_at + LINE - step) % LINE * PLANE + (plane_at ^ mask)
        for whole, first, last in targets:
            for ref, offset, begin, end in parts:
                low, high = max(first, begin), min(last, end)
                if low < high:
                    source = slice(offset + low - begin, offset + high - begin)
                    whole[chip, :, low - first : high - first] = ref[:, source]


def gather_blocks(where, refs, base, width, targets):
    line_at, plane_at = where[0], where[1]
    half = LINE // 2
    for mask in range(PLANE):
        for step in range(LINE):
            if mask == 0:
                ref, offset = refs[step], 0
            elif mask == 3:
                ref = refs[LINE + 3] if step < half else refs[LINE + 2]
                offset = step % half * width
            else:
                ref, offset = refs[LINE + mask - 1], base + step * width
            chip = (line_at + LINE - step) % LINE * PLANE + (plane_at ^ mask)
            for whole, first, last in targets:
                whole[chip] = ref[:, offset + first : offset + last]


def whole_rows(ref):
    value = ref[...]
    return value.reshape(value.shape[0] * value.shape[1], value.shape[2])


def prepare_first_kernel(where, seg, seg_vec, cls_vec, flags, out, live_out, sems):
    core_at = where[2]
    pairs = []
    for piece in range(4):
        source = seg.at[:, pl.ds(aligned(piece * MODEL + core_at * HALF), HALF)]
        pairs.append((source, out.at[:, piece * HALF : (piece + 1) * HALF]))
    run_copies(pairs, sems)
    size = seg_vec.shape[0]
    vecs = [vec[...].astype(WIDE).reshape(1, size) for vec in (seg_vec, cls_vec)]
    lines = -(-size // LANES)
    block = jnp.zeros((OWN, LANES), WIDE)
    row_at = lax.broadcasted_iota(jnp.int32, (OWN, LANES), 0)
    for which in range(2):
        for line in range(lines):
            width = min(LANES, size - line * LANES)
            value = vecs[which][:, line * LANES : line * LANES + width]
            if width < LANES:
                value = jnp.concatenate([value, jnp.zeros((1, LANES - width), WIDE)], axis=1)
            block = jnp.where(row_at == which * lines + line, value, block)
    live = flags[...].astype(WIDE).reshape(1, SEG)
    live_out[...] = live
    count = jnp.sum(live, axis=1, keepdims=True)
    block = jnp.where(row_at == 2 * lines, count, block)
    out[:, 4 * HALF :] = block.astype(LOW)


def prepare_rest_kernel(where, seg, cls, *refs):
    second_out, third_out = refs[:2]
    step_outs, out_half, order_out = refs[2 : 2 + LINE], refs[2 + LINE], refs[3 + LINE]
    quarters, sems = refs[4 + LINE :]
    line_at, plane_at, core_at = where[0], where[1], where[2]
    start = core_at * FF_HALF
    pairs = [
        (seg.at[:, pl.ds(aligned(4 * MODEL + start), FF_HALF)], second_out),
        (seg.at[:, pl.ds(aligned(4 * MODEL + FF + start), FF_HALF)], third_out),
        (cls.at[:, pl.ds(aligned(3 * MODEL + core_at * HALF), HALF)], out_half),
    ]
    part = FF // LINE
    for at in range(LINE):
        first = TILE_START[at] * LANES
        plan = [(piece * MODEL + first, SPAN, piece * SPAN) for piece in range(3)]
        plan += [
            (4 * MODEL + piece * FF + at * part, part, 3 * SPAN + piece * part)
            for piece in range(2)
        ]
        for source, size, target in plan:
            pairs.append(
                (
                    cls.at[:, source : source + size],
                    quarters.at[at, :, target : target + size],
                )
            )
    run_copies(pairs, sems)
    lanes = pl.ds(aligned(core_at * QUARTER_HALF), QUARTER_HALF)
    for step, out in enumerate(step_outs):
        out[...] = quarters[(line_at + step) % LINE, :, lanes]
    column = lax.broadcasted_iota(jnp.int32, (1, SPAN), 1)
    feature = lax.broadcasted_iota(jnp.int32, (MODEL, SPAN), 0)
    turn = sum((column >= OWN * step).astype(jnp.int32) for step in range(1, LINE))
    held = column - OWN * turn
    turn = (line_at + turn) % LINE
    for mask in range(PLANE):
        source = (turn * PLANE + (plane_at ^ mask)) * OWN + held
        source = jnp.where(column < OWN * LINE, source, -1)
        order_out[:, mask * SPAN : (mask + 1) * SPAN] = (feature == source).astype(LOW)


def prepare_kernel(where, seg, cls, *refs):
    (seg_vec, cls_vec, flags, first_out, live_out), refs = refs[:5], refs[5:]
    rest, (first_sems, quarters, sems) = refs[:-3], refs[-3:]
    prepare_first_kernel(where, seg, seg_vec, cls_vec, flags, first_out, live_out, first_sems)
    prepare_rest_kernel(where, seg, cls, *rest, quarters, sems)


def lane_mask(rows, head):
    lane = lax.broadcasted_iota(jnp.int32, (rows, LANES), 1)
    return (lane < HEAD_DIM) if head == 0 else (lane >= HEAD_DIM)


def masked(value, mask):
    return jnp.where(mask, value, jnp.zeros_like(value))


def head_probabilities(query, key, allowed):
    scores = product_right(query, key) * HEAD_DIM ** (-0.5)
    scores = jnp.where(allowed, scores, MASK_FILL)
    raised = jnp.exp(scores - jnp.max(scores, axis=-1, keepdims=True))
    return raised / jnp.sum(raised, axis=-1, keepdims=True)


def attend_tiles(qkv, width, allowed):
    rows = qkv.shape[0]
    mixed = []
    for tile in range(width // LANES):
        at = tile * LANES
        query, key, value = (
            qkv[:, piece * width + at : piece * width + at + LANES] for piece in range(3)
        )
        total = jnp.zeros((rows, LANES), WIDE)
        for head in range(2):
            mask = lane_mask(rows, head)
            weights = head_probabilities(masked(query, mask), key, allowed).astype(LOW)
            total = total + product_plain(weights, masked(value, mask))
        mixed.append(total.astype(LOW))
    return mixed


def attend_tiles_back(qkv, grad_mixed, width, allowed):
    rows = qkv.shape[0]
    scale = HEAD_DIM ** (-0.5)
    results = ([], [], [])
    for tile in range(width // LANES):
        at = tile * LANES
        query, key, value = (
            qkv[:, piece * width + at : piece * width + at + LANES] for piece in range(3)
        )
        grad = grad_mixed[:, at : at + LANES]
        totals = [jnp.zeros((rows, LANES), WIDE) for _ in range(3)]
        for head in range(2):
            mask = lane_mask(rows, head)
            query_low, key_low, grad_low = (masked(x, mask) for x in (query, key, grad))
            chance = head_probabilities(query_low, key, allowed)
            grad_chance = product_right(grad_low, value)
            inner = jnp.sum(grad_chance * chance, axis=-1, keepdims=True)
            grad_scores = (chance * (grad_chance - inner)).astype(LOW)
            totals[0] = totals[0] + product_plain(grad_scores, key_low)
            totals[1] = totals[1] + product_left(grad_scores, query_low)
            totals[2] = totals[2] + product_left(chance.astype(LOW), grad_low)
        results[0].append((totals[0] * scale).astype(LOW))
        results[1].append((totals[1] * scale).astype(LOW))
        results[2].append(totals[2].astype(LOW))
    return results[0] + results[1] + results[2]


def token_allowed(live_row):
    shape = (SEG, SEG)
    same = lax.broadcasted_iota(jnp.int32, shape, 0) == lax.broadcasted_iota(jnp.int32, shape, 1)
    return (live_row > 0.5) | same


def qkv_kernel(where, *refs):
    blocks = refs[:12]
    hidden, hidden_got, live_row, live_got, order = refs[12:17]
    weight, out_low, out_high, qkv_out, mixed_out = refs[17:22]
    vectors_out, count_out, ordered_out = refs[22:25]
    vec_rows, flat, inputs, out_half = refs[25:]
    core_at = where[2]
    gather_group(
        where,
        0,
        blocks,
        (
            (weight, 0, 3 * HALF),
            (out_half, 3 * HALF, 4 * HALF),
            (vec_rows, 4 * HALF, 4 * HALF + LANES),
        ),
    )
    out_low[...] = out_half[: GROUP // 2]
    out_high[...] = out_half[GROUP // 2 :]
    piece = (8 * MODEL + FF) // GROUP
    lines = -(-piece // LANES)
    count = jnp.zeros((1, LANES), WIDE)
    for chip in range(GROUP):
        rows = vec_rows[chip, 0:16, :].astype(WIDE)
        for block in range(2):
            joined = jnp.concatenate(
                [rows[block * lines + r : block * lines + r + 1] for r in range(lines)], axis=1
            )
            flat[block : block + 1, chip * piece : (chip + 1) * piece] = joined[:, :piece]
        count = count + rows[2 * lines : 2 * lines + 1]
    rows_each = (8 * MODEL + FF) // MODEL
    for block in range(2):
        for row in range(rows_each):
            vectors_out[block * rows_each + row : block * rows_each + row + 1, :] = flat[
                block : block + 1, row * MODEL : (row + 1) * MODEL
            ]
    count_out[...] = jnp.broadcast_to(count, count_out.shape)
    inputs[:SEG] = hidden[...]
    inputs[SEG:] = hidden_got[...]
    projected = product_plain(inputs[...], whole_rows(weight))
    lanes = pl.ds(aligned(core_at * HALF), HALF)
    qkv_out[:, :HALF] = (projected[:, :HALF] + vectors_out[0:1, lanes]).astype(LOW)
    qkv_out[:, HALF : 2 * HALF] = projected[:, HALF : 2 * HALF].astype(LOW)
    qkv_out[:, 2 * HALF :] = (projected[:, 2 * HALF :] + vectors_out[1:2, lanes]).astype(LOW)
    for part, live in enumerate((live_row, live_got)):
        rows = slice(part * SEG, (part + 1) * SEG)
        tiles = attend_tiles(qkv_out[rows, :], HALF, token_allowed(live[...]))
        for tile, value in enumerate(tiles):
            mixed_out[rows, tile * LANES : (tile + 1) * LANES] = value
    ordered_out[...] = product_plain(inputs[...], order[...]).astype(LOW)


def norm_rows(summed):
    row_mean = jnp.mean(summed, axis=-1, keepdims=True)
    centered = summed - row_mean
    inv_dev = lax.rsqrt(jnp.mean(centered * centered, axis=-1, keepdims=True) + NORM_EPS)
    return centered * inv_dev, inv_dev


def norm_rows_back(grad_out, normed, inv_dev, gain):
    scaled = grad_out * gain
    mean_one = jnp.mean(scaled, axis=-1, keepdims=True)
    mean_two = jnp.mean(scaled * normed, axis=-1, keepdims=True)
    return inv_dev * (scaled - mean_one - normed * mean_two)


def column_sum(value):
    return jnp.sum(value.astype(WIDE), axis=0, keepdims=True)


def four_rows(vectors, first):
    return jnp.concatenate([vectors[first + at : first + at + 1, :] for at in range(4)], axis=1)


def gelu_both(before):
    half = 0.5 * (1.0 + lax.erf(before * SQRT_HALF))
    slope = half + before * jnp.exp(-0.5 * before * before) * INV_SQRT_TWO_PI
    return before * half, slope


def out_kernel(where, hidden, mixed, mixed_got, low, high, low_got, high_got, *refs):
    vectors, order, full_out, ordered_out, normed_out, inv_out, low_out, mixed_full = refs
    core_at = where[2]
    own, other = aligned(core_at * HALF), aligned((1 - core_at) * HALF)
    rows = MODEL // 2
    full_out[:rows, pl.ds(own, HALF)] = whole_rows(low)
    full_out[rows:, pl.ds(own, HALF)] = whole_rows(high)
    full_out[:rows, pl.ds(other, HALF)] = whole_rows(low_got)
    full_out[rows:, pl.ds(other, HALF)] = whole_rows(high_got)
    mixed_full[:, pl.ds(own, HALF)] = mixed[...]
    mixed_full[:SEG, pl.ds(other, HALF)] = mixed_got[SEG:, :]
    mixed_full[SEG:, pl.ds(other, HALF)] = mixed_got[:SEG, :]
    branch = product_plain(mixed_full[:SEG, :], full_out[...])
    normed, inv_dev = norm_rows(hidden[...].astype(WIDE) + branch + vectors[2:3, :])
    normed_out[...] = normed
    inv_out[...] = inv_dev
    low_out[...] = (normed * vectors[4:5, :] + vectors[5:6, :]).astype(LOW)
    ordered_out[...] = product_plain(mixed_full[...], order[...]).astype(LOW)


def up_kernel(where, *refs):
    blocks = refs[:12]
    low, low_got, vectors = refs[12:15]
    weight, act_out, slope_out, both = refs[15:]
    core_at = where[2]
    gather_group(where, 1, blocks, ((weight, 0, FF_HALF),))
    both[:SEG] = low[...]
    both[SEG:] = low_got[...]
    for at in range(FF_HALF // MODEL):
        columns = slice(at * MODEL, (at + 1) * MODEL)
        held = weight[:, :, columns]
        before = product_plain(both[...], held.reshape(MODEL, MODEL))
        bias = vectors[pl.ds(8 + core_at * (FF_HALF // MODEL) + at, 1), :]
        value, slope = gelu_both(before + bias)
        act_out[:, columns] = value.astype(LOW)
        slope_out[:, columns] = slope


def down_kernel(where, *refs):
    blocks, act = refs[:12], refs[12]
    weight, own_out, send_out = refs[13:]
    gather_group(where, 2, blocks, ((weight, 0, FF_HALF),))
    partial = product_right(act[...], whole_rows(weight))
    own_out[...] = partial[:SEG]
    send_out[...] = partial[SEG:]


def seg_rows_kernel(where, *refs):
    own, got, normed_first, vectors, targets, live, seg_pos = refs[:7]
    normed_out, inv_out, diff_out, rows_out, head_out = refs[7:]
    doc, number = where[3], where[4]
    first = normed_first[...] * vectors[4:5, :] + vectors[5:6, :]
    normed, inv_dev = norm_rows(first + own[...] + got[...] + vectors[3:4, :])
    normed_out[...] = normed
    inv_out[...] = inv_dev
    rows = normed * vectors[6:7, :] + vectors[7:8, :]
    shape = (SEG, SEG)
    same = lax.broadcasted_iota(jnp.int32, shape, 0) == lax.broadcasted_iota(jnp.int32, shape, 1)
    live_rows = jnp.sum(jnp.where(same, live[...], 0.0), axis=1, keepdims=True)
    target_rows = targets[...].astype(WIDE)
    output = rows * live_rows
    rows_out[...] = output
    diff = (output - target_rows) * live_rows
    row_at = lax.broadcasted_iota(jnp.int32, (SEG, 1), 0)
    diff = jnp.where(row_at > 0, diff, 0.0)
    diff_out[...] = diff
    table = seg_pos[...].astype(WIDE)
    chosen = lax.broadcasted_iota(jnp.int32, table.shape, 0) == number
    position = jnp.sum(jnp.where(chosen, table, 0.0), axis=0, keepdims=True)
    head_out[:, :MODEL] = rows[0:1, :] + position
    head_out[:, MODEL : 2 * MODEL] = target_rows[0:1, :]
    square = jnp.sum(column_sum(diff * diff), axis=1, keepdims=True)
    lane = lax.broadcasted_iota(jnp.int32, (1, LANES), 1)
    facts = jnp.where(lane == 0, live_rows[0:1, :], 0.0)
    facts = jnp.where(lane == 1, doc.astype(WIDE), facts)
    facts = jnp.where(lane == 2, number.astype(WIDE), facts)
    facts = jnp.where(lane == 3, square, facts)
    head_out[:, 2 * MODEL :] = facts


def second_norm_kernel(where, diff, count, normed, inv_dev, vectors, grad_out, low_out, sums_out):
    grad_top = diff[...] * ((SEG * GROUP * CORES) / count[0:1, 0:1])
    normed_rows = normed[...]
    grad = norm_rows_back(grad_top, normed_rows, inv_dev[...], vectors[6:7, :])
    low = grad.astype(LOW)
    grad_out[...] = grad
    low_out[...] = low
    sums_out[0:1, :] = column_sum(low)
    sums_out[1:2, :] = column_sum(grad_top * normed_rows)
    sums_out[2:3, :] = column_sum(grad_top)


def mlp_back_kernel(where, *refs):
    low, low_got, down_weight, up_weight, slope = refs[:5]
    pre_out, own_out, send_out, sums_out, both = refs[5:]
    both[:SEG] = low[...]
    both[SEG:] = low_got[...]
    for at in range(FF_HALF // MODEL):
        columns = slice(at * MODEL, (at + 1) * MODEL)
        held = down_weight[:, :, columns]
        before = product_plain(both[...], held.reshape(MODEL, MODEL))
        pre = (before * slope[:, columns]).astype(LOW)
        pre_out[:, columns] = pre
        sums_out[at : at + 1, :] = column_sum(pre)
    partial = product_right(pre_out[...], whole_rows(up_weight))
    own_out[...] = partial[:SEG]
    send_out[...] = partial[SEG:]


def scatter_parts(where, parts, outs, sems):
    line_at, plane_at = where[0], where[1]
    far_low, far_high, to_x, to_y, kept = outs
    half = LINE // 2
    copies = []
    for mask in range(PLANE):
        for step in range(LINE):
            source = parts.at[(line_at + step) % LINE * PLANE + (plane_at ^ mask)]
            if mask == 3:
                target = far_low.at[step] if step < half else far_high.at[step - half]
            else:
                target = (kept, to_x, to_y)[mask].at[step]
            copies.append(pltpu.make_async_copy(source, target, sems.at[len(copies)]))
    for copy in copies:
        copy.start()
    wait_all(copies)


def mlp_weight_kernel(where, *refs):
    first, first_got, second, second_got, pre, act = refs[:6]
    outs = refs[6:11]
    left, parts, sems = refs[11:]
    for at, (own, got, right) in enumerate(((first, first_got, pre), (second, second_got, act))):
        left[:SEG] = own[...]
        left[SEG:] = got[...]
        for piece in range(FF_HALF // MODEL):
            start = piece * MODEL
            product = product_left(left[...], right[:, start : start + MODEL]).astype(LOW)
            target = at * FF_HALF + start
            parts[:, :, target : target + MODEL] = product.reshape(GROUP, OWN, MODEL)
    scatter_parts(where, parts, outs, sems)


def attn_product(where, refs, mask, piece):
    hidden, mixed, proj, branch, got = refs
    lanes = slice(mask * SPAN, (mask + 1) * SPAN)
    if piece < 3:
        right = proj[:, piece * HALF : (piece + 1) * HALF]
        product = product_left(hidden[:, lanes], right)
    else:
        own = branch[:, pl.ds(aligned(where[2] * HALF), HALF)]
        product = product_left(mixed[:SEG, lanes], own)
        product = product + product_left(mixed[SEG:, lanes], got[:, HALF:])
    return product[: LINE * OWN].astype(LOW).reshape(LINE, OWN, HALF)


def attn_far_kernel(where, *refs):
    low_out, high_out = refs[5:]
    half = LINE // 2
    for piece in range(4):
        columns = slice(piece * HALF, (piece + 1) * HALF)
        product = attn_product(where, refs[:5], 3, piece)
        low_out[:, :, columns] = product[:half]
        high_out[:, :, columns] = product[half:]


def attn_near_kernel(where, *refs):
    top_row, out_rows, live_row = refs[5:8]
    row_at = lax.broadcasted_iota(jnp.int32, (SEG, 1), 0)
    output = jnp.where(row_at == 0, top_row[...] * live_row[:, 0:1], out_rows[...])
    refs[11][...] = output.astype(LOW)
    for mask, out in ((1, refs[8]), (2, refs[9]), (0, refs[10])):
        for piece in range(4):
            columns = slice(piece * HALF, (piece + 1) * HALF)
            out[:, :, columns] = attn_product(where, refs[:5], mask, piece)


def fold_kernel(where, kept, got_x, got_y, *refs):
    extra, own_out, sent = refs[: -LINE], refs[-LINE], refs[1 - LINE :]
    rows = kept.shape[1]
    for step in range(LINE):
        total = kept[step].astype(WIDE) + got_x[step].astype(WIDE) + got_y[step].astype(WIDE)
        if step == 0:
            own_out[...] = total
            continue
        out = sent[step - 1]
        out[:rows, :] = total.astype(LOW)
        if extra:
            out[rows:, :] = jnp.zeros_like(out[rows:, :])
            out[rows:, : extra[0].shape[1]] = extra[0][...]


def reduce_far(parts):
    return together(in_plane(parts[0], 2), in_plane(parts[1], 1))


def reduce_add(where, parts, far):
    shape = parts[2].shape
    return run_kernel(
        add_far_kernel,
        "add_far",
        [shape_of(shape, LOW)] * 2,
        where,
        (),
        tuple(far) + (parts[2], parts[3]),
    )


def reduce_fold(where, kept, got, *extra):
    _, rows, columns = kept.shape
    more = sum(value.shape[0] for value in extra)
    return run_kernel(
        fold_kernel,
        "fold",
        [shape_of((rows, columns))] + [shape_of((rows + more, columns), LOW)] * (LINE - 1),
        where,
        (),
        (kept,) + tuple(got) + extra,
    )


def reduce_line(own, pieces):
    total = own
    for piece in pieces:
        total = total + piece[: own.shape[0]].astype(WIDE)
    return total


def head_back_kernel(where, *refs):
    grad, grad_got, down_weight, up_weight, slope, act, low, low_got = refs[:8]
    own_out, send_out, data_out = refs[8:]
    few = 16
    row_at = lax.broadcasted_iota(jnp.int32, (few, 1), 0)

    def two_rows(first, second):
        return jnp.where(row_at == 0, first, jnp.where(row_at == 1, second, 0.0))

    second = two_rows(grad[...], grad_got[...]).astype(LOW)
    data_out[0:1, :] = low[0:1, :].astype(WIDE)
    data_out[1:2, :] = low_got[0:1, :].astype(WIDE)
    data_out[2:4, :] = second[0:2].astype(WIDE)
    partial = jnp.zeros((few, MODEL), WIDE)
    for at in range(FF_HALF // MODEL):
        columns = slice(at * MODEL, (at + 1) * MODEL)
        before = product_plain(second, down_weight[:, :, columns].reshape(MODEL, MODEL))
        slopes = two_rows(slope[0:1, columns], slope[SEG : SEG + 1, columns])
        pre = (before * slopes).astype(LOW)
        partial = partial + product_right(pre, up_weight[:, :, columns].reshape(MODEL, MODEL))
        data_out[4 + 2 * at : 6 + 2 * at, :] = pre[0:2].astype(WIDE)
        data_out[8 + 2 * at : 9 + 2 * at, :] = act[0:1, columns].astype(WIDE)
        data_out[9 + 2 * at : 10 + 2 * at, :] = act[SEG : SEG + 1, columns].astype(WIDE)
    own_out[...] = partial[0:1]
    send_out[...] = partial[1:2]


def first_norm_kernel(where, *refs):
    second_grad, own, got, head_grad, head_own, head_got = refs[:6]
    normed_rows, inv_dev, vectors, out_weight = refs[6:10]
    grad_out, branch_out, mixed_out, send_out, sums_out = refs[10:]
    core_at = where[2]
    grad_rows = second_grad[...] + own[...] + got[...]
    head = head_grad[...] + head_own[...] + head_got[...]
    row_at = lax.broadcasted_iota(jnp.int32, (SEG, 1), 0)
    grad_rows = jnp.where(row_at == 0, head, grad_rows)
    normed = normed_rows[...]
    grad = norm_rows_back(grad_rows, normed, inv_dev[...], vectors[4:5, :])
    grad_out[...] = grad
    branch = grad.astype(LOW)
    branch_out[...] = branch
    mixed_out[...] = product_right(branch, out_weight[...]).astype(LOW)
    other = pl.ds(aligned((1 - core_at) * HALF), HALF)
    send_out[:, :HALF] = mixed_out[:, other]
    send_out[:, HALF:] = branch_out[:, other]
    sums_out[0:1, :] = column_sum(branch)
    sums_out[1:2, :] = column_sum(grad_rows * normed)
    sums_out[2:3, :] = column_sum(grad_rows)


def attn_back_kernel(where, *refs):
    qkv, mixed_grad, got, live_row, live_got, weight = refs[:6]
    sums_first, sums_second, sums_up, head_top, head_normed, data = refs[6:12]
    proj_out, own_out, send_out, payload_out, rows = refs[12:]
    core_at = where[2]
    lanes = pl.ds(aligned(core_at * HALF), HALF)
    for part, live in enumerate((live_row, live_got)):
        at = slice(part * SEG, (part + 1) * SEG)
        grad = mixed_grad[:, lanes] if part == 0 else got[:, :HALF]
        pieces = attend_tiles_back(qkv[at, :], grad, HALF, token_allowed(live[...]))
        for tile, value in enumerate(pieces):
            proj_out[at, tile * LANES : (tile + 1) * LANES] = value
    partial = product_right(proj_out[...], whole_rows(weight))
    own_out[...] = partial[:SEG]
    send_out[...] = partial[SEG:]
    rows[...] = jnp.zeros_like(rows)
    rows[0:12, :] = data[0:12, :]
    rows[12:13, lanes] = column_sum(proj_out[:, :HALF])
    rows[13:14, lanes] = column_sum(proj_out[:, 2 * HALF :])
    rows[14:15, :] = sums_first[0:1, :]
    rows[15:16, :] = sums_second[0:1, :] + data[2:3, :]
    rows[16:18, :] = sums_first[1:3, :]
    rows[18:19, :] = sums_second[1:2, :] + head_top[...] * head_normed[0:1, :]
    rows[19:20, :] = sums_second[2:3, :] + head_top[...]
    for at in range(FF_HALF // MODEL):
        total = sums_up[at : at + 1, :] + data[4 + 2 * at : 5 + 2 * at, :]
        total = total + data[5 + 2 * at : 6 + 2 * at, :]
        rows[pl.ds(20 + core_at * (FF_HALF // MODEL) + at, 1), :] = total
    payload_out[...] = rows[...].astype(LOW)


def cls_gather_kernel(where, *refs):
    blocks = refs[:8]
    own_out, from_x, from_y, far_x = refs[8], refs[4], refs[5], refs[6]
    weight_out, out_rows = refs[9:]
    plane_at = where[1]
    gather_blocks(where, blocks, 0, QUARTER_HALF, ((weight_out, 0, QUARTER_HALF),))
    first = LINE * QUARTER_HALF
    out_rows[plane_at] = own_out[...]
    out_rows[plane_at ^ 1] = from_x[:, first : first + HALF]
    out_rows[plane_at ^ 2] = from_y[:, first : first + HALF]
    first = LINE // 2 * QUARTER_HALF
    out_rows[plane_at ^ 3] = far_x[:, first : first + HALF]


def cls_weight_kernel(where, own, got, out_half, out_got, weight_out, out_full):
    line_at, core_at = where[0], where[2]
    out_full[...] = jnp.zeros_like(out_full)
    for value, part, core in ((own, out_half, core_at), (got, out_got, 1 - core_at)):
        weight_out[:, :, pl.ds(aligned(core * QUARTER_HALF), QUARTER_HALF)] = value[...]
        rows = part[...].reshape(3, HEAD_DIM, HALF)
        out_full[pl.ds(line_at % 2, 3), :, pl.ds(aligned(core * HALF), HALF)] = rows


def add_far_kernel(where, far_low, far_high, to_x, to_y, x_out, y_out):
    half = LINE // 2
    x_out[:half] = to_x[:half] + far_low[...]
    x_out[half:] = to_x[half:]
    y_out[:half] = to_y[:half]
    y_out[half:] = to_y[half:] + far_high[...]


def row_from_column(column, size):
    shape = (size, size)
    same = lax.broadcasted_iota(jnp.int32, shape, 0) == lax.broadcasted_iota(jnp.int32, shape, 1)
    return jnp.sum(jnp.where(same, column, 0.0), axis=0, keepdims=True)


def head_allowed(heads):
    facts = heads[:, 2 * MODEL :]
    live, doc = facts[:, 0:1], facts[:, 1:2]
    shape = (GROUP, GROUP)
    same = lax.broadcasted_iota(jnp.int32, shape, 0) == lax.broadcasted_iota(jnp.int32, shape, 1)
    live_row, doc_row = row_from_column(live, GROUP), row_from_column(doc, GROUP)
    return ((live_row > 0.5) & (doc == doc_row)) | same


def quarter_mask(quarter):
    lane = lax.broadcasted_iota(jnp.int32, (GROUP, SPAN), 1)
    first = (quarter % 2) * HEAD_DIM
    return (lane >= first) & (lane < first + 3 * HEAD_DIM)


def quarter_piece(vectors, row, quarter):
    value = jnp.zeros((1, SPAN), WIDE)
    for at in range(LINE):
        first = TILE_START[at] * LANES
        value = jnp.where(quarter == at, vectors[row : row + 1, first : first + SPAN], value)
    return value


def cls_attend_kernel(where, *refs):
    stacks, vectors, weight, out_weight = refs[:4], refs[4], refs[5], refs[6]
    heads_out, qkv_out, mixed_out, part_out = refs[7:]
    line_at, plane_at = where[0], where[1]
    for step, stack in enumerate(stacks):
        for mask in range(PLANE):
            row = (line_at + LINE - step) % LINE * PLANE + (plane_at ^ mask)
            heads_out[pl.ds(row, 1), :] = stack[mask : mask + 1, :]
    heads = heads_out[...]
    inputs = heads[:, :MODEL].astype(LOW)
    projected = product_plain(inputs, weight[:, : 3 * SPAN])
    query = projected[:, :SPAN] + quarter_piece(vectors, 12, line_at)
    value = projected[:, 2 * SPAN :] + quarter_piece(vectors, 13, line_at)
    qkv_out[:, :SPAN] = query.astype(LOW)
    qkv_out[:, SPAN : 2 * SPAN] = projected[:, SPAN : 2 * SPAN].astype(LOW)
    qkv_out[:, 2 * SPAN :] = value.astype(LOW)
    mixed = attend_tiles(qkv_out[...], SPAN, head_allowed(heads))
    mixed = masked(jnp.concatenate(mixed, axis=1), quarter_mask(line_at))
    mixed_out[...] = mixed
    part_out[...] = product_plain(mixed, out_weight[...])


def cls_mlp_kernel(where, *refs):
    heads, own, got_one, got_two, got_three, vectors, weight = refs[:7]
    normed_out, inv_out, low_out, act_out, slope_out, part_out = refs[7:]
    line_at = where[0]
    branch = own[...] + got_one[...] + got_two[...] + got_three[...]
    normed, inv_dev = norm_rows(heads[:, :MODEL] + branch + vectors[14:15, :])
    normed_out[...] = normed
    inv_out[...] = inv_dev
    low = (normed * vectors[16:17, :] + vectors[17:18, :]).astype(LOW)
    low_out[...] = low
    part = FF // LINE
    first = 3 * SPAN
    bias = vectors[pl.ds(20 + line_at, 1), :]
    before = product_plain(low, weight[:, first : first + part]) + bias
    value, slope = gelu_both(before)
    act = value.astype(LOW)
    act_out[...] = act
    slope_out[...] = slope
    part_out[...] = product_right(act, weight[:, first + part :])


def cls_top_kernel(where, *refs):
    heads, own, got_one, got_two, got_three, vectors, weight = refs[:7]
    normed_first, count, slope = refs[7:10]
    top_out, square_out, grad_out, second_out, pre_out, part_out, sums_out = refs[10:17]
    held = refs[17]
    rank = where[0] * PLANE + where[1]
    first = normed_first[...] * vectors[16:17, :] + vectors[17:18, :]
    down = own[...] + got_one[...] + got_two[...] + got_three[...]
    normed, inv_dev = norm_rows(first + down + vectors[15:16, :])
    rows = normed * vectors[18:19, :] + vectors[19:20, :]
    held[...] = rows
    top_out[...] = held[pl.ds(rank, 1), :]
    facts = heads[:, 2 * MODEL :]
    live = facts[:, 0:1]
    diff = (rows * live - heads[:, MODEL : 2 * MODEL]) * live
    square = jnp.sum(column_sum(diff * diff), axis=1, keepdims=True)
    square = square + jnp.sum(facts[:, 3:4], axis=0, keepdims=True)
    square_out[...] = jnp.broadcast_to(square, square_out.shape)
    grad_top = diff * ((SEG * GROUP * CORES) / count[0:1, 0:1])
    grad = norm_rows_back(grad_top, normed, inv_dev, vectors[18:19, :])
    sums_out[0:1, :] = column_sum(grad_top * normed)
    sums_out[1:2, :] = column_sum(grad_top)
    grad_out[...] = grad
    second = grad.astype(LOW)
    second_out[...] = second
    part = FF // LINE
    at = 3 * SPAN
    pre = (product_plain(second, weight[:, at + part :]) * slope[...]).astype(LOW)
    pre_out[...] = pre
    part_out[...] = product_right(pre, weight[:, at : at + part])


def cls_attend_back_kernel(where, *refs):
    heads, own, got_one, got_two, got_three, vectors, weight, out_weight = refs[:8]
    grad_in, normed_first, inv_first, qkv = refs[8:12]
    grad_out, branch_out, proj_out, part_out, sums_out = refs[12:]
    line_at = where[0]
    grad_first = grad_in[...] + own[...] + got_one[...] + got_two[...] + got_three[...]
    normed = normed_first[...]
    grad = norm_rows_back(grad_first, normed, inv_first[...], vectors[16:17, :])
    sums_out[0:1, :] = column_sum(grad_first * normed)
    sums_out[1:2, :] = column_sum(grad_first)
    grad_out[...] = grad
    branch = grad.astype(LOW)
    branch_out[...] = branch
    mask = quarter_mask(line_at)
    mixed_grad = masked(product_right(branch, out_weight[...]).astype(LOW), mask)
    pieces = attend_tiles_back(qkv[...], mixed_grad, SPAN, head_allowed(heads[...]))
    tiles = SPAN // LANES
    for piece in range(3):
        joined = jnp.concatenate(pieces[piece * tiles : (piece + 1) * tiles], axis=1)
        proj_out[:, piece * SPAN : (piece + 1) * SPAN] = masked(joined, mask)
    part_out[...] = product_right(proj_out[...], weight[:, : 3 * SPAN])


def cls_end_kernel(where, *refs):
    heads, grad, own, got_one, got_two, got_three = refs[:6]
    square, sums_back, sums_top = refs[6:9]
    normed_second, inv_second, vectors = refs[9:12]
    row_out, second_out, shared_out, held = refs[12:]
    rank = where[0] * PLANE + where[1]
    total = grad[...] + own[...] + got_one[...] + got_two[...] + got_three[...]
    held[...] = total
    row = held[pl.ds(rank, 1), :]
    row_out[...] = row
    second_out[...] = norm_rows_back(
        row, normed_second[0:1, :], inv_second[0:1, :], vectors[6:7, :]
    )
    number = row_from_column(heads[:, 2 * MODEL + 2 : 2 * MODEL + 3], GROUP)
    entry = lax.broadcasted_iota(jnp.int32, (GROUP, GROUP), 0).astype(WIDE)
    hot = (entry == number).astype(WIDE)
    shared_out[0:GROUP, :] = jnp.dot(hot, total, precision=lax.Precision.HIGHEST)
    shared_out[GROUP : GROUP + 1, 0:LANES] = square[0:1, :]
    shared_out[GROUP + 1 : GROUP + 3, :] = sums_back[0:2, :]
    shared_out[GROUP + 3 : GROUP + 5, :] = sums_top[0:2, :]


def head_mlp_kernel(where, *refs):
    cls_mlp_kernel(where, *refs[:7], *refs[11:17])
    add_far_kernel(where, *refs[7:11], *refs[17:])


def head_end_kernel(where, *refs):
    cls_end_kernel(where, *refs[:12], *refs[16:19], refs[23])
    fold_kernel(where, *refs[12:16], *refs[19:23])


def attn_add_kernel(where, *refs):
    far_low, far_high, to_x, to_y, grad, own, got, x_out, y_out, input_out = refs
    add_far_kernel(where, far_low, far_high, to_x, to_y, x_out, y_out)
    input_out[...] = (grad[...] + own[...] + got[...]).astype(LOW)


def cls_rows_kernel(where, *refs):
    packs = refs[:4]
    heads, branch, low, second = refs[4:8]
    out, kept = refs[8:]
    line_at = where[0]
    rows, width = kept.shape[1:]
    for step, pack in enumerate(packs):
        first = pack.shape[0] - rows
        kept[(line_at + LINE - step) % LINE] = pack[first:, :width]
    starts = (MODEL, 2 * MODEL, 3 * MODEL, 4 * MODEL)
    out[:, 0:MODEL] = heads[:, :MODEL].astype(LOW)
    for piece, start in enumerate(starts):
        from_at = piece * SPAN
        for tile in range(MODEL // LANES):
            total = None
            for at in range(PLANE):
                inner = tile - TILE_START[at]
                if inner in (0, 1):
                    first = from_at + inner * LANES
                    value = kept[at, :, first : first + LANES]
                    total = value if total is None else total + value
            out[:, start + tile * LANES : start + (tile + 1) * LANES] = total
    out[:, 5 * MODEL : 6 * MODEL] = branch[...]
    out[:, 6 * MODEL : 7 * MODEL] = low[...]
    out[:, 7 * MODEL + FF : 8 * MODEL + FF] = second[...]
    part = FF // LINE
    for at in range(PLANE):
        first = 4 * SPAN
        out[:, 7 * MODEL + at * part : 7 * MODEL + (at + 1) * part] = kept[
            at, :, first : first + part
        ]
        out[:, 8 * MODEL + FF + at * part : 8 * MODEL + FF + (at + 1) * part] = kept[
            at, :, first + part : first + 2 * part
        ]


def own_features(rank, width):
    shape = (MODEL, width)
    feature = lax.broadcasted_iota(jnp.int32, shape, 0)
    column = lax.broadcasted_iota(jnp.int32, shape, 1)
    return (feature == rank * width + column).astype(LOW)


def own_vector(rank, pieces, out, flat):
    size = out.shape[0]
    for at, piece in enumerate(pieces):
        flat[:, at * MODEL : (at + 1) * MODEL] = piece
    value = jnp.zeros((1, size), WIDE)
    for chip in range(GROUP):
        value = jnp.where(rank == chip, flat[:, chip * size : (chip + 1) * size], value)
    out[...] = value.reshape(size)


def cls_owner_kernel(where, *refs):
    own, got, shared, mats_out, vec_out, rows, flat = refs
    rank = where[0] * PLANE + where[1]
    width = mats_out.shape[0]
    rows[:GROUP] = own[...]
    rows[GROUP:] = got[...]
    chosen = own_features(rank, width)
    plan = (
        (0, MODEL, 3 * MODEL, 0),
        (4 * MODEL, 5 * MODEL, MODEL, 3 * MODEL),
        (6 * MODEL, 7 * MODEL, FF, 4 * MODEL),
        (7 * MODEL + FF, 8 * MODEL + FF, FF, 4 * MODEL + FF),
    )
    for left, right, size, target in plan:
        side = product_plain(rows[:, left : left + MODEL], chosen).astype(LOW)
        mats_out[:, target : target + size] = product_left(side, rows[:, right : right + size])
    starts = (MODEL, 3 * MODEL, 5 * MODEL, 7 * MODEL + FF)
    pieces = [column_sum(rows[:, start : start + MODEL]) for start in starts]
    pieces += [shared[GROUP + 1 + at : GROUP + 2 + at, :] for at in range(4)]
    starts = [7 * MODEL + at * MODEL for at in range(FF // MODEL)]
    pieces += [column_sum(rows[:, start : start + MODEL]) for start in starts]
    own_vector(rank, pieces, vec_out, flat)


def head_share_kernel(where, *refs):
    packs, mlp = refs[:4], refs[4]
    mine_out, vecs_out, rows = refs[5:]
    rank = where[0] * PLANE + where[1]
    count = LINE * 24
    for at, pack in enumerate(packs):
        rows[at * count : (at + 1) * count] = pack[...]
    total = PLANE * count

    def chosen(base, apart):
        shape = (CORES * GROUP, total)
        row = lax.broadcasted_iota(jnp.int32, shape, 0)
        column = lax.broadcasted_iota(jnp.int32, shape, 1)
        hot = (column == row // 2 * 24 + base + row % 2 * apart).astype(LOW)
        return product_plain(hot, rows[...]).astype(LOW)

    own = own_features(rank, OWN)
    for at, (left, right) in enumerate(((0, 4), (2, 8))):
        side = product_plain(chosen(left, 1), own).astype(LOW)
        for piece in range(FF_HALF // MODEL):
            columns = slice(at * FF_HALF + piece * MODEL, at * FF_HALF + (piece + 1) * MODEL)
            share = product_left(side, chosen(right + 2 * piece, 1))
            mine_out[:, columns] = mlp[:, columns] + share
    shape = (16, total)
    row = lax.broadcasted_iota(jnp.int32, shape, 0)
    column = lax.broadcasted_iota(jnp.int32, shape, 1)
    hot = ((column % 24 == row + 12) & (row < 12)).astype(LOW)
    vecs_out[...] = product_plain(hot, rows[...])


def share_owner_kernel(where, *refs):
    head_share_kernel(where, *refs[:5], *refs[9:11], refs[15])
    cls_owner_kernel(where, *refs[5:8], *refs[11:13], *refs[16:])
    shared, count, pos_out, loss_out = refs[7], refs[8], refs[13], refs[14]
    pos_out[...] = shared[:GROUP, :]
    loss_out[...] = shared[GROUP : GROUP + 1, 0:1] / (count[0:1, 0:1] * MODEL)


def seg_vec_kernel(where, vecs, vecs_got, vec_out, flat):
    rank = where[0] * PLANE + where[1]
    rows = (8 * MODEL + FF) // MODEL
    pieces = [vecs[at : at + 1, :] + vecs_got[at : at + 1, :] for at in range(rows)]
    own_vector(rank, pieces, vec_out, flat)


def column_copies(where, out, base, size, own, got, first):
    core_at = where[2]
    lanes = slice(first, first + size)
    return [
        (own.at[:, lanes], out.at[:, pl.ds(aligned(base + core_at * size), size)]),
        (got.at[:, lanes], out.at[:, pl.ds(aligned(base + (1 - core_at) * size), size)]),
    ]


def store_kernel(where, attn, attn_got, mlp, mlp_got, vecs, vecs_got, out, vec_out, flat, sems):
    pairs = []
    for piece in range(4):
        pairs += column_copies(where, out, piece * MODEL, HALF, attn, attn_got, piece * HALF)
    for piece in range(2):
        base = 4 * MODEL + piece * FF
        pairs += column_copies(where, out, base, FF_HALF, mlp, mlp_got, piece * FF_HALF)
    copies = [
        pltpu.make_async_copy(source, target, sems.at[at])
        for at, (source, target) in enumerate(pairs)
    ]
    for copy in copies:
        copy.start()
    seg_vec_kernel(where, vecs, vecs_got, vec_out, flat)
    wait_all(copies)


def plane_parts(part):
    return (part,) + together(*(in_plane(part, mask) for mask in range(1, PLANE)))


def line_parts(part):
    return (part,) + together(*(along_line(part, apart) for apart in range(1, LINE)))


def slice_local(
    hidden_in,
    targets,
    doc_ids,
    seg_nums,
    valid_flags,
    seg_mats,
    seg_vecs,
    cls_mats,
    cls_vecs,
    seg_pos,
):
    rank, core_at = lax.axis_index("fsdp"), lax.axis_index("rep")
    line_at, plane_at = rank // PLANE, rank % PLANE
    where = jnp.stack([line_at, plane_at, core_at, doc_ids[0], seg_nums[0]]).astype(jnp.int32)
    own_rows, total_columns = seg_mats.shape
    vec_size = seg_vecs.shape[0]
    both_rows = CORES * SEG

    first_piece, live_row, *rest = run_kernel(
        prepare_kernel,
        "prepare",
        [shape_of((own_rows, FIRST), LOW), shape_of((1, SEG))]
        + [shape_of((own_rows, FF_HALF), LOW)] * 2
        + [shape_of((own_rows, QUARTER_HALF), LOW)] * LINE
        + [shape_of((own_rows, HALF), LOW), shape_of((MODEL, PLANE * SPAN), LOW)],
        where,
        (seg_mats, cls_mats),
        (seg_vecs, cls_vecs, valid_flags),
        [
            pltpu.SemaphoreType.DMA((4,)),
            pltpu.VMEM((LINE, own_rows, QUARTER), LOW),
            pltpu.SemaphoreType.DMA((3 + 5 * LINE,)),
        ],
    )
    first_line = line_parts(first_piece)
    second_piece, third_piece, quarters, cls_out_piece, order = (
        rest[0],
        rest[1],
        rest[2:-2],
        rest[-2],
        rest[-1],
    )

    def joined(*pieces):
        return jnp.concatenate(pieces, axis=1)

    def sent_both(to_x, to_y):
        to_x, to_y = together(to_x, to_y)
        return together(in_plane(to_x, 1), in_plane(to_y, 2))

    own_sent = joined(first_piece, second_piece, third_piece)
    own_x, own_y = sent_both(own_sent, own_sent)
    first_line = first_line[:1] + tuple(after(got, own_x, own_y) for got in first_line[1:])
    hidden_got = other_core(after(hidden_in, own_x, own_y))
    live_got = other_core(after(live_row, own_x, own_y))
    to_x = joined(after(own_y, hidden_got, live_got)[:, OWN_CUT:], *first_line[1:])
    to_y = joined(own_x[:, :OWN_CUT], *first_line[1:])
    first_x, first_y = sent_both(to_x, to_y)
    second_line = line_parts(after(second_piece, to_x, to_y))

    def halves(group, from_x, from_y):
        width, cut = WIDTHS[group], LINE_CUTS[group]
        if group == 0:
            base_x, base_y = sum(WIDTHS) - OWN_CUT, OWN_CUT
        else:
            before, before_cut = WIDTHS[group - 1], LINE_CUTS[group - 1]
            base_x, base_y = 2 * before - before_cut, before + before_cut
        return (
            from_y[:, base_y + width + cut : base_y + 3 * width],
            from_x[:, base_x : base_x + width + cut],
        )

    high, low = halves(0, first_x, first_y)
    to_x, to_y = joined(high, *second_line[1:]), joined(low, *second_line[1:])
    second_x, second_y = sent_both(to_x, to_y)
    third_line = line_parts(after(third_piece, to_x, to_y))
    high, low = halves(1, second_x, second_y)
    to_x, to_y = joined(high, *third_line[1:]), joined(low, *third_line[1:])
    third_x, third_y = sent_both(to_x, to_y)
    own_parts = (own_x, own_y, first_x, first_y)
    cls_line = (quarters[0],) + tuple(
        along_line(after(quarters[apart], to_x, to_y), apart)
        for apart in range(1, LINE)
    )

    qkv_weight, out_low, out_high, qkv, mixed, vectors, count, hidden_ordered = run_kernel(
        qkv_kernel,
        "seg_qkv",
        [
            shape_of((GROUP, own_rows, 3 * HALF), LOW),
            shape_of((GROUP // 2, own_rows, HALF), LOW),
            shape_of((GROUP // 2, own_rows, HALF), LOW),
            shape_of((both_rows, 3 * HALF), LOW),
            shape_of((both_rows, HALF), LOW),
            shape_of((2 * (8 * MODEL + FF) // MODEL, MODEL)),
            shape_of((8, LANES)),
            shape_of((both_rows, PLANE * SPAN), LOW),
        ],
        where,
        (),
        first_line
        + own_parts
        + (first_x, first_y, second_x, second_y)
        + (hidden_in, hidden_got, live_row, live_got, order),
        [
            pltpu.VMEM((GROUP, own_rows, LANES), LOW),
            pltpu.VMEM((2, 8 * MODEL + FF), WIDE),
            pltpu.VMEM((both_rows, MODEL), LOW),
            pltpu.VMEM((GROUP, own_rows, HALF), LOW),
        ],
        flops=2 * SEG * MODEL * 3 * MODEL,
    )
    out_weight, mixed_ordered, normed_first, inv_first, first_low = run_kernel(
        out_kernel,
        "seg_out",
        [
            shape_of((MODEL, MODEL), LOW),
            shape_of((both_rows, PLANE * SPAN), LOW),
            shape_of((SEG, MODEL)),
            shape_of((SEG, 1)),
            shape_of((SEG, MODEL), LOW),
        ],
        where,
        (),
        (
            hidden_in,
            mixed,
            after(other_core(mixed), third_x, third_y),
            out_low,
            out_high,
            other_core(out_low),
            other_core(out_high),
            vectors,
            order,
        ),
        [pltpu.VMEM((both_rows, MODEL), LOW)],
        flops=2 * SEG * MODEL * MODEL,
    )
    fourth_x, fourth_y = sent_both(*halves(2, third_x, third_y))
    first_got = after(other_core(first_low), fourth_x, fourth_y)
    count = count + other_core(after(count, first_got))
    up_weight, act, slope = run_kernel(
        up_kernel,
        "seg_up",
        [
            shape_of((GROUP, own_rows, FF_HALF), LOW),
            shape_of((both_rows, FF_HALF), LOW),
            shape_of((both_rows, FF_HALF)),
        ],
        where,
        (),
        second_line
        + own_parts
        + (second_x, second_y, third_x, third_y)
        + (first_low, first_got, vectors),
        [pltpu.VMEM((both_rows, MODEL), LOW)],
        flops=2 * SEG * MODEL * FF,
    )
    cls_sent = joined(*cls_line, cls_out_piece)
    cls_sent = after(cls_sent, act)
    cls_x, cls_y = sent_both(cls_sent, cls_sent)
    down_weight, down_own, down_send = run_kernel(
        down_kernel,
        "seg_down",
        [
            shape_of((GROUP, own_rows, FF_HALF), LOW),
            shape_of((SEG, MODEL)),
            shape_of((SEG, MODEL)),
        ],
        where,
        (),
        third_line + own_parts + (third_x, third_y, fourth_x, fourth_y) + (act,),
        flops=2 * SEG * MODEL * FF,
    )
    normed_second, inv_second, diff, out_rows, head_row = run_kernel(
        seg_rows_kernel,
        "seg_rows",
        [
            shape_of((SEG, MODEL)),
            shape_of((SEG, 1)),
            shape_of((SEG, MODEL)),
            shape_of((SEG, MODEL)),
            shape_of((1, 2 * MODEL + LANES)),
        ],
        where,
        (),
        (
            down_own,
            other_core(down_send),
            normed_first,
            vectors,
            targets,
            live_row,
            seg_pos,
        ),
    )
    head_planes = plane_parts(head_row)
    head_lines = line_parts(jnp.concatenate(head_planes))
    size = LINE // 2 * QUARTER_HALF
    cls_far = sent_both(
        after(cls_y[:, size:], *head_planes[1:]), after(cls_x[:, :size], *head_planes[1:])
    )

    second_grad, second_low, second_sums = run_kernel(
        second_norm_kernel,
        "seg_second_norm",
        [shape_of((SEG, MODEL)), shape_of((SEG, MODEL), LOW), shape_of((3, MODEL))],
        where,
        (),
        (diff, count, normed_second, inv_second, vectors),
    )
    second_got = other_core(second_low)
    pre, first_grad_own, first_grad_send, up_sums = run_kernel(
        mlp_back_kernel,
        "seg_mlp_back",
        [
            shape_of((both_rows, FF_HALF), LOW),
            shape_of((SEG, MODEL)),
            shape_of((SEG, MODEL)),
            shape_of((FF_HALF // MODEL, MODEL)),
        ],
        where,
        (),
        (second_low, second_got, down_weight, up_weight, slope),
        [pltpu.VMEM((both_rows, MODEL), LOW)],
        flops=4 * SEG * MODEL * FF,
    )
    first_grad_got = other_core(first_grad_send)

    def part_shapes(columns):
        return [
            shape_of((count_of, own_rows, columns), LOW)
            for count_of in (LINE // 2, LINE // 2, LINE, LINE, LINE)
        ]

    head_lines = head_lines[:1] + together(*(after(got, pre) for got in head_lines[1:]))
    cls_far = together(*(after(got, *head_lines[1:]) for got in cls_far))
    cls_half, cls_out_half = run_kernel(
        cls_gather_kernel,
        "head_gather",
        [
            shape_of((GROUP, own_rows, QUARTER_HALF), LOW),
            shape_of((PLANE, own_rows, HALF), LOW),
        ],
        where,
        (),
        cls_line + (cls_x, cls_y) + cls_far + (cls_out_piece,),
    )
    mlp_parts = run_kernel(
        mlp_weight_kernel,
        "seg_mlp_weight",
        part_shapes(FF),
        where,
        (),
        (first_low, first_got, second_low, second_got, after(pre, cls_half), act),
        [
            pltpu.VMEM((both_rows, MODEL), LOW),
            pltpu.VMEM((GROUP, own_rows, FF), LOW),
            pltpu.SemaphoreType.DMA((GROUP,)),
        ],
        far=range(5),
        flops=4 * SEG * MODEL * FF,
    )
    mlp_far = reduce_far(tuple(after(part, *cls_far) for part in mlp_parts[:2]))
    cls_weight, cls_out = run_kernel(
        cls_weight_kernel,
        "head_weight",
        [
            shape_of((GROUP, own_rows, QUARTER), LOW),
            shape_of((4, HEAD_DIM, MODEL), LOW),
        ],
        where,
        (),
        (cls_half, other_core(cls_half), cls_out_half, other_core(cls_out_half)),
    )
    cls_weight = cls_weight.reshape(MODEL, QUARTER)
    cls_out = cls_out.reshape(SPAN, MODEL)
    heads, cls_qkv, cls_mixed, part = run_kernel(
        cls_attend_kernel,
        "head_attend",
        [
            shape_of((GROUP, 2 * MODEL + LANES)),
            shape_of((GROUP, 3 * SPAN), LOW),
            shape_of((GROUP, SPAN), LOW),
            shape_of((GROUP, MODEL)),
        ],
        where,
        (),
        tuple(after(got, mlp_parts[0], first_grad_got) for got in head_lines)
        + (vectors, cls_weight, cls_out),
    )
    cls_normed, cls_inv, cls_low, cls_act, cls_slope, part, *mlp_sent = run_kernel(
        head_mlp_kernel,
        "head_mlp",
        [
            shape_of((GROUP, MODEL)),
            shape_of((GROUP, 1)),
            shape_of((GROUP, MODEL), LOW),
            shape_of((GROUP, FF // LINE), LOW),
            shape_of((GROUP, FF // LINE)),
            shape_of((GROUP, MODEL)),
            shape_of(mlp_parts[2].shape, LOW),
            shape_of(mlp_parts[2].shape, LOW),
        ],
        where,
        (),
        (heads,) + line_parts(part) + (vectors, cls_weight) + mlp_far + tuple(mlp_parts[2:4]),
    )
    mlp_plane = sent_both(*mlp_sent)
    cls_parts = line_parts(part)
    top_row, square, cls_grad, cls_second, cls_pre, part, top_sums = run_kernel(
        cls_top_kernel,
        "head_top",
        [
            shape_of((1, MODEL)),
            shape_of((8, LANES)),
            shape_of((GROUP, MODEL)),
            shape_of((GROUP, MODEL), LOW),
            shape_of((GROUP, FF // LINE), LOW),
            shape_of((GROUP, MODEL)),
            shape_of((2, MODEL)),
        ],
        where,
        (),
        (heads,)
        + cls_parts
        + (vectors, cls_weight, cls_normed, count, cls_slope),
        [pltpu.VMEM((GROUP, MODEL), WIDE)],
    )
    top_parts = line_parts(part)
    cls_grad, cls_branch, cls_proj, part, back_sums = run_kernel(
        cls_attend_back_kernel,
        "head_attend_back",
        [
            shape_of((GROUP, MODEL)),
            shape_of((GROUP, MODEL), LOW),
            shape_of((GROUP, 3 * SPAN), LOW),
            shape_of((GROUP, MODEL)),
            shape_of((2, MODEL)),
        ],
        where,
        (),
        (heads,)
        + top_parts
        + (vectors, cls_weight, cls_out, cls_grad, cls_normed, cls_inv, cls_qkv),
    )
    end_parts = line_parts(part)
    pack = jnp.concatenate([cls_proj, cls_mixed, cls_pre, cls_act], axis=1)
    folded = [shape_of((own_rows, FF))] + [shape_of((own_rows + GROUP, FF), LOW)] * (LINE - 1)
    dheads, head_grad, shared, mlp_own, *mlp_sent = run_kernel(
        head_end_kernel,
        "head_end",
        [shape_of((1, MODEL)), shape_of((1, MODEL)), shape_of((GROUP + 8, MODEL))] + folded,
        where,
        (),
        (heads, cls_grad)
        + end_parts
        + (square, back_sums, top_sums, normed_second, inv_second, vectors)
        + (mlp_parts[4],)
        + mlp_plane
        + (pack,),
        [pltpu.VMEM((GROUP, MODEL), WIDE)],
    )
    got_three, got_two = along_line(mlp_sent[2], 3), along_line(mlp_sent[1], 2)
    mlp_last = mlp_sent[0]
    mlp_got = [None, got_two, got_three]

    head_own, head_send, head_data = run_kernel(
        head_back_kernel,
        "seg_head_back",
        [shape_of((1, MODEL)), shape_of((1, MODEL)), shape_of((12, MODEL))],
        where,
        (),
        (
            head_grad,
            other_core(head_grad),
            down_weight,
            up_weight,
            slope,
            act,
            first_low,
            first_got,
        ),
    )
    grad_summed, branch, mixed_grad, attn_send, first_sums = run_kernel(
        first_norm_kernel,
        "seg_first_norm",
        [
            shape_of((SEG, MODEL)),
            shape_of((SEG, MODEL), LOW),
            shape_of((SEG, MODEL), LOW),
            shape_of((SEG, MODEL), LOW),
            shape_of((3, MODEL)),
        ],
        where,
        (),
        (
            second_grad,
            first_grad_own,
            first_grad_got,
            head_grad,
            head_own,
            other_core(head_send),
            normed_first,
            inv_first,
            vectors,
            out_weight,
        ),
    )
    attn_got = other_core(attn_send)
    proj, input_own, input_send, payload = run_kernel(
        attn_back_kernel,
        "seg_attn_back",
        [
            shape_of((both_rows, 3 * HALF), LOW),
            shape_of((SEG, MODEL)),
            shape_of((SEG, MODEL)),
            shape_of((24, MODEL), LOW),
        ],
        where,
        (),
        (
            qkv,
            mixed_grad,
            attn_got,
            live_row,
            live_got,
            qkv_weight,
            first_sums,
            second_sums,
            up_sums,
            dheads,
            normed_second,
            head_data,
        ),
        [pltpu.VMEM((24, MODEL), WIDE)],
        flops=4 * SEG * MODEL * 3 * MODEL,
    )
    attn_data = (hidden_ordered, mixed_ordered, proj, branch, attn_got)
    attn_far = run_kernel(
        attn_far_kernel,
        "seg_attn_far",
        part_shapes(4 * HALF)[:2],
        where,
        (),
        attn_data,
        flops=SEG * MODEL * 2 * MODEL,
    )
    attn_far = reduce_far(tuple(after(part, mlp_got[-1]) for part in attn_far))
    attn_near = run_kernel(
        attn_near_kernel,
        "seg_attn_near",
        part_shapes(4 * HALF)[2:] + [shape_of((SEG, MODEL), LOW)],
        where,
        (),
        attn_data + (top_row, out_rows, live_row),
        flops=3 * SEG * MODEL * 2 * MODEL,
    )
    output = attn_near[3]
    *attn_sent, input_grad = run_kernel(
        attn_add_kernel,
        "seg_attn_add",
        [shape_of(attn_near[0].shape, LOW)] * 2 + [shape_of((SEG, MODEL), LOW)],
        where,
        (),
        attn_far
        + tuple(attn_near[:2])
        + (after(grad_summed, got_two), input_own, other_core(input_send)),
    )
    attn_plane = sent_both(*attn_sent)
    payload_parts = line_parts(after(payload, *attn_sent))
    mlp_got[0] = along_line(after(mlp_last, *payload_parts[1:]), 1)
    mlp_got = [after(got, attn_plane[0]) for got in mlp_got]
    mlp_sum = reduce_line(mlp_own, mlp_got)
    shared = shared + other_core(after(shared, attn_sent[0]))
    row_width = 8 * MODEL + 2 * FF
    cls_rows = run_kernel(
        cls_rows_kernel,
        "head_rows",
        [shape_of((GROUP, row_width), LOW)],
        where,
        (),
        (pack,) + tuple(mlp_got) + (heads, cls_branch, cls_low, cls_second),
        [pltpu.VMEM((LINE,) + pack.shape, LOW)],
    )[0]
    cls_got = other_core(cls_rows)
    attn_plane = tuple(after(got, output, input_grad, shared) for got in attn_plane)
    attn_own, *attn_sent = reduce_fold(where, attn_near[2], attn_plane)
    attn_lines = list(
        together(*(along_line(attn_sent[apart - 1], apart) for apart in range(1, LINE)))
    )
    flat = pltpu.VMEM((1, 8 * MODEL + FF), WIDE)
    payload_line = jnp.concatenate(payload_parts)
    mlp_mine, own_vecs, cls_mats_grad, cls_vec_grad, pos_total, loss_value = run_kernel(
        share_owner_kernel,
        "head_owner",
        [
            shape_of((own_rows, FF)),
            shape_of((16, MODEL)),
            shape_of((own_rows, total_columns)),
            shape_of((vec_size,)),
            shape_of((GROUP, MODEL)),
            shape_of((1, 1)),
        ],
        where,
        (),
        tuple(after(got, attn_own) for got in plane_parts(after(payload_line, *attn_plane)))
        + (mlp_sum, cls_rows, cls_got, shared, count),
        [
            pltpu.VMEM((GROUP * 24, MODEL), LOW),
            pltpu.VMEM((CORES * GROUP, row_width), LOW),
            flat,
        ],
        flops=64 * own_rows * total_columns,
    )
    loss_value = loss_value.reshape(())
    attn_lines = together(*(after(got, mlp_mine) for got in attn_lines))
    attn_sum = reduce_line(attn_own, attn_lines)
    seg_mats_grad, seg_vec_grad = run_kernel(
        store_kernel,
        "seg_owner",
        [shape_of((own_rows, total_columns)), shape_of((vec_size,))],
        where,
        (),
        (attn_sum, other_core(attn_sum), mlp_mine, other_core(mlp_mine))
        + (own_vecs, other_core(own_vecs)),
        [flat, pltpu.SemaphoreType.DMA((12,))],
        far=(0,),
    )

    return (
        output,
        input_grad,
        seg_mats_grad,
        seg_vec_grad,
        cls_mats_grad,
        cls_vec_grad,
        pos_total,
        loss_value,
    )


def solution(mesh):
    in_specs = (
        P(("rep", "fsdp"), None),
        P(("rep", "fsdp"), None),
        P(("rep", "fsdp")),
        P(("rep", "fsdp")),
        P(("rep", "fsdp")),
        P("fsdp", None),
        P("fsdp"),
        P("fsdp", None),
        P("fsdp"),
        P(),
    )
    out_specs = (
        P(("rep", "fsdp"), None),
        P(("rep", "fsdp"), None),
        P("fsdp", None),
        P("fsdp"),
        P("fsdp", None),
        P("fsdp"),
        P(),
        P(),
    )
    one_slice = dict(mesh.shape) == {"rep": CORES, "fsdp": LINE * PLANE}
    body = slice_local if one_slice else local
    return jax.shard_map(body, mesh=mesh, in_specs=in_specs, out_specs=out_specs, check_vma=False)
```

```python
import math

import jax
import jax.numpy as jnp
from jax import lax
from jax.experimental import pallas as pl
from jax.experimental.pallas import tpu as pltpu
from jax.sharding import PartitionSpec as P

HEADS = 12
HEAD_DIM = 64
FF = 3072
SEG = 128
SEQ = 2048


NORM_EPS = 1e-05
MASK_FILL = -1e30
SQRT_HALF = 0.7071067811865476
INV_SQRT_TWO_PI = 0.3989422804014327


def swapped(value, axis, apart):
    mask = 2**apart
    pairs = [(source, source ^ mask) for source in range(lax.axis_size(axis))]
    return lax.ppermute(value, axis, pairs)


def product_plain(left_side, right_side):
    return jnp.dot(left_side, right_side, preferred_element_type=jnp.float32)


def product_left(left_side, right_side):
    return lax.dot_general(
        left_side, right_side, (((0,), (0,)), ((), ())), preferred_element_type=jnp.float32
    )


def product_right(left_side, right_side):
    return lax.dot_general(
        left_side, right_side, (((1,), (1,)), ((), ())), preferred_element_type=jnp.float32
    )


def row_total(array_in):
    return jnp.sum(array_in.astype(jnp.float32), axis=0)


def unpack_weights(gathered, model_width, ff_width):
    matrix, vector = gathered
    vector = vector.astype(jnp.float32)
    pieces = tuple(
        (vector[offset * model_width : (offset + 1) * model_width] for offset in range(8))
    )
    return (
        (
            matrix[:, : 3 * model_width],
            matrix[:, 3 * model_width : 4 * model_width],
            matrix[:, 4 * model_width : 4 * model_width + ff_width],
            matrix[:, 4 * model_width + ff_width :],
        )
        + pieces
        + (vector[8 * model_width :],)
    )


def norm_forward(summed, gain_vec, shift_vec):
    row_mean = jnp.mean(summed, axis=-1, keepdims=True)
    centered = summed - row_mean
    inv_dev = lax.rsqrt(jnp.mean(centered * centered, axis=-1, keepdims=True) + NORM_EPS)
    normed = centered * inv_dev
    return (normed * gain_vec + shift_vec, normed, inv_dev)


def norm_backward(grad_out, normed, inv_dev, gain_vec):
    scaled = grad_out * gain_vec
    mean_one = jnp.mean(scaled, axis=-1, keepdims=True)
    mean_two = jnp.mean(scaled * normed, axis=-1, keepdims=True)
    grad_in = inv_dev * (scaled - mean_one - normed * mean_two)
    return (grad_in, jnp.sum(grad_out * normed, axis=0), jnp.sum(grad_out, axis=0))


def gelu_value(before):
    return 0.5 * before * (1.0 + lax.erf(before * SQRT_HALF))


def gelu_slope(before):
    return (
        0.5 * (1.0 + lax.erf(before * SQRT_HALF))
        + before * jnp.exp(-0.5 * before * before) * INV_SQRT_TWO_PI
    )


def attention_scores(queries, keys_in, allowed, score_scale):
    raw_scores = (
        jnp.einsum("bqhe,bkhe->bhqk", queries, keys_in, preferred_element_type=jnp.float32)
        * score_scale
    )
    return jnp.where(allowed, raw_scores, MASK_FILL)


def attention_forward(queries, keys_in, values, allowed, score_scale):
    scores = attention_scores(queries, keys_in, allowed, score_scale)
    row_top = jnp.max(scores, axis=-1, keepdims=True)
    log_total = row_top + jnp.log(jnp.sum(jnp.exp(scores - row_top), axis=-1, keepdims=True))
    weights = jnp.exp(scores - log_total).astype(jnp.bfloat16)
    mixed_rows = jnp.einsum("bhqk,bkhe->bqhe", weights, values, preferred_element_type=jnp.float32)
    return (mixed_rows, log_total)


def attention_backward(queries, keys_in, values, allowed, score_scale, log_total, grad_mixed):
    probabilities = jnp.exp(attention_scores(queries, keys_in, allowed, score_scale) - log_total)
    grad_probs = jnp.einsum(
        "bqhe,bkhe->bhqk", grad_mixed, values, preferred_element_type=jnp.float32
    )
    inner_sum = jnp.sum(grad_probs * probabilities, axis=-1, keepdims=True)
    grad_scores = (probabilities * (grad_probs - inner_sum)).astype(jnp.bfloat16)
    grad_query = (
        jnp.einsum("bhqk,bkhe->bqhe", grad_scores, keys_in, preferred_element_type=jnp.float32)
        * score_scale
    )
    grad_key = (
        jnp.einsum("bhqk,bqhe->bkhe", grad_scores, queries, preferred_element_type=jnp.float32)
        * score_scale
    )
    grad_value = jnp.einsum(
        "bhqk,bqhe->bkhe",
        probabilities.astype(jnp.bfloat16),
        grad_mixed,
        preferred_element_type=jnp.float32,
    )
    return (grad_query, grad_key, grad_value)


def block_forward(rows_in, unpacked, attend):
    (
        qkv_weight,
        out_weight,
        up_weight,
        down_weight,
        query_bias,
        value_bias,
        out_bias,
        down_bias,
        gain_first,
        shift_first,
        gain_second,
        shift_second,
        up_bias,
    ) = unpacked
    model_width = rows_in.shape[1]
    inputs = rows_in.astype(jnp.bfloat16)
    projected = product_plain(inputs, qkv_weight)
    queries = (projected[:, :model_width] + query_bias).astype(jnp.bfloat16)
    keys_in = projected[:, model_width : 2 * model_width].astype(jnp.bfloat16)
    values = (projected[:, 2 * model_width :] + value_bias).astype(jnp.bfloat16)
    mixed_rows, attend_kept = attend(queries, keys_in, values)
    mixed_rows = mixed_rows.astype(jnp.bfloat16)
    summed_first = rows_in + product_plain(mixed_rows, out_weight) + out_bias
    first_out, normed_first, inv_first = norm_forward(summed_first, gain_first, shift_first)
    first_low = first_out.astype(jnp.bfloat16)
    pre_act = product_plain(first_low, up_weight) + up_bias
    activated = gelu_value(pre_act).astype(jnp.bfloat16)
    summed_second = first_out + product_right(activated, down_weight) + down_bias
    block_out, normed_second, inv_second = norm_forward(summed_second, gain_second, shift_second)
    saved_state = (
        inputs,
        queries,
        keys_in,
        values,
        attend_kept,
        mixed_rows,
        normed_first,
        inv_first,
        first_low,
        pre_act,
        activated,
        normed_second,
        inv_second,
    )
    return (block_out, saved_state)


def block_backward(grad_out, unpacked, saved_state, attend_back):
    (
        qkv_weight,
        out_weight,
        up_weight,
        down_weight,
        query_bias,
        value_bias,
        out_bias,
        down_bias,
        gain_first,
        shift_first,
        gain_second,
        shift_second,
        up_bias,
    ) = unpacked
    (
        inputs,
        queries,
        keys_in,
        values,
        attend_kept,
        mixed_rows,
        normed_first,
        inv_first,
        first_low,
        pre_act,
        activated,
        normed_second,
        inv_second,
    ) = saved_state
    grad_second, grad_gain_second, grad_shift_second = norm_backward(
        grad_out, normed_second, inv_second, gain_second
    )
    second_low = grad_second.astype(jnp.bfloat16)
    grad_pre = (product_plain(second_low, down_weight) * gelu_slope(pre_act)).astype(jnp.bfloat16)
    grad_first = grad_second + product_right(grad_pre, up_weight)
    grad_summed, grad_gain_first, grad_shift_first = norm_backward(
        grad_first, normed_first, inv_first, gain_first
    )
    branch_low = grad_summed.astype(jnp.bfloat16)
    grad_mixed = product_right(branch_low, out_weight).astype(jnp.bfloat16)
    grad_query, grad_key, grad_value = attend_back(
        queries, keys_in, values, attend_kept, grad_mixed
    )
    grad_proj = jnp.concatenate([grad_query, grad_key, grad_value], axis=1)
    grad_rows = grad_summed + product_right(grad_proj, qkv_weight)
    vector_grad = jnp.concatenate(
        [
            row_total(grad_query),
            row_total(grad_value),
            row_total(branch_low),
            row_total(second_low),
            grad_gain_first,
            grad_shift_first,
            grad_gain_second,
            grad_shift_second,
            row_total(grad_pre),
        ]
    )
    weight_rows = (
        inputs,
        grad_proj,
        mixed_rows,
        branch_low,
        first_low,
        grad_pre,
        second_low,
        activated,
    )
    return (grad_rows, weight_rows, vector_grad)


def weight_products(weight_rows):
    inputs, grad_proj, mixed_rows, branch_low, first_low, grad_pre, second_low, activated = (
        weight_rows
    )
    return (
        product_left(inputs, grad_proj),
        product_left(mixed_rows, branch_low),
        product_left(first_low, grad_pre),
        product_left(second_low, activated),
    )


def local(
    hidden_in,
    targets,
    doc_ids,
    seg_nums,
    valid_flags,
    seg_mats,
    seg_vecs,
    cls_mats,
    cls_vecs,
    seg_pos,
):
    tok_rows, model_width = hidden_in.shape
    ff_width = FF
    seg_len = SEG
    group_span = SEQ // tok_rows
    seg_count = tok_rows // seg_len
    score_scale = HEAD_DIM ** (-0.5)
    head_shape = (HEADS, HEAD_DIM)
    live_rows = valid_flags.astype(jnp.float32)
    rank_full = lax.axis_index("fsdp")
    seg_gathered = (
        lax.all_gather(seg_mats, "fsdp", axis=0, tiled=True),
        lax.all_gather(seg_vecs, "fsdp", axis=0, tiled=True),
    )
    seg_unpacked = unpack_weights(seg_gathered, model_width, ff_width)
    cls_gathered = (
        lax.all_gather(cls_mats, "fsdp", axis=0, tiled=True),
        lax.all_gather(cls_vecs, "fsdp", axis=0, tiled=True),
    )
    cls_unpacked = unpack_weights(cls_gathered, model_width, ff_width)
    seg_allowed = (live_rows.reshape(seg_count, 1, 1, seg_len) > 0.5) | jnp.eye(seg_len, dtype=bool)
    seg_shape = (seg_count, seg_len) + head_shape

    def seg_attend(queries, keys_in, values):
        mixed_rows, log_total = attention_forward(
            queries.reshape(seg_shape),
            keys_in.reshape(seg_shape),
            values.reshape(seg_shape),
            seg_allowed,
            score_scale,
        )
        return (mixed_rows.reshape(tok_rows, model_width), log_total)

    def seg_attend_back(queries, keys_in, values, log_total, grad_mixed):
        grad_parts = attention_backward(
            queries.reshape(seg_shape),
            keys_in.reshape(seg_shape),
            values.reshape(seg_shape),
            seg_allowed,
            score_scale,
            log_total,
            grad_mixed.reshape(seg_shape),
        )
        return tuple(
            (
                grad_part.reshape(tok_rows, model_width).astype(jnp.bfloat16)
                for grad_part in grad_parts
            )
        )

    first_out, seg_saved = block_forward(hidden_in.astype(jnp.float32), seg_unpacked, seg_attend)
    first_grid = first_out.reshape(seg_count, seg_len, model_width)
    position_hot = (seg_nums[:, None] == jnp.arange(seg_pos.shape[0])[None, :]).astype(jnp.float32)
    position_rows = jnp.sum(
        position_hot[:, :, None] * seg_pos.astype(jnp.float32)[None, :, :], axis=1
    )
    heads_in = first_grid[:, 0, :] + position_rows
    lead_live = live_rows.reshape(seg_count, seg_len)[:, 0]
    lead_doc = doc_ids.reshape(seg_count, seg_len)[:, 0]
    lead_labels = jnp.where(lead_live > 0.5, lead_doc, -1).astype(jnp.bfloat16)
    lead_doc_low = lead_doc.astype(jnp.bfloat16)
    bit_count = group_span.bit_length() - 1
    key_total = group_span * seg_count
    own_slot = rank_full % group_span * seg_count + jnp.arange(seg_count)
    query_shape = (1, seg_count) + head_shape
    key_shape = (1, key_total) + head_shape

    def cls_attend(queries, keys_in, values):
        paired = jnp.concatenate([keys_in, values], axis=1)
        labels = lead_labels
        for bit_level in range(bit_count):
            other_pair, other_labels = swapped((paired, labels), "fsdp", bit_level)
            upper_half = rank_full // (1 << bit_level) % 2 == 1
            paired = jnp.where(
                upper_half,
                jnp.concatenate([other_pair, paired]),
                jnp.concatenate([paired, other_pair]),
            )
            labels = jnp.where(
                upper_half,
                jnp.concatenate([other_labels, labels]),
                jnp.concatenate([labels, other_labels]),
            )
        allowed = (labels[None, :] == lead_doc_low[:, None]) | (
            jnp.arange(key_total)[None, :] == own_slot[:, None]
        )
        allowed = allowed[None, None]
        mixed_rows, log_total = attention_forward(
            queries.reshape(query_shape),
            paired[:, :model_width].reshape(key_shape),
            paired[:, model_width:].reshape(key_shape),
            allowed,
            score_scale,
        )
        return (mixed_rows.reshape(seg_count, model_width), (paired, allowed, log_total))

    def cls_attend_back(queries, keys_in, values, attend_kept, grad_mixed):
        paired, allowed, log_total = attend_kept
        grad_query, grad_key, grad_value = attention_backward(
            queries.reshape(query_shape),
            paired[:, :model_width].reshape(key_shape),
            paired[:, model_width:].reshape(key_shape),
            allowed,
            score_scale,
            log_total,
            grad_mixed.reshape(query_shape),
        )
        grad_pair = jnp.concatenate(
            [grad_key.reshape(key_total, model_width), grad_value.reshape(key_total, model_width)],
            axis=1,
        )
        for bit_level in reversed(range(bit_count)):
            half_rows = grad_pair.shape[0] // 2
            upper_half = rank_full // (1 << bit_level) % 2 == 1
            kept_half = jnp.where(upper_half, grad_pair[half_rows:], grad_pair[:half_rows])
            sent_half = jnp.where(upper_half, grad_pair[:half_rows], grad_pair[half_rows:])
            grad_pair = kept_half + swapped(
                sent_half.astype(jnp.bfloat16), "fsdp", bit_level
            ).astype(sent_half.dtype)
        grad_pair = grad_pair.astype(jnp.bfloat16)
        return (
            grad_query.reshape(seg_count, model_width).astype(jnp.bfloat16),
            grad_pair[:, :model_width],
            grad_pair[:, model_width:],
        )

    top_out, cls_saved = block_forward(heads_in, cls_unpacked, cls_attend)
    combined = jnp.concatenate([top_out[:, None, :], first_grid[:, 1:, :]], axis=1).reshape(
        tok_rows, model_width
    )
    output_rows = combined * live_rows[:, None]
    diff_rows = (output_rows - targets.astype(jnp.float32)) * live_rows[:, None]
    count_all, square_all = lax.psum(
        (jnp.sum(live_rows), jnp.sum(diff_rows * diff_rows)), ("rep", "fsdp")
    )
    loss_value = square_all / (count_all * model_width)
    slots_all = tok_rows * lax.axis_size("rep") * lax.axis_size("fsdp")
    grad_grid = (diff_rows * (slots_all / count_all)).reshape(seg_count, seg_len, model_width)
    cls_back = unpack_weights(
        (
            lax.all_gather(cls_mats, "fsdp", axis=0, tiled=True),
            lax.all_gather(cls_vecs, "fsdp", axis=0, tiled=True),
        ),
        model_width,
        ff_width,
    )
    heads_grad, cls_weight_rows, cls_g_vec = block_backward(
        grad_grid[:, 0, :], cls_back, cls_saved, cls_attend_back
    )
    cls_g_qkv, cls_g_out, cls_g_up, cls_g_down = weight_products(cls_weight_rows)
    pos_local = jnp.sum(position_hot[:, :, None] * heads_grad[:, None, :], axis=0)
    seg_grad_out = jnp.concatenate([heads_grad[:, None, :], grad_grid[:, 1:, :]], axis=1).reshape(
        tok_rows, model_width
    )
    seg_back = unpack_weights(
        (
            lax.all_gather(seg_mats, "fsdp", axis=0, tiled=True),
            lax.all_gather(seg_vecs, "fsdp", axis=0, tiled=True),
        ),
        model_width,
        ff_width,
    )
    input_grad, seg_weight_rows, seg_g_vec = block_backward(
        seg_grad_out, seg_back, seg_saved, seg_attend_back
    )
    seg_g_qkv, seg_g_out, seg_g_up, seg_g_down = weight_products(seg_weight_rows)
    owner_rows = tuple(
        (
            lax.psum_scatter(seg_g_qkv, "fsdp", scatter_dimension=0, tiled=True),
            lax.psum_scatter(seg_g_out, "fsdp", scatter_dimension=0, tiled=True),
            lax.psum_scatter(seg_g_up, "fsdp", scatter_dimension=0, tiled=True),
            lax.psum_scatter(seg_g_down, "fsdp", scatter_dimension=0, tiled=True),
            lax.psum_scatter(seg_g_vec, "fsdp", scatter_dimension=0, tiled=True),
            lax.psum_scatter(cls_g_qkv, "fsdp", scatter_dimension=0, tiled=True),
            lax.psum_scatter(cls_g_out, "fsdp", scatter_dimension=0, tiled=True),
            lax.psum_scatter(cls_g_up, "fsdp", scatter_dimension=0, tiled=True),
            lax.psum_scatter(cls_g_down, "fsdp", scatter_dimension=0, tiled=True),
            lax.psum_scatter(cls_g_vec, "fsdp", scatter_dimension=0, tiled=True),
        )
    )
    replica_share = (
        lax.psum_scatter(
            owner_rows[0].astype(jnp.bfloat16), "rep", scatter_dimension=1, tiled=True
        ).astype(jnp.float32),
        lax.psum_scatter(
            owner_rows[1].astype(jnp.bfloat16), "rep", scatter_dimension=1, tiled=True
        ).astype(jnp.float32),
        lax.psum_scatter(
            owner_rows[2].astype(jnp.bfloat16), "rep", scatter_dimension=1, tiled=True
        ).astype(jnp.float32),
        lax.psum_scatter(
            owner_rows[3].astype(jnp.bfloat16), "rep", scatter_dimension=1, tiled=True
        ).astype(jnp.float32),
        lax.psum_scatter(
            owner_rows[4].astype(jnp.bfloat16), "rep", scatter_dimension=0, tiled=True
        ).astype(jnp.float32),
        lax.psum_scatter(
            owner_rows[5].astype(jnp.bfloat16), "rep", scatter_dimension=1, tiled=True
        ).astype(jnp.float32),
        lax.psum_scatter(
            owner_rows[6].astype(jnp.bfloat16), "rep", scatter_dimension=1, tiled=True
        ).astype(jnp.float32),
        lax.psum_scatter(
            owner_rows[7].astype(jnp.bfloat16), "rep", scatter_dimension=1, tiled=True
        ).astype(jnp.float32),
        lax.psum_scatter(
            owner_rows[8].astype(jnp.bfloat16), "rep", scatter_dimension=1, tiled=True
        ).astype(jnp.float32),
        lax.psum_scatter(
            owner_rows[9].astype(jnp.bfloat16), "rep", scatter_dimension=0, tiled=True
        ).astype(jnp.float32),
    )
    all_summed = (
        lax.all_gather(replica_share[0].astype(jnp.bfloat16), "rep", axis=1, tiled=True).astype(
            jnp.float32
        ),
        lax.all_gather(replica_share[1].astype(jnp.bfloat16), "rep", axis=1, tiled=True).astype(
            jnp.float32
        ),
        lax.all_gather(replica_share[2].astype(jnp.bfloat16), "rep", axis=1, tiled=True).astype(
            jnp.float32
        ),
        lax.all_gather(replica_share[3].astype(jnp.bfloat16), "rep", axis=1, tiled=True).astype(
            jnp.float32
        ),
        lax.all_gather(replica_share[4].astype(jnp.bfloat16), "rep", axis=0, tiled=True).astype(
            jnp.float32
        ),
        lax.all_gather(replica_share[5].astype(jnp.bfloat16), "rep", axis=1, tiled=True).astype(
            jnp.float32
        ),
        lax.all_gather(replica_share[6].astype(jnp.bfloat16), "rep", axis=1, tiled=True).astype(
            jnp.float32
        ),
        lax.all_gather(replica_share[7].astype(jnp.bfloat16), "rep", axis=1, tiled=True).astype(
            jnp.float32
        ),
        lax.all_gather(replica_share[8].astype(jnp.bfloat16), "rep", axis=1, tiled=True).astype(
            jnp.float32
        ),
        lax.all_gather(replica_share[9].astype(jnp.bfloat16), "rep", axis=0, tiled=True).astype(
            jnp.float32
        ),
    )
    seg_summed = all_summed[:5]
    cls_summed = all_summed[5:]
    pos_total = lax.psum(pos_local, ("rep", "fsdp"))
    seg_mat_grad = jnp.concatenate(
        [seg_summed[0], seg_summed[1], seg_summed[2], seg_summed[3]], axis=1
    )
    cls_mat_grad = jnp.concatenate(
        [cls_summed[0], cls_summed[1], cls_summed[2], cls_summed[3]], axis=1
    )
    return (
        output_rows.astype(jnp.bfloat16),
        input_grad.astype(jnp.bfloat16),
        seg_mat_grad,
        seg_summed[4],
        cls_mat_grad,
        cls_summed[4],
        pos_total,
        loss_value,
    )


LINE = 4
PLANE = 4
CORES = 2
LANES = 128
GROUP = LINE * PLANE
LOW, WIDE = jnp.bfloat16, jnp.float32
MODEL = HEADS * HEAD_DIM
SPAN = 2 * LANES
TILE_START = (0, 1, 3, 4)


def line_pairs(apart):
    return [(source, (source + apart * PLANE) % GROUP) for source in range(GROUP)]


def plane_pairs(mask):
    return [(source, source ^ mask) for source in range(GROUP)]


def along_line(value, apart):
    return lax.ppermute(value, "fsdp", line_pairs(apart))


def in_plane(value, mask):
    return lax.ppermute(value, "fsdp", plane_pairs(mask))


def other_core(value):
    return lax.ppermute(value, "rep", [(0, 1), (1, 0)])


def after(value, *events):
    return lax.optimization_barrier((value,) + events)[0]


def together(*values):
    return tuple(lax.optimization_barrier(values))


def shape_of(dims, dtype=WIDE):
    return jax.ShapeDtypeStruct(dims, dtype)


def run_kernel(body, name, outs, where, blocks, arrays, scratch=(), far=(), flops=0):
    in_specs = [pl.BlockSpec(memory_space=pltpu.SMEM)]
    in_specs += [pl.BlockSpec(memory_space=pltpu.HBM)] * len(blocks)
    in_specs += [pl.BlockSpec(memory_space=pltpu.VMEM)] * len(arrays)
    spaces = [pltpu.HBM if at in far else pltpu.VMEM for at in range(len(outs))]
    moved = sum(x.size * x.dtype.itemsize for x in list(blocks) + list(arrays))
    moved += sum(math.prod(o.shape) * jnp.dtype(o.dtype).itemsize for o in outs)
    return pl.pallas_call(
        body,
        name=name,
        out_shape=tuple(outs),
        in_specs=in_specs,
        out_specs=tuple(pl.BlockSpec(memory_space=space) for space in spaces),
        scratch_shapes=list(scratch),
        cost_estimate=pl.CostEstimate(flops=flops, bytes_accessed=moved, transcendentals=0),
        compiler_params=pltpu.CompilerParams(vmem_limit_bytes=VMEM_BYTES),
    )(where, *blocks, *arrays)


VMEM_BYTES = 24 * 1024 * 1024
HALF = MODEL // CORES
FF_HALF = FF // CORES
OWN = MODEL // GROUP
QUARTER = 3 * SPAN + 2 * FF // LINE
QUARTER_HALF = QUARTER // CORES


def aligned(start):
    return pl.multiple_of(start, LANES)


def wait_all(copies):
    for copy in copies:
        copy.wait()


def run_copies(pairs, sems):
    copies = [
        pltpu.make_async_copy(source, target, sems.at[at])
        for at, (source, target) in enumerate(pairs)
    ]
    for copy in copies:
        copy.start()
    wait_all(copies)


FIRST = 4 * HALF + LANES
OWN_CUT = FIRST + FF_HALF // 2
LINE_CUTS = (7 * LANES, FF_HALF // 2, FF_HALF // 2)
WIDTHS = (FIRST, FF_HALF, FF_HALF)


def group_pieces(group, refs):
    own, rest = refs[:LINE], refs[LINE:]
    own_x, own_y, far_x, far_y, line_x, line_y, late_x, late_y = rest
    width, cut = WIDTHS[group], LINE_CUTS[group]
    start = sum(WIDTHS[:group])
    if group == 0:
        bases = (sum(WIDTHS) - OWN_CUT, OWN_CUT)
    else:
        before, before_cut = WIDTHS[group - 1], LINE_CUTS[group - 1]
        bases = (2 * before - before_cut, before + before_cut)
    pieces = {(0, step): [(own[step], 0, 0, width)] for step in range(LINE)}
    for mask, whole, line, base in ((1, own_x, line_x, bases[0]), (2, own_y, line_y, bases[1])):
        pieces[mask, 0] = [(whole, start, 0, width)]
        for step in range(1, LINE):
            pieces[mask, step] = [(line, base + (step - 1) * width, 0, width)]
    middle = min(max(OWN_CUT - start, 0), width)
    far = []
    if middle > 0:
        far.append((far_y, start, 0, middle))
    if middle < width:
        far.append((far_x, start + middle - OWN_CUT, middle, width))
    pieces[3, 0] = far
    pieces[3, 1] = [(late_y, 0, 0, width)]
    pieces[3, 2] = [(late_y, width, 0, cut), (late_x, 0, cut, width)]
    pieces[3, 3] = [(late_x, width - cut, 0, width)]
    return pieces


def gather_group(where, group, refs, targets):
    line_at, plane_at = where[0], where[1]
    for (mask, step), parts in group_pieces(group, refs).items():
        chip = (line_at + LINE - step) % LINE * PLANE + (plane_at ^ mask)
        for whole, first, last in targets:
            for ref, offset, begin, end in parts:
                low, high = max(first, begin), min(last, end)
                if low < high:
                    source = slice(offset + low - begin, offset + high - begin)
                    whole[chip, :, low - first : high - first] = ref[:, source]


def gather_blocks(where, refs, base, width, targets):
    line_at, plane_at = where[0], where[1]
    half = LINE // 2
    for mask in range(PLANE):
        for step in range(LINE):
            if mask == 0:
                ref, offset = refs[step], 0
            elif mask == 3:
                ref = refs[LINE + 3] if step < half else refs[LINE + 2]
                offset = step % half * width
            else:
                ref, offset = refs[LINE + mask - 1], base + step * width
            chip = (line_at + LINE - step) % LINE * PLANE + (plane_at ^ mask)
            for whole, first, last in targets:
                whole[chip] = ref[:, offset + first : offset + last]


def whole_rows(ref):
    value = ref[...]
    return value.reshape(value.shape[0] * value.shape[1], value.shape[2])


def prepare_first_kernel(where, seg, seg_vec, cls_vec, flags, out, live_out, sems):
    core_at = where[2]
    pairs = []
    for piece in range(4):
        source = seg.at[:, pl.ds(aligned(piece * MODEL + core_at * HALF), HALF)]
        pairs.append((source, out.at[:, piece * HALF : (piece + 1) * HALF]))
    run_copies(pairs, sems)
    size = seg_vec.shape[0]
    vecs = [vec[...].astype(WIDE).reshape(1, size) for vec in (seg_vec, cls_vec)]
    lines = -(-size // LANES)
    block = jnp.zeros((OWN, LANES), WIDE)
    row_at = lax.broadcasted_iota(jnp.int32, (OWN, LANES), 0)
    for which in range(2):
        for line in range(lines):
            width = min(LANES, size - line * LANES)
            value = vecs[which][:, line * LANES : line * LANES + width]
            if width < LANES:
                value = jnp.concatenate([value, jnp.zeros((1, LANES - width), WIDE)], axis=1)
            block = jnp.where(row_at == which * lines + line, value, block)
    live = flags[...].astype(WIDE).reshape(1, SEG)
    live_out[...] = live
    count = jnp.sum(live, axis=1, keepdims=True)
    block = jnp.where(row_at == 2 * lines, count, block)
    out[:, 4 * HALF :] = block.astype(LOW)


def prepare_rest_kernel(where, seg, cls, *refs):
    second_out, third_out = refs[:2]
    step_outs, out_half, order_out = refs[2 : 2 + LINE], refs[2 + LINE], refs[3 + LINE]
    quarters, sems = refs[4 + LINE :]
    line_at, plane_at, core_at = where[0], where[1], where[2]
    start = core_at * FF_HALF
    pairs = [
        (seg.at[:, pl.ds(aligned(4 * MODEL + start), FF_HALF)], second_out),
        (seg.at[:, pl.ds(aligned(4 * MODEL + FF + start), FF_HALF)], third_out),
        (cls.at[:, pl.ds(aligned(3 * MODEL + core_at * HALF), HALF)], out_half),
    ]
    part = FF // LINE
    for at in range(LINE):
        first = TILE_START[at] * LANES
        plan = [(piece * MODEL + first, SPAN, piece * SPAN) for piece in range(3)]
        plan += [
            (4 * MODEL + piece * FF + at * part, part, 3 * SPAN + piece * part)
            for piece in range(2)
        ]
        for source, size, target in plan:
            pairs.append(
                (
                    cls.at[:, source : source + size],
                    quarters.at[at, :, target : target + size],
                )
            )
    run_copies(pairs, sems)
    lanes = pl.ds(aligned(core_at * QUARTER_HALF), QUARTER_HALF)
    for step, out in enumerate(step_outs):
        out[...] = quarters[(line_at + step) % LINE, :, lanes]
    column = lax.broadcasted_iota(jnp.int32, (1, SPAN), 1)
    feature = lax.broadcasted_iota(jnp.int32, (MODEL, SPAN), 0)
    turn = sum((column >= OWN * step).astype(jnp.int32) for step in range(1, LINE))
    held = column - OWN * turn
    turn = (line_at + turn) % LINE
    for mask in range(PLANE):
        source = (turn * PLANE + (plane_at ^ mask)) * OWN + held
        source = jnp.where(column < OWN * LINE, source, -1)
        order_out[:, mask * SPAN : (mask + 1) * SPAN] = (feature == source).astype(LOW)


def prepare_kernel(where, seg, cls, *refs):
    (seg_vec, cls_vec, flags, first_out, live_out), refs = refs[:5], refs[5:]
    rest, (first_sems, quarters, sems) = refs[:-3], refs[-3:]
    prepare_first_kernel(where, seg, seg_vec, cls_vec, flags, first_out, live_out, first_sems)
    prepare_rest_kernel(where, seg, cls, *rest, quarters, sems)


def lane_mask(rows, head):
    lane = lax.broadcasted_iota(jnp.int32, (rows, LANES), 1)
    return (lane < HEAD_DIM) if head == 0 else (lane >= HEAD_DIM)


def masked(value, mask):
    return jnp.where(mask, value, jnp.zeros_like(value))


def head_probabilities(query, key, allowed):
    scores = product_right(query, key) * HEAD_DIM ** (-0.5)
    scores = jnp.where(allowed, scores, MASK_FILL)
    raised = jnp.exp(scores - jnp.max(scores, axis=-1, keepdims=True))
    return raised / jnp.sum(raised, axis=-1, keepdims=True)


def attend_tiles(qkv, width, allowed):
    rows = qkv.shape[0]
    mixed = []
    for tile in range(width // LANES):
        at = tile * LANES
        query, key, value = (
            qkv[:, piece * width + at : piece * width + at + LANES] for piece in range(3)
        )
        total = jnp.zeros((rows, LANES), WIDE)
        for head in range(2):
            mask = lane_mask(rows, head)
            weights = head_probabilities(masked(query, mask), key, allowed).astype(LOW)
            total = total + product_plain(weights, masked(value, mask))
        mixed.append(total.astype(LOW))
    return mixed


def attend_tiles_back(qkv, grad_mixed, width, allowed):
    rows = qkv.shape[0]
    scale = HEAD_DIM ** (-0.5)
    results = ([], [], [])
    for tile in range(width // LANES):
        at = tile * LANES
        query, key, value = (
            qkv[:, piece * width + at : piece * width + at + LANES] for piece in range(3)
        )
        grad = grad_mixed[:, at : at + LANES]
        totals = [jnp.zeros((rows, LANES), WIDE) for _ in range(3)]
        for head in range(2):
            mask = lane_mask(rows, head)
            query_low, key_low, grad_low = (masked(x, mask) for x in (query, key, grad))
            chance = head_probabilities(query_low, key, allowed)
            grad_chance = product_right(grad_low, value)
            inner = jnp.sum(grad_chance * chance, axis=-1, keepdims=True)
            grad_scores = (chance * (grad_chance - inner)).astype(LOW)
            totals[0] = totals[0] + product_plain(grad_scores, key_low)
            totals[1] = totals[1] + product_left(grad_scores, query_low)
            totals[2] = totals[2] + product_left(chance.astype(LOW), grad_low)
        results[0].append((totals[0] * scale).astype(LOW))
        results[1].append((totals[1] * scale).astype(LOW))
        results[2].append(totals[2].astype(LOW))
    return results[0] + results[1] + results[2]


def token_allowed(live_row):
    shape = (SEG, SEG)
    same = lax.broadcasted_iota(jnp.int32, shape, 0) == lax.broadcasted_iota(jnp.int32, shape, 1)
    return (live_row > 0.5) | same


def qkv_kernel(where, *refs):
    blocks = refs[:12]
    hidden, hidden_got, live_row, live_got, order = refs[12:17]
    weight, out_low, out_high, qkv_out, mixed_out = refs[17:22]
    vectors_out, count_out, ordered_out = refs[22:25]
    vec_rows, flat, inputs, out_half = refs[25:]
    core_at = where[2]
    gather_group(
        where,
        0,
        blocks,
        (
            (weight, 0, 3 * HALF),
            (out_half, 3 * HALF, 4 * HALF),
            (vec_rows, 4 * HALF, 4 * HALF + LANES),
        ),
    )
    out_low[...] = out_half[: GROUP // 2]
    out_high[...] = out_half[GROUP // 2 :]
    piece = (8 * MODEL + FF) // GROUP
    lines = -(-piece // LANES)
    count = jnp.zeros((1, LANES), WIDE)
    for chip in range(GROUP):
        rows = vec_rows[chip, 0:16, :].astype(WIDE)
        for block in range(2):
            joined = jnp.concatenate(
                [rows[block * lines + r : block * lines + r + 1] for r in range(lines)], axis=1
            )
            flat[block : block + 1, chip * piece : (chip + 1) * piece] = joined[:, :piece]
        count = count + rows[2 * lines : 2 * lines + 1]
    rows_each = (8 * MODEL + FF) // MODEL
    for block in range(2):
        for row in range(rows_each):
            vectors_out[block * rows_each + row : block * rows_each + row + 1, :] = flat[
                block : block + 1, row * MODEL : (row + 1) * MODEL
            ]
    count_out[...] = jnp.broadcast_to(count, count_out.shape)
    inputs[:SEG] = hidden[...]
    inputs[SEG:] = hidden_got[...]
    projected = product_plain(inputs[...], whole_rows(weight))
    lanes = pl.ds(aligned(core_at * HALF), HALF)
    qkv_out[:, :HALF] = (projected[:, :HALF] + vectors_out[0:1, lanes]).astype(LOW)
    qkv_out[:, HALF : 2 * HALF] = projected[:, HALF : 2 * HALF].astype(LOW)
    qkv_out[:, 2 * HALF :] = (projected[:, 2 * HALF :] + vectors_out[1:2, lanes]).astype(LOW)
    for part, live in enumerate((live_row, live_got)):
        rows = slice(part * SEG, (part + 1) * SEG)
        tiles = attend_tiles(qkv_out[rows, :], HALF, token_allowed(live[...]))
        for tile, value in enumerate(tiles):
            mixed_out[rows, tile * LANES : (tile + 1) * LANES] = value
    ordered_out[...] = product_plain(inputs[...], order[...]).astype(LOW)


def norm_rows(summed):
    row_mean = jnp.mean(summed, axis=-1, keepdims=True)
    centered = summed - row_mean
    inv_dev = lax.rsqrt(jnp.mean(centered * centered, axis=-1, keepdims=True) + NORM_EPS)
    return centered * inv_dev, inv_dev


def norm_rows_back(grad_out, normed, inv_dev, gain):
    scaled = grad_out * gain
    mean_one = jnp.mean(scaled, axis=-1, keepdims=True)
    mean_two = jnp.mean(scaled * normed, axis=-1, keepdims=True)
    return inv_dev * (scaled - mean_one - normed * mean_two)


def column_sum(value):
    return jnp.sum(value.astype(WIDE), axis=0, keepdims=True)


def four_rows(vectors, first):
    return jnp.concatenate([vectors[first + at : first + at + 1, :] for at in range(4)], axis=1)


def gelu_both(before):
    half = 0.5 * (1.0 + lax.erf(before * SQRT_HALF))
    slope = half + before * jnp.exp(-0.5 * before * before) * INV_SQRT_TWO_PI
    return before * half, slope


def out_kernel(where, hidden, mixed, mixed_got, low, high, low_got, high_got, *refs):
    vectors, order, full_out, ordered_out, normed_out, inv_out, low_out, mixed_full = refs
    core_at = where[2]
    own, other = aligned(core_at * HALF), aligned((1 - core_at) * HALF)
    rows = MODEL // 2
    full_out[:rows, pl.ds(own, HALF)] = whole_rows(low)
    full_out[rows:, pl.ds(own, HALF)] = whole_rows(high)
    full_out[:rows, pl.ds(other, HALF)] = whole_rows(low_got)
    full_out[rows:, pl.ds(other, HALF)] = whole_rows(high_got)
    mixed_full[:, pl.ds(own, HALF)] = mixed[...]
    mixed_full[:SEG, pl.ds(other, HALF)] = mixed_got[SEG:, :]
    mixed_full[SEG:, pl.ds(other, HALF)] = mixed_got[:SEG, :]
    branch = product_plain(mixed_full[:SEG, :], full_out[...])
    normed, inv_dev = norm_rows(hidden[...].astype(WIDE) + branch + vectors[2:3, :])
    normed_out[...] = normed
    inv_out[...] = inv_dev
    low_out[...] = (normed * vectors[4:5, :] + vectors[5:6, :]).astype(LOW)
    ordered_out[...] = product_plain(mixed_full[...], order[...]).astype(LOW)


def up_kernel(where, *refs):
    blocks = refs[:12]
    low, low_got, vectors = refs[12:15]
    weight, act_out, slope_out, both = refs[15:]
    core_at = where[2]
    gather_group(where, 1, blocks, ((weight, 0, FF_HALF),))
    both[:SEG] = low[...]
    both[SEG:] = low_got[...]
    for at in range(FF_HALF // MODEL):
        columns = slice(at * MODEL, (at + 1) * MODEL)
        held = weight[:, :, columns]
        before = product_plain(both[...], held.reshape(MODEL, MODEL))
        bias = vectors[pl.ds(8 + core_at * (FF_HALF // MODEL) + at, 1), :]
        value, slope = gelu_both(before + bias)
        act_out[:, columns] = value.astype(LOW)
        slope_out[:, columns] = slope


def down_kernel(where, *refs):
    blocks, act = refs[:12], refs[12]
    weight, own_out, send_out = refs[13:]
    gather_group(where, 2, blocks, ((weight, 0, FF_HALF),))
    partial = product_right(act[...], whole_rows(weight))
    own_out[...] = partial[:SEG]
    send_out[...] = partial[SEG:]


def seg_rows_kernel(where, *refs):
    own, got, normed_first, vectors, targets, live, seg_pos = refs[:7]
    normed_out, inv_out, diff_out, rows_out, head_out = refs[7:]
    doc, number = where[3], where[4]
    first = normed_first[...] * vectors[4:5, :] + vectors[5:6, :]
    normed, inv_dev = norm_rows(first + own[...] + got[...] + vectors[3:4, :])
    normed_out[...] = normed
    inv_out[...] = inv_dev
    rows = normed * vectors[6:7, :] + vectors[7:8, :]
    shape = (SEG, SEG)
    same = lax.broadcasted_iota(jnp.int32, shape, 0) == lax.broadcasted_iota(jnp.int32, shape, 1)
    live_rows = jnp.sum(jnp.where(same, live[...], 0.0), axis=1, keepdims=True)
    target_rows = targets[...].astype(WIDE)
    output = rows * live_rows
    rows_out[...] = output
    diff = (output - target_rows) * live_rows
    row_at = lax.broadcasted_iota(jnp.int32, (SEG, 1), 0)
    diff = jnp.where(row_at > 0, diff, 0.0)
    diff_out[...] = diff
    table = seg_pos[...].astype(WIDE)
    chosen = lax.broadcasted_iota(jnp.int32, table.shape, 0) == number
    position = jnp.sum(jnp.where(chosen, table, 0.0), axis=0, keepdims=True)
    head_out[:, :MODEL] = rows[0:1, :] + position
    head_out[:, MODEL : 2 * MODEL] = target_rows[0:1, :]
    square = jnp.sum(column_sum(diff * diff), axis=1, keepdims=True)
    lane = lax.broadcasted_iota(jnp.int32, (1, LANES), 1)
    facts = jnp.where(lane == 0, live_rows[0:1, :], 0.0)
    facts = jnp.where(lane == 1, doc.astype(WIDE), facts)
    facts = jnp.where(lane == 2, number.astype(WIDE), facts)
    facts = jnp.where(lane == 3, square, facts)
    head_out[:, 2 * MODEL :] = facts


def second_norm_kernel(where, diff, count, normed, inv_dev, vectors, grad_out, low_out, sums_out):
    grad_top = diff[...] * ((SEG * GROUP * CORES) / count[0:1, 0:1])
    normed_rows = normed[...]
    grad = norm_rows_back(grad_top, normed_rows, inv_dev[...], vectors[6:7, :])
    low = grad.astype(LOW)
    grad_out[...] = grad
    low_out[...] = low
    sums_out[0:1, :] = column_sum(low)
    sums_out[1:2, :] = column_sum(grad_top * normed_rows)
    sums_out[2:3, :] = column_sum(grad_top)


def mlp_back_kernel(where, *refs):
    low, low_got, down_weight, up_weight, slope = refs[:5]
    pre_out, own_out, send_out, sums_out, both = refs[5:]
    both[:SEG] = low[...]
    both[SEG:] = low_got[...]
    for at in range(FF_HALF // MODEL):
        columns = slice(at * MODEL, (at + 1) * MODEL)
        held = down_weight[:, :, columns]
        before = product_plain(both[...], held.reshape(MODEL, MODEL))
        pre = (before * slope[:, columns]).astype(LOW)
        pre_out[:, columns] = pre
        sums_out[at : at + 1, :] = column_sum(pre)
    partial = product_right(pre_out[...], whole_rows(up_weight))
    own_out[...] = partial[:SEG]
    send_out[...] = partial[SEG:]


def scatter_parts(where, parts, outs, sems):
    line_at, plane_at = where[0], where[1]
    far_low, far_high, to_x, to_y, kept = outs
    half = LINE // 2
    copies = []
    for mask in range(PLANE):
        for step in range(LINE):
            source = parts.at[(line_at + step) % LINE * PLANE + (plane_at ^ mask)]
            if mask == 3:
                target = far_low.at[step] if step < half else far_high.at[step - half]
            else:
                target = (kept, to_x, to_y)[mask].at[step]
            copies.append(pltpu.make_async_copy(source, target, sems.at[len(copies)]))
    for copy in copies:
        copy.start()
    wait_all(copies)


def mlp_weight_kernel(where, *refs):
    first, first_got, second, second_got, pre, act = refs[:6]
    outs = refs[6:11]
    left, parts, sems = refs[11:]
    for at, (own, got, right) in enumerate(((first, first_got, pre), (second, second_got, act))):
        left[:SEG] = own[...]
        left[SEG:] = got[...]
        for piece in range(FF_HALF // MODEL):
            start = piece * MODEL
            product = product_left(left[...], right[:, start : start + MODEL]).astype(LOW)
            target = at * FF_HALF + start
            parts[:, :, target : target + MODEL] = product.reshape(GROUP, OWN, MODEL)
    scatter_parts(where, parts, outs, sems)


def attn_product(where, refs, mask, piece):
    hidden, mixed, proj, branch, got = refs
    lanes = slice(mask * SPAN, (mask + 1) * SPAN)
    if piece < 3:
        right = proj[:, piece * HALF : (piece + 1) * HALF]
        product = product_left(hidden[:, lanes], right)
    else:
        own = branch[:, pl.ds(aligned(where[2] * HALF), HALF)]
        product = product_left(mixed[:SEG, lanes], own)
        product = product + product_left(mixed[SEG:, lanes], got[:, HALF:])
    return product[: LINE * OWN].astype(LOW).reshape(LINE, OWN, HALF)


def attn_far_kernel(where, *refs):
    low_out, high_out = refs[5:]
    half = LINE // 2
    for piece in range(4):
        columns = slice(piece * HALF, (piece + 1) * HALF)
        product = attn_product(where, refs[:5], 3, piece)
        low_out[:, :, columns] = product[:half]
        high_out[:, :, columns] = product[half:]


def attn_near_kernel(where, *refs):
    top_row, out_rows, live_row = refs[5:8]
    row_at = lax.broadcasted_iota(jnp.int32, (SEG, 1), 0)
    output = jnp.where(row_at == 0, top_row[...] * live_row[:, 0:1], out_rows[...])
    refs[11][...] = output.astype(LOW)
    for mask, out in ((1, refs[8]), (2, refs[9]), (0, refs[10])):
        for piece in range(4):
            columns = slice(piece * HALF, (piece + 1) * HALF)
            out[:, :, columns] = attn_product(where, refs[:5], mask, piece)


def fold_kernel(where, kept, got_x, got_y, *refs):
    extra, own_out, sent = refs[: -LINE], refs[-LINE], refs[1 - LINE :]
    rows = kept.shape[1]
    for step in range(LINE):
        total = kept[step].astype(WIDE) + got_x[step].astype(WIDE) + got_y[step].astype(WIDE)
        if step == 0:
            own_out[...] = total
            continue
        out = sent[step - 1]
        out[:rows, :] = total.astype(LOW)
        if extra:
            out[rows:, :] = jnp.zeros_like(out[rows:, :])
            out[rows:, : extra[0].shape[1]] = extra[0][...]


def reduce_far(parts):
    return together(in_plane(parts[0], 2), in_plane(parts[1], 1))


def reduce_add(where, parts, far):
    shape = parts[2].shape
    return run_kernel(
        add_far_kernel,
        "add_far",
        [shape_of(shape, LOW)] * 2,
        where,
        (),
        tuple(far) + (parts[2], parts[3]),
    )


def reduce_fold(where, kept, got, *extra):
    _, rows, columns = kept.shape
    more = sum(value.shape[0] for value in extra)
    return run_kernel(
        fold_kernel,
        "fold",
        [shape_of((rows, columns))] + [shape_of((rows + more, columns), LOW)] * (LINE - 1),
        where,
        (),
        (kept,) + tuple(got) + extra,
    )


def reduce_line(own, pieces):
    total = own
    for piece in pieces:
        total = total + piece[: own.shape[0]].astype(WIDE)
    return total


def head_back_kernel(where, *refs):
    grad, grad_got, down_weight, up_weight, slope, act, low, low_got = refs[:8]
    own_out, send_out, data_out = refs[8:]
    few = 16
    row_at = lax.broadcasted_iota(jnp.int32, (few, 1), 0)

    def two_rows(first, second):
        return jnp.where(row_at == 0, first, jnp.where(row_at == 1, second, 0.0))

    second = two_rows(grad[...], grad_got[...]).astype(LOW)
    data_out[0:1, :] = low[0:1, :].astype(WIDE)
    data_out[1:2, :] = low_got[0:1, :].astype(WIDE)
    data_out[2:4, :] = second[0:2].astype(WIDE)
    partial = jnp.zeros((few, MODEL), WIDE)
    for at in range(FF_HALF // MODEL):
        columns = slice(at * MODEL, (at + 1) * MODEL)
        before = product_plain(second, down_weight[:, :, columns].reshape(MODEL, MODEL))
        slopes = two_rows(slope[0:1, columns], slope[SEG : SEG + 1, columns])
        pre = (before * slopes).astype(LOW)
        partial = partial + product_right(pre, up_weight[:, :, columns].reshape(MODEL, MODEL))
        data_out[4 + 2 * at : 6 + 2 * at, :] = pre[0:2].astype(WIDE)
        data_out[8 + 2 * at : 9 + 2 * at, :] = act[0:1, columns].astype(WIDE)
        data_out[9 + 2 * at : 10 + 2 * at, :] = act[SEG : SEG + 1, columns].astype(WIDE)
    own_out[...] = partial[0:1]
    send_out[...] = partial[1:2]


def first_norm_kernel(where, *refs):
    second_grad, own, got, head_grad, head_own, head_got = refs[:6]
    normed_rows, inv_dev, vectors, out_weight = refs[6:10]
    grad_out, branch_out, mixed_out, send_out, sums_out = refs[10:]
    core_at = where[2]
    grad_rows = second_grad[...] + own[...] + got[...]
    head = head_grad[...] + head_own[...] + head_got[...]
    row_at = lax.broadcasted_iota(jnp.int32, (SEG, 1), 0)
    grad_rows = jnp.where(row_at == 0, head, grad_rows)
    normed = normed_rows[...]
    grad = norm_rows_back(grad_rows, normed, inv_dev[...], vectors[4:5, :])
    grad_out[...] = grad
    branch = grad.astype(LOW)
    branch_out[...] = branch
    mixed_out[...] = product_right(branch, out_weight[...]).astype(LOW)
    other = pl.ds(aligned((1 - core_at) * HALF), HALF)
    send_out[:, :HALF] = mixed_out[:, other]
    send_out[:, HALF:] = branch_out[:, other]
    sums_out[0:1, :] = column_sum(branch)
    sums_out[1:2, :] = column_sum(grad_rows * normed)
    sums_out[2:3, :] = column_sum(grad_rows)


def attn_back_kernel(where, *refs):
    qkv, mixed_grad, got, live_row, live_got, weight = refs[:6]
    sums_first, sums_second, sums_up, head_top, head_normed, data = refs[6:12]
    proj_out, own_out, send_out, payload_out, rows = refs[12:]
    core_at = where[2]
    lanes = pl.ds(aligned(core_at * HALF), HALF)
    for part, live in enumerate((live_row, live_got)):
        at = slice(part * SEG, (part + 1) * SEG)
        grad = mixed_grad[:, lanes] if part == 0 else got[:, :HALF]
        pieces = attend_tiles_back(qkv[at, :], grad, HALF, token_allowed(live[...]))
        for tile, value in enumerate(pieces):
            proj_out[at, tile * LANES : (tile + 1) * LANES] = value
    partial = product_right(proj_out[...], whole_rows(weight))
    own_out[...] = partial[:SEG]
    send_out[...] = partial[SEG:]
    rows[...] = jnp.zeros_like(rows)
    rows[0:12, :] = data[0:12, :]
    rows[12:13, lanes] = column_sum(proj_out[:, :HALF])
    rows[13:14, lanes] = column_sum(proj_out[:, 2 * HALF :])
    rows[14:15, :] = sums_first[0:1, :]
    rows[15:16, :] = sums_second[0:1, :] + data[2:3, :]
    rows[16:18, :] = sums_first[1:3, :]
    rows[18:19, :] = sums_second[1:2, :] + head_top[...] * head_normed[0:1, :]
    rows[19:20, :] = sums_second[2:3, :] + head_top[...]
    for at in range(FF_HALF // MODEL):
        total = sums_up[at : at + 1, :] + data[4 + 2 * at : 5 + 2 * at, :]
        total = total + data[5 + 2 * at : 6 + 2 * at, :]
        rows[pl.ds(20 + core_at * (FF_HALF // MODEL) + at, 1), :] = total
    payload_out[...] = rows[...].astype(LOW)


def cls_gather_kernel(where, *refs):
    blocks = refs[:8]
    own_out, from_x, from_y, far_x = refs[8], refs[4], refs[5], refs[6]
    weight_out, out_rows = refs[9:]
    plane_at = where[1]
    gather_blocks(where, blocks, 0, QUARTER_HALF, ((weight_out, 0, QUARTER_HALF),))
    first = LINE * QUARTER_HALF
    out_rows[plane_at] = own_out[...]
    out_rows[plane_at ^ 1] = from_x[:, first : first + HALF]
    out_rows[plane_at ^ 2] = from_y[:, first : first + HALF]
    first = LINE // 2 * QUARTER_HALF
    out_rows[plane_at ^ 3] = far_x[:, first : first + HALF]


def cls_weight_kernel(where, own, got, out_half, out_got, weight_out, out_full):
    line_at, core_at = where[0], where[2]
    out_full[...] = jnp.zeros_like(out_full)
    for value, part, core in ((own, out_half, core_at), (got, out_got, 1 - core_at)):
        weight_out[:, :, pl.ds(aligned(core * QUARTER_HALF), QUARTER_HALF)] = value[...]
        rows = part[...].reshape(3, HEAD_DIM, HALF)
        out_full[pl.ds(line_at % 2, 3), :, pl.ds(aligned(core * HALF), HALF)] = rows


def add_far_kernel(where, far_low, far_high, to_x, to_y, x_out, y_out):
    half = LINE // 2
    x_out[:half] = to_x[:half] + far_low[...]
    x_out[half:] = to_x[half:]
    y_out[:half] = to_y[:half]
    y_out[half:] = to_y[half:] + far_high[...]


def row_from_column(column, size):
    shape = (size, size)
    same = lax.broadcasted_iota(jnp.int32, shape, 0) == lax.broadcasted_iota(jnp.int32, shape, 1)
    return jnp.sum(jnp.where(same, column, 0.0), axis=0, keepdims=True)


def head_allowed(heads):
    facts = heads[:, 2 * MODEL :]
    live, doc = facts[:, 0:1], facts[:, 1:2]
    shape = (GROUP, GROUP)
    same = lax.broadcasted_iota(jnp.int32, shape, 0) == lax.broadcasted_iota(jnp.int32, shape, 1)
    live_row, doc_row = row_from_column(live, GROUP), row_from_column(doc, GROUP)
    return ((live_row > 0.5) & (doc == doc_row)) | same


def quarter_mask(quarter):
    lane = lax.broadcasted_iota(jnp.int32, (GROUP, SPAN), 1)
    first = (quarter % 2) * HEAD_DIM
    return (lane >= first) & (lane < first + 3 * HEAD_DIM)


def quarter_piece(vectors, row, quarter):
    value = jnp.zeros((1, SPAN), WIDE)
    for at in range(LINE):
        first = TILE_START[at] * LANES
        value = jnp.where(quarter == at, vectors[row : row + 1, first : first + SPAN], value)
    return value


def cls_attend_kernel(where, *refs):
    stacks, vectors, weight, out_weight = refs[:4], refs[4], refs[5], refs[6]
    heads_out, qkv_out, mixed_out, part_out = refs[7:]
    line_at, plane_at = where[0], where[1]
    for step, stack in enumerate(stacks):
        for mask in range(PLANE):
            row = (line_at + LINE - step) % LINE * PLANE + (plane_at ^ mask)
            heads_out[pl.ds(row, 1), :] = stack[mask : mask + 1, :]
    heads = heads_out[...]
    inputs = heads[:, :MODEL].astype(LOW)
    projected = product_plain(inputs, weight[:, : 3 * SPAN])
    query = projected[:, :SPAN] + quarter_piece(vectors, 12, line_at)
    value = projected[:, 2 * SPAN :] + quarter_piece(vectors, 13, line_at)
    qkv_out[:, :SPAN] = query.astype(LOW)
    qkv_out[:, SPAN : 2 * SPAN] = projected[:, SPAN : 2 * SPAN].astype(LOW)
    qkv_out[:, 2 * SPAN :] = value.astype(LOW)
    mixed = attend_tiles(qkv_out[...], SPAN, head_allowed(heads))
    mixed = masked(jnp.concatenate(mixed, axis=1), quarter_mask(line_at))
    mixed_out[...] = mixed
    part_out[...] = product_plain(mixed, out_weight[...])


def cls_mlp_kernel(where, *refs):
    heads, own, got_one, got_two, got_three, vectors, weight = refs[:7]
    normed_out, inv_out, low_out, act_out, slope_out, part_out = refs[7:]
    line_at = where[0]
    branch = own[...] + got_one[...] + got_two[...] + got_three[...]
    normed, inv_dev = norm_rows(heads[:, :MODEL] + branch + vectors[14:15, :])
    normed_out[...] = normed
    inv_out[...] = inv_dev
    low = (normed * vectors[16:17, :] + vectors[17:18, :]).astype(LOW)
    low_out[...] = low
    part = FF // LINE
    first = 3 * SPAN
    bias = vectors[pl.ds(20 + line_at, 1), :]
    before = product_plain(low, weight[:, first : first + part]) + bias
    value, slope = gelu_both(before)
    act = value.astype(LOW)
    act_out[...] = act
    slope_out[...] = slope
    part_out[...] = product_right(act, weight[:, first + part :])


def cls_top_kernel(where, *refs):
    heads, own, got_one, got_two, got_three, vectors, weight = refs[:7]
    normed_first, count, slope = refs[7:10]
    top_out, square_out, grad_out, second_out, pre_out, part_out, sums_out = refs[10:17]
    held = refs[17]
    rank = where[0] * PLANE + where[1]
    first = normed_first[...] * vectors[16:17, :] + vectors[17:18, :]
    down = own[...] + got_one[...] + got_two[...] + got_three[...]
    normed, inv_dev = norm_rows(first + down + vectors[15:16, :])
    rows = normed * vectors[18:19, :] + vectors[19:20, :]
    held[...] = rows
    top_out[...] = held[pl.ds(rank, 1), :]
    facts = heads[:, 2 * MODEL :]
    live = facts[:, 0:1]
    diff = (rows * live - heads[:, MODEL : 2 * MODEL]) * live
    square = jnp.sum(column_sum(diff * diff), axis=1, keepdims=True)
    square = square + jnp.sum(facts[:, 3:4], axis=0, keepdims=True)
    square_out[...] = jnp.broadcast_to(square, square_out.shape)
    grad_top = diff * ((SEG * GROUP * CORES) / count[0:1, 0:1])
    grad = norm_rows_back(grad_top, normed, inv_dev, vectors[18:19, :])
    sums_out[0:1, :] = column_sum(grad_top * normed)
    sums_out[1:2, :] = column_sum(grad_top)
    grad_out[...] = grad
    second = grad.astype(LOW)
    second_out[...] = second
    part = FF // LINE
    at = 3 * SPAN
    pre = (product_plain(second, weight[:, at + part :]) * slope[...]).astype(LOW)
    pre_out[...] = pre
    part_out[...] = product_right(pre, weight[:, at : at + part])


def cls_attend_back_kernel(where, *refs):
    heads, own, got_one, got_two, got_three, vectors, weight, out_weight = refs[:8]
    grad_in, normed_first, inv_first, qkv = refs[8:12]
    grad_out, branch_out, proj_out, part_out, sums_out = refs[12:]
    line_at = where[0]
    grad_first = grad_in[...] + own[...] + got_one[...] + got_two[...] + got_three[...]
    normed = normed_first[...]
    grad = norm_rows_back(grad_first, normed, inv_first[...], vectors[16:17, :])
    sums_out[0:1, :] = column_sum(grad_first * normed)
    sums_out[1:2, :] = column_sum(grad_first)
    grad_out[...] = grad
    branch = grad.astype(LOW)
    branch_out[...] = branch
    mask = quarter_mask(line_at)
    mixed_grad = masked(product_right(branch, out_weight[...]).astype(LOW), mask)
    pieces = attend_tiles_back(qkv[...], mixed_grad, SPAN, head_allowed(heads[...]))
    tiles = SPAN // LANES
    for piece in range(3):
        joined = jnp.concatenate(pieces[piece * tiles : (piece + 1) * tiles], axis=1)
        proj_out[:, piece * SPAN : (piece + 1) * SPAN] = masked(joined, mask)
    part_out[...] = product_right(proj_out[...], weight[:, : 3 * SPAN])


def cls_end_kernel(where, *refs):
    heads, grad, own, got_one, got_two, got_three = refs[:6]
    square, sums_back, sums_top = refs[6:9]
    normed_second, inv_second, vectors = refs[9:12]
    row_out, second_out, shared_out, held = refs[12:]
    rank = where[0] * PLANE + where[1]
    total = grad[...] + own[...] + got_one[...] + got_two[...] + got_three[...]
    held[...] = total
    row = held[pl.ds(rank, 1), :]
    row_out[...] = row
    second_out[...] = norm_rows_back(
        row, normed_second[0:1, :], inv_second[0:1, :], vectors[6:7, :]
    )
    number = row_from_column(heads[:, 2 * MODEL + 2 : 2 * MODEL + 3], GROUP)
    entry = lax.broadcasted_iota(jnp.int32, (GROUP, GROUP), 0).astype(WIDE)
    hot = (entry == number).astype(WIDE)
    shared_out[0:GROUP, :] = jnp.dot(hot, total, precision=lax.Precision.HIGHEST)
    shared_out[GROUP : GROUP + 1, 0:LANES] = square[0:1, :]
    shared_out[GROUP + 1 : GROUP + 3, :] = sums_back[0:2, :]
    shared_out[GROUP + 3 : GROUP + 5, :] = sums_top[0:2, :]


def head_mlp_kernel(where, *refs):
    cls_mlp_kernel(where, *refs[:7], *refs[11:17])
    add_far_kernel(where, *refs[7:11], *refs[17:])


def head_end_kernel(where, *refs):
    cls_end_kernel(where, *refs[:12], *refs[16:19], refs[23])
    fold_kernel(where, *refs[12:16], *refs[19:23])


def attn_add_kernel(where, *refs):
    far_low, far_high, to_x, to_y, grad, own, got, x_out, y_out, input_out = refs
    add_far_kernel(where, far_low, far_high, to_x, to_y, x_out, y_out)
    input_out[...] = (grad[...] + own[...] + got[...]).astype(LOW)


def cls_rows_kernel(where, *refs):
    packs = refs[:4]
    heads, branch, low, second = refs[4:8]
    out, kept = refs[8:]
    line_at = where[0]
    rows, width = kept.shape[1:]
    for step, pack in enumerate(packs):
        first = pack.shape[0] - rows
        kept[(line_at + LINE - step) % LINE] = pack[first:, :width]
    starts = (MODEL, 2 * MODEL, 3 * MODEL, 4 * MODEL)
    out[:, 0:MODEL] = heads[:, :MODEL].astype(LOW)
    for piece, start in enumerate(starts):
        from_at = piece * SPAN
        for tile in range(MODEL // LANES):
            total = None
            for at in range(PLANE):
                inner = tile - TILE_START[at]
                if inner in (0, 1):
                    first = from_at + inner * LANES
                    value = kept[at, :, first : first + LANES]
                    total = value if total is None else total + value
            out[:, start + tile * LANES : start + (tile + 1) * LANES] = total
    out[:, 5 * MODEL : 6 * MODEL] = branch[...]
    out[:, 6 * MODEL : 7 * MODEL] = low[...]
    out[:, 7 * MODEL + FF : 8 * MODEL + FF] = second[...]
    part = FF // LINE
    for at in range(PLANE):
        first = 4 * SPAN
        out[:, 7 * MODEL + at * part : 7 * MODEL + (at + 1) * part] = kept[
            at, :, first : first + part
        ]
        out[:, 8 * MODEL + FF + at * part : 8 * MODEL + FF + (at + 1) * part] = kept[
            at, :, first + part : first + 2 * part
        ]


def own_features(rank, width):
    shape = (MODEL, width)
    feature = lax.broadcasted_iota(jnp.int32, shape, 0)
    column = lax.broadcasted_iota(jnp.int32, shape, 1)
    return (feature == rank * width + column).astype(LOW)


def own_vector(rank, pieces, out, flat):
    size = out.shape[0]
    for at, piece in enumerate(pieces):
        flat[:, at * MODEL : (at + 1) * MODEL] = piece
    value = jnp.zeros((1, size), WIDE)
    for chip in range(GROUP):
        value = jnp.where(rank == chip, flat[:, chip * size : (chip + 1) * size], value)
    out[...] = value.reshape(size)


def cls_owner_kernel(where, *refs):
    own, got, shared, mats_out, vec_out, rows, flat = refs
    rank = where[0] * PLANE + where[1]
    width = mats_out.shape[0]
    rows[:GROUP] = own[...]
    rows[GROUP:] = got[...]
    chosen = own_features(rank, width)
    plan = (
        (0, MODEL, 3 * MODEL, 0),
        (4 * MODEL, 5 * MODEL, MODEL, 3 * MODEL),
        (6 * MODEL, 7 * MODEL, FF, 4 * MODEL),
        (7 * MODEL + FF, 8 * MODEL + FF, FF, 4 * MODEL + FF),
    )
    for left, right, size, target in plan:
        side = product_plain(rows[:, left : left + MODEL], chosen).astype(LOW)
        mats_out[:, target : target + size] = product_left(side, rows[:, right : right + size])
    starts = (MODEL, 3 * MODEL, 5 * MODEL, 7 * MODEL + FF)
    pieces = [column_sum(rows[:, start : start + MODEL]) for start in starts]
    pieces += [shared[GROUP + 1 + at : GROUP + 2 + at, :] for at in range(4)]
    starts = [7 * MODEL + at * MODEL for at in range(FF // MODEL)]
    pieces += [column_sum(rows[:, start : start + MODEL]) for start in starts]
    own_vector(rank, pieces, vec_out, flat)


def head_share_kernel(where, *refs):
    packs, mlp = refs[:4], refs[4]
    mine_out, vecs_out, rows = refs[5:]
    rank = where[0] * PLANE + where[1]
    count = LINE * 24
    for at, pack in enumerate(packs):
        rows[at * count : (at + 1) * count] = pack[...]
    total = PLANE * count

    def chosen(base, apart):
        shape = (CORES * GROUP, total)
        row = lax.broadcasted_iota(jnp.int32, shape, 0)
        column = lax.broadcasted_iota(jnp.int32, shape, 1)
        hot = (column == row // 2 * 24 + base + row % 2 * apart).astype(LOW)
        return product_plain(hot, rows[...]).astype(LOW)

    own = own_features(rank, OWN)
    for at, (left, right) in enumerate(((0, 4), (2, 8))):
        side = product_plain(chosen(left, 1), own).astype(LOW)
        for piece in range(FF_HALF // MODEL):
            columns = slice(at * FF_HALF + piece * MODEL, at * FF_HALF + (piece + 1) * MODEL)
            share = product_left(side, chosen(right + 2 * piece, 1))
            mine_out[:, columns] = mlp[:, columns] + share
    shape = (16, total)
    row = lax.broadcasted_iota(jnp.int32, shape, 0)
    column = lax.broadcasted_iota(jnp.int32, shape, 1)
    hot = ((column % 24 == row + 12) & (row < 12)).astype(LOW)
    vecs_out[...] = product_plain(hot, rows[...])


def share_owner_kernel(where, *refs):
    head_share_kernel(where, *refs[:5], *refs[9:11], refs[15])
    cls_owner_kernel(where, *refs[5:8], *refs[11:13], *refs[16:])
    shared, count, pos_out, loss_out = refs[7], refs[8], refs[13], refs[14]
    pos_out[...] = shared[:GROUP, :]
    loss_out[...] = shared[GROUP : GROUP + 1, 0:1] / (count[0:1, 0:1] * MODEL)


def seg_vec_kernel(where, vecs, vecs_got, vec_out, flat):
    rank = where[0] * PLANE + where[1]
    rows = (8 * MODEL + FF) // MODEL
    pieces = [vecs[at : at + 1, :] + vecs_got[at : at + 1, :] for at in range(rows)]
    own_vector(rank, pieces, vec_out, flat)


def column_copies(where, out, base, size, own, got, first):
    core_at = where[2]
    lanes = slice(first, first + size)
    return [
        (own.at[:, lanes], out.at[:, pl.ds(aligned(base + core_at * size), size)]),
        (got.at[:, lanes], out.at[:, pl.ds(aligned(base + (1 - core_at) * size), size)]),
    ]


def store_kernel(where, attn, attn_got, mlp, mlp_got, vecs, vecs_got, out, vec_out, flat, sems):
    pairs = []
    for piece in range(4):
        pairs += column_copies(where, out, piece * MODEL, HALF, attn, attn_got, piece * HALF)
    for piece in range(2):
        base = 4 * MODEL + piece * FF
        pairs += column_copies(where, out, base, FF_HALF, mlp, mlp_got, piece * FF_HALF)
    copies = [
        pltpu.make_async_copy(source, target, sems.at[at])
        for at, (source, target) in enumerate(pairs)
    ]
    for copy in copies:
        copy.start()
    seg_vec_kernel(where, vecs, vecs_got, vec_out, flat)
    wait_all(copies)


def plane_parts(part):
    return (part,) + together(*(in_plane(part, mask) for mask in range(1, PLANE)))


def line_parts(part):
    return (part,) + together(*(along_line(part, apart) for apart in range(1, LINE)))


def slice_local(
    hidden_in,
    targets,
    doc_ids,
    seg_nums,
    valid_flags,
    seg_mats,
    seg_vecs,
    cls_mats,
    cls_vecs,
    seg_pos,
):
    rank, core_at = lax.axis_index("fsdp"), lax.axis_index("rep")
    line_at, plane_at = rank // PLANE, rank % PLANE
    where = jnp.stack([line_at, plane_at, core_at, doc_ids[0], seg_nums[0]]).astype(jnp.int32)
    own_rows, total_columns = seg_mats.shape
    vec_size = seg_vecs.shape[0]
    both_rows = CORES * SEG

    first_piece, live_row, *rest = run_kernel(
        prepare_kernel,
        "prepare",
        [shape_of((own_rows, FIRST), LOW), shape_of((1, SEG))]
        + [shape_of((own_rows, FF_HALF), LOW)] * 2
        + [shape_of((own_rows, QUARTER_HALF), LOW)] * LINE
        + [shape_of((own_rows, HALF), LOW), shape_of((MODEL, PLANE * SPAN), LOW)],
        where,
        (seg_mats, cls_mats),
        (seg_vecs, cls_vecs, valid_flags),
        [
            pltpu.SemaphoreType.DMA((4,)),
            pltpu.VMEM((LINE, own_rows, QUARTER), LOW),
            pltpu.SemaphoreType.DMA((3 + 5 * LINE,)),
        ],
    )
    first_line = line_parts(first_piece)
    second_piece, third_piece, quarters, cls_out_piece, order = (
        rest[0],
        rest[1],
        rest[2:-2],
        rest[-2],
        rest[-1],
    )

    def joined(*pieces):
        return jnp.concatenate(pieces, axis=1)

    def sent_both(to_x, to_y):
        to_x, to_y = together(to_x, to_y)
        return together(in_plane(to_x, 1), in_plane(to_y, 2))

    own_sent = joined(first_piece, second_piece, third_piece)
    own_x, own_y = sent_both(own_sent, own_sent)
    first_line = first_line[:1] + tuple(after(got, own_x, own_y) for got in first_line[1:])
    hidden_got = other_core(after(hidden_in, own_x, own_y))
    live_got = other_core(after(live_row, own_x, own_y))
    to_x = joined(after(own_y, hidden_got, live_got)[:, OWN_CUT:], *first_line[1:])
    to_y = joined(own_x[:, :OWN_CUT], *first_line[1:])
    first_x, first_y = sent_both(to_x, to_y)
    second_line = line_parts(after(second_piece, to_x, to_y))

    def halves(group, from_x, from_y):
        width, cut = WIDTHS[group], LINE_CUTS[group]
        if group == 0:
            base_x, base_y = sum(WIDTHS) - OWN_CUT, OWN_CUT
        else:
            before, before_cut = WIDTHS[group - 1], LINE_CUTS[group - 1]
            base_x, base_y = 2 * before - before_cut, before + before_cut
        return (
            from_y[:, base_y + width + cut : base_y + 3 * width],
            from_x[:, base_x : base_x + width + cut],
        )

    high, low = halves(0, first_x, first_y)
    to_x, to_y = joined(high, *second_line[1:]), joined(low, *second_line[1:])
    second_x, second_y = sent_both(to_x, to_y)
    third_line = line_parts(after(third_piece, to_x, to_y))
    high, low = halves(1, second_x, second_y)
    to_x, to_y = joined(high, *third_line[1:]), joined(low, *third_line[1:])
    third_x, third_y = sent_both(to_x, to_y)
    own_parts = (own_x, own_y, first_x, first_y)
    cls_line = (quarters[0],) + tuple(
        along_line(after(quarters[apart], to_x, to_y), apart)
        for apart in range(1, LINE)
    )

    qkv_weight, out_low, out_high, qkv, mixed, vectors, count, hidden_ordered = run_kernel(
        qkv_kernel,
        "seg_qkv",
        [
            shape_of((GROUP, own_rows, 3 * HALF), LOW),
            shape_of((GROUP // 2, own_rows, HALF), LOW),
            shape_of((GROUP // 2, own_rows, HALF), LOW),
            shape_of((both_rows, 3 * HALF), LOW),
            shape_of((both_rows, HALF), LOW),
            shape_of((2 * (8 * MODEL + FF) // MODEL, MODEL)),
            shape_of((8, LANES)),
            shape_of((both_rows, PLANE * SPAN), LOW),
        ],
        where,
        (),
        first_line
        + own_parts
        + (first_x, first_y, second_x, second_y)
        + (hidden_in, hidden_got, live_row, live_got, order),
        [
            pltpu.VMEM((GROUP, own_rows, LANES), LOW),
            pltpu.VMEM((2, 8 * MODEL + FF), WIDE),
            pltpu.VMEM((both_rows, MODEL), LOW),
            pltpu.VMEM((GROUP, own_rows, HALF), LOW),
        ],
        flops=2 * SEG * MODEL * 3 * MODEL,
    )
    out_weight, mixed_ordered, normed_first, inv_first, first_low = run_kernel(
        out_kernel,
        "seg_out",
        [
            shape_of((MODEL, MODEL), LOW),
            shape_of((both_rows, PLANE * SPAN), LOW),
            shape_of((SEG, MODEL)),
            shape_of((SEG, 1)),
            shape_of((SEG, MODEL), LOW),
        ],
        where,
        (),
        (
            hidden_in,
            mixed,
            after(other_core(mixed), third_x, third_y),
            out_low,
            out_high,
            other_core(out_low),
            other_core(out_high),
            vectors,
            order,
        ),
        [pltpu.VMEM((both_rows, MODEL), LOW)],
        flops=2 * SEG * MODEL * MODEL,
    )
    fourth_x, fourth_y = sent_both(*halves(2, third_x, third_y))
    first_got = after(other_core(first_low), fourth_x, fourth_y)
    count = count + other_core(after(count, first_got))
    up_weight, act, slope = run_kernel(
        up_kernel,
        "seg_up",
        [
            shape_of((GROUP, own_rows, FF_HALF), LOW),
            shape_of((both_rows, FF_HALF), LOW),
            shape_of((both_rows, FF_HALF)),
        ],
        where,
        (),
        second_line
        + own_parts
        + (second_x, second_y, third_x, third_y)
        + (first_low, first_got, vectors),
        [pltpu.VMEM((both_rows, MODEL), LOW)],
        flops=2 * SEG * MODEL * FF,
    )
    cls_sent = joined(*cls_line, cls_out_piece)
    cls_sent = after(cls_sent, act)
    cls_x, cls_y = sent_both(cls_sent, cls_sent)
    down_weight, down_own, down_send = run_kernel(
        down_kernel,
        "seg_down",
        [
            shape_of((GROUP, own_rows, FF_HALF), LOW),
            shape_of((SEG, MODEL)),
            shape_of((SEG, MODEL)),
        ],
        where,
        (),
        third_line + own_parts + (third_x, third_y, fourth_x, fourth_y) + (act,),
        flops=2 * SEG * MODEL * FF,
    )
    normed_second, inv_second, diff, out_rows, head_row = run_kernel(
        seg_rows_kernel,
        "seg_rows",
        [
            shape_of((SEG, MODEL)),
            shape_of((SEG, 1)),
            shape_of((SEG, MODEL)),
            shape_of((SEG, MODEL)),
            shape_of((1, 2 * MODEL + LANES)),
        ],
        where,
        (),
        (
            down_own,
            other_core(down_send),
            normed_first,
            vectors,
            targets,
            live_row,
            seg_pos,
        ),
    )
    head_planes = plane_parts(head_row)
    head_lines = line_parts(jnp.concatenate(head_planes))
    size = LINE // 2 * QUARTER_HALF
    cls_far = sent_both(
        after(cls_y[:, size:], *head_planes[1:]), after(cls_x[:, :size], *head_planes[1:])
    )

    second_grad, second_low, second_sums = run_kernel(
        second_norm_kernel,
        "seg_second_norm",
        [shape_of((SEG, MODEL)), shape_of((SEG, MODEL), LOW), shape_of((3, MODEL))],
        where,
        (),
        (diff, count, normed_second, inv_second, vectors),
    )
    second_got = other_core(second_low)
    pre, first_grad_own, first_grad_send, up_sums = run_kernel(
        mlp_back_kernel,
        "seg_mlp_back",
        [
            shape_of((both_rows, FF_HALF), LOW),
            shape_of((SEG, MODEL)),
            shape_of((SEG, MODEL)),
            shape_of((FF_HALF // MODEL, MODEL)),
        ],
        where,
        (),
        (second_low, second_got, down_weight, up_weight, slope),
        [pltpu.VMEM((both_rows, MODEL), LOW)],
        flops=4 * SEG * MODEL * FF,
    )
    first_grad_got = other_core(first_grad_send)

    def part_shapes(columns):
        return [
            shape_of((count_of, own_rows, columns), LOW)
            for count_of in (LINE // 2, LINE // 2, LINE, LINE, LINE)
        ]

    head_lines = head_lines[:1] + together(*(after(got, pre) for got in head_lines[1:]))
    cls_far = together(*(after(got, *head_lines[1:]) for got in cls_far))
    cls_half, cls_out_half = run_kernel(
        cls_gather_kernel,
        "head_gather",
        [
            shape_of((GROUP, own_rows, QUARTER_HALF), LOW),
            shape_of((PLANE, own_rows, HALF), LOW),
        ],
        where,
        (),
        cls_line + (cls_x, cls_y) + cls_far + (cls_out_piece,),
    )
    mlp_parts = run_kernel(
        mlp_weight_kernel,
        "seg_mlp_weight",
        part_shapes(FF),
        where,
        (),
        (first_low, first_got, second_low, second_got, after(pre, cls_half), act),
        [
            pltpu.VMEM((both_rows, MODEL), LOW),
            pltpu.VMEM((GROUP, own_rows, FF), LOW),
            pltpu.SemaphoreType.DMA((GROUP,)),
        ],
        far=range(5),
        flops=4 * SEG * MODEL * FF,
    )
    mlp_far = reduce_far(tuple(after(part, *cls_far) for part in mlp_parts[:2]))
    cls_weight, cls_out = run_kernel(
        cls_weight_kernel,
        "head_weight",
        [
            shape_of((GROUP, own_rows, QUARTER), LOW),
            shape_of((4, HEAD_DIM, MODEL), LOW),
        ],
        where,
        (),
        (cls_half, other_core(cls_half), cls_out_half, other_core(cls_out_half)),
    )
    cls_weight = cls_weight.reshape(MODEL, QUARTER)
    cls_out = cls_out.reshape(SPAN, MODEL)
    heads, cls_qkv, cls_mixed, part = run_kernel(
        cls_attend_kernel,
        "head_attend",
        [
            shape_of((GROUP, 2 * MODEL + LANES)),
            shape_of((GROUP, 3 * SPAN), LOW),
            shape_of((GROUP, SPAN), LOW),
            shape_of((GROUP, MODEL)),
        ],
        where,
        (),
        tuple(after(got, mlp_parts[0], first_grad_got) for got in head_lines)
        + (vectors, cls_weight, cls_out),
    )
    cls_normed, cls_inv, cls_low, cls_act, cls_slope, part, *mlp_sent = run_kernel(
        head_mlp_kernel,
        "head_mlp",
        [
            shape_of((GROUP, MODEL)),
            shape_of((GROUP, 1)),
            shape_of((GROUP, MODEL), LOW),
            shape_of((GROUP, FF // LINE), LOW),
            shape_of((GROUP, FF // LINE)),
            shape_of((GROUP, MODEL)),
            shape_of(mlp_parts[2].shape, LOW),
            shape_of(mlp_parts[2].shape, LOW),
        ],
        where,
        (),
        (heads,) + line_parts(part) + (vectors, cls_weight) + mlp_far + tuple(mlp_parts[2:4]),
    )
    mlp_plane = sent_both(*mlp_sent)
    cls_parts = line_parts(part)
    top_row, square, cls_grad, cls_second, cls_pre, part, top_sums = run_kernel(
        cls_top_kernel,
        "head_top",
        [
            shape_of((1, MODEL)),
            shape_of((8, LANES)),
            shape_of((GROUP, MODEL)),
            shape_of((GROUP, MODEL), LOW),
            shape_of((GROUP, FF // LINE), LOW),
            shape_of((GROUP, MODEL)),
            shape_of((2, MODEL)),
        ],
        where,
        (),
        (heads,)
        + cls_parts
        + (vectors, cls_weight, cls_normed, count, cls_slope),
        [pltpu.VMEM((GROUP, MODEL), WIDE)],
    )
    top_parts = line_parts(part)
    cls_grad, cls_branch, cls_proj, part, back_sums = run_kernel(
        cls_attend_back_kernel,
        "head_attend_back",
        [
            shape_of((GROUP, MODEL)),
            shape_of((GROUP, MODEL), LOW),
            shape_of((GROUP, 3 * SPAN), LOW),
            shape_of((GROUP, MODEL)),
            shape_of((2, MODEL)),
        ],
        where,
        (),
        (heads,)
        + top_parts
        + (vectors, cls_weight, cls_out, cls_grad, cls_normed, cls_inv, cls_qkv),
    )
    end_parts = line_parts(part)
    pack = jnp.concatenate([cls_proj, cls_mixed, cls_pre, cls_act], axis=1)
    folded = [shape_of((own_rows, FF))] + [shape_of((own_rows + GROUP, FF), LOW)] * (LINE - 1)
    dheads, head_grad, shared, mlp_own, *mlp_sent = run_kernel(
        head_end_kernel,
        "head_end",
        [shape_of((1, MODEL)), shape_of((1, MODEL)), shape_of((GROUP + 8, MODEL))] + folded,
        where,
        (),
        (heads, cls_grad)
        + end_parts
        + (square, back_sums, top_sums, normed_second, inv_second, vectors)
        + (mlp_parts[4],)
        + mlp_plane
        + (pack,),
        [pltpu.VMEM((GROUP, MODEL), WIDE)],
    )
    got_three, got_two = along_line(mlp_sent[2], 3), along_line(mlp_sent[1], 2)
    mlp_last = mlp_sent[0]
    mlp_got = [None, got_two, got_three]

    head_own, head_send, head_data = run_kernel(
        head_back_kernel,
        "seg_head_back",
        [shape_of((1, MODEL)), shape_of((1, MODEL)), shape_of((12, MODEL))],
        where,
        (),
        (
            head_grad,
            other_core(head_grad),
            down_weight,
            up_weight,
            slope,
            act,
            first_low,
            first_got,
        ),
    )
    grad_summed, branch, mixed_grad, attn_send, first_sums = run_kernel(
        first_norm_kernel,
        "seg_first_norm",
        [
            shape_of((SEG, MODEL)),
            shape_of((SEG, MODEL), LOW),
            shape_of((SEG, MODEL), LOW),
            shape_of((SEG, MODEL), LOW),
            shape_of((3, MODEL)),
        ],
        where,
        (),
        (
            second_grad,
            first_grad_own,
            first_grad_got,
            head_grad,
            head_own,
            other_core(head_send),
            normed_first,
            inv_first,
            vectors,
            out_weight,
        ),
    )
    attn_got = other_core(attn_send)
    proj, input_own, input_send, payload = run_kernel(
        attn_back_kernel,
        "seg_attn_back",
        [
            shape_of((both_rows, 3 * HALF), LOW),
            shape_of((SEG, MODEL)),
            shape_of((SEG, MODEL)),
            shape_of((24, MODEL), LOW),
        ],
        where,
        (),
        (
            qkv,
            mixed_grad,
            attn_got,
            live_row,
            live_got,
            qkv_weight,
            first_sums,
            second_sums,
            up_sums,
            dheads,
            normed_second,
            head_data,
        ),
        [pltpu.VMEM((24, MODEL), WIDE)],
        flops=4 * SEG * MODEL * 3 * MODEL,
    )
    attn_data = (hidden_ordered, mixed_ordered, proj, branch, attn_got)
    attn_far = run_kernel(
        attn_far_kernel,
        "seg_attn_far",
        part_shapes(4 * HALF)[:2],
        where,
        (),
        attn_data,
        flops=SEG * MODEL * 2 * MODEL,
    )
    attn_far = reduce_far(tuple(after(part, mlp_got[-1]) for part in attn_far))
    attn_near = run_kernel(
        attn_near_kernel,
        "seg_attn_near",
        part_shapes(4 * HALF)[2:] + [shape_of((SEG, MODEL), LOW)],
        where,
        (),
        attn_data + (top_row, out_rows, live_row),
        flops=3 * SEG * MODEL * 2 * MODEL,
    )
    output = attn_near[3]
    *attn_sent, input_grad = run_kernel(
        attn_add_kernel,
        "seg_attn_add",
        [shape_of(attn_near[0].shape, LOW)] * 2 + [shape_of((SEG, MODEL), LOW)],
        where,
        (),
        attn_far
        + tuple(attn_near[:2])
        + (after(grad_summed, got_two), input_own, other_core(input_send)),
    )
    attn_plane = sent_both(*attn_sent)
    mlp_got[0] = along_line(after(mlp_last, *attn_sent), 1)
    payload_parts = line_parts(after(payload, mlp_got[0]))
    mlp_got = [after(got, attn_plane[0]) for got in mlp_got]
    mlp_sum = reduce_line(mlp_own, mlp_got)
    shared = shared + other_core(after(shared, attn_sent[0]))
    row_width = 8 * MODEL + 2 * FF
    cls_rows = run_kernel(
        cls_rows_kernel,
        "head_rows",
        [shape_of((GROUP, row_width), LOW)],
        where,
        (),
        (pack,) + tuple(mlp_got) + (heads, cls_branch, cls_low, cls_second),
        [pltpu.VMEM((LINE,) + pack.shape, LOW)],
    )[0]
    cls_got = other_core(cls_rows)
    attn_plane = tuple(after(got, output, input_grad, shared) for got in attn_plane)
    attn_own, *attn_sent = reduce_fold(where, attn_near[2], attn_plane)
    attn_lines = list(
        together(*(along_line(attn_sent[apart - 1], apart) for apart in range(1, LINE)))
    )
    flat = pltpu.VMEM((1, 8 * MODEL + FF), WIDE)
    payload_line = jnp.concatenate(payload_parts)
    mlp_mine, own_vecs, cls_mats_grad, cls_vec_grad, pos_total, loss_value = run_kernel(
        share_owner_kernel,
        "head_owner",
        [
            shape_of((own_rows, FF)),
            shape_of((16, MODEL)),
            shape_of((own_rows, total_columns)),
            shape_of((vec_size,)),
            shape_of((GROUP, MODEL)),
            shape_of((1, 1)),
        ],
        where,
        (),
        tuple(after(got, attn_own) for got in plane_parts(after(payload_line, *attn_plane)))
        + (mlp_sum, cls_rows, cls_got, shared, count),
        [
            pltpu.VMEM((GROUP * 24, MODEL), LOW),
            pltpu.VMEM((CORES * GROUP, row_width), LOW),
            flat,
        ],
        flops=64 * own_rows * total_columns,
    )
    loss_value = loss_value.reshape(())
    attn_lines = together(*(after(got, mlp_mine) for got in attn_lines))
    attn_sum = reduce_line(attn_own, attn_lines)
    seg_mats_grad, seg_vec_grad = run_kernel(
        store_kernel,
        "seg_owner",
        [shape_of((own_rows, total_columns)), shape_of((vec_size,))],
        where,
        (),
        (attn_sum, other_core(attn_sum), mlp_mine, other_core(mlp_mine))
        + (own_vecs, other_core(own_vecs)),
        [flat, pltpu.SemaphoreType.DMA((12,))],
        far=(0,),
    )

    return (
        output,
        input_grad,
        seg_mats_grad,
        seg_vec_grad,
        cls_mats_grad,
        cls_vec_grad,
        pos_total,
        loss_value,
    )


def solution(mesh):
    in_specs = (
        P(("rep", "fsdp"), None),
        P(("rep", "fsdp"), None),
        P(("rep", "fsdp")),
        P(("rep", "fsdp")),
        P(("rep", "fsdp")),
        P("fsdp", None),
        P("fsdp"),
        P("fsdp", None),
        P("fsdp"),
        P(),
    )
    out_specs = (
        P(("rep", "fsdp"), None),
        P(("rep", "fsdp"), None),
        P("fsdp", None),
        P("fsdp"),
        P("fsdp", None),
        P("fsdp"),
        P(),
        P(),
    )
    one_slice = dict(mesh.shape) == {"rep": CORES, "fsdp": LINE * PLANE}
    body = slice_local if one_slice else local
    return jax.shard_map(body, mesh=mesh, in_specs=in_specs, out_specs=out_specs, check_vma=False)
```

```python
import math

import jax
import jax.numpy as jnp
from jax import lax
from jax.experimental import pallas as pl
from jax.experimental.pallas import tpu as pltpu
from jax.sharding import PartitionSpec as P

HEADS = 12
HEAD_DIM = 64
FF = 3072
SEG = 128
SEQ = 2048


NORM_EPS = 1e-05
MASK_FILL = -1e30
SQRT_HALF = 0.7071067811865476
INV_SQRT_TWO_PI = 0.3989422804014327


def swapped(value, axis, apart):
    mask = 2**apart
    pairs = [(source, source ^ mask) for source in range(lax.axis_size(axis))]
    return lax.ppermute(value, axis, pairs)


def product_plain(left_side, right_side):
    return jnp.dot(left_side, right_side, preferred_element_type=jnp.float32)


def product_left(left_side, right_side):
    return lax.dot_general(
        left_side, right_side, (((0,), (0,)), ((), ())), preferred_element_type=jnp.float32
    )


def product_right(left_side, right_side):
    return lax.dot_general(
        left_side, right_side, (((1,), (1,)), ((), ())), preferred_element_type=jnp.float32
    )


def row_total(array_in):
    return jnp.sum(array_in.astype(jnp.float32), axis=0)


def unpack_weights(gathered, model_width, ff_width):
    matrix, vector = gathered
    vector = vector.astype(jnp.float32)
    pieces = tuple(
        (vector[offset * model_width : (offset + 1) * model_width] for offset in range(8))
    )
    return (
        (
            matrix[:, : 3 * model_width],
            matrix[:, 3 * model_width : 4 * model_width],
            matrix[:, 4 * model_width : 4 * model_width + ff_width],
            matrix[:, 4 * model_width + ff_width :],
        )
        + pieces
        + (vector[8 * model_width :],)
    )


def norm_forward(summed, gain_vec, shift_vec):
    row_mean = jnp.mean(summed, axis=-1, keepdims=True)
    centered = summed - row_mean
    inv_dev = lax.rsqrt(jnp.mean(centered * centered, axis=-1, keepdims=True) + NORM_EPS)
    normed = centered * inv_dev
    return (normed * gain_vec + shift_vec, normed, inv_dev)


def norm_backward(grad_out, normed, inv_dev, gain_vec):
    scaled = grad_out * gain_vec
    mean_one = jnp.mean(scaled, axis=-1, keepdims=True)
    mean_two = jnp.mean(scaled * normed, axis=-1, keepdims=True)
    grad_in = inv_dev * (scaled - mean_one - normed * mean_two)
    return (grad_in, jnp.sum(grad_out * normed, axis=0), jnp.sum(grad_out, axis=0))


def gelu_value(before):
    return 0.5 * before * (1.0 + lax.erf(before * SQRT_HALF))


def gelu_slope(before):
    return (
        0.5 * (1.0 + lax.erf(before * SQRT_HALF))
        + before * jnp.exp(-0.5 * before * before) * INV_SQRT_TWO_PI
    )


def attention_scores(queries, keys_in, allowed, score_scale):
    raw_scores = (
        jnp.einsum("bqhe,bkhe->bhqk", queries, keys_in, preferred_element_type=jnp.float32)
        * score_scale
    )
    return jnp.where(allowed, raw_scores, MASK_FILL)


def attention_forward(queries, keys_in, values, allowed, score_scale):
    scores = attention_scores(queries, keys_in, allowed, score_scale)
    row_top = jnp.max(scores, axis=-1, keepdims=True)
    log_total = row_top + jnp.log(jnp.sum(jnp.exp(scores - row_top), axis=-1, keepdims=True))
    weights = jnp.exp(scores - log_total).astype(jnp.bfloat16)
    mixed_rows = jnp.einsum("bhqk,bkhe->bqhe", weights, values, preferred_element_type=jnp.float32)
    return (mixed_rows, log_total)


def attention_backward(queries, keys_in, values, allowed, score_scale, log_total, grad_mixed):
    probabilities = jnp.exp(attention_scores(queries, keys_in, allowed, score_scale) - log_total)
    grad_probs = jnp.einsum(
        "bqhe,bkhe->bhqk", grad_mixed, values, preferred_element_type=jnp.float32
    )
    inner_sum = jnp.sum(grad_probs * probabilities, axis=-1, keepdims=True)
    grad_scores = (probabilities * (grad_probs - inner_sum)).astype(jnp.bfloat16)
    grad_query = (
        jnp.einsum("bhqk,bkhe->bqhe", grad_scores, keys_in, preferred_element_type=jnp.float32)
        * score_scale
    )
    grad_key = (
        jnp.einsum("bhqk,bqhe->bkhe", grad_scores, queries, preferred_element_type=jnp.float32)
        * score_scale
    )
    grad_value = jnp.einsum(
        "bhqk,bqhe->bkhe",
        probabilities.astype(jnp.bfloat16),
        grad_mixed,
        preferred_element_type=jnp.float32,
    )
    return (grad_query, grad_key, grad_value)


def block_forward(rows_in, unpacked, attend):
    (
        qkv_weight,
        out_weight,
        up_weight,
        down_weight,
        query_bias,
        value_bias,
        out_bias,
        down_bias,
        gain_first,
        shift_first,
        gain_second,
        shift_second,
        up_bias,
    ) = unpacked
    model_width = rows_in.shape[1]
    inputs = rows_in.astype(jnp.bfloat16)
    projected = product_plain(inputs, qkv_weight)
    queries = (projected[:, :model_width] + query_bias).astype(jnp.bfloat16)
    keys_in = projected[:, model_width : 2 * model_width].astype(jnp.bfloat16)
    values = (projected[:, 2 * model_width :] + value_bias).astype(jnp.bfloat16)
    mixed_rows, attend_kept = attend(queries, keys_in, values)
    mixed_rows = mixed_rows.astype(jnp.bfloat16)
    summed_first = rows_in + product_plain(mixed_rows, out_weight) + out_bias
    first_out, normed_first, inv_first = norm_forward(summed_first, gain_first, shift_first)
    first_low = first_out.astype(jnp.bfloat16)
    pre_act = product_plain(first_low, up_weight) + up_bias
    activated = gelu_value(pre_act).astype(jnp.bfloat16)
    summed_second = first_out + product_right(activated, down_weight) + down_bias
    block_out, normed_second, inv_second = norm_forward(summed_second, gain_second, shift_second)
    saved_state = (
        inputs,
        queries,
        keys_in,
        values,
        attend_kept,
        mixed_rows,
        normed_first,
        inv_first,
        first_low,
        pre_act,
        activated,
        normed_second,
        inv_second,
    )
    return (block_out, saved_state)


def block_backward(grad_out, unpacked, saved_state, attend_back):
    (
        qkv_weight,
        out_weight,
        up_weight,
        down_weight,
        query_bias,
        value_bias,
        out_bias,
        down_bias,
        gain_first,
        shift_first,
        gain_second,
        shift_second,
        up_bias,
    ) = unpacked
    (
        inputs,
        queries,
        keys_in,
        values,
        attend_kept,
        mixed_rows,
        normed_first,
        inv_first,
        first_low,
        pre_act,
        activated,
        normed_second,
        inv_second,
    ) = saved_state
    grad_second, grad_gain_second, grad_shift_second = norm_backward(
        grad_out, normed_second, inv_second, gain_second
    )
    second_low = grad_second.astype(jnp.bfloat16)
    grad_pre = (product_plain(second_low, down_weight) * gelu_slope(pre_act)).astype(jnp.bfloat16)
    grad_first = grad_second + product_right(grad_pre, up_weight)
    grad_summed, grad_gain_first, grad_shift_first = norm_backward(
        grad_first, normed_first, inv_first, gain_first
    )
    branch_low = grad_summed.astype(jnp.bfloat16)
    grad_mixed = product_right(branch_low, out_weight).astype(jnp.bfloat16)
    grad_query, grad_key, grad_value = attend_back(
        queries, keys_in, values, attend_kept, grad_mixed
    )
    grad_proj = jnp.concatenate([grad_query, grad_key, grad_value], axis=1)
    grad_rows = grad_summed + product_right(grad_proj, qkv_weight)
    vector_grad = jnp.concatenate(
        [
            row_total(grad_query),
            row_total(grad_value),
            row_total(branch_low),
            row_total(second_low),
            grad_gain_first,
            grad_shift_first,
            grad_gain_second,
            grad_shift_second,
            row_total(grad_pre),
        ]
    )
    weight_rows = (
        inputs,
        grad_proj,
        mixed_rows,
        branch_low,
        first_low,
        grad_pre,
        second_low,
        activated,
    )
    return (grad_rows, weight_rows, vector_grad)


def weight_products(weight_rows):
    inputs, grad_proj, mixed_rows, branch_low, first_low, grad_pre, second_low, activated = (
        weight_rows
    )
    return (
        product_left(inputs, grad_proj),
        product_left(mixed_rows, branch_low),
        product_left(first_low, grad_pre),
        product_left(second_low, activated),
    )


def local(
    hidden_in,
    targets,
    doc_ids,
    seg_nums,
    valid_flags,
    seg_mats,
    seg_vecs,
    cls_mats,
    cls_vecs,
    seg_pos,
):
    tok_rows, model_width = hidden_in.shape
    ff_width = FF
    seg_len = SEG
    group_span = SEQ // tok_rows
    seg_count = tok_rows // seg_len
    score_scale = HEAD_DIM ** (-0.5)
    head_shape = (HEADS, HEAD_DIM)
    live_rows = valid_flags.astype(jnp.float32)
    rank_full = lax.axis_index("fsdp")
    seg_gathered = (
        lax.all_gather(seg_mats, "fsdp", axis=0, tiled=True),
        lax.all_gather(seg_vecs, "fsdp", axis=0, tiled=True),
    )
    seg_unpacked = unpack_weights(seg_gathered, model_width, ff_width)
    cls_gathered = (
        lax.all_gather(cls_mats, "fsdp", axis=0, tiled=True),
        lax.all_gather(cls_vecs, "fsdp", axis=0, tiled=True),
    )
    cls_unpacked = unpack_weights(cls_gathered, model_width, ff_width)
    seg_allowed = (live_rows.reshape(seg_count, 1, 1, seg_len) > 0.5) | jnp.eye(seg_len, dtype=bool)
    seg_shape = (seg_count, seg_len) + head_shape

    def seg_attend(queries, keys_in, values):
        mixed_rows, log_total = attention_forward(
            queries.reshape(seg_shape),
            keys_in.reshape(seg_shape),
            values.reshape(seg_shape),
            seg_allowed,
            score_scale,
        )
        return (mixed_rows.reshape(tok_rows, model_width), log_total)

    def seg_attend_back(queries, keys_in, values, log_total, grad_mixed):
        grad_parts = attention_backward(
            queries.reshape(seg_shape),
            keys_in.reshape(seg_shape),
            values.reshape(seg_shape),
            seg_allowed,
            score_scale,
            log_total,
            grad_mixed.reshape(seg_shape),
        )
        return tuple(
            (
                grad_part.reshape(tok_rows, model_width).astype(jnp.bfloat16)
                for grad_part in grad_parts
            )
        )

    first_out, seg_saved = block_forward(hidden_in.astype(jnp.float32), seg_unpacked, seg_attend)
    first_grid = first_out.reshape(seg_count, seg_len, model_width)
    position_hot = (seg_nums[:, None] == jnp.arange(seg_pos.shape[0])[None, :]).astype(jnp.float32)
    position_rows = jnp.sum(
        position_hot[:, :, None] * seg_pos.astype(jnp.float32)[None, :, :], axis=1
    )
    heads_in = first_grid[:, 0, :] + position_rows
    lead_live = live_rows.reshape(seg_count, seg_len)[:, 0]
    lead_doc = doc_ids.reshape(seg_count, seg_len)[:, 0]
    lead_labels = jnp.where(lead_live > 0.5, lead_doc, -1).astype(jnp.bfloat16)
    lead_doc_low = lead_doc.astype(jnp.bfloat16)
    bit_count = group_span.bit_length() - 1
    key_total = group_span * seg_count
    own_slot = rank_full % group_span * seg_count + jnp.arange(seg_count)
    query_shape = (1, seg_count) + head_shape
    key_shape = (1, key_total) + head_shape

    def cls_attend(queries, keys_in, values):
        paired = jnp.concatenate([keys_in, values], axis=1)
        labels = lead_labels
        for bit_level in range(bit_count):
            other_pair, other_labels = swapped((paired, labels), "fsdp", bit_level)
            upper_half = rank_full // (1 << bit_level) % 2 == 1
            paired = jnp.where(
                upper_half,
                jnp.concatenate([other_pair, paired]),
                jnp.concatenate([paired, other_pair]),
            )
            labels = jnp.where(
                upper_half,
                jnp.concatenate([other_labels, labels]),
                jnp.concatenate([labels, other_labels]),
            )
        allowed = (labels[None, :] == lead_doc_low[:, None]) | (
            jnp.arange(key_total)[None, :] == own_slot[:, None]
        )
        allowed = allowed[None, None]
        mixed_rows, log_total = attention_forward(
            queries.reshape(query_shape),
            paired[:, :model_width].reshape(key_shape),
            paired[:, model_width:].reshape(key_shape),
            allowed,
            score_scale,
        )
        return (mixed_rows.reshape(seg_count, model_width), (paired, allowed, log_total))

    def cls_attend_back(queries, keys_in, values, attend_kept, grad_mixed):
        paired, allowed, log_total = attend_kept
        grad_query, grad_key, grad_value = attention_backward(
            queries.reshape(query_shape),
            paired[:, :model_width].reshape(key_shape),
            paired[:, model_width:].reshape(key_shape),
            allowed,
            score_scale,
            log_total,
            grad_mixed.reshape(query_shape),
        )
        grad_pair = jnp.concatenate(
            [grad_key.reshape(key_total, model_width), grad_value.reshape(key_total, model_width)],
            axis=1,
        )
        for bit_level in reversed(range(bit_count)):
            half_rows = grad_pair.shape[0] // 2
            upper_half = rank_full // (1 << bit_level) % 2 == 1
            kept_half = jnp.where(upper_half, grad_pair[half_rows:], grad_pair[:half_rows])
            sent_half = jnp.where(upper_half, grad_pair[:half_rows], grad_pair[half_rows:])
            grad_pair = kept_half + swapped(
                sent_half.astype(jnp.bfloat16), "fsdp", bit_level
            ).astype(sent_half.dtype)
        grad_pair = grad_pair.astype(jnp.bfloat16)
        return (
            grad_query.reshape(seg_count, model_width).astype(jnp.bfloat16),
            grad_pair[:, :model_width],
            grad_pair[:, model_width:],
        )

    top_out, cls_saved = block_forward(heads_in, cls_unpacked, cls_attend)
    combined = jnp.concatenate([top_out[:, None, :], first_grid[:, 1:, :]], axis=1).reshape(
        tok_rows, model_width
    )
    output_rows = combined * live_rows[:, None]
    diff_rows = (output_rows - targets.astype(jnp.float32)) * live_rows[:, None]
    count_all, square_all = lax.psum(
        (jnp.sum(live_rows), jnp.sum(diff_rows * diff_rows)), ("rep", "fsdp")
    )
    loss_value = square_all / (count_all * model_width)
    slots_all = tok_rows * lax.axis_size("rep") * lax.axis_size("fsdp")
    grad_grid = (diff_rows * (slots_all / count_all)).reshape(seg_count, seg_len, model_width)
    cls_back = unpack_weights(
        (
            lax.all_gather(cls_mats, "fsdp", axis=0, tiled=True),
            lax.all_gather(cls_vecs, "fsdp", axis=0, tiled=True),
        ),
        model_width,
        ff_width,
    )
    heads_grad, cls_weight_rows, cls_g_vec = block_backward(
        grad_grid[:, 0, :], cls_back, cls_saved, cls_attend_back
    )
    cls_g_qkv, cls_g_out, cls_g_up, cls_g_down = weight_products(cls_weight_rows)
    pos_local = jnp.sum(position_hot[:, :, None] * heads_grad[:, None, :], axis=0)
    seg_grad_out = jnp.concatenate([heads_grad[:, None, :], grad_grid[:, 1:, :]], axis=1).reshape(
        tok_rows, model_width
    )
    seg_back = unpack_weights(
        (
            lax.all_gather(seg_mats, "fsdp", axis=0, tiled=True),
            lax.all_gather(seg_vecs, "fsdp", axis=0, tiled=True),
        ),
        model_width,
        ff_width,
    )
    input_grad, seg_weight_rows, seg_g_vec = block_backward(
        seg_grad_out, seg_back, seg_saved, seg_attend_back
    )
    seg_g_qkv, seg_g_out, seg_g_up, seg_g_down = weight_products(seg_weight_rows)
    owner_rows = tuple(
        (
            lax.psum_scatter(seg_g_qkv, "fsdp", scatter_dimension=0, tiled=True),
            lax.psum_scatter(seg_g_out, "fsdp", scatter_dimension=0, tiled=True),
            lax.psum_scatter(seg_g_up, "fsdp", scatter_dimension=0, tiled=True),
            lax.psum_scatter(seg_g_down, "fsdp", scatter_dimension=0, tiled=True),
            lax.psum_scatter(seg_g_vec, "fsdp", scatter_dimension=0, tiled=True),
            lax.psum_scatter(cls_g_qkv, "fsdp", scatter_dimension=0, tiled=True),
            lax.psum_scatter(cls_g_out, "fsdp", scatter_dimension=0, tiled=True),
            lax.psum_scatter(cls_g_up, "fsdp", scatter_dimension=0, tiled=True),
            lax.psum_scatter(cls_g_down, "fsdp", scatter_dimension=0, tiled=True),
            lax.psum_scatter(cls_g_vec, "fsdp", scatter_dimension=0, tiled=True),
        )
    )
    replica_share = (
        lax.psum_scatter(
            owner_rows[0].astype(jnp.bfloat16), "rep", scatter_dimension=1, tiled=True
        ).astype(jnp.float32),
        lax.psum_scatter(
            owner_rows[1].astype(jnp.bfloat16), "rep", scatter_dimension=1, tiled=True
        ).astype(jnp.float32),
        lax.psum_scatter(
            owner_rows[2].astype(jnp.bfloat16), "rep", scatter_dimension=1, tiled=True
        ).astype(jnp.float32),
        lax.psum_scatter(
            owner_rows[3].astype(jnp.bfloat16), "rep", scatter_dimension=1, tiled=True
        ).astype(jnp.float32),
        lax.psum_scatter(
            owner_rows[4].astype(jnp.bfloat16), "rep", scatter_dimension=0, tiled=True
        ).astype(jnp.float32),
        lax.psum_scatter(
            owner_rows[5].astype(jnp.bfloat16), "rep", scatter_dimension=1, tiled=True
        ).astype(jnp.float32),
        lax.psum_scatter(
            owner_rows[6].astype(jnp.bfloat16), "rep", scatter_dimension=1, tiled=True
        ).astype(jnp.float32),
        lax.psum_scatter(
            owner_rows[7].astype(jnp.bfloat16), "rep", scatter_dimension=1, tiled=True
        ).astype(jnp.float32),
        lax.psum_scatter(
            owner_rows[8].astype(jnp.bfloat16), "rep", scatter_dimension=1, tiled=True
        ).astype(jnp.float32),
        lax.psum_scatter(
            owner_rows[9].astype(jnp.bfloat16), "rep", scatter_dimension=0, tiled=True
        ).astype(jnp.float32),
    )
    all_summed = (
        lax.all_gather(replica_share[0].astype(jnp.bfloat16), "rep", axis=1, tiled=True).astype(
            jnp.float32
        ),
        lax.all_gather(replica_share[1].astype(jnp.bfloat16), "rep", axis=1, tiled=True).astype(
            jnp.float32
        ),
        lax.all_gather(replica_share[2].astype(jnp.bfloat16), "rep", axis=1, tiled=True).astype(
            jnp.float32
        ),
        lax.all_gather(replica_share[3].astype(jnp.bfloat16), "rep", axis=1, tiled=True).astype(
            jnp.float32
        ),
        lax.all_gather(replica_share[4].astype(jnp.bfloat16), "rep", axis=0, tiled=True).astype(
            jnp.float32
        ),
        lax.all_gather(replica_share[5].astype(jnp.bfloat16), "rep", axis=1, tiled=True).astype(
            jnp.float32
        ),
        lax.all_gather(replica_share[6].astype(jnp.bfloat16), "rep", axis=1, tiled=True).astype(
            jnp.float32
        ),
        lax.all_gather(replica_share[7].astype(jnp.bfloat16), "rep", axis=1, tiled=True).astype(
            jnp.float32
        ),
        lax.all_gather(replica_share[8].astype(jnp.bfloat16), "rep", axis=1, tiled=True).astype(
            jnp.float32
        ),
        lax.all_gather(replica_share[9].astype(jnp.bfloat16), "rep", axis=0, tiled=True).astype(
            jnp.float32
        ),
    )
    seg_summed = all_summed[:5]
    cls_summed = all_summed[5:]
    pos_total = lax.psum(pos_local, ("rep", "fsdp"))
    seg_mat_grad = jnp.concatenate(
        [seg_summed[0], seg_summed[1], seg_summed[2], seg_summed[3]], axis=1
    )
    cls_mat_grad = jnp.concatenate(
        [cls_summed[0], cls_summed[1], cls_summed[2], cls_summed[3]], axis=1
    )
    return (
        output_rows.astype(jnp.bfloat16),
        input_grad.astype(jnp.bfloat16),
        seg_mat_grad,
        seg_summed[4],
        cls_mat_grad,
        cls_summed[4],
        pos_total,
        loss_value,
    )


LINE = 4
PLANE = 4
CORES = 2
LANES = 128
GROUP = LINE * PLANE
LOW, WIDE = jnp.bfloat16, jnp.float32
MODEL = HEADS * HEAD_DIM
SPAN = 2 * LANES
TILE_START = (0, 1, 3, 4)


def line_pairs(apart):
    return [(source, (source + apart * PLANE) % GROUP) for source in range(GROUP)]


def plane_pairs(mask):
    return [(source, source ^ mask) for source in range(GROUP)]


def along_line(value, apart):
    return lax.ppermute(value, "fsdp", line_pairs(apart))


def in_plane(value, mask):
    return lax.ppermute(value, "fsdp", plane_pairs(mask))


def other_core(value):
    return lax.ppermute(value, "rep", [(0, 1), (1, 0)])


def after(value, *events):
    return lax.optimization_barrier((value,) + events)[0]


def together(*values):
    return tuple(lax.optimization_barrier(values))


def shape_of(dims, dtype=WIDE):
    return jax.ShapeDtypeStruct(dims, dtype)


def run_kernel(body, name, outs, where, blocks, arrays, scratch=(), far=(), flops=0):
    in_specs = [pl.BlockSpec(memory_space=pltpu.SMEM)]
    in_specs += [pl.BlockSpec(memory_space=pltpu.HBM)] * len(blocks)
    in_specs += [pl.BlockSpec(memory_space=pltpu.VMEM)] * len(arrays)
    spaces = [pltpu.HBM if at in far else pltpu.VMEM for at in range(len(outs))]
    moved = sum(x.size * x.dtype.itemsize for x in list(blocks) + list(arrays))
    moved += sum(math.prod(o.shape) * jnp.dtype(o.dtype).itemsize for o in outs)
    return pl.pallas_call(
        body,
        name=name,
        out_shape=tuple(outs),
        in_specs=in_specs,
        out_specs=tuple(pl.BlockSpec(memory_space=space) for space in spaces),
        scratch_shapes=list(scratch),
        cost_estimate=pl.CostEstimate(flops=flops, bytes_accessed=moved, transcendentals=0),
        compiler_params=pltpu.CompilerParams(vmem_limit_bytes=VMEM_BYTES),
    )(where, *blocks, *arrays)


VMEM_BYTES = 24 * 1024 * 1024
HALF = MODEL // CORES
FF_HALF = FF // CORES
OWN = MODEL // GROUP
QUARTER = 3 * SPAN + 2 * FF // LINE
QUARTER_HALF = QUARTER // CORES


def aligned(start):
    return pl.multiple_of(start, LANES)


def wait_all(copies):
    for copy in copies:
        copy.wait()


def run_copies(pairs, sems):
    copies = [
        pltpu.make_async_copy(source, target, sems.at[at])
        for at, (source, target) in enumerate(pairs)
    ]
    for copy in copies:
        copy.start()
    wait_all(copies)


FIRST = 4 * HALF + LANES
OWN_CUT = FIRST + FF_HALF // 2
LINE_CUTS = (7 * LANES, FF_HALF // 2, FF_HALF // 2)
WIDTHS = (FIRST, FF_HALF, FF_HALF)


def group_pieces(group, refs):
    own, rest = refs[:LINE], refs[LINE:]
    own_x, own_y, far_x, far_y, line_x, line_y, late_x, late_y = rest
    width, cut = WIDTHS[group], LINE_CUTS[group]
    start = sum(WIDTHS[:group])
    if group == 0:
        bases = (sum(WIDTHS) - OWN_CUT, OWN_CUT)
    else:
        before, before_cut = WIDTHS[group - 1], LINE_CUTS[group - 1]
        bases = (2 * before - before_cut, before + before_cut)
    pieces = {(0, step): [(own[step], 0, 0, width)] for step in range(LINE)}
    for mask, whole, line, base in ((1, own_x, line_x, bases[0]), (2, own_y, line_y, bases[1])):
        pieces[mask, 0] = [(whole, start, 0, width)]
        for step in range(1, LINE):
            pieces[mask, step] = [(line, base + (step - 1) * width, 0, width)]
    middle = min(max(OWN_CUT - start, 0), width)
    far = []
    if middle > 0:
        far.append((far_y, start, 0, middle))
    if middle < width:
        far.append((far_x, start + middle - OWN_CUT, middle, width))
    pieces[3, 0] = far
    pieces[3, 1] = [(late_y, 0, 0, width)]
    pieces[3, 2] = [(late_y, width, 0, cut), (late_x, 0, cut, width)]
    pieces[3, 3] = [(late_x, width - cut, 0, width)]
    return pieces


def gather_group(where, group, refs, targets):
    line_at, plane_at = where[0], where[1]
    for (mask, step), parts in group_pieces(group, refs).items():
        chip = (line_at + LINE - step) % LINE * PLANE + (plane_at ^ mask)
        for whole, first, last in targets:
            for ref, offset, begin, end in parts:
                low, high = max(first, begin), min(last, end)
                if low < high:
                    source = slice(offset + low - begin, offset + high - begin)
                    whole[chip, :, low - first : high - first] = ref[:, source]


def gather_blocks(where, refs, base, width, targets):
    line_at, plane_at = where[0], where[1]
    half = LINE // 2
    for mask in range(PLANE):
        for step in range(LINE):
            if mask == 0:
                ref, offset = refs[step], 0
            elif mask == 3:
                ref = refs[LINE + 3] if step < half else refs[LINE + 2]
                offset = step % half * width
            else:
                ref, offset = refs[LINE + mask - 1], base + step * width
            chip = (line_at + LINE - step) % LINE * PLANE + (plane_at ^ mask)
            for whole, first, last in targets:
                whole[chip] = ref[:, offset + first : offset + last]


def whole_rows(ref):
    value = ref[...]
    return value.reshape(value.shape[0] * value.shape[1], value.shape[2])


def prepare_first_kernel(where, seg, seg_vec, cls_vec, flags, out, live_out, sems):
    core_at = where[2]
    pairs = []
    for piece in range(4):
        source = seg.at[:, pl.ds(aligned(piece * MODEL + core_at * HALF), HALF)]
        pairs.append((source, out.at[:, piece * HALF : (piece + 1) * HALF]))
    run_copies(pairs, sems)
    size = seg_vec.shape[0]
    vecs = [vec[...].astype(WIDE).reshape(1, size) for vec in (seg_vec, cls_vec)]
    lines = -(-size // LANES)
    block = jnp.zeros((OWN, LANES), WIDE)
    row_at = lax.broadcasted_iota(jnp.int32, (OWN, LANES), 0)
    for which in range(2):
        for line in range(lines):
            width = min(LANES, size - line * LANES)
            value = vecs[which][:, line * LANES : line * LANES + width]
            if width < LANES:
                value = jnp.concatenate([value, jnp.zeros((1, LANES - width), WIDE)], axis=1)
            block = jnp.where(row_at == which * lines + line, value, block)
    live = flags[...].astype(WIDE).reshape(1, SEG)
    live_out[...] = live
    count = jnp.sum(live, axis=1, keepdims=True)
    block = jnp.where(row_at == 2 * lines, count, block)
    out[:, 4 * HALF :] = block.astype(LOW)


def prepare_rest_kernel(where, seg, cls, *refs):
    second_out, third_out = refs[:2]
    step_outs, out_half, order_out = refs[2 : 2 + LINE], refs[2 + LINE], refs[3 + LINE]
    quarters, sems = refs[4 + LINE :]
    line_at, plane_at, core_at = where[0], where[1], where[2]
    start = core_at * FF_HALF
    pairs = [
        (seg.at[:, pl.ds(aligned(4 * MODEL + start), FF_HALF)], second_out),
        (seg.at[:, pl.ds(aligned(4 * MODEL + FF + start), FF_HALF)], third_out),
        (cls.at[:, pl.ds(aligned(3 * MODEL + core_at * HALF), HALF)], out_half),
    ]
    part = FF // LINE
    for at in range(LINE):
        first = TILE_START[at] * LANES
        plan = [(piece * MODEL + first, SPAN, piece * SPAN) for piece in range(3)]
        plan += [
            (4 * MODEL + piece * FF + at * part, part, 3 * SPAN + piece * part)
            for piece in range(2)
        ]
        for source, size, target in plan:
            pairs.append(
                (
                    cls.at[:, source : source + size],
                    quarters.at[at, :, target : target + size],
                )
            )
    run_copies(pairs, sems)
    lanes = pl.ds(aligned(core_at * QUARTER_HALF), QUARTER_HALF)
    for step, out in enumerate(step_outs):
        out[...] = quarters[(line_at + step) % LINE, :, lanes]
    column = lax.broadcasted_iota(jnp.int32, (1, SPAN), 1)
    feature = lax.broadcasted_iota(jnp.int32, (MODEL, SPAN), 0)
    turn = sum((column >= OWN * step).astype(jnp.int32) for step in range(1, LINE))
    held = column - OWN * turn
    turn = (line_at + turn) % LINE
    for mask in range(PLANE):
        source = (turn * PLANE + (plane_at ^ mask)) * OWN + held
        source = jnp.where(column < OWN * LINE, source, -1)
        order_out[:, mask * SPAN : (mask + 1) * SPAN] = (feature == source).astype(LOW)


def prepare_kernel(where, seg, cls, *refs):
    (seg_vec, cls_vec, flags, first_out, live_out), refs = refs[:5], refs[5:]
    rest, (first_sems, quarters, sems) = refs[:-3], refs[-3:]
    prepare_first_kernel(where, seg, seg_vec, cls_vec, flags, first_out, live_out, first_sems)
    prepare_rest_kernel(where, seg, cls, *rest, quarters, sems)


def lane_mask(rows, head):
    lane = lax.broadcasted_iota(jnp.int32, (rows, LANES), 1)
    return (lane < HEAD_DIM) if head == 0 else (lane >= HEAD_DIM)


def masked(value, mask):
    return jnp.where(mask, value, jnp.zeros_like(value))


def head_probabilities(query, key, allowed):
    scores = product_right(query, key) * HEAD_DIM ** (-0.5)
    scores = jnp.where(allowed, scores, MASK_FILL)
    raised = jnp.exp(scores - jnp.max(scores, axis=-1, keepdims=True))
    return raised / jnp.sum(raised, axis=-1, keepdims=True)


def attend_tiles(qkv, width, allowed):
    rows = qkv.shape[0]
    mixed = []
    for tile in range(width // LANES):
        at = tile * LANES
        query, key, value = (
            qkv[:, piece * width + at : piece * width + at + LANES] for piece in range(3)
        )
        total = jnp.zeros((rows, LANES), WIDE)
        for head in range(2):
            mask = lane_mask(rows, head)
            weights = head_probabilities(masked(query, mask), key, allowed).astype(LOW)
            total = total + product_plain(weights, masked(value, mask))
        mixed.append(total.astype(LOW))
    return mixed


def attend_tiles_back(qkv, grad_mixed, width, allowed):
    rows = qkv.shape[0]
    scale = HEAD_DIM ** (-0.5)
    results = ([], [], [])
    for tile in range(width // LANES):
        at = tile * LANES
        query, key, value = (
            qkv[:, piece * width + at : piece * width + at + LANES] for piece in range(3)
        )
        grad = grad_mixed[:, at : at + LANES]
        totals = [jnp.zeros((rows, LANES), WIDE) for _ in range(3)]
        for head in range(2):
            mask = lane_mask(rows, head)
            query_low, key_low, grad_low = (masked(x, mask) for x in (query, key, grad))
            chance = head_probabilities(query_low, key, allowed)
            grad_chance = product_right(grad_low, value)
            inner = jnp.sum(grad_chance * chance, axis=-1, keepdims=True)
            grad_scores = (chance * (grad_chance - inner)).astype(LOW)
            totals[0] = totals[0] + product_plain(grad_scores, key_low)
            totals[1] = totals[1] + product_left(grad_scores, query_low)
            totals[2] = totals[2] + product_left(chance.astype(LOW), grad_low)
        results[0].append((totals[0] * scale).astype(LOW))
        results[1].append((totals[1] * scale).astype(LOW))
        results[2].append(totals[2].astype(LOW))
    return results[0] + results[1] + results[2]


def token_allowed(live_row):
    shape = (SEG, SEG)
    same = lax.broadcasted_iota(jnp.int32, shape, 0) == lax.broadcasted_iota(jnp.int32, shape, 1)
    return (live_row > 0.5) | same


def qkv_kernel(where, *refs):
    blocks = refs[:12]
    hidden, hidden_got, live_row, live_got, order = refs[12:17]
    weight, out_low, out_high, qkv_out, mixed_out = refs[17:22]
    vectors_out, count_out, ordered_out = refs[22:25]
    vec_rows, flat, inputs, out_half = refs[25:]
    core_at = where[2]
    gather_group(
        where,
        0,
        blocks,
        (
            (weight, 0, 3 * HALF),
            (out_half, 3 * HALF, 4 * HALF),
            (vec_rows, 4 * HALF, 4 * HALF + LANES),
        ),
    )
    out_low[...] = out_half[: GROUP // 2]
    out_high[...] = out_half[GROUP // 2 :]
    piece = (8 * MODEL + FF) // GROUP
    lines = -(-piece // LANES)
    count = jnp.zeros((1, LANES), WIDE)
    for chip in range(GROUP):
        rows = vec_rows[chip, 0:16, :].astype(WIDE)
        for block in range(2):
            joined = jnp.concatenate(
                [rows[block * lines + r : block * lines + r + 1] for r in range(lines)], axis=1
            )
            flat[block : block + 1, chip * piece : (chip + 1) * piece] = joined[:, :piece]
        count = count + rows[2 * lines : 2 * lines + 1]
    rows_each = (8 * MODEL + FF) // MODEL
    for block in range(2):
        for row in range(rows_each):
            vectors_out[block * rows_each + row : block * rows_each + row + 1, :] = flat[
                block : block + 1, row * MODEL : (row + 1) * MODEL
            ]
    count_out[...] = jnp.broadcast_to(count, count_out.shape)
    inputs[:SEG] = hidden[...]
    inputs[SEG:] = hidden_got[...]
    projected = product_plain(inputs[...], whole_rows(weight))
    lanes = pl.ds(aligned(core_at * HALF), HALF)
    qkv_out[:, :HALF] = (projected[:, :HALF] + vectors_out[0:1, lanes]).astype(LOW)
    qkv_out[:, HALF : 2 * HALF] = projected[:, HALF : 2 * HALF].astype(LOW)
    qkv_out[:, 2 * HALF :] = (projected[:, 2 * HALF :] + vectors_out[1:2, lanes]).astype(LOW)
    for part, live in enumerate((live_row, live_got)):
        rows = slice(part * SEG, (part + 1) * SEG)
        tiles = attend_tiles(qkv_out[rows, :], HALF, token_allowed(live[...]))
        for tile, value in enumerate(tiles):
            mixed_out[rows, tile * LANES : (tile + 1) * LANES] = value
    ordered_out[...] = product_plain(inputs[...], order[...]).astype(LOW)


def norm_rows(summed):
    row_mean = jnp.mean(summed, axis=-1, keepdims=True)
    centered = summed - row_mean
    inv_dev = lax.rsqrt(jnp.mean(centered * centered, axis=-1, keepdims=True) + NORM_EPS)
    return centered * inv_dev, inv_dev


def norm_rows_back(grad_out, normed, inv_dev, gain):
    scaled = grad_out * gain
    mean_one = jnp.mean(scaled, axis=-1, keepdims=True)
    mean_two = jnp.mean(scaled * normed, axis=-1, keepdims=True)
    return inv_dev * (scaled - mean_one - normed * mean_two)


def column_sum(value):
    return jnp.sum(value.astype(WIDE), axis=0, keepdims=True)


def four_rows(vectors, first):
    return jnp.concatenate([vectors[first + at : first + at + 1, :] for at in range(4)], axis=1)


def gelu_both(before):
    half = 0.5 * (1.0 + lax.erf(before * SQRT_HALF))
    slope = half + before * jnp.exp(-0.5 * before * before) * INV_SQRT_TWO_PI
    return before * half, slope


def out_kernel(where, hidden, mixed, mixed_got, low, high, low_got, high_got, *refs):
    vectors, order, full_out, ordered_out, normed_out, inv_out, low_out, mixed_full = refs
    core_at = where[2]
    own, other = aligned(core_at * HALF), aligned((1 - core_at) * HALF)
    rows = MODEL // 2
    full_out[:rows, pl.ds(own, HALF)] = whole_rows(low)
    full_out[rows:, pl.ds(own, HALF)] = whole_rows(high)
    full_out[:rows, pl.ds(other, HALF)] = whole_rows(low_got)
    full_out[rows:, pl.ds(other, HALF)] = whole_rows(high_got)
    mixed_full[:, pl.ds(own, HALF)] = mixed[...]
    mixed_full[:SEG, pl.ds(other, HALF)] = mixed_got[SEG:, :]
    mixed_full[SEG:, pl.ds(other, HALF)] = mixed_got[:SEG, :]
    branch = product_plain(mixed_full[:SEG, :], full_out[...])
    normed, inv_dev = norm_rows(hidden[...].astype(WIDE) + branch + vectors[2:3, :])
    normed_out[...] = normed
    inv_out[...] = inv_dev
    low_out[...] = (normed * vectors[4:5, :] + vectors[5:6, :]).astype(LOW)
    ordered_out[...] = product_plain(mixed_full[...], order[...]).astype(LOW)


def up_kernel(where, *refs):
    blocks = refs[:12]
    low, low_got, vectors = refs[12:15]
    weight, act_out, slope_out, both = refs[15:]
    core_at = where[2]
    gather_group(where, 1, blocks, ((weight, 0, FF_HALF),))
    both[:SEG] = low[...]
    both[SEG:] = low_got[...]
    for at in range(FF_HALF // MODEL):
        columns = slice(at * MODEL, (at + 1) * MODEL)
        held = weight[:, :, columns]
        before = product_plain(both[...], held.reshape(MODEL, MODEL))
        bias = vectors[pl.ds(8 + core_at * (FF_HALF // MODEL) + at, 1), :]
        value, slope = gelu_both(before + bias)
        act_out[:, columns] = value.astype(LOW)
        slope_out[:, columns] = slope


def down_kernel(where, *refs):
    blocks, act = refs[:12], refs[12]
    weight, own_out, send_out = refs[13:]
    gather_group(where, 2, blocks, ((weight, 0, FF_HALF),))
    partial = product_right(act[...], whole_rows(weight))
    own_out[...] = partial[:SEG]
    send_out[...] = partial[SEG:]


def seg_rows_kernel(where, *refs):
    own, got, normed_first, vectors, targets, live, seg_pos = refs[:7]
    normed_out, inv_out, diff_out, rows_out, head_out = refs[7:]
    doc, number = where[3], where[4]
    first = normed_first[...] * vectors[4:5, :] + vectors[5:6, :]
    normed, inv_dev = norm_rows(first + own[...] + got[...] + vectors[3:4, :])
    normed_out[...] = normed
    inv_out[...] = inv_dev
    rows = normed * vectors[6:7, :] + vectors[7:8, :]
    shape = (SEG, SEG)
    same = lax.broadcasted_iota(jnp.int32, shape, 0) == lax.broadcasted_iota(jnp.int32, shape, 1)
    live_rows = jnp.sum(jnp.where(same, live[...], 0.0), axis=1, keepdims=True)
    target_rows = targets[...].astype(WIDE)
    output = rows * live_rows
    rows_out[...] = output
    diff = (output - target_rows) * live_rows
    row_at = lax.broadcasted_iota(jnp.int32, (SEG, 1), 0)
    diff = jnp.where(row_at > 0, diff, 0.0)
    diff_out[...] = diff
    table = seg_pos[...].astype(WIDE)
    chosen = lax.broadcasted_iota(jnp.int32, table.shape, 0) == number
    position = jnp.sum(jnp.where(chosen, table, 0.0), axis=0, keepdims=True)
    head_out[:, :MODEL] = rows[0:1, :] + position
    head_out[:, MODEL : 2 * MODEL] = target_rows[0:1, :]
    square = jnp.sum(column_sum(diff * diff), axis=1, keepdims=True)
    lane = lax.broadcasted_iota(jnp.int32, (1, LANES), 1)
    facts = jnp.where(lane == 0, live_rows[0:1, :], 0.0)
    facts = jnp.where(lane == 1, doc.astype(WIDE), facts)
    facts = jnp.where(lane == 2, number.astype(WIDE), facts)
    facts = jnp.where(lane == 3, square, facts)
    head_out[:, 2 * MODEL :] = facts


def second_norm_kernel(where, diff, count, normed, inv_dev, vectors, grad_out, low_out, sums_out):
    grad_top = diff[...] * ((SEG * GROUP * CORES) / count[0:1, 0:1])
    normed_rows = normed[...]
    grad = norm_rows_back(grad_top, normed_rows, inv_dev[...], vectors[6:7, :])
    low = grad.astype(LOW)
    grad_out[...] = grad
    low_out[...] = low
    sums_out[0:1, :] = column_sum(low)
    sums_out[1:2, :] = column_sum(grad_top * normed_rows)
    sums_out[2:3, :] = column_sum(grad_top)


def mlp_back_kernel(where, *refs):
    low, low_got, down_weight, up_weight, slope = refs[:5]
    pre_out, own_out, send_out, sums_out, both = refs[5:]
    both[:SEG] = low[...]
    both[SEG:] = low_got[...]
    for at in range(FF_HALF // MODEL):
        columns = slice(at * MODEL, (at + 1) * MODEL)
        held = down_weight[:, :, columns]
        before = product_plain(both[...], held.reshape(MODEL, MODEL))
        pre = (before * slope[:, columns]).astype(LOW)
        pre_out[:, columns] = pre
        sums_out[at : at + 1, :] = column_sum(pre)
    partial = product_right(pre_out[...], whole_rows(up_weight))
    own_out[...] = partial[:SEG]
    send_out[...] = partial[SEG:]


def scatter_parts(where, parts, outs, sems):
    line_at, plane_at = where[0], where[1]
    far_low, far_high, to_x, to_y, kept = outs
    half = LINE // 2
    copies = []
    for mask in range(PLANE):
        for step in range(LINE):
            source = parts.at[(line_at + step) % LINE * PLANE + (plane_at ^ mask)]
            if mask == 3:
                target = far_low.at[step] if step < half else far_high.at[step - half]
            else:
                target = (kept, to_x, to_y)[mask].at[step]
            copies.append(pltpu.make_async_copy(source, target, sems.at[len(copies)]))
    for copy in copies:
        copy.start()
    wait_all(copies)


def mlp_weight_kernel(where, *refs):
    first, first_got, second, second_got, pre, act = refs[:6]
    outs = refs[6:11]
    left, parts, sems = refs[11:]
    for at, (own, got, right) in enumerate(((first, first_got, pre), (second, second_got, act))):
        left[:SEG] = own[...]
        left[SEG:] = got[...]
        for piece in range(FF_HALF // MODEL):
            start = piece * MODEL
            product = product_left(left[...], right[:, start : start + MODEL]).astype(LOW)
            target = at * FF_HALF + start
            parts[:, :, target : target + MODEL] = product.reshape(GROUP, OWN, MODEL)
    scatter_parts(where, parts, outs, sems)


def attn_product(where, refs, mask, piece):
    hidden, mixed, proj, branch, got = refs
    lanes = slice(mask * SPAN, (mask + 1) * SPAN)
    if piece < 3:
        right = proj[:, piece * HALF : (piece + 1) * HALF]
        product = product_left(hidden[:, lanes], right)
    else:
        own = branch[:, pl.ds(aligned(where[2] * HALF), HALF)]
        product = product_left(mixed[:SEG, lanes], own)
        product = product + product_left(mixed[SEG:, lanes], got[:, HALF:])
    return product[: LINE * OWN].astype(LOW).reshape(LINE, OWN, HALF)


def attn_far_kernel(where, *refs):
    low_out, high_out = refs[5:]
    half = LINE // 2
    for piece in range(4):
        columns = slice(piece * HALF, (piece + 1) * HALF)
        product = attn_product(where, refs[:5], 3, piece)
        low_out[:, :, columns] = product[:half]
        high_out[:, :, columns] = product[half:]


def attn_near_kernel(where, *refs):
    proj, (top_row, out_rows, live_row) = refs[2], refs[5:8]
    weight, sums_first, sums_second, sums_up, head_top, head_normed, data = refs[8:15]
    x_out, y_out, kept_out, output_out, own_out, send_out, payload_out, rows = refs[15:]
    core_at = where[2]
    partial = product_right(proj[...], whole_rows(weight))
    own_out[...] = partial[:SEG]
    send_out[...] = partial[SEG:]
    row_at = lax.broadcasted_iota(jnp.int32, (SEG, 1), 0)
    output = jnp.where(row_at == 0, top_row[...] * live_row[:, 0:1], out_rows[...])
    output_out[...] = output.astype(LOW)
    for mask, out in ((1, x_out), (2, y_out), (0, kept_out)):
        for piece in range(4):
            columns = slice(piece * HALF, (piece + 1) * HALF)
            out[:, :, columns] = attn_product(where, refs[:5], mask, piece)
    lanes = pl.ds(aligned(core_at * HALF), HALF)
    rows[...] = jnp.zeros_like(rows)
    rows[0:12, :] = data[0:12, :]
    rows[12:13, lanes] = column_sum(proj[:, :HALF])
    rows[13:14, lanes] = column_sum(proj[:, 2 * HALF :])
    rows[14:15, :] = sums_first[0:1, :]
    rows[15:16, :] = sums_second[0:1, :] + data[2:3, :]
    rows[16:18, :] = sums_first[1:3, :]
    rows[18:19, :] = sums_second[1:2, :] + head_top[...] * head_normed[0:1, :]
    rows[19:20, :] = sums_second[2:3, :] + head_top[...]
    for at in range(FF_HALF // MODEL):
        total = sums_up[at : at + 1, :] + data[4 + 2 * at : 5 + 2 * at, :]
        total = total + data[5 + 2 * at : 6 + 2 * at, :]
        rows[pl.ds(20 + core_at * (FF_HALF // MODEL) + at, 1), :] = total
    payload_out[...] = rows[...].astype(LOW)


def fold_kernel(where, kept, got_x, got_y, *refs):
    extra, own_out, sent = refs[: -LINE], refs[-LINE], refs[1 - LINE :]
    rows = kept.shape[1]
    for step in range(LINE):
        total = kept[step].astype(WIDE) + got_x[step].astype(WIDE) + got_y[step].astype(WIDE)
        if step == 0:
            own_out[...] = total
            continue
        out = sent[step - 1]
        out[:rows, :] = total.astype(LOW)
        if extra:
            out[rows:, :] = jnp.zeros_like(out[rows:, :])
            out[rows:, : extra[0].shape[1]] = extra[0][...]


def reduce_far(parts):
    return together(in_plane(parts[0], 2), in_plane(parts[1], 1))


def reduce_add(where, parts, far):
    shape = parts[2].shape
    return run_kernel(
        add_far_kernel,
        "add_far",
        [shape_of(shape, LOW)] * 2,
        where,
        (),
        tuple(far) + (parts[2], parts[3]),
    )


def reduce_fold(where, kept, got, *extra):
    _, rows, columns = kept.shape
    more = sum(value.shape[0] for value in extra)
    return run_kernel(
        fold_kernel,
        "fold",
        [shape_of((rows, columns))] + [shape_of((rows + more, columns), LOW)] * (LINE - 1),
        where,
        (),
        (kept,) + tuple(got) + extra,
    )


def reduce_line(own, pieces):
    total = own
    for piece in pieces:
        total = total + piece[: own.shape[0]].astype(WIDE)
    return total


def head_back_kernel(where, *refs):
    grad, grad_got, down_weight, up_weight, slope, act, low, low_got = refs[:8]
    own_out, send_out, data_out = refs[8:]
    few = 16
    row_at = lax.broadcasted_iota(jnp.int32, (few, 1), 0)

    def two_rows(first, second):
        return jnp.where(row_at == 0, first, jnp.where(row_at == 1, second, 0.0))

    second = two_rows(grad[...], grad_got[...]).astype(LOW)
    data_out[0:1, :] = low[0:1, :].astype(WIDE)
    data_out[1:2, :] = low_got[0:1, :].astype(WIDE)
    data_out[2:4, :] = second[0:2].astype(WIDE)
    partial = jnp.zeros((few, MODEL), WIDE)
    for at in range(FF_HALF // MODEL):
        columns = slice(at * MODEL, (at + 1) * MODEL)
        before = product_plain(second, down_weight[:, :, columns].reshape(MODEL, MODEL))
        slopes = two_rows(slope[0:1, columns], slope[SEG : SEG + 1, columns])
        pre = (before * slopes).astype(LOW)
        partial = partial + product_right(pre, up_weight[:, :, columns].reshape(MODEL, MODEL))
        data_out[4 + 2 * at : 6 + 2 * at, :] = pre[0:2].astype(WIDE)
        data_out[8 + 2 * at : 9 + 2 * at, :] = act[0:1, columns].astype(WIDE)
        data_out[9 + 2 * at : 10 + 2 * at, :] = act[SEG : SEG + 1, columns].astype(WIDE)
    own_out[...] = partial[0:1]
    send_out[...] = partial[1:2]


def first_norm_kernel(where, *refs):
    second_grad, own, got, head_grad, head_own, head_got = refs[:6]
    normed_rows, inv_dev, vectors, out_weight = refs[6:10]
    grad_out, branch_out, mixed_out, send_out, sums_out = refs[10:]
    core_at = where[2]
    grad_rows = second_grad[...] + own[...] + got[...]
    head = head_grad[...] + head_own[...] + head_got[...]
    row_at = lax.broadcasted_iota(jnp.int32, (SEG, 1), 0)
    grad_rows = jnp.where(row_at == 0, head, grad_rows)
    normed = normed_rows[...]
    grad = norm_rows_back(grad_rows, normed, inv_dev[...], vectors[4:5, :])
    grad_out[...] = grad
    branch = grad.astype(LOW)
    branch_out[...] = branch
    mixed_out[...] = product_right(branch, out_weight[...]).astype(LOW)
    other = pl.ds(aligned((1 - core_at) * HALF), HALF)
    send_out[:, :HALF] = mixed_out[:, other]
    send_out[:, HALF:] = branch_out[:, other]
    sums_out[0:1, :] = column_sum(branch)
    sums_out[1:2, :] = column_sum(grad_rows * normed)
    sums_out[2:3, :] = column_sum(grad_rows)


def attn_back_kernel(where, *refs):
    qkv, mixed_grad, got, live_row, live_got, proj_out = refs
    core_at = where[2]
    lanes = pl.ds(aligned(core_at * HALF), HALF)
    for part, live in enumerate((live_row, live_got)):
        at = slice(part * SEG, (part + 1) * SEG)
        grad = mixed_grad[:, lanes] if part == 0 else got[:, :HALF]
        pieces = attend_tiles_back(qkv[at, :], grad, HALF, token_allowed(live[...]))
        for tile, value in enumerate(pieces):
            proj_out[at, tile * LANES : (tile + 1) * LANES] = value


def cls_gather_kernel(where, *refs):
    blocks = refs[:8]
    own_out, from_x, from_y, far_x = refs[8], refs[4], refs[5], refs[6]
    weight_out, out_rows = refs[9:]
    plane_at = where[1]
    gather_blocks(where, blocks, 0, QUARTER_HALF, ((weight_out, 0, QUARTER_HALF),))
    first = LINE * QUARTER_HALF
    out_rows[plane_at] = own_out[...]
    out_rows[plane_at ^ 1] = from_x[:, first : first + HALF]
    out_rows[plane_at ^ 2] = from_y[:, first : first + HALF]
    first = LINE // 2 * QUARTER_HALF
    out_rows[plane_at ^ 3] = far_x[:, first : first + HALF]


def cls_weight_kernel(where, own, got, out_half, out_got, weight_out, out_full):
    line_at, core_at = where[0], where[2]
    out_full[...] = jnp.zeros_like(out_full)
    for value, part, core in ((own, out_half, core_at), (got, out_got, 1 - core_at)):
        weight_out[:, :, pl.ds(aligned(core * QUARTER_HALF), QUARTER_HALF)] = value[...]
        rows = part[...].reshape(3, HEAD_DIM, HALF)
        out_full[pl.ds(line_at % 2, 3), :, pl.ds(aligned(core * HALF), HALF)] = rows


def add_far_kernel(where, far_low, far_high, to_x, to_y, x_out, y_out):
    half = LINE // 2
    x_out[:half] = to_x[:half] + far_low[...]
    x_out[half:] = to_x[half:]
    y_out[:half] = to_y[:half]
    y_out[half:] = to_y[half:] + far_high[...]


def row_from_column(column, size):
    shape = (size, size)
    same = lax.broadcasted_iota(jnp.int32, shape, 0) == lax.broadcasted_iota(jnp.int32, shape, 1)
    return jnp.sum(jnp.where(same, column, 0.0), axis=0, keepdims=True)


def head_allowed(heads):
    facts = heads[:, 2 * MODEL :]
    live, doc = facts[:, 0:1], facts[:, 1:2]
    shape = (GROUP, GROUP)
    same = lax.broadcasted_iota(jnp.int32, shape, 0) == lax.broadcasted_iota(jnp.int32, shape, 1)
    live_row, doc_row = row_from_column(live, GROUP), row_from_column(doc, GROUP)
    return ((live_row > 0.5) & (doc == doc_row)) | same


def quarter_mask(quarter):
    lane = lax.broadcasted_iota(jnp.int32, (GROUP, SPAN), 1)
    first = (quarter % 2) * HEAD_DIM
    return (lane >= first) & (lane < first + 3 * HEAD_DIM)


def quarter_piece(vectors, row, quarter):
    value = jnp.zeros((1, SPAN), WIDE)
    for at in range(LINE):
        first = TILE_START[at] * LANES
        value = jnp.where(quarter == at, vectors[row : row + 1, first : first + SPAN], value)
    return value


def cls_attend_kernel(where, *refs):
    stacks, vectors, weight, out_weight = refs[:4], refs[4], refs[5], refs[6]
    heads_out, qkv_out, mixed_out, part_out = refs[7:]
    line_at, plane_at = where[0], where[1]
    for step, stack in enumerate(stacks):
        for mask in range(PLANE):
            row = (line_at + LINE - step) % LINE * PLANE + (plane_at ^ mask)
            heads_out[pl.ds(row, 1), :] = stack[mask : mask + 1, :]
    heads = heads_out[...]
    inputs = heads[:, :MODEL].astype(LOW)
    projected = product_plain(inputs, weight[:, : 3 * SPAN])
    query = projected[:, :SPAN] + quarter_piece(vectors, 12, line_at)
    value = projected[:, 2 * SPAN :] + quarter_piece(vectors, 13, line_at)
    qkv_out[:, :SPAN] = query.astype(LOW)
    qkv_out[:, SPAN : 2 * SPAN] = projected[:, SPAN : 2 * SPAN].astype(LOW)
    qkv_out[:, 2 * SPAN :] = value.astype(LOW)
    mixed = attend_tiles(qkv_out[...], SPAN, head_allowed(heads))
    mixed = masked(jnp.concatenate(mixed, axis=1), quarter_mask(line_at))
    mixed_out[...] = mixed
    part_out[...] = product_plain(mixed, out_weight[...])


def cls_mlp_kernel(where, *refs):
    heads, own, got_one, got_two, got_three, vectors, weight = refs[:7]
    normed_out, inv_out, low_out, act_out, slope_out, part_out = refs[7:]
    line_at = where[0]
    branch = own[...] + got_one[...] + got_two[...] + got_three[...]
    normed, inv_dev = norm_rows(heads[:, :MODEL] + branch + vectors[14:15, :])
    normed_out[...] = normed
    inv_out[...] = inv_dev
    low = (normed * vectors[16:17, :] + vectors[17:18, :]).astype(LOW)
    low_out[...] = low
    part = FF // LINE
    first = 3 * SPAN
    bias = vectors[pl.ds(20 + line_at, 1), :]
    before = product_plain(low, weight[:, first : first + part]) + bias
    value, slope = gelu_both(before)
    act = value.astype(LOW)
    act_out[...] = act
    slope_out[...] = slope
    part_out[...] = product_right(act, weight[:, first + part :])


def cls_top_kernel(where, *refs):
    heads, own, got_one, got_two, got_three, vectors, weight = refs[:7]
    normed_first, count, slope = refs[7:10]
    top_out, square_out, grad_out, second_out, pre_out, part_out, sums_out = refs[10:17]
    held = refs[17]
    rank = where[0] * PLANE + where[1]
    first = normed_first[...] * vectors[16:17, :] + vectors[17:18, :]
    down = own[...] + got_one[...] + got_two[...] + got_three[...]
    normed, inv_dev = norm_rows(first + down + vectors[15:16, :])
    rows = normed * vectors[18:19, :] + vectors[19:20, :]
    held[...] = rows
    top_out[...] = held[pl.ds(rank, 1), :]
    facts = heads[:, 2 * MODEL :]
    live = facts[:, 0:1]
    diff = (rows * live - heads[:, MODEL : 2 * MODEL]) * live
    square = jnp.sum(column_sum(diff * diff), axis=1, keepdims=True)
    square = square + jnp.sum(facts[:, 3:4], axis=0, keepdims=True)
    square_out[...] = jnp.broadcast_to(square, square_out.shape)
    grad_top = diff * ((SEG * GROUP * CORES) / count[0:1, 0:1])
    grad = norm_rows_back(grad_top, normed, inv_dev, vectors[18:19, :])
    sums_out[0:1, :] = column_sum(grad_top * normed)
    sums_out[1:2, :] = column_sum(grad_top)
    grad_out[...] = grad
    second = grad.astype(LOW)
    second_out[...] = second
    part = FF // LINE
    at = 3 * SPAN
    pre = (product_plain(second, weight[:, at + part :]) * slope[...]).astype(LOW)
    pre_out[...] = pre
    part_out[...] = product_right(pre, weight[:, at : at + part])


def cls_attend_back_kernel(where, *refs):
    heads, own, got_one, got_two, got_three, vectors, weight, out_weight = refs[:8]
    grad_in, normed_first, inv_first, qkv = refs[8:12]
    grad_out, branch_out, proj_out, part_out, sums_out = refs[12:]
    line_at = where[0]
    grad_first = grad_in[...] + own[...] + got_one[...] + got_two[...] + got_three[...]
    normed = normed_first[...]
    grad = norm_rows_back(grad_first, normed, inv_first[...], vectors[16:17, :])
    sums_out[0:1, :] = column_sum(grad_first * normed)
    sums_out[1:2, :] = column_sum(grad_first)
    grad_out[...] = grad
    branch = grad.astype(LOW)
    branch_out[...] = branch
    mask = quarter_mask(line_at)
    mixed_grad = masked(product_right(branch, out_weight[...]).astype(LOW), mask)
    pieces = attend_tiles_back(qkv[...], mixed_grad, SPAN, head_allowed(heads[...]))
    tiles = SPAN // LANES
    for piece in range(3):
        joined = jnp.concatenate(pieces[piece * tiles : (piece + 1) * tiles], axis=1)
        proj_out[:, piece * SPAN : (piece + 1) * SPAN] = masked(joined, mask)
    part_out[...] = product_right(proj_out[...], weight[:, : 3 * SPAN])


def cls_end_kernel(where, *refs):
    heads, grad, own, got_one, got_two, got_three = refs[:6]
    square, sums_back, sums_top = refs[6:9]
    normed_second, inv_second, vectors = refs[9:12]
    row_out, second_out, shared_out, held = refs[12:]
    rank = where[0] * PLANE + where[1]
    total = grad[...] + own[...] + got_one[...] + got_two[...] + got_three[...]
    held[...] = total
    row = held[pl.ds(rank, 1), :]
    row_out[...] = row
    second_out[...] = norm_rows_back(
        row, normed_second[0:1, :], inv_second[0:1, :], vectors[6:7, :]
    )
    number = row_from_column(heads[:, 2 * MODEL + 2 : 2 * MODEL + 3], GROUP)
    entry = lax.broadcasted_iota(jnp.int32, (GROUP, GROUP), 0).astype(WIDE)
    hot = (entry == number).astype(WIDE)
    shared_out[0:GROUP, :] = jnp.dot(hot, total, precision=lax.Precision.HIGHEST)
    shared_out[GROUP : GROUP + 1, 0:LANES] = square[0:1, :]
    shared_out[GROUP + 1 : GROUP + 3, :] = sums_back[0:2, :]
    shared_out[GROUP + 3 : GROUP + 5, :] = sums_top[0:2, :]


def head_mlp_kernel(where, *refs):
    cls_mlp_kernel(where, *refs[:7], *refs[11:17])
    add_far_kernel(where, *refs[7:11], *refs[17:])


def head_end_kernel(where, *refs):
    cls_end_kernel(where, *refs[:12], *refs[16:19], refs[23])
    fold_kernel(where, *refs[12:16], *refs[19:23])


def attn_add_kernel(where, *refs):
    far_low, far_high, to_x, to_y, grad, own, got, x_out, y_out, input_out = refs
    add_far_kernel(where, far_low, far_high, to_x, to_y, x_out, y_out)
    input_out[...] = (grad[...] + own[...] + got[...]).astype(LOW)


def rows_input_kernel(where, *refs):
    cls_rows_kernel(where, *refs[:8], refs[11], refs[13])
    grad, own, got, input_out = refs[8], refs[9], refs[10], refs[12]
    input_out[...] = (grad[...] + own[...] + got[...]).astype(LOW)


def cls_rows_kernel(where, *refs):
    packs = refs[:4]
    heads, branch, low, second = refs[4:8]
    out, kept = refs[8:]
    line_at = where[0]
    rows, width = kept.shape[1:]
    for step, pack in enumerate(packs):
        first = pack.shape[0] - rows
        kept[(line_at + LINE - step) % LINE] = pack[first:, :width]
    starts = (MODEL, 2 * MODEL, 3 * MODEL, 4 * MODEL)
    out[:, 0:MODEL] = heads[:, :MODEL].astype(LOW)
    for piece, start in enumerate(starts):
        from_at = piece * SPAN
        for tile in range(MODEL // LANES):
            total = None
            for at in range(PLANE):
                inner = tile - TILE_START[at]
                if inner in (0, 1):
                    first = from_at + inner * LANES
                    value = kept[at, :, first : first + LANES]
                    total = value if total is None else total + value
            out[:, start + tile * LANES : start + (tile + 1) * LANES] = total
    out[:, 5 * MODEL : 6 * MODEL] = branch[...]
    out[:, 6 * MODEL : 7 * MODEL] = low[...]
    out[:, 7 * MODEL + FF : 8 * MODEL + FF] = second[...]
    part = FF // LINE
    for at in range(PLANE):
        first = 4 * SPAN
        out[:, 7 * MODEL + at * part : 7 * MODEL + (at + 1) * part] = kept[
            at, :, first : first + part
        ]
        out[:, 8 * MODEL + FF + at * part : 8 * MODEL + FF + (at + 1) * part] = kept[
            at, :, first + part : first + 2 * part
        ]


def own_features(rank, width):
    shape = (MODEL, width)
    feature = lax.broadcasted_iota(jnp.int32, shape, 0)
    column = lax.broadcasted_iota(jnp.int32, shape, 1)
    return (feature == rank * width + column).astype(LOW)


def own_vector(rank, pieces, out, flat):
    size = out.shape[0]
    for at, piece in enumerate(pieces):
        flat[:, at * MODEL : (at + 1) * MODEL] = piece
    value = jnp.zeros((1, size), WIDE)
    for chip in range(GROUP):
        value = jnp.where(rank == chip, flat[:, chip * size : (chip + 1) * size], value)
    out[...] = value.reshape(size)


def cls_owner_kernel(where, *refs):
    own, got, shared, mats_out, vec_out, rows, flat = refs
    rank = where[0] * PLANE + where[1]
    width = mats_out.shape[0]
    rows[:GROUP] = own[...]
    rows[GROUP:] = got[...]
    chosen = own_features(rank, width)
    plan = (
        (0, MODEL, 3 * MODEL, 0),
        (4 * MODEL, 5 * MODEL, MODEL, 3 * MODEL),
        (6 * MODEL, 7 * MODEL, FF, 4 * MODEL),
        (7 * MODEL + FF, 8 * MODEL + FF, FF, 4 * MODEL + FF),
    )
    for left, right, size, target in plan:
        side = product_plain(rows[:, left : left + MODEL], chosen).astype(LOW)
        mats_out[:, target : target + size] = product_left(side, rows[:, right : right + size])
    starts = (MODEL, 3 * MODEL, 5 * MODEL, 7 * MODEL + FF)
    pieces = [column_sum(rows[:, start : start + MODEL]) for start in starts]
    pieces += [shared[GROUP + 1 + at : GROUP + 2 + at, :] for at in range(4)]
    starts = [7 * MODEL + at * MODEL for at in range(FF // MODEL)]
    pieces += [column_sum(rows[:, start : start + MODEL]) for start in starts]
    own_vector(rank, pieces, vec_out, flat)


def head_share_kernel(where, *refs):
    packs, mlp = refs[:4], refs[4]
    mine_out, vecs_out, rows = refs[5:]
    rank = where[0] * PLANE + where[1]
    count = LINE * 24
    for at, pack in enumerate(packs):
        rows[at * count : (at + 1) * count] = pack[...]
    total = PLANE * count

    def chosen(base, apart):
        shape = (CORES * GROUP, total)
        row = lax.broadcasted_iota(jnp.int32, shape, 0)
        column = lax.broadcasted_iota(jnp.int32, shape, 1)
        hot = (column == row // 2 * 24 + base + row % 2 * apart).astype(LOW)
        return product_plain(hot, rows[...]).astype(LOW)

    own = own_features(rank, OWN)
    for at, (left, right) in enumerate(((0, 4), (2, 8))):
        side = product_plain(chosen(left, 1), own).astype(LOW)
        for piece in range(FF_HALF // MODEL):
            columns = slice(at * FF_HALF + piece * MODEL, at * FF_HALF + (piece + 1) * MODEL)
            share = product_left(side, chosen(right + 2 * piece, 1))
            mine_out[:, columns] = mlp[:, columns] + share
    shape = (16, total)
    row = lax.broadcasted_iota(jnp.int32, shape, 0)
    column = lax.broadcasted_iota(jnp.int32, shape, 1)
    hot = ((column % 24 == row + 12) & (row < 12)).astype(LOW)
    vecs_out[...] = product_plain(hot, rows[...])


def share_owner_kernel(where, *refs):
    head_share_kernel(where, *refs[:5], *refs[9:11], refs[15])
    cls_owner_kernel(where, *refs[5:8], *refs[11:13], *refs[16:])
    shared, count, pos_out, loss_out = refs[7], refs[8], refs[13], refs[14]
    pos_out[...] = shared[:GROUP, :]
    loss_out[...] = shared[GROUP : GROUP + 1, 0:1] / (count[0:1, 0:1] * MODEL)


def seg_vec_kernel(where, vecs, vecs_got, vec_out, flat):
    rank = where[0] * PLANE + where[1]
    rows = (8 * MODEL + FF) // MODEL
    pieces = [vecs[at : at + 1, :] + vecs_got[at : at + 1, :] for at in range(rows)]
    own_vector(rank, pieces, vec_out, flat)


def column_copies(where, out, base, size, own, got, first):
    core_at = where[2]
    lanes = slice(first, first + size)
    return [
        (own.at[:, lanes], out.at[:, pl.ds(aligned(base + core_at * size), size)]),
        (got.at[:, lanes], out.at[:, pl.ds(aligned(base + (1 - core_at) * size), size)]),
    ]


def store_kernel(where, attn, attn_got, mlp, mlp_got, vecs, vecs_got, out, vec_out, flat, sems):
    pairs = []
    for piece in range(4):
        pairs += column_copies(where, out, piece * MODEL, HALF, attn, attn_got, piece * HALF)
    for piece in range(2):
        base = 4 * MODEL + piece * FF
        pairs += column_copies(where, out, base, FF_HALF, mlp, mlp_got, piece * FF_HALF)
    copies = [
        pltpu.make_async_copy(source, target, sems.at[at])
        for at, (source, target) in enumerate(pairs)
    ]
    for copy in copies:
        copy.start()
    seg_vec_kernel(where, vecs, vecs_got, vec_out, flat)
    wait_all(copies)


def plane_parts(part):
    return (part,) + together(*(in_plane(part, mask) for mask in range(1, PLANE)))


def line_parts(part):
    return (part,) + together(*(along_line(part, apart) for apart in range(1, LINE)))


def slice_local(
    hidden_in,
    targets,
    doc_ids,
    seg_nums,
    valid_flags,
    seg_mats,
    seg_vecs,
    cls_mats,
    cls_vecs,
    seg_pos,
):
    rank, core_at = lax.axis_index("fsdp"), lax.axis_index("rep")
    line_at, plane_at = rank // PLANE, rank % PLANE
    where = jnp.stack([line_at, plane_at, core_at, doc_ids[0], seg_nums[0]]).astype(jnp.int32)
    own_rows, total_columns = seg_mats.shape
    vec_size = seg_vecs.shape[0]
    both_rows = CORES * SEG

    first_piece, live_row, *rest = run_kernel(
        prepare_kernel,
        "prepare",
        [shape_of((own_rows, FIRST), LOW), shape_of((1, SEG))]
        + [shape_of((own_rows, FF_HALF), LOW)] * 2
        + [shape_of((own_rows, QUARTER_HALF), LOW)] * LINE
        + [shape_of((own_rows, HALF), LOW), shape_of((MODEL, PLANE * SPAN), LOW)],
        where,
        (seg_mats, cls_mats),
        (seg_vecs, cls_vecs, valid_flags),
        [
            pltpu.SemaphoreType.DMA((4,)),
            pltpu.VMEM((LINE, own_rows, QUARTER), LOW),
            pltpu.SemaphoreType.DMA((3 + 5 * LINE,)),
        ],
    )
    first_line = line_parts(first_piece)
    second_piece, third_piece, quarters, cls_out_piece, order = (
        rest[0],
        rest[1],
        rest[2:-2],
        rest[-2],
        rest[-1],
    )

    def joined(*pieces):
        return jnp.concatenate(pieces, axis=1)

    def sent_both(to_x, to_y):
        to_x, to_y = together(to_x, to_y)
        return together(in_plane(to_x, 1), in_plane(to_y, 2))

    own_sent = joined(first_piece, second_piece, third_piece)
    own_x, own_y = sent_both(own_sent, own_sent)
    first_line = first_line[:1] + tuple(after(got, own_x, own_y) for got in first_line[1:])
    hidden_got = other_core(after(hidden_in, own_x, own_y))
    live_got = other_core(after(live_row, own_x, own_y))
    to_x = joined(after(own_y, hidden_got, live_got)[:, OWN_CUT:], *first_line[1:])
    to_y = joined(own_x[:, :OWN_CUT], *first_line[1:])
    first_x, first_y = sent_both(to_x, to_y)
    second_line = line_parts(after(second_piece, to_x, to_y))

    def halves(group, from_x, from_y):
        width, cut = WIDTHS[group], LINE_CUTS[group]
        if group == 0:
            base_x, base_y = sum(WIDTHS) - OWN_CUT, OWN_CUT
        else:
            before, before_cut = WIDTHS[group - 1], LINE_CUTS[group - 1]
            base_x, base_y = 2 * before - before_cut, before + before_cut
        return (
            from_y[:, base_y + width + cut : base_y + 3 * width],
            from_x[:, base_x : base_x + width + cut],
        )

    high, low = halves(0, first_x, first_y)
    to_x, to_y = joined(high, *second_line[1:]), joined(low, *second_line[1:])
    second_x, second_y = sent_both(to_x, to_y)
    third_line = line_parts(after(third_piece, to_x, to_y))
    high, low = halves(1, second_x, second_y)
    to_x, to_y = joined(high, *third_line[1:]), joined(low, *third_line[1:])
    third_x, third_y = sent_both(to_x, to_y)
    own_parts = (own_x, own_y, first_x, first_y)
    cls_line = (quarters[0],) + tuple(
        along_line(after(quarters[apart], to_x, to_y), apart)
        for apart in range(1, LINE)
    )

    qkv_weight, out_low, out_high, qkv, mixed, vectors, count, hidden_ordered = run_kernel(
        qkv_kernel,
        "seg_qkv",
        [
            shape_of((GROUP, own_rows, 3 * HALF), LOW),
            shape_of((GROUP // 2, own_rows, HALF), LOW),
            shape_of((GROUP // 2, own_rows, HALF), LOW),
            shape_of((both_rows, 3 * HALF), LOW),
            shape_of((both_rows, HALF), LOW),
            shape_of((2 * (8 * MODEL + FF) // MODEL, MODEL)),
            shape_of((8, LANES)),
            shape_of((both_rows, PLANE * SPAN), LOW),
        ],
        where,
        (),
        first_line
        + own_parts
        + (first_x, first_y, second_x, second_y)
        + (hidden_in, hidden_got, live_row, live_got, order),
        [
            pltpu.VMEM((GROUP, own_rows, LANES), LOW),
            pltpu.VMEM((2, 8 * MODEL + FF), WIDE),
            pltpu.VMEM((both_rows, MODEL), LOW),
            pltpu.VMEM((GROUP, own_rows, HALF), LOW),
        ],
        flops=2 * SEG * MODEL * 3 * MODEL,
    )
    out_weight, mixed_ordered, normed_first, inv_first, first_low = run_kernel(
        out_kernel,
        "seg_out",
        [
            shape_of((MODEL, MODEL), LOW),
            shape_of((both_rows, PLANE * SPAN), LOW),
            shape_of((SEG, MODEL)),
            shape_of((SEG, 1)),
            shape_of((SEG, MODEL), LOW),
        ],
        where,
        (),
        (
            hidden_in,
            mixed,
            after(other_core(mixed), third_x, third_y),
            out_low,
            out_high,
            other_core(out_low),
            other_core(out_high),
            vectors,
            order,
        ),
        [pltpu.VMEM((both_rows, MODEL), LOW)],
        flops=2 * SEG * MODEL * MODEL,
    )
    fourth_x, fourth_y = sent_both(*halves(2, third_x, third_y))
    first_got = after(other_core(first_low), fourth_x, fourth_y)
    count = count + other_core(after(count, first_got))
    up_weight, act, slope = run_kernel(
        up_kernel,
        "seg_up",
        [
            shape_of((GROUP, own_rows, FF_HALF), LOW),
            shape_of((both_rows, FF_HALF), LOW),
            shape_of((both_rows, FF_HALF)),
        ],
        where,
        (),
        second_line
        + own_parts
        + (second_x, second_y, third_x, third_y)
        + (first_low, first_got, vectors),
        [pltpu.VMEM((both_rows, MODEL), LOW)],
        flops=2 * SEG * MODEL * FF,
    )
    cls_sent = joined(*cls_line, cls_out_piece)
    cls_sent = after(cls_sent, act)
    cls_x, cls_y = sent_both(cls_sent, cls_sent)
    down_weight, down_own, down_send = run_kernel(
        down_kernel,
        "seg_down",
        [
            shape_of((GROUP, own_rows, FF_HALF), LOW),
            shape_of((SEG, MODEL)),
            shape_of((SEG, MODEL)),
        ],
        where,
        (),
        third_line + own_parts + (third_x, third_y, fourth_x, fourth_y) + (act,),
        flops=2 * SEG * MODEL * FF,
    )
    normed_second, inv_second, diff, out_rows, head_row = run_kernel(
        seg_rows_kernel,
        "seg_rows",
        [
            shape_of((SEG, MODEL)),
            shape_of((SEG, 1)),
            shape_of((SEG, MODEL)),
            shape_of((SEG, MODEL)),
            shape_of((1, 2 * MODEL + LANES)),
        ],
        where,
        (),
        (
            down_own,
            other_core(down_send),
            normed_first,
            vectors,
            targets,
            live_row,
            seg_pos,
        ),
    )
    head_planes = plane_parts(head_row)
    head_lines = line_parts(jnp.concatenate(head_planes))
    size = LINE // 2 * QUARTER_HALF
    cls_far = sent_both(
        after(cls_y[:, size:], *head_planes[1:]), after(cls_x[:, :size], *head_planes[1:])
    )

    second_grad, second_low, second_sums = run_kernel(
        second_norm_kernel,
        "seg_second_norm",
        [shape_of((SEG, MODEL)), shape_of((SEG, MODEL), LOW), shape_of((3, MODEL))],
        where,
        (),
        (diff, count, normed_second, inv_second, vectors),
    )
    second_got = other_core(second_low)
    pre, first_grad_own, first_grad_send, up_sums = run_kernel(
        mlp_back_kernel,
        "seg_mlp_back",
        [
            shape_of((both_rows, FF_HALF), LOW),
            shape_of((SEG, MODEL)),
            shape_of((SEG, MODEL)),
            shape_of((FF_HALF // MODEL, MODEL)),
        ],
        where,
        (),
        (second_low, second_got, down_weight, up_weight, slope),
        [pltpu.VMEM((both_rows, MODEL), LOW)],
        flops=4 * SEG * MODEL * FF,
    )
    first_grad_got = other_core(first_grad_send)

    def part_shapes(columns):
        return [
            shape_of((count_of, own_rows, columns), LOW)
            for count_of in (LINE // 2, LINE // 2, LINE, LINE, LINE)
        ]

    head_lines = head_lines[:1] + together(*(after(got, pre) for got in head_lines[1:]))
    cls_far = together(*(after(got, *head_lines[1:]) for got in cls_far))
    cls_half, cls_out_half = run_kernel(
        cls_gather_kernel,
        "head_gather",
        [
            shape_of((GROUP, own_rows, QUARTER_HALF), LOW),
            shape_of((PLANE, own_rows, HALF), LOW),
        ],
        where,
        (),
        cls_line + (cls_x, cls_y) + cls_far + (cls_out_piece,),
    )
    mlp_parts = run_kernel(
        mlp_weight_kernel,
        "seg_mlp_weight",
        part_shapes(FF),
        where,
        (),
        (first_low, first_got, second_low, second_got, after(pre, cls_half), act),
        [
            pltpu.VMEM((both_rows, MODEL), LOW),
            pltpu.VMEM((GROUP, own_rows, FF), LOW),
            pltpu.SemaphoreType.DMA((GROUP,)),
        ],
        far=range(5),
        flops=4 * SEG * MODEL * FF,
    )
    mlp_far = reduce_far(tuple(after(part, *cls_far) for part in mlp_parts[:2]))
    cls_weight, cls_out = run_kernel(
        cls_weight_kernel,
        "head_weight",
        [
            shape_of((GROUP, own_rows, QUARTER), LOW),
            shape_of((4, HEAD_DIM, MODEL), LOW),
        ],
        where,
        (),
        (cls_half, other_core(cls_half), cls_out_half, other_core(cls_out_half)),
    )
    cls_weight = cls_weight.reshape(MODEL, QUARTER)
    cls_out = cls_out.reshape(SPAN, MODEL)
    heads, cls_qkv, cls_mixed, part = run_kernel(
        cls_attend_kernel,
        "head_attend",
        [
            shape_of((GROUP, 2 * MODEL + LANES)),
            shape_of((GROUP, 3 * SPAN), LOW),
            shape_of((GROUP, SPAN), LOW),
            shape_of((GROUP, MODEL)),
        ],
        where,
        (),
        tuple(after(got, mlp_parts[0], first_grad_got) for got in head_lines)
        + (vectors, cls_weight, cls_out),
    )
    cls_normed, cls_inv, cls_low, cls_act, cls_slope, part, *mlp_sent = run_kernel(
        head_mlp_kernel,
        "head_mlp",
        [
            shape_of((GROUP, MODEL)),
            shape_of((GROUP, 1)),
            shape_of((GROUP, MODEL), LOW),
            shape_of((GROUP, FF // LINE), LOW),
            shape_of((GROUP, FF // LINE)),
            shape_of((GROUP, MODEL)),
            shape_of(mlp_parts[2].shape, LOW),
            shape_of(mlp_parts[2].shape, LOW),
        ],
        where,
        (),
        (heads,) + line_parts(part) + (vectors, cls_weight) + mlp_far + tuple(mlp_parts[2:4]),
    )
    mlp_plane = sent_both(*mlp_sent)
    cls_parts = line_parts(part)
    top_row, square, cls_grad, cls_second, cls_pre, part, top_sums = run_kernel(
        cls_top_kernel,
        "head_top",
        [
            shape_of((1, MODEL)),
            shape_of((8, LANES)),
            shape_of((GROUP, MODEL)),
            shape_of((GROUP, MODEL), LOW),
            shape_of((GROUP, FF // LINE), LOW),
            shape_of((GROUP, MODEL)),
            shape_of((2, MODEL)),
        ],
        where,
        (),
        (heads,)
        + cls_parts
        + (vectors, cls_weight, cls_normed, count, cls_slope),
        [pltpu.VMEM((GROUP, MODEL), WIDE)],
    )
    top_parts = line_parts(part)
    cls_grad, cls_branch, cls_proj, part, back_sums = run_kernel(
        cls_attend_back_kernel,
        "head_attend_back",
        [
            shape_of((GROUP, MODEL)),
            shape_of((GROUP, MODEL), LOW),
            shape_of((GROUP, 3 * SPAN), LOW),
            shape_of((GROUP, MODEL)),
            shape_of((2, MODEL)),
        ],
        where,
        (),
        (heads,)
        + top_parts
        + (vectors, cls_weight, cls_out, cls_grad, cls_normed, cls_inv, cls_qkv),
    )
    end_parts = line_parts(part)
    pack = jnp.concatenate([cls_proj, cls_mixed, cls_pre, cls_act], axis=1)
    folded = [shape_of((own_rows, FF))] + [shape_of((own_rows + GROUP, FF), LOW)] * (LINE - 1)
    dheads, head_grad, shared, mlp_own, *mlp_sent = run_kernel(
        head_end_kernel,
        "head_end",
        [shape_of((1, MODEL)), shape_of((1, MODEL)), shape_of((GROUP + 8, MODEL))] + folded,
        where,
        (),
        (heads, cls_grad)
        + end_parts
        + (square, back_sums, top_sums, normed_second, inv_second, vectors)
        + (mlp_parts[4],)
        + mlp_plane
        + (pack,),
        [pltpu.VMEM((GROUP, MODEL), WIDE)],
    )
    got_three, got_two = along_line(mlp_sent[2], 3), along_line(mlp_sent[1], 2)
    mlp_last = mlp_sent[0]
    mlp_got = [None, got_two, got_three]

    head_own, head_send, head_data = run_kernel(
        head_back_kernel,
        "seg_head_back",
        [shape_of((1, MODEL)), shape_of((1, MODEL)), shape_of((12, MODEL))],
        where,
        (),
        (
            head_grad,
            other_core(head_grad),
            down_weight,
            up_weight,
            slope,
            act,
            first_low,
            first_got,
        ),
    )
    grad_summed, branch, mixed_grad, attn_send, first_sums = run_kernel(
        first_norm_kernel,
        "seg_first_norm",
        [
            shape_of((SEG, MODEL)),
            shape_of((SEG, MODEL), LOW),
            shape_of((SEG, MODEL), LOW),
            shape_of((SEG, MODEL), LOW),
            shape_of((3, MODEL)),
        ],
        where,
        (),
        (
            second_grad,
            first_grad_own,
            first_grad_got,
            head_grad,
            head_own,
            other_core(head_send),
            normed_first,
            inv_first,
            vectors,
            out_weight,
        ),
    )
    attn_got = other_core(attn_send)
    proj = run_kernel(
        attn_back_kernel,
        "seg_attn_back",
        [shape_of((both_rows, 3 * HALF), LOW)],
        where,
        (),
        (qkv, mixed_grad, attn_got, live_row, live_got),
        flops=2 * SEG * MODEL * 3 * MODEL,
    )[0]
    attn_data = (hidden_ordered, mixed_ordered, proj, branch, attn_got)
    attn_far = run_kernel(
        attn_far_kernel,
        "seg_attn_far",
        part_shapes(4 * HALF)[:2],
        where,
        (),
        attn_data,
        flops=SEG * MODEL * 2 * MODEL,
    )
    attn_far = reduce_far(tuple(after(part, mlp_got[-1]) for part in attn_far))
    *attn_near, output, input_own, input_send, payload = run_kernel(
        attn_near_kernel,
        "seg_attn_near",
        part_shapes(4 * HALF)[2:]
        + [
            shape_of((SEG, MODEL), LOW),
            shape_of((SEG, MODEL)),
            shape_of((SEG, MODEL)),
            shape_of((24, MODEL), LOW),
        ],
        where,
        (),
        attn_data
        + (top_row, out_rows, live_row, qkv_weight, first_sums, second_sums, up_sums)
        + (dheads, normed_second, head_data),
        [pltpu.VMEM((24, MODEL), WIDE)],
        flops=3 * SEG * MODEL * 2 * MODEL,
    )
    attn_sent = run_kernel(
        add_far_kernel,
        "seg_attn_add",
        [shape_of(attn_near[0].shape, LOW)] * 2,
        where,
        (),
        attn_far + (after(attn_near[0], got_two), attn_near[1]),
    )
    attn_plane = sent_both(*attn_sent)
    mlp_got[0] = along_line(after(mlp_last, *attn_sent), 1)
    input_got = other_core(after(input_send, *attn_sent))
    shared = shared + other_core(after(shared, attn_sent[0]))
    payload_parts = line_parts(after(payload, mlp_got[0], input_got, shared))
    mlp_got = [after(got, attn_plane[0]) for got in mlp_got]
    mlp_sum = reduce_line(mlp_own, mlp_got)
    row_width = 8 * MODEL + 2 * FF
    cls_rows, input_grad = run_kernel(
        rows_input_kernel,
        "head_rows",
        [shape_of((GROUP, row_width), LOW), shape_of((SEG, MODEL), LOW)],
        where,
        (),
        (pack,)
        + tuple(mlp_got)
        + (heads, cls_branch, cls_low, cls_second)
        + (grad_summed, input_own, input_got),
        [pltpu.VMEM((LINE,) + pack.shape, LOW)],
    )
    cls_got = other_core(cls_rows)
    attn_plane = tuple(after(got, output, shared) for got in attn_plane)
    attn_own, *attn_sent = reduce_fold(where, attn_near[2], attn_plane)
    attn_lines = list(
        together(*(along_line(attn_sent[apart - 1], apart) for apart in range(1, LINE)))
    )
    flat = pltpu.VMEM((1, 8 * MODEL + FF), WIDE)
    payload_line = jnp.concatenate(payload_parts)
    mlp_mine, own_vecs, cls_mats_grad, cls_vec_grad, pos_total, loss_value = run_kernel(
        share_owner_kernel,
        "head_owner",
        [
            shape_of((own_rows, FF)),
            shape_of((16, MODEL)),
            shape_of((own_rows, total_columns)),
            shape_of((vec_size,)),
            shape_of((GROUP, MODEL)),
            shape_of((1, 1)),
        ],
        where,
        (),
        tuple(after(got, attn_own) for got in plane_parts(after(payload_line, *attn_plane)))
        + (mlp_sum, cls_rows, cls_got, shared, count),
        [
            pltpu.VMEM((GROUP * 24, MODEL), LOW),
            pltpu.VMEM((CORES * GROUP, row_width), LOW),
            flat,
        ],
        flops=64 * own_rows * total_columns,
    )
    loss_value = loss_value.reshape(())
    attn_lines = together(*(after(got, mlp_mine) for got in attn_lines))
    attn_sum = reduce_line(attn_own, attn_lines)
    seg_mats_grad, seg_vec_grad = run_kernel(
        store_kernel,
        "seg_owner",
        [shape_of((own_rows, total_columns)), shape_of((vec_size,))],
        where,
        (),
        (attn_sum, other_core(attn_sum), mlp_mine, other_core(mlp_mine))
        + (own_vecs, other_core(own_vecs)),
        [flat, pltpu.SemaphoreType.DMA((12,))],
        far=(0,),
    )

    return (
        output,
        input_grad,
        seg_mats_grad,
        seg_vec_grad,
        cls_mats_grad,
        cls_vec_grad,
        pos_total,
        loss_value,
    )


def solution(mesh):
    in_specs = (
        P(("rep", "fsdp"), None),
        P(("rep", "fsdp"), None),
        P(("rep", "fsdp")),
        P(("rep", "fsdp")),
        P(("rep", "fsdp")),
        P("fsdp", None),
        P("fsdp"),
        P("fsdp", None),
        P("fsdp"),
        P(),
    )
    out_specs = (
        P(("rep", "fsdp"), None),
        P(("rep", "fsdp"), None),
        P("fsdp", None),
        P("fsdp"),
        P("fsdp", None),
        P("fsdp"),
        P(),
        P(),
    )
    one_slice = dict(mesh.shape) == {"rep": CORES, "fsdp": LINE * PLANE}
    body = slice_local if one_slice else local
    return jax.shard_map(body, mesh=mesh, in_specs=in_specs, out_specs=out_specs, check_vma=False)
```

```python
import math

import jax
import jax.numpy as jnp
from jax import lax
from jax.experimental import pallas as pl
from jax.experimental.pallas import tpu as pltpu
from jax.sharding import PartitionSpec as P

HEADS = 12
HEAD_DIM = 64
FF = 3072
SEG = 128
SEQ = 2048


NORM_EPS = 1e-05
MASK_FILL = -1e30
SQRT_HALF = 0.7071067811865476
INV_SQRT_TWO_PI = 0.3989422804014327


def swapped(value, axis, apart):
    mask = 2**apart
    pairs = [(source, source ^ mask) for source in range(lax.axis_size(axis))]
    return lax.ppermute(value, axis, pairs)


def product_plain(left_side, right_side):
    return jnp.dot(left_side, right_side, preferred_element_type=jnp.float32)


def product_left(left_side, right_side):
    return lax.dot_general(
        left_side, right_side, (((0,), (0,)), ((), ())), preferred_element_type=jnp.float32
    )


def product_right(left_side, right_side):
    return lax.dot_general(
        left_side, right_side, (((1,), (1,)), ((), ())), preferred_element_type=jnp.float32
    )


def row_total(array_in):
    return jnp.sum(array_in.astype(jnp.float32), axis=0)


def unpack_weights(gathered, model_width, ff_width):
    matrix, vector = gathered
    vector = vector.astype(jnp.float32)
    pieces = tuple(
        (vector[offset * model_width : (offset + 1) * model_width] for offset in range(8))
    )
    return (
        (
            matrix[:, : 3 * model_width],
            matrix[:, 3 * model_width : 4 * model_width],
            matrix[:, 4 * model_width : 4 * model_width + ff_width],
            matrix[:, 4 * model_width + ff_width :],
        )
        + pieces
        + (vector[8 * model_width :],)
    )


def norm_forward(summed, gain_vec, shift_vec):
    row_mean = jnp.mean(summed, axis=-1, keepdims=True)
    centered = summed - row_mean
    inv_dev = lax.rsqrt(jnp.mean(centered * centered, axis=-1, keepdims=True) + NORM_EPS)
    normed = centered * inv_dev
    return (normed * gain_vec + shift_vec, normed, inv_dev)


def norm_backward(grad_out, normed, inv_dev, gain_vec):
    scaled = grad_out * gain_vec
    mean_one = jnp.mean(scaled, axis=-1, keepdims=True)
    mean_two = jnp.mean(scaled * normed, axis=-1, keepdims=True)
    grad_in = inv_dev * (scaled - mean_one - normed * mean_two)
    return (grad_in, jnp.sum(grad_out * normed, axis=0), jnp.sum(grad_out, axis=0))


def gelu_value(before):
    return 0.5 * before * (1.0 + lax.erf(before * SQRT_HALF))


def gelu_slope(before):
    return (
        0.5 * (1.0 + lax.erf(before * SQRT_HALF))
        + before * jnp.exp(-0.5 * before * before) * INV_SQRT_TWO_PI
    )


def attention_scores(queries, keys_in, allowed, score_scale):
    raw_scores = (
        jnp.einsum("bqhe,bkhe->bhqk", queries, keys_in, preferred_element_type=jnp.float32)
        * score_scale
    )
    return jnp.where(allowed, raw_scores, MASK_FILL)


def attention_forward(queries, keys_in, values, allowed, score_scale):
    scores = attention_scores(queries, keys_in, allowed, score_scale)
    row_top = jnp.max(scores, axis=-1, keepdims=True)
    log_total = row_top + jnp.log(jnp.sum(jnp.exp(scores - row_top), axis=-1, keepdims=True))
    weights = jnp.exp(scores - log_total).astype(jnp.bfloat16)
    mixed_rows = jnp.einsum("bhqk,bkhe->bqhe", weights, values, preferred_element_type=jnp.float32)
    return (mixed_rows, log_total)


def attention_backward(queries, keys_in, values, allowed, score_scale, log_total, grad_mixed):
    probabilities = jnp.exp(attention_scores(queries, keys_in, allowed, score_scale) - log_total)
    grad_probs = jnp.einsum(
        "bqhe,bkhe->bhqk", grad_mixed, values, preferred_element_type=jnp.float32
    )
    inner_sum = jnp.sum(grad_probs * probabilities, axis=-1, keepdims=True)
    grad_scores = (probabilities * (grad_probs - inner_sum)).astype(jnp.bfloat16)
    grad_query = (
        jnp.einsum("bhqk,bkhe->bqhe", grad_scores, keys_in, preferred_element_type=jnp.float32)
        * score_scale
    )
    grad_key = (
        jnp.einsum("bhqk,bqhe->bkhe", grad_scores, queries, preferred_element_type=jnp.float32)
        * score_scale
    )
    grad_value = jnp.einsum(
        "bhqk,bqhe->bkhe",
        probabilities.astype(jnp.bfloat16),
        grad_mixed,
        preferred_element_type=jnp.float32,
    )
    return (grad_query, grad_key, grad_value)


def block_forward(rows_in, unpacked, attend):
    (
        qkv_weight,
        out_weight,
        up_weight,
        down_weight,
        query_bias,
        value_bias,
        out_bias,
        down_bias,
        gain_first,
        shift_first,
        gain_second,
        shift_second,
        up_bias,
    ) = unpacked
    model_width = rows_in.shape[1]
    inputs = rows_in.astype(jnp.bfloat16)
    projected = product_plain(inputs, qkv_weight)
    queries = (projected[:, :model_width] + query_bias).astype(jnp.bfloat16)
    keys_in = projected[:, model_width : 2 * model_width].astype(jnp.bfloat16)
    values = (projected[:, 2 * model_width :] + value_bias).astype(jnp.bfloat16)
    mixed_rows, attend_kept = attend(queries, keys_in, values)
    mixed_rows = mixed_rows.astype(jnp.bfloat16)
    summed_first = rows_in + product_plain(mixed_rows, out_weight) + out_bias
    first_out, normed_first, inv_first = norm_forward(summed_first, gain_first, shift_first)
    first_low = first_out.astype(jnp.bfloat16)
    pre_act = product_plain(first_low, up_weight) + up_bias
    activated = gelu_value(pre_act).astype(jnp.bfloat16)
    summed_second = first_out + product_right(activated, down_weight) + down_bias
    block_out, normed_second, inv_second = norm_forward(summed_second, gain_second, shift_second)
    saved_state = (
        inputs,
        queries,
        keys_in,
        values,
        attend_kept,
        mixed_rows,
        normed_first,
        inv_first,
        first_low,
        pre_act,
        activated,
        normed_second,
        inv_second,
    )
    return (block_out, saved_state)


def block_backward(grad_out, unpacked, saved_state, attend_back):
    (
        qkv_weight,
        out_weight,
        up_weight,
        down_weight,
        query_bias,
        value_bias,
        out_bias,
        down_bias,
        gain_first,
        shift_first,
        gain_second,
        shift_second,
        up_bias,
    ) = unpacked
    (
        inputs,
        queries,
        keys_in,
        values,
        attend_kept,
        mixed_rows,
        normed_first,
        inv_first,
        first_low,
        pre_act,
        activated,
        normed_second,
        inv_second,
    ) = saved_state
    grad_second, grad_gain_second, grad_shift_second = norm_backward(
        grad_out, normed_second, inv_second, gain_second
    )
    second_low = grad_second.astype(jnp.bfloat16)
    grad_pre = (product_plain(second_low, down_weight) * gelu_slope(pre_act)).astype(jnp.bfloat16)
    grad_first = grad_second + product_right(grad_pre, up_weight)
    grad_summed, grad_gain_first, grad_shift_first = norm_backward(
        grad_first, normed_first, inv_first, gain_first
    )
    branch_low = grad_summed.astype(jnp.bfloat16)
    grad_mixed = product_right(branch_low, out_weight).astype(jnp.bfloat16)
    grad_query, grad_key, grad_value = attend_back(
        queries, keys_in, values, attend_kept, grad_mixed
    )
    grad_proj = jnp.concatenate([grad_query, grad_key, grad_value], axis=1)
    grad_rows = grad_summed + product_right(grad_proj, qkv_weight)
    vector_grad = jnp.concatenate(
        [
            row_total(grad_query),
            row_total(grad_value),
            row_total(branch_low),
            row_total(second_low),
            grad_gain_first,
            grad_shift_first,
            grad_gain_second,
            grad_shift_second,
            row_total(grad_pre),
        ]
    )
    weight_rows = (
        inputs,
        grad_proj,
        mixed_rows,
        branch_low,
        first_low,
        grad_pre,
        second_low,
        activated,
    )
    return (grad_rows, weight_rows, vector_grad)


def weight_products(weight_rows):
    inputs, grad_proj, mixed_rows, branch_low, first_low, grad_pre, second_low, activated = (
        weight_rows
    )
    return (
        product_left(inputs, grad_proj),
        product_left(mixed_rows, branch_low),
        product_left(first_low, grad_pre),
        product_left(second_low, activated),
    )


def local(
    hidden_in,
    targets,
    doc_ids,
    seg_nums,
    valid_flags,
    seg_mats,
    seg_vecs,
    cls_mats,
    cls_vecs,
    seg_pos,
):
    tok_rows, model_width = hidden_in.shape
    ff_width = FF
    seg_len = SEG
    group_span = SEQ // tok_rows
    seg_count = tok_rows // seg_len
    score_scale = HEAD_DIM ** (-0.5)
    head_shape = (HEADS, HEAD_DIM)
    live_rows = valid_flags.astype(jnp.float32)
    rank_full = lax.axis_index("fsdp")
    seg_gathered = (
        lax.all_gather(seg_mats, "fsdp", axis=0, tiled=True),
        lax.all_gather(seg_vecs, "fsdp", axis=0, tiled=True),
    )
    seg_unpacked = unpack_weights(seg_gathered, model_width, ff_width)
    cls_gathered = (
        lax.all_gather(cls_mats, "fsdp", axis=0, tiled=True),
        lax.all_gather(cls_vecs, "fsdp", axis=0, tiled=True),
    )
    cls_unpacked = unpack_weights(cls_gathered, model_width, ff_width)
    seg_allowed = (live_rows.reshape(seg_count, 1, 1, seg_len) > 0.5) | jnp.eye(seg_len, dtype=bool)
    seg_shape = (seg_count, seg_len) + head_shape

    def seg_attend(queries, keys_in, values):
        mixed_rows, log_total = attention_forward(
            queries.reshape(seg_shape),
            keys_in.reshape(seg_shape),
            values.reshape(seg_shape),
            seg_allowed,
            score_scale,
        )
        return (mixed_rows.reshape(tok_rows, model_width), log_total)

    def seg_attend_back(queries, keys_in, values, log_total, grad_mixed):
        grad_parts = attention_backward(
            queries.reshape(seg_shape),
            keys_in.reshape(seg_shape),
            values.reshape(seg_shape),
            seg_allowed,
            score_scale,
            log_total,
            grad_mixed.reshape(seg_shape),
        )
        return tuple(
            (
                grad_part.reshape(tok_rows, model_width).astype(jnp.bfloat16)
                for grad_part in grad_parts
            )
        )

    first_out, seg_saved = block_forward(hidden_in.astype(jnp.float32), seg_unpacked, seg_attend)
    first_grid = first_out.reshape(seg_count, seg_len, model_width)
    position_hot = (seg_nums[:, None] == jnp.arange(seg_pos.shape[0])[None, :]).astype(jnp.float32)
    position_rows = jnp.sum(
        position_hot[:, :, None] * seg_pos.astype(jnp.float32)[None, :, :], axis=1
    )
    heads_in = first_grid[:, 0, :] + position_rows
    lead_live = live_rows.reshape(seg_count, seg_len)[:, 0]
    lead_doc = doc_ids.reshape(seg_count, seg_len)[:, 0]
    lead_labels = jnp.where(lead_live > 0.5, lead_doc, -1).astype(jnp.bfloat16)
    lead_doc_low = lead_doc.astype(jnp.bfloat16)
    bit_count = group_span.bit_length() - 1
    key_total = group_span * seg_count
    own_slot = rank_full % group_span * seg_count + jnp.arange(seg_count)
    query_shape = (1, seg_count) + head_shape
    key_shape = (1, key_total) + head_shape

    def cls_attend(queries, keys_in, values):
        paired = jnp.concatenate([keys_in, values], axis=1)
        labels = lead_labels
        for bit_level in range(bit_count):
            other_pair, other_labels = swapped((paired, labels), "fsdp", bit_level)
            upper_half = rank_full // (1 << bit_level) % 2 == 1
            paired = jnp.where(
                upper_half,
                jnp.concatenate([other_pair, paired]),
                jnp.concatenate([paired, other_pair]),
            )
            labels = jnp.where(
                upper_half,
                jnp.concatenate([other_labels, labels]),
                jnp.concatenate([labels, other_labels]),
            )
        allowed = (labels[None, :] == lead_doc_low[:, None]) | (
            jnp.arange(key_total)[None, :] == own_slot[:, None]
        )
        allowed = allowed[None, None]
        mixed_rows, log_total = attention_forward(
            queries.reshape(query_shape),
            paired[:, :model_width].reshape(key_shape),
            paired[:, model_width:].reshape(key_shape),
            allowed,
            score_scale,
        )
        return (mixed_rows.reshape(seg_count, model_width), (paired, allowed, log_total))

    def cls_attend_back(queries, keys_in, values, attend_kept, grad_mixed):
        paired, allowed, log_total = attend_kept
        grad_query, grad_key, grad_value = attention_backward(
            queries.reshape(query_shape),
            paired[:, :model_width].reshape(key_shape),
            paired[:, model_width:].reshape(key_shape),
            allowed,
            score_scale,
            log_total,
            grad_mixed.reshape(query_shape),
        )
        grad_pair = jnp.concatenate(
            [grad_key.reshape(key_total, model_width), grad_value.reshape(key_total, model_width)],
            axis=1,
        )
        for bit_level in reversed(range(bit_count)):
            half_rows = grad_pair.shape[0] // 2
            upper_half = rank_full // (1 << bit_level) % 2 == 1
            kept_half = jnp.where(upper_half, grad_pair[half_rows:], grad_pair[:half_rows])
            sent_half = jnp.where(upper_half, grad_pair[:half_rows], grad_pair[half_rows:])
            grad_pair = kept_half + swapped(
                sent_half.astype(jnp.bfloat16), "fsdp", bit_level
            ).astype(sent_half.dtype)
        grad_pair = grad_pair.astype(jnp.bfloat16)
        return (
            grad_query.reshape(seg_count, model_width).astype(jnp.bfloat16),
            grad_pair[:, :model_width],
            grad_pair[:, model_width:],
        )

    top_out, cls_saved = block_forward(heads_in, cls_unpacked, cls_attend)
    combined = jnp.concatenate([top_out[:, None, :], first_grid[:, 1:, :]], axis=1).reshape(
        tok_rows, model_width
    )
    output_rows = combined * live_rows[:, None]
    diff_rows = (output_rows - targets.astype(jnp.float32)) * live_rows[:, None]
    count_all, square_all = lax.psum(
        (jnp.sum(live_rows), jnp.sum(diff_rows * diff_rows)), ("rep", "fsdp")
    )
    loss_value = square_all / (count_all * model_width)
    slots_all = tok_rows * lax.axis_size("rep") * lax.axis_size("fsdp")
    grad_grid = (diff_rows * (slots_all / count_all)).reshape(seg_count, seg_len, model_width)
    cls_back = unpack_weights(
        (
            lax.all_gather(cls_mats, "fsdp", axis=0, tiled=True),
            lax.all_gather(cls_vecs, "fsdp", axis=0, tiled=True),
        ),
        model_width,
        ff_width,
    )
    heads_grad, cls_weight_rows, cls_g_vec = block_backward(
        grad_grid[:, 0, :], cls_back, cls_saved, cls_attend_back
    )
    cls_g_qkv, cls_g_out, cls_g_up, cls_g_down = weight_products(cls_weight_rows)
    pos_local = jnp.sum(position_hot[:, :, None] * heads_grad[:, None, :], axis=0)
    seg_grad_out = jnp.concatenate([heads_grad[:, None, :], grad_grid[:, 1:, :]], axis=1).reshape(
        tok_rows, model_width
    )
    seg_back = unpack_weights(
        (
            lax.all_gather(seg_mats, "fsdp", axis=0, tiled=True),
            lax.all_gather(seg_vecs, "fsdp", axis=0, tiled=True),
        ),
        model_width,
        ff_width,
    )
    input_grad, seg_weight_rows, seg_g_vec = block_backward(
        seg_grad_out, seg_back, seg_saved, seg_attend_back
    )
    seg_g_qkv, seg_g_out, seg_g_up, seg_g_down = weight_products(seg_weight_rows)
    owner_rows = tuple(
        (
            lax.psum_scatter(seg_g_qkv, "fsdp", scatter_dimension=0, tiled=True),
            lax.psum_scatter(seg_g_out, "fsdp", scatter_dimension=0, tiled=True),
            lax.psum_scatter(seg_g_up, "fsdp", scatter_dimension=0, tiled=True),
            lax.psum_scatter(seg_g_down, "fsdp", scatter_dimension=0, tiled=True),
            lax.psum_scatter(seg_g_vec, "fsdp", scatter_dimension=0, tiled=True),
            lax.psum_scatter(cls_g_qkv, "fsdp", scatter_dimension=0, tiled=True),
            lax.psum_scatter(cls_g_out, "fsdp", scatter_dimension=0, tiled=True),
            lax.psum_scatter(cls_g_up, "fsdp", scatter_dimension=0, tiled=True),
            lax.psum_scatter(cls_g_down, "fsdp", scatter_dimension=0, tiled=True),
            lax.psum_scatter(cls_g_vec, "fsdp", scatter_dimension=0, tiled=True),
        )
    )
    replica_share = (
        lax.psum_scatter(
            owner_rows[0].astype(jnp.bfloat16), "rep", scatter_dimension=1, tiled=True
        ).astype(jnp.float32),
        lax.psum_scatter(
            owner_rows[1].astype(jnp.bfloat16), "rep", scatter_dimension=1, tiled=True
        ).astype(jnp.float32),
        lax.psum_scatter(
            owner_rows[2].astype(jnp.bfloat16), "rep", scatter_dimension=1, tiled=True
        ).astype(jnp.float32),
        lax.psum_scatter(
            owner_rows[3].astype(jnp.bfloat16), "rep", scatter_dimension=1, tiled=True
        ).astype(jnp.float32),
        lax.psum_scatter(
            owner_rows[4].astype(jnp.bfloat16), "rep", scatter_dimension=0, tiled=True
        ).astype(jnp.float32),
        lax.psum_scatter(
            owner_rows[5].astype(jnp.bfloat16), "rep", scatter_dimension=1, tiled=True
        ).astype(jnp.float32),
        lax.psum_scatter(
            owner_rows[6].astype(jnp.bfloat16), "rep", scatter_dimension=1, tiled=True
        ).astype(jnp.float32),
        lax.psum_scatter(
            owner_rows[7].astype(jnp.bfloat16), "rep", scatter_dimension=1, tiled=True
        ).astype(jnp.float32),
        lax.psum_scatter(
            owner_rows[8].astype(jnp.bfloat16), "rep", scatter_dimension=1, tiled=True
        ).astype(jnp.float32),
        lax.psum_scatter(
            owner_rows[9].astype(jnp.bfloat16), "rep", scatter_dimension=0, tiled=True
        ).astype(jnp.float32),
    )
    all_summed = (
        lax.all_gather(replica_share[0].astype(jnp.bfloat16), "rep", axis=1, tiled=True).astype(
            jnp.float32
        ),
        lax.all_gather(replica_share[1].astype(jnp.bfloat16), "rep", axis=1, tiled=True).astype(
            jnp.float32
        ),
        lax.all_gather(replica_share[2].astype(jnp.bfloat16), "rep", axis=1, tiled=True).astype(
            jnp.float32
        ),
        lax.all_gather(replica_share[3].astype(jnp.bfloat16), "rep", axis=1, tiled=True).astype(
            jnp.float32
        ),
        lax.all_gather(replica_share[4].astype(jnp.bfloat16), "rep", axis=0, tiled=True).astype(
            jnp.float32
        ),
        lax.all_gather(replica_share[5].astype(jnp.bfloat16), "rep", axis=1, tiled=True).astype(
            jnp.float32
        ),
        lax.all_gather(replica_share[6].astype(jnp.bfloat16), "rep", axis=1, tiled=True).astype(
            jnp.float32
        ),
        lax.all_gather(replica_share[7].astype(jnp.bfloat16), "rep", axis=1, tiled=True).astype(
            jnp.float32
        ),
        lax.all_gather(replica_share[8].astype(jnp.bfloat16), "rep", axis=1, tiled=True).astype(
            jnp.float32
        ),
        lax.all_gather(replica_share[9].astype(jnp.bfloat16), "rep", axis=0, tiled=True).astype(
            jnp.float32
        ),
    )
    seg_summed = all_summed[:5]
    cls_summed = all_summed[5:]
    pos_total = lax.psum(pos_local, ("rep", "fsdp"))
    seg_mat_grad = jnp.concatenate(
        [seg_summed[0], seg_summed[1], seg_summed[2], seg_summed[3]], axis=1
    )
    cls_mat_grad = jnp.concatenate(
        [cls_summed[0], cls_summed[1], cls_summed[2], cls_summed[3]], axis=1
    )
    return (
        output_rows.astype(jnp.bfloat16),
        input_grad.astype(jnp.bfloat16),
        seg_mat_grad,
        seg_summed[4],
        cls_mat_grad,
        cls_summed[4],
        pos_total,
        loss_value,
    )


LINE = 4
PLANE = 4
CORES = 2
LANES = 128
GROUP = LINE * PLANE
LOW, WIDE = jnp.bfloat16, jnp.float32
MODEL = HEADS * HEAD_DIM
SPAN = 2 * LANES
TILE_START = (0, 1, 3, 4)


def line_pairs(apart):
    return [(source, (source + apart * PLANE) % GROUP) for source in range(GROUP)]


def plane_pairs(mask):
    return [(source, source ^ mask) for source in range(GROUP)]


def along_line(value, apart):
    return lax.ppermute(value, "fsdp", line_pairs(apart))


def in_plane(value, mask):
    return lax.ppermute(value, "fsdp", plane_pairs(mask))


def other_core(value):
    return lax.ppermute(value, "rep", [(0, 1), (1, 0)])


def after(value, *events):
    return lax.optimization_barrier((value,) + events)[0]


def together(*values):
    return tuple(lax.optimization_barrier(values))


def shape_of(dims, dtype=WIDE):
    return jax.ShapeDtypeStruct(dims, dtype)


def run_kernel(body, name, outs, where, blocks, arrays, scratch=(), far=(), flops=0):
    in_specs = [pl.BlockSpec(memory_space=pltpu.SMEM)]
    in_specs += [pl.BlockSpec(memory_space=pltpu.HBM)] * len(blocks)
    in_specs += [pl.BlockSpec(memory_space=pltpu.VMEM)] * len(arrays)
    spaces = [pltpu.HBM if at in far else pltpu.VMEM for at in range(len(outs))]
    moved = sum(x.size * x.dtype.itemsize for x in list(blocks) + list(arrays))
    moved += sum(math.prod(o.shape) * jnp.dtype(o.dtype).itemsize for o in outs)
    return pl.pallas_call(
        body,
        name=name,
        out_shape=tuple(outs),
        in_specs=in_specs,
        out_specs=tuple(pl.BlockSpec(memory_space=space) for space in spaces),
        scratch_shapes=list(scratch),
        cost_estimate=pl.CostEstimate(flops=flops, bytes_accessed=moved, transcendentals=0),
        compiler_params=pltpu.CompilerParams(vmem_limit_bytes=VMEM_BYTES),
    )(where, *blocks, *arrays)


VMEM_BYTES = 24 * 1024 * 1024
HALF = MODEL // CORES
FF_HALF = FF // CORES
OWN = MODEL // GROUP
QUARTER = 3 * SPAN + 2 * FF // LINE
QUARTER_HALF = QUARTER // CORES


def aligned(start):
    return pl.multiple_of(start, LANES)


def wait_all(copies):
    for copy in copies:
        copy.wait()


def run_copies(pairs, sems):
    copies = [
        pltpu.make_async_copy(source, target, sems.at[at])
        for at, (source, target) in enumerate(pairs)
    ]
    for copy in copies:
        copy.start()
    wait_all(copies)


FIRST = 4 * HALF + LANES
OWN_CUT = FIRST + FF_HALF // 2
LINE_CUTS = (7 * LANES, FF_HALF // 2, FF_HALF // 2)
WIDTHS = (FIRST, FF_HALF, FF_HALF)


def group_pieces(group, refs):
    own, rest = refs[:LINE], refs[LINE:]
    own_x, own_y, far_x, far_y, line_x, line_y, late_x, late_y = rest
    width, cut = WIDTHS[group], LINE_CUTS[group]
    start = sum(WIDTHS[:group])
    if group == 0:
        bases = (sum(WIDTHS) - OWN_CUT, OWN_CUT)
    else:
        before, before_cut = WIDTHS[group - 1], LINE_CUTS[group - 1]
        bases = (2 * before - before_cut, before + before_cut)
    pieces = {(0, step): [(own[step], 0, 0, width)] for step in range(LINE)}
    for mask, whole, line, base in ((1, own_x, line_x, bases[0]), (2, own_y, line_y, bases[1])):
        pieces[mask, 0] = [(whole, start, 0, width)]
        for step in range(1, LINE):
            pieces[mask, step] = [(line, base + (step - 1) * width, 0, width)]
    middle = min(max(OWN_CUT - start, 0), width)
    far = []
    if middle > 0:
        far.append((far_y, start, 0, middle))
    if middle < width:
        far.append((far_x, start + middle - OWN_CUT, middle, width))
    pieces[3, 0] = far
    pieces[3, 1] = [(late_y, 0, 0, width)]
    pieces[3, 2] = [(late_y, width, 0, cut), (late_x, 0, cut, width)]
    pieces[3, 3] = [(late_x, width - cut, 0, width)]
    return pieces


def gather_group(where, group, refs, targets):
    line_at, plane_at = where[0], where[1]
    for (mask, step), parts in group_pieces(group, refs).items():
        chip = (line_at + LINE - step) % LINE * PLANE + (plane_at ^ mask)
        for whole, first, last in targets:
            for ref, offset, begin, end in parts:
                low, high = max(first, begin), min(last, end)
                if low < high:
                    source = slice(offset + low - begin, offset + high - begin)
                    whole[chip, :, low - first : high - first] = ref[:, source]


def gather_blocks(where, refs, base, width, targets):
    line_at, plane_at = where[0], where[1]
    half = LINE // 2
    for mask in range(PLANE):
        for step in range(LINE):
            if mask == 0:
                ref, offset = refs[step], 0
            elif mask == 3:
                ref = refs[LINE + 3] if step < half else refs[LINE + 2]
                offset = step % half * width
            else:
                ref, offset = refs[LINE + mask - 1], base + step * width
            chip = (line_at + LINE - step) % LINE * PLANE + (plane_at ^ mask)
            for whole, first, last in targets:
                whole[chip] = ref[:, offset + first : offset + last]


def whole_rows(ref):
    value = ref[...]
    return value.reshape(value.shape[0] * value.shape[1], value.shape[2])


def prepare_first_kernel(where, seg, seg_vec, cls_vec, flags, out, live_out, sems):
    core_at = where[2]
    pairs = []
    for piece in range(4):
        source = seg.at[:, pl.ds(aligned(piece * MODEL + core_at * HALF), HALF)]
        pairs.append((source, out.at[:, piece * HALF : (piece + 1) * HALF]))
    run_copies(pairs, sems)
    size = seg_vec.shape[0]
    vecs = [vec[...].astype(WIDE).reshape(1, size) for vec in (seg_vec, cls_vec)]
    lines = -(-size // LANES)
    block = jnp.zeros((OWN, LANES), WIDE)
    row_at = lax.broadcasted_iota(jnp.int32, (OWN, LANES), 0)
    for which in range(2):
        for line in range(lines):
            width = min(LANES, size - line * LANES)
            value = vecs[which][:, line * LANES : line * LANES + width]
            if width < LANES:
                value = jnp.concatenate([value, jnp.zeros((1, LANES - width), WIDE)], axis=1)
            block = jnp.where(row_at == which * lines + line, value, block)
    live = flags[...].astype(WIDE).reshape(1, SEG)
    live_out[...] = live
    count = jnp.sum(live, axis=1, keepdims=True)
    block = jnp.where(row_at == 2 * lines, count, block)
    out[:, 4 * HALF :] = block.astype(LOW)


def prepare_rest_kernel(where, seg, cls, *refs):
    second_out, third_out = refs[:2]
    step_outs, out_half, order_out = refs[2 : 2 + LINE], refs[2 + LINE], refs[3 + LINE]
    quarters, sems = refs[4 + LINE :]
    line_at, plane_at, core_at = where[0], where[1], where[2]
    start = core_at * FF_HALF
    pairs = [
        (seg.at[:, pl.ds(aligned(4 * MODEL + start), FF_HALF)], second_out),
        (seg.at[:, pl.ds(aligned(4 * MODEL + FF + start), FF_HALF)], third_out),
        (cls.at[:, pl.ds(aligned(3 * MODEL + core_at * HALF), HALF)], out_half),
    ]
    part = FF // LINE
    for at in range(LINE):
        first = TILE_START[at] * LANES
        plan = [(piece * MODEL + first, SPAN, piece * SPAN) for piece in range(3)]
        plan += [
            (4 * MODEL + piece * FF + at * part, part, 3 * SPAN + piece * part)
            for piece in range(2)
        ]
        for source, size, target in plan:
            pairs.append(
                (
                    cls.at[:, source : source + size],
                    quarters.at[at, :, target : target + size],
                )
            )
    run_copies(pairs, sems)
    lanes = pl.ds(aligned(core_at * QUARTER_HALF), QUARTER_HALF)
    for step, out in enumerate(step_outs):
        out[...] = quarters[(line_at + step) % LINE, :, lanes]
    column = lax.broadcasted_iota(jnp.int32, (1, SPAN), 1)
    feature = lax.broadcasted_iota(jnp.int32, (MODEL, SPAN), 0)
    turn = sum((column >= OWN * step).astype(jnp.int32) for step in range(1, LINE))
    held = column - OWN * turn
    turn = (line_at + turn) % LINE
    for mask in range(PLANE):
        source = (turn * PLANE + (plane_at ^ mask)) * OWN + held
        source = jnp.where(column < OWN * LINE, source, -1)
        order_out[:, mask * SPAN : (mask + 1) * SPAN] = (feature == source).astype(LOW)


def prepare_kernel(where, seg, cls, *refs):
    (seg_vec, cls_vec, flags, first_out, live_out), refs = refs[:5], refs[5:]
    rest, (first_sems, quarters, sems) = refs[:-3], refs[-3:]
    prepare_first_kernel(where, seg, seg_vec, cls_vec, flags, first_out, live_out, first_sems)
    prepare_rest_kernel(where, seg, cls, *rest, quarters, sems)


def lane_mask(rows, head):
    lane = lax.broadcasted_iota(jnp.int32, (rows, LANES), 1)
    return (lane < HEAD_DIM) if head == 0 else (lane >= HEAD_DIM)


def masked(value, mask):
    return jnp.where(mask, value, jnp.zeros_like(value))


def head_probabilities(query, key, allowed):
    scores = product_right(query, key) * HEAD_DIM ** (-0.5)
    scores = jnp.where(allowed, scores, MASK_FILL)
    raised = jnp.exp(scores - jnp.max(scores, axis=-1, keepdims=True))
    return raised / jnp.sum(raised, axis=-1, keepdims=True)


def attend_tiles(qkv, width, allowed):
    rows = qkv.shape[0]
    mixed = []
    for tile in range(width // LANES):
        at = tile * LANES
        query, key, value = (
            qkv[:, piece * width + at : piece * width + at + LANES] for piece in range(3)
        )
        total = jnp.zeros((rows, LANES), WIDE)
        for head in range(2):
            mask = lane_mask(rows, head)
            weights = head_probabilities(masked(query, mask), key, allowed).astype(LOW)
            total = total + product_plain(weights, masked(value, mask))
        mixed.append(total.astype(LOW))
    return mixed


def attend_tiles_back(qkv, grad_mixed, width, allowed):
    rows = qkv.shape[0]
    scale = HEAD_DIM ** (-0.5)
    results = ([], [], [])
    for tile in range(width // LANES):
        at = tile * LANES
        query, key, value = (
            qkv[:, piece * width + at : piece * width + at + LANES] for piece in range(3)
        )
        grad = grad_mixed[:, at : at + LANES]
        totals = [jnp.zeros((rows, LANES), WIDE) for _ in range(3)]
        for head in range(2):
            mask = lane_mask(rows, head)
            query_low, key_low, grad_low = (masked(x, mask) for x in (query, key, grad))
            chance = head_probabilities(query_low, key, allowed)
            grad_chance = product_right(grad_low, value)
            inner = jnp.sum(grad_chance * chance, axis=-1, keepdims=True)
            grad_scores = (chance * (grad_chance - inner)).astype(LOW)
            totals[0] = totals[0] + product_plain(grad_scores, key_low)
            totals[1] = totals[1] + product_left(grad_scores, query_low)
            totals[2] = totals[2] + product_left(chance.astype(LOW), grad_low)
        results[0].append((totals[0] * scale).astype(LOW))
        results[1].append((totals[1] * scale).astype(LOW))
        results[2].append(totals[2].astype(LOW))
    return results[0] + results[1] + results[2]


def token_allowed(live_row):
    shape = (SEG, SEG)
    same = lax.broadcasted_iota(jnp.int32, shape, 0) == lax.broadcasted_iota(jnp.int32, shape, 1)
    return (live_row > 0.5) | same


def qkv_kernel(where, *refs):
    blocks = refs[:12]
    hidden, hidden_got, live_row, live_got, order = refs[12:17]
    weight, out_low, out_high, qkv_out, mixed_out = refs[17:22]
    vectors_out, count_out, ordered_out = refs[22:25]
    vec_rows, flat, inputs, out_half = refs[25:]
    core_at = where[2]
    gather_group(
        where,
        0,
        blocks,
        (
            (weight, 0, 3 * HALF),
            (out_half, 3 * HALF, 4 * HALF),
            (vec_rows, 4 * HALF, 4 * HALF + LANES),
        ),
    )
    out_low[...] = out_half[: GROUP // 2]
    out_high[...] = out_half[GROUP // 2 :]
    piece = (8 * MODEL + FF) // GROUP
    lines = -(-piece // LANES)
    count = jnp.zeros((1, LANES), WIDE)
    for chip in range(GROUP):
        rows = vec_rows[chip, 0:16, :].astype(WIDE)
        for block in range(2):
            joined = jnp.concatenate(
                [rows[block * lines + r : block * lines + r + 1] for r in range(lines)], axis=1
            )
            flat[block : block + 1, chip * piece : (chip + 1) * piece] = joined[:, :piece]
        count = count + rows[2 * lines : 2 * lines + 1]
    rows_each = (8 * MODEL + FF) // MODEL
    for block in range(2):
        for row in range(rows_each):
            vectors_out[block * rows_each + row : block * rows_each + row + 1, :] = flat[
                block : block + 1, row * MODEL : (row + 1) * MODEL
            ]
    count_out[...] = jnp.broadcast_to(count, count_out.shape)
    inputs[:SEG] = hidden[...]
    inputs[SEG:] = hidden_got[...]
    projected = product_plain(inputs[...], whole_rows(weight))
    lanes = pl.ds(aligned(core_at * HALF), HALF)
    qkv_out[:, :HALF] = (projected[:, :HALF] + vectors_out[0:1, lanes]).astype(LOW)
    qkv_out[:, HALF : 2 * HALF] = projected[:, HALF : 2 * HALF].astype(LOW)
    qkv_out[:, 2 * HALF :] = (projected[:, 2 * HALF :] + vectors_out[1:2, lanes]).astype(LOW)
    for part, live in enumerate((live_row, live_got)):
        rows = slice(part * SEG, (part + 1) * SEG)
        tiles = attend_tiles(qkv_out[rows, :], HALF, token_allowed(live[...]))
        for tile, value in enumerate(tiles):
            mixed_out[rows, tile * LANES : (tile + 1) * LANES] = value
    ordered_out[...] = product_plain(inputs[...], order[...]).astype(LOW)


def norm_rows(summed):
    row_mean = jnp.mean(summed, axis=-1, keepdims=True)
    centered = summed - row_mean
    inv_dev = lax.rsqrt(jnp.mean(centered * centered, axis=-1, keepdims=True) + NORM_EPS)
    return centered * inv_dev, inv_dev


def norm_rows_back(grad_out, normed, inv_dev, gain):
    scaled = grad_out * gain
    mean_one = jnp.mean(scaled, axis=-1, keepdims=True)
    mean_two = jnp.mean(scaled * normed, axis=-1, keepdims=True)
    return inv_dev * (scaled - mean_one - normed * mean_two)


def column_sum(value):
    return jnp.sum(value.astype(WIDE), axis=0, keepdims=True)


def four_rows(vectors, first):
    return jnp.concatenate([vectors[first + at : first + at + 1, :] for at in range(4)], axis=1)


def gelu_both(before):
    half = 0.5 * (1.0 + lax.erf(before * SQRT_HALF))
    slope = half + before * jnp.exp(-0.5 * before * before) * INV_SQRT_TWO_PI
    return before * half, slope


def out_kernel(where, hidden, mixed, mixed_got, low, high, low_got, high_got, *refs):
    vectors, order, full_out, ordered_out, normed_out, inv_out, low_out, mixed_full = refs
    core_at = where[2]
    own, other = aligned(core_at * HALF), aligned((1 - core_at) * HALF)
    rows = MODEL // 2
    full_out[:rows, pl.ds(own, HALF)] = whole_rows(low)
    full_out[rows:, pl.ds(own, HALF)] = whole_rows(high)
    full_out[:rows, pl.ds(other, HALF)] = whole_rows(low_got)
    full_out[rows:, pl.ds(other, HALF)] = whole_rows(high_got)
    mixed_full[:, pl.ds(own, HALF)] = mixed[...]
    mixed_full[:SEG, pl.ds(other, HALF)] = mixed_got[SEG:, :]
    mixed_full[SEG:, pl.ds(other, HALF)] = mixed_got[:SEG, :]
    branch = product_plain(mixed_full[:SEG, :], full_out[...])
    normed, inv_dev = norm_rows(hidden[...].astype(WIDE) + branch + vectors[2:3, :])
    normed_out[...] = normed
    inv_out[...] = inv_dev
    low_out[...] = (normed * vectors[4:5, :] + vectors[5:6, :]).astype(LOW)
    ordered_out[...] = product_plain(mixed_full[...], order[...]).astype(LOW)


def up_kernel(where, *refs):
    blocks = refs[:12]
    low, low_got, vectors = refs[12:15]
    weight, act_out, slope_out, both = refs[15:]
    core_at = where[2]
    gather_group(where, 1, blocks, ((weight, 0, FF_HALF),))
    both[:SEG] = low[...]
    both[SEG:] = low_got[...]
    for at in range(FF_HALF // MODEL):
        columns = slice(at * MODEL, (at + 1) * MODEL)
        held = weight[:, :, columns]
        before = product_plain(both[...], held.reshape(MODEL, MODEL))
        bias = vectors[pl.ds(8 + core_at * (FF_HALF // MODEL) + at, 1), :]
        value, slope = gelu_both(before + bias)
        act_out[:, columns] = value.astype(LOW)
        slope_out[:, columns] = slope


def down_kernel(where, *refs):
    blocks, act = refs[:12], refs[12]
    weight, own_out, send_out = refs[13:]
    gather_group(where, 2, blocks, ((weight, 0, FF_HALF),))
    partial = product_right(act[...], whole_rows(weight))
    own_out[...] = partial[:SEG]
    send_out[...] = partial[SEG:]


def seg_rows_kernel(where, *refs):
    own, got, normed_first, vectors, targets, live, seg_pos = refs[:7]
    normed_out, inv_out, diff_out, rows_out, head_out = refs[7:]
    doc, number = where[3], where[4]
    first = normed_first[...] * vectors[4:5, :] + vectors[5:6, :]
    normed, inv_dev = norm_rows(first + own[...] + got[...] + vectors[3:4, :])
    normed_out[...] = normed
    inv_out[...] = inv_dev
    rows = normed * vectors[6:7, :] + vectors[7:8, :]
    shape = (SEG, SEG)
    same = lax.broadcasted_iota(jnp.int32, shape, 0) == lax.broadcasted_iota(jnp.int32, shape, 1)
    live_rows = jnp.sum(jnp.where(same, live[...], 0.0), axis=1, keepdims=True)
    target_rows = targets[...].astype(WIDE)
    output = rows * live_rows
    rows_out[...] = output
    diff = (output - target_rows) * live_rows
    row_at = lax.broadcasted_iota(jnp.int32, (SEG, 1), 0)
    diff = jnp.where(row_at > 0, diff, 0.0)
    diff_out[...] = diff
    table = seg_pos[...].astype(WIDE)
    chosen = lax.broadcasted_iota(jnp.int32, table.shape, 0) == number
    position = jnp.sum(jnp.where(chosen, table, 0.0), axis=0, keepdims=True)
    head_out[:, :MODEL] = rows[0:1, :] + position
    head_out[:, MODEL : 2 * MODEL] = target_rows[0:1, :]
    square = jnp.sum(column_sum(diff * diff), axis=1, keepdims=True)
    lane = lax.broadcasted_iota(jnp.int32, (1, LANES), 1)
    facts = jnp.where(lane == 0, live_rows[0:1, :], 0.0)
    facts = jnp.where(lane == 1, doc.astype(WIDE), facts)
    facts = jnp.where(lane == 2, number.astype(WIDE), facts)
    facts = jnp.where(lane == 3, square, facts)
    head_out[:, 2 * MODEL :] = facts


def second_norm_kernel(where, *refs):
    diff, count, normed, inv_dev, vectors, first, first_got, order = refs[:8]
    grad_out, low_out, sums_out, ordered_out, both = refs[8:]
    grad_top = diff[...] * ((SEG * GROUP * CORES) / count[0:1, 0:1])
    normed_rows = normed[...]
    grad = norm_rows_back(grad_top, normed_rows, inv_dev[...], vectors[6:7, :])
    low = grad.astype(LOW)
    grad_out[...] = grad
    low_out[...] = low
    sums_out[0:1, :] = column_sum(low)
    sums_out[1:2, :] = column_sum(grad_top * normed_rows)
    sums_out[2:3, :] = column_sum(grad_top)
    both[:SEG] = first[...]
    both[SEG:] = first_got[...]
    ordered_out[...] = product_plain(both[...], order[...]).astype(LOW)


def mlp_back_kernel(where, *refs):
    low, low_got, down_weight, up_weight, slope = refs[:5]
    pre_out, own_out, send_out, sums_out, both = refs[5:]
    both[:SEG] = low[...]
    both[SEG:] = low_got[...]
    for at in range(FF_HALF // MODEL):
        columns = slice(at * MODEL, (at + 1) * MODEL)
        held = down_weight[:, :, columns]
        before = product_plain(both[...], held.reshape(MODEL, MODEL))
        pre = (before * slope[:, columns]).astype(LOW)
        pre_out[:, columns] = pre
        sums_out[at : at + 1, :] = column_sum(pre)
    partial = product_right(pre_out[...], whole_rows(up_weight))
    own_out[...] = partial[:SEG]
    send_out[...] = partial[SEG:]


def scatter_parts(where, parts, outs, sems):
    line_at, plane_at = where[0], where[1]
    far_low, far_high, to_x, to_y, kept = outs
    half = LINE // 2
    copies = []
    for mask in range(PLANE):
        for step in range(LINE):
            source = parts.at[(line_at + step) % LINE * PLANE + (plane_at ^ mask)]
            if mask == 3:
                target = far_low.at[step] if step < half else far_high.at[step - half]
            else:
                target = (kept, to_x, to_y)[mask].at[step]
            copies.append(pltpu.make_async_copy(source, target, sems.at[len(copies)]))
    for copy in copies:
        copy.start()
    wait_all(copies)


def mlp_products(refs, masks, both, store):
    first, second, second_got, pre, act, order = refs
    both[:SEG] = second[...]
    both[SEG:] = second_got[...]
    for mask in masks:
        lanes = slice(mask * SPAN, (mask + 1) * SPAN)
        turned = product_plain(both[...], order[:, lanes]).astype(LOW)
        for at, (left, right) in enumerate(((first[:, lanes], pre), (turned, act))):
            for piece in range(FF_HALF // MODEL):
                start = piece * MODEL
                product = product_left(left, right[:, start : start + MODEL])
                product = product[: LINE * OWN].astype(LOW).reshape(LINE, OWN, MODEL)
                target = at * FF_HALF + start
                store(mask, slice(target, target + MODEL), product)


def mlp_far_kernel(where, *refs):
    low_out, high_out, both = refs[6:]
    half = LINE // 2

    def store(mask, columns, product):
        low_out[:, :, columns] = product[:half]
        high_out[:, :, columns] = product[half:]

    mlp_products(refs[:6], (3,), both, store)


def mlp_near_kernel(where, *refs):
    outs, both = refs[6:9], refs[9]

    def store(mask, columns, product):
        outs[mask - 1][:, :, columns] = product

    mlp_products(refs[:6], (1, 2, 0), both, store)


def attn_product(where, refs, mask, piece):
    hidden, mixed, proj, branch, got = refs
    lanes = slice(mask * SPAN, (mask + 1) * SPAN)
    if piece < 3:
        right = proj[:, piece * HALF : (piece + 1) * HALF]
        product = product_left(hidden[:, lanes], right)
    else:
        own = branch[:, pl.ds(aligned(where[2] * HALF), HALF)]
        product = product_left(mixed[:SEG, lanes], own)
        product = product + product_left(mixed[SEG:, lanes], got[:, HALF:])
    return product[: LINE * OWN].astype(LOW).reshape(LINE, OWN, HALF)


def attn_far_kernel(where, *refs):
    low_out, high_out = refs[5:]
    half = LINE // 2
    for piece in range(4):
        columns = slice(piece * HALF, (piece + 1) * HALF)
        product = attn_product(where, refs[:5], 3, piece)
        low_out[:, :, columns] = product[:half]
        high_out[:, :, columns] = product[half:]


def attn_near_kernel(where, *refs):
    proj, (top_row, out_rows, live_row) = refs[2], refs[5:8]
    weight, sums_first, sums_second, sums_up, head_top, head_normed, data = refs[8:15]
    x_out, y_out, kept_out, output_out, own_out, send_out, payload_out, rows = refs[15:]
    core_at = where[2]
    partial = product_right(proj[...], whole_rows(weight))
    own_out[...] = partial[:SEG]
    send_out[...] = partial[SEG:]
    row_at = lax.broadcasted_iota(jnp.int32, (SEG, 1), 0)
    output = jnp.where(row_at == 0, top_row[...] * live_row[:, 0:1], out_rows[...])
    output_out[...] = output.astype(LOW)
    for mask, out in ((1, x_out), (2, y_out), (0, kept_out)):
        for piece in range(4):
            columns = slice(piece * HALF, (piece + 1) * HALF)
            out[:, :, columns] = attn_product(where, refs[:5], mask, piece)
    lanes = pl.ds(aligned(core_at * HALF), HALF)
    rows[...] = jnp.zeros_like(rows)
    rows[0:12, :] = data[0:12, :]
    rows[12:13, lanes] = column_sum(proj[:, :HALF])
    rows[13:14, lanes] = column_sum(proj[:, 2 * HALF :])
    rows[14:15, :] = sums_first[0:1, :]
    rows[15:16, :] = sums_second[0:1, :] + data[2:3, :]
    rows[16:18, :] = sums_first[1:3, :]
    rows[18:19, :] = sums_second[1:2, :] + head_top[...] * head_normed[0:1, :]
    rows[19:20, :] = sums_second[2:3, :] + head_top[...]
    for at in range(FF_HALF // MODEL):
        total = sums_up[at : at + 1, :] + data[4 + 2 * at : 5 + 2 * at, :]
        total = total + data[5 + 2 * at : 6 + 2 * at, :]
        rows[pl.ds(20 + core_at * (FF_HALF // MODEL) + at, 1), :] = total
    payload_out[...] = rows[...].astype(LOW)


def fold_kernel(where, kept, got_x, got_y, *refs):
    extra, own_out, sent = refs[: -LINE], refs[-LINE], refs[1 - LINE :]
    rows = kept.shape[1]
    for step in range(LINE):
        total = kept[step].astype(WIDE) + got_x[step].astype(WIDE) + got_y[step].astype(WIDE)
        if step == 0:
            own_out[...] = total
            continue
        out = sent[step - 1]
        out[:rows, :] = total.astype(LOW)
        if extra:
            out[rows:, :] = jnp.zeros_like(out[rows:, :])
            out[rows:, : extra[0].shape[1]] = extra[0][...]


def reduce_far(parts):
    return together(in_plane(parts[0], 2), in_plane(parts[1], 1))


def reduce_add(where, parts, far):
    shape = parts[2].shape
    return run_kernel(
        add_far_kernel,
        "add_far",
        [shape_of(shape, LOW)] * 2,
        where,
        (),
        tuple(far) + (parts[2], parts[3]),
    )


def reduce_fold(where, kept, got, *extra):
    _, rows, columns = kept.shape
    more = sum(value.shape[0] for value in extra)
    return run_kernel(
        fold_kernel,
        "fold",
        [shape_of((rows, columns))] + [shape_of((rows + more, columns), LOW)] * (LINE - 1),
        where,
        (),
        (kept,) + tuple(got) + extra,
    )


def reduce_line(own, pieces):
    total = own
    for piece in pieces:
        total = total + piece[: own.shape[0]].astype(WIDE)
    return total


def head_back_kernel(where, *refs):
    grad, grad_got, down_weight, up_weight, slope, act, low, low_got = refs[:8]
    own_out, send_out, data_out = refs[8:]
    few = 16
    row_at = lax.broadcasted_iota(jnp.int32, (few, 1), 0)

    def two_rows(first, second):
        return jnp.where(row_at == 0, first, jnp.where(row_at == 1, second, 0.0))

    second = two_rows(grad[...], grad_got[...]).astype(LOW)
    data_out[0:1, :] = low[0:1, :].astype(WIDE)
    data_out[1:2, :] = low_got[0:1, :].astype(WIDE)
    data_out[2:4, :] = second[0:2].astype(WIDE)
    partial = jnp.zeros((few, MODEL), WIDE)
    for at in range(FF_HALF // MODEL):
        columns = slice(at * MODEL, (at + 1) * MODEL)
        before = product_plain(second, down_weight[:, :, columns].reshape(MODEL, MODEL))
        slopes = two_rows(slope[0:1, columns], slope[SEG : SEG + 1, columns])
        pre = (before * slopes).astype(LOW)
        partial = partial + product_right(pre, up_weight[:, :, columns].reshape(MODEL, MODEL))
        data_out[4 + 2 * at : 6 + 2 * at, :] = pre[0:2].astype(WIDE)
        data_out[8 + 2 * at : 9 + 2 * at, :] = act[0:1, columns].astype(WIDE)
        data_out[9 + 2 * at : 10 + 2 * at, :] = act[SEG : SEG + 1, columns].astype(WIDE)
    own_out[...] = partial[0:1]
    send_out[...] = partial[1:2]


def first_norm_kernel(where, *refs):
    second_grad, own, got, head_grad, head_own, head_got = refs[:6]
    normed_rows, inv_dev, vectors, out_weight = refs[6:10]
    grad_out, branch_out, mixed_out, send_out, sums_out = refs[10:]
    core_at = where[2]
    grad_rows = second_grad[...] + own[...] + got[...]
    head = head_grad[...] + head_own[...] + head_got[...]
    row_at = lax.broadcasted_iota(jnp.int32, (SEG, 1), 0)
    grad_rows = jnp.where(row_at == 0, head, grad_rows)
    normed = normed_rows[...]
    grad = norm_rows_back(grad_rows, normed, inv_dev[...], vectors[4:5, :])
    grad_out[...] = grad
    branch = grad.astype(LOW)
    branch_out[...] = branch
    mixed_out[...] = product_right(branch, out_weight[...]).astype(LOW)
    other = pl.ds(aligned((1 - core_at) * HALF), HALF)
    send_out[:, :HALF] = mixed_out[:, other]
    send_out[:, HALF:] = branch_out[:, other]
    sums_out[0:1, :] = column_sum(branch)
    sums_out[1:2, :] = column_sum(grad_rows * normed)
    sums_out[2:3, :] = column_sum(grad_rows)


def attn_back_kernel(where, *refs):
    qkv, mixed_grad, got, live_row, live_got, proj_out = refs
    core_at = where[2]
    lanes = pl.ds(aligned(core_at * HALF), HALF)
    for part, live in enumerate((live_row, live_got)):
        at = slice(part * SEG, (part + 1) * SEG)
        grad = mixed_grad[:, lanes] if part == 0 else got[:, :HALF]
        pieces = attend_tiles_back(qkv[at, :], grad, HALF, token_allowed(live[...]))
        for tile, value in enumerate(pieces):
            proj_out[at, tile * LANES : (tile + 1) * LANES] = value


def cls_gather_kernel(where, *refs):
    blocks = refs[:8]
    own_out, from_x, from_y, far_x = refs[8], refs[4], refs[5], refs[6]
    weight_out, out_rows = refs[9:]
    plane_at = where[1]
    gather_blocks(where, blocks, 0, QUARTER_HALF, ((weight_out, 0, QUARTER_HALF),))
    first = LINE * QUARTER_HALF
    out_rows[plane_at] = own_out[...]
    out_rows[plane_at ^ 1] = from_x[:, first : first + HALF]
    out_rows[plane_at ^ 2] = from_y[:, first : first + HALF]
    first = LINE // 2 * QUARTER_HALF
    out_rows[plane_at ^ 3] = far_x[:, first : first + HALF]


def cls_weight_kernel(where, own, got, out_half, out_got, weight_out, out_full):
    line_at, core_at = where[0], where[2]
    out_full[...] = jnp.zeros_like(out_full)
    for value, part, core in ((own, out_half, core_at), (got, out_got, 1 - core_at)):
        weight_out[:, :, pl.ds(aligned(core * QUARTER_HALF), QUARTER_HALF)] = value[...]
        rows = part[...].reshape(3, HEAD_DIM, HALF)
        out_full[pl.ds(line_at % 2, 3), :, pl.ds(aligned(core * HALF), HALF)] = rows


def add_far_kernel(where, far_low, far_high, to_x, to_y, x_out, y_out):
    half = LINE // 2
    x_out[:half] = to_x[:half] + far_low[...]
    x_out[half:] = to_x[half:]
    y_out[:half] = to_y[:half]
    y_out[half:] = to_y[half:] + far_high[...]


def row_from_column(column, size):
    shape = (size, size)
    same = lax.broadcasted_iota(jnp.int32, shape, 0) == lax.broadcasted_iota(jnp.int32, shape, 1)
    return jnp.sum(jnp.where(same, column, 0.0), axis=0, keepdims=True)


def head_allowed(heads):
    facts = heads[:, 2 * MODEL :]
    live, doc = facts[:, 0:1], facts[:, 1:2]
    shape = (GROUP, GROUP)
    same = lax.broadcasted_iota(jnp.int32, shape, 0) == lax.broadcasted_iota(jnp.int32, shape, 1)
    live_row, doc_row = row_from_column(live, GROUP), row_from_column(doc, GROUP)
    return ((live_row > 0.5) & (doc == doc_row)) | same


def quarter_mask(quarter):
    lane = lax.broadcasted_iota(jnp.int32, (GROUP, SPAN), 1)
    first = (quarter % 2) * HEAD_DIM
    return (lane >= first) & (lane < first + 3 * HEAD_DIM)


def quarter_piece(vectors, row, quarter):
    value = jnp.zeros((1, SPAN), WIDE)
    for at in range(LINE):
        first = TILE_START[at] * LANES
        value = jnp.where(quarter == at, vectors[row : row + 1, first : first + SPAN], value)
    return value


def cls_attend_kernel(where, *refs):
    stacks, vectors, weight, out_weight = refs[:4], refs[4], refs[5], refs[6]
    heads_out, qkv_out, mixed_out, part_out = refs[7:]
    line_at, plane_at = where[0], where[1]
    for step, stack in enumerate(stacks):
        for mask in range(PLANE):
            row = (line_at + LINE - step) % LINE * PLANE + (plane_at ^ mask)
            heads_out[pl.ds(row, 1), :] = stack[mask : mask + 1, :]
    heads = heads_out[...]
    inputs = heads[:, :MODEL].astype(LOW)
    projected = product_plain(inputs, weight[:, : 3 * SPAN])
    query = projected[:, :SPAN] + quarter_piece(vectors, 12, line_at)
    value = projected[:, 2 * SPAN :] + quarter_piece(vectors, 13, line_at)
    qkv_out[:, :SPAN] = query.astype(LOW)
    qkv_out[:, SPAN : 2 * SPAN] = projected[:, SPAN : 2 * SPAN].astype(LOW)
    qkv_out[:, 2 * SPAN :] = value.astype(LOW)
    mixed = attend_tiles(qkv_out[...], SPAN, head_allowed(heads))
    mixed = masked(jnp.concatenate(mixed, axis=1), quarter_mask(line_at))
    mixed_out[...] = mixed
    part_out[...] = product_plain(mixed, out_weight[...])


def cls_mlp_kernel(where, *refs):
    heads, own, got_one, got_two, got_three, vectors, weight = refs[:7]
    normed_out, inv_out, low_out, act_out, slope_out, part_out = refs[7:]
    line_at = where[0]
    branch = own[...] + got_one[...] + got_two[...] + got_three[...]
    normed, inv_dev = norm_rows(heads[:, :MODEL] + branch + vectors[14:15, :])
    normed_out[...] = normed
    inv_out[...] = inv_dev
    low = (normed * vectors[16:17, :] + vectors[17:18, :]).astype(LOW)
    low_out[...] = low
    part = FF // LINE
    first = 3 * SPAN
    bias = vectors[pl.ds(20 + line_at, 1), :]
    before = product_plain(low, weight[:, first : first + part]) + bias
    value, slope = gelu_both(before)
    act = value.astype(LOW)
    act_out[...] = act
    slope_out[...] = slope
    part_out[...] = product_right(act, weight[:, first + part :])


def cls_top_kernel(where, *refs):
    heads, own, got_one, got_two, got_three, vectors, weight = refs[:7]
    normed_first, count, slope = refs[7:10]
    top_out, square_out, grad_out, second_out, pre_out, part_out, sums_out = refs[10:17]
    held = refs[17]
    rank = where[0] * PLANE + where[1]
    first = normed_first[...] * vectors[16:17, :] + vectors[17:18, :]
    down = own[...] + got_one[...] + got_two[...] + got_three[...]
    normed, inv_dev = norm_rows(first + down + vectors[15:16, :])
    rows = normed * vectors[18:19, :] + vectors[19:20, :]
    held[...] = rows
    top_out[...] = held[pl.ds(rank, 1), :]
    facts = heads[:, 2 * MODEL :]
    live = facts[:, 0:1]
    diff = (rows * live - heads[:, MODEL : 2 * MODEL]) * live
    square = jnp.sum(column_sum(diff * diff), axis=1, keepdims=True)
    square = square + jnp.sum(facts[:, 3:4], axis=0, keepdims=True)
    square_out[...] = jnp.broadcast_to(square, square_out.shape)
    grad_top = diff * ((SEG * GROUP * CORES) / count[0:1, 0:1])
    grad = norm_rows_back(grad_top, normed, inv_dev, vectors[18:19, :])
    sums_out[0:1, :] = column_sum(grad_top * normed)
    sums_out[1:2, :] = column_sum(grad_top)
    grad_out[...] = grad
    second = grad.astype(LOW)
    second_out[...] = second
    part = FF // LINE
    at = 3 * SPAN
    pre = (product_plain(second, weight[:, at + part :]) * slope[...]).astype(LOW)
    pre_out[...] = pre
    part_out[...] = product_right(pre, weight[:, at : at + part])


def cls_attend_back_kernel(where, *refs):
    heads, own, got_one, got_two, got_three, vectors, weight, out_weight = refs[:8]
    grad_in, normed_first, inv_first, qkv = refs[8:12]
    grad_out, branch_out, proj_out, part_out, sums_out = refs[12:]
    line_at = where[0]
    grad_first = grad_in[...] + own[...] + got_one[...] + got_two[...] + got_three[...]
    normed = normed_first[...]
    grad = norm_rows_back(grad_first, normed, inv_first[...], vectors[16:17, :])
    sums_out[0:1, :] = column_sum(grad_first * normed)
    sums_out[1:2, :] = column_sum(grad_first)
    grad_out[...] = grad
    branch = grad.astype(LOW)
    branch_out[...] = branch
    mask = quarter_mask(line_at)
    mixed_grad = masked(product_right(branch, out_weight[...]).astype(LOW), mask)
    pieces = attend_tiles_back(qkv[...], mixed_grad, SPAN, head_allowed(heads[...]))
    tiles = SPAN // LANES
    for piece in range(3):
        joined = jnp.concatenate(pieces[piece * tiles : (piece + 1) * tiles], axis=1)
        proj_out[:, piece * SPAN : (piece + 1) * SPAN] = masked(joined, mask)
    part_out[...] = product_right(proj_out[...], weight[:, : 3 * SPAN])


def cls_end_kernel(where, *refs):
    heads, grad, own, got_one, got_two, got_three = refs[:6]
    square, sums_back, sums_top = refs[6:9]
    normed_second, inv_second, vectors = refs[9:12]
    row_out, second_out, shared_out, held = refs[12:]
    rank = where[0] * PLANE + where[1]
    total = grad[...] + own[...] + got_one[...] + got_two[...] + got_three[...]
    held[...] = total
    row = held[pl.ds(rank, 1), :]
    row_out[...] = row
    second_out[...] = norm_rows_back(
        row, normed_second[0:1, :], inv_second[0:1, :], vectors[6:7, :]
    )
    number = row_from_column(heads[:, 2 * MODEL + 2 : 2 * MODEL + 3], GROUP)
    entry = lax.broadcasted_iota(jnp.int32, (GROUP, GROUP), 0).astype(WIDE)
    hot = (entry == number).astype(WIDE)
    shared_out[0:GROUP, :] = jnp.dot(hot, total, precision=lax.Precision.HIGHEST)
    shared_out[GROUP : GROUP + 1, 0:LANES] = square[0:1, :]
    shared_out[GROUP + 1 : GROUP + 3, :] = sums_back[0:2, :]
    shared_out[GROUP + 3 : GROUP + 5, :] = sums_top[0:2, :]


def head_mlp_kernel(where, *refs):
    cls_mlp_kernel(where, *refs[:7], *refs[11:17])
    add_far_kernel(where, *refs[7:11], *refs[17:])


def head_end_kernel(where, *refs):
    cls_end_kernel(where, *refs[:12], *refs[16:19], refs[23])
    fold_kernel(where, *refs[12:16], *refs[19:23])


def attn_add_kernel(where, *refs):
    far_low, far_high, to_x, to_y, grad, own, got, x_out, y_out, input_out = refs
    add_far_kernel(where, far_low, far_high, to_x, to_y, x_out, y_out)
    input_out[...] = (grad[...] + own[...] + got[...]).astype(LOW)


def rows_input_kernel(where, *refs):
    cls_rows_kernel(where, *refs[:8], refs[11], refs[13])
    grad, own, got, input_out = refs[8], refs[9], refs[10], refs[12]
    input_out[...] = (grad[...] + own[...] + got[...]).astype(LOW)


def cls_rows_kernel(where, *refs):
    packs = refs[:4]
    heads, branch, low, second = refs[4:8]
    out, kept = refs[8:]
    line_at = where[0]
    rows, width = kept.shape[1:]
    for step, pack in enumerate(packs):
        first = pack.shape[0] - rows
        kept[(line_at + LINE - step) % LINE] = pack[first:, :width]
    starts = (MODEL, 2 * MODEL, 3 * MODEL, 4 * MODEL)
    out[:, 0:MODEL] = heads[:, :MODEL].astype(LOW)
    for piece, start in enumerate(starts):
        from_at = piece * SPAN
        for tile in range(MODEL // LANES):
            total = None
            for at in range(PLANE):
                inner = tile - TILE_START[at]
                if inner in (0, 1):
                    first = from_at + inner * LANES
                    value = kept[at, :, first : first + LANES]
                    total = value if total is None else total + value
            out[:, start + tile * LANES : start + (tile + 1) * LANES] = total
    out[:, 5 * MODEL : 6 * MODEL] = branch[...]
    out[:, 6 * MODEL : 7 * MODEL] = low[...]
    out[:, 7 * MODEL + FF : 8 * MODEL + FF] = second[...]
    part = FF // LINE
    for at in range(PLANE):
        first = 4 * SPAN
        out[:, 7 * MODEL + at * part : 7 * MODEL + (at + 1) * part] = kept[
            at, :, first : first + part
        ]
        out[:, 8 * MODEL + FF + at * part : 8 * MODEL + FF + (at + 1) * part] = kept[
            at, :, first + part : first + 2 * part
        ]


def own_features(rank, width):
    shape = (MODEL, width)
    feature = lax.broadcasted_iota(jnp.int32, shape, 0)
    column = lax.broadcasted_iota(jnp.int32, shape, 1)
    return (feature == rank * width + column).astype(LOW)


def own_vector(rank, pieces, out, flat):
    size = out.shape[0]
    for at, piece in enumerate(pieces):
        flat[:, at * MODEL : (at + 1) * MODEL] = piece
    value = jnp.zeros((1, size), WIDE)
    for chip in range(GROUP):
        value = jnp.where(rank == chip, flat[:, chip * size : (chip + 1) * size], value)
    out[...] = value.reshape(size)


def cls_owner_kernel(where, *refs):
    own, got, shared, mats_out, vec_out, rows, flat = refs
    rank = where[0] * PLANE + where[1]
    width = mats_out.shape[0]
    rows[:GROUP] = own[...]
    rows[GROUP:] = got[...]
    chosen = own_features(rank, width)
    plan = (
        (0, MODEL, 3 * MODEL, 0),
        (4 * MODEL, 5 * MODEL, MODEL, 3 * MODEL),
        (6 * MODEL, 7 * MODEL, FF, 4 * MODEL),
        (7 * MODEL + FF, 8 * MODEL + FF, FF, 4 * MODEL + FF),
    )
    for left, right, size, target in plan:
        side = product_plain(rows[:, left : left + MODEL], chosen).astype(LOW)
        mats_out[:, target : target + size] = product_left(side, rows[:, right : right + size])
    starts = (MODEL, 3 * MODEL, 5 * MODEL, 7 * MODEL + FF)
    pieces = [column_sum(rows[:, start : start + MODEL]) for start in starts]
    pieces += [shared[GROUP + 1 + at : GROUP + 2 + at, :] for at in range(4)]
    starts = [7 * MODEL + at * MODEL for at in range(FF // MODEL)]
    pieces += [column_sum(rows[:, start : start + MODEL]) for start in starts]
    own_vector(rank, pieces, vec_out, flat)


def head_share_kernel(where, *refs):
    packs, mlp = refs[:4], refs[4]
    mine_out, vecs_out, rows = refs[5:]
    rank = where[0] * PLANE + where[1]
    count = LINE * 24
    for at, pack in enumerate(packs):
        rows[at * count : (at + 1) * count] = pack[...]
    total = PLANE * count

    def chosen(base, apart):
        shape = (CORES * GROUP, total)
        row = lax.broadcasted_iota(jnp.int32, shape, 0)
        column = lax.broadcasted_iota(jnp.int32, shape, 1)
        hot = (column == row // 2 * 24 + base + row % 2 * apart).astype(LOW)
        return product_plain(hot, rows[...]).astype(LOW)

    own = own_features(rank, OWN)
    for at, (left, right) in enumerate(((0, 4), (2, 8))):
        side = product_plain(chosen(left, 1), own).astype(LOW)
        for piece in range(FF_HALF // MODEL):
            columns = slice(at * FF_HALF + piece * MODEL, at * FF_HALF + (piece + 1) * MODEL)
            share = product_left(side, chosen(right + 2 * piece, 1))
            mine_out[:, columns] = mlp[:, columns] + share
    shape = (16, total)
    row = lax.broadcasted_iota(jnp.int32, shape, 0)
    column = lax.broadcasted_iota(jnp.int32, shape, 1)
    hot = ((column % 24 == row + 12) & (row < 12)).astype(LOW)
    vecs_out[...] = product_plain(hot, rows[...])


def share_owner_kernel(where, *refs):
    head_share_kernel(where, *refs[:5], *refs[9:11], refs[15])
    cls_owner_kernel(where, *refs[5:8], *refs[11:13], *refs[16:])
    shared, count, pos_out, loss_out = refs[7], refs[8], refs[13], refs[14]
    pos_out[...] = shared[:GROUP, :]
    loss_out[...] = shared[GROUP : GROUP + 1, 0:1] / (count[0:1, 0:1] * MODEL)


def seg_vec_kernel(where, vecs, vecs_got, vec_out, flat):
    rank = where[0] * PLANE + where[1]
    rows = (8 * MODEL + FF) // MODEL
    pieces = [vecs[at : at + 1, :] + vecs_got[at : at + 1, :] for at in range(rows)]
    own_vector(rank, pieces, vec_out, flat)


def column_copies(where, out, base, size, own, got, first):
    core_at = where[2]
    lanes = slice(first, first + size)
    return [
        (own.at[:, lanes], out.at[:, pl.ds(aligned(base + core_at * size), size)]),
        (got.at[:, lanes], out.at[:, pl.ds(aligned(base + (1 - core_at) * size), size)]),
    ]


def store_kernel(where, attn, attn_got, mlp, mlp_got, vecs, vecs_got, out, vec_out, flat, sems):
    pairs = []
    for piece in range(4):
        pairs += column_copies(where, out, piece * MODEL, HALF, attn, attn_got, piece * HALF)
    for piece in range(2):
        base = 4 * MODEL + piece * FF
        pairs += column_copies(where, out, base, FF_HALF, mlp, mlp_got, piece * FF_HALF)
    copies = [
        pltpu.make_async_copy(source, target, sems.at[at])
        for at, (source, target) in enumerate(pairs)
    ]
    for copy in copies:
        copy.start()
    seg_vec_kernel(where, vecs, vecs_got, vec_out, flat)
    wait_all(copies)


def plane_parts(part):
    return (part,) + together(*(in_plane(part, mask) for mask in range(1, PLANE)))


def line_parts(part):
    return (part,) + together(*(along_line(part, apart) for apart in range(1, LINE)))


def slice_local(
    hidden_in,
    targets,
    doc_ids,
    seg_nums,
    valid_flags,
    seg_mats,
    seg_vecs,
    cls_mats,
    cls_vecs,
    seg_pos,
):
    rank, core_at = lax.axis_index("fsdp"), lax.axis_index("rep")
    line_at, plane_at = rank // PLANE, rank % PLANE
    where = jnp.stack([line_at, plane_at, core_at, doc_ids[0], seg_nums[0]]).astype(jnp.int32)
    own_rows, total_columns = seg_mats.shape
    vec_size = seg_vecs.shape[0]
    both_rows = CORES * SEG

    first_piece, live_row, *rest = run_kernel(
        prepare_kernel,
        "prepare",
        [shape_of((own_rows, FIRST), LOW), shape_of((1, SEG))]
        + [shape_of((own_rows, FF_HALF), LOW)] * 2
        + [shape_of((own_rows, QUARTER_HALF), LOW)] * LINE
        + [shape_of((own_rows, HALF), LOW), shape_of((MODEL, PLANE * SPAN), LOW)],
        where,
        (seg_mats, cls_mats),
        (seg_vecs, cls_vecs, valid_flags),
        [
            pltpu.SemaphoreType.DMA((4,)),
            pltpu.VMEM((LINE, own_rows, QUARTER), LOW),
            pltpu.SemaphoreType.DMA((3 + 5 * LINE,)),
        ],
    )
    first_line = line_parts(first_piece)
    second_piece, third_piece, quarters, cls_out_piece, order = (
        rest[0],
        rest[1],
        rest[2:-2],
        rest[-2],
        rest[-1],
    )

    def joined(*pieces):
        return jnp.concatenate(pieces, axis=1)

    def sent_both(to_x, to_y):
        to_x, to_y = together(to_x, to_y)
        return together(in_plane(to_x, 1), in_plane(to_y, 2))

    own_sent = joined(first_piece, second_piece, third_piece)
    own_x, own_y = sent_both(own_sent, own_sent)
    first_line = first_line[:1] + tuple(after(got, own_x, own_y) for got in first_line[1:])
    hidden_got = other_core(after(hidden_in, own_x, own_y))
    live_got = other_core(after(live_row, own_x, own_y))
    to_x = joined(after(own_y, hidden_got, live_got)[:, OWN_CUT:], *first_line[1:])
    to_y = joined(own_x[:, :OWN_CUT], *first_line[1:])
    first_x, first_y = sent_both(to_x, to_y)
    second_line = line_parts(after(second_piece, to_x, to_y))

    def halves(group, from_x, from_y):
        width, cut = WIDTHS[group], LINE_CUTS[group]
        if group == 0:
            base_x, base_y = sum(WIDTHS) - OWN_CUT, OWN_CUT
        else:
            before, before_cut = WIDTHS[group - 1], LINE_CUTS[group - 1]
            base_x, base_y = 2 * before - before_cut, before + before_cut
        return (
            from_y[:, base_y + width + cut : base_y + 3 * width],
            from_x[:, base_x : base_x + width + cut],
        )

    high, low = halves(0, first_x, first_y)
    to_x, to_y = joined(high, *second_line[1:]), joined(low, *second_line[1:])
    second_x, second_y = sent_both(to_x, to_y)
    third_line = line_parts(after(third_piece, to_x, to_y))
    high, low = halves(1, second_x, second_y)
    to_x, to_y = joined(high, *third_line[1:]), joined(low, *third_line[1:])
    third_x, third_y = sent_both(to_x, to_y)
    own_parts = (own_x, own_y, first_x, first_y)
    cls_line = (quarters[0],) + tuple(
        along_line(after(quarters[apart], to_x, to_y), apart)
        for apart in range(1, LINE)
    )

    qkv_weight, out_low, out_high, qkv, mixed, vectors, count, hidden_ordered = run_kernel(
        qkv_kernel,
        "seg_qkv",
        [
            shape_of((GROUP, own_rows, 3 * HALF), LOW),
            shape_of((GROUP // 2, own_rows, HALF), LOW),
            shape_of((GROUP // 2, own_rows, HALF), LOW),
            shape_of((both_rows, 3 * HALF), LOW),
            shape_of((both_rows, HALF), LOW),
            shape_of((2 * (8 * MODEL + FF) // MODEL, MODEL)),
            shape_of((8, LANES)),
            shape_of((both_rows, PLANE * SPAN), LOW),
        ],
        where,
        (),
        first_line
        + own_parts
        + (first_x, first_y, second_x, second_y)
        + (hidden_in, hidden_got, live_row, live_got, order),
        [
            pltpu.VMEM((GROUP, own_rows, LANES), LOW),
            pltpu.VMEM((2, 8 * MODEL + FF), WIDE),
            pltpu.VMEM((both_rows, MODEL), LOW),
            pltpu.VMEM((GROUP, own_rows, HALF), LOW),
        ],
        flops=2 * SEG * MODEL * 3 * MODEL,
    )
    out_weight, mixed_ordered, normed_first, inv_first, first_low = run_kernel(
        out_kernel,
        "seg_out",
        [
            shape_of((MODEL, MODEL), LOW),
            shape_of((both_rows, PLANE * SPAN), LOW),
            shape_of((SEG, MODEL)),
            shape_of((SEG, 1)),
            shape_of((SEG, MODEL), LOW),
        ],
        where,
        (),
        (
            hidden_in,
            mixed,
            after(other_core(mixed), third_x, third_y),
            out_low,
            out_high,
            other_core(out_low),
            other_core(out_high),
            vectors,
            order,
        ),
        [pltpu.VMEM((both_rows, MODEL), LOW)],
        flops=2 * SEG * MODEL * MODEL,
    )
    fourth_x, fourth_y = sent_both(*halves(2, third_x, third_y))
    first_got = after(other_core(first_low), fourth_x, fourth_y)
    count = count + other_core(after(count, first_got))
    up_weight, act, slope = run_kernel(
        up_kernel,
        "seg_up",
        [
            shape_of((GROUP, own_rows, FF_HALF), LOW),
            shape_of((both_rows, FF_HALF), LOW),
            shape_of((both_rows, FF_HALF)),
        ],
        where,
        (),
        second_line
        + own_parts
        + (second_x, second_y, third_x, third_y)
        + (first_low, first_got, vectors),
        [pltpu.VMEM((both_rows, MODEL), LOW)],
        flops=2 * SEG * MODEL * FF,
    )
    cls_sent = joined(*cls_line, cls_out_piece)
    cls_sent = after(cls_sent, act)
    cls_x, cls_y = sent_both(cls_sent, cls_sent)
    down_weight, down_own, down_send = run_kernel(
        down_kernel,
        "seg_down",
        [
            shape_of((GROUP, own_rows, FF_HALF), LOW),
            shape_of((SEG, MODEL)),
            shape_of((SEG, MODEL)),
        ],
        where,
        (),
        third_line + own_parts + (third_x, third_y, fourth_x, fourth_y) + (act,),
        flops=2 * SEG * MODEL * FF,
    )
    normed_second, inv_second, diff, out_rows, head_row = run_kernel(
        seg_rows_kernel,
        "seg_rows",
        [
            shape_of((SEG, MODEL)),
            shape_of((SEG, 1)),
            shape_of((SEG, MODEL)),
            shape_of((SEG, MODEL)),
            shape_of((1, 2 * MODEL + LANES)),
        ],
        where,
        (),
        (
            down_own,
            other_core(down_send),
            normed_first,
            vectors,
            targets,
            live_row,
            seg_pos,
        ),
    )
    head_planes = plane_parts(head_row)
    head_lines = line_parts(jnp.concatenate(head_planes))
    size = LINE // 2 * QUARTER_HALF
    cls_far = sent_both(
        after(cls_y[:, size:], *head_planes[1:]), after(cls_x[:, :size], *head_planes[1:])
    )

    second_grad, second_low, second_sums, first_ordered = run_kernel(
        second_norm_kernel,
        "seg_second_norm",
        [
            shape_of((SEG, MODEL)),
            shape_of((SEG, MODEL), LOW),
            shape_of((3, MODEL)),
            shape_of((both_rows, PLANE * SPAN), LOW),
        ],
        where,
        (),
        (diff, count, normed_second, inv_second, vectors, first_low, first_got, order),
        [pltpu.VMEM((both_rows, MODEL), LOW)],
    )
    second_got = other_core(second_low)
    pre, first_grad_own, first_grad_send, up_sums = run_kernel(
        mlp_back_kernel,
        "seg_mlp_back",
        [
            shape_of((both_rows, FF_HALF), LOW),
            shape_of((SEG, MODEL)),
            shape_of((SEG, MODEL)),
            shape_of((FF_HALF // MODEL, MODEL)),
        ],
        where,
        (),
        (second_low, second_got, down_weight, up_weight, slope),
        [pltpu.VMEM((both_rows, MODEL), LOW)],
        flops=4 * SEG * MODEL * FF,
    )
    first_grad_got = other_core(first_grad_send)

    def part_shapes(columns):
        return [
            shape_of((count_of, own_rows, columns), LOW)
            for count_of in (LINE // 2, LINE // 2, LINE, LINE, LINE)
        ]

    head_lines = head_lines[:1] + together(*(after(got, pre) for got in head_lines[1:]))
    cls_far = together(*(after(got, *head_lines[1:]) for got in cls_far))
    cls_half, cls_out_half = run_kernel(
        cls_gather_kernel,
        "head_gather",
        [
            shape_of((GROUP, own_rows, QUARTER_HALF), LOW),
            shape_of((PLANE, own_rows, HALF), LOW),
        ],
        where,
        (),
        cls_line + (cls_x, cls_y) + cls_far + (cls_out_piece,),
    )
    mlp_data = (first_ordered, second_low, second_got, after(pre, cls_half), act, order)
    mlp_far = run_kernel(
        mlp_far_kernel,
        "seg_mlp_far",
        part_shapes(FF)[:2],
        where,
        (),
        mlp_data,
        [pltpu.VMEM((both_rows, MODEL), LOW)],
        flops=SEG * MODEL * FF,
    )
    mlp_parts = list(mlp_far) + list(
        run_kernel(
            mlp_near_kernel,
            "seg_mlp_near",
            part_shapes(FF)[2:],
            where,
            (),
            mlp_data,
            [pltpu.VMEM((both_rows, MODEL), LOW)],
            flops=3 * SEG * MODEL * FF,
        )
    )
    mlp_far = reduce_far(tuple(after(part, *cls_far) for part in mlp_parts[:2]))
    cls_weight, cls_out = run_kernel(
        cls_weight_kernel,
        "head_weight",
        [
            shape_of((GROUP, own_rows, QUARTER), LOW),
            shape_of((4, HEAD_DIM, MODEL), LOW),
        ],
        where,
        (),
        (cls_half, other_core(cls_half), cls_out_half, other_core(cls_out_half)),
    )
    cls_weight = cls_weight.reshape(MODEL, QUARTER)
    cls_out = cls_out.reshape(SPAN, MODEL)
    heads, cls_qkv, cls_mixed, part = run_kernel(
        cls_attend_kernel,
        "head_attend",
        [
            shape_of((GROUP, 2 * MODEL + LANES)),
            shape_of((GROUP, 3 * SPAN), LOW),
            shape_of((GROUP, SPAN), LOW),
            shape_of((GROUP, MODEL)),
        ],
        where,
        (),
        tuple(after(got, mlp_parts[0], first_grad_got) for got in head_lines)
        + (vectors, cls_weight, cls_out),
    )
    cls_normed, cls_inv, cls_low, cls_act, cls_slope, part, *mlp_sent = run_kernel(
        head_mlp_kernel,
        "head_mlp",
        [
            shape_of((GROUP, MODEL)),
            shape_of((GROUP, 1)),
            shape_of((GROUP, MODEL), LOW),
            shape_of((GROUP, FF // LINE), LOW),
            shape_of((GROUP, FF // LINE)),
            shape_of((GROUP, MODEL)),
            shape_of(mlp_parts[2].shape, LOW),
            shape_of(mlp_parts[2].shape, LOW),
        ],
        where,
        (),
        (heads,) + line_parts(part) + (vectors, cls_weight) + mlp_far + tuple(mlp_parts[2:4]),
    )
    mlp_plane = sent_both(*mlp_sent)
    cls_parts = line_parts(part)
    top_row, square, cls_grad, cls_second, cls_pre, part, top_sums = run_kernel(
        cls_top_kernel,
        "head_top",
        [
            shape_of((1, MODEL)),
            shape_of((8, LANES)),
            shape_of((GROUP, MODEL)),
            shape_of((GROUP, MODEL), LOW),
            shape_of((GROUP, FF // LINE), LOW),
            shape_of((GROUP, MODEL)),
            shape_of((2, MODEL)),
        ],
        where,
        (),
        (heads,)
        + cls_parts
        + (vectors, cls_weight, cls_normed, count, cls_slope),
        [pltpu.VMEM((GROUP, MODEL), WIDE)],
    )
    top_parts = line_parts(part)
    cls_grad, cls_branch, cls_proj, part, back_sums = run_kernel(
        cls_attend_back_kernel,
        "head_attend_back",
        [
            shape_of((GROUP, MODEL)),
            shape_of((GROUP, MODEL), LOW),
            shape_of((GROUP, 3 * SPAN), LOW),
            shape_of((GROUP, MODEL)),
            shape_of((2, MODEL)),
        ],
        where,
        (),
        (heads,)
        + top_parts
        + (vectors, cls_weight, cls_out, cls_grad, cls_normed, cls_inv, cls_qkv),
    )
    end_parts = line_parts(part)
    pack = jnp.concatenate([cls_proj, cls_mixed, cls_pre, cls_act], axis=1)
    folded = [shape_of((own_rows, FF))] + [shape_of((own_rows + GROUP, FF), LOW)] * (LINE - 1)
    dheads, head_grad, shared, mlp_own, *mlp_sent = run_kernel(
        head_end_kernel,
        "head_end",
        [shape_of((1, MODEL)), shape_of((1, MODEL)), shape_of((GROUP + 8, MODEL))] + folded,
        where,
        (),
        (heads, cls_grad)
        + end_parts
        + (square, back_sums, top_sums, normed_second, inv_second, vectors)
        + (mlp_parts[4],)
        + mlp_plane
        + (pack,),
        [pltpu.VMEM((GROUP, MODEL), WIDE)],
    )
    got_three, got_two = along_line(mlp_sent[2], 3), along_line(mlp_sent[1], 2)
    mlp_last = mlp_sent[0]
    mlp_got = [None, got_two, got_three]

    head_own, head_send, head_data = run_kernel(
        head_back_kernel,
        "seg_head_back",
        [shape_of((1, MODEL)), shape_of((1, MODEL)), shape_of((12, MODEL))],
        where,
        (),
        (
            head_grad,
            other_core(head_grad),
            down_weight,
            up_weight,
            slope,
            act,
            first_low,
            first_got,
        ),
    )
    grad_summed, branch, mixed_grad, attn_send, first_sums = run_kernel(
        first_norm_kernel,
        "seg_first_norm",
        [
            shape_of((SEG, MODEL)),
            shape_of((SEG, MODEL), LOW),
            shape_of((SEG, MODEL), LOW),
            shape_of((SEG, MODEL), LOW),
            shape_of((3, MODEL)),
        ],
        where,
        (),
        (
            second_grad,
            first_grad_own,
            first_grad_got,
            head_grad,
            head_own,
            other_core(head_send),
            normed_first,
            inv_first,
            vectors,
            out_weight,
        ),
    )
    attn_got = other_core(attn_send)
    proj = run_kernel(
        attn_back_kernel,
        "seg_attn_back",
        [shape_of((both_rows, 3 * HALF), LOW)],
        where,
        (),
        (qkv, mixed_grad, attn_got, live_row, live_got),
        flops=2 * SEG * MODEL * 3 * MODEL,
    )[0]
    attn_data = (hidden_ordered, mixed_ordered, proj, branch, attn_got)
    attn_far = run_kernel(
        attn_far_kernel,
        "seg_attn_far",
        part_shapes(4 * HALF)[:2],
        where,
        (),
        attn_data,
        flops=SEG * MODEL * 2 * MODEL,
    )
    attn_far = reduce_far(tuple(after(part, mlp_got[-1]) for part in attn_far))
    *attn_near, output, input_own, input_send, payload = run_kernel(
        attn_near_kernel,
        "seg_attn_near",
        part_shapes(4 * HALF)[2:]
        + [
            shape_of((SEG, MODEL), LOW),
            shape_of((SEG, MODEL)),
            shape_of((SEG, MODEL)),
            shape_of((24, MODEL), LOW),
        ],
        where,
        (),
        attn_data
        + (top_row, out_rows, live_row, qkv_weight, first_sums, second_sums, up_sums)
        + (dheads, normed_second, head_data),
        [pltpu.VMEM((24, MODEL), WIDE)],
        flops=3 * SEG * MODEL * 2 * MODEL,
    )
    attn_sent = run_kernel(
        add_far_kernel,
        "seg_attn_add",
        [shape_of(attn_near[0].shape, LOW)] * 2,
        where,
        (),
        attn_far + (after(attn_near[0], got_two), attn_near[1]),
    )
    attn_plane = sent_both(*attn_sent)
    mlp_got[0] = along_line(after(mlp_last, *attn_sent), 1)
    input_got = other_core(after(input_send, *attn_sent))
    shared = shared + other_core(after(shared, attn_sent[0]))
    payload_parts = line_parts(after(payload, mlp_got[0], input_got, shared))
    mlp_got = [after(got, attn_plane[0]) for got in mlp_got]
    mlp_sum = reduce_line(mlp_own, mlp_got)
    row_width = 8 * MODEL + 2 * FF
    cls_rows, input_grad = run_kernel(
        rows_input_kernel,
        "head_rows",
        [shape_of((GROUP, row_width), LOW), shape_of((SEG, MODEL), LOW)],
        where,
        (),
        (pack,)
        + tuple(mlp_got)
        + (heads, cls_branch, cls_low, cls_second)
        + (grad_summed, input_own, input_got),
        [pltpu.VMEM((LINE,) + pack.shape, LOW)],
    )
    cls_got = other_core(cls_rows)
    attn_plane = tuple(after(got, output, shared) for got in attn_plane)
    attn_own, *attn_sent = reduce_fold(where, attn_near[2], attn_plane)
    attn_lines = list(
        together(*(along_line(attn_sent[apart - 1], apart) for apart in range(1, LINE)))
    )
    flat = pltpu.VMEM((1, 8 * MODEL + FF), WIDE)
    payload_line = jnp.concatenate(payload_parts)
    mlp_mine, own_vecs, cls_mats_grad, cls_vec_grad, pos_total, loss_value = run_kernel(
        share_owner_kernel,
        "head_owner",
        [
            shape_of((own_rows, FF)),
            shape_of((16, MODEL)),
            shape_of((own_rows, total_columns)),
            shape_of((vec_size,)),
            shape_of((GROUP, MODEL)),
            shape_of((1, 1)),
        ],
        where,
        (),
        tuple(after(got, attn_own) for got in plane_parts(after(payload_line, *attn_plane)))
        + (mlp_sum, cls_rows, cls_got, shared, count),
        [
            pltpu.VMEM((GROUP * 24, MODEL), LOW),
            pltpu.VMEM((CORES * GROUP, row_width), LOW),
            flat,
        ],
        flops=64 * own_rows * total_columns,
    )
    loss_value = loss_value.reshape(())
    attn_lines = together(*(after(got, mlp_mine) for got in attn_lines))
    attn_sum = reduce_line(attn_own, attn_lines)
    seg_mats_grad, seg_vec_grad = run_kernel(
        store_kernel,
        "seg_owner",
        [shape_of((own_rows, total_columns)), shape_of((vec_size,))],
        where,
        (),
        (attn_sum, other_core(attn_sum), mlp_mine, other_core(mlp_mine))
        + (own_vecs, other_core(own_vecs)),
        [flat, pltpu.SemaphoreType.DMA((12,))],
        far=(0,),
    )

    return (
        output,
        input_grad,
        seg_mats_grad,
        seg_vec_grad,
        cls_mats_grad,
        cls_vec_grad,
        pos_total,
        loss_value,
    )


def solution(mesh):
    in_specs = (
        P(("rep", "fsdp"), None),
        P(("rep", "fsdp"), None),
        P(("rep", "fsdp")),
        P(("rep", "fsdp")),
        P(("rep", "fsdp")),
        P("fsdp", None),
        P("fsdp"),
        P("fsdp", None),
        P("fsdp"),
        P(),
    )
    out_specs = (
        P(("rep", "fsdp"), None),
        P(("rep", "fsdp"), None),
        P("fsdp", None),
        P("fsdp"),
        P("fsdp", None),
        P("fsdp"),
        P(),
        P(),
    )
    one_slice = dict(mesh.shape) == {"rep": CORES, "fsdp": LINE * PLANE}
    body = slice_local if one_slice else local
    return jax.shard_map(body, mesh=mesh, in_specs=in_specs, out_specs=out_specs, check_vma=False)
```

```python
import math

import jax
import jax.numpy as jnp
from jax import lax
from jax.experimental import pallas as pl
from jax.experimental.pallas import tpu as pltpu
from jax.sharding import PartitionSpec as P

HEADS = 12
HEAD_DIM = 64
FF = 3072
SEG = 128
SEQ = 2048


NORM_EPS = 1e-05
MASK_FILL = -1e30
SQRT_HALF = 0.7071067811865476
INV_SQRT_TWO_PI = 0.3989422804014327


def swapped(value, axis, apart):
    mask = 2**apart
    pairs = [(source, source ^ mask) for source in range(lax.axis_size(axis))]
    return lax.ppermute(value, axis, pairs)


def product_plain(left_side, right_side):
    return jnp.dot(left_side, right_side, preferred_element_type=jnp.float32)


def product_left(left_side, right_side):
    return lax.dot_general(
        left_side, right_side, (((0,), (0,)), ((), ())), preferred_element_type=jnp.float32
    )


def product_right(left_side, right_side):
    return lax.dot_general(
        left_side, right_side, (((1,), (1,)), ((), ())), preferred_element_type=jnp.float32
    )


def row_total(array_in):
    return jnp.sum(array_in.astype(jnp.float32), axis=0)


def unpack_weights(gathered, model_width, ff_width):
    matrix, vector = gathered
    vector = vector.astype(jnp.float32)
    pieces = tuple(
        (vector[offset * model_width : (offset + 1) * model_width] for offset in range(8))
    )
    return (
        (
            matrix[:, : 3 * model_width],
            matrix[:, 3 * model_width : 4 * model_width],
            matrix[:, 4 * model_width : 4 * model_width + ff_width],
            matrix[:, 4 * model_width + ff_width :],
        )
        + pieces
        + (vector[8 * model_width :],)
    )


def norm_forward(summed, gain_vec, shift_vec):
    row_mean = jnp.mean(summed, axis=-1, keepdims=True)
    centered = summed - row_mean
    inv_dev = lax.rsqrt(jnp.mean(centered * centered, axis=-1, keepdims=True) + NORM_EPS)
    normed = centered * inv_dev
    return (normed * gain_vec + shift_vec, normed, inv_dev)


def norm_backward(grad_out, normed, inv_dev, gain_vec):
    scaled = grad_out * gain_vec
    mean_one = jnp.mean(scaled, axis=-1, keepdims=True)
    mean_two = jnp.mean(scaled * normed, axis=-1, keepdims=True)
    grad_in = inv_dev * (scaled - mean_one - normed * mean_two)
    return (grad_in, jnp.sum(grad_out * normed, axis=0), jnp.sum(grad_out, axis=0))


def gelu_value(before):
    return 0.5 * before * (1.0 + lax.erf(before * SQRT_HALF))


def gelu_slope(before):
    return (
        0.5 * (1.0 + lax.erf(before * SQRT_HALF))
        + before * jnp.exp(-0.5 * before * before) * INV_SQRT_TWO_PI
    )


def attention_scores(queries, keys_in, allowed, score_scale):
    raw_scores = (
        jnp.einsum("bqhe,bkhe->bhqk", queries, keys_in, preferred_element_type=jnp.float32)
        * score_scale
    )
    return jnp.where(allowed, raw_scores, MASK_FILL)


def attention_forward(queries, keys_in, values, allowed, score_scale):
    scores = attention_scores(queries, keys_in, allowed, score_scale)
    row_top = jnp.max(scores, axis=-1, keepdims=True)
    log_total = row_top + jnp.log(jnp.sum(jnp.exp(scores - row_top), axis=-1, keepdims=True))
    weights = jnp.exp(scores - log_total).astype(jnp.bfloat16)
    mixed_rows = jnp.einsum("bhqk,bkhe->bqhe", weights, values, preferred_element_type=jnp.float32)
    return (mixed_rows, log_total)


def attention_backward(queries, keys_in, values, allowed, score_scale, log_total, grad_mixed):
    probabilities = jnp.exp(attention_scores(queries, keys_in, allowed, score_scale) - log_total)
    grad_probs = jnp.einsum(
        "bqhe,bkhe->bhqk", grad_mixed, values, preferred_element_type=jnp.float32
    )
    inner_sum = jnp.sum(grad_probs * probabilities, axis=-1, keepdims=True)
    grad_scores = (probabilities * (grad_probs - inner_sum)).astype(jnp.bfloat16)
    grad_query = (
        jnp.einsum("bhqk,bkhe->bqhe", grad_scores, keys_in, preferred_element_type=jnp.float32)
        * score_scale
    )
    grad_key = (
        jnp.einsum("bhqk,bqhe->bkhe", grad_scores, queries, preferred_element_type=jnp.float32)
        * score_scale
    )
    grad_value = jnp.einsum(
        "bhqk,bqhe->bkhe",
        probabilities.astype(jnp.bfloat16),
        grad_mixed,
        preferred_element_type=jnp.float32,
    )
    return (grad_query, grad_key, grad_value)


def block_forward(rows_in, unpacked, attend):
    (
        qkv_weight,
        out_weight,
        up_weight,
        down_weight,
        query_bias,
        value_bias,
        out_bias,
        down_bias,
        gain_first,
        shift_first,
        gain_second,
        shift_second,
        up_bias,
    ) = unpacked
    model_width = rows_in.shape[1]
    inputs = rows_in.astype(jnp.bfloat16)
    projected = product_plain(inputs, qkv_weight)
    queries = (projected[:, :model_width] + query_bias).astype(jnp.bfloat16)
    keys_in = projected[:, model_width : 2 * model_width].astype(jnp.bfloat16)
    values = (projected[:, 2 * model_width :] + value_bias).astype(jnp.bfloat16)
    mixed_rows, attend_kept = attend(queries, keys_in, values)
    mixed_rows = mixed_rows.astype(jnp.bfloat16)
    summed_first = rows_in + product_plain(mixed_rows, out_weight) + out_bias
    first_out, normed_first, inv_first = norm_forward(summed_first, gain_first, shift_first)
    first_low = first_out.astype(jnp.bfloat16)
    pre_act = product_plain(first_low, up_weight) + up_bias
    activated = gelu_value(pre_act).astype(jnp.bfloat16)
    summed_second = first_out + product_right(activated, down_weight) + down_bias
    block_out, normed_second, inv_second = norm_forward(summed_second, gain_second, shift_second)
    saved_state = (
        inputs,
        queries,
        keys_in,
        values,
        attend_kept,
        mixed_rows,
        normed_first,
        inv_first,
        first_low,
        pre_act,
        activated,
        normed_second,
        inv_second,
    )
    return (block_out, saved_state)


def block_backward(grad_out, unpacked, saved_state, attend_back):
    (
        qkv_weight,
        out_weight,
        up_weight,
        down_weight,
        query_bias,
        value_bias,
        out_bias,
        down_bias,
        gain_first,
        shift_first,
        gain_second,
        shift_second,
        up_bias,
    ) = unpacked
    (
        inputs,
        queries,
        keys_in,
        values,
        attend_kept,
        mixed_rows,
        normed_first,
        inv_first,
        first_low,
        pre_act,
        activated,
        normed_second,
        inv_second,
    ) = saved_state
    grad_second, grad_gain_second, grad_shift_second = norm_backward(
        grad_out, normed_second, inv_second, gain_second
    )
    second_low = grad_second.astype(jnp.bfloat16)
    grad_pre = (product_plain(second_low, down_weight) * gelu_slope(pre_act)).astype(jnp.bfloat16)
    grad_first = grad_second + product_right(grad_pre, up_weight)
    grad_summed, grad_gain_first, grad_shift_first = norm_backward(
        grad_first, normed_first, inv_first, gain_first
    )
    branch_low = grad_summed.astype(jnp.bfloat16)
    grad_mixed = product_right(branch_low, out_weight).astype(jnp.bfloat16)
    grad_query, grad_key, grad_value = attend_back(
        queries, keys_in, values, attend_kept, grad_mixed
    )
    grad_proj = jnp.concatenate([grad_query, grad_key, grad_value], axis=1)
    grad_rows = grad_summed + product_right(grad_proj, qkv_weight)
    vector_grad = jnp.concatenate(
        [
            row_total(grad_query),
            row_total(grad_value),
            row_total(branch_low),
            row_total(second_low),
            grad_gain_first,
            grad_shift_first,
            grad_gain_second,
            grad_shift_second,
            row_total(grad_pre),
        ]
    )
    weight_rows = (
        inputs,
        grad_proj,
        mixed_rows,
        branch_low,
        first_low,
        grad_pre,
        second_low,
        activated,
    )
    return (grad_rows, weight_rows, vector_grad)


def weight_products(weight_rows):
    inputs, grad_proj, mixed_rows, branch_low, first_low, grad_pre, second_low, activated = (
        weight_rows
    )
    return (
        product_left(inputs, grad_proj),
        product_left(mixed_rows, branch_low),
        product_left(first_low, grad_pre),
        product_left(second_low, activated),
    )


def local(
    hidden_in,
    targets,
    doc_ids,
    seg_nums,
    valid_flags,
    seg_mats,
    seg_vecs,
    cls_mats,
    cls_vecs,
    seg_pos,
):
    tok_rows, model_width = hidden_in.shape
    ff_width = FF
    seg_len = SEG
    group_span = SEQ // tok_rows
    seg_count = tok_rows // seg_len
    score_scale = HEAD_DIM ** (-0.5)
    head_shape = (HEADS, HEAD_DIM)
    live_rows = valid_flags.astype(jnp.float32)
    rank_full = lax.axis_index("fsdp")
    seg_gathered = (
        lax.all_gather(seg_mats, "fsdp", axis=0, tiled=True),
        lax.all_gather(seg_vecs, "fsdp", axis=0, tiled=True),
    )
    seg_unpacked = unpack_weights(seg_gathered, model_width, ff_width)
    cls_gathered = (
        lax.all_gather(cls_mats, "fsdp", axis=0, tiled=True),
        lax.all_gather(cls_vecs, "fsdp", axis=0, tiled=True),
    )
    cls_unpacked = unpack_weights(cls_gathered, model_width, ff_width)
    seg_allowed = (live_rows.reshape(seg_count, 1, 1, seg_len) > 0.5) | jnp.eye(seg_len, dtype=bool)
    seg_shape = (seg_count, seg_len) + head_shape

    def seg_attend(queries, keys_in, values):
        mixed_rows, log_total = attention_forward(
            queries.reshape(seg_shape),
            keys_in.reshape(seg_shape),
            values.reshape(seg_shape),
            seg_allowed,
            score_scale,
        )
        return (mixed_rows.reshape(tok_rows, model_width), log_total)

    def seg_attend_back(queries, keys_in, values, log_total, grad_mixed):
        grad_parts = attention_backward(
            queries.reshape(seg_shape),
            keys_in.reshape(seg_shape),
            values.reshape(seg_shape),
            seg_allowed,
            score_scale,
            log_total,
            grad_mixed.reshape(seg_shape),
        )
        return tuple(
            (
                grad_part.reshape(tok_rows, model_width).astype(jnp.bfloat16)
                for grad_part in grad_parts
            )
        )

    first_out, seg_saved = block_forward(hidden_in.astype(jnp.float32), seg_unpacked, seg_attend)
    first_grid = first_out.reshape(seg_count, seg_len, model_width)
    position_hot = (seg_nums[:, None] == jnp.arange(seg_pos.shape[0])[None, :]).astype(jnp.float32)
    position_rows = jnp.sum(
        position_hot[:, :, None] * seg_pos.astype(jnp.float32)[None, :, :], axis=1
    )
    heads_in = first_grid[:, 0, :] + position_rows
    lead_live = live_rows.reshape(seg_count, seg_len)[:, 0]
    lead_doc = doc_ids.reshape(seg_count, seg_len)[:, 0]
    lead_labels = jnp.where(lead_live > 0.5, lead_doc, -1).astype(jnp.bfloat16)
    lead_doc_low = lead_doc.astype(jnp.bfloat16)
    bit_count = group_span.bit_length() - 1
    key_total = group_span * seg_count
    own_slot = rank_full % group_span * seg_count + jnp.arange(seg_count)
    query_shape = (1, seg_count) + head_shape
    key_shape = (1, key_total) + head_shape

    def cls_attend(queries, keys_in, values):
        paired = jnp.concatenate([keys_in, values], axis=1)
        labels = lead_labels
        for bit_level in range(bit_count):
            other_pair, other_labels = swapped((paired, labels), "fsdp", bit_level)
            upper_half = rank_full // (1 << bit_level) % 2 == 1
            paired = jnp.where(
                upper_half,
                jnp.concatenate([other_pair, paired]),
                jnp.concatenate([paired, other_pair]),
            )
            labels = jnp.where(
                upper_half,
                jnp.concatenate([other_labels, labels]),
                jnp.concatenate([labels, other_labels]),
            )
        allowed = (labels[None, :] == lead_doc_low[:, None]) | (
            jnp.arange(key_total)[None, :] == own_slot[:, None]
        )
        allowed = allowed[None, None]
        mixed_rows, log_total = attention_forward(
            queries.reshape(query_shape),
            paired[:, :model_width].reshape(key_shape),
            paired[:, model_width:].reshape(key_shape),
            allowed,
            score_scale,
        )
        return (mixed_rows.reshape(seg_count, model_width), (paired, allowed, log_total))

    def cls_attend_back(queries, keys_in, values, attend_kept, grad_mixed):
        paired, allowed, log_total = attend_kept
        grad_query, grad_key, grad_value = attention_backward(
            queries.reshape(query_shape),
            paired[:, :model_width].reshape(key_shape),
            paired[:, model_width:].reshape(key_shape),
            allowed,
            score_scale,
            log_total,
            grad_mixed.reshape(query_shape),
        )
        grad_pair = jnp.concatenate(
            [grad_key.reshape(key_total, model_width), grad_value.reshape(key_total, model_width)],
            axis=1,
        )
        for bit_level in reversed(range(bit_count)):
            half_rows = grad_pair.shape[0] // 2
            upper_half = rank_full // (1 << bit_level) % 2 == 1
            kept_half = jnp.where(upper_half, grad_pair[half_rows:], grad_pair[:half_rows])
            sent_half = jnp.where(upper_half, grad_pair[:half_rows], grad_pair[half_rows:])
            grad_pair = kept_half + swapped(
                sent_half.astype(jnp.bfloat16), "fsdp", bit_level
            ).astype(sent_half.dtype)
        grad_pair = grad_pair.astype(jnp.bfloat16)
        return (
            grad_query.reshape(seg_count, model_width).astype(jnp.bfloat16),
            grad_pair[:, :model_width],
            grad_pair[:, model_width:],
        )

    top_out, cls_saved = block_forward(heads_in, cls_unpacked, cls_attend)
    combined = jnp.concatenate([top_out[:, None, :], first_grid[:, 1:, :]], axis=1).reshape(
        tok_rows, model_width
    )
    output_rows = combined * live_rows[:, None]
    diff_rows = (output_rows - targets.astype(jnp.float32)) * live_rows[:, None]
    count_all, square_all = lax.psum(
        (jnp.sum(live_rows), jnp.sum(diff_rows * diff_rows)), ("rep", "fsdp")
    )
    loss_value = square_all / (count_all * model_width)
    slots_all = tok_rows * lax.axis_size("rep") * lax.axis_size("fsdp")
    grad_grid = (diff_rows * (slots_all / count_all)).reshape(seg_count, seg_len, model_width)
    cls_back = unpack_weights(
        (
            lax.all_gather(cls_mats, "fsdp", axis=0, tiled=True),
            lax.all_gather(cls_vecs, "fsdp", axis=0, tiled=True),
        ),
        model_width,
        ff_width,
    )
    heads_grad, cls_weight_rows, cls_g_vec = block_backward(
        grad_grid[:, 0, :], cls_back, cls_saved, cls_attend_back
    )
    cls_g_qkv, cls_g_out, cls_g_up, cls_g_down = weight_products(cls_weight_rows)
    pos_local = jnp.sum(position_hot[:, :, None] * heads_grad[:, None, :], axis=0)
    seg_grad_out = jnp.concatenate([heads_grad[:, None, :], grad_grid[:, 1:, :]], axis=1).reshape(
        tok_rows, model_width
    )
    seg_back = unpack_weights(
        (
            lax.all_gather(seg_mats, "fsdp", axis=0, tiled=True),
            lax.all_gather(seg_vecs, "fsdp", axis=0, tiled=True),
        ),
        model_width,
        ff_width,
    )
    input_grad, seg_weight_rows, seg_g_vec = block_backward(
        seg_grad_out, seg_back, seg_saved, seg_attend_back
    )
    seg_g_qkv, seg_g_out, seg_g_up, seg_g_down = weight_products(seg_weight_rows)
    owner_rows = tuple(
        (
            lax.psum_scatter(seg_g_qkv, "fsdp", scatter_dimension=0, tiled=True),
            lax.psum_scatter(seg_g_out, "fsdp", scatter_dimension=0, tiled=True),
            lax.psum_scatter(seg_g_up, "fsdp", scatter_dimension=0, tiled=True),
            lax.psum_scatter(seg_g_down, "fsdp", scatter_dimension=0, tiled=True),
            lax.psum_scatter(seg_g_vec, "fsdp", scatter_dimension=0, tiled=True),
            lax.psum_scatter(cls_g_qkv, "fsdp", scatter_dimension=0, tiled=True),
            lax.psum_scatter(cls_g_out, "fsdp", scatter_dimension=0, tiled=True),
            lax.psum_scatter(cls_g_up, "fsdp", scatter_dimension=0, tiled=True),
            lax.psum_scatter(cls_g_down, "fsdp", scatter_dimension=0, tiled=True),
            lax.psum_scatter(cls_g_vec, "fsdp", scatter_dimension=0, tiled=True),
        )
    )
    replica_share = (
        lax.psum_scatter(
            owner_rows[0].astype(jnp.bfloat16), "rep", scatter_dimension=1, tiled=True
        ).astype(jnp.float32),
        lax.psum_scatter(
            owner_rows[1].astype(jnp.bfloat16), "rep", scatter_dimension=1, tiled=True
        ).astype(jnp.float32),
        lax.psum_scatter(
            owner_rows[2].astype(jnp.bfloat16), "rep", scatter_dimension=1, tiled=True
        ).astype(jnp.float32),
        lax.psum_scatter(
            owner_rows[3].astype(jnp.bfloat16), "rep", scatter_dimension=1, tiled=True
        ).astype(jnp.float32),
        lax.psum_scatter(
            owner_rows[4].astype(jnp.bfloat16), "rep", scatter_dimension=0, tiled=True
        ).astype(jnp.float32),
        lax.psum_scatter(
            owner_rows[5].astype(jnp.bfloat16), "rep", scatter_dimension=1, tiled=True
        ).astype(jnp.float32),
        lax.psum_scatter(
            owner_rows[6].astype(jnp.bfloat16), "rep", scatter_dimension=1, tiled=True
        ).astype(jnp.float32),
        lax.psum_scatter(
            owner_rows[7].astype(jnp.bfloat16), "rep", scatter_dimension=1, tiled=True
        ).astype(jnp.float32),
        lax.psum_scatter(
            owner_rows[8].astype(jnp.bfloat16), "rep", scatter_dimension=1, tiled=True
        ).astype(jnp.float32),
        lax.psum_scatter(
            owner_rows[9].astype(jnp.bfloat16), "rep", scatter_dimension=0, tiled=True
        ).astype(jnp.float32),
    )
    all_summed = (
        lax.all_gather(replica_share[0].astype(jnp.bfloat16), "rep", axis=1, tiled=True).astype(
            jnp.float32
        ),
        lax.all_gather(replica_share[1].astype(jnp.bfloat16), "rep", axis=1, tiled=True).astype(
            jnp.float32
        ),
        lax.all_gather(replica_share[2].astype(jnp.bfloat16), "rep", axis=1, tiled=True).astype(
            jnp.float32
        ),
        lax.all_gather(replica_share[3].astype(jnp.bfloat16), "rep", axis=1, tiled=True).astype(
            jnp.float32
        ),
        lax.all_gather(replica_share[4].astype(jnp.bfloat16), "rep", axis=0, tiled=True).astype(
            jnp.float32
        ),
        lax.all_gather(replica_share[5].astype(jnp.bfloat16), "rep", axis=1, tiled=True).astype(
            jnp.float32
        ),
        lax.all_gather(replica_share[6].astype(jnp.bfloat16), "rep", axis=1, tiled=True).astype(
            jnp.float32
        ),
        lax.all_gather(replica_share[7].astype(jnp.bfloat16), "rep", axis=1, tiled=True).astype(
            jnp.float32
        ),
        lax.all_gather(replica_share[8].astype(jnp.bfloat16), "rep", axis=1, tiled=True).astype(
            jnp.float32
        ),
        lax.all_gather(replica_share[9].astype(jnp.bfloat16), "rep", axis=0, tiled=True).astype(
            jnp.float32
        ),
    )
    seg_summed = all_summed[:5]
    cls_summed = all_summed[5:]
    pos_total = lax.psum(pos_local, ("rep", "fsdp"))
    seg_mat_grad = jnp.concatenate(
        [seg_summed[0], seg_summed[1], seg_summed[2], seg_summed[3]], axis=1
    )
    cls_mat_grad = jnp.concatenate(
        [cls_summed[0], cls_summed[1], cls_summed[2], cls_summed[3]], axis=1
    )
    return (
        output_rows.astype(jnp.bfloat16),
        input_grad.astype(jnp.bfloat16),
        seg_mat_grad,
        seg_summed[4],
        cls_mat_grad,
        cls_summed[4],
        pos_total,
        loss_value,
    )


LINE = 4
PLANE = 4
CORES = 2
LANES = 128
GROUP = LINE * PLANE
LOW, WIDE = jnp.bfloat16, jnp.float32
MODEL = HEADS * HEAD_DIM
SPAN = 2 * LANES
TILE_START = (0, 1, 3, 4)


def line_pairs(apart):
    return [(source, (source + apart * PLANE) % GROUP) for source in range(GROUP)]


def plane_pairs(mask):
    return [(source, source ^ mask) for source in range(GROUP)]


def along_line(value, apart):
    return lax.ppermute(value, "fsdp", line_pairs(apart))


def in_plane(value, mask):
    return lax.ppermute(value, "fsdp", plane_pairs(mask))


def other_core(value):
    return lax.ppermute(value, "rep", [(0, 1), (1, 0)])


def after(value, *events):
    return lax.optimization_barrier((value,) + events)[0]


def together(*values):
    return tuple(lax.optimization_barrier(values))


def shape_of(dims, dtype=WIDE):
    return jax.ShapeDtypeStruct(dims, dtype)


def run_kernel(body, name, outs, where, blocks, arrays, scratch=(), far=(), flops=0):
    in_specs = [pl.BlockSpec(memory_space=pltpu.SMEM)]
    in_specs += [pl.BlockSpec(memory_space=pltpu.HBM)] * len(blocks)
    in_specs += [pl.BlockSpec(memory_space=pltpu.VMEM)] * len(arrays)
    spaces = [pltpu.HBM if at in far else pltpu.VMEM for at in range(len(outs))]
    moved = sum(x.size * x.dtype.itemsize for x in list(blocks) + list(arrays))
    moved += sum(math.prod(o.shape) * jnp.dtype(o.dtype).itemsize for o in outs)
    return pl.pallas_call(
        body,
        name=name,
        out_shape=tuple(outs),
        in_specs=in_specs,
        out_specs=tuple(pl.BlockSpec(memory_space=space) for space in spaces),
        scratch_shapes=list(scratch),
        cost_estimate=pl.CostEstimate(flops=flops, bytes_accessed=moved, transcendentals=0),
        compiler_params=pltpu.CompilerParams(vmem_limit_bytes=VMEM_BYTES),
    )(where, *blocks, *arrays)


VMEM_BYTES = 24 * 1024 * 1024
HALF = MODEL // CORES
FF_HALF = FF // CORES
OWN = MODEL // GROUP
QUARTER = 3 * SPAN + 2 * FF // LINE
QUARTER_HALF = QUARTER // CORES


def aligned(start):
    return pl.multiple_of(start, LANES)


def wait_all(copies):
    for copy in copies:
        copy.wait()


def run_copies(pairs, sems):
    copies = [
        pltpu.make_async_copy(source, target, sems.at[at])
        for at, (source, target) in enumerate(pairs)
    ]
    for copy in copies:
        copy.start()
    wait_all(copies)


FIRST = 4 * HALF + LANES
OWN_CUT = FIRST + FF_HALF // 2
LINE_CUTS = (7 * LANES, FF_HALF // 2, FF_HALF // 2)
WIDTHS = (FIRST, FF_HALF, FF_HALF)


def group_pieces(group, refs):
    own, rest = refs[:LINE], refs[LINE:]
    own_x, own_y, far_x, far_y, line_x, line_y, late_x, late_y = rest
    width, cut = WIDTHS[group], LINE_CUTS[group]
    start = sum(WIDTHS[:group])
    if group == 0:
        bases = (sum(WIDTHS) - OWN_CUT, OWN_CUT)
    else:
        before, before_cut = WIDTHS[group - 1], LINE_CUTS[group - 1]
        bases = (2 * before - before_cut, before + before_cut)
    pieces = {(0, step): [(own[step], 0, 0, width)] for step in range(LINE)}
    for mask, whole, line, base in ((1, own_x, line_x, bases[0]), (2, own_y, line_y, bases[1])):
        pieces[mask, 0] = [(whole, start, 0, width)]
        for step in range(1, LINE):
            pieces[mask, step] = [(line, base + (step - 1) * width, 0, width)]
    middle = min(max(OWN_CUT - start, 0), width)
    far = []
    if middle > 0:
        far.append((far_y, start, 0, middle))
    if middle < width:
        far.append((far_x, start + middle - OWN_CUT, middle, width))
    pieces[3, 0] = far
    pieces[3, 1] = [(late_y, 0, 0, width)]
    pieces[3, 2] = [(late_y, width, 0, cut), (late_x, 0, cut, width)]
    pieces[3, 3] = [(late_x, width - cut, 0, width)]
    return pieces


def gather_group(where, group, refs, targets):
    line_at, plane_at = where[0], where[1]
    for (mask, step), parts in group_pieces(group, refs).items():
        chip = (line_at + LINE - step) % LINE * PLANE + (plane_at ^ mask)
        for whole, first, last in targets:
            for ref, offset, begin, end in parts:
                low, high = max(first, begin), min(last, end)
                if low < high:
                    source = slice(offset + low - begin, offset + high - begin)
                    whole[chip, :, low - first : high - first] = ref[:, source]


def gather_blocks(where, refs, base, width, targets):
    line_at, plane_at = where[0], where[1]
    half = LINE // 2
    for mask in range(PLANE):
        for step in range(LINE):
            if mask == 0:
                ref, offset = refs[step], 0
            elif mask == 3:
                ref = refs[LINE + 3] if step < half else refs[LINE + 2]
                offset = step % half * width
            else:
                ref, offset = refs[LINE + mask - 1], base + step * width
            chip = (line_at + LINE - step) % LINE * PLANE + (plane_at ^ mask)
            for whole, first, last in targets:
                whole[chip] = ref[:, offset + first : offset + last]


def whole_rows(ref):
    value = ref[...]
    return value.reshape(value.shape[0] * value.shape[1], value.shape[2])


def prepare_first_kernel(where, seg, seg_vec, cls_vec, flags, out, live_out, sems):
    core_at = where[2]
    pairs = []
    for piece in range(4):
        source = seg.at[:, pl.ds(aligned(piece * MODEL + core_at * HALF), HALF)]
        pairs.append((source, out.at[:, piece * HALF : (piece + 1) * HALF]))
    run_copies(pairs, sems)
    size = seg_vec.shape[0]
    vecs = [vec[...].astype(WIDE).reshape(1, size) for vec in (seg_vec, cls_vec)]
    lines = -(-size // LANES)
    block = jnp.zeros((OWN, LANES), WIDE)
    row_at = lax.broadcasted_iota(jnp.int32, (OWN, LANES), 0)
    for which in range(2):
        for line in range(lines):
            width = min(LANES, size - line * LANES)
            value = vecs[which][:, line * LANES : line * LANES + width]
            if width < LANES:
                value = jnp.concatenate([value, jnp.zeros((1, LANES - width), WIDE)], axis=1)
            block = jnp.where(row_at == which * lines + line, value, block)
    live = flags[...].astype(WIDE).reshape(1, SEG)
    live_out[...] = live
    count = jnp.sum(live, axis=1, keepdims=True)
    block = jnp.where(row_at == 2 * lines, count, block)
    out[:, 4 * HALF :] = block.astype(LOW)


def prepare_rest_kernel(where, seg, cls, *refs):
    second_out, third_out = refs[:2]
    step_outs, out_half, order_out = refs[2 : 2 + LINE], refs[2 + LINE], refs[3 + LINE]
    quarters, sems = refs[4 + LINE :]
    line_at, plane_at, core_at = where[0], where[1], where[2]
    start = core_at * FF_HALF
    pairs = [
        (seg.at[:, pl.ds(aligned(4 * MODEL + start), FF_HALF)], second_out),
        (seg.at[:, pl.ds(aligned(4 * MODEL + FF + start), FF_HALF)], third_out),
        (cls.at[:, pl.ds(aligned(3 * MODEL + core_at * HALF), HALF)], out_half),
    ]
    part = FF // LINE
    for at in range(LINE):
        first = TILE_START[at] * LANES
        plan = [(piece * MODEL + first, SPAN, piece * SPAN) for piece in range(3)]
        plan += [
            (4 * MODEL + piece * FF + at * part, part, 3 * SPAN + piece * part)
            for piece in range(2)
        ]
        for source, size, target in plan:
            pairs.append(
                (
                    cls.at[:, source : source + size],
                    quarters.at[at, :, target : target + size],
                )
            )
    run_copies(pairs, sems)
    lanes = pl.ds(aligned(core_at * QUARTER_HALF), QUARTER_HALF)
    for step, out in enumerate(step_outs):
        out[...] = quarters[(line_at + step) % LINE, :, lanes]
    column = lax.broadcasted_iota(jnp.int32, (1, SPAN), 1)
    feature = lax.broadcasted_iota(jnp.int32, (MODEL, SPAN), 0)
    turn = sum((column >= OWN * step).astype(jnp.int32) for step in range(1, LINE))
    held = column - OWN * turn
    turn = (line_at + turn) % LINE
    for mask in range(PLANE):
        source = (turn * PLANE + (plane_at ^ mask)) * OWN + held
        source = jnp.where(column < OWN * LINE, source, -1)
        order_out[:, mask * SPAN : (mask + 1) * SPAN] = (feature == source).astype(LOW)


def prepare_kernel(where, seg, cls, *refs):
    (seg_vec, cls_vec, flags, first_out, live_out), refs = refs[:5], refs[5:]
    rest, (first_sems, quarters, sems) = refs[:-3], refs[-3:]
    prepare_first_kernel(where, seg, seg_vec, cls_vec, flags, first_out, live_out, first_sems)
    prepare_rest_kernel(where, seg, cls, *rest, quarters, sems)


def lane_mask(rows, head):
    lane = lax.broadcasted_iota(jnp.int32, (rows, LANES), 1)
    return (lane < HEAD_DIM) if head == 0 else (lane >= HEAD_DIM)


def masked(value, mask):
    return jnp.where(mask, value, jnp.zeros_like(value))


def head_probabilities(query, key, allowed):
    scores = product_right(query, key) * HEAD_DIM ** (-0.5)
    scores = jnp.where(allowed, scores, MASK_FILL)
    raised = jnp.exp(scores - jnp.max(scores, axis=-1, keepdims=True))
    return raised / jnp.sum(raised, axis=-1, keepdims=True)


def attend_tiles(qkv, width, allowed):
    rows = qkv.shape[0]
    mixed = []
    for tile in range(width // LANES):
        at = tile * LANES
        query, key, value = (
            qkv[:, piece * width + at : piece * width + at + LANES] for piece in range(3)
        )
        total = jnp.zeros((rows, LANES), WIDE)
        for head in range(2):
            mask = lane_mask(rows, head)
            weights = head_probabilities(masked(query, mask), key, allowed).astype(LOW)
            total = total + product_plain(weights, masked(value, mask))
        mixed.append(total.astype(LOW))
    return mixed


def attend_tiles_back(qkv, grad_mixed, width, allowed):
    rows = qkv.shape[0]
    scale = HEAD_DIM ** (-0.5)
    results = ([], [], [])
    for tile in range(width // LANES):
        at = tile * LANES
        query, key, value = (
            qkv[:, piece * width + at : piece * width + at + LANES] for piece in range(3)
        )
        grad = grad_mixed[:, at : at + LANES]
        totals = [jnp.zeros((rows, LANES), WIDE) for _ in range(3)]
        for head in range(2):
            mask = lane_mask(rows, head)
            query_low, key_low, grad_low = (masked(x, mask) for x in (query, key, grad))
            chance = head_probabilities(query_low, key, allowed)
            grad_chance = product_right(grad_low, value)
            inner = jnp.sum(grad_chance * chance, axis=-1, keepdims=True)
            grad_scores = (chance * (grad_chance - inner)).astype(LOW)
            totals[0] = totals[0] + product_plain(grad_scores, key_low)
            totals[1] = totals[1] + product_left(grad_scores, query_low)
            totals[2] = totals[2] + product_left(chance.astype(LOW), grad_low)
        results[0].append((totals[0] * scale).astype(LOW))
        results[1].append((totals[1] * scale).astype(LOW))
        results[2].append(totals[2].astype(LOW))
    return results[0] + results[1] + results[2]


def token_allowed(live_row):
    shape = (SEG, SEG)
    same = lax.broadcasted_iota(jnp.int32, shape, 0) == lax.broadcasted_iota(jnp.int32, shape, 1)
    return (live_row > 0.5) | same


def qkv_kernel(where, *refs):
    blocks = refs[:12]
    hidden, hidden_got, live_row, live_got, order = refs[12:17]
    weight, out_low, out_high, qkv_out, mixed_out = refs[17:22]
    vectors_out, count_out, ordered_out = refs[22:25]
    vec_rows, flat, inputs, out_half = refs[25:]
    core_at = where[2]
    gather_group(
        where,
        0,
        blocks,
        (
            (weight, 0, 3 * HALF),
            (out_half, 3 * HALF, 4 * HALF),
            (vec_rows, 4 * HALF, 4 * HALF + LANES),
        ),
    )
    out_low[...] = out_half[: GROUP // 2]
    out_high[...] = out_half[GROUP // 2 :]
    piece = (8 * MODEL + FF) // GROUP
    lines = -(-piece // LANES)
    count = jnp.zeros((1, LANES), WIDE)
    for chip in range(GROUP):
        rows = vec_rows[chip, 0:16, :].astype(WIDE)
        for block in range(2):
            joined = jnp.concatenate(
                [rows[block * lines + r : block * lines + r + 1] for r in range(lines)], axis=1
            )
            flat[block : block + 1, chip * piece : (chip + 1) * piece] = joined[:, :piece]
        count = count + rows[2 * lines : 2 * lines + 1]
    rows_each = (8 * MODEL + FF) // MODEL
    for block in range(2):
        for row in range(rows_each):
            vectors_out[block * rows_each + row : block * rows_each + row + 1, :] = flat[
                block : block + 1, row * MODEL : (row + 1) * MODEL
            ]
    count_out[...] = jnp.broadcast_to(count, count_out.shape)
    inputs[:SEG] = hidden[...]
    inputs[SEG:] = hidden_got[...]
    projected = product_plain(inputs[...], whole_rows(weight))
    lanes = pl.ds(aligned(core_at * HALF), HALF)
    qkv_out[:, :HALF] = (projected[:, :HALF] + vectors_out[0:1, lanes]).astype(LOW)
    qkv_out[:, HALF : 2 * HALF] = projected[:, HALF : 2 * HALF].astype(LOW)
    qkv_out[:, 2 * HALF :] = (projected[:, 2 * HALF :] + vectors_out[1:2, lanes]).astype(LOW)
    for part, live in enumerate((live_row, live_got)):
        rows = slice(part * SEG, (part + 1) * SEG)
        tiles = attend_tiles(qkv_out[rows, :], HALF, token_allowed(live[...]))
        for tile, value in enumerate(tiles):
            mixed_out[rows, tile * LANES : (tile + 1) * LANES] = value
    ordered_out[...] = product_plain(inputs[...], order[...]).astype(LOW)


def norm_rows(summed):
    row_mean = jnp.mean(summed, axis=-1, keepdims=True)
    centered = summed - row_mean
    inv_dev = lax.rsqrt(jnp.mean(centered * centered, axis=-1, keepdims=True) + NORM_EPS)
    return centered * inv_dev, inv_dev


def norm_rows_back(grad_out, normed, inv_dev, gain):
    scaled = grad_out * gain
    mean_one = jnp.mean(scaled, axis=-1, keepdims=True)
    mean_two = jnp.mean(scaled * normed, axis=-1, keepdims=True)
    return inv_dev * (scaled - mean_one - normed * mean_two)


def column_sum(value):
    return jnp.sum(value.astype(WIDE), axis=0, keepdims=True)


def four_rows(vectors, first):
    return jnp.concatenate([vectors[first + at : first + at + 1, :] for at in range(4)], axis=1)


def gelu_both(before):
    half = 0.5 * (1.0 + lax.erf(before * SQRT_HALF))
    slope = half + before * jnp.exp(-0.5 * before * before) * INV_SQRT_TWO_PI
    return before * half, slope


def out_kernel(where, hidden, mixed, mixed_got, low, high, low_got, high_got, *refs):
    vectors, order, full_out, ordered_out, normed_out, inv_out, low_out, mixed_full = refs
    core_at = where[2]
    own, other = aligned(core_at * HALF), aligned((1 - core_at) * HALF)
    rows = MODEL // 2
    full_out[:rows, pl.ds(own, HALF)] = whole_rows(low)
    full_out[rows:, pl.ds(own, HALF)] = whole_rows(high)
    full_out[:rows, pl.ds(other, HALF)] = whole_rows(low_got)
    full_out[rows:, pl.ds(other, HALF)] = whole_rows(high_got)
    mixed_full[:, pl.ds(own, HALF)] = mixed[...]
    mixed_full[:SEG, pl.ds(other, HALF)] = mixed_got[SEG:, :]
    mixed_full[SEG:, pl.ds(other, HALF)] = mixed_got[:SEG, :]
    branch = product_plain(mixed_full[:SEG, :], full_out[...])
    normed, inv_dev = norm_rows(hidden[...].astype(WIDE) + branch + vectors[2:3, :])
    normed_out[...] = normed
    inv_out[...] = inv_dev
    low_out[...] = (normed * vectors[4:5, :] + vectors[5:6, :]).astype(LOW)
    ordered_out[...] = product_plain(mixed_full[...], order[...]).astype(LOW)


def up_kernel(where, *refs):
    blocks = refs[:12]
    low, low_got, vectors = refs[12:15]
    weight, act_out, slope_out, both = refs[15:]
    core_at = where[2]
    gather_group(where, 1, blocks, ((weight, 0, FF_HALF),))
    both[:SEG] = low[...]
    both[SEG:] = low_got[...]
    for at in range(FF_HALF // MODEL):
        columns = slice(at * MODEL, (at + 1) * MODEL)
        held = weight[:, :, columns]
        before = product_plain(both[...], held.reshape(MODEL, MODEL))
        bias = vectors[pl.ds(8 + core_at * (FF_HALF // MODEL) + at, 1), :]
        value, slope = gelu_both(before + bias)
        act_out[:, columns] = value.astype(LOW)
        slope_out[:, columns] = slope


def down_kernel(where, *refs):
    blocks, act = refs[:12], refs[12]
    weight, own_out, send_out = refs[13:]
    gather_group(where, 2, blocks, ((weight, 0, FF_HALF),))
    partial = product_right(act[...], whole_rows(weight))
    own_out[...] = partial[:SEG]
    send_out[...] = partial[SEG:]


def seg_rows_kernel(where, *refs):
    own, got, normed_first, vectors, targets, live, seg_pos = refs[:7]
    normed_out, inv_out, diff_out, rows_out, head_out = refs[7:]
    doc, number = where[3], where[4]
    first = normed_first[...] * vectors[4:5, :] + vectors[5:6, :]
    normed, inv_dev = norm_rows(first + own[...] + got[...] + vectors[3:4, :])
    normed_out[...] = normed
    inv_out[...] = inv_dev
    rows = normed * vectors[6:7, :] + vectors[7:8, :]
    shape = (SEG, SEG)
    same = lax.broadcasted_iota(jnp.int32, shape, 0) == lax.broadcasted_iota(jnp.int32, shape, 1)
    live_rows = jnp.sum(jnp.where(same, live[...], 0.0), axis=1, keepdims=True)
    target_rows = targets[...].astype(WIDE)
    output = rows * live_rows
    rows_out[...] = output
    diff = (output - target_rows) * live_rows
    row_at = lax.broadcasted_iota(jnp.int32, (SEG, 1), 0)
    diff = jnp.where(row_at > 0, diff, 0.0)
    diff_out[...] = diff
    table = seg_pos[...].astype(WIDE)
    chosen = lax.broadcasted_iota(jnp.int32, table.shape, 0) == number
    position = jnp.sum(jnp.where(chosen, table, 0.0), axis=0, keepdims=True)
    head_out[:, :MODEL] = rows[0:1, :] + position
    head_out[:, MODEL : 2 * MODEL] = target_rows[0:1, :]
    square = jnp.sum(column_sum(diff * diff), axis=1, keepdims=True)
    lane = lax.broadcasted_iota(jnp.int32, (1, LANES), 1)
    facts = jnp.where(lane == 0, live_rows[0:1, :], 0.0)
    facts = jnp.where(lane == 1, doc.astype(WIDE), facts)
    facts = jnp.where(lane == 2, number.astype(WIDE), facts)
    facts = jnp.where(lane == 3, square, facts)
    head_out[:, 2 * MODEL :] = facts


def second_norm_kernel(where, *refs):
    diff, count, normed, inv_dev, vectors, first, first_got, order = refs[:8]
    grad_out, low_out, sums_out, ordered_out, both = refs[8:]
    grad_top = diff[...] * ((SEG * GROUP * CORES) / count[0:1, 0:1])
    normed_rows = normed[...]
    grad = norm_rows_back(grad_top, normed_rows, inv_dev[...], vectors[6:7, :])
    low = grad.astype(LOW)
    grad_out[...] = grad
    low_out[...] = low
    sums_out[0:1, :] = column_sum(low)
    sums_out[1:2, :] = column_sum(grad_top * normed_rows)
    sums_out[2:3, :] = column_sum(grad_top)
    both[:SEG] = first[...]
    both[SEG:] = first_got[...]
    ordered_out[...] = product_plain(both[...], order[...]).astype(LOW)


def mlp_back_kernel(where, *refs):
    low, low_got, down_weight, up_weight, slope = refs[:5]
    pre_out, own_out, send_out, sums_out, both = refs[5:]
    both[:SEG] = low[...]
    both[SEG:] = low_got[...]
    for at in range(FF_HALF // MODEL):
        columns = slice(at * MODEL, (at + 1) * MODEL)
        held = down_weight[:, :, columns]
        before = product_plain(both[...], held.reshape(MODEL, MODEL))
        pre = (before * slope[:, columns]).astype(LOW)
        pre_out[:, columns] = pre
        sums_out[at : at + 1, :] = column_sum(pre)
    partial = product_right(pre_out[...], whole_rows(up_weight))
    own_out[...] = partial[:SEG]
    send_out[...] = partial[SEG:]


def scatter_parts(where, parts, outs, sems):
    line_at, plane_at = where[0], where[1]
    far_low, far_high, to_x, to_y, kept = outs
    half = LINE // 2
    copies = []
    for mask in range(PLANE):
        for step in range(LINE):
            source = parts.at[(line_at + step) % LINE * PLANE + (plane_at ^ mask)]
            if mask == 3:
                target = far_low.at[step] if step < half else far_high.at[step - half]
            else:
                target = (kept, to_x, to_y)[mask].at[step]
            copies.append(pltpu.make_async_copy(source, target, sems.at[len(copies)]))
    for copy in copies:
        copy.start()
    wait_all(copies)


def mlp_products(refs, masks, both, store):
    first, second, second_got, pre, act, order = refs
    both[:SEG] = second[...]
    both[SEG:] = second_got[...]
    for mask in masks:
        lanes = slice(mask * SPAN, (mask + 1) * SPAN)
        turned = product_plain(both[...], order[:, lanes]).astype(LOW)
        for at, (left, right) in enumerate(((first[:, lanes], pre), (turned, act))):
            for piece in range(FF_HALF // MODEL):
                start = piece * MODEL
                product = product_left(left, right[:, start : start + MODEL])
                product = product[: LINE * OWN].astype(LOW).reshape(LINE, OWN, MODEL)
                target = at * FF_HALF + start
                store(mask, slice(target, target + MODEL), product)


def mlp_far_kernel(where, *refs):
    low_out, high_out, both = refs[6:]
    half = LINE // 2

    def store(mask, columns, product):
        low_out[:, :, columns] = product[:half]
        high_out[:, :, columns] = product[half:]

    mlp_products(refs[:6], (3,), both, store)


def mlp_near_kernel(where, *refs):
    outs, both = refs[6:9], refs[9]

    def store(mask, columns, product):
        outs[mask - 1][:, :, columns] = product

    mlp_products(refs[:6], (1, 2, 0), both, store)


def attn_product(where, refs, mask, piece):
    hidden, mixed, proj, branch, got = refs
    lanes = slice(mask * SPAN, (mask + 1) * SPAN)
    if piece < 3:
        right = proj[:, piece * HALF : (piece + 1) * HALF]
        product = product_left(hidden[:, lanes], right)
    else:
        own = branch[:, pl.ds(aligned(where[2] * HALF), HALF)]
        product = product_left(mixed[:SEG, lanes], own)
        product = product + product_left(mixed[SEG:, lanes], got[:, HALF:])
    return product[: LINE * OWN].astype(LOW).reshape(LINE, OWN, HALF)


def attn_far_kernel(where, *refs):
    low_out, high_out = refs[5:]
    half = LINE // 2
    for piece in range(4):
        columns = slice(piece * HALF, (piece + 1) * HALF)
        product = attn_product(where, refs[:5], 3, piece)
        low_out[:, :, columns] = product[:half]
        high_out[:, :, columns] = product[half:]


def attn_near_kernel(where, *refs):
    proj, (top_row, out_rows, live_row) = refs[2], refs[5:8]
    weight, sums_first, sums_second, sums_up, head_top, head_normed, data = refs[8:15]
    x_out, y_out, kept_out, output_out, own_out, send_out, payload_out, rows = refs[15:]
    core_at = where[2]
    partial = product_right(proj[...], whole_rows(weight))
    own_out[...] = partial[:SEG]
    send_out[...] = partial[SEG:]
    row_at = lax.broadcasted_iota(jnp.int32, (SEG, 1), 0)
    output = jnp.where(row_at == 0, top_row[...] * live_row[:, 0:1], out_rows[...])
    output_out[...] = output.astype(LOW)
    for mask, out in ((1, x_out), (2, y_out), (0, kept_out)):
        for piece in range(4):
            columns = slice(piece * HALF, (piece + 1) * HALF)
            out[:, :, columns] = attn_product(where, refs[:5], mask, piece)
    lanes = pl.ds(aligned(core_at * HALF), HALF)
    rows[...] = jnp.zeros_like(rows)
    rows[0:12, :] = data[0:12, :]
    rows[12:13, lanes] = column_sum(proj[:, :HALF])
    rows[13:14, lanes] = column_sum(proj[:, 2 * HALF :])
    rows[14:15, :] = sums_first[0:1, :]
    rows[15:16, :] = sums_second[0:1, :] + data[2:3, :]
    rows[16:18, :] = sums_first[1:3, :]
    rows[18:19, :] = sums_second[1:2, :] + head_top[...] * head_normed[0:1, :]
    rows[19:20, :] = sums_second[2:3, :] + head_top[...]
    for at in range(FF_HALF // MODEL):
        total = sums_up[at : at + 1, :] + data[4 + 2 * at : 5 + 2 * at, :]
        total = total + data[5 + 2 * at : 6 + 2 * at, :]
        rows[pl.ds(20 + core_at * (FF_HALF // MODEL) + at, 1), :] = total
    payload_out[...] = rows[...].astype(LOW)


def fold_kernel(where, kept, got_x, got_y, *refs):
    extra, own_out, sent = refs[: -LINE], refs[-LINE], refs[1 - LINE :]
    rows = kept.shape[1]
    for step in range(LINE):
        total = kept[step].astype(WIDE) + got_x[step].astype(WIDE) + got_y[step].astype(WIDE)
        if step == 0:
            own_out[...] = total
            continue
        out = sent[step - 1]
        out[:rows, :] = total.astype(LOW)
        if extra:
            out[rows:, :] = jnp.zeros_like(out[rows:, :])
            out[rows:, : extra[0].shape[1]] = extra[0][...]


def reduce_far(parts):
    return together(in_plane(parts[0], 2), in_plane(parts[1], 1))


def reduce_add(where, parts, far):
    shape = parts[2].shape
    return run_kernel(
        add_far_kernel,
        "add_far",
        [shape_of(shape, LOW)] * 2,
        where,
        (),
        tuple(far) + (parts[2], parts[3]),
    )


def reduce_fold(where, kept, got, *extra):
    _, rows, columns = kept.shape
    more = sum(value.shape[0] for value in extra)
    return run_kernel(
        fold_kernel,
        "fold",
        [shape_of((rows, columns))] + [shape_of((rows + more, columns), LOW)] * (LINE - 1),
        where,
        (),
        (kept,) + tuple(got) + extra,
    )


def reduce_line(own, pieces):
    total = own
    for piece in pieces:
        total = total + piece[: own.shape[0]].astype(WIDE)
    return total


def head_back_kernel(where, *refs):
    grad, grad_got, down_weight, up_weight, slope, act, low, low_got = refs[:8]
    own_out, send_out, data_out = refs[8:]
    few = 16
    row_at = lax.broadcasted_iota(jnp.int32, (few, 1), 0)

    def two_rows(first, second):
        return jnp.where(row_at == 0, first, jnp.where(row_at == 1, second, 0.0))

    second = two_rows(grad[...], grad_got[...]).astype(LOW)
    data_out[0:1, :] = low[0:1, :].astype(WIDE)
    data_out[1:2, :] = low_got[0:1, :].astype(WIDE)
    data_out[2:4, :] = second[0:2].astype(WIDE)
    partial = jnp.zeros((few, MODEL), WIDE)
    for at in range(FF_HALF // MODEL):
        columns = slice(at * MODEL, (at + 1) * MODEL)
        before = product_plain(second, down_weight[:, :, columns].reshape(MODEL, MODEL))
        slopes = two_rows(slope[0:1, columns], slope[SEG : SEG + 1, columns])
        pre = (before * slopes).astype(LOW)
        partial = partial + product_right(pre, up_weight[:, :, columns].reshape(MODEL, MODEL))
        data_out[4 + 2 * at : 6 + 2 * at, :] = pre[0:2].astype(WIDE)
        data_out[8 + 2 * at : 9 + 2 * at, :] = act[0:1, columns].astype(WIDE)
        data_out[9 + 2 * at : 10 + 2 * at, :] = act[SEG : SEG + 1, columns].astype(WIDE)
    own_out[...] = partial[0:1]
    send_out[...] = partial[1:2]


def first_norm_kernel(where, *refs):
    second_grad, own, got, head_grad, head_own, head_got = refs[:6]
    normed_rows, inv_dev, vectors, out_weight = refs[6:10]
    grad_out, branch_out, mixed_out, send_out, sums_out = refs[10:]
    core_at = where[2]
    grad_rows = second_grad[...] + own[...] + got[...]
    head = head_grad[...] + head_own[...] + head_got[...]
    row_at = lax.broadcasted_iota(jnp.int32, (SEG, 1), 0)
    grad_rows = jnp.where(row_at == 0, head, grad_rows)
    normed = normed_rows[...]
    grad = norm_rows_back(grad_rows, normed, inv_dev[...], vectors[4:5, :])
    grad_out[...] = grad
    branch = grad.astype(LOW)
    branch_out[...] = branch
    mixed_out[...] = product_right(branch, out_weight[...]).astype(LOW)
    other = pl.ds(aligned((1 - core_at) * HALF), HALF)
    send_out[:, :HALF] = mixed_out[:, other]
    send_out[:, HALF:] = branch_out[:, other]
    sums_out[0:1, :] = column_sum(branch)
    sums_out[1:2, :] = column_sum(grad_rows * normed)
    sums_out[2:3, :] = column_sum(grad_rows)


def attn_back_kernel(where, *refs):
    qkv, mixed_grad, got, live_row, live_got, proj_out = refs
    core_at = where[2]
    lanes = pl.ds(aligned(core_at * HALF), HALF)
    for part, live in enumerate((live_row, live_got)):
        at = slice(part * SEG, (part + 1) * SEG)
        grad = mixed_grad[:, lanes] if part == 0 else got[:, :HALF]
        pieces = attend_tiles_back(qkv[at, :], grad, HALF, token_allowed(live[...]))
        for tile, value in enumerate(pieces):
            proj_out[at, tile * LANES : (tile + 1) * LANES] = value


def cls_gather_kernel(where, *refs):
    blocks = refs[:8]
    own_out, from_x, from_y, far_x = refs[8], refs[4], refs[5], refs[6]
    weight_out, out_rows = refs[9:]
    plane_at = where[1]
    gather_blocks(where, blocks, 0, QUARTER_HALF, ((weight_out, 0, QUARTER_HALF),))
    first = LINE * QUARTER_HALF
    out_rows[plane_at] = own_out[...]
    out_rows[plane_at ^ 1] = from_x[:, first : first + HALF]
    out_rows[plane_at ^ 2] = from_y[:, first : first + HALF]
    first = LINE // 2 * QUARTER_HALF
    out_rows[plane_at ^ 3] = far_x[:, first : first + HALF]


def cls_weight_kernel(where, own, got, out_half, out_got, weight_out, out_full):
    line_at, core_at = where[0], where[2]
    out_full[...] = jnp.zeros_like(out_full)
    for value, part, core in ((own, out_half, core_at), (got, out_got, 1 - core_at)):
        weight_out[:, :, pl.ds(aligned(core * QUARTER_HALF), QUARTER_HALF)] = value[...]
        rows = part[...].reshape(3, HEAD_DIM, HALF)
        out_full[pl.ds(line_at % 2, 3), :, pl.ds(aligned(core * HALF), HALF)] = rows


def add_far_kernel(where, far_low, far_high, to_x, to_y, x_out, y_out):
    half = LINE // 2
    x_out[:half] = to_x[:half] + far_low[...]
    x_out[half:] = to_x[half:]
    y_out[:half] = to_y[:half]
    y_out[half:] = to_y[half:] + far_high[...]


def row_from_column(column, size):
    shape = (size, size)
    same = lax.broadcasted_iota(jnp.int32, shape, 0) == lax.broadcasted_iota(jnp.int32, shape, 1)
    return jnp.sum(jnp.where(same, column, 0.0), axis=0, keepdims=True)


def head_allowed(heads):
    facts = heads[:, 2 * MODEL :]
    live, doc = facts[:, 0:1], facts[:, 1:2]
    shape = (GROUP, GROUP)
    same = lax.broadcasted_iota(jnp.int32, shape, 0) == lax.broadcasted_iota(jnp.int32, shape, 1)
    live_row, doc_row = row_from_column(live, GROUP), row_from_column(doc, GROUP)
    return ((live_row > 0.5) & (doc == doc_row)) | same


def quarter_mask(quarter):
    lane = lax.broadcasted_iota(jnp.int32, (GROUP, SPAN), 1)
    first = (quarter % 2) * HEAD_DIM
    return (lane >= first) & (lane < first + 3 * HEAD_DIM)


def quarter_piece(vectors, row, quarter):
    value = jnp.zeros((1, SPAN), WIDE)
    for at in range(LINE):
        first = TILE_START[at] * LANES
        value = jnp.where(quarter == at, vectors[row : row + 1, first : first + SPAN], value)
    return value


def cls_attend_kernel(where, *refs):
    stacks, vectors, weight, out_weight = refs[:4], refs[4], refs[5], refs[6]
    heads_out, qkv_out, mixed_out, part_out = refs[7:]
    line_at, plane_at = where[0], where[1]
    for step, stack in enumerate(stacks):
        for mask in range(PLANE):
            row = (line_at + LINE - step) % LINE * PLANE + (plane_at ^ mask)
            heads_out[pl.ds(row, 1), :] = stack[mask : mask + 1, :]
    heads = heads_out[...]
    inputs = heads[:, :MODEL].astype(LOW)
    projected = product_plain(inputs, weight[:, : 3 * SPAN])
    query = projected[:, :SPAN] + quarter_piece(vectors, 12, line_at)
    value = projected[:, 2 * SPAN :] + quarter_piece(vectors, 13, line_at)
    qkv_out[:, :SPAN] = query.astype(LOW)
    qkv_out[:, SPAN : 2 * SPAN] = projected[:, SPAN : 2 * SPAN].astype(LOW)
    qkv_out[:, 2 * SPAN :] = value.astype(LOW)
    mixed = attend_tiles(qkv_out[...], SPAN, head_allowed(heads))
    mixed = masked(jnp.concatenate(mixed, axis=1), quarter_mask(line_at))
    mixed_out[...] = mixed
    part_out[...] = product_plain(mixed, out_weight[...])


def cls_mlp_kernel(where, *refs):
    heads, own, got_one, got_two, got_three, vectors, weight = refs[:7]
    normed_out, inv_out, low_out, act_out, slope_out, part_out = refs[7:]
    line_at = where[0]
    branch = own[...] + got_one[...] + got_two[...] + got_three[...]
    normed, inv_dev = norm_rows(heads[:, :MODEL] + branch + vectors[14:15, :])
    normed_out[...] = normed
    inv_out[...] = inv_dev
    low = (normed * vectors[16:17, :] + vectors[17:18, :]).astype(LOW)
    low_out[...] = low
    part = FF // LINE
    first = 3 * SPAN
    bias = vectors[pl.ds(20 + line_at, 1), :]
    before = product_plain(low, weight[:, first : first + part]) + bias
    value, slope = gelu_both(before)
    act = value.astype(LOW)
    act_out[...] = act
    slope_out[...] = slope
    part_out[...] = product_right(act, weight[:, first + part :])


def cls_top_kernel(where, *refs):
    heads, own, got_one, got_two, got_three, vectors, weight = refs[:7]
    normed_first, count, slope = refs[7:10]
    top_out, square_out, grad_out, second_out, pre_out, part_out, sums_out = refs[10:17]
    held = refs[17]
    rank = where[0] * PLANE + where[1]
    first = normed_first[...] * vectors[16:17, :] + vectors[17:18, :]
    down = own[...] + got_one[...] + got_two[...] + got_three[...]
    normed, inv_dev = norm_rows(first + down + vectors[15:16, :])
    rows = normed * vectors[18:19, :] + vectors[19:20, :]
    held[...] = rows
    top_out[...] = held[pl.ds(rank, 1), :]
    facts = heads[:, 2 * MODEL :]
    live = facts[:, 0:1]
    diff = (rows * live - heads[:, MODEL : 2 * MODEL]) * live
    square = jnp.sum(column_sum(diff * diff), axis=1, keepdims=True)
    square = square + jnp.sum(facts[:, 3:4], axis=0, keepdims=True)
    square_out[...] = jnp.broadcast_to(square, square_out.shape)
    grad_top = diff * ((SEG * GROUP * CORES) / count[0:1, 0:1])
    grad = norm_rows_back(grad_top, normed, inv_dev, vectors[18:19, :])
    sums_out[0:1, :] = column_sum(grad_top * normed)
    sums_out[1:2, :] = column_sum(grad_top)
    grad_out[...] = grad
    second = grad.astype(LOW)
    second_out[...] = second
    part = FF // LINE
    at = 3 * SPAN
    pre = (product_plain(second, weight[:, at + part :]) * slope[...]).astype(LOW)
    pre_out[...] = pre
    part_out[...] = product_right(pre, weight[:, at : at + part])


def cls_attend_back_kernel(where, *refs):
    heads, own, got_one, got_two, got_three, vectors, weight, out_weight = refs[:8]
    grad_in, normed_first, inv_first, qkv = refs[8:12]
    grad_out, branch_out, proj_out, part_out, sums_out = refs[12:]
    line_at = where[0]
    grad_first = grad_in[...] + own[...] + got_one[...] + got_two[...] + got_three[...]
    normed = normed_first[...]
    grad = norm_rows_back(grad_first, normed, inv_first[...], vectors[16:17, :])
    sums_out[0:1, :] = column_sum(grad_first * normed)
    sums_out[1:2, :] = column_sum(grad_first)
    grad_out[...] = grad
    branch = grad.astype(LOW)
    branch_out[...] = branch
    mask = quarter_mask(line_at)
    mixed_grad = masked(product_right(branch, out_weight[...]).astype(LOW), mask)
    pieces = attend_tiles_back(qkv[...], mixed_grad, SPAN, head_allowed(heads[...]))
    tiles = SPAN // LANES
    for piece in range(3):
        joined = jnp.concatenate(pieces[piece * tiles : (piece + 1) * tiles], axis=1)
        proj_out[:, piece * SPAN : (piece + 1) * SPAN] = masked(joined, mask)
    part_out[...] = product_right(proj_out[...], weight[:, : 3 * SPAN])


def cls_end_kernel(where, *refs):
    heads, grad, own, got_one, got_two, got_three = refs[:6]
    square, sums_back, sums_top = refs[6:9]
    normed_second, inv_second, vectors = refs[9:12]
    row_out, second_out, shared_out, held = refs[12:]
    rank = where[0] * PLANE + where[1]
    total = grad[...] + own[...] + got_one[...] + got_two[...] + got_three[...]
    held[...] = total
    row = held[pl.ds(rank, 1), :]
    row_out[...] = row
    second_out[...] = norm_rows_back(
        row, normed_second[0:1, :], inv_second[0:1, :], vectors[6:7, :]
    )
    number = row_from_column(heads[:, 2 * MODEL + 2 : 2 * MODEL + 3], GROUP)
    entry = lax.broadcasted_iota(jnp.int32, (GROUP, GROUP), 0).astype(WIDE)
    hot = (entry == number).astype(WIDE)
    shared_out[0:GROUP, :] = jnp.dot(hot, total, precision=lax.Precision.HIGHEST)
    shared_out[GROUP : GROUP + 1, 0:LANES] = square[0:1, :]
    shared_out[GROUP + 1 : GROUP + 3, :] = sums_back[0:2, :]
    shared_out[GROUP + 3 : GROUP + 5, :] = sums_top[0:2, :]


def head_mlp_kernel(where, *refs):
    cls_mlp_kernel(where, *refs[:7], *refs[11:17])
    add_far_kernel(where, *refs[7:11], *refs[17:])


def head_end_kernel(where, *refs):
    cls_end_kernel(where, *refs[:12], *refs[16:19], refs[23])
    fold_kernel(where, *refs[12:16], *refs[19:23])


def attn_add_kernel(where, *refs):
    far_low, far_high, to_x, to_y, grad, own, got, x_out, y_out, input_out = refs
    add_far_kernel(where, far_low, far_high, to_x, to_y, x_out, y_out)
    input_out[...] = (grad[...] + own[...] + got[...]).astype(LOW)


def rows_input_kernel(where, *refs):
    cls_rows_kernel(where, *refs[:8], refs[11], refs[13])
    grad, own, got, input_out = refs[8], refs[9], refs[10], refs[12]
    input_out[...] = (grad[...] + own[...] + got[...]).astype(LOW)


def cls_rows_kernel(where, *refs):
    packs = refs[:4]
    heads, branch, low, second = refs[4:8]
    out, kept = refs[8:]
    line_at = where[0]
    rows, width = kept.shape[1:]
    for step, pack in enumerate(packs):
        first = pack.shape[0] - rows
        kept[(line_at + LINE - step) % LINE] = pack[first:, :width]
    starts = (MODEL, 2 * MODEL, 3 * MODEL, 4 * MODEL)
    out[:, 0:MODEL] = heads[:, :MODEL].astype(LOW)
    for piece, start in enumerate(starts):
        from_at = piece * SPAN
        for tile in range(MODEL // LANES):
            total = None
            for at in range(PLANE):
                inner = tile - TILE_START[at]
                if inner in (0, 1):
                    first = from_at + inner * LANES
                    value = kept[at, :, first : first + LANES]
                    total = value if total is None else total + value
            out[:, start + tile * LANES : start + (tile + 1) * LANES] = total
    out[:, 5 * MODEL : 6 * MODEL] = branch[...]
    out[:, 6 * MODEL : 7 * MODEL] = low[...]
    out[:, 7 * MODEL + FF : 8 * MODEL + FF] = second[...]
    part = FF // LINE
    for at in range(PLANE):
        first = 4 * SPAN
        out[:, 7 * MODEL + at * part : 7 * MODEL + (at + 1) * part] = kept[
            at, :, first : first + part
        ]
        out[:, 8 * MODEL + FF + at * part : 8 * MODEL + FF + (at + 1) * part] = kept[
            at, :, first + part : first + 2 * part
        ]


def own_features(rank, width):
    shape = (MODEL, width)
    feature = lax.broadcasted_iota(jnp.int32, shape, 0)
    column = lax.broadcasted_iota(jnp.int32, shape, 1)
    return (feature == rank * width + column).astype(LOW)


def own_vector(rank, pieces, out, flat):
    size = out.shape[0]
    for at, piece in enumerate(pieces):
        flat[:, at * MODEL : (at + 1) * MODEL] = piece
    value = jnp.zeros((1, size), WIDE)
    for chip in range(GROUP):
        value = jnp.where(rank == chip, flat[:, chip * size : (chip + 1) * size], value)
    out[...] = value.reshape(size)


def cls_owner_kernel(where, *refs):
    own, got, shared, mats_out, vec_out, rows, flat = refs
    rank = where[0] * PLANE + where[1]
    width = mats_out.shape[0]
    rows[:GROUP] = own[...]
    rows[GROUP:] = got[...]
    chosen = own_features(rank, width)
    plan = (
        (0, MODEL, 3 * MODEL, 0),
        (4 * MODEL, 5 * MODEL, MODEL, 3 * MODEL),
        (6 * MODEL, 7 * MODEL, FF, 4 * MODEL),
        (7 * MODEL + FF, 8 * MODEL + FF, FF, 4 * MODEL + FF),
    )
    for left, right, size, target in plan:
        side = product_plain(rows[:, left : left + MODEL], chosen).astype(LOW)
        mats_out[:, target : target + size] = product_left(side, rows[:, right : right + size])
    starts = (MODEL, 3 * MODEL, 5 * MODEL, 7 * MODEL + FF)
    pieces = [column_sum(rows[:, start : start + MODEL]) for start in starts]
    pieces += [shared[GROUP + 1 + at : GROUP + 2 + at, :] for at in range(4)]
    starts = [7 * MODEL + at * MODEL for at in range(FF // MODEL)]
    pieces += [column_sum(rows[:, start : start + MODEL]) for start in starts]
    own_vector(rank, pieces, vec_out, flat)


def head_share_kernel(where, *refs):
    packs, mlp = refs[:4], refs[4]
    mine_out, vecs_out, rows = refs[5:]
    rank = where[0] * PLANE + where[1]
    count = LINE * 24
    for at, pack in enumerate(packs):
        rows[at * count : (at + 1) * count] = pack[...]
    total = PLANE * count

    def chosen(base, apart):
        shape = (CORES * GROUP, total)
        row = lax.broadcasted_iota(jnp.int32, shape, 0)
        column = lax.broadcasted_iota(jnp.int32, shape, 1)
        hot = (column == row // 2 * 24 + base + row % 2 * apart).astype(LOW)
        return product_plain(hot, rows[...]).astype(LOW)

    own = own_features(rank, OWN)
    for at, (left, right) in enumerate(((0, 4), (2, 8))):
        side = product_plain(chosen(left, 1), own).astype(LOW)
        for piece in range(FF_HALF // MODEL):
            columns = slice(at * FF_HALF + piece * MODEL, at * FF_HALF + (piece + 1) * MODEL)
            share = product_left(side, chosen(right + 2 * piece, 1))
            mine_out[:, columns] = mlp[:, columns] + share
    shape = (16, total)
    row = lax.broadcasted_iota(jnp.int32, shape, 0)
    column = lax.broadcasted_iota(jnp.int32, shape, 1)
    hot = ((column % 24 == row + 12) & (row < 12)).astype(LOW)
    vecs_out[...] = product_plain(hot, rows[...])


def share_owner_kernel(where, *refs):
    head_share_kernel(where, *refs[:5], *refs[9:11], refs[15])
    cls_owner_kernel(where, *refs[5:8], *refs[11:13], *refs[16:])
    shared, count, pos_out, loss_out = refs[7], refs[8], refs[13], refs[14]
    pos_out[...] = shared[:GROUP, :]
    loss_out[...] = shared[GROUP : GROUP + 1, 0:1] / (count[0:1, 0:1] * MODEL)


def seg_vec_kernel(where, vecs, vecs_got, vec_out, flat):
    rank = where[0] * PLANE + where[1]
    rows = (8 * MODEL + FF) // MODEL
    pieces = [vecs[at : at + 1, :] + vecs_got[at : at + 1, :] for at in range(rows)]
    own_vector(rank, pieces, vec_out, flat)


def column_copies(where, out, base, size, own, got, first):
    core_at = where[2]
    lanes = slice(first, first + size)
    return [
        (own.at[:, lanes], out.at[:, pl.ds(aligned(base + core_at * size), size)]),
        (got.at[:, lanes], out.at[:, pl.ds(aligned(base + (1 - core_at) * size), size)]),
    ]


def store_kernel(where, attn, attn_got, mlp, mlp_got, vecs, vecs_got, out, vec_out, flat, sems):
    pairs = []
    for piece in range(4):
        pairs += column_copies(where, out, piece * MODEL, HALF, attn, attn_got, piece * HALF)
    for piece in range(2):
        base = 4 * MODEL + piece * FF
        pairs += column_copies(where, out, base, FF_HALF, mlp, mlp_got, piece * FF_HALF)
    copies = [
        pltpu.make_async_copy(source, target, sems.at[at])
        for at, (source, target) in enumerate(pairs)
    ]
    for copy in copies:
        copy.start()
    seg_vec_kernel(where, vecs, vecs_got, vec_out, flat)
    wait_all(copies)


def plane_parts(part):
    return (part,) + together(*(in_plane(part, mask) for mask in range(1, PLANE)))


def line_parts(part):
    return (part,) + together(*(along_line(part, apart) for apart in range(1, LINE)))


def slice_local(
    hidden_in,
    targets,
    doc_ids,
    seg_nums,
    valid_flags,
    seg_mats,
    seg_vecs,
    cls_mats,
    cls_vecs,
    seg_pos,
):
    rank, core_at = lax.axis_index("fsdp"), lax.axis_index("rep")
    line_at, plane_at = rank // PLANE, rank % PLANE
    where = jnp.stack([line_at, plane_at, core_at, doc_ids[0], seg_nums[0]]).astype(jnp.int32)
    own_rows, total_columns = seg_mats.shape
    vec_size = seg_vecs.shape[0]
    both_rows = CORES * SEG

    first_piece, live_row, *rest = run_kernel(
        prepare_kernel,
        "prepare",
        [shape_of((own_rows, FIRST), LOW), shape_of((1, SEG))]
        + [shape_of((own_rows, FF_HALF), LOW)] * 2
        + [shape_of((own_rows, QUARTER_HALF), LOW)] * LINE
        + [shape_of((own_rows, HALF), LOW), shape_of((MODEL, PLANE * SPAN), LOW)],
        where,
        (seg_mats, cls_mats),
        (seg_vecs, cls_vecs, valid_flags),
        [
            pltpu.SemaphoreType.DMA((4,)),
            pltpu.VMEM((LINE, own_rows, QUARTER), LOW),
            pltpu.SemaphoreType.DMA((3 + 5 * LINE,)),
        ],
    )
    first_line = line_parts(first_piece)
    second_piece, third_piece, quarters, cls_out_piece, order = (
        rest[0],
        rest[1],
        rest[2:-2],
        rest[-2],
        rest[-1],
    )

    def joined(*pieces):
        return jnp.concatenate(pieces, axis=1)

    def sent_both(to_x, to_y):
        to_x, to_y = together(to_x, to_y)
        return together(in_plane(to_x, 1), in_plane(to_y, 2))

    own_sent = joined(first_piece, second_piece, third_piece)
    own_x, own_y = sent_both(own_sent, own_sent)
    first_line = first_line[:1] + tuple(after(got, own_x, own_y) for got in first_line[1:])
    hidden_got = other_core(after(hidden_in, own_x, own_y))
    live_got = other_core(after(live_row, own_x, own_y))
    to_x = joined(after(own_y, hidden_got, live_got)[:, OWN_CUT:], *first_line[1:])
    to_y = joined(own_x[:, :OWN_CUT], *first_line[1:])
    first_x, first_y = sent_both(to_x, to_y)
    second_line = line_parts(after(second_piece, to_x, to_y))

    def halves(group, from_x, from_y):
        width, cut = WIDTHS[group], LINE_CUTS[group]
        if group == 0:
            base_x, base_y = sum(WIDTHS) - OWN_CUT, OWN_CUT
        else:
            before, before_cut = WIDTHS[group - 1], LINE_CUTS[group - 1]
            base_x, base_y = 2 * before - before_cut, before + before_cut
        return (
            from_y[:, base_y + width + cut : base_y + 3 * width],
            from_x[:, base_x : base_x + width + cut],
        )

    high, low = halves(0, first_x, first_y)
    to_x, to_y = joined(high, *second_line[1:]), joined(low, *second_line[1:])
    second_x, second_y = sent_both(to_x, to_y)
    third_line = line_parts(after(third_piece, to_x, to_y))
    high, low = halves(1, second_x, second_y)
    to_x, to_y = joined(high, *third_line[1:]), joined(low, *third_line[1:])
    third_x, third_y = sent_both(to_x, to_y)
    own_parts = (own_x, own_y, first_x, first_y)
    cls_line = (quarters[0],) + tuple(
        along_line(after(quarters[apart], to_x, to_y), apart)
        for apart in range(1, LINE)
    )

    qkv_weight, out_low, out_high, qkv, mixed, vectors, count, hidden_ordered = run_kernel(
        qkv_kernel,
        "seg_qkv",
        [
            shape_of((GROUP, own_rows, 3 * HALF), LOW),
            shape_of((GROUP // 2, own_rows, HALF), LOW),
            shape_of((GROUP // 2, own_rows, HALF), LOW),
            shape_of((both_rows, 3 * HALF), LOW),
            shape_of((both_rows, HALF), LOW),
            shape_of((2 * (8 * MODEL + FF) // MODEL, MODEL)),
            shape_of((8, LANES)),
            shape_of((both_rows, PLANE * SPAN), LOW),
        ],
        where,
        (),
        first_line
        + own_parts
        + (first_x, first_y, second_x, second_y)
        + (hidden_in, hidden_got, live_row, live_got, order),
        [
            pltpu.VMEM((GROUP, own_rows, LANES), LOW),
            pltpu.VMEM((2, 8 * MODEL + FF), WIDE),
            pltpu.VMEM((both_rows, MODEL), LOW),
            pltpu.VMEM((GROUP, own_rows, HALF), LOW),
        ],
        flops=2 * SEG * MODEL * 3 * MODEL,
    )
    out_weight, mixed_ordered, normed_first, inv_first, first_low = run_kernel(
        out_kernel,
        "seg_out",
        [
            shape_of((MODEL, MODEL), LOW),
            shape_of((both_rows, PLANE * SPAN), LOW),
            shape_of((SEG, MODEL)),
            shape_of((SEG, 1)),
            shape_of((SEG, MODEL), LOW),
        ],
        where,
        (),
        (
            hidden_in,
            mixed,
            after(other_core(mixed), third_x, third_y),
            out_low,
            out_high,
            other_core(out_low),
            other_core(out_high),
            vectors,
            order,
        ),
        [pltpu.VMEM((both_rows, MODEL), LOW)],
        flops=2 * SEG * MODEL * MODEL,
    )
    fourth_x, fourth_y = sent_both(*halves(2, third_x, third_y))
    first_got = after(other_core(first_low), fourth_x, fourth_y)
    count = count + other_core(after(count, first_got))
    up_weight, act, slope = run_kernel(
        up_kernel,
        "seg_up",
        [
            shape_of((GROUP, own_rows, FF_HALF), LOW),
            shape_of((both_rows, FF_HALF), LOW),
            shape_of((both_rows, FF_HALF)),
        ],
        where,
        (),
        second_line
        + own_parts
        + (second_x, second_y, third_x, third_y)
        + (first_low, first_got, vectors),
        [pltpu.VMEM((both_rows, MODEL), LOW)],
        flops=2 * SEG * MODEL * FF,
    )
    cls_sent = joined(*cls_line, cls_out_piece)
    cls_sent = after(cls_sent, act)
    cls_x, cls_y = sent_both(cls_sent, cls_sent)
    down_weight, down_own, down_send = run_kernel(
        down_kernel,
        "seg_down",
        [
            shape_of((GROUP, own_rows, FF_HALF), LOW),
            shape_of((SEG, MODEL)),
            shape_of((SEG, MODEL)),
        ],
        where,
        (),
        third_line + own_parts + (third_x, third_y, fourth_x, fourth_y) + (act,),
        flops=2 * SEG * MODEL * FF,
    )
    normed_second, inv_second, diff, out_rows, head_row = run_kernel(
        seg_rows_kernel,
        "seg_rows",
        [
            shape_of((SEG, MODEL)),
            shape_of((SEG, 1)),
            shape_of((SEG, MODEL)),
            shape_of((SEG, MODEL)),
            shape_of((1, 2 * MODEL + LANES)),
        ],
        where,
        (),
        (
            down_own,
            other_core(down_send),
            normed_first,
            vectors,
            targets,
            live_row,
            seg_pos,
        ),
    )
    head_planes = plane_parts(head_row)
    head_lines = line_parts(jnp.concatenate(head_planes))
    size = LINE // 2 * QUARTER_HALF
    cls_far = sent_both(
        after(cls_y[:, size:], *head_planes[1:]), after(cls_x[:, :size], *head_planes[1:])
    )

    second_grad, second_low, second_sums, first_ordered = run_kernel(
        second_norm_kernel,
        "seg_second_norm",
        [
            shape_of((SEG, MODEL)),
            shape_of((SEG, MODEL), LOW),
            shape_of((3, MODEL)),
            shape_of((both_rows, PLANE * SPAN), LOW),
        ],
        where,
        (),
        (diff, count, normed_second, inv_second, vectors, first_low, first_got, order),
        [pltpu.VMEM((both_rows, MODEL), LOW)],
    )
    second_got = other_core(second_low)
    pre, first_grad_own, first_grad_send, up_sums = run_kernel(
        mlp_back_kernel,
        "seg_mlp_back",
        [
            shape_of((both_rows, FF_HALF), LOW),
            shape_of((SEG, MODEL)),
            shape_of((SEG, MODEL)),
            shape_of((FF_HALF // MODEL, MODEL)),
        ],
        where,
        (),
        (second_low, second_got, down_weight, up_weight, slope),
        [pltpu.VMEM((both_rows, MODEL), LOW)],
        flops=4 * SEG * MODEL * FF,
    )
    first_grad_got = other_core(first_grad_send)

    def part_shapes(columns):
        return [
            shape_of((count_of, own_rows, columns), LOW)
            for count_of in (LINE // 2, LINE // 2, LINE, LINE, LINE)
        ]

    cls_far = together(*(after(got, second_got, *head_lines[1:]) for got in cls_far))
    cls_half, cls_out_half = run_kernel(
        cls_gather_kernel,
        "head_gather",
        [
            shape_of((GROUP, own_rows, QUARTER_HALF), LOW),
            shape_of((PLANE, own_rows, HALF), LOW),
        ],
        where,
        (),
        cls_line + (cls_x, cls_y) + cls_far + (cls_out_piece,),
    )
    mlp_data = (first_ordered, second_low, second_got, after(pre, cls_half), act, order)
    mlp_far = run_kernel(
        mlp_far_kernel,
        "seg_mlp_far",
        part_shapes(FF)[:2],
        where,
        (),
        mlp_data,
        [pltpu.VMEM((both_rows, MODEL), LOW)],
        flops=SEG * MODEL * FF,
    )
    mlp_parts = list(mlp_far) + list(
        run_kernel(
            mlp_near_kernel,
            "seg_mlp_near",
            part_shapes(FF)[2:],
            where,
            (),
            mlp_data,
            [pltpu.VMEM((both_rows, MODEL), LOW)],
            flops=3 * SEG * MODEL * FF,
        )
    )
    mlp_far = reduce_far(tuple(after(part, *cls_far) for part in mlp_parts[:2]))
    cls_weight, cls_out = run_kernel(
        cls_weight_kernel,
        "head_weight",
        [
            shape_of((GROUP, own_rows, QUARTER), LOW),
            shape_of((4, HEAD_DIM, MODEL), LOW),
        ],
        where,
        (),
        (cls_half, other_core(cls_half), cls_out_half, other_core(cls_out_half)),
    )
    cls_weight = cls_weight.reshape(MODEL, QUARTER)
    cls_out = cls_out.reshape(SPAN, MODEL)
    heads, cls_qkv, cls_mixed, part = run_kernel(
        cls_attend_kernel,
        "head_attend",
        [
            shape_of((GROUP, 2 * MODEL + LANES)),
            shape_of((GROUP, 3 * SPAN), LOW),
            shape_of((GROUP, SPAN), LOW),
            shape_of((GROUP, MODEL)),
        ],
        where,
        (),
        tuple(after(got, mlp_parts[0], first_grad_got) for got in head_lines)
        + (vectors, cls_weight, cls_out),
    )
    cls_normed, cls_inv, cls_low, cls_act, cls_slope, part, *mlp_sent = run_kernel(
        head_mlp_kernel,
        "head_mlp",
        [
            shape_of((GROUP, MODEL)),
            shape_of((GROUP, 1)),
            shape_of((GROUP, MODEL), LOW),
            shape_of((GROUP, FF // LINE), LOW),
            shape_of((GROUP, FF // LINE)),
            shape_of((GROUP, MODEL)),
            shape_of(mlp_parts[2].shape, LOW),
            shape_of(mlp_parts[2].shape, LOW),
        ],
        where,
        (),
        (heads,) + line_parts(part) + (vectors, cls_weight) + mlp_far + tuple(mlp_parts[2:4]),
    )
    mlp_plane = sent_both(*mlp_sent)
    cls_parts = line_parts(part)
    top_row, square, cls_grad, cls_second, cls_pre, part, top_sums = run_kernel(
        cls_top_kernel,
        "head_top",
        [
            shape_of((1, MODEL)),
            shape_of((8, LANES)),
            shape_of((GROUP, MODEL)),
            shape_of((GROUP, MODEL), LOW),
            shape_of((GROUP, FF // LINE), LOW),
            shape_of((GROUP, MODEL)),
            shape_of((2, MODEL)),
        ],
        where,
        (),
        (heads,)
        + cls_parts
        + (vectors, cls_weight, cls_normed, count, cls_slope),
        [pltpu.VMEM((GROUP, MODEL), WIDE)],
    )
    top_parts = line_parts(part)
    cls_grad, cls_branch, cls_proj, part, back_sums = run_kernel(
        cls_attend_back_kernel,
        "head_attend_back",
        [
            shape_of((GROUP, MODEL)),
            shape_of((GROUP, MODEL), LOW),
            shape_of((GROUP, 3 * SPAN), LOW),
            shape_of((GROUP, MODEL)),
            shape_of((2, MODEL)),
        ],
        where,
        (),
        (heads,)
        + top_parts
        + (vectors, cls_weight, cls_out, cls_grad, cls_normed, cls_inv, cls_qkv),
    )
    end_parts = line_parts(part)
    pack = jnp.concatenate([cls_proj, cls_mixed, cls_pre, cls_act], axis=1)
    folded = [shape_of((own_rows, FF))] + [shape_of((own_rows + GROUP, FF), LOW)] * (LINE - 1)
    dheads, head_grad, shared, mlp_own, *mlp_sent = run_kernel(
        head_end_kernel,
        "head_end",
        [shape_of((1, MODEL)), shape_of((1, MODEL)), shape_of((GROUP + 8, MODEL))] + folded,
        where,
        (),
        (heads, cls_grad)
        + end_parts
        + (square, back_sums, top_sums, normed_second, inv_second, vectors)
        + (mlp_parts[4],)
        + mlp_plane
        + (pack,),
        [pltpu.VMEM((GROUP, MODEL), WIDE)],
    )
    got_three, got_two = along_line(mlp_sent[2], 3), along_line(mlp_sent[1], 2)
    mlp_last = mlp_sent[0]
    mlp_got = [None, got_two, got_three]

    head_own, head_send, head_data = run_kernel(
        head_back_kernel,
        "seg_head_back",
        [shape_of((1, MODEL)), shape_of((1, MODEL)), shape_of((12, MODEL))],
        where,
        (),
        (
            head_grad,
            other_core(head_grad),
            down_weight,
            up_weight,
            slope,
            act,
            first_low,
            first_got,
        ),
    )
    grad_summed, branch, mixed_grad, attn_send, first_sums = run_kernel(
        first_norm_kernel,
        "seg_first_norm",
        [
            shape_of((SEG, MODEL)),
            shape_of((SEG, MODEL), LOW),
            shape_of((SEG, MODEL), LOW),
            shape_of((SEG, MODEL), LOW),
            shape_of((3, MODEL)),
        ],
        where,
        (),
        (
            second_grad,
            first_grad_own,
            first_grad_got,
            head_grad,
            head_own,
            other_core(head_send),
            normed_first,
            inv_first,
            vectors,
            out_weight,
        ),
    )
    attn_got = other_core(attn_send)
    proj = run_kernel(
        attn_back_kernel,
        "seg_attn_back",
        [shape_of((both_rows, 3 * HALF), LOW)],
        where,
        (),
        (qkv, mixed_grad, attn_got, live_row, live_got),
        flops=2 * SEG * MODEL * 3 * MODEL,
    )[0]
    attn_data = (hidden_ordered, mixed_ordered, proj, branch, attn_got)
    attn_far = run_kernel(
        attn_far_kernel,
        "seg_attn_far",
        part_shapes(4 * HALF)[:2],
        where,
        (),
        attn_data,
        flops=SEG * MODEL * 2 * MODEL,
    )
    attn_far = reduce_far(tuple(after(part, mlp_got[-1]) for part in attn_far))
    *attn_near, output, input_own, input_send, payload = run_kernel(
        attn_near_kernel,
        "seg_attn_near",
        part_shapes(4 * HALF)[2:]
        + [
            shape_of((SEG, MODEL), LOW),
            shape_of((SEG, MODEL)),
            shape_of((SEG, MODEL)),
            shape_of((24, MODEL), LOW),
        ],
        where,
        (),
        attn_data
        + (top_row, out_rows, live_row, qkv_weight, first_sums, second_sums, up_sums)
        + (dheads, normed_second, head_data),
        [pltpu.VMEM((24, MODEL), WIDE)],
        flops=3 * SEG * MODEL * 2 * MODEL,
    )
    attn_sent = run_kernel(
        add_far_kernel,
        "seg_attn_add",
        [shape_of(attn_near[0].shape, LOW)] * 2,
        where,
        (),
        attn_far + (after(attn_near[0], got_two), attn_near[1]),
    )
    attn_plane = sent_both(*attn_sent)
    mlp_got[0] = along_line(after(mlp_last, *attn_sent), 1)
    input_got = other_core(after(input_send, *attn_sent))
    shared = shared + other_core(after(shared, attn_sent[0]))
    payload_parts = line_parts(after(payload, mlp_got[0], input_got, shared))
    mlp_got = [after(got, attn_plane[0]) for got in mlp_got]
    mlp_sum = reduce_line(mlp_own, mlp_got)
    row_width = 8 * MODEL + 2 * FF
    cls_rows, input_grad = run_kernel(
        rows_input_kernel,
        "head_rows",
        [shape_of((GROUP, row_width), LOW), shape_of((SEG, MODEL), LOW)],
        where,
        (),
        (pack,)
        + tuple(mlp_got)
        + (heads, cls_branch, cls_low, cls_second)
        + (grad_summed, input_own, input_got),
        [pltpu.VMEM((LINE,) + pack.shape, LOW)],
    )
    cls_got = other_core(cls_rows)
    attn_plane = tuple(after(got, output, shared) for got in attn_plane)
    attn_own, *attn_sent = reduce_fold(where, attn_near[2], attn_plane)
    attn_lines = list(
        together(*(along_line(attn_sent[apart - 1], apart) for apart in range(1, LINE)))
    )
    flat = pltpu.VMEM((1, 8 * MODEL + FF), WIDE)
    payload_line = jnp.concatenate(payload_parts)
    mlp_mine, own_vecs, cls_mats_grad, cls_vec_grad, pos_total, loss_value = run_kernel(
        share_owner_kernel,
        "head_owner",
        [
            shape_of((own_rows, FF)),
            shape_of((16, MODEL)),
            shape_of((own_rows, total_columns)),
            shape_of((vec_size,)),
            shape_of((GROUP, MODEL)),
            shape_of((1, 1)),
        ],
        where,
        (),
        tuple(after(got, attn_own) for got in plane_parts(after(payload_line, *attn_plane)))
        + (mlp_sum, cls_rows, cls_got, shared, count),
        [
            pltpu.VMEM((GROUP * 24, MODEL), LOW),
            pltpu.VMEM((CORES * GROUP, row_width), LOW),
            flat,
        ],
        flops=64 * own_rows * total_columns,
    )
    loss_value = loss_value.reshape(())
    attn_lines = together(*(after(got, mlp_mine) for got in attn_lines))
    attn_sum = reduce_line(attn_own, attn_lines)
    seg_mats_grad, seg_vec_grad = run_kernel(
        store_kernel,
        "seg_owner",
        [shape_of((own_rows, total_columns)), shape_of((vec_size,))],
        where,
        (),
        (attn_sum, other_core(attn_sum), mlp_mine, other_core(mlp_mine))
        + (own_vecs, other_core(own_vecs)),
        [flat, pltpu.SemaphoreType.DMA((12,))],
        far=(0,),
    )

    return (
        output,
        input_grad,
        seg_mats_grad,
        seg_vec_grad,
        cls_mats_grad,
        cls_vec_grad,
        pos_total,
        loss_value,
    )


def solution(mesh):
    in_specs = (
        P(("rep", "fsdp"), None),
        P(("rep", "fsdp"), None),
        P(("rep", "fsdp")),
        P(("rep", "fsdp")),
        P(("rep", "fsdp")),
        P("fsdp", None),
        P("fsdp"),
        P("fsdp", None),
        P("fsdp"),
        P(),
    )
    out_specs = (
        P(("rep", "fsdp"), None),
        P(("rep", "fsdp"), None),
        P("fsdp", None),
        P("fsdp"),
        P("fsdp", None),
        P("fsdp"),
        P(),
        P(),
    )
    one_slice = dict(mesh.shape) == {"rep": CORES, "fsdp": LINE * PLANE}
    body = slice_local if one_slice else local
    return jax.shard_map(body, mesh=mesh, in_specs=in_specs, out_specs=out_specs, check_vma=False)
```

```python
import math

import jax
import jax.numpy as jnp
from jax import lax
from jax.experimental import pallas as pl
from jax.experimental.pallas import tpu as pltpu
from jax.sharding import PartitionSpec as P

HEADS = 12
HEAD_DIM = 64
FF = 3072
SEG = 128
SEQ = 2048


NORM_EPS = 1e-05
MASK_FILL = -1e30
SQRT_HALF = 0.7071067811865476
INV_SQRT_TWO_PI = 0.3989422804014327


def swapped(value, axis, apart):
    mask = 2**apart
    pairs = [(source, source ^ mask) for source in range(lax.axis_size(axis))]
    return lax.ppermute(value, axis, pairs)


def product_plain(left_side, right_side):
    return jnp.dot(left_side, right_side, preferred_element_type=jnp.float32)


def product_left(left_side, right_side):
    return lax.dot_general(
        left_side, right_side, (((0,), (0,)), ((), ())), preferred_element_type=jnp.float32
    )


def product_right(left_side, right_side):
    return lax.dot_general(
        left_side, right_side, (((1,), (1,)), ((), ())), preferred_element_type=jnp.float32
    )


def row_total(array_in):
    return jnp.sum(array_in.astype(jnp.float32), axis=0)


def unpack_weights(gathered, model_width, ff_width):
    matrix, vector = gathered
    vector = vector.astype(jnp.float32)
    pieces = tuple(
        (vector[offset * model_width : (offset + 1) * model_width] for offset in range(8))
    )
    return (
        (
            matrix[:, : 3 * model_width],
            matrix[:, 3 * model_width : 4 * model_width],
            matrix[:, 4 * model_width : 4 * model_width + ff_width],
            matrix[:, 4 * model_width + ff_width :],
        )
        + pieces
        + (vector[8 * model_width :],)
    )


def norm_forward(summed, gain_vec, shift_vec):
    row_mean = jnp.mean(summed, axis=-1, keepdims=True)
    centered = summed - row_mean
    inv_dev = lax.rsqrt(jnp.mean(centered * centered, axis=-1, keepdims=True) + NORM_EPS)
    normed = centered * inv_dev
    return (normed * gain_vec + shift_vec, normed, inv_dev)


def norm_backward(grad_out, normed, inv_dev, gain_vec):
    scaled = grad_out * gain_vec
    mean_one = jnp.mean(scaled, axis=-1, keepdims=True)
    mean_two = jnp.mean(scaled * normed, axis=-1, keepdims=True)
    grad_in = inv_dev * (scaled - mean_one - normed * mean_two)
    return (grad_in, jnp.sum(grad_out * normed, axis=0), jnp.sum(grad_out, axis=0))


def gelu_value(before):
    return 0.5 * before * (1.0 + lax.erf(before * SQRT_HALF))


def gelu_slope(before):
    return (
        0.5 * (1.0 + lax.erf(before * SQRT_HALF))
        + before * jnp.exp(-0.5 * before * before) * INV_SQRT_TWO_PI
    )


def attention_scores(queries, keys_in, allowed, score_scale):
    raw_scores = (
        jnp.einsum("bqhe,bkhe->bhqk", queries, keys_in, preferred_element_type=jnp.float32)
        * score_scale
    )
    return jnp.where(allowed, raw_scores, MASK_FILL)


def attention_forward(queries, keys_in, values, allowed, score_scale):
    scores = attention_scores(queries, keys_in, allowed, score_scale)
    row_top = jnp.max(scores, axis=-1, keepdims=True)
    log_total = row_top + jnp.log(jnp.sum(jnp.exp(scores - row_top), axis=-1, keepdims=True))
    weights = jnp.exp(scores - log_total).astype(jnp.bfloat16)
    mixed_rows = jnp.einsum("bhqk,bkhe->bqhe", weights, values, preferred_element_type=jnp.float32)
    return (mixed_rows, log_total)


def attention_backward(queries, keys_in, values, allowed, score_scale, log_total, grad_mixed):
    probabilities = jnp.exp(attention_scores(queries, keys_in, allowed, score_scale) - log_total)
    grad_probs = jnp.einsum(
        "bqhe,bkhe->bhqk", grad_mixed, values, preferred_element_type=jnp.float32
    )
    inner_sum = jnp.sum(grad_probs * probabilities, axis=-1, keepdims=True)
    grad_scores = (probabilities * (grad_probs - inner_sum)).astype(jnp.bfloat16)
    grad_query = (
        jnp.einsum("bhqk,bkhe->bqhe", grad_scores, keys_in, preferred_element_type=jnp.float32)
        * score_scale
    )
    grad_key = (
        jnp.einsum("bhqk,bqhe->bkhe", grad_scores, queries, preferred_element_type=jnp.float32)
        * score_scale
    )
    grad_value = jnp.einsum(
        "bhqk,bqhe->bkhe",
        probabilities.astype(jnp.bfloat16),
        grad_mixed,
        preferred_element_type=jnp.float32,
    )
    return (grad_query, grad_key, grad_value)


def block_forward(rows_in, unpacked, attend):
    (
        qkv_weight,
        out_weight,
        up_weight,
        down_weight,
        query_bias,
        value_bias,
        out_bias,
        down_bias,
        gain_first,
        shift_first,
        gain_second,
        shift_second,
        up_bias,
    ) = unpacked
    model_width = rows_in.shape[1]
    inputs = rows_in.astype(jnp.bfloat16)
    projected = product_plain(inputs, qkv_weight)
    queries = (projected[:, :model_width] + query_bias).astype(jnp.bfloat16)
    keys_in = projected[:, model_width : 2 * model_width].astype(jnp.bfloat16)
    values = (projected[:, 2 * model_width :] + value_bias).astype(jnp.bfloat16)
    mixed_rows, attend_kept = attend(queries, keys_in, values)
    mixed_rows = mixed_rows.astype(jnp.bfloat16)
    summed_first = rows_in + product_plain(mixed_rows, out_weight) + out_bias
    first_out, normed_first, inv_first = norm_forward(summed_first, gain_first, shift_first)
    first_low = first_out.astype(jnp.bfloat16)
    pre_act = product_plain(first_low, up_weight) + up_bias
    activated = gelu_value(pre_act).astype(jnp.bfloat16)
    summed_second = first_out + product_right(activated, down_weight) + down_bias
    block_out, normed_second, inv_second = norm_forward(summed_second, gain_second, shift_second)
    saved_state = (
        inputs,
        queries,
        keys_in,
        values,
        attend_kept,
        mixed_rows,
        normed_first,
        inv_first,
        first_low,
        pre_act,
        activated,
        normed_second,
        inv_second,
    )
    return (block_out, saved_state)


def block_backward(grad_out, unpacked, saved_state, attend_back):
    (
        qkv_weight,
        out_weight,
        up_weight,
        down_weight,
        query_bias,
        value_bias,
        out_bias,
        down_bias,
        gain_first,
        shift_first,
        gain_second,
        shift_second,
        up_bias,
    ) = unpacked
    (
        inputs,
        queries,
        keys_in,
        values,
        attend_kept,
        mixed_rows,
        normed_first,
        inv_first,
        first_low,
        pre_act,
        activated,
        normed_second,
        inv_second,
    ) = saved_state
    grad_second, grad_gain_second, grad_shift_second = norm_backward(
        grad_out, normed_second, inv_second, gain_second
    )
    second_low = grad_second.astype(jnp.bfloat16)
    grad_pre = (product_plain(second_low, down_weight) * gelu_slope(pre_act)).astype(jnp.bfloat16)
    grad_first = grad_second + product_right(grad_pre, up_weight)
    grad_summed, grad_gain_first, grad_shift_first = norm_backward(
        grad_first, normed_first, inv_first, gain_first
    )
    branch_low = grad_summed.astype(jnp.bfloat16)
    grad_mixed = product_right(branch_low, out_weight).astype(jnp.bfloat16)
    grad_query, grad_key, grad_value = attend_back(
        queries, keys_in, values, attend_kept, grad_mixed
    )
    grad_proj = jnp.concatenate([grad_query, grad_key, grad_value], axis=1)
    grad_rows = grad_summed + product_right(grad_proj, qkv_weight)
    vector_grad = jnp.concatenate(
        [
            row_total(grad_query),
            row_total(grad_value),
            row_total(branch_low),
            row_total(second_low),
            grad_gain_first,
            grad_shift_first,
            grad_gain_second,
            grad_shift_second,
            row_total(grad_pre),
        ]
    )
    weight_rows = (
        inputs,
        grad_proj,
        mixed_rows,
        branch_low,
        first_low,
        grad_pre,
        second_low,
        activated,
    )
    return (grad_rows, weight_rows, vector_grad)


def weight_products(weight_rows):
    inputs, grad_proj, mixed_rows, branch_low, first_low, grad_pre, second_low, activated = (
        weight_rows
    )
    return (
        product_left(inputs, grad_proj),
        product_left(mixed_rows, branch_low),
        product_left(first_low, grad_pre),
        product_left(second_low, activated),
    )


def local(
    hidden_in,
    targets,
    doc_ids,
    seg_nums,
    valid_flags,
    seg_mats,
    seg_vecs,
    cls_mats,
    cls_vecs,
    seg_pos,
):
    tok_rows, model_width = hidden_in.shape
    ff_width = FF
    seg_len = SEG
    group_span = SEQ // tok_rows
    seg_count = tok_rows // seg_len
    score_scale = HEAD_DIM ** (-0.5)
    head_shape = (HEADS, HEAD_DIM)
    live_rows = valid_flags.astype(jnp.float32)
    rank_full = lax.axis_index("fsdp")
    seg_gathered = (
        lax.all_gather(seg_mats, "fsdp", axis=0, tiled=True),
        lax.all_gather(seg_vecs, "fsdp", axis=0, tiled=True),
    )
    seg_unpacked = unpack_weights(seg_gathered, model_width, ff_width)
    cls_gathered = (
        lax.all_gather(cls_mats, "fsdp", axis=0, tiled=True),
        lax.all_gather(cls_vecs, "fsdp", axis=0, tiled=True),
    )
    cls_unpacked = unpack_weights(cls_gathered, model_width, ff_width)
    seg_allowed = (live_rows.reshape(seg_count, 1, 1, seg_len) > 0.5) | jnp.eye(seg_len, dtype=bool)
    seg_shape = (seg_count, seg_len) + head_shape

    def seg_attend(queries, keys_in, values):
        mixed_rows, log_total = attention_forward(
            queries.reshape(seg_shape),
            keys_in.reshape(seg_shape),
            values.reshape(seg_shape),
            seg_allowed,
            score_scale,
        )
        return (mixed_rows.reshape(tok_rows, model_width), log_total)

    def seg_attend_back(queries, keys_in, values, log_total, grad_mixed):
        grad_parts = attention_backward(
            queries.reshape(seg_shape),
            keys_in.reshape(seg_shape),
            values.reshape(seg_shape),
            seg_allowed,
            score_scale,
            log_total,
            grad_mixed.reshape(seg_shape),
        )
        return tuple(
            (
                grad_part.reshape(tok_rows, model_width).astype(jnp.bfloat16)
                for grad_part in grad_parts
            )
        )

    first_out, seg_saved = block_forward(hidden_in.astype(jnp.float32), seg_unpacked, seg_attend)
    first_grid = first_out.reshape(seg_count, seg_len, model_width)
    position_hot = (seg_nums[:, None] == jnp.arange(seg_pos.shape[0])[None, :]).astype(jnp.float32)
    position_rows = jnp.sum(
        position_hot[:, :, None] * seg_pos.astype(jnp.float32)[None, :, :], axis=1
    )
    heads_in = first_grid[:, 0, :] + position_rows
    lead_live = live_rows.reshape(seg_count, seg_len)[:, 0]
    lead_doc = doc_ids.reshape(seg_count, seg_len)[:, 0]
    lead_labels = jnp.where(lead_live > 0.5, lead_doc, -1).astype(jnp.bfloat16)
    lead_doc_low = lead_doc.astype(jnp.bfloat16)
    bit_count = group_span.bit_length() - 1
    key_total = group_span * seg_count
    own_slot = rank_full % group_span * seg_count + jnp.arange(seg_count)
    query_shape = (1, seg_count) + head_shape
    key_shape = (1, key_total) + head_shape

    def cls_attend(queries, keys_in, values):
        paired = jnp.concatenate([keys_in, values], axis=1)
        labels = lead_labels
        for bit_level in range(bit_count):
            other_pair, other_labels = swapped((paired, labels), "fsdp", bit_level)
            upper_half = rank_full // (1 << bit_level) % 2 == 1
            paired = jnp.where(
                upper_half,
                jnp.concatenate([other_pair, paired]),
                jnp.concatenate([paired, other_pair]),
            )
            labels = jnp.where(
                upper_half,
                jnp.concatenate([other_labels, labels]),
                jnp.concatenate([labels, other_labels]),
            )
        allowed = (labels[None, :] == lead_doc_low[:, None]) | (
            jnp.arange(key_total)[None, :] == own_slot[:, None]
        )
        allowed = allowed[None, None]
        mixed_rows, log_total = attention_forward(
            queries.reshape(query_shape),
            paired[:, :model_width].reshape(key_shape),
            paired[:, model_width:].reshape(key_shape),
            allowed,
            score_scale,
        )
        return (mixed_rows.reshape(seg_count, model_width), (paired, allowed, log_total))

    def cls_attend_back(queries, keys_in, values, attend_kept, grad_mixed):
        paired, allowed, log_total = attend_kept
        grad_query, grad_key, grad_value = attention_backward(
            queries.reshape(query_shape),
            paired[:, :model_width].reshape(key_shape),
            paired[:, model_width:].reshape(key_shape),
            allowed,
            score_scale,
            log_total,
            grad_mixed.reshape(query_shape),
        )
        grad_pair = jnp.concatenate(
            [grad_key.reshape(key_total, model_width), grad_value.reshape(key_total, model_width)],
            axis=1,
        )
        for bit_level in reversed(range(bit_count)):
            half_rows = grad_pair.shape[0] // 2
            upper_half = rank_full // (1 << bit_level) % 2 == 1
            kept_half = jnp.where(upper_half, grad_pair[half_rows:], grad_pair[:half_rows])
            sent_half = jnp.where(upper_half, grad_pair[:half_rows], grad_pair[half_rows:])
            grad_pair = kept_half + swapped(
                sent_half.astype(jnp.bfloat16), "fsdp", bit_level
            ).astype(sent_half.dtype)
        grad_pair = grad_pair.astype(jnp.bfloat16)
        return (
            grad_query.reshape(seg_count, model_width).astype(jnp.bfloat16),
            grad_pair[:, :model_width],
            grad_pair[:, model_width:],
        )

    top_out, cls_saved = block_forward(heads_in, cls_unpacked, cls_attend)
    combined = jnp.concatenate([top_out[:, None, :], first_grid[:, 1:, :]], axis=1).reshape(
        tok_rows, model_width
    )
    output_rows = combined * live_rows[:, None]
    diff_rows = (output_rows - targets.astype(jnp.float32)) * live_rows[:, None]
    count_all, square_all = lax.psum(
        (jnp.sum(live_rows), jnp.sum(diff_rows * diff_rows)), ("rep", "fsdp")
    )
    loss_value = square_all / (count_all * model_width)
    slots_all = tok_rows * lax.axis_size("rep") * lax.axis_size("fsdp")
    grad_grid = (diff_rows * (slots_all / count_all)).reshape(seg_count, seg_len, model_width)
    cls_back = unpack_weights(
        (
            lax.all_gather(cls_mats, "fsdp", axis=0, tiled=True),
            lax.all_gather(cls_vecs, "fsdp", axis=0, tiled=True),
        ),
        model_width,
        ff_width,
    )
    heads_grad, cls_weight_rows, cls_g_vec = block_backward(
        grad_grid[:, 0, :], cls_back, cls_saved, cls_attend_back
    )
    cls_g_qkv, cls_g_out, cls_g_up, cls_g_down = weight_products(cls_weight_rows)
    pos_local = jnp.sum(position_hot[:, :, None] * heads_grad[:, None, :], axis=0)
    seg_grad_out = jnp.concatenate([heads_grad[:, None, :], grad_grid[:, 1:, :]], axis=1).reshape(
        tok_rows, model_width
    )
    seg_back = unpack_weights(
        (
            lax.all_gather(seg_mats, "fsdp", axis=0, tiled=True),
            lax.all_gather(seg_vecs, "fsdp", axis=0, tiled=True),
        ),
        model_width,
        ff_width,
    )
    input_grad, seg_weight_rows, seg_g_vec = block_backward(
        seg_grad_out, seg_back, seg_saved, seg_attend_back
    )
    seg_g_qkv, seg_g_out, seg_g_up, seg_g_down = weight_products(seg_weight_rows)
    owner_rows = tuple(
        (
            lax.psum_scatter(seg_g_qkv, "fsdp", scatter_dimension=0, tiled=True),
            lax.psum_scatter(seg_g_out, "fsdp", scatter_dimension=0, tiled=True),
            lax.psum_scatter(seg_g_up, "fsdp", scatter_dimension=0, tiled=True),
            lax.psum_scatter(seg_g_down, "fsdp", scatter_dimension=0, tiled=True),
            lax.psum_scatter(seg_g_vec, "fsdp", scatter_dimension=0, tiled=True),
            lax.psum_scatter(cls_g_qkv, "fsdp", scatter_dimension=0, tiled=True),
            lax.psum_scatter(cls_g_out, "fsdp", scatter_dimension=0, tiled=True),
            lax.psum_scatter(cls_g_up, "fsdp", scatter_dimension=0, tiled=True),
            lax.psum_scatter(cls_g_down, "fsdp", scatter_dimension=0, tiled=True),
            lax.psum_scatter(cls_g_vec, "fsdp", scatter_dimension=0, tiled=True),
        )
    )
    replica_share = (
        lax.psum_scatter(
            owner_rows[0].astype(jnp.bfloat16), "rep", scatter_dimension=1, tiled=True
        ).astype(jnp.float32),
        lax.psum_scatter(
            owner_rows[1].astype(jnp.bfloat16), "rep", scatter_dimension=1, tiled=True
        ).astype(jnp.float32),
        lax.psum_scatter(
            owner_rows[2].astype(jnp.bfloat16), "rep", scatter_dimension=1, tiled=True
        ).astype(jnp.float32),
        lax.psum_scatter(
            owner_rows[3].astype(jnp.bfloat16), "rep", scatter_dimension=1, tiled=True
        ).astype(jnp.float32),
        lax.psum_scatter(
            owner_rows[4].astype(jnp.bfloat16), "rep", scatter_dimension=0, tiled=True
        ).astype(jnp.float32),
        lax.psum_scatter(
            owner_rows[5].astype(jnp.bfloat16), "rep", scatter_dimension=1, tiled=True
        ).astype(jnp.float32),
        lax.psum_scatter(
            owner_rows[6].astype(jnp.bfloat16), "rep", scatter_dimension=1, tiled=True
        ).astype(jnp.float32),
        lax.psum_scatter(
            owner_rows[7].astype(jnp.bfloat16), "rep", scatter_dimension=1, tiled=True
        ).astype(jnp.float32),
        lax.psum_scatter(
            owner_rows[8].astype(jnp.bfloat16), "rep", scatter_dimension=1, tiled=True
        ).astype(jnp.float32),
        lax.psum_scatter(
            owner_rows[9].astype(jnp.bfloat16), "rep", scatter_dimension=0, tiled=True
        ).astype(jnp.float32),
    )
    all_summed = (
        lax.all_gather(replica_share[0].astype(jnp.bfloat16), "rep", axis=1, tiled=True).astype(
            jnp.float32
        ),
        lax.all_gather(replica_share[1].astype(jnp.bfloat16), "rep", axis=1, tiled=True).astype(
            jnp.float32
        ),
        lax.all_gather(replica_share[2].astype(jnp.bfloat16), "rep", axis=1, tiled=True).astype(
            jnp.float32
        ),
        lax.all_gather(replica_share[3].astype(jnp.bfloat16), "rep", axis=1, tiled=True).astype(
            jnp.float32
        ),
        lax.all_gather(replica_share[4].astype(jnp.bfloat16), "rep", axis=0, tiled=True).astype(
            jnp.float32
        ),
        lax.all_gather(replica_share[5].astype(jnp.bfloat16), "rep", axis=1, tiled=True).astype(
            jnp.float32
        ),
        lax.all_gather(replica_share[6].astype(jnp.bfloat16), "rep", axis=1, tiled=True).astype(
            jnp.float32
        ),
        lax.all_gather(replica_share[7].astype(jnp.bfloat16), "rep", axis=1, tiled=True).astype(
            jnp.float32
        ),
        lax.all_gather(replica_share[8].astype(jnp.bfloat16), "rep", axis=1, tiled=True).astype(
            jnp.float32
        ),
        lax.all_gather(replica_share[9].astype(jnp.bfloat16), "rep", axis=0, tiled=True).astype(
            jnp.float32
        ),
    )
    seg_summed = all_summed[:5]
    cls_summed = all_summed[5:]
    pos_total = lax.psum(pos_local, ("rep", "fsdp"))
    seg_mat_grad = jnp.concatenate(
        [seg_summed[0], seg_summed[1], seg_summed[2], seg_summed[3]], axis=1
    )
    cls_mat_grad = jnp.concatenate(
        [cls_summed[0], cls_summed[1], cls_summed[2], cls_summed[3]], axis=1
    )
    return (
        output_rows.astype(jnp.bfloat16),
        input_grad.astype(jnp.bfloat16),
        seg_mat_grad,
        seg_summed[4],
        cls_mat_grad,
        cls_summed[4],
        pos_total,
        loss_value,
    )


LINE = 4
PLANE = 4
CORES = 2
LANES = 128
GROUP = LINE * PLANE
LOW, WIDE = jnp.bfloat16, jnp.float32
MODEL = HEADS * HEAD_DIM
SPAN = 2 * LANES
TILE_START = (0, 1, 3, 4)


def line_pairs(apart):
    return [(source, (source + apart * PLANE) % GROUP) for source in range(GROUP)]


def plane_pairs(mask):
    return [(source, source ^ mask) for source in range(GROUP)]


def along_line(value, apart):
    return lax.ppermute(value, "fsdp", line_pairs(apart))


def in_plane(value, mask):
    return lax.ppermute(value, "fsdp", plane_pairs(mask))


def other_core(value):
    return lax.ppermute(value, "rep", [(0, 1), (1, 0)])


def after(value, *events):
    return lax.optimization_barrier((value,) + events)[0]


def together(*values):
    return tuple(lax.optimization_barrier(values))


def shape_of(dims, dtype=WIDE):
    return jax.ShapeDtypeStruct(dims, dtype)


def run_kernel(body, name, outs, where, blocks, arrays, scratch=(), far=(), flops=0):
    in_specs = [pl.BlockSpec(memory_space=pltpu.SMEM)]
    in_specs += [pl.BlockSpec(memory_space=pltpu.HBM)] * len(blocks)
    in_specs += [pl.BlockSpec(memory_space=pltpu.VMEM)] * len(arrays)
    spaces = [pltpu.HBM if at in far else pltpu.VMEM for at in range(len(outs))]
    moved = sum(x.size * x.dtype.itemsize for x in list(blocks) + list(arrays))
    moved += sum(math.prod(o.shape) * jnp.dtype(o.dtype).itemsize for o in outs)
    return pl.pallas_call(
        body,
        name=name,
        out_shape=tuple(outs),
        in_specs=in_specs,
        out_specs=tuple(pl.BlockSpec(memory_space=space) for space in spaces),
        scratch_shapes=list(scratch),
        cost_estimate=pl.CostEstimate(flops=flops, bytes_accessed=moved, transcendentals=0),
        compiler_params=pltpu.CompilerParams(vmem_limit_bytes=VMEM_BYTES),
    )(where, *blocks, *arrays)


VMEM_BYTES = 24 * 1024 * 1024
HALF = MODEL // CORES
FF_HALF = FF // CORES
OWN = MODEL // GROUP
QUARTER = 3 * SPAN + 2 * FF // LINE
QUARTER_HALF = QUARTER // CORES


def aligned(start):
    return pl.multiple_of(start, LANES)


def wait_all(copies):
    for copy in copies:
        copy.wait()


def run_copies(pairs, sems):
    copies = [
        pltpu.make_async_copy(source, target, sems.at[at])
        for at, (source, target) in enumerate(pairs)
    ]
    for copy in copies:
        copy.start()
    wait_all(copies)


FIRST = 4 * HALF + LANES
OWN_CUT = FIRST + FF_HALF // 2
LINE_CUTS = (7 * LANES, FF_HALF // 2, FF_HALF // 2)
WIDTHS = (FIRST, FF_HALF, FF_HALF)


def group_pieces(group, refs):
    own, rest = refs[:LINE], refs[LINE:]
    own_x, own_y, far_x, far_y, line_x, line_y, late_x, late_y = rest
    width, cut = WIDTHS[group], LINE_CUTS[group]
    start = sum(WIDTHS[:group])
    if group == 0:
        bases = (sum(WIDTHS) - OWN_CUT, OWN_CUT)
    else:
        before, before_cut = WIDTHS[group - 1], LINE_CUTS[group - 1]
        bases = (2 * before - before_cut, before + before_cut)
    pieces = {(0, step): [(own[step], 0, 0, width)] for step in range(LINE)}
    for mask, whole, line, base in ((1, own_x, line_x, bases[0]), (2, own_y, line_y, bases[1])):
        pieces[mask, 0] = [(whole, start, 0, width)]
        for step in range(1, LINE):
            pieces[mask, step] = [(line, base + (step - 1) * width, 0, width)]
    middle = min(max(OWN_CUT - start, 0), width)
    far = []
    if middle > 0:
        far.append((far_y, start, 0, middle))
    if middle < width:
        far.append((far_x, start + middle - OWN_CUT, middle, width))
    pieces[3, 0] = far
    pieces[3, 1] = [(late_y, 0, 0, width)]
    pieces[3, 2] = [(late_y, width, 0, cut), (late_x, 0, cut, width)]
    pieces[3, 3] = [(late_x, width - cut, 0, width)]
    return pieces


def gather_group(where, group, refs, targets):
    line_at, plane_at = where[0], where[1]
    for (mask, step), parts in group_pieces(group, refs).items():
        chip = (line_at + LINE - step) % LINE * PLANE + (plane_at ^ mask)
        for whole, first, last in targets:
            for ref, offset, begin, end in parts:
                low, high = max(first, begin), min(last, end)
                if low < high:
                    source = slice(offset + low - begin, offset + high - begin)
                    whole[chip, :, low - first : high - first] = ref[:, source]


def gather_blocks(where, refs, base, width, targets):
    line_at, plane_at = where[0], where[1]
    half = LINE // 2
    for mask in range(PLANE):
        for step in range(LINE):
            if mask == 0:
                ref, offset = refs[step], 0
            elif mask == 3:
                ref = refs[LINE + 3] if step < half else refs[LINE + 2]
                offset = step % half * width
            else:
                ref, offset = refs[LINE + mask - 1], base + step * width
            chip = (line_at + LINE - step) % LINE * PLANE + (plane_at ^ mask)
            for whole, first, last in targets:
                whole[chip] = ref[:, offset + first : offset + last]


def whole_rows(ref):
    value = ref[...]
    return value.reshape(value.shape[0] * value.shape[1], value.shape[2])


def prepare_first_kernel(where, seg, seg_vec, cls_vec, flags, out, live_out, sems):
    core_at = where[2]
    pairs = []
    for piece in range(4):
        source = seg.at[:, pl.ds(aligned(piece * MODEL + core_at * HALF), HALF)]
        pairs.append((source, out.at[:, piece * HALF : (piece + 1) * HALF]))
    run_copies(pairs, sems)
    size = seg_vec.shape[0]
    vecs = [vec[...].astype(WIDE).reshape(1, size) for vec in (seg_vec, cls_vec)]
    lines = -(-size // LANES)
    block = jnp.zeros((OWN, LANES), WIDE)
    row_at = lax.broadcasted_iota(jnp.int32, (OWN, LANES), 0)
    for which in range(2):
        for line in range(lines):
            width = min(LANES, size - line * LANES)
            value = vecs[which][:, line * LANES : line * LANES + width]
            if width < LANES:
                value = jnp.concatenate([value, jnp.zeros((1, LANES - width), WIDE)], axis=1)
            block = jnp.where(row_at == which * lines + line, value, block)
    live = flags[...].astype(WIDE).reshape(1, SEG)
    live_out[...] = live
    count = jnp.sum(live, axis=1, keepdims=True)
    block = jnp.where(row_at == 2 * lines, count, block)
    out[:, 4 * HALF :] = block.astype(LOW)


def prepare_rest_kernel(where, seg, cls, *refs):
    second_out, third_out = refs[:2]
    step_outs, out_half, order_out = refs[2 : 2 + LINE], refs[2 + LINE], refs[3 + LINE]
    quarters, sems = refs[4 + LINE :]
    line_at, plane_at, core_at = where[0], where[1], where[2]
    start = core_at * FF_HALF
    pairs = [
        (seg.at[:, pl.ds(aligned(4 * MODEL + start), FF_HALF)], second_out),
        (seg.at[:, pl.ds(aligned(4 * MODEL + FF + start), FF_HALF)], third_out),
        (cls.at[:, pl.ds(aligned(3 * MODEL + core_at * HALF), HALF)], out_half),
    ]
    part = FF // LINE
    for at in range(LINE):
        first = TILE_START[at] * LANES
        plan = [(piece * MODEL + first, SPAN, piece * SPAN) for piece in range(3)]
        plan += [
            (4 * MODEL + piece * FF + at * part, part, 3 * SPAN + piece * part)
            for piece in range(2)
        ]
        for source, size, target in plan:
            pairs.append(
                (
                    cls.at[:, source : source + size],
                    quarters.at[at, :, target : target + size],
                )
            )
    run_copies(pairs, sems)
    lanes = pl.ds(aligned(core_at * QUARTER_HALF), QUARTER_HALF)
    for step, out in enumerate(step_outs):
        out[...] = quarters[(line_at + step) % LINE, :, lanes]
    column = lax.broadcasted_iota(jnp.int32, (1, SPAN), 1)
    feature = lax.broadcasted_iota(jnp.int32, (MODEL, SPAN), 0)
    turn = sum((column >= OWN * step).astype(jnp.int32) for step in range(1, LINE))
    held = column - OWN * turn
    turn = (line_at + turn) % LINE
    for mask in range(PLANE):
        source = (turn * PLANE + (plane_at ^ mask)) * OWN + held
        source = jnp.where(column < OWN * LINE, source, -1)
        order_out[:, mask * SPAN : (mask + 1) * SPAN] = (feature == source).astype(LOW)


def prepare_kernel(where, seg, cls, *refs):
    (seg_vec, cls_vec, flags, first_out, live_out), refs = refs[:5], refs[5:]
    rest, (first_sems, quarters, sems) = refs[:-3], refs[-3:]
    prepare_first_kernel(where, seg, seg_vec, cls_vec, flags, first_out, live_out, first_sems)
    prepare_rest_kernel(where, seg, cls, *rest, quarters, sems)


def lane_mask(rows, head):
    lane = lax.broadcasted_iota(jnp.int32, (rows, LANES), 1)
    return (lane < HEAD_DIM) if head == 0 else (lane >= HEAD_DIM)


def masked(value, mask):
    return jnp.where(mask, value, jnp.zeros_like(value))


def head_probabilities(query, key, allowed):
    scores = product_right(query, key) * HEAD_DIM ** (-0.5)
    scores = jnp.where(allowed, scores, MASK_FILL)
    raised = jnp.exp(scores - jnp.max(scores, axis=-1, keepdims=True))
    return raised / jnp.sum(raised, axis=-1, keepdims=True)


def attend_tiles(qkv, width, allowed):
    rows = qkv.shape[0]
    mixed = []
    for tile in range(width // LANES):
        at = tile * LANES
        query, key, value = (
            qkv[:, piece * width + at : piece * width + at + LANES] for piece in range(3)
        )
        total = jnp.zeros((rows, LANES), WIDE)
        for head in range(2):
            mask = lane_mask(rows, head)
            weights = head_probabilities(masked(query, mask), key, allowed).astype(LOW)
            total = total + product_plain(weights, masked(value, mask))
        mixed.append(total.astype(LOW))
    return mixed


def attend_tiles_back(qkv, grad_mixed, width, allowed):
    rows = qkv.shape[0]
    scale = HEAD_DIM ** (-0.5)
    results = ([], [], [])
    for tile in range(width // LANES):
        at = tile * LANES
        query, key, value = (
            qkv[:, piece * width + at : piece * width + at + LANES] for piece in range(3)
        )
        grad = grad_mixed[:, at : at + LANES]
        totals = [jnp.zeros((rows, LANES), WIDE) for _ in range(3)]
        for head in range(2):
            mask = lane_mask(rows, head)
            query_low, key_low, grad_low = (masked(x, mask) for x in (query, key, grad))
            chance = head_probabilities(query_low, key, allowed)
            grad_chance = product_right(grad_low, value)
            inner = jnp.sum(grad_chance * chance, axis=-1, keepdims=True)
            grad_scores = (chance * (grad_chance - inner)).astype(LOW)
            totals[0] = totals[0] + product_plain(grad_scores, key_low)
            totals[1] = totals[1] + product_left(grad_scores, query_low)
            totals[2] = totals[2] + product_left(chance.astype(LOW), grad_low)
        results[0].append((totals[0] * scale).astype(LOW))
        results[1].append((totals[1] * scale).astype(LOW))
        results[2].append(totals[2].astype(LOW))
    return results[0] + results[1] + results[2]


def token_allowed(live_row):
    shape = (SEG, SEG)
    same = lax.broadcasted_iota(jnp.int32, shape, 0) == lax.broadcasted_iota(jnp.int32, shape, 1)
    return (live_row > 0.5) | same


def qkv_kernel(where, *refs):
    blocks = refs[:12]
    hidden, hidden_got, live_row, live_got, order = refs[12:17]
    weight, out_low, out_high, qkv_out, mixed_out = refs[17:22]
    vectors_out, count_out, ordered_out = refs[22:25]
    vec_rows, flat, inputs, out_half = refs[25:]
    core_at = where[2]
    gather_group(
        where,
        0,
        blocks,
        (
            (weight, 0, 3 * HALF),
            (out_half, 3 * HALF, 4 * HALF),
            (vec_rows, 4 * HALF, 4 * HALF + LANES),
        ),
    )
    out_low[...] = out_half[: GROUP // 2]
    out_high[...] = out_half[GROUP // 2 :]
    piece = (8 * MODEL + FF) // GROUP
    lines = -(-piece // LANES)
    count = jnp.zeros((1, LANES), WIDE)
    for chip in range(GROUP):
        rows = vec_rows[chip, 0:16, :].astype(WIDE)
        for block in range(2):
            joined = jnp.concatenate(
                [rows[block * lines + r : block * lines + r + 1] for r in range(lines)], axis=1
            )
            flat[block : block + 1, chip * piece : (chip + 1) * piece] = joined[:, :piece]
        count = count + rows[2 * lines : 2 * lines + 1]
    rows_each = (8 * MODEL + FF) // MODEL
    for block in range(2):
        for row in range(rows_each):
            vectors_out[block * rows_each + row : block * rows_each + row + 1, :] = flat[
                block : block + 1, row * MODEL : (row + 1) * MODEL
            ]
    count_out[...] = jnp.broadcast_to(count, count_out.shape)
    inputs[:SEG] = hidden[...]
    inputs[SEG:] = hidden_got[...]
    projected = product_plain(inputs[...], whole_rows(weight))
    lanes = pl.ds(aligned(core_at * HALF), HALF)
    qkv_out[:, :HALF] = (projected[:, :HALF] + vectors_out[0:1, lanes]).astype(LOW)
    qkv_out[:, HALF : 2 * HALF] = projected[:, HALF : 2 * HALF].astype(LOW)
    qkv_out[:, 2 * HALF :] = (projected[:, 2 * HALF :] + vectors_out[1:2, lanes]).astype(LOW)
    for part, live in enumerate((live_row, live_got)):
        rows = slice(part * SEG, (part + 1) * SEG)
        tiles = attend_tiles(qkv_out[rows, :], HALF, token_allowed(live[...]))
        for tile, value in enumerate(tiles):
            mixed_out[rows, tile * LANES : (tile + 1) * LANES] = value
    ordered_out[...] = product_plain(inputs[...], order[...]).astype(LOW)


def norm_rows(summed):
    row_mean = jnp.mean(summed, axis=-1, keepdims=True)
    centered = summed - row_mean
    inv_dev = lax.rsqrt(jnp.mean(centered * centered, axis=-1, keepdims=True) + NORM_EPS)
    return centered * inv_dev, inv_dev


def norm_rows_back(grad_out, normed, inv_dev, gain):
    scaled = grad_out * gain
    mean_one = jnp.mean(scaled, axis=-1, keepdims=True)
    mean_two = jnp.mean(scaled * normed, axis=-1, keepdims=True)
    return inv_dev * (scaled - mean_one - normed * mean_two)


def column_sum(value):
    return jnp.sum(value.astype(WIDE), axis=0, keepdims=True)


def four_rows(vectors, first):
    return jnp.concatenate([vectors[first + at : first + at + 1, :] for at in range(4)], axis=1)


def gelu_both(before):
    half = 0.5 * (1.0 + lax.erf(before * SQRT_HALF))
    slope = half + before * jnp.exp(-0.5 * before * before) * INV_SQRT_TWO_PI
    return before * half, slope


def out_kernel(where, hidden, mixed, mixed_got, low, high, low_got, high_got, *refs):
    vectors, order, full_out, ordered_out, normed_out, inv_out, low_out, mixed_full = refs
    core_at = where[2]
    own, other = aligned(core_at * HALF), aligned((1 - core_at) * HALF)
    rows = MODEL // 2
    full_out[:rows, pl.ds(own, HALF)] = whole_rows(low)
    full_out[rows:, pl.ds(own, HALF)] = whole_rows(high)
    full_out[:rows, pl.ds(other, HALF)] = whole_rows(low_got)
    full_out[rows:, pl.ds(other, HALF)] = whole_rows(high_got)
    mixed_full[:, pl.ds(own, HALF)] = mixed[...]
    mixed_full[:SEG, pl.ds(other, HALF)] = mixed_got[SEG:, :]
    mixed_full[SEG:, pl.ds(other, HALF)] = mixed_got[:SEG, :]
    branch = product_plain(mixed_full[:SEG, :], full_out[...])
    normed, inv_dev = norm_rows(hidden[...].astype(WIDE) + branch + vectors[2:3, :])
    normed_out[...] = normed
    inv_out[...] = inv_dev
    low_out[...] = (normed * vectors[4:5, :] + vectors[5:6, :]).astype(LOW)
    ordered_out[...] = product_plain(mixed_full[...], order[...]).astype(LOW)


def up_kernel(where, *refs):
    blocks = refs[:12]
    low, low_got, vectors = refs[12:15]
    weight, act_out, slope_out, both = refs[15:]
    core_at = where[2]
    gather_group(where, 1, blocks, ((weight, 0, FF_HALF),))
    both[:SEG] = low[...]
    both[SEG:] = low_got[...]
    for at in range(FF_HALF // MODEL):
        columns = slice(at * MODEL, (at + 1) * MODEL)
        held = weight[:, :, columns]
        before = product_plain(both[...], held.reshape(MODEL, MODEL))
        bias = vectors[pl.ds(8 + core_at * (FF_HALF // MODEL) + at, 1), :]
        value, slope = gelu_both(before + bias)
        act_out[:, columns] = value.astype(LOW)
        slope_out[:, columns] = slope


def down_kernel(where, *refs):
    blocks, act = refs[:12], refs[12]
    weight, own_out, send_out = refs[13:]
    gather_group(where, 2, blocks, ((weight, 0, FF_HALF),))
    partial = product_right(act[...], whole_rows(weight))
    own_out[...] = partial[:SEG]
    send_out[...] = partial[SEG:]


def seg_rows_kernel(where, *refs):
    own, got, normed_first, vectors, targets, live, seg_pos = refs[:7]
    normed_out, inv_out, diff_out, rows_out, head_out = refs[7:]
    doc, number = where[3], where[4]
    first = normed_first[...] * vectors[4:5, :] + vectors[5:6, :]
    normed, inv_dev = norm_rows(first + own[...] + got[...] + vectors[3:4, :])
    normed_out[...] = normed
    inv_out[...] = inv_dev
    rows = normed * vectors[6:7, :] + vectors[7:8, :]
    shape = (SEG, SEG)
    same = lax.broadcasted_iota(jnp.int32, shape, 0) == lax.broadcasted_iota(jnp.int32, shape, 1)
    live_rows = jnp.sum(jnp.where(same, live[...], 0.0), axis=1, keepdims=True)
    target_rows = targets[...].astype(WIDE)
    output = rows * live_rows
    rows_out[...] = output
    diff = (output - target_rows) * live_rows
    row_at = lax.broadcasted_iota(jnp.int32, (SEG, 1), 0)
    diff = jnp.where(row_at > 0, diff, 0.0)
    diff_out[...] = diff
    table = seg_pos[...].astype(WIDE)
    chosen = lax.broadcasted_iota(jnp.int32, table.shape, 0) == number
    position = jnp.sum(jnp.where(chosen, table, 0.0), axis=0, keepdims=True)
    head_out[:, :MODEL] = rows[0:1, :] + position
    head_out[:, MODEL : 2 * MODEL] = target_rows[0:1, :]
    square = jnp.sum(column_sum(diff * diff), axis=1, keepdims=True)
    lane = lax.broadcasted_iota(jnp.int32, (1, LANES), 1)
    facts = jnp.where(lane == 0, live_rows[0:1, :], 0.0)
    facts = jnp.where(lane == 1, doc.astype(WIDE), facts)
    facts = jnp.where(lane == 2, number.astype(WIDE), facts)
    facts = jnp.where(lane == 3, square, facts)
    head_out[:, 2 * MODEL :] = facts


def second_norm_kernel(where, *refs):
    diff, count, normed, inv_dev, vectors, first, first_got, order = refs[:8]
    grad_out, low_out, sums_out, ordered_out, both = refs[8:]
    grad_top = diff[...] * ((SEG * GROUP * CORES) / count[0:1, 0:1])
    normed_rows = normed[...]
    grad = norm_rows_back(grad_top, normed_rows, inv_dev[...], vectors[6:7, :])
    low = grad.astype(LOW)
    grad_out[...] = grad
    low_out[...] = low
    sums_out[0:1, :] = column_sum(low)
    sums_out[1:2, :] = column_sum(grad_top * normed_rows)
    sums_out[2:3, :] = column_sum(grad_top)
    both[:SEG] = first[...]
    both[SEG:] = first_got[...]
    ordered_out[...] = product_plain(both[...], order[...]).astype(LOW)


def mlp_back_kernel(where, *refs):
    low, low_got, down_weight, up_weight, slope = refs[:5]
    pre_out, own_out, send_out, sums_out, both = refs[5:]
    both[:SEG] = low[...]
    both[SEG:] = low_got[...]
    for at in range(FF_HALF // MODEL):
        columns = slice(at * MODEL, (at + 1) * MODEL)
        held = down_weight[:, :, columns]
        before = product_plain(both[...], held.reshape(MODEL, MODEL))
        pre = (before * slope[:, columns]).astype(LOW)
        pre_out[:, columns] = pre
        sums_out[at : at + 1, :] = column_sum(pre)
    partial = product_right(pre_out[...], whole_rows(up_weight))
    own_out[...] = partial[:SEG]
    send_out[...] = partial[SEG:]


def scatter_parts(where, parts, outs, sems):
    line_at, plane_at = where[0], where[1]
    far_low, far_high, to_x, to_y, kept = outs
    half = LINE // 2
    copies = []
    for mask in range(PLANE):
        for step in range(LINE):
            source = parts.at[(line_at + step) % LINE * PLANE + (plane_at ^ mask)]
            if mask == 3:
                target = far_low.at[step] if step < half else far_high.at[step - half]
            else:
                target = (kept, to_x, to_y)[mask].at[step]
            copies.append(pltpu.make_async_copy(source, target, sems.at[len(copies)]))
    for copy in copies:
        copy.start()
    wait_all(copies)


def mlp_products(refs, masks, both, store):
    first, second, second_got, pre, act, order = refs
    both[:SEG] = second[...]
    both[SEG:] = second_got[...]
    for mask in masks:
        lanes = slice(mask * SPAN, (mask + 1) * SPAN)
        turned = product_plain(both[...], order[:, lanes]).astype(LOW)
        for at, (left, right) in enumerate(((first[:, lanes], pre), (turned, act))):
            for piece in range(FF_HALF // MODEL):
                start = piece * MODEL
                product = product_left(left, right[:, start : start + MODEL])
                product = product[: LINE * OWN].astype(LOW).reshape(LINE, OWN, MODEL)
                target = at * FF_HALF + start
                store(mask, slice(target, target + MODEL), product)


def mlp_far_kernel(where, *refs):
    low_out, high_out, both = refs[6:]
    half = LINE // 2

    def store(mask, columns, product):
        low_out[:, :, columns] = product[:half]
        high_out[:, :, columns] = product[half:]

    mlp_products(refs[:6], (3,), both, store)


def mlp_near_kernel(where, *refs):
    outs, both = refs[6:9], refs[9]

    def store(mask, columns, product):
        outs[mask - 1][:, :, columns] = product

    mlp_products(refs[:6], (1, 2, 0), both, store)


def attn_product(where, refs, mask, piece):
    hidden, mixed, proj, branch, got = refs
    lanes = slice(mask * SPAN, (mask + 1) * SPAN)
    if piece < 3:
        right = proj[:, piece * HALF : (piece + 1) * HALF]
        product = product_left(hidden[:, lanes], right)
    else:
        own = branch[:, pl.ds(aligned(where[2] * HALF), HALF)]
        product = product_left(mixed[:SEG, lanes], own)
        product = product + product_left(mixed[SEG:, lanes], got[:, HALF:])
    return product[: LINE * OWN].astype(LOW).reshape(LINE, OWN, HALF)


def attn_far_kernel(where, *refs):
    low_out, high_out = refs[5:]
    half = LINE // 2
    for piece in range(4):
        columns = slice(piece * HALF, (piece + 1) * HALF)
        product = attn_product(where, refs[:5], 3, piece)
        low_out[:, :, columns] = product[:half]
        high_out[:, :, columns] = product[half:]


def attn_near_kernel(where, *refs):
    proj, (top_row, out_rows, live_row) = refs[2], refs[5:8]
    weight, sums_first, sums_second, sums_up, head_top, head_normed, data = refs[8:15]
    x_out, y_out, kept_out, output_out, own_out, send_out, payload_out, rows = refs[15:]
    core_at = where[2]
    partial = product_right(proj[...], whole_rows(weight))
    own_out[...] = partial[:SEG]
    send_out[...] = partial[SEG:]
    row_at = lax.broadcasted_iota(jnp.int32, (SEG, 1), 0)
    output = jnp.where(row_at == 0, top_row[...] * live_row[:, 0:1], out_rows[...])
    output_out[...] = output.astype(LOW)
    for mask, out in ((1, x_out), (2, y_out), (0, kept_out)):
        for piece in range(4):
            columns = slice(piece * HALF, (piece + 1) * HALF)
            out[:, :, columns] = attn_product(where, refs[:5], mask, piece)
    lanes = pl.ds(aligned(core_at * HALF), HALF)
    rows[...] = jnp.zeros_like(rows)
    rows[0:12, :] = data[0:12, :]
    rows[12:13, lanes] = column_sum(proj[:, :HALF])
    rows[13:14, lanes] = column_sum(proj[:, 2 * HALF :])
    rows[14:15, :] = sums_first[0:1, :]
    rows[15:16, :] = sums_second[0:1, :] + data[2:3, :]
    rows[16:18, :] = sums_first[1:3, :]
    rows[18:19, :] = sums_second[1:2, :] + head_top[...] * head_normed[0:1, :]
    rows[19:20, :] = sums_second[2:3, :] + head_top[...]
    for at in range(FF_HALF // MODEL):
        total = sums_up[at : at + 1, :] + data[4 + 2 * at : 5 + 2 * at, :]
        total = total + data[5 + 2 * at : 6 + 2 * at, :]
        rows[pl.ds(20 + core_at * (FF_HALF // MODEL) + at, 1), :] = total
    payload_out[...] = rows[...].astype(LOW)


def fold_kernel(where, kept, got_x, got_y, *refs):
    extra, own_out, sent = refs[: -LINE], refs[-LINE], refs[1 - LINE :]
    rows = kept.shape[1]
    for step in range(LINE):
        total = kept[step].astype(WIDE) + got_x[step].astype(WIDE) + got_y[step].astype(WIDE)
        if step == 0:
            own_out[...] = total
            continue
        out = sent[step - 1]
        out[:rows, :] = total.astype(LOW)
        if extra:
            out[rows:, :] = jnp.zeros_like(out[rows:, :])
            out[rows:, : extra[0].shape[1]] = extra[0][...]


def reduce_far(parts):
    return together(in_plane(parts[0], 2), in_plane(parts[1], 1))


def reduce_add(where, parts, far):
    shape = parts[2].shape
    return run_kernel(
        add_far_kernel,
        "add_far",
        [shape_of(shape, LOW)] * 2,
        where,
        (),
        tuple(far) + (parts[2], parts[3]),
    )


def reduce_fold(where, kept, got, *extra):
    _, rows, columns = kept.shape
    more = sum(value.shape[0] for value in extra)
    return run_kernel(
        fold_kernel,
        "fold",
        [shape_of((rows, columns))] + [shape_of((rows + more, columns), LOW)] * (LINE - 1),
        where,
        (),
        (kept,) + tuple(got) + extra,
    )


def reduce_line(own, pieces):
    total = own
    for piece in pieces:
        total = total + piece[: own.shape[0]].astype(WIDE)
    return total


def head_back_kernel(where, *refs):
    grad, grad_got, down_weight, up_weight, slope, act, low, low_got = refs[:8]
    own_out, send_out, data_out = refs[8:]
    few = 16
    row_at = lax.broadcasted_iota(jnp.int32, (few, 1), 0)

    def two_rows(first, second):
        return jnp.where(row_at == 0, first, jnp.where(row_at == 1, second, 0.0))

    second = two_rows(grad[...], grad_got[...]).astype(LOW)
    data_out[0:1, :] = low[0:1, :].astype(WIDE)
    data_out[1:2, :] = low_got[0:1, :].astype(WIDE)
    data_out[2:4, :] = second[0:2].astype(WIDE)
    partial = jnp.zeros((few, MODEL), WIDE)
    for at in range(FF_HALF // MODEL):
        columns = slice(at * MODEL, (at + 1) * MODEL)
        before = product_plain(second, down_weight[:, :, columns].reshape(MODEL, MODEL))
        slopes = two_rows(slope[0:1, columns], slope[SEG : SEG + 1, columns])
        pre = (before * slopes).astype(LOW)
        partial = partial + product_right(pre, up_weight[:, :, columns].reshape(MODEL, MODEL))
        data_out[4 + 2 * at : 6 + 2 * at, :] = pre[0:2].astype(WIDE)
        data_out[8 + 2 * at : 9 + 2 * at, :] = act[0:1, columns].astype(WIDE)
        data_out[9 + 2 * at : 10 + 2 * at, :] = act[SEG : SEG + 1, columns].astype(WIDE)
    own_out[...] = partial[0:1]
    send_out[...] = partial[1:2]


def first_norm_kernel(where, *refs):
    second_grad, own, got, head_grad, head_own, head_got = refs[:6]
    normed_rows, inv_dev, vectors, out_weight = refs[6:10]
    grad_out, branch_out, mixed_out, send_out, sums_out = refs[10:]
    core_at = where[2]
    grad_rows = second_grad[...] + own[...] + got[...]
    head = head_grad[...] + head_own[...] + head_got[...]
    row_at = lax.broadcasted_iota(jnp.int32, (SEG, 1), 0)
    grad_rows = jnp.where(row_at == 0, head, grad_rows)
    normed = normed_rows[...]
    grad = norm_rows_back(grad_rows, normed, inv_dev[...], vectors[4:5, :])
    grad_out[...] = grad
    branch = grad.astype(LOW)
    branch_out[...] = branch
    mixed_out[...] = product_right(branch, out_weight[...]).astype(LOW)
    other = pl.ds(aligned((1 - core_at) * HALF), HALF)
    send_out[:, :HALF] = mixed_out[:, other]
    send_out[:, HALF:] = branch_out[:, other]
    sums_out[0:1, :] = column_sum(branch)
    sums_out[1:2, :] = column_sum(grad_rows * normed)
    sums_out[2:3, :] = column_sum(grad_rows)


def attn_back_kernel(where, *refs):
    qkv, mixed_grad, got, live_row, live_got, proj_out = refs
    core_at = where[2]
    lanes = pl.ds(aligned(core_at * HALF), HALF)
    for part, live in enumerate((live_row, live_got)):
        at = slice(part * SEG, (part + 1) * SEG)
        grad = mixed_grad[:, lanes] if part == 0 else got[:, :HALF]
        pieces = attend_tiles_back(qkv[at, :], grad, HALF, token_allowed(live[...]))
        for tile, value in enumerate(pieces):
            proj_out[at, tile * LANES : (tile + 1) * LANES] = value


def cls_gather_kernel(where, *refs):
    blocks = refs[:8]
    own_out, from_x, from_y, far_x = refs[8], refs[4], refs[5], refs[6]
    weight_out, out_rows = refs[9:]
    plane_at = where[1]
    gather_blocks(where, blocks, 0, QUARTER_HALF, ((weight_out, 0, QUARTER_HALF),))
    first = LINE * QUARTER_HALF
    out_rows[plane_at] = own_out[...]
    out_rows[plane_at ^ 1] = from_x[:, first : first + HALF]
    out_rows[plane_at ^ 2] = from_y[:, first : first + HALF]
    first = LINE // 2 * QUARTER_HALF
    out_rows[plane_at ^ 3] = far_x[:, first : first + HALF]


def cls_weight_kernel(where, own, got, out_half, out_got, weight_out, out_full):
    line_at, core_at = where[0], where[2]
    out_full[...] = jnp.zeros_like(out_full)
    for value, part, core in ((own, out_half, core_at), (got, out_got, 1 - core_at)):
        weight_out[:, :, pl.ds(aligned(core * QUARTER_HALF), QUARTER_HALF)] = value[...]
        rows = part[...].reshape(3, HEAD_DIM, HALF)
        out_full[pl.ds(line_at % 2, 3), :, pl.ds(aligned(core * HALF), HALF)] = rows


def add_far_kernel(where, far_low, far_high, to_x, to_y, x_out, y_out):
    half = LINE // 2
    x_out[:half] = to_x[:half] + far_low[...]
    x_out[half:] = to_x[half:]
    y_out[:half] = to_y[:half]
    y_out[half:] = to_y[half:] + far_high[...]


def row_from_column(column, size):
    shape = (size, size)
    same = lax.broadcasted_iota(jnp.int32, shape, 0) == lax.broadcasted_iota(jnp.int32, shape, 1)
    return jnp.sum(jnp.where(same, column, 0.0), axis=0, keepdims=True)


def head_allowed(heads):
    facts = heads[:, 2 * MODEL :]
    live, doc = facts[:, 0:1], facts[:, 1:2]
    shape = (GROUP, GROUP)
    same = lax.broadcasted_iota(jnp.int32, shape, 0) == lax.broadcasted_iota(jnp.int32, shape, 1)
    live_row, doc_row = row_from_column(live, GROUP), row_from_column(doc, GROUP)
    return ((live_row > 0.5) & (doc == doc_row)) | same


def quarter_mask(quarter):
    lane = lax.broadcasted_iota(jnp.int32, (GROUP, SPAN), 1)
    first = (quarter % 2) * HEAD_DIM
    return (lane >= first) & (lane < first + 3 * HEAD_DIM)


def quarter_piece(vectors, row, quarter):
    value = jnp.zeros((1, SPAN), WIDE)
    for at in range(LINE):
        first = TILE_START[at] * LANES
        value = jnp.where(quarter == at, vectors[row : row + 1, first : first + SPAN], value)
    return value


def cls_attend_kernel(where, *refs):
    stacks, vectors, weight, out_weight = refs[:4], refs[4], refs[5], refs[6]
    heads_out, qkv_out, mixed_out, part_out = refs[7:]
    line_at, plane_at = where[0], where[1]
    for step, stack in enumerate(stacks):
        for mask in range(PLANE):
            row = (line_at + LINE - step) % LINE * PLANE + (plane_at ^ mask)
            heads_out[pl.ds(row, 1), :] = stack[mask : mask + 1, :]
    heads = heads_out[...]
    inputs = heads[:, :MODEL].astype(LOW)
    projected = product_plain(inputs, weight[:, : 3 * SPAN])
    query = projected[:, :SPAN] + quarter_piece(vectors, 12, line_at)
    value = projected[:, 2 * SPAN :] + quarter_piece(vectors, 13, line_at)
    qkv_out[:, :SPAN] = query.astype(LOW)
    qkv_out[:, SPAN : 2 * SPAN] = projected[:, SPAN : 2 * SPAN].astype(LOW)
    qkv_out[:, 2 * SPAN :] = value.astype(LOW)
    mixed = attend_tiles(qkv_out[...], SPAN, head_allowed(heads))
    mixed = masked(jnp.concatenate(mixed, axis=1), quarter_mask(line_at))
    mixed_out[...] = mixed
    part_out[...] = product_plain(mixed, out_weight[...])


def cls_mlp_kernel(where, *refs):
    heads, own, got_one, got_two, got_three, vectors, weight = refs[:7]
    normed_out, inv_out, low_out, act_out, slope_out, part_out = refs[7:]
    line_at = where[0]
    branch = own[...] + got_one[...] + got_two[...] + got_three[...]
    normed, inv_dev = norm_rows(heads[:, :MODEL] + branch + vectors[14:15, :])
    normed_out[...] = normed
    inv_out[...] = inv_dev
    low = (normed * vectors[16:17, :] + vectors[17:18, :]).astype(LOW)
    low_out[...] = low
    part = FF // LINE
    first = 3 * SPAN
    bias = vectors[pl.ds(20 + line_at, 1), :]
    before = product_plain(low, weight[:, first : first + part]) + bias
    value, slope = gelu_both(before)
    act = value.astype(LOW)
    act_out[...] = act
    slope_out[...] = slope
    part_out[...] = product_right(act, weight[:, first + part :])


def cls_top_kernel(where, *refs):
    heads, own, got_one, got_two, got_three, vectors, weight = refs[:7]
    normed_first, count, slope = refs[7:10]
    top_out, square_out, grad_out, second_out, pre_out, part_out, sums_out = refs[10:17]
    held = refs[17]
    rank = where[0] * PLANE + where[1]
    first = normed_first[...] * vectors[16:17, :] + vectors[17:18, :]
    down = own[...] + got_one[...] + got_two[...] + got_three[...]
    normed, inv_dev = norm_rows(first + down + vectors[15:16, :])
    rows = normed * vectors[18:19, :] + vectors[19:20, :]
    held[...] = rows
    top_out[...] = held[pl.ds(rank, 1), :]
    facts = heads[:, 2 * MODEL :]
    live = facts[:, 0:1]
    diff = (rows * live - heads[:, MODEL : 2 * MODEL]) * live
    square = jnp.sum(column_sum(diff * diff), axis=1, keepdims=True)
    square = square + jnp.sum(facts[:, 3:4], axis=0, keepdims=True)
    square_out[...] = jnp.broadcast_to(square, square_out.shape)
    grad_top = diff * ((SEG * GROUP * CORES) / count[0:1, 0:1])
    grad = norm_rows_back(grad_top, normed, inv_dev, vectors[18:19, :])
    sums_out[0:1, :] = column_sum(grad_top * normed)
    sums_out[1:2, :] = column_sum(grad_top)
    grad_out[...] = grad
    second = grad.astype(LOW)
    second_out[...] = second
    part = FF // LINE
    at = 3 * SPAN
    pre = (product_plain(second, weight[:, at + part :]) * slope[...]).astype(LOW)
    pre_out[...] = pre
    part_out[...] = product_right(pre, weight[:, at : at + part])


def cls_attend_back_kernel(where, *refs):
    heads, own, got_one, got_two, got_three, vectors, weight, out_weight = refs[:8]
    grad_in, normed_first, inv_first, qkv = refs[8:12]
    grad_out, branch_out, proj_out, part_out, sums_out = refs[12:]
    line_at = where[0]
    grad_first = grad_in[...] + own[...] + got_one[...] + got_two[...] + got_three[...]
    normed = normed_first[...]
    grad = norm_rows_back(grad_first, normed, inv_first[...], vectors[16:17, :])
    sums_out[0:1, :] = column_sum(grad_first * normed)
    sums_out[1:2, :] = column_sum(grad_first)
    grad_out[...] = grad
    branch = grad.astype(LOW)
    branch_out[...] = branch
    mask = quarter_mask(line_at)
    mixed_grad = masked(product_right(branch, out_weight[...]).astype(LOW), mask)
    pieces = attend_tiles_back(qkv[...], mixed_grad, SPAN, head_allowed(heads[...]))
    tiles = SPAN // LANES
    for piece in range(3):
        joined = jnp.concatenate(pieces[piece * tiles : (piece + 1) * tiles], axis=1)
        proj_out[:, piece * SPAN : (piece + 1) * SPAN] = masked(joined, mask)
    part_out[...] = product_right(proj_out[...], weight[:, : 3 * SPAN])


def cls_end_kernel(where, *refs):
    heads, grad, own, got_one, got_two, got_three = refs[:6]
    square, sums_back, sums_top = refs[6:9]
    normed_second, inv_second, vectors = refs[9:12]
    row_out, second_out, shared_out, held = refs[12:]
    rank = where[0] * PLANE + where[1]
    total = grad[...] + own[...] + got_one[...] + got_two[...] + got_three[...]
    held[...] = total
    row = held[pl.ds(rank, 1), :]
    row_out[...] = row
    second_out[...] = norm_rows_back(
        row, normed_second[0:1, :], inv_second[0:1, :], vectors[6:7, :]
    )
    number = row_from_column(heads[:, 2 * MODEL + 2 : 2 * MODEL + 3], GROUP)
    entry = lax.broadcasted_iota(jnp.int32, (GROUP, GROUP), 0).astype(WIDE)
    hot = (entry == number).astype(WIDE)
    shared_out[0:GROUP, :] = jnp.dot(hot, total, precision=lax.Precision.HIGHEST)
    shared_out[GROUP : GROUP + 1, 0:LANES] = square[0:1, :]
    shared_out[GROUP + 1 : GROUP + 3, :] = sums_back[0:2, :]
    shared_out[GROUP + 3 : GROUP + 5, :] = sums_top[0:2, :]


def head_mlp_kernel(where, *refs):
    cls_mlp_kernel(where, *refs[:7], *refs[11:17])
    add_far_kernel(where, *refs[7:11], *refs[17:])


def head_end_kernel(where, *refs):
    cls_end_kernel(where, *refs[:12], *refs[16:19], refs[23])
    fold_kernel(where, *refs[12:16], *refs[19:23])


def attn_add_kernel(where, *refs):
    far_low, far_high, to_x, to_y, grad, own, got, x_out, y_out, input_out = refs
    add_far_kernel(where, far_low, far_high, to_x, to_y, x_out, y_out)
    input_out[...] = (grad[...] + own[...] + got[...]).astype(LOW)


def rows_input_kernel(where, *refs):
    cls_rows_kernel(where, *refs[:8], refs[11], refs[13])
    grad, own, got, input_out = refs[8], refs[9], refs[10], refs[12]
    input_out[...] = (grad[...] + own[...] + got[...]).astype(LOW)


def cls_rows_kernel(where, *refs):
    packs = refs[:4]
    heads, branch, low, second = refs[4:8]
    out, kept = refs[8:]
    line_at = where[0]
    rows, width = kept.shape[1:]
    for step, pack in enumerate(packs):
        first = pack.shape[0] - rows
        kept[(line_at + LINE - step) % LINE] = pack[first:, :width]
    starts = (MODEL, 2 * MODEL, 3 * MODEL, 4 * MODEL)
    out[:, 0:MODEL] = heads[:, :MODEL].astype(LOW)
    for piece, start in enumerate(starts):
        from_at = piece * SPAN
        for tile in range(MODEL // LANES):
            total = None
            for at in range(PLANE):
                inner = tile - TILE_START[at]
                if inner in (0, 1):
                    first = from_at + inner * LANES
                    value = kept[at, :, first : first + LANES]
                    total = value if total is None else total + value
            out[:, start + tile * LANES : start + (tile + 1) * LANES] = total
    out[:, 5 * MODEL : 6 * MODEL] = branch[...]
    out[:, 6 * MODEL : 7 * MODEL] = low[...]
    out[:, 7 * MODEL + FF : 8 * MODEL + FF] = second[...]
    part = FF // LINE
    for at in range(PLANE):
        first = 4 * SPAN
        out[:, 7 * MODEL + at * part : 7 * MODEL + (at + 1) * part] = kept[
            at, :, first : first + part
        ]
        out[:, 8 * MODEL + FF + at * part : 8 * MODEL + FF + (at + 1) * part] = kept[
            at, :, first + part : first + 2 * part
        ]


def own_features(rank, width):
    shape = (MODEL, width)
    feature = lax.broadcasted_iota(jnp.int32, shape, 0)
    column = lax.broadcasted_iota(jnp.int32, shape, 1)
    return (feature == rank * width + column).astype(LOW)


def own_vector(rank, pieces, out, flat):
    size = out.shape[0]
    for at, piece in enumerate(pieces):
        flat[:, at * MODEL : (at + 1) * MODEL] = piece
    value = jnp.zeros((1, size), WIDE)
    for chip in range(GROUP):
        value = jnp.where(rank == chip, flat[:, chip * size : (chip + 1) * size], value)
    out[...] = value.reshape(size)


def cls_owner_kernel(where, *refs):
    own, got, shared, mats_out, vec_out, rows, flat = refs
    rank = where[0] * PLANE + where[1]
    width = mats_out.shape[0]
    rows[:GROUP] = own[...]
    rows[GROUP:] = got[...]
    chosen = own_features(rank, width)
    plan = (
        (0, MODEL, 3 * MODEL, 0),
        (4 * MODEL, 5 * MODEL, MODEL, 3 * MODEL),
        (6 * MODEL, 7 * MODEL, FF, 4 * MODEL),
        (7 * MODEL + FF, 8 * MODEL + FF, FF, 4 * MODEL + FF),
    )
    for left, right, size, target in plan:
        side = product_plain(rows[:, left : left + MODEL], chosen).astype(LOW)
        mats_out[:, target : target + size] = product_left(side, rows[:, right : right + size])
    starts = (MODEL, 3 * MODEL, 5 * MODEL, 7 * MODEL + FF)
    pieces = [column_sum(rows[:, start : start + MODEL]) for start in starts]
    pieces += [shared[GROUP + 1 + at : GROUP + 2 + at, :] for at in range(4)]
    starts = [7 * MODEL + at * MODEL for at in range(FF // MODEL)]
    pieces += [column_sum(rows[:, start : start + MODEL]) for start in starts]
    own_vector(rank, pieces, vec_out, flat)


def head_share_kernel(where, *refs):
    packs, mlp = refs[:4], refs[4]
    mine_out, vecs_out, rows = refs[5:]
    rank = where[0] * PLANE + where[1]
    count = LINE * 24
    for at, pack in enumerate(packs):
        rows[at * count : (at + 1) * count] = pack[...]
    total = PLANE * count

    def chosen(base, apart):
        shape = (CORES * GROUP, total)
        row = lax.broadcasted_iota(jnp.int32, shape, 0)
        column = lax.broadcasted_iota(jnp.int32, shape, 1)
        hot = (column == row // 2 * 24 + base + row % 2 * apart).astype(LOW)
        return product_plain(hot, rows[...]).astype(LOW)

    own = own_features(rank, OWN)
    for at, (left, right) in enumerate(((0, 4), (2, 8))):
        side = product_plain(chosen(left, 1), own).astype(LOW)
        for piece in range(FF_HALF // MODEL):
            columns = slice(at * FF_HALF + piece * MODEL, at * FF_HALF + (piece + 1) * MODEL)
            share = product_left(side, chosen(right + 2 * piece, 1))
            mine_out[:, columns] = mlp[:, columns] + share
    shape = (16, total)
    row = lax.broadcasted_iota(jnp.int32, shape, 0)
    column = lax.broadcasted_iota(jnp.int32, shape, 1)
    hot = ((column % 24 == row + 12) & (row < 12)).astype(LOW)
    vecs_out[...] = product_plain(hot, rows[...])


def share_owner_kernel(where, *refs):
    head_share_kernel(where, *refs[:5], *refs[9:11], refs[15])
    cls_owner_kernel(where, *refs[5:8], *refs[11:13], *refs[16:])
    shared, count, pos_out, loss_out = refs[7], refs[8], refs[13], refs[14]
    pos_out[...] = shared[:GROUP, :]
    loss_out[...] = shared[GROUP : GROUP + 1, 0:1] / (count[0:1, 0:1] * MODEL)


def seg_vec_kernel(where, vecs, vecs_got, vec_out, flat):
    rank = where[0] * PLANE + where[1]
    rows = (8 * MODEL + FF) // MODEL
    pieces = [vecs[at : at + 1, :] + vecs_got[at : at + 1, :] for at in range(rows)]
    own_vector(rank, pieces, vec_out, flat)


def column_copies(where, out, base, size, own, got, first):
    core_at = where[2]
    lanes = slice(first, first + size)
    return [
        (own.at[:, lanes], out.at[:, pl.ds(aligned(base + core_at * size), size)]),
        (got.at[:, lanes], out.at[:, pl.ds(aligned(base + (1 - core_at) * size), size)]),
    ]


def store_kernel(where, attn, attn_got, mlp, mlp_got, vecs, vecs_got, out, vec_out, flat, sems):
    pairs = []
    for piece in range(4):
        pairs += column_copies(where, out, piece * MODEL, HALF, attn, attn_got, piece * HALF)
    for piece in range(2):
        base = 4 * MODEL + piece * FF
        pairs += column_copies(where, out, base, FF_HALF, mlp, mlp_got, piece * FF_HALF)
    copies = [
        pltpu.make_async_copy(source, target, sems.at[at])
        for at, (source, target) in enumerate(pairs)
    ]
    for copy in copies:
        copy.start()
    seg_vec_kernel(where, vecs, vecs_got, vec_out, flat)
    wait_all(copies)


def plane_parts(part):
    return (part,) + together(*(in_plane(part, mask) for mask in range(1, PLANE)))


def line_parts(part):
    return (part,) + together(*(along_line(part, apart) for apart in range(1, LINE)))


def slice_local(
    hidden_in,
    targets,
    doc_ids,
    seg_nums,
    valid_flags,
    seg_mats,
    seg_vecs,
    cls_mats,
    cls_vecs,
    seg_pos,
):
    rank, core_at = lax.axis_index("fsdp"), lax.axis_index("rep")
    line_at, plane_at = rank // PLANE, rank % PLANE
    where = jnp.stack([line_at, plane_at, core_at, doc_ids[0], seg_nums[0]]).astype(jnp.int32)
    own_rows, total_columns = seg_mats.shape
    vec_size = seg_vecs.shape[0]
    both_rows = CORES * SEG

    first_piece, live_row, *rest = run_kernel(
        prepare_kernel,
        "prepare",
        [shape_of((own_rows, FIRST), LOW), shape_of((1, SEG))]
        + [shape_of((own_rows, FF_HALF), LOW)] * 2
        + [shape_of((own_rows, QUARTER_HALF), LOW)] * LINE
        + [shape_of((own_rows, HALF), LOW), shape_of((MODEL, PLANE * SPAN), LOW)],
        where,
        (seg_mats, cls_mats),
        (seg_vecs, cls_vecs, valid_flags),
        [
            pltpu.SemaphoreType.DMA((4,)),
            pltpu.VMEM((LINE, own_rows, QUARTER), LOW),
            pltpu.SemaphoreType.DMA((3 + 5 * LINE,)),
        ],
    )
    first_line = line_parts(first_piece)
    second_piece, third_piece, quarters, cls_out_piece, order = (
        rest[0],
        rest[1],
        rest[2:-2],
        rest[-2],
        rest[-1],
    )

    def joined(*pieces):
        return jnp.concatenate(pieces, axis=1)

    def sent_both(to_x, to_y):
        to_x, to_y = together(to_x, to_y)
        return together(in_plane(to_x, 1), in_plane(to_y, 2))

    own_sent = joined(first_piece, second_piece, third_piece)
    own_x, own_y = sent_both(own_sent, own_sent)
    first_line = first_line[:1] + tuple(after(got, own_x, own_y) for got in first_line[1:])
    hidden_got = other_core(after(hidden_in, own_x, own_y))
    live_got = other_core(after(live_row, own_x, own_y))
    to_x = joined(after(own_y, hidden_got, live_got)[:, OWN_CUT:], *first_line[1:])
    to_y = joined(own_x[:, :OWN_CUT], *first_line[1:])
    first_x, first_y = sent_both(to_x, to_y)
    second_line = line_parts(after(second_piece, to_x, to_y))

    def halves(group, from_x, from_y):
        width, cut = WIDTHS[group], LINE_CUTS[group]
        if group == 0:
            base_x, base_y = sum(WIDTHS) - OWN_CUT, OWN_CUT
        else:
            before, before_cut = WIDTHS[group - 1], LINE_CUTS[group - 1]
            base_x, base_y = 2 * before - before_cut, before + before_cut
        return (
            from_y[:, base_y + width + cut : base_y + 3 * width],
            from_x[:, base_x : base_x + width + cut],
        )

    high, low = halves(0, first_x, first_y)
    to_x, to_y = joined(high, *second_line[1:]), joined(low, *second_line[1:])
    second_x, second_y = sent_both(to_x, to_y)
    third_line = line_parts(after(third_piece, to_x, to_y))
    high, low = halves(1, second_x, second_y)
    to_x, to_y = joined(high, *third_line[1:]), joined(low, *third_line[1:])
    third_x, third_y = sent_both(to_x, to_y)
    own_parts = (own_x, own_y, first_x, first_y)
    cls_line = (quarters[0],) + tuple(
        along_line(after(quarters[apart], to_x, to_y), apart)
        for apart in range(1, LINE)
    )

    qkv_weight, out_low, out_high, qkv, mixed, vectors, count, hidden_ordered = run_kernel(
        qkv_kernel,
        "seg_qkv",
        [
            shape_of((GROUP, own_rows, 3 * HALF), LOW),
            shape_of((GROUP // 2, own_rows, HALF), LOW),
            shape_of((GROUP // 2, own_rows, HALF), LOW),
            shape_of((both_rows, 3 * HALF), LOW),
            shape_of((both_rows, HALF), LOW),
            shape_of((2 * (8 * MODEL + FF) // MODEL, MODEL)),
            shape_of((8, LANES)),
            shape_of((both_rows, PLANE * SPAN), LOW),
        ],
        where,
        (),
        first_line
        + own_parts
        + (first_x, first_y, second_x, second_y)
        + (hidden_in, hidden_got, live_row, live_got, order),
        [
            pltpu.VMEM((GROUP, own_rows, LANES), LOW),
            pltpu.VMEM((2, 8 * MODEL + FF), WIDE),
            pltpu.VMEM((both_rows, MODEL), LOW),
            pltpu.VMEM((GROUP, own_rows, HALF), LOW),
        ],
        flops=2 * SEG * MODEL * 3 * MODEL,
    )
    out_weight, mixed_ordered, normed_first, inv_first, first_low = run_kernel(
        out_kernel,
        "seg_out",
        [
            shape_of((MODEL, MODEL), LOW),
            shape_of((both_rows, PLANE * SPAN), LOW),
            shape_of((SEG, MODEL)),
            shape_of((SEG, 1)),
            shape_of((SEG, MODEL), LOW),
        ],
        where,
        (),
        (
            hidden_in,
            mixed,
            after(other_core(mixed), third_x, third_y),
            out_low,
            out_high,
            other_core(out_low),
            other_core(out_high),
            vectors,
            order,
        ),
        [pltpu.VMEM((both_rows, MODEL), LOW)],
        flops=2 * SEG * MODEL * MODEL,
    )
    fourth_x, fourth_y = sent_both(*halves(2, third_x, third_y))
    first_got = after(other_core(first_low), fourth_x, fourth_y)
    count = count + other_core(after(count, first_got))
    up_weight, act, slope = run_kernel(
        up_kernel,
        "seg_up",
        [
            shape_of((GROUP, own_rows, FF_HALF), LOW),
            shape_of((both_rows, FF_HALF), LOW),
            shape_of((both_rows, FF_HALF)),
        ],
        where,
        (),
        second_line
        + own_parts
        + (second_x, second_y, third_x, third_y)
        + (first_low, first_got, vectors),
        [pltpu.VMEM((both_rows, MODEL), LOW)],
        flops=2 * SEG * MODEL * FF,
    )
    cls_sent = joined(*cls_line, cls_out_piece)
    cls_sent = after(cls_sent, act)
    cls_x, cls_y = sent_both(cls_sent, cls_sent)
    down_weight, down_own, down_send = run_kernel(
        down_kernel,
        "seg_down",
        [
            shape_of((GROUP, own_rows, FF_HALF), LOW),
            shape_of((SEG, MODEL)),
            shape_of((SEG, MODEL)),
        ],
        where,
        (),
        third_line + own_parts + (third_x, third_y, fourth_x, fourth_y) + (act,),
        flops=2 * SEG * MODEL * FF,
    )
    normed_second, inv_second, diff, out_rows, head_row = run_kernel(
        seg_rows_kernel,
        "seg_rows",
        [
            shape_of((SEG, MODEL)),
            shape_of((SEG, 1)),
            shape_of((SEG, MODEL)),
            shape_of((SEG, MODEL)),
            shape_of((1, 2 * MODEL + LANES)),
        ],
        where,
        (),
        (
            down_own,
            other_core(down_send),
            normed_first,
            vectors,
            targets,
            live_row,
            seg_pos,
        ),
    )
    head_planes = plane_parts(head_row)
    size = LINE // 2 * QUARTER_HALF
    cls_far = sent_both(
        after(cls_y[:, size:], *head_planes[1:]), after(cls_x[:, :size], *head_planes[1:])
    )

    second_grad, second_low, second_sums, first_ordered = run_kernel(
        second_norm_kernel,
        "seg_second_norm",
        [
            shape_of((SEG, MODEL)),
            shape_of((SEG, MODEL), LOW),
            shape_of((3, MODEL)),
            shape_of((both_rows, PLANE * SPAN), LOW),
        ],
        where,
        (),
        (diff, count, normed_second, inv_second, vectors, first_low, first_got, order),
        [pltpu.VMEM((both_rows, MODEL), LOW)],
    )
    second_got = other_core(second_low)
    head_lines = line_parts(after(jnp.concatenate(head_planes), second_got))
    pre, first_grad_own, first_grad_send, up_sums = run_kernel(
        mlp_back_kernel,
        "seg_mlp_back",
        [
            shape_of((both_rows, FF_HALF), LOW),
            shape_of((SEG, MODEL)),
            shape_of((SEG, MODEL)),
            shape_of((FF_HALF // MODEL, MODEL)),
        ],
        where,
        (),
        (second_low, second_got, down_weight, up_weight, slope),
        [pltpu.VMEM((both_rows, MODEL), LOW)],
        flops=4 * SEG * MODEL * FF,
    )
    first_grad_got = other_core(first_grad_send)

    def part_shapes(columns):
        return [
            shape_of((count_of, own_rows, columns), LOW)
            for count_of in (LINE // 2, LINE // 2, LINE, LINE, LINE)
        ]

    mlp_data = (first_ordered, second_low, second_got, pre, act, order)
    mlp_far = run_kernel(
        mlp_far_kernel,
        "seg_mlp_far",
        part_shapes(FF)[:2],
        where,
        (),
        mlp_data,
        [pltpu.VMEM((both_rows, MODEL), LOW)],
        flops=SEG * MODEL * FF,
    )
    head_lines = head_lines[:1] + together(
        *(after(got, mlp_far[0]) for got in head_lines[1:])
    )
    cls_far = together(*(after(got, *head_lines[1:]) for got in cls_far))
    cls_half, cls_out_half = run_kernel(
        cls_gather_kernel,
        "head_gather",
        [
            shape_of((GROUP, own_rows, QUARTER_HALF), LOW),
            shape_of((PLANE, own_rows, HALF), LOW),
        ],
        where,
        (),
        cls_line + (cls_x, cls_y) + cls_far + (cls_out_piece,),
    )
    mlp_parts = list(mlp_far) + list(
        run_kernel(
            mlp_near_kernel,
            "seg_mlp_near",
            part_shapes(FF)[2:],
            where,
            (),
            mlp_data,
            [pltpu.VMEM((both_rows, MODEL), LOW)],
            flops=3 * SEG * MODEL * FF,
        )
    )
    mlp_far = reduce_far(tuple(after(part, *cls_far) for part in mlp_parts[:2]))
    cls_weight, cls_out = run_kernel(
        cls_weight_kernel,
        "head_weight",
        [
            shape_of((GROUP, own_rows, QUARTER), LOW),
            shape_of((4, HEAD_DIM, MODEL), LOW),
        ],
        where,
        (),
        (cls_half, other_core(cls_half), cls_out_half, other_core(cls_out_half)),
    )
    cls_weight = cls_weight.reshape(MODEL, QUARTER)
    cls_out = cls_out.reshape(SPAN, MODEL)
    heads, cls_qkv, cls_mixed, part = run_kernel(
        cls_attend_kernel,
        "head_attend",
        [
            shape_of((GROUP, 2 * MODEL + LANES)),
            shape_of((GROUP, 3 * SPAN), LOW),
            shape_of((GROUP, SPAN), LOW),
            shape_of((GROUP, MODEL)),
        ],
        where,
        (),
        tuple(after(got, mlp_parts[0], first_grad_got) for got in head_lines)
        + (vectors, cls_weight, cls_out),
    )
    cls_normed, cls_inv, cls_low, cls_act, cls_slope, part, *mlp_sent = run_kernel(
        head_mlp_kernel,
        "head_mlp",
        [
            shape_of((GROUP, MODEL)),
            shape_of((GROUP, 1)),
            shape_of((GROUP, MODEL), LOW),
            shape_of((GROUP, FF // LINE), LOW),
            shape_of((GROUP, FF // LINE)),
            shape_of((GROUP, MODEL)),
            shape_of(mlp_parts[2].shape, LOW),
            shape_of(mlp_parts[2].shape, LOW),
        ],
        where,
        (),
        (heads,) + line_parts(part) + (vectors, cls_weight) + mlp_far + tuple(mlp_parts[2:4]),
    )
    mlp_plane = sent_both(*mlp_sent)
    cls_parts = line_parts(part)
    top_row, square, cls_grad, cls_second, cls_pre, part, top_sums = run_kernel(
        cls_top_kernel,
        "head_top",
        [
            shape_of((1, MODEL)),
            shape_of((8, LANES)),
            shape_of((GROUP, MODEL)),
            shape_of((GROUP, MODEL), LOW),
            shape_of((GROUP, FF // LINE), LOW),
            shape_of((GROUP, MODEL)),
            shape_of((2, MODEL)),
        ],
        where,
        (),
        (heads,)
        + cls_parts
        + (vectors, cls_weight, cls_normed, count, cls_slope),
        [pltpu.VMEM((GROUP, MODEL), WIDE)],
    )
    top_parts = line_parts(part)
    cls_grad, cls_branch, cls_proj, part, back_sums = run_kernel(
        cls_attend_back_kernel,
        "head_attend_back",
        [
            shape_of((GROUP, MODEL)),
            shape_of((GROUP, MODEL), LOW),
            shape_of((GROUP, 3 * SPAN), LOW),
            shape_of((GROUP, MODEL)),
            shape_of((2, MODEL)),
        ],
        where,
        (),
        (heads,)
        + top_parts
        + (vectors, cls_weight, cls_out, cls_grad, cls_normed, cls_inv, cls_qkv),
    )
    end_parts = line_parts(part)
    pack = jnp.concatenate([cls_proj, cls_mixed, cls_pre, cls_act], axis=1)
    folded = [shape_of((own_rows, FF))] + [shape_of((own_rows + GROUP, FF), LOW)] * (LINE - 1)
    dheads, head_grad, shared, mlp_own, *mlp_sent = run_kernel(
        head_end_kernel,
        "head_end",
        [shape_of((1, MODEL)), shape_of((1, MODEL)), shape_of((GROUP + 8, MODEL))] + folded,
        where,
        (),
        (heads, cls_grad)
        + end_parts
        + (square, back_sums, top_sums, normed_second, inv_second, vectors)
        + (mlp_parts[4],)
        + mlp_plane
        + (pack,),
        [pltpu.VMEM((GROUP, MODEL), WIDE)],
    )
    got_three, got_two = along_line(mlp_sent[2], 3), along_line(mlp_sent[1], 2)
    mlp_last = mlp_sent[0]
    mlp_got = [None, got_two, got_three]

    head_own, head_send, head_data = run_kernel(
        head_back_kernel,
        "seg_head_back",
        [shape_of((1, MODEL)), shape_of((1, MODEL)), shape_of((12, MODEL))],
        where,
        (),
        (
            head_grad,
            other_core(head_grad),
            down_weight,
            up_weight,
            slope,
            act,
            first_low,
            first_got,
        ),
    )
    grad_summed, branch, mixed_grad, attn_send, first_sums = run_kernel(
        first_norm_kernel,
        "seg_first_norm",
        [
            shape_of((SEG, MODEL)),
            shape_of((SEG, MODEL), LOW),
            shape_of((SEG, MODEL), LOW),
            shape_of((SEG, MODEL), LOW),
            shape_of((3, MODEL)),
        ],
        where,
        (),
        (
            second_grad,
            first_grad_own,
            first_grad_got,
            head_grad,
            head_own,
            other_core(head_send),
            normed_first,
            inv_first,
            vectors,
            out_weight,
        ),
    )
    attn_got = other_core(attn_send)
    proj = run_kernel(
        attn_back_kernel,
        "seg_attn_back",
        [shape_of((both_rows, 3 * HALF), LOW)],
        where,
        (),
        (qkv, mixed_grad, attn_got, live_row, live_got),
        flops=2 * SEG * MODEL * 3 * MODEL,
    )[0]
    attn_data = (hidden_ordered, mixed_ordered, proj, branch, attn_got)
    attn_far = run_kernel(
        attn_far_kernel,
        "seg_attn_far",
        part_shapes(4 * HALF)[:2],
        where,
        (),
        attn_data,
        flops=SEG * MODEL * 2 * MODEL,
    )
    attn_far = reduce_far(tuple(after(part, mlp_got[-1]) for part in attn_far))
    *attn_near, output, input_own, input_send, payload = run_kernel(
        attn_near_kernel,
        "seg_attn_near",
        part_shapes(4 * HALF)[2:]
        + [
            shape_of((SEG, MODEL), LOW),
            shape_of((SEG, MODEL)),
            shape_of((SEG, MODEL)),
            shape_of((24, MODEL), LOW),
        ],
        where,
        (),
        attn_data
        + (top_row, out_rows, live_row, qkv_weight, first_sums, second_sums, up_sums)
        + (dheads, normed_second, head_data),
        [pltpu.VMEM((24, MODEL), WIDE)],
        flops=3 * SEG * MODEL * 2 * MODEL,
    )
    attn_sent = run_kernel(
        add_far_kernel,
        "seg_attn_add",
        [shape_of(attn_near[0].shape, LOW)] * 2,
        where,
        (),
        attn_far + (after(attn_near[0], got_two), attn_near[1]),
    )
    attn_plane = sent_both(*attn_sent)
    mlp_got[0] = along_line(after(mlp_last, *attn_sent), 1)
    input_got = other_core(after(input_send, *attn_sent))
    shared = shared + other_core(after(shared, attn_sent[0]))
    payload_parts = line_parts(after(payload, mlp_got[0], input_got, shared))
    mlp_got = [after(got, attn_plane[0]) for got in mlp_got]
    mlp_sum = reduce_line(mlp_own, mlp_got)
    row_width = 8 * MODEL + 2 * FF
    cls_rows, input_grad = run_kernel(
        rows_input_kernel,
        "head_rows",
        [shape_of((GROUP, row_width), LOW), shape_of((SEG, MODEL), LOW)],
        where,
        (),
        (pack,)
        + tuple(mlp_got)
        + (heads, cls_branch, cls_low, cls_second)
        + (grad_summed, input_own, input_got),
        [pltpu.VMEM((LINE,) + pack.shape, LOW)],
    )
    cls_got = other_core(cls_rows)
    attn_plane = tuple(after(got, output, shared) for got in attn_plane)
    attn_own, *attn_sent = reduce_fold(where, attn_near[2], attn_plane)
    attn_lines = list(
        together(*(along_line(attn_sent[apart - 1], apart) for apart in range(1, LINE)))
    )
    flat = pltpu.VMEM((1, 8 * MODEL + FF), WIDE)
    payload_line = jnp.concatenate(payload_parts)
    mlp_mine, own_vecs, cls_mats_grad, cls_vec_grad, pos_total, loss_value = run_kernel(
        share_owner_kernel,
        "head_owner",
        [
            shape_of((own_rows, FF)),
            shape_of((16, MODEL)),
            shape_of((own_rows, total_columns)),
            shape_of((vec_size,)),
            shape_of((GROUP, MODEL)),
            shape_of((1, 1)),
        ],
        where,
        (),
        tuple(after(got, attn_own) for got in plane_parts(after(payload_line, *attn_plane)))
        + (mlp_sum, cls_rows, cls_got, shared, count),
        [
            pltpu.VMEM((GROUP * 24, MODEL), LOW),
            pltpu.VMEM((CORES * GROUP, row_width), LOW),
            flat,
        ],
        flops=64 * own_rows * total_columns,
    )
    loss_value = loss_value.reshape(())
    attn_lines = together(*(after(got, mlp_mine) for got in attn_lines))
    attn_sum = reduce_line(attn_own, attn_lines)
    seg_mats_grad, seg_vec_grad = run_kernel(
        store_kernel,
        "seg_owner",
        [shape_of((own_rows, total_columns)), shape_of((vec_size,))],
        where,
        (),
        (attn_sum, other_core(attn_sum), mlp_mine, other_core(mlp_mine))
        + (own_vecs, other_core(own_vecs)),
        [flat, pltpu.SemaphoreType.DMA((12,))],
        far=(0,),
    )

    return (
        output,
        input_grad,
        seg_mats_grad,
        seg_vec_grad,
        cls_mats_grad,
        cls_vec_grad,
        pos_total,
        loss_value,
    )


def solution(mesh):
    in_specs = (
        P(("rep", "fsdp"), None),
        P(("rep", "fsdp"), None),
        P(("rep", "fsdp")),
        P(("rep", "fsdp")),
        P(("rep", "fsdp")),
        P("fsdp", None),
        P("fsdp"),
        P("fsdp", None),
        P("fsdp"),
        P(),
    )
    out_specs = (
        P(("rep", "fsdp"), None),
        P(("rep", "fsdp"), None),
        P("fsdp", None),
        P("fsdp"),
        P("fsdp", None),
        P("fsdp"),
        P(),
        P(),
    )
    one_slice = dict(mesh.shape) == {"rep": CORES, "fsdp": LINE * PLANE}
    body = slice_local if one_slice else local
    return jax.shard_map(body, mesh=mesh, in_specs=in_specs, out_specs=out_specs, check_vma=False)
```

```python
import math

import jax
import jax.numpy as jnp
from jax import lax
from jax.experimental import pallas as pl
from jax.experimental.pallas import tpu as pltpu
from jax.sharding import PartitionSpec as P

HEADS = 12
HEAD_DIM = 64
FF = 3072
SEG = 128
SEQ = 2048


NORM_EPS = 1e-05
MASK_FILL = -1e30
SQRT_HALF = 0.7071067811865476
INV_SQRT_TWO_PI = 0.3989422804014327


def swapped(value, axis, apart):
    mask = 2**apart
    pairs = [(source, source ^ mask) for source in range(lax.axis_size(axis))]
    return lax.ppermute(value, axis, pairs)


def product_plain(left_side, right_side):
    return jnp.dot(left_side, right_side, preferred_element_type=jnp.float32)


def product_left(left_side, right_side):
    return lax.dot_general(
        left_side, right_side, (((0,), (0,)), ((), ())), preferred_element_type=jnp.float32
    )


def product_right(left_side, right_side):
    return lax.dot_general(
        left_side, right_side, (((1,), (1,)), ((), ())), preferred_element_type=jnp.float32
    )


def row_total(array_in):
    return jnp.sum(array_in.astype(jnp.float32), axis=0)


def unpack_weights(gathered, model_width, ff_width):
    matrix, vector = gathered
    vector = vector.astype(jnp.float32)
    pieces = tuple(
        (vector[offset * model_width : (offset + 1) * model_width] for offset in range(8))
    )
    return (
        (
            matrix[:, : 3 * model_width],
            matrix[:, 3 * model_width : 4 * model_width],
            matrix[:, 4 * model_width : 4 * model_width + ff_width],
            matrix[:, 4 * model_width + ff_width :],
        )
        + pieces
        + (vector[8 * model_width :],)
    )


def norm_forward(summed, gain_vec, shift_vec):
    row_mean = jnp.mean(summed, axis=-1, keepdims=True)
    centered = summed - row_mean
    inv_dev = lax.rsqrt(jnp.mean(centered * centered, axis=-1, keepdims=True) + NORM_EPS)
    normed = centered * inv_dev
    return (normed * gain_vec + shift_vec, normed, inv_dev)


def norm_backward(grad_out, normed, inv_dev, gain_vec):
    scaled = grad_out * gain_vec
    mean_one = jnp.mean(scaled, axis=-1, keepdims=True)
    mean_two = jnp.mean(scaled * normed, axis=-1, keepdims=True)
    grad_in = inv_dev * (scaled - mean_one - normed * mean_two)
    return (grad_in, jnp.sum(grad_out * normed, axis=0), jnp.sum(grad_out, axis=0))


def gelu_value(before):
    return 0.5 * before * (1.0 + lax.erf(before * SQRT_HALF))


def gelu_slope(before):
    return (
        0.5 * (1.0 + lax.erf(before * SQRT_HALF))
        + before * jnp.exp(-0.5 * before * before) * INV_SQRT_TWO_PI
    )


def attention_scores(queries, keys_in, allowed, score_scale):
    raw_scores = (
        jnp.einsum("bqhe,bkhe->bhqk", queries, keys_in, preferred_element_type=jnp.float32)
        * score_scale
    )
    return jnp.where(allowed, raw_scores, MASK_FILL)


def attention_forward(queries, keys_in, values, allowed, score_scale):
    scores = attention_scores(queries, keys_in, allowed, score_scale)
    row_top = jnp.max(scores, axis=-1, keepdims=True)
    log_total = row_top + jnp.log(jnp.sum(jnp.exp(scores - row_top), axis=-1, keepdims=True))
    weights = jnp.exp(scores - log_total).astype(jnp.bfloat16)
    mixed_rows = jnp.einsum("bhqk,bkhe->bqhe", weights, values, preferred_element_type=jnp.float32)
    return (mixed_rows, log_total)


def attention_backward(queries, keys_in, values, allowed, score_scale, log_total, grad_mixed):
    probabilities = jnp.exp(attention_scores(queries, keys_in, allowed, score_scale) - log_total)
    grad_probs = jnp.einsum(
        "bqhe,bkhe->bhqk", grad_mixed, values, preferred_element_type=jnp.float32
    )
    inner_sum = jnp.sum(grad_probs * probabilities, axis=-1, keepdims=True)
    grad_scores = (probabilities * (grad_probs - inner_sum)).astype(jnp.bfloat16)
    grad_query = (
        jnp.einsum("bhqk,bkhe->bqhe", grad_scores, keys_in, preferred_element_type=jnp.float32)
        * score_scale
    )
    grad_key = (
        jnp.einsum("bhqk,bqhe->bkhe", grad_scores, queries, preferred_element_type=jnp.float32)
        * score_scale
    )
    grad_value = jnp.einsum(
        "bhqk,bqhe->bkhe",
        probabilities.astype(jnp.bfloat16),
        grad_mixed,
        preferred_element_type=jnp.float32,
    )
    return (grad_query, grad_key, grad_value)


def block_forward(rows_in, unpacked, attend):
    (
        qkv_weight,
        out_weight,
        up_weight,
        down_weight,
        query_bias,
        value_bias,
        out_bias,
        down_bias,
        gain_first,
        shift_first,
        gain_second,
        shift_second,
        up_bias,
    ) = unpacked
    model_width = rows_in.shape[1]
    inputs = rows_in.astype(jnp.bfloat16)
    projected = product_plain(inputs, qkv_weight)
    queries = (projected[:, :model_width] + query_bias).astype(jnp.bfloat16)
    keys_in = projected[:, model_width : 2 * model_width].astype(jnp.bfloat16)
    values = (projected[:, 2 * model_width :] + value_bias).astype(jnp.bfloat16)
    mixed_rows, attend_kept = attend(queries, keys_in, values)
    mixed_rows = mixed_rows.astype(jnp.bfloat16)
    summed_first = rows_in + product_plain(mixed_rows, out_weight) + out_bias
    first_out, normed_first, inv_first = norm_forward(summed_first, gain_first, shift_first)
    first_low = first_out.astype(jnp.bfloat16)
    pre_act = product_plain(first_low, up_weight) + up_bias
    activated = gelu_value(pre_act).astype(jnp.bfloat16)
    summed_second = first_out + product_right(activated, down_weight) + down_bias
    block_out, normed_second, inv_second = norm_forward(summed_second, gain_second, shift_second)
    saved_state = (
        inputs,
        queries,
        keys_in,
        values,
        attend_kept,
        mixed_rows,
        normed_first,
        inv_first,
        first_low,
        pre_act,
        activated,
        normed_second,
        inv_second,
    )
    return (block_out, saved_state)


def block_backward(grad_out, unpacked, saved_state, attend_back):
    (
        qkv_weight,
        out_weight,
        up_weight,
        down_weight,
        query_bias,
        value_bias,
        out_bias,
        down_bias,
        gain_first,
        shift_first,
        gain_second,
        shift_second,
        up_bias,
    ) = unpacked
    (
        inputs,
        queries,
        keys_in,
        values,
        attend_kept,
        mixed_rows,
        normed_first,
        inv_first,
        first_low,
        pre_act,
        activated,
        normed_second,
        inv_second,
    ) = saved_state
    grad_second, grad_gain_second, grad_shift_second = norm_backward(
        grad_out, normed_second, inv_second, gain_second
    )
    second_low = grad_second.astype(jnp.bfloat16)
    grad_pre = (product_plain(second_low, down_weight) * gelu_slope(pre_act)).astype(jnp.bfloat16)
    grad_first = grad_second + product_right(grad_pre, up_weight)
    grad_summed, grad_gain_first, grad_shift_first = norm_backward(
        grad_first, normed_first, inv_first, gain_first
    )
    branch_low = grad_summed.astype(jnp.bfloat16)
    grad_mixed = product_right(branch_low, out_weight).astype(jnp.bfloat16)
    grad_query, grad_key, grad_value = attend_back(
        queries, keys_in, values, attend_kept, grad_mixed
    )
    grad_proj = jnp.concatenate([grad_query, grad_key, grad_value], axis=1)
    grad_rows = grad_summed + product_right(grad_proj, qkv_weight)
    vector_grad = jnp.concatenate(
        [
            row_total(grad_query),
            row_total(grad_value),
            row_total(branch_low),
            row_total(second_low),
            grad_gain_first,
            grad_shift_first,
            grad_gain_second,
            grad_shift_second,
            row_total(grad_pre),
        ]
    )
    weight_rows = (
        inputs,
        grad_proj,
        mixed_rows,
        branch_low,
        first_low,
        grad_pre,
        second_low,
        activated,
    )
    return (grad_rows, weight_rows, vector_grad)


def weight_products(weight_rows):
    inputs, grad_proj, mixed_rows, branch_low, first_low, grad_pre, second_low, activated = (
        weight_rows
    )
    return (
        product_left(inputs, grad_proj),
        product_left(mixed_rows, branch_low),
        product_left(first_low, grad_pre),
        product_left(second_low, activated),
    )


def local(
    hidden_in,
    targets,
    doc_ids,
    seg_nums,
    valid_flags,
    seg_mats,
    seg_vecs,
    cls_mats,
    cls_vecs,
    seg_pos,
):
    tok_rows, model_width = hidden_in.shape
    ff_width = FF
    seg_len = SEG
    group_span = SEQ // tok_rows
    seg_count = tok_rows // seg_len
    score_scale = HEAD_DIM ** (-0.5)
    head_shape = (HEADS, HEAD_DIM)
    live_rows = valid_flags.astype(jnp.float32)
    rank_full = lax.axis_index("fsdp")
    seg_gathered = (
        lax.all_gather(seg_mats, "fsdp", axis=0, tiled=True),
        lax.all_gather(seg_vecs, "fsdp", axis=0, tiled=True),
    )
    seg_unpacked = unpack_weights(seg_gathered, model_width, ff_width)
    cls_gathered = (
        lax.all_gather(cls_mats, "fsdp", axis=0, tiled=True),
        lax.all_gather(cls_vecs, "fsdp", axis=0, tiled=True),
    )
    cls_unpacked = unpack_weights(cls_gathered, model_width, ff_width)
    seg_allowed = (live_rows.reshape(seg_count, 1, 1, seg_len) > 0.5) | jnp.eye(seg_len, dtype=bool)
    seg_shape = (seg_count, seg_len) + head_shape

    def seg_attend(queries, keys_in, values):
        mixed_rows, log_total = attention_forward(
            queries.reshape(seg_shape),
            keys_in.reshape(seg_shape),
            values.reshape(seg_shape),
            seg_allowed,
            score_scale,
        )
        return (mixed_rows.reshape(tok_rows, model_width), log_total)

    def seg_attend_back(queries, keys_in, values, log_total, grad_mixed):
        grad_parts = attention_backward(
            queries.reshape(seg_shape),
            keys_in.reshape(seg_shape),
            values.reshape(seg_shape),
            seg_allowed,
            score_scale,
            log_total,
            grad_mixed.reshape(seg_shape),
        )
        return tuple(
            (
                grad_part.reshape(tok_rows, model_width).astype(jnp.bfloat16)
                for grad_part in grad_parts
            )
        )

    first_out, seg_saved = block_forward(hidden_in.astype(jnp.float32), seg_unpacked, seg_attend)
    first_grid = first_out.reshape(seg_count, seg_len, model_width)
    position_hot = (seg_nums[:, None] == jnp.arange(seg_pos.shape[0])[None, :]).astype(jnp.float32)
    position_rows = jnp.sum(
        position_hot[:, :, None] * seg_pos.astype(jnp.float32)[None, :, :], axis=1
    )
    heads_in = first_grid[:, 0, :] + position_rows
    lead_live = live_rows.reshape(seg_count, seg_len)[:, 0]
    lead_doc = doc_ids.reshape(seg_count, seg_len)[:, 0]
    lead_labels = jnp.where(lead_live > 0.5, lead_doc, -1).astype(jnp.bfloat16)
    lead_doc_low = lead_doc.astype(jnp.bfloat16)
    bit_count = group_span.bit_length() - 1
    key_total = group_span * seg_count
    own_slot = rank_full % group_span * seg_count + jnp.arange(seg_count)
    query_shape = (1, seg_count) + head_shape
    key_shape = (1, key_total) + head_shape

    def cls_attend(queries, keys_in, values):
        paired = jnp.concatenate([keys_in, values], axis=1)
        labels = lead_labels
        for bit_level in range(bit_count):
            other_pair, other_labels = swapped((paired, labels), "fsdp", bit_level)
            upper_half = rank_full // (1 << bit_level) % 2 == 1
            paired = jnp.where(
                upper_half,
                jnp.concatenate([other_pair, paired]),
                jnp.concatenate([paired, other_pair]),
            )
            labels = jnp.where(
                upper_half,
                jnp.concatenate([other_labels, labels]),
                jnp.concatenate([labels, other_labels]),
            )
        allowed = (labels[None, :] == lead_doc_low[:, None]) | (
            jnp.arange(key_total)[None, :] == own_slot[:, None]
        )
        allowed = allowed[None, None]
        mixed_rows, log_total = attention_forward(
            queries.reshape(query_shape),
            paired[:, :model_width].reshape(key_shape),
            paired[:, model_width:].reshape(key_shape),
            allowed,
            score_scale,
        )
        return (mixed_rows.reshape(seg_count, model_width), (paired, allowed, log_total))

    def cls_attend_back(queries, keys_in, values, attend_kept, grad_mixed):
        paired, allowed, log_total = attend_kept
        grad_query, grad_key, grad_value = attention_backward(
            queries.reshape(query_shape),
            paired[:, :model_width].reshape(key_shape),
            paired[:, model_width:].reshape(key_shape),
            allowed,
            score_scale,
            log_total,
            grad_mixed.reshape(query_shape),
        )
        grad_pair = jnp.concatenate(
            [grad_key.reshape(key_total, model_width), grad_value.reshape(key_total, model_width)],
            axis=1,
        )
        for bit_level in reversed(range(bit_count)):
            half_rows = grad_pair.shape[0] // 2
            upper_half = rank_full // (1 << bit_level) % 2 == 1
            kept_half = jnp.where(upper_half, grad_pair[half_rows:], grad_pair[:half_rows])
            sent_half = jnp.where(upper_half, grad_pair[:half_rows], grad_pair[half_rows:])
            grad_pair = kept_half + swapped(
                sent_half.astype(jnp.bfloat16), "fsdp", bit_level
            ).astype(sent_half.dtype)
        grad_pair = grad_pair.astype(jnp.bfloat16)
        return (
            grad_query.reshape(seg_count, model_width).astype(jnp.bfloat16),
            grad_pair[:, :model_width],
            grad_pair[:, model_width:],
        )

    top_out, cls_saved = block_forward(heads_in, cls_unpacked, cls_attend)
    combined = jnp.concatenate([top_out[:, None, :], first_grid[:, 1:, :]], axis=1).reshape(
        tok_rows, model_width
    )
    output_rows = combined * live_rows[:, None]
    diff_rows = (output_rows - targets.astype(jnp.float32)) * live_rows[:, None]
    count_all, square_all = lax.psum(
        (jnp.sum(live_rows), jnp.sum(diff_rows * diff_rows)), ("rep", "fsdp")
    )
    loss_value = square_all / (count_all * model_width)
    slots_all = tok_rows * lax.axis_size("rep") * lax.axis_size("fsdp")
    grad_grid = (diff_rows * (slots_all / count_all)).reshape(seg_count, seg_len, model_width)
    cls_back = unpack_weights(
        (
            lax.all_gather(cls_mats, "fsdp", axis=0, tiled=True),
            lax.all_gather(cls_vecs, "fsdp", axis=0, tiled=True),
        ),
        model_width,
        ff_width,
    )
    heads_grad, cls_weight_rows, cls_g_vec = block_backward(
        grad_grid[:, 0, :], cls_back, cls_saved, cls_attend_back
    )
    cls_g_qkv, cls_g_out, cls_g_up, cls_g_down = weight_products(cls_weight_rows)
    pos_local = jnp.sum(position_hot[:, :, None] * heads_grad[:, None, :], axis=0)
    seg_grad_out = jnp.concatenate([heads_grad[:, None, :], grad_grid[:, 1:, :]], axis=1).reshape(
        tok_rows, model_width
    )
    seg_back = unpack_weights(
        (
            lax.all_gather(seg_mats, "fsdp", axis=0, tiled=True),
            lax.all_gather(seg_vecs, "fsdp", axis=0, tiled=True),
        ),
        model_width,
        ff_width,
    )
    input_grad, seg_weight_rows, seg_g_vec = block_backward(
        seg_grad_out, seg_back, seg_saved, seg_attend_back
    )
    seg_g_qkv, seg_g_out, seg_g_up, seg_g_down = weight_products(seg_weight_rows)
    owner_rows = tuple(
        (
            lax.psum_scatter(seg_g_qkv, "fsdp", scatter_dimension=0, tiled=True),
            lax.psum_scatter(seg_g_out, "fsdp", scatter_dimension=0, tiled=True),
            lax.psum_scatter(seg_g_up, "fsdp", scatter_dimension=0, tiled=True),
            lax.psum_scatter(seg_g_down, "fsdp", scatter_dimension=0, tiled=True),
            lax.psum_scatter(seg_g_vec, "fsdp", scatter_dimension=0, tiled=True),
            lax.psum_scatter(cls_g_qkv, "fsdp", scatter_dimension=0, tiled=True),
            lax.psum_scatter(cls_g_out, "fsdp", scatter_dimension=0, tiled=True),
            lax.psum_scatter(cls_g_up, "fsdp", scatter_dimension=0, tiled=True),
            lax.psum_scatter(cls_g_down, "fsdp", scatter_dimension=0, tiled=True),
            lax.psum_scatter(cls_g_vec, "fsdp", scatter_dimension=0, tiled=True),
        )
    )
    replica_share = (
        lax.psum_scatter(
            owner_rows[0].astype(jnp.bfloat16), "rep", scatter_dimension=1, tiled=True
        ).astype(jnp.float32),
        lax.psum_scatter(
            owner_rows[1].astype(jnp.bfloat16), "rep", scatter_dimension=1, tiled=True
        ).astype(jnp.float32),
        lax.psum_scatter(
            owner_rows[2].astype(jnp.bfloat16), "rep", scatter_dimension=1, tiled=True
        ).astype(jnp.float32),
        lax.psum_scatter(
            owner_rows[3].astype(jnp.bfloat16), "rep", scatter_dimension=1, tiled=True
        ).astype(jnp.float32),
        lax.psum_scatter(
            owner_rows[4].astype(jnp.bfloat16), "rep", scatter_dimension=0, tiled=True
        ).astype(jnp.float32),
        lax.psum_scatter(
            owner_rows[5].astype(jnp.bfloat16), "rep", scatter_dimension=1, tiled=True
        ).astype(jnp.float32),
        lax.psum_scatter(
            owner_rows[6].astype(jnp.bfloat16), "rep", scatter_dimension=1, tiled=True
        ).astype(jnp.float32),
        lax.psum_scatter(
            owner_rows[7].astype(jnp.bfloat16), "rep", scatter_dimension=1, tiled=True
        ).astype(jnp.float32),
        lax.psum_scatter(
            owner_rows[8].astype(jnp.bfloat16), "rep", scatter_dimension=1, tiled=True
        ).astype(jnp.float32),
        lax.psum_scatter(
            owner_rows[9].astype(jnp.bfloat16), "rep", scatter_dimension=0, tiled=True
        ).astype(jnp.float32),
    )
    all_summed = (
        lax.all_gather(replica_share[0].astype(jnp.bfloat16), "rep", axis=1, tiled=True).astype(
            jnp.float32
        ),
        lax.all_gather(replica_share[1].astype(jnp.bfloat16), "rep", axis=1, tiled=True).astype(
            jnp.float32
        ),
        lax.all_gather(replica_share[2].astype(jnp.bfloat16), "rep", axis=1, tiled=True).astype(
            jnp.float32
        ),
        lax.all_gather(replica_share[3].astype(jnp.bfloat16), "rep", axis=1, tiled=True).astype(
            jnp.float32
        ),
        lax.all_gather(replica_share[4].astype(jnp.bfloat16), "rep", axis=0, tiled=True).astype(
            jnp.float32
        ),
        lax.all_gather(replica_share[5].astype(jnp.bfloat16), "rep", axis=1, tiled=True).astype(
            jnp.float32
        ),
        lax.all_gather(replica_share[6].astype(jnp.bfloat16), "rep", axis=1, tiled=True).astype(
            jnp.float32
        ),
        lax.all_gather(replica_share[7].astype(jnp.bfloat16), "rep", axis=1, tiled=True).astype(
            jnp.float32
        ),
        lax.all_gather(replica_share[8].astype(jnp.bfloat16), "rep", axis=1, tiled=True).astype(
            jnp.float32
        ),
        lax.all_gather(replica_share[9].astype(jnp.bfloat16), "rep", axis=0, tiled=True).astype(
            jnp.float32
        ),
    )
    seg_summed = all_summed[:5]
    cls_summed = all_summed[5:]
    pos_total = lax.psum(pos_local, ("rep", "fsdp"))
    seg_mat_grad = jnp.concatenate(
        [seg_summed[0], seg_summed[1], seg_summed[2], seg_summed[3]], axis=1
    )
    cls_mat_grad = jnp.concatenate(
        [cls_summed[0], cls_summed[1], cls_summed[2], cls_summed[3]], axis=1
    )
    return (
        output_rows.astype(jnp.bfloat16),
        input_grad.astype(jnp.bfloat16),
        seg_mat_grad,
        seg_summed[4],
        cls_mat_grad,
        cls_summed[4],
        pos_total,
        loss_value,
    )


LINE = 4
PLANE = 4
CORES = 2
LANES = 128
GROUP = LINE * PLANE
LOW, WIDE = jnp.bfloat16, jnp.float32
MODEL = HEADS * HEAD_DIM
SPAN = 2 * LANES
TILE_START = (0, 1, 3, 4)


def line_pairs(apart):
    return [(source, (source + apart * PLANE) % GROUP) for source in range(GROUP)]


def plane_pairs(mask):
    return [(source, source ^ mask) for source in range(GROUP)]


def along_line(value, apart):
    return lax.ppermute(value, "fsdp", line_pairs(apart))


def in_plane(value, mask):
    return lax.ppermute(value, "fsdp", plane_pairs(mask))


def other_core(value):
    return lax.ppermute(value, "rep", [(0, 1), (1, 0)])


def after(value, *events):
    return lax.optimization_barrier((value,) + events)[0]


def together(*values):
    return tuple(lax.optimization_barrier(values))


def shape_of(dims, dtype=WIDE):
    return jax.ShapeDtypeStruct(dims, dtype)


def run_kernel(body, name, outs, where, blocks, arrays, scratch=(), far=(), flops=0):
    in_specs = [pl.BlockSpec(memory_space=pltpu.SMEM)]
    in_specs += [pl.BlockSpec(memory_space=pltpu.HBM)] * len(blocks)
    in_specs += [pl.BlockSpec(memory_space=pltpu.VMEM)] * len(arrays)
    spaces = [pltpu.HBM if at in far else pltpu.VMEM for at in range(len(outs))]
    moved = sum(x.size * x.dtype.itemsize for x in list(blocks) + list(arrays))
    moved += sum(math.prod(o.shape) * jnp.dtype(o.dtype).itemsize for o in outs)
    return pl.pallas_call(
        body,
        name=name,
        out_shape=tuple(outs),
        in_specs=in_specs,
        out_specs=tuple(pl.BlockSpec(memory_space=space) for space in spaces),
        scratch_shapes=list(scratch),
        cost_estimate=pl.CostEstimate(flops=flops, bytes_accessed=moved, transcendentals=0),
        compiler_params=pltpu.CompilerParams(vmem_limit_bytes=VMEM_BYTES),
    )(where, *blocks, *arrays)


VMEM_BYTES = 24 * 1024 * 1024
HALF = MODEL // CORES
FF_HALF = FF // CORES
OWN = MODEL // GROUP
QUARTER = 3 * SPAN + 2 * FF // LINE
QUARTER_HALF = QUARTER // CORES


def aligned(start):
    return pl.multiple_of(start, LANES)


def wait_all(copies):
    for copy in copies:
        copy.wait()


def run_copies(pairs, sems):
    copies = [
        pltpu.make_async_copy(source, target, sems.at[at])
        for at, (source, target) in enumerate(pairs)
    ]
    for copy in copies:
        copy.start()
    wait_all(copies)


FIRST = 4 * HALF + LANES
OWN_CUT = FIRST + FF_HALF // 2
LINE_CUTS = (7 * LANES, FF_HALF // 2, FF_HALF // 2)
WIDTHS = (FIRST, FF_HALF, FF_HALF)


def group_pieces(group, refs):
    own, rest = refs[:LINE], refs[LINE:]
    own_x, own_y, far_x, far_y, line_x, line_y, late_x, late_y = rest
    width, cut = WIDTHS[group], LINE_CUTS[group]
    start = sum(WIDTHS[:group])
    if group == 0:
        bases = (sum(WIDTHS) - OWN_CUT, OWN_CUT)
    else:
        before, before_cut = WIDTHS[group - 1], LINE_CUTS[group - 1]
        bases = (2 * before - before_cut, before + before_cut)
    pieces = {(0, step): [(own[step], 0, 0, width)] for step in range(LINE)}
    for mask, whole, line, base in ((1, own_x, line_x, bases[0]), (2, own_y, line_y, bases[1])):
        pieces[mask, 0] = [(whole, start, 0, width)]
        for step in range(1, LINE):
            pieces[mask, step] = [(line, base + (step - 1) * width, 0, width)]
    middle = min(max(OWN_CUT - start, 0), width)
    far = []
    if middle > 0:
        far.append((far_y, start, 0, middle))
    if middle < width:
        far.append((far_x, start + middle - OWN_CUT, middle, width))
    pieces[3, 0] = far
    pieces[3, 1] = [(late_y, 0, 0, width)]
    pieces[3, 2] = [(late_y, width, 0, cut), (late_x, 0, cut, width)]
    pieces[3, 3] = [(late_x, width - cut, 0, width)]
    return pieces


def gather_group(where, group, refs, targets):
    line_at, plane_at = where[0], where[1]
    for (mask, step), parts in group_pieces(group, refs).items():
        chip = (line_at + LINE - step) % LINE * PLANE + (plane_at ^ mask)
        for whole, first, last in targets:
            for ref, offset, begin, end in parts:
                low, high = max(first, begin), min(last, end)
                if low < high:
                    source = slice(offset + low - begin, offset + high - begin)
                    whole[chip, :, low - first : high - first] = ref[:, source]


def gather_blocks(where, refs, base, width, targets):
    line_at, plane_at = where[0], where[1]
    half = LINE // 2
    for mask in range(PLANE):
        for step in range(LINE):
            if mask == 0:
                ref, offset = refs[step], 0
            elif mask == 3:
                ref = refs[LINE + 3] if step < half else refs[LINE + 2]
                offset = step % half * width
            else:
                ref, offset = refs[LINE + mask - 1], base + step * width
            chip = (line_at + LINE - step) % LINE * PLANE + (plane_at ^ mask)
            for whole, first, last in targets:
                whole[chip] = ref[:, offset + first : offset + last]


def whole_rows(ref):
    value = ref[...]
    return value.reshape(value.shape[0] * value.shape[1], value.shape[2])


def prepare_first_kernel(where, seg, seg_vec, cls_vec, flags, out, live_out, sems):
    core_at = where[2]
    pairs = []
    for piece in range(4):
        source = seg.at[:, pl.ds(aligned(piece * MODEL + core_at * HALF), HALF)]
        pairs.append((source, out.at[:, piece * HALF : (piece + 1) * HALF]))
    run_copies(pairs, sems)
    size = seg_vec.shape[0]
    vecs = [vec[...].astype(WIDE).reshape(1, size) for vec in (seg_vec, cls_vec)]
    lines = -(-size // LANES)
    block = jnp.zeros((OWN, LANES), WIDE)
    row_at = lax.broadcasted_iota(jnp.int32, (OWN, LANES), 0)
    for which in range(2):
        for line in range(lines):
            width = min(LANES, size - line * LANES)
            value = vecs[which][:, line * LANES : line * LANES + width]
            if width < LANES:
                value = jnp.concatenate([value, jnp.zeros((1, LANES - width), WIDE)], axis=1)
            block = jnp.where(row_at == which * lines + line, value, block)
    live = flags[...].astype(WIDE).reshape(1, SEG)
    live_out[...] = live
    count = jnp.sum(live, axis=1, keepdims=True)
    block = jnp.where(row_at == 2 * lines, count, block)
    out[:, 4 * HALF :] = block.astype(LOW)


def prepare_rest_kernel(where, seg, cls, *refs):
    second_out, third_out = refs[:2]
    step_outs, out_half, order_out = refs[2 : 2 + LINE], refs[2 + LINE], refs[3 + LINE]
    quarters, sems = refs[4 + LINE :]
    line_at, plane_at, core_at = where[0], where[1], where[2]
    start = core_at * FF_HALF
    pairs = [
        (seg.at[:, pl.ds(aligned(4 * MODEL + start), FF_HALF)], second_out),
        (seg.at[:, pl.ds(aligned(4 * MODEL + FF + start), FF_HALF)], third_out),
        (cls.at[:, pl.ds(aligned(3 * MODEL + core_at * HALF), HALF)], out_half),
    ]
    part = FF // LINE
    for at in range(LINE):
        first = TILE_START[at] * LANES
        plan = [(piece * MODEL + first, SPAN, piece * SPAN) for piece in range(3)]
        plan += [
            (4 * MODEL + piece * FF + at * part, part, 3 * SPAN + piece * part)
            for piece in range(2)
        ]
        for source, size, target in plan:
            pairs.append(
                (
                    cls.at[:, source : source + size],
                    quarters.at[at, :, target : target + size],
                )
            )
    run_copies(pairs, sems)
    lanes = pl.ds(aligned(core_at * QUARTER_HALF), QUARTER_HALF)
    for step, out in enumerate(step_outs):
        out[...] = quarters[(line_at + step) % LINE, :, lanes]
    column = lax.broadcasted_iota(jnp.int32, (1, SPAN), 1)
    feature = lax.broadcasted_iota(jnp.int32, (MODEL, SPAN), 0)
    turn = sum((column >= OWN * step).astype(jnp.int32) for step in range(1, LINE))
    held = column - OWN * turn
    turn = (line_at + turn) % LINE
    for mask in range(PLANE):
        source = (turn * PLANE + (plane_at ^ mask)) * OWN + held
        source = jnp.where(column < OWN * LINE, source, -1)
        order_out[:, mask * SPAN : (mask + 1) * SPAN] = (feature == source).astype(LOW)


def prepare_kernel(where, seg, cls, *refs):
    (seg_vec, cls_vec, flags, first_out, live_out), refs = refs[:5], refs[5:]
    rest, (first_sems, quarters, sems) = refs[:-3], refs[-3:]
    prepare_first_kernel(where, seg, seg_vec, cls_vec, flags, first_out, live_out, first_sems)
    prepare_rest_kernel(where, seg, cls, *rest, quarters, sems)


def lane_mask(rows, head):
    lane = lax.broadcasted_iota(jnp.int32, (rows, LANES), 1)
    return (lane < HEAD_DIM) if head == 0 else (lane >= HEAD_DIM)


def masked(value, mask):
    return jnp.where(mask, value, jnp.zeros_like(value))


def head_probabilities(query, key, allowed):
    scores = product_right(query, key) * HEAD_DIM ** (-0.5)
    scores = jnp.where(allowed, scores, MASK_FILL)
    raised = jnp.exp(scores - jnp.max(scores, axis=-1, keepdims=True))
    return raised / jnp.sum(raised, axis=-1, keepdims=True)


def attend_tiles(qkv, width, allowed):
    rows = qkv.shape[0]
    mixed = []
    for tile in range(width // LANES):
        at = tile * LANES
        query, key, value = (
            qkv[:, piece * width + at : piece * width + at + LANES] for piece in range(3)
        )
        total = jnp.zeros((rows, LANES), WIDE)
        for head in range(2):
            mask = lane_mask(rows, head)
            weights = head_probabilities(masked(query, mask), key, allowed).astype(LOW)
            total = total + product_plain(weights, masked(value, mask))
        mixed.append(total.astype(LOW))
    return mixed


def attend_tiles_back(qkv, grad_mixed, width, allowed):
    rows = qkv.shape[0]
    scale = HEAD_DIM ** (-0.5)
    results = ([], [], [])
    for tile in range(width // LANES):
        at = tile * LANES
        query, key, value = (
            qkv[:, piece * width + at : piece * width + at + LANES] for piece in range(3)
        )
        grad = grad_mixed[:, at : at + LANES]
        totals = [jnp.zeros((rows, LANES), WIDE) for _ in range(3)]
        for head in range(2):
            mask = lane_mask(rows, head)
            query_low, key_low, grad_low = (masked(x, mask) for x in (query, key, grad))
            chance = head_probabilities(query_low, key, allowed)
            grad_chance = product_right(grad_low, value)
            inner = jnp.sum(grad_chance * chance, axis=-1, keepdims=True)
            grad_scores = (chance * (grad_chance - inner)).astype(LOW)
            totals[0] = totals[0] + product_plain(grad_scores, key_low)
            totals[1] = totals[1] + product_left(grad_scores, query_low)
            totals[2] = totals[2] + product_left(chance.astype(LOW), grad_low)
        results[0].append((totals[0] * scale).astype(LOW))
        results[1].append((totals[1] * scale).astype(LOW))
        results[2].append(totals[2].astype(LOW))
    return results[0] + results[1] + results[2]


def token_allowed(live_row):
    shape = (SEG, SEG)
    same = lax.broadcasted_iota(jnp.int32, shape, 0) == lax.broadcasted_iota(jnp.int32, shape, 1)
    return (live_row > 0.5) | same


def qkv_kernel(where, *refs):
    blocks = refs[:12]
    hidden, hidden_got, live_row, live_got, order = refs[12:17]
    weight, out_low, out_high, qkv_out, mixed_out = refs[17:22]
    vectors_out, count_out, ordered_out = refs[22:25]
    vec_rows, flat, inputs, out_half = refs[25:]
    core_at = where[2]
    gather_group(
        where,
        0,
        blocks,
        (
            (weight, 0, 3 * HALF),
            (out_half, 3 * HALF, 4 * HALF),
            (vec_rows, 4 * HALF, 4 * HALF + LANES),
        ),
    )
    out_low[...] = out_half[: GROUP // 2]
    out_high[...] = out_half[GROUP // 2 :]
    piece = (8 * MODEL + FF) // GROUP
    lines = -(-piece // LANES)
    count = jnp.zeros((1, LANES), WIDE)
    for chip in range(GROUP):
        rows = vec_rows[chip, 0:16, :].astype(WIDE)
        for block in range(2):
            joined = jnp.concatenate(
                [rows[block * lines + r : block * lines + r + 1] for r in range(lines)], axis=1
            )
            flat[block : block + 1, chip * piece : (chip + 1) * piece] = joined[:, :piece]
        count = count + rows[2 * lines : 2 * lines + 1]
    rows_each = (8 * MODEL + FF) // MODEL
    for block in range(2):
        for row in range(rows_each):
            vectors_out[block * rows_each + row : block * rows_each + row + 1, :] = flat[
                block : block + 1, row * MODEL : (row + 1) * MODEL
            ]
    count_out[...] = jnp.broadcast_to(count, count_out.shape)
    inputs[:SEG] = hidden[...]
    inputs[SEG:] = hidden_got[...]
    projected = product_plain(inputs[...], whole_rows(weight))
    lanes = pl.ds(aligned(core_at * HALF), HALF)
    qkv_out[:, :HALF] = (projected[:, :HALF] + vectors_out[0:1, lanes]).astype(LOW)
    qkv_out[:, HALF : 2 * HALF] = projected[:, HALF : 2 * HALF].astype(LOW)
    qkv_out[:, 2 * HALF :] = (projected[:, 2 * HALF :] + vectors_out[1:2, lanes]).astype(LOW)
    for part, live in enumerate((live_row, live_got)):
        rows = slice(part * SEG, (part + 1) * SEG)
        tiles = attend_tiles(qkv_out[rows, :], HALF, token_allowed(live[...]))
        for tile, value in enumerate(tiles):
            mixed_out[rows, tile * LANES : (tile + 1) * LANES] = value
    ordered_out[...] = product_plain(inputs[...], order[...]).astype(LOW)


def norm_rows(summed):
    row_mean = jnp.mean(summed, axis=-1, keepdims=True)
    centered = summed - row_mean
    inv_dev = lax.rsqrt(jnp.mean(centered * centered, axis=-1, keepdims=True) + NORM_EPS)
    return centered * inv_dev, inv_dev


def norm_rows_back(grad_out, normed, inv_dev, gain):
    scaled = grad_out * gain
    mean_one = jnp.mean(scaled, axis=-1, keepdims=True)
    mean_two = jnp.mean(scaled * normed, axis=-1, keepdims=True)
    return inv_dev * (scaled - mean_one - normed * mean_two)


def column_sum(value):
    return jnp.sum(value.astype(WIDE), axis=0, keepdims=True)


def four_rows(vectors, first):
    return jnp.concatenate([vectors[first + at : first + at + 1, :] for at in range(4)], axis=1)


def gelu_both(before):
    half = 0.5 * (1.0 + lax.erf(before * SQRT_HALF))
    slope = half + before * jnp.exp(-0.5 * before * before) * INV_SQRT_TWO_PI
    return before * half, slope


def out_kernel(where, hidden, mixed, mixed_got, low, high, low_got, high_got, *refs):
    vectors, order, full_out, ordered_out, normed_out, inv_out, low_out, mixed_full = refs
    core_at = where[2]
    own, other = aligned(core_at * HALF), aligned((1 - core_at) * HALF)
    rows = MODEL // 2
    full_out[:rows, pl.ds(own, HALF)] = whole_rows(low)
    full_out[rows:, pl.ds(own, HALF)] = whole_rows(high)
    full_out[:rows, pl.ds(other, HALF)] = whole_rows(low_got)
    full_out[rows:, pl.ds(other, HALF)] = whole_rows(high_got)
    mixed_full[:, pl.ds(own, HALF)] = mixed[...]
    mixed_full[:SEG, pl.ds(other, HALF)] = mixed_got[SEG:, :]
    mixed_full[SEG:, pl.ds(other, HALF)] = mixed_got[:SEG, :]
    branch = product_plain(mixed_full[:SEG, :], full_out[...])
    normed, inv_dev = norm_rows(hidden[...].astype(WIDE) + branch + vectors[2:3, :])
    normed_out[...] = normed
    inv_out[...] = inv_dev
    low_out[...] = (normed * vectors[4:5, :] + vectors[5:6, :]).astype(LOW)
    ordered_out[...] = product_plain(mixed_full[...], order[...]).astype(LOW)


def up_kernel(where, *refs):
    blocks = refs[:12]
    low, low_got, vectors = refs[12:15]
    weight, act_out, slope_out, both = refs[15:]
    core_at = where[2]
    gather_group(where, 1, blocks, ((weight, 0, FF_HALF),))
    both[:SEG] = low[...]
    both[SEG:] = low_got[...]
    for at in range(FF_HALF // MODEL):
        columns = slice(at * MODEL, (at + 1) * MODEL)
        held = weight[:, :, columns]
        before = product_plain(both[...], held.reshape(MODEL, MODEL))
        bias = vectors[pl.ds(8 + core_at * (FF_HALF // MODEL) + at, 1), :]
        value, slope = gelu_both(before + bias)
        act_out[:, columns] = value.astype(LOW)
        slope_out[:, columns] = slope


def down_kernel(where, *refs):
    blocks, act = refs[:12], refs[12]
    weight, own_out, send_out = refs[13:]
    gather_group(where, 2, blocks, ((weight, 0, FF_HALF),))
    partial = product_right(act[...], whole_rows(weight))
    own_out[...] = partial[:SEG]
    send_out[...] = partial[SEG:]


def seg_rows_kernel(where, *refs):
    own, got, normed_first, vectors, targets, live, seg_pos = refs[:7]
    normed_out, inv_out, diff_out, rows_out, head_out = refs[7:]
    doc, number = where[3], where[4]
    first = normed_first[...] * vectors[4:5, :] + vectors[5:6, :]
    normed, inv_dev = norm_rows(first + own[...] + got[...] + vectors[3:4, :])
    normed_out[...] = normed
    inv_out[...] = inv_dev
    rows = normed * vectors[6:7, :] + vectors[7:8, :]
    shape = (SEG, SEG)
    same = lax.broadcasted_iota(jnp.int32, shape, 0) == lax.broadcasted_iota(jnp.int32, shape, 1)
    live_rows = jnp.sum(jnp.where(same, live[...], 0.0), axis=1, keepdims=True)
    target_rows = targets[...].astype(WIDE)
    output = rows * live_rows
    rows_out[...] = output
    diff = (output - target_rows) * live_rows
    row_at = lax.broadcasted_iota(jnp.int32, (SEG, 1), 0)
    diff = jnp.where(row_at > 0, diff, 0.0)
    diff_out[...] = diff
    table = seg_pos[...].astype(WIDE)
    chosen = lax.broadcasted_iota(jnp.int32, table.shape, 0) == number
    position = jnp.sum(jnp.where(chosen, table, 0.0), axis=0, keepdims=True)
    head_out[:, :MODEL] = rows[0:1, :] + position
    head_out[:, MODEL : 2 * MODEL] = target_rows[0:1, :]
    square = jnp.sum(column_sum(diff * diff), axis=1, keepdims=True)
    lane = lax.broadcasted_iota(jnp.int32, (1, LANES), 1)
    facts = jnp.where(lane == 0, live_rows[0:1, :], 0.0)
    facts = jnp.where(lane == 1, doc.astype(WIDE), facts)
    facts = jnp.where(lane == 2, number.astype(WIDE), facts)
    facts = jnp.where(lane == 3, square, facts)
    head_out[:, 2 * MODEL :] = facts


def second_norm_kernel(where, *refs):
    diff, count, normed, inv_dev, vectors, first, first_got, order = refs[:8]
    grad_out, low_out, sums_out, ordered_out, both = refs[8:]
    grad_top = diff[...] * ((SEG * GROUP * CORES) / count[0:1, 0:1])
    normed_rows = normed[...]
    grad = norm_rows_back(grad_top, normed_rows, inv_dev[...], vectors[6:7, :])
    low = grad.astype(LOW)
    grad_out[...] = grad
    low_out[...] = low
    sums_out[0:1, :] = column_sum(low)
    sums_out[1:2, :] = column_sum(grad_top * normed_rows)
    sums_out[2:3, :] = column_sum(grad_top)
    both[:SEG] = first[...]
    both[SEG:] = first_got[...]
    ordered_out[...] = product_plain(both[...], order[...]).astype(LOW)


def mlp_back_kernel(where, *refs):
    low, low_got, down_weight, up_weight, slope = refs[:5]
    pre_out, own_out, send_out, sums_out, both = refs[5:]
    both[:SEG] = low[...]
    both[SEG:] = low_got[...]
    for at in range(FF_HALF // MODEL):
        columns = slice(at * MODEL, (at + 1) * MODEL)
        held = down_weight[:, :, columns]
        before = product_plain(both[...], held.reshape(MODEL, MODEL))
        pre = (before * slope[:, columns]).astype(LOW)
        pre_out[:, columns] = pre
        sums_out[at : at + 1, :] = column_sum(pre)
    partial = product_right(pre_out[...], whole_rows(up_weight))
    own_out[...] = partial[:SEG]
    send_out[...] = partial[SEG:]


def scatter_parts(where, parts, outs, sems):
    line_at, plane_at = where[0], where[1]
    far_low, far_high, to_x, to_y, kept = outs
    half = LINE // 2
    copies = []
    for mask in range(PLANE):
        for step in range(LINE):
            source = parts.at[(line_at + step) % LINE * PLANE + (plane_at ^ mask)]
            if mask == 3:
                target = far_low.at[step] if step < half else far_high.at[step - half]
            else:
                target = (kept, to_x, to_y)[mask].at[step]
            copies.append(pltpu.make_async_copy(source, target, sems.at[len(copies)]))
    for copy in copies:
        copy.start()
    wait_all(copies)


def mlp_products(refs, masks, both, store):
    first, second, second_got, pre, act, order = refs
    both[:SEG] = second[...]
    both[SEG:] = second_got[...]
    for mask in masks:
        lanes = slice(mask * SPAN, (mask + 1) * SPAN)
        turned = product_plain(both[...], order[:, lanes]).astype(LOW)
        for at, (left, right) in enumerate(((first[:, lanes], pre), (turned, act))):
            for piece in range(FF_HALF // MODEL):
                start = piece * MODEL
                product = product_left(left, right[:, start : start + MODEL])
                product = product[: LINE * OWN].astype(LOW).reshape(LINE, OWN, MODEL)
                target = at * FF_HALF + start
                store(mask, slice(target, target + MODEL), product)


def mlp_far_kernel(where, *refs):
    low_out, high_out, both = refs[6:]
    half = LINE // 2

    def store(mask, columns, product):
        low_out[:, :, columns] = product[:half]
        high_out[:, :, columns] = product[half:]

    mlp_products(refs[:6], (3,), both, store)


def mlp_near_kernel(where, *refs):
    outs, both = refs[6:9], refs[9]

    def store(mask, columns, product):
        outs[mask - 1][:, :, columns] = product

    mlp_products(refs[:6], (1, 2, 0), both, store)


def attn_product(where, refs, mask, piece):
    hidden, mixed, proj, branch, got = refs
    lanes = slice(mask * SPAN, (mask + 1) * SPAN)
    if piece < 3:
        right = proj[:, piece * HALF : (piece + 1) * HALF]
        product = product_left(hidden[:, lanes], right)
    else:
        own = branch[:, pl.ds(aligned(where[2] * HALF), HALF)]
        product = product_left(mixed[:SEG, lanes], own)
        product = product + product_left(mixed[SEG:, lanes], got[:, HALF:])
    return product[: LINE * OWN].astype(LOW).reshape(LINE, OWN, HALF)


def attn_far_kernel(where, *refs):
    low_out, high_out = refs[5:]
    half = LINE // 2
    for piece in range(4):
        columns = slice(piece * HALF, (piece + 1) * HALF)
        product = attn_product(where, refs[:5], 3, piece)
        low_out[:, :, columns] = product[:half]
        high_out[:, :, columns] = product[half:]


def attn_near_kernel(where, *refs):
    proj, (top_row, out_rows, live_row) = refs[2], refs[5:8]
    weight, sums_first, sums_second, sums_up, head_top, head_normed, data = refs[8:15]
    x_out, y_out, kept_out, output_out, own_out, send_out, payload_out, rows = refs[15:]
    core_at = where[2]
    partial = product_right(proj[...], whole_rows(weight))
    own_out[...] = partial[:SEG]
    send_out[...] = partial[SEG:]
    row_at = lax.broadcasted_iota(jnp.int32, (SEG, 1), 0)
    output = jnp.where(row_at == 0, top_row[...] * live_row[:, 0:1], out_rows[...])
    output_out[...] = output.astype(LOW)
    for mask, out in ((1, x_out), (2, y_out), (0, kept_out)):
        for piece in range(4):
            columns = slice(piece * HALF, (piece + 1) * HALF)
            out[:, :, columns] = attn_product(where, refs[:5], mask, piece)
    lanes = pl.ds(aligned(core_at * HALF), HALF)
    rows[...] = jnp.zeros_like(rows)
    rows[0:12, :] = data[0:12, :]
    rows[12:13, lanes] = column_sum(proj[:, :HALF])
    rows[13:14, lanes] = column_sum(proj[:, 2 * HALF :])
    rows[14:15, :] = sums_first[0:1, :]
    rows[15:16, :] = sums_second[0:1, :] + data[2:3, :]
    rows[16:18, :] = sums_first[1:3, :]
    rows[18:19, :] = sums_second[1:2, :] + head_top[...] * head_normed[0:1, :]
    rows[19:20, :] = sums_second[2:3, :] + head_top[...]
    for at in range(FF_HALF // MODEL):
        total = sums_up[at : at + 1, :] + data[4 + 2 * at : 5 + 2 * at, :]
        total = total + data[5 + 2 * at : 6 + 2 * at, :]
        rows[pl.ds(20 + core_at * (FF_HALF // MODEL) + at, 1), :] = total
    payload_out[...] = rows[...].astype(LOW)


def fold_kernel(where, kept, got_x, got_y, *refs):
    extra, own_out, sent = refs[: -LINE], refs[-LINE], refs[1 - LINE :]
    rows = kept.shape[1]
    for step in range(LINE):
        total = kept[step].astype(WIDE) + got_x[step].astype(WIDE) + got_y[step].astype(WIDE)
        if step == 0:
            own_out[...] = total
            continue
        out = sent[step - 1]
        out[:rows, :] = total.astype(LOW)
        if extra:
            out[rows:, :] = jnp.zeros_like(out[rows:, :])
            out[rows:, : extra[0].shape[1]] = extra[0][...]


def reduce_far(parts):
    return together(in_plane(parts[0], 2), in_plane(parts[1], 1))


def reduce_add(where, parts, far):
    shape = parts[2].shape
    return run_kernel(
        add_far_kernel,
        "add_far",
        [shape_of(shape, LOW)] * 2,
        where,
        (),
        tuple(far) + (parts[2], parts[3]),
    )


def reduce_fold(where, kept, got, *extra):
    _, rows, columns = kept.shape
    more = sum(value.shape[0] for value in extra)
    return run_kernel(
        fold_kernel,
        "fold",
        [shape_of((rows, columns))] + [shape_of((rows + more, columns), LOW)] * (LINE - 1),
        where,
        (),
        (kept,) + tuple(got) + extra,
    )


def reduce_line(own, pieces):
    total = own
    for piece in pieces:
        total = total + piece[: own.shape[0]].astype(WIDE)
    return total


def head_back_kernel(where, *refs):
    grad, grad_got, down_weight, up_weight, slope, act, low, low_got = refs[:8]
    own_out, send_out, data_out = refs[8:]
    few = 16
    row_at = lax.broadcasted_iota(jnp.int32, (few, 1), 0)

    def two_rows(first, second):
        return jnp.where(row_at == 0, first, jnp.where(row_at == 1, second, 0.0))

    second = two_rows(grad[...], grad_got[...]).astype(LOW)
    data_out[0:1, :] = low[0:1, :].astype(WIDE)
    data_out[1:2, :] = low_got[0:1, :].astype(WIDE)
    data_out[2:4, :] = second[0:2].astype(WIDE)
    partial = jnp.zeros((few, MODEL), WIDE)
    for at in range(FF_HALF // MODEL):
        columns = slice(at * MODEL, (at + 1) * MODEL)
        before = product_plain(second, down_weight[:, :, columns].reshape(MODEL, MODEL))
        slopes = two_rows(slope[0:1, columns], slope[SEG : SEG + 1, columns])
        pre = (before * slopes).astype(LOW)
        partial = partial + product_right(pre, up_weight[:, :, columns].reshape(MODEL, MODEL))
        data_out[4 + 2 * at : 6 + 2 * at, :] = pre[0:2].astype(WIDE)
        data_out[8 + 2 * at : 9 + 2 * at, :] = act[0:1, columns].astype(WIDE)
        data_out[9 + 2 * at : 10 + 2 * at, :] = act[SEG : SEG + 1, columns].astype(WIDE)
    own_out[...] = partial[0:1]
    send_out[...] = partial[1:2]


def first_norm_kernel(where, *refs):
    second_grad, own, got, head_grad, head_own, head_got = refs[:6]
    normed_rows, inv_dev, vectors, out_weight = refs[6:10]
    grad_out, branch_out, mixed_out, send_out, sums_out = refs[10:]
    core_at = where[2]
    grad_rows = second_grad[...] + own[...] + got[...]
    head = head_grad[...] + head_own[...] + head_got[...]
    row_at = lax.broadcasted_iota(jnp.int32, (SEG, 1), 0)
    grad_rows = jnp.where(row_at == 0, head, grad_rows)
    normed = normed_rows[...]
    grad = norm_rows_back(grad_rows, normed, inv_dev[...], vectors[4:5, :])
    grad_out[...] = grad
    branch = grad.astype(LOW)
    branch_out[...] = branch
    mixed_out[...] = product_right(branch, out_weight[...]).astype(LOW)
    other = pl.ds(aligned((1 - core_at) * HALF), HALF)
    send_out[:, :HALF] = mixed_out[:, other]
    send_out[:, HALF:] = branch_out[:, other]
    sums_out[0:1, :] = column_sum(branch)
    sums_out[1:2, :] = column_sum(grad_rows * normed)
    sums_out[2:3, :] = column_sum(grad_rows)


def attn_back_kernel(where, *refs):
    qkv, mixed_grad, got, live_row, live_got, proj_out = refs
    core_at = where[2]
    lanes = pl.ds(aligned(core_at * HALF), HALF)
    for part, live in enumerate((live_row, live_got)):
        at = slice(part * SEG, (part + 1) * SEG)
        grad = mixed_grad[:, lanes] if part == 0 else got[:, :HALF]
        pieces = attend_tiles_back(qkv[at, :], grad, HALF, token_allowed(live[...]))
        for tile, value in enumerate(pieces):
            proj_out[at, tile * LANES : (tile + 1) * LANES] = value


def cls_gather_kernel(where, *refs):
    blocks = refs[:8]
    own_out, from_x, from_y, far_x = refs[8], refs[4], refs[5], refs[6]
    weight_out, out_rows = refs[9:]
    plane_at = where[1]
    gather_blocks(where, blocks, 0, QUARTER_HALF, ((weight_out, 0, QUARTER_HALF),))
    first = LINE * QUARTER_HALF
    out_rows[plane_at] = own_out[...]
    out_rows[plane_at ^ 1] = from_x[:, first : first + HALF]
    out_rows[plane_at ^ 2] = from_y[:, first : first + HALF]
    first = LINE // 2 * QUARTER_HALF
    out_rows[plane_at ^ 3] = far_x[:, first : first + HALF]


def cls_weight_kernel(where, own, got, out_half, out_got, weight_out, out_full):
    line_at, core_at = where[0], where[2]
    out_full[...] = jnp.zeros_like(out_full)
    for value, part, core in ((own, out_half, core_at), (got, out_got, 1 - core_at)):
        weight_out[:, :, pl.ds(aligned(core * QUARTER_HALF), QUARTER_HALF)] = value[...]
        rows = part[...].reshape(3, HEAD_DIM, HALF)
        out_full[pl.ds(line_at % 2, 3), :, pl.ds(aligned(core * HALF), HALF)] = rows


def add_far_kernel(where, far_low, far_high, to_x, to_y, x_out, y_out):
    half = LINE // 2
    x_out[:half] = to_x[:half] + far_low[...]
    x_out[half:] = to_x[half:]
    y_out[:half] = to_y[:half]
    y_out[half:] = to_y[half:] + far_high[...]


def row_from_column(column, size):
    shape = (size, size)
    same = lax.broadcasted_iota(jnp.int32, shape, 0) == lax.broadcasted_iota(jnp.int32, shape, 1)
    return jnp.sum(jnp.where(same, column, 0.0), axis=0, keepdims=True)


def head_allowed(heads):
    facts = heads[:, 2 * MODEL :]
    live, doc = facts[:, 0:1], facts[:, 1:2]
    shape = (GROUP, GROUP)
    same = lax.broadcasted_iota(jnp.int32, shape, 0) == lax.broadcasted_iota(jnp.int32, shape, 1)
    live_row, doc_row = row_from_column(live, GROUP), row_from_column(doc, GROUP)
    return ((live_row > 0.5) & (doc == doc_row)) | same


def quarter_mask(quarter):
    lane = lax.broadcasted_iota(jnp.int32, (GROUP, SPAN), 1)
    first = (quarter % 2) * HEAD_DIM
    return (lane >= first) & (lane < first + 3 * HEAD_DIM)


def quarter_piece(vectors, row, quarter):
    value = jnp.zeros((1, SPAN), WIDE)
    for at in range(LINE):
        first = TILE_START[at] * LANES
        value = jnp.where(quarter == at, vectors[row : row + 1, first : first + SPAN], value)
    return value


def cls_attend_kernel(where, *refs):
    stacks, vectors, weight, out_weight = refs[:4], refs[4], refs[5], refs[6]
    heads_out, qkv_out, mixed_out, part_out = refs[7:]
    line_at, plane_at = where[0], where[1]
    for step, stack in enumerate(stacks):
        for mask in range(PLANE):
            row = (line_at + LINE - step) % LINE * PLANE + (plane_at ^ mask)
            heads_out[pl.ds(row, 1), :] = stack[mask : mask + 1, :]
    heads = heads_out[...]
    inputs = heads[:, :MODEL].astype(LOW)
    projected = product_plain(inputs, weight[:, : 3 * SPAN])
    query = projected[:, :SPAN] + quarter_piece(vectors, 12, line_at)
    value = projected[:, 2 * SPAN :] + quarter_piece(vectors, 13, line_at)
    qkv_out[:, :SPAN] = query.astype(LOW)
    qkv_out[:, SPAN : 2 * SPAN] = projected[:, SPAN : 2 * SPAN].astype(LOW)
    qkv_out[:, 2 * SPAN :] = value.astype(LOW)
    mixed = attend_tiles(qkv_out[...], SPAN, head_allowed(heads))
    mixed = masked(jnp.concatenate(mixed, axis=1), quarter_mask(line_at))
    mixed_out[...] = mixed
    part_out[...] = product_plain(mixed, out_weight[...])


def cls_mlp_kernel(where, *refs):
    heads, own, got_one, got_two, got_three, vectors, weight = refs[:7]
    normed_out, inv_out, low_out, act_out, slope_out, part_out = refs[7:]
    line_at = where[0]
    branch = own[...] + got_one[...] + got_two[...] + got_three[...]
    normed, inv_dev = norm_rows(heads[:, :MODEL] + branch + vectors[14:15, :])
    normed_out[...] = normed
    inv_out[...] = inv_dev
    low = (normed * vectors[16:17, :] + vectors[17:18, :]).astype(LOW)
    low_out[...] = low
    part = FF // LINE
    first = 3 * SPAN
    bias = vectors[pl.ds(20 + line_at, 1), :]
    before = product_plain(low, weight[:, first : first + part]) + bias
    value, slope = gelu_both(before)
    act = value.astype(LOW)
    act_out[...] = act
    slope_out[...] = slope
    part_out[...] = product_right(act, weight[:, first + part :])


def cls_top_kernel(where, *refs):
    heads, own, got_one, got_two, got_three, vectors, weight = refs[:7]
    normed_first, count, slope = refs[7:10]
    top_out, square_out, grad_out, second_out, pre_out, part_out, sums_out = refs[10:17]
    held = refs[17]
    rank = where[0] * PLANE + where[1]
    first = normed_first[...] * vectors[16:17, :] + vectors[17:18, :]
    down = own[...] + got_one[...] + got_two[...] + got_three[...]
    normed, inv_dev = norm_rows(first + down + vectors[15:16, :])
    rows = normed * vectors[18:19, :] + vectors[19:20, :]
    held[...] = rows
    top_out[...] = held[pl.ds(rank, 1), :]
    facts = heads[:, 2 * MODEL :]
    live = facts[:, 0:1]
    diff = (rows * live - heads[:, MODEL : 2 * MODEL]) * live
    square = jnp.sum(column_sum(diff * diff), axis=1, keepdims=True)
    square = square + jnp.sum(facts[:, 3:4], axis=0, keepdims=True)
    square_out[...] = jnp.broadcast_to(square, square_out.shape)
    grad_top = diff * ((SEG * GROUP * CORES) / count[0:1, 0:1])
    grad = norm_rows_back(grad_top, normed, inv_dev, vectors[18:19, :])
    sums_out[0:1, :] = column_sum(grad_top * normed)
    sums_out[1:2, :] = column_sum(grad_top)
    grad_out[...] = grad
    second = grad.astype(LOW)
    second_out[...] = second
    part = FF // LINE
    at = 3 * SPAN
    pre = (product_plain(second, weight[:, at + part :]) * slope[...]).astype(LOW)
    pre_out[...] = pre
    part_out[...] = product_right(pre, weight[:, at : at + part])


def cls_attend_back_kernel(where, *refs):
    heads, own, got_one, got_two, got_three, vectors, weight, out_weight = refs[:8]
    grad_in, normed_first, inv_first, qkv = refs[8:12]
    grad_out, branch_out, proj_out, part_out, sums_out = refs[12:]
    line_at = where[0]
    grad_first = grad_in[...] + own[...] + got_one[...] + got_two[...] + got_three[...]
    normed = normed_first[...]
    grad = norm_rows_back(grad_first, normed, inv_first[...], vectors[16:17, :])
    sums_out[0:1, :] = column_sum(grad_first * normed)
    sums_out[1:2, :] = column_sum(grad_first)
    grad_out[...] = grad
    branch = grad.astype(LOW)
    branch_out[...] = branch
    mask = quarter_mask(line_at)
    mixed_grad = masked(product_right(branch, out_weight[...]).astype(LOW), mask)
    pieces = attend_tiles_back(qkv[...], mixed_grad, SPAN, head_allowed(heads[...]))
    tiles = SPAN // LANES
    for piece in range(3):
        joined = jnp.concatenate(pieces[piece * tiles : (piece + 1) * tiles], axis=1)
        proj_out[:, piece * SPAN : (piece + 1) * SPAN] = masked(joined, mask)
    part_out[...] = product_right(proj_out[...], weight[:, : 3 * SPAN])


def cls_end_kernel(where, *refs):
    heads, grad, own, got_one, got_two, got_three = refs[:6]
    square, sums_back, sums_top = refs[6:9]
    normed_second, inv_second, vectors = refs[9:12]
    row_out, second_out, shared_out, held = refs[12:]
    rank = where[0] * PLANE + where[1]
    total = grad[...] + own[...] + got_one[...] + got_two[...] + got_three[...]
    held[...] = total
    row = held[pl.ds(rank, 1), :]
    row_out[...] = row
    second_out[...] = norm_rows_back(
        row, normed_second[0:1, :], inv_second[0:1, :], vectors[6:7, :]
    )
    number = row_from_column(heads[:, 2 * MODEL + 2 : 2 * MODEL + 3], GROUP)
    entry = lax.broadcasted_iota(jnp.int32, (GROUP, GROUP), 0).astype(WIDE)
    hot = (entry == number).astype(WIDE)
    shared_out[0:GROUP, :] = jnp.dot(hot, total, precision=lax.Precision.HIGHEST)
    shared_out[GROUP : GROUP + 1, 0:LANES] = square[0:1, :]
    shared_out[GROUP + 1 : GROUP + 3, :] = sums_back[0:2, :]
    shared_out[GROUP + 3 : GROUP + 5, :] = sums_top[0:2, :]


def head_mlp_kernel(where, *refs):
    cls_mlp_kernel(where, *refs[:7], *refs[11:17])
    add_far_kernel(where, *refs[7:11], *refs[17:])


def head_end_kernel(where, *refs):
    cls_end_kernel(where, *refs[:12], *refs[16:19], refs[23])
    fold_kernel(where, *refs[12:16], *refs[19:23])


def attn_add_kernel(where, *refs):
    far_low, far_high, to_x, to_y, grad, own, got, x_out, y_out, input_out = refs
    add_far_kernel(where, far_low, far_high, to_x, to_y, x_out, y_out)
    input_out[...] = (grad[...] + own[...] + got[...]).astype(LOW)


def rows_input_kernel(where, *refs):
    cls_rows_kernel(where, *refs[:8], refs[11], refs[13])
    grad, own, got, input_out = refs[8], refs[9], refs[10], refs[12]
    input_out[...] = (grad[...] + own[...] + got[...]).astype(LOW)


def cls_rows_kernel(where, *refs):
    packs = refs[:4]
    heads, branch, low, second = refs[4:8]
    out, kept = refs[8:]
    line_at = where[0]
    rows, width = kept.shape[1:]
    for step, pack in enumerate(packs):
        first = pack.shape[0] - rows
        kept[(line_at + LINE - step) % LINE] = pack[first:, :width]
    starts = (MODEL, 2 * MODEL, 3 * MODEL, 4 * MODEL)
    out[:, 0:MODEL] = heads[:, :MODEL].astype(LOW)
    for piece, start in enumerate(starts):
        from_at = piece * SPAN
        for tile in range(MODEL // LANES):
            total = None
            for at in range(PLANE):
                inner = tile - TILE_START[at]
                if inner in (0, 1):
                    first = from_at + inner * LANES
                    value = kept[at, :, first : first + LANES]
                    total = value if total is None else total + value
            out[:, start + tile * LANES : start + (tile + 1) * LANES] = total
    out[:, 5 * MODEL : 6 * MODEL] = branch[...]
    out[:, 6 * MODEL : 7 * MODEL] = low[...]
    out[:, 7 * MODEL + FF : 8 * MODEL + FF] = second[...]
    part = FF // LINE
    for at in range(PLANE):
        first = 4 * SPAN
        out[:, 7 * MODEL + at * part : 7 * MODEL + (at + 1) * part] = kept[
            at, :, first : first + part
        ]
        out[:, 8 * MODEL + FF + at * part : 8 * MODEL + FF + (at + 1) * part] = kept[
            at, :, first + part : first + 2 * part
        ]


def own_features(rank, width):
    shape = (MODEL, width)
    feature = lax.broadcasted_iota(jnp.int32, shape, 0)
    column = lax.broadcasted_iota(jnp.int32, shape, 1)
    return (feature == rank * width + column).astype(LOW)


def own_vector(rank, pieces, out, flat):
    size = out.shape[0]
    for at, piece in enumerate(pieces):
        flat[:, at * MODEL : (at + 1) * MODEL] = piece
    value = jnp.zeros((1, size), WIDE)
    for chip in range(GROUP):
        value = jnp.where(rank == chip, flat[:, chip * size : (chip + 1) * size], value)
    out[...] = value.reshape(size)


def cls_owner_kernel(where, *refs):
    own, got, shared, mats_out, vec_out, rows, flat = refs
    rank = where[0] * PLANE + where[1]
    width = mats_out.shape[0]
    rows[:GROUP] = own[...]
    rows[GROUP:] = got[...]
    chosen = own_features(rank, width)
    plan = (
        (0, MODEL, 3 * MODEL, 0),
        (4 * MODEL, 5 * MODEL, MODEL, 3 * MODEL),
        (6 * MODEL, 7 * MODEL, FF, 4 * MODEL),
        (7 * MODEL + FF, 8 * MODEL + FF, FF, 4 * MODEL + FF),
    )
    for left, right, size, target in plan:
        side = product_plain(rows[:, left : left + MODEL], chosen).astype(LOW)
        mats_out[:, target : target + size] = product_left(side, rows[:, right : right + size])
    starts = (MODEL, 3 * MODEL, 5 * MODEL, 7 * MODEL + FF)
    pieces = [column_sum(rows[:, start : start + MODEL]) for start in starts]
    pieces += [shared[GROUP + 1 + at : GROUP + 2 + at, :] for at in range(4)]
    starts = [7 * MODEL + at * MODEL for at in range(FF // MODEL)]
    pieces += [column_sum(rows[:, start : start + MODEL]) for start in starts]
    own_vector(rank, pieces, vec_out, flat)


def head_share_kernel(where, *refs):
    packs, mlp = refs[:4], refs[4]
    mine_out, vecs_out, rows = refs[5:]
    rank = where[0] * PLANE + where[1]
    count = LINE * 24
    for at, pack in enumerate(packs):
        rows[at * count : (at + 1) * count] = pack[...]
    total = PLANE * count

    def chosen(base, apart):
        shape = (CORES * GROUP, total)
        row = lax.broadcasted_iota(jnp.int32, shape, 0)
        column = lax.broadcasted_iota(jnp.int32, shape, 1)
        hot = (column == row // 2 * 24 + base + row % 2 * apart).astype(LOW)
        return product_plain(hot, rows[...]).astype(LOW)

    own = own_features(rank, OWN)
    for at, (left, right) in enumerate(((0, 4), (2, 8))):
        side = product_plain(chosen(left, 1), own).astype(LOW)
        for piece in range(FF_HALF // MODEL):
            columns = slice(at * FF_HALF + piece * MODEL, at * FF_HALF + (piece + 1) * MODEL)
            share = product_left(side, chosen(right + 2 * piece, 1))
            mine_out[:, columns] = mlp[:, columns] + share
    shape = (16, total)
    row = lax.broadcasted_iota(jnp.int32, shape, 0)
    column = lax.broadcasted_iota(jnp.int32, shape, 1)
    hot = ((column % 24 == row + 12) & (row < 12)).astype(LOW)
    vecs_out[...] = product_plain(hot, rows[...])


def share_owner_kernel(where, *refs):
    head_share_kernel(where, *refs[:5], *refs[9:11], refs[15])
    cls_owner_kernel(where, *refs[5:8], *refs[11:13], *refs[16:])
    shared, count, pos_out, loss_out = refs[7], refs[8], refs[13], refs[14]
    pos_out[...] = shared[:GROUP, :]
    loss_out[...] = shared[GROUP : GROUP + 1, 0:1] / (count[0:1, 0:1] * MODEL)


def seg_vec_kernel(where, vecs, vecs_got, vec_out, flat):
    rank = where[0] * PLANE + where[1]
    rows = (8 * MODEL + FF) // MODEL
    pieces = [vecs[at : at + 1, :] + vecs_got[at : at + 1, :] for at in range(rows)]
    own_vector(rank, pieces, vec_out, flat)


def column_copies(where, out, base, size, own, got, first):
    core_at = where[2]
    lanes = slice(first, first + size)
    return [
        (own.at[:, lanes], out.at[:, pl.ds(aligned(base + core_at * size), size)]),
        (got.at[:, lanes], out.at[:, pl.ds(aligned(base + (1 - core_at) * size), size)]),
    ]


def store_kernel(where, attn, attn_got, mlp, mlp_got, vecs, vecs_got, out, vec_out, flat, sems):
    pairs = []
    for piece in range(4):
        pairs += column_copies(where, out, piece * MODEL, HALF, attn, attn_got, piece * HALF)
    for piece in range(2):
        base = 4 * MODEL + piece * FF
        pairs += column_copies(where, out, base, FF_HALF, mlp, mlp_got, piece * FF_HALF)
    copies = [
        pltpu.make_async_copy(source, target, sems.at[at])
        for at, (source, target) in enumerate(pairs)
    ]
    for copy in copies:
        copy.start()
    seg_vec_kernel(where, vecs, vecs_got, vec_out, flat)
    wait_all(copies)


def plane_parts(part):
    return (part,) + together(*(in_plane(part, mask) for mask in range(1, PLANE)))


def line_parts(part):
    return (part,) + together(*(along_line(part, apart) for apart in range(1, LINE)))


def slice_local(
    hidden_in,
    targets,
    doc_ids,
    seg_nums,
    valid_flags,
    seg_mats,
    seg_vecs,
    cls_mats,
    cls_vecs,
    seg_pos,
):
    rank, core_at = lax.axis_index("fsdp"), lax.axis_index("rep")
    line_at, plane_at = rank // PLANE, rank % PLANE
    where = jnp.stack([line_at, plane_at, core_at, doc_ids[0], seg_nums[0]]).astype(jnp.int32)
    own_rows, total_columns = seg_mats.shape
    vec_size = seg_vecs.shape[0]
    both_rows = CORES * SEG

    first_piece, live_row, *rest = run_kernel(
        prepare_kernel,
        "prepare",
        [shape_of((own_rows, FIRST), LOW), shape_of((1, SEG))]
        + [shape_of((own_rows, FF_HALF), LOW)] * 2
        + [shape_of((own_rows, QUARTER_HALF), LOW)] * LINE
        + [shape_of((own_rows, HALF), LOW), shape_of((MODEL, PLANE * SPAN), LOW)],
        where,
        (seg_mats, cls_mats),
        (seg_vecs, cls_vecs, valid_flags),
        [
            pltpu.SemaphoreType.DMA((4,)),
            pltpu.VMEM((LINE, own_rows, QUARTER), LOW),
            pltpu.SemaphoreType.DMA((3 + 5 * LINE,)),
        ],
    )
    first_line = line_parts(first_piece)
    second_piece, third_piece, quarters, cls_out_piece, order = (
        rest[0],
        rest[1],
        rest[2:-2],
        rest[-2],
        rest[-1],
    )

    def joined(*pieces):
        return jnp.concatenate(pieces, axis=1)

    def sent_both(to_x, to_y):
        to_x, to_y = together(to_x, to_y)
        return together(in_plane(to_x, 1), in_plane(to_y, 2))

    own_sent = joined(first_piece, second_piece, third_piece)
    own_x, own_y = sent_both(own_sent, own_sent)
    first_line = first_line[:1] + tuple(after(got, own_x, own_y) for got in first_line[1:])
    hidden_got = other_core(after(hidden_in, own_x, own_y))
    live_got = other_core(after(live_row, own_x, own_y))
    to_x = joined(after(own_y, hidden_got, live_got)[:, OWN_CUT:], *first_line[1:])
    to_y = joined(own_x[:, :OWN_CUT], *first_line[1:])
    first_x, first_y = sent_both(to_x, to_y)
    second_line = line_parts(after(second_piece, to_x, to_y))

    def halves(group, from_x, from_y):
        width, cut = WIDTHS[group], LINE_CUTS[group]
        if group == 0:
            base_x, base_y = sum(WIDTHS) - OWN_CUT, OWN_CUT
        else:
            before, before_cut = WIDTHS[group - 1], LINE_CUTS[group - 1]
            base_x, base_y = 2 * before - before_cut, before + before_cut
        return (
            from_y[:, base_y + width + cut : base_y + 3 * width],
            from_x[:, base_x : base_x + width + cut],
        )

    high, low = halves(0, first_x, first_y)
    to_x, to_y = joined(high, *second_line[1:]), joined(low, *second_line[1:])
    second_x, second_y = sent_both(to_x, to_y)
    third_line = line_parts(after(third_piece, to_x, to_y))
    high, low = halves(1, second_x, second_y)
    to_x, to_y = joined(high, *third_line[1:]), joined(low, *third_line[1:])
    third_x, third_y = sent_both(to_x, to_y)
    own_parts = (own_x, own_y, first_x, first_y)
    cls_line = (quarters[0],) + tuple(
        along_line(after(quarters[apart], to_x, to_y), apart)
        for apart in range(1, LINE)
    )

    qkv_weight, out_low, out_high, qkv, mixed, vectors, count, hidden_ordered = run_kernel(
        qkv_kernel,
        "seg_qkv",
        [
            shape_of((GROUP, own_rows, 3 * HALF), LOW),
            shape_of((GROUP // 2, own_rows, HALF), LOW),
            shape_of((GROUP // 2, own_rows, HALF), LOW),
            shape_of((both_rows, 3 * HALF), LOW),
            shape_of((both_rows, HALF), LOW),
            shape_of((2 * (8 * MODEL + FF) // MODEL, MODEL)),
            shape_of((8, LANES)),
            shape_of((both_rows, PLANE * SPAN), LOW),
        ],
        where,
        (),
        first_line
        + own_parts
        + (first_x, first_y, second_x, second_y)
        + (hidden_in, hidden_got, live_row, live_got, order),
        [
            pltpu.VMEM((GROUP, own_rows, LANES), LOW),
            pltpu.VMEM((2, 8 * MODEL + FF), WIDE),
            pltpu.VMEM((both_rows, MODEL), LOW),
            pltpu.VMEM((GROUP, own_rows, HALF), LOW),
        ],
        flops=2 * SEG * MODEL * 3 * MODEL,
    )
    out_weight, mixed_ordered, normed_first, inv_first, first_low = run_kernel(
        out_kernel,
        "seg_out",
        [
            shape_of((MODEL, MODEL), LOW),
            shape_of((both_rows, PLANE * SPAN), LOW),
            shape_of((SEG, MODEL)),
            shape_of((SEG, 1)),
            shape_of((SEG, MODEL), LOW),
        ],
        where,
        (),
        (
            hidden_in,
            mixed,
            after(other_core(mixed), third_x, third_y),
            out_low,
            out_high,
            other_core(out_low),
            other_core(out_high),
            vectors,
            order,
        ),
        [pltpu.VMEM((both_rows, MODEL), LOW)],
        flops=2 * SEG * MODEL * MODEL,
    )
    fourth_x, fourth_y = sent_both(*halves(2, third_x, third_y))
    first_got = after(other_core(first_low), fourth_x, fourth_y)
    count = count + other_core(after(count, first_got))
    up_weight, act, slope = run_kernel(
        up_kernel,
        "seg_up",
        [
            shape_of((GROUP, own_rows, FF_HALF), LOW),
            shape_of((both_rows, FF_HALF), LOW),
            shape_of((both_rows, FF_HALF)),
        ],
        where,
        (),
        second_line
        + own_parts
        + (second_x, second_y, third_x, third_y)
        + (first_low, first_got, vectors),
        [pltpu.VMEM((both_rows, MODEL), LOW)],
        flops=2 * SEG * MODEL * FF,
    )
    cls_sent = joined(*cls_line, cls_out_piece)
    cls_sent = after(cls_sent, act)
    cls_x, cls_y = sent_both(cls_sent, cls_sent)
    down_weight, down_own, down_send = run_kernel(
        down_kernel,
        "seg_down",
        [
            shape_of((GROUP, own_rows, FF_HALF), LOW),
            shape_of((SEG, MODEL)),
            shape_of((SEG, MODEL)),
        ],
        where,
        (),
        third_line + own_parts + (third_x, third_y, fourth_x, fourth_y) + (act,),
        flops=2 * SEG * MODEL * FF,
    )
    normed_second, inv_second, diff, out_rows, head_row = run_kernel(
        seg_rows_kernel,
        "seg_rows",
        [
            shape_of((SEG, MODEL)),
            shape_of((SEG, 1)),
            shape_of((SEG, MODEL)),
            shape_of((SEG, MODEL)),
            shape_of((1, 2 * MODEL + LANES)),
        ],
        where,
        (),
        (
            down_own,
            other_core(down_send),
            normed_first,
            vectors,
            targets,
            live_row,
            seg_pos,
        ),
    )
    head_planes = plane_parts(head_row)
    size = LINE // 2 * QUARTER_HALF
    cls_far = sent_both(
        after(cls_y[:, size:], *head_planes[1:]), after(cls_x[:, :size], *head_planes[1:])
    )

    second_grad, second_low, second_sums, first_ordered = run_kernel(
        second_norm_kernel,
        "seg_second_norm",
        [
            shape_of((SEG, MODEL)),
            shape_of((SEG, MODEL), LOW),
            shape_of((3, MODEL)),
            shape_of((both_rows, PLANE * SPAN), LOW),
        ],
        where,
        (),
        (diff, count, normed_second, inv_second, vectors, first_low, first_got, order),
        [pltpu.VMEM((both_rows, MODEL), LOW)],
    )
    second_got = other_core(second_low)
    head_lines = line_parts(after(jnp.concatenate(head_planes), second_got))
    pre, first_grad_own, first_grad_send, up_sums = run_kernel(
        mlp_back_kernel,
        "seg_mlp_back",
        [
            shape_of((both_rows, FF_HALF), LOW),
            shape_of((SEG, MODEL)),
            shape_of((SEG, MODEL)),
            shape_of((FF_HALF // MODEL, MODEL)),
        ],
        where,
        (),
        (second_low, second_got, down_weight, up_weight, slope),
        [pltpu.VMEM((both_rows, MODEL), LOW)],
        flops=4 * SEG * MODEL * FF,
    )
    first_grad_got = other_core(first_grad_send)

    def part_shapes(columns):
        return [
            shape_of((count_of, own_rows, columns), LOW)
            for count_of in (LINE // 2, LINE // 2, LINE, LINE, LINE)
        ]

    mlp_data = (first_ordered, second_low, second_got, pre, act, order)
    mlp_far = run_kernel(
        mlp_far_kernel,
        "seg_mlp_far",
        part_shapes(FF)[:2],
        where,
        (),
        mlp_data,
        [pltpu.VMEM((both_rows, MODEL), LOW)],
        flops=SEG * MODEL * FF,
    )
    head_lines = head_lines[:1] + together(
        *(after(got, mlp_far[0]) for got in head_lines[1:])
    )
    cls_far = together(*(after(got, *head_lines[1:]) for got in cls_far))
    cls_half, cls_out_half = run_kernel(
        cls_gather_kernel,
        "head_gather",
        [
            shape_of((GROUP, own_rows, QUARTER_HALF), LOW),
            shape_of((PLANE, own_rows, HALF), LOW),
        ],
        where,
        (),
        cls_line + (cls_x, cls_y) + cls_far + (cls_out_piece,),
    )
    mlp_parts = list(mlp_far) + list(
        run_kernel(
            mlp_near_kernel,
            "seg_mlp_near",
            part_shapes(FF)[2:],
            where,
            (),
            mlp_data,
            [pltpu.VMEM((both_rows, MODEL), LOW)],
            flops=3 * SEG * MODEL * FF,
        )
    )
    mlp_far = reduce_far(tuple(after(part, *cls_far) for part in mlp_parts[:2]))
    cls_weight, cls_out = run_kernel(
        cls_weight_kernel,
        "head_weight",
        [
            shape_of((GROUP, own_rows, QUARTER), LOW),
            shape_of((4, HEAD_DIM, MODEL), LOW),
        ],
        where,
        (),
        (cls_half, other_core(cls_half), cls_out_half, other_core(cls_out_half)),
    )
    cls_weight = cls_weight.reshape(MODEL, QUARTER)
    cls_out = cls_out.reshape(SPAN, MODEL)
    heads, cls_qkv, cls_mixed, part = run_kernel(
        cls_attend_kernel,
        "head_attend",
        [
            shape_of((GROUP, 2 * MODEL + LANES)),
            shape_of((GROUP, 3 * SPAN), LOW),
            shape_of((GROUP, SPAN), LOW),
            shape_of((GROUP, MODEL)),
        ],
        where,
        (),
        tuple(after(got, mlp_parts[0], first_grad_got) for got in head_lines)
        + (vectors, cls_weight, cls_out),
    )
    cls_normed, cls_inv, cls_low, cls_act, cls_slope, part, *mlp_sent = run_kernel(
        head_mlp_kernel,
        "head_mlp",
        [
            shape_of((GROUP, MODEL)),
            shape_of((GROUP, 1)),
            shape_of((GROUP, MODEL), LOW),
            shape_of((GROUP, FF // LINE), LOW),
            shape_of((GROUP, FF // LINE)),
            shape_of((GROUP, MODEL)),
            shape_of(mlp_parts[2].shape, LOW),
            shape_of(mlp_parts[2].shape, LOW),
        ],
        where,
        (),
        (heads,) + line_parts(part) + (vectors, cls_weight) + mlp_far + tuple(mlp_parts[2:4]),
    )
    mlp_plane = sent_both(*mlp_sent)
    cls_parts = line_parts(part)
    top_row, square, cls_grad, cls_second, cls_pre, part, top_sums = run_kernel(
        cls_top_kernel,
        "head_top",
        [
            shape_of((1, MODEL)),
            shape_of((8, LANES)),
            shape_of((GROUP, MODEL)),
            shape_of((GROUP, MODEL), LOW),
            shape_of((GROUP, FF // LINE), LOW),
            shape_of((GROUP, MODEL)),
            shape_of((2, MODEL)),
        ],
        where,
        (),
        (heads,)
        + cls_parts
        + (vectors, cls_weight, cls_normed, count, cls_slope),
        [pltpu.VMEM((GROUP, MODEL), WIDE)],
    )
    top_parts = line_parts(part)
    cls_grad, cls_branch, cls_proj, part, back_sums = run_kernel(
        cls_attend_back_kernel,
        "head_attend_back",
        [
            shape_of((GROUP, MODEL)),
            shape_of((GROUP, MODEL), LOW),
            shape_of((GROUP, 3 * SPAN), LOW),
            shape_of((GROUP, MODEL)),
            shape_of((2, MODEL)),
        ],
        where,
        (),
        (heads,)
        + top_parts
        + (vectors, cls_weight, cls_out, cls_grad, cls_normed, cls_inv, cls_qkv),
    )
    end_parts = line_parts(part)
    pack = jnp.concatenate([cls_proj, cls_mixed, cls_pre, cls_act], axis=1)
    folded = [shape_of((own_rows, FF))] + [shape_of((own_rows + GROUP, FF), LOW)] * (LINE - 1)
    dheads, head_grad, shared, mlp_own, *mlp_sent = run_kernel(
        head_end_kernel,
        "head_end",
        [shape_of((1, MODEL)), shape_of((1, MODEL)), shape_of((GROUP + 8, MODEL))] + folded,
        where,
        (),
        (heads, cls_grad)
        + end_parts
        + (square, back_sums, top_sums, normed_second, inv_second, vectors)
        + (mlp_parts[4],)
        + mlp_plane
        + (pack,),
        [pltpu.VMEM((GROUP, MODEL), WIDE)],
    )
    got_three, got_two = along_line(mlp_sent[2], 3), along_line(mlp_sent[1], 2)
    mlp_last = mlp_sent[0]
    mlp_got = [None, got_two, got_three]

    head_own, head_send, head_data = run_kernel(
        head_back_kernel,
        "seg_head_back",
        [shape_of((1, MODEL)), shape_of((1, MODEL)), shape_of((12, MODEL))],
        where,
        (),
        (
            head_grad,
            other_core(head_grad),
            down_weight,
            up_weight,
            slope,
            act,
            first_low,
            first_got,
        ),
    )
    grad_summed, branch, mixed_grad, attn_send, first_sums = run_kernel(
        first_norm_kernel,
        "seg_first_norm",
        [
            shape_of((SEG, MODEL)),
            shape_of((SEG, MODEL), LOW),
            shape_of((SEG, MODEL), LOW),
            shape_of((SEG, MODEL), LOW),
            shape_of((3, MODEL)),
        ],
        where,
        (),
        (
            second_grad,
            first_grad_own,
            first_grad_got,
            head_grad,
            head_own,
            other_core(head_send),
            normed_first,
            inv_first,
            vectors,
            out_weight,
        ),
    )
    attn_got = other_core(attn_send)
    proj = run_kernel(
        attn_back_kernel,
        "seg_attn_back",
        [shape_of((both_rows, 3 * HALF), LOW)],
        where,
        (),
        (qkv, mixed_grad, attn_got, live_row, live_got),
        flops=2 * SEG * MODEL * 3 * MODEL,
    )[0]
    attn_data = (hidden_ordered, mixed_ordered, proj, branch, attn_got)
    attn_far = run_kernel(
        attn_far_kernel,
        "seg_attn_far",
        part_shapes(4 * HALF)[:2],
        where,
        (),
        attn_data,
        flops=SEG * MODEL * 2 * MODEL,
    )
    attn_far = reduce_far(tuple(after(part, mlp_got[-1]) for part in attn_far))
    *attn_near, output, input_own, input_send, payload = run_kernel(
        attn_near_kernel,
        "seg_attn_near",
        part_shapes(4 * HALF)[2:]
        + [
            shape_of((SEG, MODEL), LOW),
            shape_of((SEG, MODEL)),
            shape_of((SEG, MODEL)),
            shape_of((24, MODEL), LOW),
        ],
        where,
        (),
        attn_data
        + (top_row, out_rows, live_row, qkv_weight, first_sums, second_sums, up_sums)
        + (dheads, normed_second, head_data),
        [pltpu.VMEM((24, MODEL), WIDE)],
        flops=3 * SEG * MODEL * 2 * MODEL,
    )
    attn_sent = run_kernel(
        add_far_kernel,
        "seg_attn_add",
        [shape_of(attn_near[0].shape, LOW)] * 2,
        where,
        (),
        attn_far + (after(attn_near[0], got_two), attn_near[1]),
    )
    attn_plane = sent_both(*attn_sent)
    mlp_got[0] = along_line(after(mlp_last, *attn_sent), 1)
    input_got = other_core(after(input_send, *attn_sent))
    shared = shared + other_core(after(shared, attn_sent[0]))
    payload_parts = line_parts(after(payload, mlp_got[0], input_got, shared))
    mlp_got = [after(got, attn_plane[0]) for got in mlp_got]
    mlp_sum = reduce_line(mlp_own, mlp_got)
    row_width = 8 * MODEL + 2 * FF
    cls_rows, input_grad = run_kernel(
        rows_input_kernel,
        "head_rows",
        [shape_of((GROUP, row_width), LOW), shape_of((SEG, MODEL), LOW)],
        where,
        (),
        (pack,)
        + tuple(mlp_got)
        + (heads, cls_branch, cls_low, cls_second)
        + (grad_summed, input_own, input_got),
        [pltpu.VMEM((LINE,) + pack.shape, LOW)],
    )
    cls_got = other_core(cls_rows)
    attn_plane = tuple(after(got, output, shared) for got in attn_plane)
    attn_own, *attn_sent = reduce_fold(where, attn_near[2], attn_plane)
    next_line = along_line(attn_sent[0], 1)
    attn_lines = [next_line] + list(
        together(*(along_line(attn_sent[apart - 1], apart) for apart in range(2, LINE)))
    )
    flat = pltpu.VMEM((1, 8 * MODEL + FF), WIDE)
    payload_line = after(jnp.concatenate(payload_parts), *attn_plane)
    payload_plane = [payload_line] + [
        in_plane(after(payload_line, next_line) if apart == PLANE - 1 else payload_line, apart)
        for apart in range(1, PLANE)
    ]
    mlp_mine, own_vecs, cls_mats_grad, cls_vec_grad, pos_total, loss_value = run_kernel(
        share_owner_kernel,
        "head_owner",
        [
            shape_of((own_rows, FF)),
            shape_of((16, MODEL)),
            shape_of((own_rows, total_columns)),
            shape_of((vec_size,)),
            shape_of((GROUP, MODEL)),
            shape_of((1, 1)),
        ],
        where,
        (),
        tuple(after(got, attn_own) for got in payload_plane)
        + (mlp_sum, cls_rows, cls_got, shared, count),
        [
            pltpu.VMEM((GROUP * 24, MODEL), LOW),
            pltpu.VMEM((CORES * GROUP, row_width), LOW),
            flat,
        ],
        flops=64 * own_rows * total_columns,
    )
    loss_value = loss_value.reshape(())
    attn_lines = together(*(after(got, mlp_mine) for got in attn_lines))
    attn_sum = reduce_line(attn_own, attn_lines)
    seg_mats_grad, seg_vec_grad = run_kernel(
        store_kernel,
        "seg_owner",
        [shape_of((own_rows, total_columns)), shape_of((vec_size,))],
        where,
        (),
        (attn_sum, other_core(attn_sum), mlp_mine, other_core(mlp_mine))
        + (own_vecs, other_core(own_vecs)),
        [flat, pltpu.SemaphoreType.DMA((12,))],
        far=(0,),
    )

    return (
        output,
        input_grad,
        seg_mats_grad,
        seg_vec_grad,
        cls_mats_grad,
        cls_vec_grad,
        pos_total,
        loss_value,
    )


def solution(mesh):
    in_specs = (
        P(("rep", "fsdp"), None),
        P(("rep", "fsdp"), None),
        P(("rep", "fsdp")),
        P(("rep", "fsdp")),
        P(("rep", "fsdp")),
        P("fsdp", None),
        P("fsdp"),
        P("fsdp", None),
        P("fsdp"),
        P(),
    )
    out_specs = (
        P(("rep", "fsdp"), None),
        P(("rep", "fsdp"), None),
        P("fsdp", None),
        P("fsdp"),
        P("fsdp", None),
        P("fsdp"),
        P(),
        P(),
    )
    one_slice = dict(mesh.shape) == {"rep": CORES, "fsdp": LINE * PLANE}
    body = slice_local if one_slice else local
    return jax.shard_map(body, mesh=mesh, in_specs=in_specs, out_specs=out_specs, check_vma=False)
```

```python
import math

import jax
import jax.numpy as jnp
from jax import lax
from jax.experimental import pallas as pl
from jax.experimental.pallas import tpu as pltpu
from jax.sharding import PartitionSpec as P

HEADS = 12
HEAD_DIM = 64
FF = 3072
SEG = 128
SEQ = 2048


NORM_EPS = 1e-05
MASK_FILL = -1e30
SQRT_HALF = 0.7071067811865476
INV_SQRT_TWO_PI = 0.3989422804014327


def swapped(value, axis, apart):
    mask = 2**apart
    pairs = [(source, source ^ mask) for source in range(lax.axis_size(axis))]
    return lax.ppermute(value, axis, pairs)


def product_plain(left_side, right_side):
    return jnp.dot(left_side, right_side, preferred_element_type=jnp.float32)


def product_left(left_side, right_side):
    return lax.dot_general(
        left_side, right_side, (((0,), (0,)), ((), ())), preferred_element_type=jnp.float32
    )


def product_right(left_side, right_side):
    return lax.dot_general(
        left_side, right_side, (((1,), (1,)), ((), ())), preferred_element_type=jnp.float32
    )


def row_total(array_in):
    return jnp.sum(array_in.astype(jnp.float32), axis=0)


def unpack_weights(gathered, model_width, ff_width):
    matrix, vector = gathered
    vector = vector.astype(jnp.float32)
    pieces = tuple(
        (vector[offset * model_width : (offset + 1) * model_width] for offset in range(8))
    )
    return (
        (
            matrix[:, : 3 * model_width],
            matrix[:, 3 * model_width : 4 * model_width],
            matrix[:, 4 * model_width : 4 * model_width + ff_width],
            matrix[:, 4 * model_width + ff_width :],
        )
        + pieces
        + (vector[8 * model_width :],)
    )


def norm_forward(summed, gain_vec, shift_vec):
    row_mean = jnp.mean(summed, axis=-1, keepdims=True)
    centered = summed - row_mean
    inv_dev = lax.rsqrt(jnp.mean(centered * centered, axis=-1, keepdims=True) + NORM_EPS)
    normed = centered * inv_dev
    return (normed * gain_vec + shift_vec, normed, inv_dev)


def norm_backward(grad_out, normed, inv_dev, gain_vec):
    scaled = grad_out * gain_vec
    mean_one = jnp.mean(scaled, axis=-1, keepdims=True)
    mean_two = jnp.mean(scaled * normed, axis=-1, keepdims=True)
    grad_in = inv_dev * (scaled - mean_one - normed * mean_two)
    return (grad_in, jnp.sum(grad_out * normed, axis=0), jnp.sum(grad_out, axis=0))


def gelu_value(before):
    return 0.5 * before * (1.0 + lax.erf(before * SQRT_HALF))


def gelu_slope(before):
    return (
        0.5 * (1.0 + lax.erf(before * SQRT_HALF))
        + before * jnp.exp(-0.5 * before * before) * INV_SQRT_TWO_PI
    )


def attention_scores(queries, keys_in, allowed, score_scale):
    raw_scores = (
        jnp.einsum("bqhe,bkhe->bhqk", queries, keys_in, preferred_element_type=jnp.float32)
        * score_scale
    )
    return jnp.where(allowed, raw_scores, MASK_FILL)


def attention_forward(queries, keys_in, values, allowed, score_scale):
    scores = attention_scores(queries, keys_in, allowed, score_scale)
    row_top = jnp.max(scores, axis=-1, keepdims=True)
    log_total = row_top + jnp.log(jnp.sum(jnp.exp(scores - row_top), axis=-1, keepdims=True))
    weights = jnp.exp(scores - log_total).astype(jnp.bfloat16)
    mixed_rows = jnp.einsum("bhqk,bkhe->bqhe", weights, values, preferred_element_type=jnp.float32)
    return (mixed_rows, log_total)


def attention_backward(queries, keys_in, values, allowed, score_scale, log_total, grad_mixed):
    probabilities = jnp.exp(attention_scores(queries, keys_in, allowed, score_scale) - log_total)
    grad_probs = jnp.einsum(
        "bqhe,bkhe->bhqk", grad_mixed, values, preferred_element_type=jnp.float32
    )
    inner_sum = jnp.sum(grad_probs * probabilities, axis=-1, keepdims=True)
    grad_scores = (probabilities * (grad_probs - inner_sum)).astype(jnp.bfloat16)
    grad_query = (
        jnp.einsum("bhqk,bkhe->bqhe", grad_scores, keys_in, preferred_element_type=jnp.float32)
        * score_scale
    )
    grad_key = (
        jnp.einsum("bhqk,bqhe->bkhe", grad_scores, queries, preferred_element_type=jnp.float32)
        * score_scale
    )
    grad_value = jnp.einsum(
        "bhqk,bqhe->bkhe",
        probabilities.astype(jnp.bfloat16),
        grad_mixed,
        preferred_element_type=jnp.float32,
    )
    return (grad_query, grad_key, grad_value)


def block_forward(rows_in, unpacked, attend):
    (
        qkv_weight,
        out_weight,
        up_weight,
        down_weight,
        query_bias,
        value_bias,
        out_bias,
        down_bias,
        gain_first,
        shift_first,
        gain_second,
        shift_second,
        up_bias,
    ) = unpacked
    model_width = rows_in.shape[1]
    inputs = rows_in.astype(jnp.bfloat16)
    projected = product_plain(inputs, qkv_weight)
    queries = (projected[:, :model_width] + query_bias).astype(jnp.bfloat16)
    keys_in = projected[:, model_width : 2 * model_width].astype(jnp.bfloat16)
    values = (projected[:, 2 * model_width :] + value_bias).astype(jnp.bfloat16)
    mixed_rows, attend_kept = attend(queries, keys_in, values)
    mixed_rows = mixed_rows.astype(jnp.bfloat16)
    summed_first = rows_in + product_plain(mixed_rows, out_weight) + out_bias
    first_out, normed_first, inv_first = norm_forward(summed_first, gain_first, shift_first)
    first_low = first_out.astype(jnp.bfloat16)
    pre_act = product_plain(first_low, up_weight) + up_bias
    activated = gelu_value(pre_act).astype(jnp.bfloat16)
    summed_second = first_out + product_right(activated, down_weight) + down_bias
    block_out, normed_second, inv_second = norm_forward(summed_second, gain_second, shift_second)
    saved_state = (
        inputs,
        queries,
        keys_in,
        values,
        attend_kept,
        mixed_rows,
        normed_first,
        inv_first,
        first_low,
        pre_act,
        activated,
        normed_second,
        inv_second,
    )
    return (block_out, saved_state)


def block_backward(grad_out, unpacked, saved_state, attend_back):
    (
        qkv_weight,
        out_weight,
        up_weight,
        down_weight,
        query_bias,
        value_bias,
        out_bias,
        down_bias,
        gain_first,
        shift_first,
        gain_second,
        shift_second,
        up_bias,
    ) = unpacked
    (
        inputs,
        queries,
        keys_in,
        values,
        attend_kept,
        mixed_rows,
        normed_first,
        inv_first,
        first_low,
        pre_act,
        activated,
        normed_second,
        inv_second,
    ) = saved_state
    grad_second, grad_gain_second, grad_shift_second = norm_backward(
        grad_out, normed_second, inv_second, gain_second
    )
    second_low = grad_second.astype(jnp.bfloat16)
    grad_pre = (product_plain(second_low, down_weight) * gelu_slope(pre_act)).astype(jnp.bfloat16)
    grad_first = grad_second + product_right(grad_pre, up_weight)
    grad_summed, grad_gain_first, grad_shift_first = norm_backward(
        grad_first, normed_first, inv_first, gain_first
    )
    branch_low = grad_summed.astype(jnp.bfloat16)
    grad_mixed = product_right(branch_low, out_weight).astype(jnp.bfloat16)
    grad_query, grad_key, grad_value = attend_back(
        queries, keys_in, values, attend_kept, grad_mixed
    )
    grad_proj = jnp.concatenate([grad_query, grad_key, grad_value], axis=1)
    grad_rows = grad_summed + product_right(grad_proj, qkv_weight)
    vector_grad = jnp.concatenate(
        [
            row_total(grad_query),
            row_total(grad_value),
            row_total(branch_low),
            row_total(second_low),
            grad_gain_first,
            grad_shift_first,
            grad_gain_second,
            grad_shift_second,
            row_total(grad_pre),
        ]
    )
    weight_rows = (
        inputs,
        grad_proj,
        mixed_rows,
        branch_low,
        first_low,
        grad_pre,
        second_low,
        activated,
    )
    return (grad_rows, weight_rows, vector_grad)


def weight_products(weight_rows):
    inputs, grad_proj, mixed_rows, branch_low, first_low, grad_pre, second_low, activated = (
        weight_rows
    )
    return (
        product_left(inputs, grad_proj),
        product_left(mixed_rows, branch_low),
        product_left(first_low, grad_pre),
        product_left(second_low, activated),
    )


def local(
    hidden_in,
    targets,
    doc_ids,
    seg_nums,
    valid_flags,
    seg_mats,
    seg_vecs,
    cls_mats,
    cls_vecs,
    seg_pos,
):
    tok_rows, model_width = hidden_in.shape
    ff_width = FF
    seg_len = SEG
    group_span = SEQ // tok_rows
    seg_count = tok_rows // seg_len
    score_scale = HEAD_DIM ** (-0.5)
    head_shape = (HEADS, HEAD_DIM)
    live_rows = valid_flags.astype(jnp.float32)
    rank_full = lax.axis_index("fsdp")
    seg_gathered = (
        lax.all_gather(seg_mats, "fsdp", axis=0, tiled=True),
        lax.all_gather(seg_vecs, "fsdp", axis=0, tiled=True),
    )
    seg_unpacked = unpack_weights(seg_gathered, model_width, ff_width)
    cls_gathered = (
        lax.all_gather(cls_mats, "fsdp", axis=0, tiled=True),
        lax.all_gather(cls_vecs, "fsdp", axis=0, tiled=True),
    )
    cls_unpacked = unpack_weights(cls_gathered, model_width, ff_width)
    seg_allowed = (live_rows.reshape(seg_count, 1, 1, seg_len) > 0.5) | jnp.eye(seg_len, dtype=bool)
    seg_shape = (seg_count, seg_len) + head_shape

    def seg_attend(queries, keys_in, values):
        mixed_rows, log_total = attention_forward(
            queries.reshape(seg_shape),
            keys_in.reshape(seg_shape),
            values.reshape(seg_shape),
            seg_allowed,
            score_scale,
        )
        return (mixed_rows.reshape(tok_rows, model_width), log_total)

    def seg_attend_back(queries, keys_in, values, log_total, grad_mixed):
        grad_parts = attention_backward(
            queries.reshape(seg_shape),
            keys_in.reshape(seg_shape),
            values.reshape(seg_shape),
            seg_allowed,
            score_scale,
            log_total,
            grad_mixed.reshape(seg_shape),
        )
        return tuple(
            (
                grad_part.reshape(tok_rows, model_width).astype(jnp.bfloat16)
                for grad_part in grad_parts
            )
        )

    first_out, seg_saved = block_forward(hidden_in.astype(jnp.float32), seg_unpacked, seg_attend)
    first_grid = first_out.reshape(seg_count, seg_len, model_width)
    position_hot = (seg_nums[:, None] == jnp.arange(seg_pos.shape[0])[None, :]).astype(jnp.float32)
    position_rows = jnp.sum(
        position_hot[:, :, None] * seg_pos.astype(jnp.float32)[None, :, :], axis=1
    )
    heads_in = first_grid[:, 0, :] + position_rows
    lead_live = live_rows.reshape(seg_count, seg_len)[:, 0]
    lead_doc = doc_ids.reshape(seg_count, seg_len)[:, 0]
    lead_labels = jnp.where(lead_live > 0.5, lead_doc, -1).astype(jnp.bfloat16)
    lead_doc_low = lead_doc.astype(jnp.bfloat16)
    bit_count = group_span.bit_length() - 1
    key_total = group_span * seg_count
    own_slot = rank_full % group_span * seg_count + jnp.arange(seg_count)
    query_shape = (1, seg_count) + head_shape
    key_shape = (1, key_total) + head_shape

    def cls_attend(queries, keys_in, values):
        paired = jnp.concatenate([keys_in, values], axis=1)
        labels = lead_labels
        for bit_level in range(bit_count):
            other_pair, other_labels = swapped((paired, labels), "fsdp", bit_level)
            upper_half = rank_full // (1 << bit_level) % 2 == 1
            paired = jnp.where(
                upper_half,
                jnp.concatenate([other_pair, paired]),
                jnp.concatenate([paired, other_pair]),
            )
            labels = jnp.where(
                upper_half,
                jnp.concatenate([other_labels, labels]),
                jnp.concatenate([labels, other_labels]),
            )
        allowed = (labels[None, :] == lead_doc_low[:, None]) | (
            jnp.arange(key_total)[None, :] == own_slot[:, None]
        )
        allowed = allowed[None, None]
        mixed_rows, log_total = attention_forward(
            queries.reshape(query_shape),
            paired[:, :model_width].reshape(key_shape),
            paired[:, model_width:].reshape(key_shape),
            allowed,
            score_scale,
        )
        return (mixed_rows.reshape(seg_count, model_width), (paired, allowed, log_total))

    def cls_attend_back(queries, keys_in, values, attend_kept, grad_mixed):
        paired, allowed, log_total = attend_kept
        grad_query, grad_key, grad_value = attention_backward(
            queries.reshape(query_shape),
            paired[:, :model_width].reshape(key_shape),
            paired[:, model_width:].reshape(key_shape),
            allowed,
            score_scale,
            log_total,
            grad_mixed.reshape(query_shape),
        )
        grad_pair = jnp.concatenate(
            [grad_key.reshape(key_total, model_width), grad_value.reshape(key_total, model_width)],
            axis=1,
        )
        for bit_level in reversed(range(bit_count)):
            half_rows = grad_pair.shape[0] // 2
            upper_half = rank_full // (1 << bit_level) % 2 == 1
            kept_half = jnp.where(upper_half, grad_pair[half_rows:], grad_pair[:half_rows])
            sent_half = jnp.where(upper_half, grad_pair[:half_rows], grad_pair[half_rows:])
            grad_pair = kept_half + swapped(
                sent_half.astype(jnp.bfloat16), "fsdp", bit_level
            ).astype(sent_half.dtype)
        grad_pair = grad_pair.astype(jnp.bfloat16)
        return (
            grad_query.reshape(seg_count, model_width).astype(jnp.bfloat16),
            grad_pair[:, :model_width],
            grad_pair[:, model_width:],
        )

    top_out, cls_saved = block_forward(heads_in, cls_unpacked, cls_attend)
    combined = jnp.concatenate([top_out[:, None, :], first_grid[:, 1:, :]], axis=1).reshape(
        tok_rows, model_width
    )
    output_rows = combined * live_rows[:, None]
    diff_rows = (output_rows - targets.astype(jnp.float32)) * live_rows[:, None]
    count_all, square_all = lax.psum(
        (jnp.sum(live_rows), jnp.sum(diff_rows * diff_rows)), ("rep", "fsdp")
    )
    loss_value = square_all / (count_all * model_width)
    slots_all = tok_rows * lax.axis_size("rep") * lax.axis_size("fsdp")
    grad_grid = (diff_rows * (slots_all / count_all)).reshape(seg_count, seg_len, model_width)
    cls_back = unpack_weights(
        (
            lax.all_gather(cls_mats, "fsdp", axis=0, tiled=True),
            lax.all_gather(cls_vecs, "fsdp", axis=0, tiled=True),
        ),
        model_width,
        ff_width,
    )
    heads_grad, cls_weight_rows, cls_g_vec = block_backward(
        grad_grid[:, 0, :], cls_back, cls_saved, cls_attend_back
    )
    cls_g_qkv, cls_g_out, cls_g_up, cls_g_down = weight_products(cls_weight_rows)
    pos_local = jnp.sum(position_hot[:, :, None] * heads_grad[:, None, :], axis=0)
    seg_grad_out = jnp.concatenate([heads_grad[:, None, :], grad_grid[:, 1:, :]], axis=1).reshape(
        tok_rows, model_width
    )
    seg_back = unpack_weights(
        (
            lax.all_gather(seg_mats, "fsdp", axis=0, tiled=True),
            lax.all_gather(seg_vecs, "fsdp", axis=0, tiled=True),
        ),
        model_width,
        ff_width,
    )
    input_grad, seg_weight_rows, seg_g_vec = block_backward(
        seg_grad_out, seg_back, seg_saved, seg_attend_back
    )
    seg_g_qkv, seg_g_out, seg_g_up, seg_g_down = weight_products(seg_weight_rows)
    owner_rows = tuple(
        (
            lax.psum_scatter(seg_g_qkv, "fsdp", scatter_dimension=0, tiled=True),
            lax.psum_scatter(seg_g_out, "fsdp", scatter_dimension=0, tiled=True),
            lax.psum_scatter(seg_g_up, "fsdp", scatter_dimension=0, tiled=True),
            lax.psum_scatter(seg_g_down, "fsdp", scatter_dimension=0, tiled=True),
            lax.psum_scatter(seg_g_vec, "fsdp", scatter_dimension=0, tiled=True),
            lax.psum_scatter(cls_g_qkv, "fsdp", scatter_dimension=0, tiled=True),
            lax.psum_scatter(cls_g_out, "fsdp", scatter_dimension=0, tiled=True),
            lax.psum_scatter(cls_g_up, "fsdp", scatter_dimension=0, tiled=True),
            lax.psum_scatter(cls_g_down, "fsdp", scatter_dimension=0, tiled=True),
            lax.psum_scatter(cls_g_vec, "fsdp", scatter_dimension=0, tiled=True),
        )
    )
    replica_share = (
        lax.psum_scatter(
            owner_rows[0].astype(jnp.bfloat16), "rep", scatter_dimension=1, tiled=True
        ).astype(jnp.float32),
        lax.psum_scatter(
            owner_rows[1].astype(jnp.bfloat16), "rep", scatter_dimension=1, tiled=True
        ).astype(jnp.float32),
        lax.psum_scatter(
            owner_rows[2].astype(jnp.bfloat16), "rep", scatter_dimension=1, tiled=True
        ).astype(jnp.float32),
        lax.psum_scatter(
            owner_rows[3].astype(jnp.bfloat16), "rep", scatter_dimension=1, tiled=True
        ).astype(jnp.float32),
        lax.psum_scatter(
            owner_rows[4].astype(jnp.bfloat16), "rep", scatter_dimension=0, tiled=True
        ).astype(jnp.float32),
        lax.psum_scatter(
            owner_rows[5].astype(jnp.bfloat16), "rep", scatter_dimension=1, tiled=True
        ).astype(jnp.float32),
        lax.psum_scatter(
            owner_rows[6].astype(jnp.bfloat16), "rep", scatter_dimension=1, tiled=True
        ).astype(jnp.float32),
        lax.psum_scatter(
            owner_rows[7].astype(jnp.bfloat16), "rep", scatter_dimension=1, tiled=True
        ).astype(jnp.float32),
        lax.psum_scatter(
            owner_rows[8].astype(jnp.bfloat16), "rep", scatter_dimension=1, tiled=True
        ).astype(jnp.float32),
        lax.psum_scatter(
            owner_rows[9].astype(jnp.bfloat16), "rep", scatter_dimension=0, tiled=True
        ).astype(jnp.float32),
    )
    all_summed = (
        lax.all_gather(replica_share[0].astype(jnp.bfloat16), "rep", axis=1, tiled=True).astype(
            jnp.float32
        ),
        lax.all_gather(replica_share[1].astype(jnp.bfloat16), "rep", axis=1, tiled=True).astype(
            jnp.float32
        ),
        lax.all_gather(replica_share[2].astype(jnp.bfloat16), "rep", axis=1, tiled=True).astype(
            jnp.float32
        ),
        lax.all_gather(replica_share[3].astype(jnp.bfloat16), "rep", axis=1, tiled=True).astype(
            jnp.float32
        ),
        lax.all_gather(replica_share[4].astype(jnp.bfloat16), "rep", axis=0, tiled=True).astype(
            jnp.float32
        ),
        lax.all_gather(replica_share[5].astype(jnp.bfloat16), "rep", axis=1, tiled=True).astype(
            jnp.float32
        ),
        lax.all_gather(replica_share[6].astype(jnp.bfloat16), "rep", axis=1, tiled=True).astype(
            jnp.float32
        ),
        lax.all_gather(replica_share[7].astype(jnp.bfloat16), "rep", axis=1, tiled=True).astype(
            jnp.float32
        ),
        lax.all_gather(replica_share[8].astype(jnp.bfloat16), "rep", axis=1, tiled=True).astype(
            jnp.float32
        ),
        lax.all_gather(replica_share[9].astype(jnp.bfloat16), "rep", axis=0, tiled=True).astype(
            jnp.float32
        ),
    )
    seg_summed = all_summed[:5]
    cls_summed = all_summed[5:]
    pos_total = lax.psum(pos_local, ("rep", "fsdp"))
    seg_mat_grad = jnp.concatenate(
        [seg_summed[0], seg_summed[1], seg_summed[2], seg_summed[3]], axis=1
    )
    cls_mat_grad = jnp.concatenate(
        [cls_summed[0], cls_summed[1], cls_summed[2], cls_summed[3]], axis=1
    )
    return (
        output_rows.astype(jnp.bfloat16),
        input_grad.astype(jnp.bfloat16),
        seg_mat_grad,
        seg_summed[4],
        cls_mat_grad,
        cls_summed[4],
        pos_total,
        loss_value,
    )


LINE = 4
PLANE = 4
CORES = 2
LANES = 128
GROUP = LINE * PLANE
LOW, WIDE = jnp.bfloat16, jnp.float32
MODEL = HEADS * HEAD_DIM
SPAN = 2 * LANES
TILE_START = (0, 1, 3, 4)


def line_pairs(apart):
    return [(source, (source + apart * PLANE) % GROUP) for source in range(GROUP)]


def plane_pairs(mask):
    return [(source, source ^ mask) for source in range(GROUP)]


def along_line(value, apart):
    return lax.ppermute(value, "fsdp", line_pairs(apart))


def in_plane(value, mask):
    return lax.ppermute(value, "fsdp", plane_pairs(mask))


def other_core(value):
    return lax.ppermute(value, "rep", [(0, 1), (1, 0)])


def after(value, *events):
    return lax.optimization_barrier((value,) + events)[0]


def together(*values):
    return tuple(lax.optimization_barrier(values))


def shape_of(dims, dtype=WIDE):
    return jax.ShapeDtypeStruct(dims, dtype)


def run_kernel(body, name, outs, where, blocks, arrays, scratch=(), far=(), flops=0):
    in_specs = [pl.BlockSpec(memory_space=pltpu.SMEM)]
    in_specs += [pl.BlockSpec(memory_space=pltpu.HBM)] * len(blocks)
    in_specs += [pl.BlockSpec(memory_space=pltpu.VMEM)] * len(arrays)
    spaces = [pltpu.HBM if at in far else pltpu.VMEM for at in range(len(outs))]
    moved = sum(x.size * x.dtype.itemsize for x in list(blocks) + list(arrays))
    moved += sum(math.prod(o.shape) * jnp.dtype(o.dtype).itemsize for o in outs)
    return pl.pallas_call(
        body,
        name=name,
        out_shape=tuple(outs),
        in_specs=in_specs,
        out_specs=tuple(pl.BlockSpec(memory_space=space) for space in spaces),
        scratch_shapes=list(scratch),
        cost_estimate=pl.CostEstimate(flops=flops, bytes_accessed=moved, transcendentals=0),
        compiler_params=pltpu.CompilerParams(vmem_limit_bytes=VMEM_BYTES),
    )(where, *blocks, *arrays)


VMEM_BYTES = 24 * 1024 * 1024
HALF = MODEL // CORES
FF_HALF = FF // CORES
OWN = MODEL // GROUP
QUARTER = 3 * SPAN + 2 * FF // LINE
QUARTER_HALF = QUARTER // CORES


def aligned(start):
    return pl.multiple_of(start, LANES)


def wait_all(copies):
    for copy in copies:
        copy.wait()


def run_copies(pairs, sems):
    copies = [
        pltpu.make_async_copy(source, target, sems.at[at])
        for at, (source, target) in enumerate(pairs)
    ]
    for copy in copies:
        copy.start()
    wait_all(copies)


FIRST = 4 * HALF + LANES
OWN_CUT = FIRST + FF_HALF // 2
LINE_CUTS = (7 * LANES, FF_HALF // 2, FF_HALF // 2)
WIDTHS = (FIRST, FF_HALF, FF_HALF)


def group_pieces(group, refs):
    own, rest = refs[:LINE], refs[LINE:]
    own_x, own_y, far_x, far_y, line_x, line_y, late_x, late_y = rest
    width, cut = WIDTHS[group], LINE_CUTS[group]
    start = sum(WIDTHS[:group])
    if group == 0:
        bases = (sum(WIDTHS) - OWN_CUT, OWN_CUT)
    else:
        before, before_cut = WIDTHS[group - 1], LINE_CUTS[group - 1]
        bases = (2 * before - before_cut, before + before_cut)
    pieces = {(0, step): [(own[step], 0, 0, width)] for step in range(LINE)}
    for mask, whole, line, base in ((1, own_x, line_x, bases[0]), (2, own_y, line_y, bases[1])):
        pieces[mask, 0] = [(whole, start, 0, width)]
        for step in range(1, LINE):
            pieces[mask, step] = [(line, base + (step - 1) * width, 0, width)]
    middle = min(max(OWN_CUT - start, 0), width)
    far = []
    if middle > 0:
        far.append((far_y, start, 0, middle))
    if middle < width:
        far.append((far_x, start + middle - OWN_CUT, middle, width))
    pieces[3, 0] = far
    pieces[3, 1] = [(late_y, 0, 0, width)]
    pieces[3, 2] = [(late_y, width, 0, cut), (late_x, 0, cut, width)]
    pieces[3, 3] = [(late_x, width - cut, 0, width)]
    return pieces


def gather_group(where, group, refs, targets):
    line_at, plane_at = where[0], where[1]
    for (mask, step), parts in group_pieces(group, refs).items():
        chip = (line_at + LINE - step) % LINE * PLANE + (plane_at ^ mask)
        for whole, first, last in targets:
            for ref, offset, begin, end in parts:
                low, high = max(first, begin), min(last, end)
                if low < high:
                    source = slice(offset + low - begin, offset + high - begin)
                    whole[chip, :, low - first : high - first] = ref[:, source]


def gather_blocks(where, refs, base, width, targets):
    line_at, plane_at = where[0], where[1]
    half = LINE // 2
    for mask in range(PLANE):
        for step in range(LINE):
            if mask == 0:
                ref, offset = refs[step], 0
            elif mask == 3:
                ref = refs[LINE + 3] if step < half else refs[LINE + 2]
                offset = step % half * width
            else:
                ref, offset = refs[LINE + mask - 1], base + step * width
            chip = (line_at + LINE - step) % LINE * PLANE + (plane_at ^ mask)
            for whole, first, last in targets:
                whole[chip] = ref[:, offset + first : offset + last]


def whole_rows(ref):
    value = ref[...]
    return value.reshape(value.shape[0] * value.shape[1], value.shape[2])


def prepare_first_kernel(where, seg, seg_vec, cls_vec, flags, out, live_out, sems):
    core_at = where[2]
    pairs = []
    for piece in range(4):
        source = seg.at[:, pl.ds(aligned(piece * MODEL + core_at * HALF), HALF)]
        pairs.append((source, out.at[:, piece * HALF : (piece + 1) * HALF]))
    run_copies(pairs, sems)
    size = seg_vec.shape[0]
    vecs = [vec[...].astype(WIDE).reshape(1, size) for vec in (seg_vec, cls_vec)]
    lines = -(-size // LANES)
    block = jnp.zeros((OWN, LANES), WIDE)
    row_at = lax.broadcasted_iota(jnp.int32, (OWN, LANES), 0)
    for which in range(2):
        for line in range(lines):
            width = min(LANES, size - line * LANES)
            value = vecs[which][:, line * LANES : line * LANES + width]
            if width < LANES:
                value = jnp.concatenate([value, jnp.zeros((1, LANES - width), WIDE)], axis=1)
            block = jnp.where(row_at == which * lines + line, value, block)
    live = flags[...].astype(WIDE).reshape(1, SEG)
    live_out[...] = live
    count = jnp.sum(live, axis=1, keepdims=True)
    block = jnp.where(row_at == 2 * lines, count, block)
    out[:, 4 * HALF :] = block.astype(LOW)


def prepare_rest_kernel(where, seg, cls, *refs):
    second_out, third_out = refs[:2]
    step_outs, out_half, order_out = refs[2 : 2 + LINE], refs[2 + LINE], refs[3 + LINE]
    quarters, sems = refs[4 + LINE :]
    line_at, plane_at, core_at = where[0], where[1], where[2]
    start = core_at * FF_HALF
    pairs = [
        (seg.at[:, pl.ds(aligned(4 * MODEL + start), FF_HALF)], second_out),
        (seg.at[:, pl.ds(aligned(4 * MODEL + FF + start), FF_HALF)], third_out),
        (cls.at[:, pl.ds(aligned(3 * MODEL + core_at * HALF), HALF)], out_half),
    ]
    part = FF // LINE
    for at in range(LINE):
        first = TILE_START[at] * LANES
        plan = [(piece * MODEL + first, SPAN, piece * SPAN) for piece in range(3)]
        plan += [
            (4 * MODEL + piece * FF + at * part, part, 3 * SPAN + piece * part)
            for piece in range(2)
        ]
        for source, size, target in plan:
            pairs.append(
                (
                    cls.at[:, source : source + size],
                    quarters.at[at, :, target : target + size],
                )
            )
    run_copies(pairs, sems)
    lanes = pl.ds(aligned(core_at * QUARTER_HALF), QUARTER_HALF)
    for step, out in enumerate(step_outs):
        out[...] = quarters[(line_at + step) % LINE, :, lanes]
    column = lax.broadcasted_iota(jnp.int32, (1, SPAN), 1)
    feature = lax.broadcasted_iota(jnp.int32, (MODEL, SPAN), 0)
    turn = sum((column >= OWN * step).astype(jnp.int32) for step in range(1, LINE))
    held = column - OWN * turn
    turn = (line_at + turn) % LINE
    for mask in range(PLANE):
        source = (turn * PLANE + (plane_at ^ mask)) * OWN + held
        source = jnp.where(column < OWN * LINE, source, -1)
        order_out[:, mask * SPAN : (mask + 1) * SPAN] = (feature == source).astype(LOW)


def prepare_kernel(where, seg, cls, *refs):
    (seg_vec, cls_vec, flags, first_out, live_out), refs = refs[:5], refs[5:]
    rest, (first_sems, quarters, sems) = refs[:-3], refs[-3:]
    prepare_first_kernel(where, seg, seg_vec, cls_vec, flags, first_out, live_out, first_sems)
    prepare_rest_kernel(where, seg, cls, *rest, quarters, sems)


def lane_mask(rows, head):
    lane = lax.broadcasted_iota(jnp.int32, (rows, LANES), 1)
    return (lane < HEAD_DIM) if head == 0 else (lane >= HEAD_DIM)


def masked(value, mask):
    return jnp.where(mask, value, jnp.zeros_like(value))


def head_probabilities(query, key, allowed):
    scores = product_right(query, key) * HEAD_DIM ** (-0.5)
    scores = jnp.where(allowed, scores, MASK_FILL)
    raised = jnp.exp(scores - jnp.max(scores, axis=-1, keepdims=True))
    return raised / jnp.sum(raised, axis=-1, keepdims=True)


def attend_tiles(qkv, width, allowed):
    rows = qkv.shape[0]
    mixed = []
    for tile in range(width // LANES):
        at = tile * LANES
        query, key, value = (
            qkv[:, piece * width + at : piece * width + at + LANES] for piece in range(3)
        )
        total = jnp.zeros((rows, LANES), WIDE)
        for head in range(2):
            mask = lane_mask(rows, head)
            weights = head_probabilities(masked(query, mask), key, allowed).astype(LOW)
            total = total + product_plain(weights, masked(value, mask))
        mixed.append(total.astype(LOW))
    return mixed


def attend_tiles_back(qkv, grad_mixed, width, allowed):
    rows = qkv.shape[0]
    scale = HEAD_DIM ** (-0.5)
    results = ([], [], [])
    for tile in range(width // LANES):
        at = tile * LANES
        query, key, value = (
            qkv[:, piece * width + at : piece * width + at + LANES] for piece in range(3)
        )
        grad = grad_mixed[:, at : at + LANES]
        totals = [jnp.zeros((rows, LANES), WIDE) for _ in range(3)]
        for head in range(2):
            mask = lane_mask(rows, head)
            query_low, key_low, grad_low = (masked(x, mask) for x in (query, key, grad))
            chance = head_probabilities(query_low, key, allowed)
            grad_chance = product_right(grad_low, value)
            inner = jnp.sum(grad_chance * chance, axis=-1, keepdims=True)
            grad_scores = (chance * (grad_chance - inner)).astype(LOW)
            totals[0] = totals[0] + product_plain(grad_scores, key_low)
            totals[1] = totals[1] + product_left(grad_scores, query_low)
            totals[2] = totals[2] + product_left(chance.astype(LOW), grad_low)
        results[0].append((totals[0] * scale).astype(LOW))
        results[1].append((totals[1] * scale).astype(LOW))
        results[2].append(totals[2].astype(LOW))
    return results[0] + results[1] + results[2]


def token_allowed(live_row):
    shape = (SEG, SEG)
    same = lax.broadcasted_iota(jnp.int32, shape, 0) == lax.broadcasted_iota(jnp.int32, shape, 1)
    return (live_row > 0.5) | same


def qkv_kernel(where, *refs):
    blocks = refs[:12]
    hidden, hidden_got, live_row, live_got, order = refs[12:17]
    weight, out_low, out_high, qkv_out, mixed_out = refs[17:22]
    vectors_out, count_out, ordered_out = refs[22:25]
    vec_rows, flat, inputs, out_half = refs[25:]
    core_at = where[2]
    gather_group(
        where,
        0,
        blocks,
        (
            (weight, 0, 3 * HALF),
            (out_half, 3 * HALF, 4 * HALF),
            (vec_rows, 4 * HALF, 4 * HALF + LANES),
        ),
    )
    out_low[...] = out_half[: GROUP // 2]
    out_high[...] = out_half[GROUP // 2 :]
    piece = (8 * MODEL + FF) // GROUP
    lines = -(-piece // LANES)
    count = jnp.zeros((1, LANES), WIDE)
    for chip in range(GROUP):
        rows = vec_rows[chip, 0:16, :].astype(WIDE)
        for block in range(2):
            joined = jnp.concatenate(
                [rows[block * lines + r : block * lines + r + 1] for r in range(lines)], axis=1
            )
            flat[block : block + 1, chip * piece : (chip + 1) * piece] = joined[:, :piece]
        count = count + rows[2 * lines : 2 * lines + 1]
    rows_each = (8 * MODEL + FF) // MODEL
    for block in range(2):
        for row in range(rows_each):
            vectors_out[block * rows_each + row : block * rows_each + row + 1, :] = flat[
                block : block + 1, row * MODEL : (row + 1) * MODEL
            ]
    count_out[...] = jnp.broadcast_to(count, count_out.shape)
    inputs[:SEG] = hidden[...]
    inputs[SEG:] = hidden_got[...]
    projected = product_plain(inputs[...], whole_rows(weight))
    lanes = pl.ds(aligned(core_at * HALF), HALF)
    qkv_out[:, :HALF] = (projected[:, :HALF] + vectors_out[0:1, lanes]).astype(LOW)
    qkv_out[:, HALF : 2 * HALF] = projected[:, HALF : 2 * HALF].astype(LOW)
    qkv_out[:, 2 * HALF :] = (projected[:, 2 * HALF :] + vectors_out[1:2, lanes]).astype(LOW)
    for part, live in enumerate((live_row, live_got)):
        rows = slice(part * SEG, (part + 1) * SEG)
        tiles = attend_tiles(qkv_out[rows, :], HALF, token_allowed(live[...]))
        for tile, value in enumerate(tiles):
            mixed_out[rows, tile * LANES : (tile + 1) * LANES] = value
    ordered_out[...] = product_plain(inputs[...], order[...]).astype(LOW)


def norm_rows(summed):
    row_mean = jnp.mean(summed, axis=-1, keepdims=True)
    centered = summed - row_mean
    inv_dev = lax.rsqrt(jnp.mean(centered * centered, axis=-1, keepdims=True) + NORM_EPS)
    return centered * inv_dev, inv_dev


def norm_rows_back(grad_out, normed, inv_dev, gain):
    scaled = grad_out * gain
    mean_one = jnp.mean(scaled, axis=-1, keepdims=True)
    mean_two = jnp.mean(scaled * normed, axis=-1, keepdims=True)
    return inv_dev * (scaled - mean_one - normed * mean_two)


def column_sum(value):
    return jnp.sum(value.astype(WIDE), axis=0, keepdims=True)


def four_rows(vectors, first):
    return jnp.concatenate([vectors[first + at : first + at + 1, :] for at in range(4)], axis=1)


def gelu_both(before):
    half = 0.5 * (1.0 + lax.erf(before * SQRT_HALF))
    slope = half + before * jnp.exp(-0.5 * before * before) * INV_SQRT_TWO_PI
    return before * half, slope


def out_kernel(where, hidden, mixed, mixed_got, low, high, low_got, high_got, *refs):
    vectors, order, full_out, ordered_out, normed_out, inv_out, low_out, mixed_full = refs
    core_at = where[2]
    own, other = aligned(core_at * HALF), aligned((1 - core_at) * HALF)
    rows = MODEL // 2
    full_out[:rows, pl.ds(own, HALF)] = whole_rows(low)
    full_out[rows:, pl.ds(own, HALF)] = whole_rows(high)
    full_out[:rows, pl.ds(other, HALF)] = whole_rows(low_got)
    full_out[rows:, pl.ds(other, HALF)] = whole_rows(high_got)
    mixed_full[:, pl.ds(own, HALF)] = mixed[...]
    mixed_full[:SEG, pl.ds(other, HALF)] = mixed_got[SEG:, :]
    mixed_full[SEG:, pl.ds(other, HALF)] = mixed_got[:SEG, :]
    branch = product_plain(mixed_full[:SEG, :], full_out[...])
    normed, inv_dev = norm_rows(hidden[...].astype(WIDE) + branch + vectors[2:3, :])
    normed_out[...] = normed
    inv_out[...] = inv_dev
    low_out[...] = (normed * vectors[4:5, :] + vectors[5:6, :]).astype(LOW)
    ordered_out[...] = product_plain(mixed_full[...], order[...]).astype(LOW)


def up_kernel(where, *refs):
    blocks = refs[:12]
    low, low_got, vectors = refs[12:15]
    weight, act_out, slope_out, both = refs[15:]
    core_at = where[2]
    gather_group(where, 1, blocks, ((weight, 0, FF_HALF),))
    both[:SEG] = low[...]
    both[SEG:] = low_got[...]
    for at in range(FF_HALF // MODEL):
        columns = slice(at * MODEL, (at + 1) * MODEL)
        held = weight[:, :, columns]
        before = product_plain(both[...], held.reshape(MODEL, MODEL))
        bias = vectors[pl.ds(8 + core_at * (FF_HALF // MODEL) + at, 1), :]
        value, slope = gelu_both(before + bias)
        act_out[:, columns] = value.astype(LOW)
        slope_out[:, columns] = slope


def down_kernel(where, *refs):
    blocks, act = refs[:12], refs[12]
    weight, own_out, send_out = refs[13:]
    gather_group(where, 2, blocks, ((weight, 0, FF_HALF),))
    partial = product_right(act[...], whole_rows(weight))
    own_out[...] = partial[:SEG]
    send_out[...] = partial[SEG:]


def seg_rows_kernel(where, *refs):
    own, got, normed_first, vectors, targets, live, seg_pos = refs[:7]
    normed_out, inv_out, diff_out, rows_out, head_out = refs[7:]
    doc, number = where[3], where[4]
    first = normed_first[...] * vectors[4:5, :] + vectors[5:6, :]
    normed, inv_dev = norm_rows(first + own[...] + got[...] + vectors[3:4, :])
    normed_out[...] = normed
    inv_out[...] = inv_dev
    rows = normed * vectors[6:7, :] + vectors[7:8, :]
    shape = (SEG, SEG)
    same = lax.broadcasted_iota(jnp.int32, shape, 0) == lax.broadcasted_iota(jnp.int32, shape, 1)
    live_rows = jnp.sum(jnp.where(same, live[...], 0.0), axis=1, keepdims=True)
    target_rows = targets[...].astype(WIDE)
    output = rows * live_rows
    rows_out[...] = output
    diff = (output - target_rows) * live_rows
    row_at = lax.broadcasted_iota(jnp.int32, (SEG, 1), 0)
    diff = jnp.where(row_at > 0, diff, 0.0)
    diff_out[...] = diff
    table = seg_pos[...].astype(WIDE)
    chosen = lax.broadcasted_iota(jnp.int32, table.shape, 0) == number
    position = jnp.sum(jnp.where(chosen, table, 0.0), axis=0, keepdims=True)
    head_out[:, :MODEL] = rows[0:1, :] + position
    head_out[:, MODEL : 2 * MODEL] = target_rows[0:1, :]
    square = jnp.sum(column_sum(diff * diff), axis=1, keepdims=True)
    lane = lax.broadcasted_iota(jnp.int32, (1, LANES), 1)
    facts = jnp.where(lane == 0, live_rows[0:1, :], 0.0)
    facts = jnp.where(lane == 1, doc.astype(WIDE), facts)
    facts = jnp.where(lane == 2, number.astype(WIDE), facts)
    facts = jnp.where(lane == 3, square, facts)
    head_out[:, 2 * MODEL :] = facts


def second_norm_kernel(where, *refs):
    diff, count, normed, inv_dev, vectors, first, first_got, order = refs[:8]
    grad_out, low_out, sums_out, ordered_out, both = refs[8:]
    grad_top = diff[...] * ((SEG * GROUP * CORES) / count[0:1, 0:1])
    normed_rows = normed[...]
    grad = norm_rows_back(grad_top, normed_rows, inv_dev[...], vectors[6:7, :])
    low = grad.astype(LOW)
    grad_out[...] = grad
    low_out[...] = low
    sums_out[0:1, :] = column_sum(low)
    sums_out[1:2, :] = column_sum(grad_top * normed_rows)
    sums_out[2:3, :] = column_sum(grad_top)
    both[:SEG] = first[...]
    both[SEG:] = first_got[...]
    ordered_out[...] = product_plain(both[...], order[...]).astype(LOW)


def mlp_back_kernel(where, *refs):
    low, low_got, down_weight, up_weight, slope = refs[:5]
    pre_out, own_out, send_out, sums_out, both = refs[5:]
    both[:SEG] = low[...]
    both[SEG:] = low_got[...]
    for at in range(FF_HALF // MODEL):
        columns = slice(at * MODEL, (at + 1) * MODEL)
        held = down_weight[:, :, columns]
        before = product_plain(both[...], held.reshape(MODEL, MODEL))
        pre = (before * slope[:, columns]).astype(LOW)
        pre_out[:, columns] = pre
        sums_out[at : at + 1, :] = column_sum(pre)
    partial = product_right(pre_out[...], whole_rows(up_weight))
    own_out[...] = partial[:SEG]
    send_out[...] = partial[SEG:]


def scatter_parts(where, parts, outs, sems):
    line_at, plane_at = where[0], where[1]
    far_low, far_high, to_x, to_y, kept = outs
    half = LINE // 2
    copies = []
    for mask in range(PLANE):
        for step in range(LINE):
            source = parts.at[(line_at + step) % LINE * PLANE + (plane_at ^ mask)]
            if mask == 3:
                target = far_low.at[step] if step < half else far_high.at[step - half]
            else:
                target = (kept, to_x, to_y)[mask].at[step]
            copies.append(pltpu.make_async_copy(source, target, sems.at[len(copies)]))
    for copy in copies:
        copy.start()
    wait_all(copies)


def mlp_products(refs, masks, both, store):
    first, second, second_got, pre, act, order = refs
    both[:SEG] = second[...]
    both[SEG:] = second_got[...]
    for mask in masks:
        lanes = slice(mask * SPAN, (mask + 1) * SPAN)
        turned = product_plain(both[...], order[:, lanes]).astype(LOW)
        for at, (left, right) in enumerate(((first[:, lanes], pre), (turned, act))):
            for piece in range(FF_HALF // MODEL):
                start = piece * MODEL
                product = product_left(left, right[:, start : start + MODEL])
                product = product[: LINE * OWN].astype(LOW).reshape(LINE, OWN, MODEL)
                target = at * FF_HALF + start
                store(mask, slice(target, target + MODEL), product)


def mlp_far_kernel(where, *refs):
    low_out, high_out, both = refs[6:]
    half = LINE // 2

    def store(mask, columns, product):
        low_out[:, :, columns] = product[:half]
        high_out[:, :, columns] = product[half:]

    mlp_products(refs[:6], (3,), both, store)


def mlp_near_kernel(where, *refs):
    outs, both = refs[6:9], refs[9]

    def store(mask, columns, product):
        outs[mask - 1][:, :, columns] = product

    mlp_products(refs[:6], (1, 2, 0), both, store)


def attn_product(where, refs, mask, piece):
    hidden, mixed, proj, branch, got = refs
    lanes = slice(mask * SPAN, (mask + 1) * SPAN)
    if piece < 3:
        right = proj[:, piece * HALF : (piece + 1) * HALF]
        product = product_left(hidden[:, lanes], right)
    else:
        own = branch[:, pl.ds(aligned(where[2] * HALF), HALF)]
        product = product_left(mixed[:SEG, lanes], own)
        product = product + product_left(mixed[SEG:, lanes], got[:, HALF:])
    return product[: LINE * OWN].astype(LOW).reshape(LINE, OWN, HALF)


def attn_far_kernel(where, *refs):
    low_out, high_out = refs[5:]
    half = LINE // 2
    for piece in range(4):
        columns = slice(piece * HALF, (piece + 1) * HALF)
        product = attn_product(where, refs[:5], 3, piece)
        low_out[:, :, columns] = product[:half]
        high_out[:, :, columns] = product[half:]


def attn_near_kernel(where, *refs):
    proj, (top_row, out_rows, live_row) = refs[2], refs[5:8]
    weight, sums_first, sums_second, sums_up, head_top, head_normed, data = refs[8:15]
    x_out, y_out, kept_out, output_out, own_out, send_out, payload_out, rows = refs[15:]
    core_at = where[2]
    partial = product_right(proj[...], whole_rows(weight))
    own_out[...] = partial[:SEG]
    send_out[...] = partial[SEG:]
    row_at = lax.broadcasted_iota(jnp.int32, (SEG, 1), 0)
    output = jnp.where(row_at == 0, top_row[...] * live_row[:, 0:1], out_rows[...])
    output_out[...] = output.astype(LOW)
    for mask, out in ((1, x_out), (2, y_out), (0, kept_out)):
        for piece in range(4):
            columns = slice(piece * HALF, (piece + 1) * HALF)
            out[:, :, columns] = attn_product(where, refs[:5], mask, piece)
    lanes = pl.ds(aligned(core_at * HALF), HALF)
    rows[...] = jnp.zeros_like(rows)
    rows[0:12, :] = data[0:12, :]
    rows[12:13, lanes] = column_sum(proj[:, :HALF])
    rows[13:14, lanes] = column_sum(proj[:, 2 * HALF :])
    rows[14:15, :] = sums_first[0:1, :]
    rows[15:16, :] = sums_second[0:1, :] + data[2:3, :]
    rows[16:18, :] = sums_first[1:3, :]
    rows[18:19, :] = sums_second[1:2, :] + head_top[...] * head_normed[0:1, :]
    rows[19:20, :] = sums_second[2:3, :] + head_top[...]
    for at in range(FF_HALF // MODEL):
        total = sums_up[at : at + 1, :] + data[4 + 2 * at : 5 + 2 * at, :]
        total = total + data[5 + 2 * at : 6 + 2 * at, :]
        rows[pl.ds(20 + core_at * (FF_HALF // MODEL) + at, 1), :] = total
    payload_out[...] = rows[...].astype(LOW)


def fold_kernel(where, kept, got_x, got_y, *refs):
    extra, own_out, sent = refs[: -LINE], refs[-LINE], refs[1 - LINE :]
    rows = kept.shape[1]
    for step in range(LINE):
        total = kept[step].astype(WIDE) + got_x[step].astype(WIDE) + got_y[step].astype(WIDE)
        if step == 0:
            own_out[...] = total
            continue
        out = sent[step - 1]
        out[:rows, :] = total.astype(LOW)
        if extra:
            out[rows:, :] = jnp.zeros_like(out[rows:, :])
            out[rows:, : extra[0].shape[1]] = extra[0][...]


def reduce_far(parts):
    return together(in_plane(parts[0], 2), in_plane(parts[1], 1))


def reduce_add(where, parts, far):
    shape = parts[2].shape
    return run_kernel(
        add_far_kernel,
        "add_far",
        [shape_of(shape, LOW)] * 2,
        where,
        (),
        tuple(far) + (parts[2], parts[3]),
    )


def reduce_fold(where, kept, got, *extra):
    _, rows, columns = kept.shape
    more = sum(value.shape[0] for value in extra)
    return run_kernel(
        fold_kernel,
        "fold",
        [shape_of((rows, columns))] + [shape_of((rows + more, columns), LOW)] * (LINE - 1),
        where,
        (),
        (kept,) + tuple(got) + extra,
    )


def reduce_line(own, pieces):
    total = own
    for piece in pieces:
        total = total + piece[: own.shape[0]].astype(WIDE)
    return total


def head_back_kernel(where, *refs):
    grad, grad_got, down_weight, up_weight, slope, act, low, low_got = refs[:8]
    own_out, send_out, data_out = refs[8:]
    few = 16
    row_at = lax.broadcasted_iota(jnp.int32, (few, 1), 0)

    def two_rows(first, second):
        return jnp.where(row_at == 0, first, jnp.where(row_at == 1, second, 0.0))

    second = two_rows(grad[...], grad_got[...]).astype(LOW)
    data_out[0:1, :] = low[0:1, :].astype(WIDE)
    data_out[1:2, :] = low_got[0:1, :].astype(WIDE)
    data_out[2:4, :] = second[0:2].astype(WIDE)
    partial = jnp.zeros((few, MODEL), WIDE)
    for at in range(FF_HALF // MODEL):
        columns = slice(at * MODEL, (at + 1) * MODEL)
        before = product_plain(second, down_weight[:, :, columns].reshape(MODEL, MODEL))
        slopes = two_rows(slope[0:1, columns], slope[SEG : SEG + 1, columns])
        pre = (before * slopes).astype(LOW)
        partial = partial + product_right(pre, up_weight[:, :, columns].reshape(MODEL, MODEL))
        data_out[4 + 2 * at : 6 + 2 * at, :] = pre[0:2].astype(WIDE)
        data_out[8 + 2 * at : 9 + 2 * at, :] = act[0:1, columns].astype(WIDE)
        data_out[9 + 2 * at : 10 + 2 * at, :] = act[SEG : SEG + 1, columns].astype(WIDE)
    own_out[...] = partial[0:1]
    send_out[...] = partial[1:2]


def first_norm_kernel(where, *refs):
    second_grad, own, got, head_grad, head_own, head_got = refs[:6]
    normed_rows, inv_dev, vectors, out_weight = refs[6:10]
    grad_out, branch_out, mixed_out, send_out, sums_out = refs[10:]
    core_at = where[2]
    grad_rows = second_grad[...] + own[...] + got[...]
    head = head_grad[...] + head_own[...] + head_got[...]
    row_at = lax.broadcasted_iota(jnp.int32, (SEG, 1), 0)
    grad_rows = jnp.where(row_at == 0, head, grad_rows)
    normed = normed_rows[...]
    grad = norm_rows_back(grad_rows, normed, inv_dev[...], vectors[4:5, :])
    grad_out[...] = grad
    branch = grad.astype(LOW)
    branch_out[...] = branch
    mixed_out[...] = product_right(branch, out_weight[...]).astype(LOW)
    other = pl.ds(aligned((1 - core_at) * HALF), HALF)
    send_out[:, :HALF] = mixed_out[:, other]
    send_out[:, HALF:] = branch_out[:, other]
    sums_out[0:1, :] = column_sum(branch)
    sums_out[1:2, :] = column_sum(grad_rows * normed)
    sums_out[2:3, :] = column_sum(grad_rows)


def attn_back_kernel(where, *refs):
    qkv, mixed_grad, got, live_row, live_got, proj_out = refs
    core_at = where[2]
    lanes = pl.ds(aligned(core_at * HALF), HALF)
    for part, live in enumerate((live_row, live_got)):
        at = slice(part * SEG, (part + 1) * SEG)
        grad = mixed_grad[:, lanes] if part == 0 else got[:, :HALF]
        pieces = attend_tiles_back(qkv[at, :], grad, HALF, token_allowed(live[...]))
        for tile, value in enumerate(pieces):
            proj_out[at, tile * LANES : (tile + 1) * LANES] = value


def cls_gather_kernel(where, *refs):
    blocks = refs[:8]
    own_out, from_x, from_y, far_x = refs[8], refs[4], refs[5], refs[6]
    weight_out, out_rows = refs[9:]
    plane_at = where[1]
    gather_blocks(where, blocks, 0, QUARTER_HALF, ((weight_out, 0, QUARTER_HALF),))
    first = LINE * QUARTER_HALF
    out_rows[plane_at] = own_out[...]
    out_rows[plane_at ^ 1] = from_x[:, first : first + HALF]
    out_rows[plane_at ^ 2] = from_y[:, first : first + HALF]
    first = LINE // 2 * QUARTER_HALF
    out_rows[plane_at ^ 3] = far_x[:, first : first + HALF]


def cls_weight_kernel(where, own, got, out_half, out_got, weight_out, out_full):
    line_at, core_at = where[0], where[2]
    out_full[...] = jnp.zeros_like(out_full)
    for value, part, core in ((own, out_half, core_at), (got, out_got, 1 - core_at)):
        weight_out[:, :, pl.ds(aligned(core * QUARTER_HALF), QUARTER_HALF)] = value[...]
        rows = part[...].reshape(3, HEAD_DIM, HALF)
        out_full[pl.ds(line_at % 2, 3), :, pl.ds(aligned(core * HALF), HALF)] = rows


def add_far_kernel(where, far_low, far_high, to_x, to_y, x_out, y_out):
    half = LINE // 2
    x_out[:half] = to_x[:half] + far_low[...]
    x_out[half:] = to_x[half:]
    y_out[:half] = to_y[:half]
    y_out[half:] = to_y[half:] + far_high[...]


def row_from_column(column, size):
    shape = (size, size)
    same = lax.broadcasted_iota(jnp.int32, shape, 0) == lax.broadcasted_iota(jnp.int32, shape, 1)
    return jnp.sum(jnp.where(same, column, 0.0), axis=0, keepdims=True)


def head_allowed(heads):
    facts = heads[:, 2 * MODEL :]
    live, doc = facts[:, 0:1], facts[:, 1:2]
    shape = (GROUP, GROUP)
    same = lax.broadcasted_iota(jnp.int32, shape, 0) == lax.broadcasted_iota(jnp.int32, shape, 1)
    live_row, doc_row = row_from_column(live, GROUP), row_from_column(doc, GROUP)
    return ((live_row > 0.5) & (doc == doc_row)) | same


def quarter_mask(quarter):
    lane = lax.broadcasted_iota(jnp.int32, (GROUP, SPAN), 1)
    first = (quarter % 2) * HEAD_DIM
    return (lane >= first) & (lane < first + 3 * HEAD_DIM)


def quarter_piece(vectors, row, quarter):
    value = jnp.zeros((1, SPAN), WIDE)
    for at in range(LINE):
        first = TILE_START[at] * LANES
        value = jnp.where(quarter == at, vectors[row : row + 1, first : first + SPAN], value)
    return value


def cls_attend_kernel(where, *refs):
    stacks, vectors, weight, out_weight = refs[:4], refs[4], refs[5], refs[6]
    heads_out, qkv_out, mixed_out, part_out = refs[7:]
    line_at, plane_at = where[0], where[1]
    for step, stack in enumerate(stacks):
        for mask in range(PLANE):
            row = (line_at + LINE - step) % LINE * PLANE + (plane_at ^ mask)
            heads_out[pl.ds(row, 1), :] = stack[mask : mask + 1, :]
    heads = heads_out[...]
    inputs = heads[:, :MODEL].astype(LOW)
    projected = product_plain(inputs, weight[:, : 3 * SPAN])
    query = projected[:, :SPAN] + quarter_piece(vectors, 12, line_at)
    value = projected[:, 2 * SPAN :] + quarter_piece(vectors, 13, line_at)
    qkv_out[:, :SPAN] = query.astype(LOW)
    qkv_out[:, SPAN : 2 * SPAN] = projected[:, SPAN : 2 * SPAN].astype(LOW)
    qkv_out[:, 2 * SPAN :] = value.astype(LOW)
    mixed = attend_tiles(qkv_out[...], SPAN, head_allowed(heads))
    mixed = masked(jnp.concatenate(mixed, axis=1), quarter_mask(line_at))
    mixed_out[...] = mixed
    part_out[...] = product_plain(mixed, out_weight[...])


def cls_mlp_kernel(where, *refs):
    heads, own, got_one, got_two, got_three, vectors, weight = refs[:7]
    normed_out, inv_out, low_out, act_out, slope_out, part_out = refs[7:]
    line_at = where[0]
    branch = own[...] + got_one[...] + got_two[...] + got_three[...]
    normed, inv_dev = norm_rows(heads[:, :MODEL] + branch + vectors[14:15, :])
    normed_out[...] = normed
    inv_out[...] = inv_dev
    low = (normed * vectors[16:17, :] + vectors[17:18, :]).astype(LOW)
    low_out[...] = low
    part = FF // LINE
    first = 3 * SPAN
    bias = vectors[pl.ds(20 + line_at, 1), :]
    before = product_plain(low, weight[:, first : first + part]) + bias
    value, slope = gelu_both(before)
    act = value.astype(LOW)
    act_out[...] = act
    slope_out[...] = slope
    part_out[...] = product_right(act, weight[:, first + part :])


def cls_top_kernel(where, *refs):
    heads, own, got_one, got_two, got_three, vectors, weight = refs[:7]
    normed_first, count, slope = refs[7:10]
    top_out, square_out, grad_out, second_out, pre_out, part_out, sums_out = refs[10:17]
    held = refs[17]
    rank = where[0] * PLANE + where[1]
    first = normed_first[...] * vectors[16:17, :] + vectors[17:18, :]
    down = own[...] + got_one[...] + got_two[...] + got_three[...]
    normed, inv_dev = norm_rows(first + down + vectors[15:16, :])
    rows = normed * vectors[18:19, :] + vectors[19:20, :]
    held[...] = rows
    top_out[...] = held[pl.ds(rank, 1), :]
    facts = heads[:, 2 * MODEL :]
    live = facts[:, 0:1]
    diff = (rows * live - heads[:, MODEL : 2 * MODEL]) * live
    square = jnp.sum(column_sum(diff * diff), axis=1, keepdims=True)
    square = square + jnp.sum(facts[:, 3:4], axis=0, keepdims=True)
    square_out[...] = jnp.broadcast_to(square, square_out.shape)
    grad_top = diff * ((SEG * GROUP * CORES) / count[0:1, 0:1])
    grad = norm_rows_back(grad_top, normed, inv_dev, vectors[18:19, :])
    sums_out[0:1, :] = column_sum(grad_top * normed)
    sums_out[1:2, :] = column_sum(grad_top)
    grad_out[...] = grad
    second = grad.astype(LOW)
    second_out[...] = second
    part = FF // LINE
    at = 3 * SPAN
    pre = (product_plain(second, weight[:, at + part :]) * slope[...]).astype(LOW)
    pre_out[...] = pre
    part_out[...] = product_right(pre, weight[:, at : at + part])


def cls_attend_back_kernel(where, *refs):
    heads, own, got_one, got_two, got_three, vectors, weight, out_weight = refs[:8]
    grad_in, normed_first, inv_first, qkv = refs[8:12]
    grad_out, branch_out, proj_out, part_out, sums_out = refs[12:]
    line_at = where[0]
    grad_first = grad_in[...] + own[...] + got_one[...] + got_two[...] + got_three[...]
    normed = normed_first[...]
    grad = norm_rows_back(grad_first, normed, inv_first[...], vectors[16:17, :])
    sums_out[0:1, :] = column_sum(grad_first * normed)
    sums_out[1:2, :] = column_sum(grad_first)
    grad_out[...] = grad
    branch = grad.astype(LOW)
    branch_out[...] = branch
    mask = quarter_mask(line_at)
    mixed_grad = masked(product_right(branch, out_weight[...]).astype(LOW), mask)
    pieces = attend_tiles_back(qkv[...], mixed_grad, SPAN, head_allowed(heads[...]))
    tiles = SPAN // LANES
    for piece in range(3):
        joined = jnp.concatenate(pieces[piece * tiles : (piece + 1) * tiles], axis=1)
        proj_out[:, piece * SPAN : (piece + 1) * SPAN] = masked(joined, mask)
    part_out[...] = product_right(proj_out[...], weight[:, : 3 * SPAN])


def cls_end_kernel(where, *refs):
    heads, grad, own, got_one, got_two, got_three = refs[:6]
    square, sums_back, sums_top = refs[6:9]
    normed_second, inv_second, vectors = refs[9:12]
    row_out, second_out, shared_out, held = refs[12:]
    rank = where[0] * PLANE + where[1]
    total = grad[...] + own[...] + got_one[...] + got_two[...] + got_three[...]
    held[...] = total
    row = held[pl.ds(rank, 1), :]
    row_out[...] = row
    second_out[...] = norm_rows_back(
        row, normed_second[0:1, :], inv_second[0:1, :], vectors[6:7, :]
    )
    number = row_from_column(heads[:, 2 * MODEL + 2 : 2 * MODEL + 3], GROUP)
    entry = lax.broadcasted_iota(jnp.int32, (GROUP, GROUP), 0).astype(WIDE)
    hot = (entry == number).astype(WIDE)
    shared_out[0:GROUP, :] = jnp.dot(hot, total, precision=lax.Precision.HIGHEST)
    shared_out[GROUP : GROUP + 1, 0:LANES] = square[0:1, :]
    shared_out[GROUP + 1 : GROUP + 3, :] = sums_back[0:2, :]
    shared_out[GROUP + 3 : GROUP + 5, :] = sums_top[0:2, :]


def head_mlp_kernel(where, *refs):
    cls_mlp_kernel(where, *refs[:7], *refs[11:17])
    add_far_kernel(where, *refs[7:11], *refs[17:])


def head_end_kernel(where, *refs):
    cls_end_kernel(where, *refs[:12], *refs[16:19], refs[23])
    fold_kernel(where, *refs[12:16], *refs[19:23])


def attn_add_kernel(where, *refs):
    far_low, far_high, to_x, to_y, grad, own, got, x_out, y_out, input_out = refs
    add_far_kernel(where, far_low, far_high, to_x, to_y, x_out, y_out)
    input_out[...] = (grad[...] + own[...] + got[...]).astype(LOW)


def rows_input_kernel(where, *refs):
    cls_rows_kernel(where, *refs[:8], refs[11], refs[13])
    grad, own, got, input_out = refs[8], refs[9], refs[10], refs[12]
    input_out[...] = (grad[...] + own[...] + got[...]).astype(LOW)


def cls_rows_kernel(where, *refs):
    packs = refs[:4]
    heads, branch, low, second = refs[4:8]
    out, kept = refs[8:]
    line_at = where[0]
    rows, width = kept.shape[1:]
    for step, pack in enumerate(packs):
        first = pack.shape[0] - rows
        kept[(line_at + LINE - step) % LINE] = pack[first:, :width]
    starts = (MODEL, 2 * MODEL, 3 * MODEL, 4 * MODEL)
    out[:, 0:MODEL] = heads[:, :MODEL].astype(LOW)
    for piece, start in enumerate(starts):
        from_at = piece * SPAN
        for tile in range(MODEL // LANES):
            total = None
            for at in range(PLANE):
                inner = tile - TILE_START[at]
                if inner in (0, 1):
                    first = from_at + inner * LANES
                    value = kept[at, :, first : first + LANES]
                    total = value if total is None else total + value
            out[:, start + tile * LANES : start + (tile + 1) * LANES] = total
    out[:, 5 * MODEL : 6 * MODEL] = branch[...]
    out[:, 6 * MODEL : 7 * MODEL] = low[...]
    out[:, 7 * MODEL + FF : 8 * MODEL + FF] = second[...]
    part = FF // LINE
    for at in range(PLANE):
        first = 4 * SPAN
        out[:, 7 * MODEL + at * part : 7 * MODEL + (at + 1) * part] = kept[
            at, :, first : first + part
        ]
        out[:, 8 * MODEL + FF + at * part : 8 * MODEL + FF + (at + 1) * part] = kept[
            at, :, first + part : first + 2 * part
        ]


def own_features(rank, width):
    shape = (MODEL, width)
    feature = lax.broadcasted_iota(jnp.int32, shape, 0)
    column = lax.broadcasted_iota(jnp.int32, shape, 1)
    return (feature == rank * width + column).astype(LOW)


def own_vector(rank, pieces, out, flat):
    size = out.shape[0]
    for at, piece in enumerate(pieces):
        flat[:, at * MODEL : (at + 1) * MODEL] = piece
    value = jnp.zeros((1, size), WIDE)
    for chip in range(GROUP):
        value = jnp.where(rank == chip, flat[:, chip * size : (chip + 1) * size], value)
    out[...] = value.reshape(size)


def cls_owner_kernel(where, *refs):
    own, got, shared, mats_out, vec_out, rows, flat = refs
    rank = where[0] * PLANE + where[1]
    width = mats_out.shape[0]
    rows[:GROUP] = own[...]
    rows[GROUP:] = got[...]
    chosen = own_features(rank, width)
    plan = (
        (0, MODEL, 3 * MODEL, 0),
        (4 * MODEL, 5 * MODEL, MODEL, 3 * MODEL),
        (6 * MODEL, 7 * MODEL, FF, 4 * MODEL),
        (7 * MODEL + FF, 8 * MODEL + FF, FF, 4 * MODEL + FF),
    )
    for left, right, size, target in plan:
        side = product_plain(rows[:, left : left + MODEL], chosen).astype(LOW)
        mats_out[:, target : target + size] = product_left(side, rows[:, right : right + size])
    starts = (MODEL, 3 * MODEL, 5 * MODEL, 7 * MODEL + FF)
    pieces = [column_sum(rows[:, start : start + MODEL]) for start in starts]
    pieces += [shared[GROUP + 1 + at : GROUP + 2 + at, :] for at in range(4)]
    starts = [7 * MODEL + at * MODEL for at in range(FF // MODEL)]
    pieces += [column_sum(rows[:, start : start + MODEL]) for start in starts]
    own_vector(rank, pieces, vec_out, flat)


def head_share_kernel(where, *refs):
    packs, mlp = refs[:4], refs[4]
    mine_out, vecs_out, rows = refs[5:]
    rank = where[0] * PLANE + where[1]
    count = LINE * 24
    for at, pack in enumerate(packs):
        rows[at * count : (at + 1) * count] = pack[...]
    total = PLANE * count

    def chosen(base, apart):
        shape = (CORES * GROUP, total)
        row = lax.broadcasted_iota(jnp.int32, shape, 0)
        column = lax.broadcasted_iota(jnp.int32, shape, 1)
        hot = (column == row // 2 * 24 + base + row % 2 * apart).astype(LOW)
        return product_plain(hot, rows[...]).astype(LOW)

    own = own_features(rank, OWN)
    for at, (left, right) in enumerate(((0, 4), (2, 8))):
        side = product_plain(chosen(left, 1), own).astype(LOW)
        for piece in range(FF_HALF // MODEL):
            columns = slice(at * FF_HALF + piece * MODEL, at * FF_HALF + (piece + 1) * MODEL)
            share = product_left(side, chosen(right + 2 * piece, 1))
            mine_out[:, columns] = mlp[:, columns] + share
    shape = (16, total)
    row = lax.broadcasted_iota(jnp.int32, shape, 0)
    column = lax.broadcasted_iota(jnp.int32, shape, 1)
    hot = ((column % 24 == row + 12) & (row < 12)).astype(LOW)
    vecs_out[...] = product_plain(hot, rows[...])


def share_owner_kernel(where, *refs):
    head_share_kernel(where, *refs[:5], *refs[9:11], refs[15])
    cls_owner_kernel(where, *refs[5:8], *refs[11:13], *refs[16:])
    shared, count, pos_out, loss_out = refs[7], refs[8], refs[13], refs[14]
    pos_out[...] = shared[:GROUP, :]
    loss_out[...] = shared[GROUP : GROUP + 1, 0:1] / (count[0:1, 0:1] * MODEL)


def seg_vec_kernel(where, vecs, vecs_got, vec_out, flat):
    rank = where[0] * PLANE + where[1]
    rows = (8 * MODEL + FF) // MODEL
    pieces = [vecs[at : at + 1, :] + vecs_got[at : at + 1, :] for at in range(rows)]
    own_vector(rank, pieces, vec_out, flat)


def column_copies(where, out, base, size, own, got, first):
    core_at = where[2]
    lanes = slice(first, first + size)
    return [
        (own.at[:, lanes], out.at[:, pl.ds(aligned(base + core_at * size), size)]),
        (got.at[:, lanes], out.at[:, pl.ds(aligned(base + (1 - core_at) * size), size)]),
    ]


def store_kernel(where, attn, attn_got, mlp, mlp_got, vecs, vecs_got, out, vec_out, flat, sems):
    pairs = []
    for piece in range(4):
        pairs += column_copies(where, out, piece * MODEL, HALF, attn, attn_got, piece * HALF)
    for piece in range(2):
        base = 4 * MODEL + piece * FF
        pairs += column_copies(where, out, base, FF_HALF, mlp, mlp_got, piece * FF_HALF)
    copies = [
        pltpu.make_async_copy(source, target, sems.at[at])
        for at, (source, target) in enumerate(pairs)
    ]
    for copy in copies:
        copy.start()
    seg_vec_kernel(where, vecs, vecs_got, vec_out, flat)
    wait_all(copies)


def plane_parts(part):
    return (part,) + together(*(in_plane(part, mask) for mask in range(1, PLANE)))


def line_parts(part):
    return (part,) + together(*(along_line(part, apart) for apart in range(1, LINE)))


def slice_local(
    hidden_in,
    targets,
    doc_ids,
    seg_nums,
    valid_flags,
    seg_mats,
    seg_vecs,
    cls_mats,
    cls_vecs,
    seg_pos,
):
    rank, core_at = lax.axis_index("fsdp"), lax.axis_index("rep")
    line_at, plane_at = rank // PLANE, rank % PLANE
    where = jnp.stack([line_at, plane_at, core_at, doc_ids[0], seg_nums[0]]).astype(jnp.int32)
    own_rows, total_columns = seg_mats.shape
    vec_size = seg_vecs.shape[0]
    both_rows = CORES * SEG

    first_piece, live_row, *rest = run_kernel(
        prepare_kernel,
        "prepare",
        [shape_of((own_rows, FIRST), LOW), shape_of((1, SEG))]
        + [shape_of((own_rows, FF_HALF), LOW)] * 2
        + [shape_of((own_rows, QUARTER_HALF), LOW)] * LINE
        + [shape_of((own_rows, HALF), LOW), shape_of((MODEL, PLANE * SPAN), LOW)],
        where,
        (seg_mats, cls_mats),
        (seg_vecs, cls_vecs, valid_flags),
        [
            pltpu.SemaphoreType.DMA((4,)),
            pltpu.VMEM((LINE, own_rows, QUARTER), LOW),
            pltpu.SemaphoreType.DMA((3 + 5 * LINE,)),
        ],
    )
    first_line = line_parts(first_piece)
    second_piece, third_piece, quarters, cls_out_piece, order = (
        rest[0],
        rest[1],
        rest[2:-2],
        rest[-2],
        rest[-1],
    )

    def joined(*pieces):
        return jnp.concatenate(pieces, axis=1)

    def sent_both(to_x, to_y):
        to_x, to_y = together(to_x, to_y)
        return together(in_plane(to_x, 1), in_plane(to_y, 2))

    own_sent = joined(first_piece, second_piece, third_piece)
    own_x, own_y = sent_both(own_sent, own_sent)
    first_line = first_line[:1] + tuple(after(got, own_x, own_y) for got in first_line[1:])
    hidden_got = other_core(after(hidden_in, own_x, own_y))
    live_got = other_core(after(live_row, own_x, own_y))
    to_x = joined(after(own_y, hidden_got, live_got)[:, OWN_CUT:], *first_line[1:])
    to_y = joined(own_x[:, :OWN_CUT], *first_line[1:])
    first_x, first_y = sent_both(to_x, to_y)
    second_line = line_parts(after(second_piece, to_x, to_y))

    def halves(group, from_x, from_y):
        width, cut = WIDTHS[group], LINE_CUTS[group]
        if group == 0:
            base_x, base_y = sum(WIDTHS) - OWN_CUT, OWN_CUT
        else:
            before, before_cut = WIDTHS[group - 1], LINE_CUTS[group - 1]
            base_x, base_y = 2 * before - before_cut, before + before_cut
        return (
            from_y[:, base_y + width + cut : base_y + 3 * width],
            from_x[:, base_x : base_x + width + cut],
        )

    high, low = halves(0, first_x, first_y)
    to_x, to_y = joined(high, *second_line[1:]), joined(low, *second_line[1:])
    second_x, second_y = sent_both(to_x, to_y)
    third_line = line_parts(after(third_piece, to_x, to_y))
    high, low = halves(1, second_x, second_y)
    to_x, to_y = joined(high, *third_line[1:]), joined(low, *third_line[1:])
    third_x, third_y = sent_both(to_x, to_y)
    own_parts = (own_x, own_y, first_x, first_y)
    cls_line = (quarters[0],) + tuple(
        along_line(after(quarters[apart], to_x, to_y), apart)
        for apart in range(1, LINE)
    )

    qkv_weight, out_low, out_high, qkv, mixed, vectors, count, hidden_ordered = run_kernel(
        qkv_kernel,
        "seg_qkv",
        [
            shape_of((GROUP, own_rows, 3 * HALF), LOW),
            shape_of((GROUP // 2, own_rows, HALF), LOW),
            shape_of((GROUP // 2, own_rows, HALF), LOW),
            shape_of((both_rows, 3 * HALF), LOW),
            shape_of((both_rows, HALF), LOW),
            shape_of((2 * (8 * MODEL + FF) // MODEL, MODEL)),
            shape_of((8, LANES)),
            shape_of((both_rows, PLANE * SPAN), LOW),
        ],
        where,
        (),
        first_line
        + own_parts
        + (first_x, first_y, second_x, second_y)
        + (hidden_in, hidden_got, live_row, live_got, order),
        [
            pltpu.VMEM((GROUP, own_rows, LANES), LOW),
            pltpu.VMEM((2, 8 * MODEL + FF), WIDE),
            pltpu.VMEM((both_rows, MODEL), LOW),
            pltpu.VMEM((GROUP, own_rows, HALF), LOW),
        ],
        flops=2 * SEG * MODEL * 3 * MODEL,
    )
    out_weight, mixed_ordered, normed_first, inv_first, first_low = run_kernel(
        out_kernel,
        "seg_out",
        [
            shape_of((MODEL, MODEL), LOW),
            shape_of((both_rows, PLANE * SPAN), LOW),
            shape_of((SEG, MODEL)),
            shape_of((SEG, 1)),
            shape_of((SEG, MODEL), LOW),
        ],
        where,
        (),
        (
            hidden_in,
            mixed,
            after(other_core(mixed), third_x, third_y),
            out_low,
            out_high,
            other_core(out_low),
            other_core(out_high),
            vectors,
            order,
        ),
        [pltpu.VMEM((both_rows, MODEL), LOW)],
        flops=2 * SEG * MODEL * MODEL,
    )
    fourth_x, fourth_y = sent_both(*halves(2, third_x, third_y))
    first_got = after(other_core(first_low), fourth_x, fourth_y)
    count = count + other_core(after(count, first_got))
    up_weight, act, slope = run_kernel(
        up_kernel,
        "seg_up",
        [
            shape_of((GROUP, own_rows, FF_HALF), LOW),
            shape_of((both_rows, FF_HALF), LOW),
            shape_of((both_rows, FF_HALF)),
        ],
        where,
        (),
        second_line
        + own_parts
        + (second_x, second_y, third_x, third_y)
        + (first_low, first_got, vectors),
        [pltpu.VMEM((both_rows, MODEL), LOW)],
        flops=2 * SEG * MODEL * FF,
    )
    cls_sent = joined(*cls_line, cls_out_piece)
    cls_sent = after(cls_sent, act)
    cls_x, cls_y = sent_both(cls_sent, cls_sent)
    down_weight, down_own, down_send = run_kernel(
        down_kernel,
        "seg_down",
        [
            shape_of((GROUP, own_rows, FF_HALF), LOW),
            shape_of((SEG, MODEL)),
            shape_of((SEG, MODEL)),
        ],
        where,
        (),
        third_line + own_parts + (third_x, third_y, fourth_x, fourth_y) + (act,),
        flops=2 * SEG * MODEL * FF,
    )
    normed_second, inv_second, diff, out_rows, head_row = run_kernel(
        seg_rows_kernel,
        "seg_rows",
        [
            shape_of((SEG, MODEL)),
            shape_of((SEG, 1)),
            shape_of((SEG, MODEL)),
            shape_of((SEG, MODEL)),
            shape_of((1, 2 * MODEL + LANES)),
        ],
        where,
        (),
        (
            down_own,
            other_core(down_send),
            normed_first,
            vectors,
            targets,
            live_row,
            seg_pos,
        ),
    )
    head_planes = plane_parts(head_row)
    size = LINE // 2 * QUARTER_HALF
    cls_far = sent_both(
        after(cls_y[:, size:], *head_planes[1:]), after(cls_x[:, :size], *head_planes[1:])
    )

    second_grad, second_low, second_sums, first_ordered = run_kernel(
        second_norm_kernel,
        "seg_second_norm",
        [
            shape_of((SEG, MODEL)),
            shape_of((SEG, MODEL), LOW),
            shape_of((3, MODEL)),
            shape_of((both_rows, PLANE * SPAN), LOW),
        ],
        where,
        (),
        (diff, count, normed_second, inv_second, vectors, first_low, first_got, order),
        [pltpu.VMEM((both_rows, MODEL), LOW)],
    )
    second_got = other_core(second_low)
    head_lines = line_parts(after(jnp.concatenate(head_planes), second_got))
    pre, first_grad_own, first_grad_send, up_sums = run_kernel(
        mlp_back_kernel,
        "seg_mlp_back",
        [
            shape_of((both_rows, FF_HALF), LOW),
            shape_of((SEG, MODEL)),
            shape_of((SEG, MODEL)),
            shape_of((FF_HALF // MODEL, MODEL)),
        ],
        where,
        (),
        (second_low, second_got, down_weight, up_weight, slope),
        [pltpu.VMEM((both_rows, MODEL), LOW)],
        flops=4 * SEG * MODEL * FF,
    )
    first_grad_got = other_core(first_grad_send)

    def part_shapes(columns):
        return [
            shape_of((count_of, own_rows, columns), LOW)
            for count_of in (LINE // 2, LINE // 2, LINE, LINE, LINE)
        ]

    mlp_data = (first_ordered, second_low, second_got, pre, act, order)
    mlp_far = run_kernel(
        mlp_far_kernel,
        "seg_mlp_far",
        part_shapes(FF)[:2],
        where,
        (),
        mlp_data,
        [pltpu.VMEM((both_rows, MODEL), LOW)],
        flops=SEG * MODEL * FF,
    )
    head_lines = head_lines[:1] + together(
        *(after(got, mlp_far[0]) for got in head_lines[1:])
    )
    cls_far = together(*(after(got, *head_lines[1:]) for got in cls_far))
    cls_half, cls_out_half = run_kernel(
        cls_gather_kernel,
        "head_gather",
        [
            shape_of((GROUP, own_rows, QUARTER_HALF), LOW),
            shape_of((PLANE, own_rows, HALF), LOW),
        ],
        where,
        (),
        cls_line + (cls_x, cls_y) + cls_far + (cls_out_piece,),
    )
    mlp_parts = list(mlp_far) + list(
        run_kernel(
            mlp_near_kernel,
            "seg_mlp_near",
            part_shapes(FF)[2:],
            where,
            (),
            mlp_data,
            [pltpu.VMEM((both_rows, MODEL), LOW)],
            flops=3 * SEG * MODEL * FF,
        )
    )
    mlp_far = reduce_far(tuple(after(part, *cls_far) for part in mlp_parts[:2]))
    cls_weight, cls_out = run_kernel(
        cls_weight_kernel,
        "head_weight",
        [
            shape_of((GROUP, own_rows, QUARTER), LOW),
            shape_of((4, HEAD_DIM, MODEL), LOW),
        ],
        where,
        (),
        (cls_half, other_core(cls_half), cls_out_half, other_core(cls_out_half)),
    )
    cls_weight = cls_weight.reshape(MODEL, QUARTER)
    cls_out = cls_out.reshape(SPAN, MODEL)
    heads, cls_qkv, cls_mixed, part = run_kernel(
        cls_attend_kernel,
        "head_attend",
        [
            shape_of((GROUP, 2 * MODEL + LANES)),
            shape_of((GROUP, 3 * SPAN), LOW),
            shape_of((GROUP, SPAN), LOW),
            shape_of((GROUP, MODEL)),
        ],
        where,
        (),
        tuple(after(got, mlp_parts[0], first_grad_got) for got in head_lines)
        + (vectors, cls_weight, cls_out),
    )
    cls_normed, cls_inv, cls_low, cls_act, cls_slope, part, *mlp_sent = run_kernel(
        head_mlp_kernel,
        "head_mlp",
        [
            shape_of((GROUP, MODEL)),
            shape_of((GROUP, 1)),
            shape_of((GROUP, MODEL), LOW),
            shape_of((GROUP, FF // LINE), LOW),
            shape_of((GROUP, FF // LINE)),
            shape_of((GROUP, MODEL)),
            shape_of(mlp_parts[2].shape, LOW),
            shape_of(mlp_parts[2].shape, LOW),
        ],
        where,
        (),
        (heads,) + line_parts(part) + (vectors, cls_weight) + mlp_far + tuple(mlp_parts[2:4]),
    )
    mlp_plane = sent_both(*mlp_sent)
    cls_parts = line_parts(part)
    top_row, square, cls_grad, cls_second, cls_pre, part, top_sums = run_kernel(
        cls_top_kernel,
        "head_top",
        [
            shape_of((1, MODEL)),
            shape_of((8, LANES)),
            shape_of((GROUP, MODEL)),
            shape_of((GROUP, MODEL), LOW),
            shape_of((GROUP, FF // LINE), LOW),
            shape_of((GROUP, MODEL)),
            shape_of((2, MODEL)),
        ],
        where,
        (),
        (heads,)
        + cls_parts
        + (vectors, cls_weight, cls_normed, count, cls_slope),
        [pltpu.VMEM((GROUP, MODEL), WIDE)],
    )
    top_parts = line_parts(part)
    cls_grad, cls_branch, cls_proj, part, back_sums = run_kernel(
        cls_attend_back_kernel,
        "head_attend_back",
        [
            shape_of((GROUP, MODEL)),
            shape_of((GROUP, MODEL), LOW),
            shape_of((GROUP, 3 * SPAN), LOW),
            shape_of((GROUP, MODEL)),
            shape_of((2, MODEL)),
        ],
        where,
        (),
        (heads,)
        + top_parts
        + (vectors, cls_weight, cls_out, cls_grad, cls_normed, cls_inv, cls_qkv),
    )
    end_parts = line_parts(part)
    pack = jnp.concatenate([cls_proj, cls_mixed, cls_pre, cls_act], axis=1)
    folded = [shape_of((own_rows, FF))] + [shape_of((own_rows + GROUP, FF), LOW)] * (LINE - 1)
    dheads, head_grad, shared, mlp_own, *mlp_sent = run_kernel(
        head_end_kernel,
        "head_end",
        [shape_of((1, MODEL)), shape_of((1, MODEL)), shape_of((GROUP + 8, MODEL))] + folded,
        where,
        (),
        (heads, cls_grad)
        + end_parts
        + (square, back_sums, top_sums, normed_second, inv_second, vectors)
        + (mlp_parts[4],)
        + mlp_plane
        + (pack,),
        [pltpu.VMEM((GROUP, MODEL), WIDE)],
    )
    got_three, got_two = along_line(mlp_sent[2], 3), along_line(mlp_sent[1], 2)
    mlp_last = mlp_sent[0]
    mlp_got = [None, got_two, got_three]

    head_own, head_send, head_data = run_kernel(
        head_back_kernel,
        "seg_head_back",
        [shape_of((1, MODEL)), shape_of((1, MODEL)), shape_of((12, MODEL))],
        where,
        (),
        (
            head_grad,
            other_core(head_grad),
            down_weight,
            up_weight,
            slope,
            act,
            first_low,
            first_got,
        ),
    )
    grad_summed, branch, mixed_grad, attn_send, first_sums = run_kernel(
        first_norm_kernel,
        "seg_first_norm",
        [
            shape_of((SEG, MODEL)),
            shape_of((SEG, MODEL), LOW),
            shape_of((SEG, MODEL), LOW),
            shape_of((SEG, MODEL), LOW),
            shape_of((3, MODEL)),
        ],
        where,
        (),
        (
            second_grad,
            first_grad_own,
            first_grad_got,
            head_grad,
            head_own,
            other_core(head_send),
            normed_first,
            inv_first,
            vectors,
            out_weight,
        ),
    )
    attn_got = other_core(attn_send)
    proj = run_kernel(
        attn_back_kernel,
        "seg_attn_back",
        [shape_of((both_rows, 3 * HALF), LOW)],
        where,
        (),
        (qkv, mixed_grad, attn_got, live_row, live_got),
        flops=2 * SEG * MODEL * 3 * MODEL,
    )[0]
    attn_data = (hidden_ordered, mixed_ordered, proj, branch, attn_got)
    attn_far = run_kernel(
        attn_far_kernel,
        "seg_attn_far",
        part_shapes(4 * HALF)[:2],
        where,
        (),
        attn_data,
        flops=SEG * MODEL * 2 * MODEL,
    )
    attn_far = reduce_far(tuple(after(part, mlp_got[-1]) for part in attn_far))
    *attn_near, output, input_own, input_send, payload = run_kernel(
        attn_near_kernel,
        "seg_attn_near",
        part_shapes(4 * HALF)[2:]
        + [
            shape_of((SEG, MODEL), LOW),
            shape_of((SEG, MODEL)),
            shape_of((SEG, MODEL)),
            shape_of((24, MODEL), LOW),
        ],
        where,
        (),
        attn_data
        + (top_row, out_rows, live_row, qkv_weight, first_sums, second_sums, up_sums)
        + (dheads, normed_second, head_data),
        [pltpu.VMEM((24, MODEL), WIDE)],
        flops=3 * SEG * MODEL * 2 * MODEL,
    )
    attn_sent = run_kernel(
        add_far_kernel,
        "seg_attn_add",
        [shape_of(attn_near[0].shape, LOW)] * 2,
        where,
        (),
        attn_far + (after(attn_near[0], got_two), attn_near[1]),
    )
    attn_plane = sent_both(*attn_sent)
    mlp_got[0] = along_line(after(mlp_last, got_two), 1)
    input_got = other_core(after(input_send, *attn_sent))
    shared = shared + other_core(after(shared, attn_sent[0]))
    payload_parts = line_parts(after(payload, mlp_got[0], input_got, shared))
    mlp_got = [after(got, attn_plane[0]) for got in mlp_got]
    mlp_sum = reduce_line(mlp_own, mlp_got)
    row_width = 8 * MODEL + 2 * FF
    cls_rows, input_grad = run_kernel(
        rows_input_kernel,
        "head_rows",
        [shape_of((GROUP, row_width), LOW), shape_of((SEG, MODEL), LOW)],
        where,
        (),
        (pack,)
        + tuple(mlp_got)
        + (heads, cls_branch, cls_low, cls_second)
        + (grad_summed, input_own, input_got),
        [pltpu.VMEM((LINE,) + pack.shape, LOW)],
    )
    cls_got = other_core(cls_rows)
    attn_plane = tuple(after(got, output, shared) for got in attn_plane)
    attn_own, *attn_sent = reduce_fold(where, attn_near[2], attn_plane)
    attn_lines = list(
        together(*(along_line(attn_sent[apart - 1], apart) for apart in range(1, LINE)))
    )
    flat = pltpu.VMEM((1, 8 * MODEL + FF), WIDE)
    payload_line = jnp.concatenate(payload_parts)
    mlp_mine, own_vecs, cls_mats_grad, cls_vec_grad, pos_total, loss_value = run_kernel(
        share_owner_kernel,
        "head_owner",
        [
            shape_of((own_rows, FF)),
            shape_of((16, MODEL)),
            shape_of((own_rows, total_columns)),
            shape_of((vec_size,)),
            shape_of((GROUP, MODEL)),
            shape_of((1, 1)),
        ],
        where,
        (),
        tuple(after(got, attn_own) for got in plane_parts(after(payload_line, *attn_plane)))
        + (mlp_sum, cls_rows, cls_got, shared, count),
        [
            pltpu.VMEM((GROUP * 24, MODEL), LOW),
            pltpu.VMEM((CORES * GROUP, row_width), LOW),
            flat,
        ],
        flops=64 * own_rows * total_columns,
    )
    loss_value = loss_value.reshape(())
    attn_lines = together(*(after(got, mlp_mine) for got in attn_lines))
    attn_sum = reduce_line(attn_own, attn_lines)
    seg_mats_grad, seg_vec_grad = run_kernel(
        store_kernel,
        "seg_owner",
        [shape_of((own_rows, total_columns)), shape_of((vec_size,))],
        where,
        (),
        (attn_sum, other_core(attn_sum), mlp_mine, other_core(mlp_mine))
        + (own_vecs, other_core(own_vecs)),
        [flat, pltpu.SemaphoreType.DMA((12,))],
        far=(0,),
    )

    return (
        output,
        input_grad,
        seg_mats_grad,
        seg_vec_grad,
        cls_mats_grad,
        cls_vec_grad,
        pos_total,
        loss_value,
    )


def solution(mesh):
    in_specs = (
        P(("rep", "fsdp"), None),
        P(("rep", "fsdp"), None),
        P(("rep", "fsdp")),
        P(("rep", "fsdp")),
        P(("rep", "fsdp")),
        P("fsdp", None),
        P("fsdp"),
        P("fsdp", None),
        P("fsdp"),
        P(),
    )
    out_specs = (
        P(("rep", "fsdp"), None),
        P(("rep", "fsdp"), None),
        P("fsdp", None),
        P("fsdp"),
        P("fsdp", None),
        P("fsdp"),
        P(),
        P(),
    )
    one_slice = dict(mesh.shape) == {"rep": CORES, "fsdp": LINE * PLANE}
    body = slice_local if one_slice else local
    return jax.shard_map(body, mesh=mesh, in_specs=in_specs, out_specs=out_specs, check_vma=False)
```
